32 devices in a mesh: dp: 16 (over z, x, core), tensor: 2 (over y).
Axes of the slice: x: 2, y: 2, z: 4, core: 2. Of those that a mesh axis runs over, the one named last changes fastest.
Arguments:
- hidden_in: bfloat16 [20480, 768], P('dp'), may hold values from -6 to 6
- cotangent: bfloat16 [20480, 768], P('dp'), may hold values from -6 to 6
- prompt_start: int32 [4], replicated, may hold values from 0 to 511
- cont_gap: int32 [4, 12], replicated, may hold values from 0 to 511
- seg_len: int32 [6, 3], replicated, may hold values from 256 to 5120, as said below
- dilation_rate: int32 [6, 3], replicated, may hold values from 1 to 6, as said below
- pre_gain: bfloat16 [768], replicated, may hold values from 0.5 to 1.5
- pre_bias: bfloat16 [768], replicated, may hold values from -1 to 1
- query_weight: bfloat16 [768, 768], P(None, 'tensor'), may hold values from -0.21875 to 0.21875
- query_bias: bfloat16 [768], P('tensor'), may hold values from -1 to 1
- key_weight: bfloat16 [768, 768], P(None, 'tensor'), may hold values from -0.21875 to 0.21875
- value_weight: bfloat16 [768, 768], P(None, 'tensor'), may hold values from -0.21875 to 0.21875
- value_bias: bfloat16 [768], P('tensor'), may hold values from -1 to 1
- sub_gain: bfloat16 [768], P('tensor'), may hold values from 0.5 to 1.5
- sub_bias: bfloat16 [768], P('tensor'), may hold values from -1 to 1
- out_weight: bfloat16 [768, 768], P('tensor'), may hold values from -0.21875 to 0.21875
- out_bias: bfloat16 [768], replicated, may hold values from -1 to 1
- mid_gain: bfloat16 [768], replicated, may hold values from 0.5 to 1.5
- mid_bias: bfloat16 [768], replicated, may hold values from -1 to 1
- inner_weight: bfloat16 [768, 3072], P(None, 'tensor'), may hold values from -0.21875 to 0.21875
- inner_bias: bfloat16 [3072], P('tensor'), may hold values from -1 to 1
- ffn_gain: bfloat16 [3072], P('tensor'), may hold values from 0.5 to 1.5
- ffn_bias: bfloat16 [3072], P('tensor'), may hold values from -1 to 1
- outer_weight: bfloat16 [3072, 768], P('tensor'), may hold values from -0.109375 to 0.109375
- outer_bias: bfloat16 [768], replicated, may hold values from -1 to 1
Outputs:
- output: bfloat16 [20480, 768], P('dp')
- input_grad: bfloat16 [20480, 768], P('dp')
- pre_gain_grad: float32 [768], P('dp')
- pre_bias_grad: float32 [768], P('dp')
- query_weight_grad: float32 [768, 768], P('dp', 'tensor')
- query_bias_grad: float32 [768], P(('tensor', 'dp'))
- key_weight_grad: float32 [768, 768], P('dp', 'tensor')
- value_weight_grad: float32 [768, 768], P('dp', 'tensor')
- value_bias_grad: float32 [768], P(('tensor', 'dp'))
- sub_gain_grad: float32 [768], P(('tensor', 'dp'))
- sub_bias_grad: float32 [768], P(('tensor', 'dp'))
- out_weight_grad: float32 [768, 768], P('tensor', 'dp')
- out_bias_grad: float32 [768], P('dp')
- mid_gain_grad: float32 [768], P('dp')
- mid_bias_grad: float32 [768], P('dp')
- inner_weight_grad: float32 [768, 3072], P('dp', 'tensor')
- inner_bias_grad: float32 [3072], P(('tensor', 'dp'))
- ffn_gain_grad: float32 [3072], P(('tensor', 'dp'))
- ffn_bias_grad: float32 [3072], P(('tensor', 'dp'))
- outer_weight_grad: float32 [3072, 768], P('tensor', 'dp')
- outer_bias_grad: float32 [768], P('dp')
The draws below stay inside these ranges and needn't reach their ends.
Inputs may be any that keep to these rules, and one draw needn't show every extreme that they name: seg_len[a, c] is the segment length of configuration c of head pair a (heads 2a and 2a + 1); one segment of the last configuration holds every position of a group. dilation_rate[a, 0] = 1 for every head pair a.
All inputs are finite; a program needn't handle non-finite values.
Results may differ from the reference program's by a relative error of at most 0.017.
Values may be sent and summed in bfloat16 or wider, within the bound.
A program may use at most 256 MiB of HBM per device.

```python
import jax
import jax.numpy as jnp
from jax import lax

D = 768
HEADS = 12
HD = 64
FF = 3072
PROMPT = 2048
CONT = 256
GDEV = 4
KDEV = 3
HGROUPS = 6
PDEV = 512
CONTS = 12
GROUPS = 4
TOK_DEV = 1280
TOKENS = 20480


def config_table(key):
    orders = [jax.random.permutation(jax.random.fold_in(key, 7 + column), HGROUPS) for column in range(5)]
    lengths = jnp.stack([CONT * (1 + orders[0] % 4), 4 * CONT * (1 + orders[1] % 2), 16 * CONT + 2 * CONT * (orders[2] % 3)], axis=1)
    periods = jnp.stack([1 + 0 * orders[3], 2 + orders[3] % 2, 4 + orders[4] % 3], axis=1)
    return (lengths.astype(jnp.int32), periods.astype(jnp.int32))


def draw_seg_len(key, part):
    return config_table(key)[0]


def draw_dilation_rate(key, part):
    return config_table(key)[1]


def place_ends(values, own_key, smallest, top_value):
    extent = values.shape
    place = [jax.random.randint(jax.random.fold_in(own_key, axis), (), 0, extent[axis]) for axis in range(len(extent))]
    values = values.at[tuple(place)].set(smallest)
    longest = extent.index(max(extent))
    place[longest] = (place[longest] + 1) % extent[longest]
    return values.at[tuple(place)].set(top_value)


def strengthened(array, rng, source, target, shards_of, factor):
    owner, partner = [(jnp.arange(array.shape[dim]) // (array.shape[dim] // shards_of)).reshape([-1 if axis == dim else 1 for axis in range(array.ndim)]) for dim in (source, target)]
    chosen = jax.random.permutation(rng, shards_of)[partner]
    strong = (owner == chosen) | (owner == (partner + shards_of // 2) % shards_of)
    return jnp.where(strong, factor * array, array)


def steps_of(key, dims, cuts, least, high):
    loudness, own = 1.0, jax.random.fold_in(key, 6)
    for dim, shards_of in cuts:
        heights = jnp.exp(jax.random.uniform(jax.random.fold_in(own, dim), (shards_of,), jnp.float32, least / len(cuts), high / len(cuts)))
        loudness = loudness * jnp.repeat(heights, dims[dim] // shards_of).reshape([-1 if axis == dim else 1 for axis in range(len(dims))])
    return loudness


def normal_values(key, shape, scale, reach, split=(), dtype=jnp.bfloat16):
    values = jax.random.normal(key, shape, jnp.float32) * scale
    if len(split) > 0:
        values = steps_of(key, shape, split, -0.22, 0.18) * values
    return jnp.clip(values, min=-reach, max=reach).astype(dtype)


def gaussian_with(rng, shape, scale, most, split, heavy, held_as=jnp.bfloat16):
    drawn = scale * jax.random.normal(rng, shape, jnp.float32)
    if split:
        drawn = drawn * steps_of(rng, shape, split, -0.22, 0.18)
    return jnp.clip(strengthened(drawn, jax.random.fold_in(rng, 3), *heavy), -most, most).astype(held_as)


def setup_inputs(seed: int = 0) -> dict:
    key_list = jax.random.split(jax.random.key(seed), 26)
    hidden_in = gaussian_with(key_list[0], (TOKENS, D), 1.0, 6.0, ((0, 16),), (0, 1, 16, 2.0))
    cotangent = gaussian_with(key_list[1], (TOKENS, D), 1.0, 6.0, ((0, 16),), (0, 1, 16, 2.0))
    prompt_start = place_ends(jax.random.randint(key_list[2], (GROUPS,), 0, 2 * CONT), jax.random.fold_in(key_list[2], 1), 0, (2 * CONT) - 1).astype(jnp.int32)
    cont_gap = place_ends(jax.random.randint(key_list[3], (GROUPS, CONTS), 0, 2 * CONT), jax.random.fold_in(key_list[3], 1), 0, (2 * CONT) - 1).astype(jnp.int32)
    seg_len = draw_seg_len(jax.random.fold_in(key_list[25], 71), 0)
    dilation_rate = draw_dilation_rate(jax.random.fold_in(key_list[25], 71), 0)
    pre_gain = jnp.clip(1.0 + 0.1 * jax.random.normal(key_list[6], (D,), jnp.float32), 0.5, 1.5).astype(jnp.bfloat16)
    pre_bias = normal_values(key_list[7], (D,), 0.2, 1.0)
    query_weight = normal_values(key_list[8], (D, D), D ** -0.5, 0.21875, ((1, 2),))
    query_bias = normal_values(key_list[9], (D,), 0.2, 1.0, ((0, 2),))
    key_weight = normal_values(key_list[10], (D, D), D ** -0.5, 0.21875, ((1, 2),))
    value_weight = normal_values(key_list[11], (D, D), D ** -0.5, 0.21875, ((1, 2),))
    value_bias = normal_values(key_list[12], (D,), 0.2, 1.0, ((0, 2),))
    sub_gain = jnp.clip(1.0 + 0.1 * jax.random.normal(key_list[13], (D,), jnp.float32), 0.5, 1.5).astype(jnp.bfloat16)
    sub_bias = normal_values(key_list[14], (D,), 0.2, 1.0, ((0, 2),))
    out_weight = normal_values(key_list[15], (D, D), D ** -0.5, 0.21875, ((0, 2),))
    out_bias = normal_values(key_list[16], (D,), 0.2, 1.0)
    mid_gain = jnp.clip(1.0 + 0.1 * jax.random.normal(key_list[17], (D,), jnp.float32), 0.5, 1.5).astype(jnp.bfloat16)
    mid_bias = normal_values(key_list[18], (D,), 0.2, 1.0)
    inner_weight = normal_values(key_list[19], (D, FF), D ** -0.5, 0.21875, ((1, 2),))
    inner_bias = normal_values(key_list[20], (FF,), 0.2, 1.0, ((0, 2),))
    ffn_gain = jnp.clip(1.0 + 0.1 * jax.random.normal(key_list[21], (FF,), jnp.float32), 0.5, 1.5).astype(jnp.bfloat16)
    ffn_bias = normal_values(key_list[22], (FF,), 0.2, 1.0, ((0, 2),))
    outer_weight = normal_values(key_list[23], (FF, D), FF ** -0.5, 0.109375, ((0, 2),))
    outer_bias = normal_values(key_list[24], (D,), 0.2, 1.0)
    return dict(hidden_in=hidden_in, cotangent=cotangent, prompt_start=prompt_start, cont_gap=cont_gap, seg_len=seg_len, dilation_rate=dilation_rate, pre_gain=pre_gain, pre_bias=pre_bias, query_weight=query_weight, query_bias=query_bias, key_weight=key_weight, value_weight=value_weight, value_bias=value_bias, sub_gain=sub_gain, sub_bias=sub_bias, out_weight=out_weight, out_bias=out_bias, mid_gain=mid_gain, mid_bias=mid_bias, inner_weight=inner_weight, inner_bias=inner_bias, ffn_gain=ffn_gain, ffn_bias=ffn_bias, outer_weight=outer_weight, outer_bias=outer_bias)


EPSILON = 1e-05

@jax.custom_vjp
def low(v):
    return lax.optimization_barrier(v.astype(jnp.bfloat16)).astype(jnp.float32)

@jax.custom_vjp
def low_back(v):
    return v

def low_keep(v):
    return (low(v), None)

def low_pass(kept, grad):
    return (grad,)

def back_keep(v):
    return (v, None)

def back_low(kept, grad):
    return (low(grad),)
low.defvjp(low_keep, low_pass)
low_back.defvjp(back_keep, back_low)

def round_both(values):
    return low_back(low(values))

def dense(left, right):
    return jnp.dot(left, right, precision=lax.Precision.HIGHEST)

def norm_rows(values, gain, bias):
    center = lax.optimization_barrier(jnp.mean(values, axis=-1, keepdims=True))
    spread = lax.optimization_barrier(jnp.mean(values * values, axis=-1, keepdims=True)) - center * center
    return (values - center) * lax.rsqrt(spread + EPSILON) * gain + bias

def multiplicity(query_at, key_at, seg_heads, rate_heads, head_ids):
    query_grid = query_at[..., None, :, None]
    key_grid = key_at[..., None, None, :]
    counted = jnp.zeros((), jnp.float32)
    for config in range(seg_heads.shape[1]):
        seg_width = seg_heads[:, config][:, None, None]
        period = rate_heads[:, config][:, None, None]
        phase_id = (head_ids % rate_heads[:, config])[:, None, None]
        in_segment = (query_grid // seg_width == key_grid // seg_width) & (query_grid % period == phase_id) & (key_grid % period == phase_id)
        counted = counted + in_segment.astype(jnp.float32)
    return jnp.where(key_grid <= query_grid, counted, 0.0)

def attend_block(queries, keys_all, values_all, weights):
    scores = low_back(jnp.einsum('rhe,khe->hrk', queries, keys_all, precision=lax.Precision.HIGHEST))
    logits = jnp.where(weights > 0, scores + jnp.log(jnp.maximum(weights, 1.0)), -jnp.inf)
    probabilities = low(jax.nn.softmax(logits, axis=-1))
    return jnp.einsum('hrk,khe->rhe', probabilities, values_all, precision=lax.Precision.HIGHEST)

def group_forward(params, group_rows, start_at, gaps, seg_heads, rate_heads):
    pre_gain, pre_bias, query_weight, query_bias, key_weight, value_weight, value_bias, sub_gain, sub_bias, out_weight, out_bias, mid_gain, mid_bias, inner_weight, inner_bias, ffn_gain, ffn_bias, outer_weight, outer_bias = params
    rows_all = group_rows.reshape(GDEV * TOK_DEV, D)
    normed = low(norm_rows(rows_all, pre_gain, pre_bias))
    queries = round_both((dense(normed, query_weight) + query_bias) * 0.125)
    keys_all = round_both(dense(normed, key_weight))
    values_all = round_both(dense(normed, value_weight) + value_bias)
    head_ids = jnp.arange(HEADS).astype(jnp.int32)
    prompt_at = (start_at + jnp.arange(PROMPT)).astype(jnp.int32)
    cont_at = (start_at + PROMPT + gaps[:, None] + jnp.arange(CONT)[None, :]).astype(jnp.int32)

    def split_rows(flat_rows):
        shaped = flat_rows.reshape(GDEV, TOK_DEV, HEADS, HD)
        return (shaped[:, :PDEV].reshape(PROMPT, HEADS, HD), shaped[:, PDEV:].reshape(CONTS, CONT, HEADS, HD))
    prompt_q, cont_q = split_rows(queries)
    prompt_k, cont_k = split_rows(keys_all)
    prompt_v, cont_v = split_rows(values_all)
    block_rows = min(512, PROMPT)
    block_count = PROMPT // block_rows

    def prompt_block(pieces):
        block_q, block_at = pieces
        return attend_block(block_q, prompt_k, prompt_v, multiplicity(block_at, prompt_at, seg_heads, rate_heads, head_ids))
    prompt_out = lax.map(jax.checkpoint(prompt_block), (prompt_q.reshape(block_count, block_rows, HEADS, HD), prompt_at.reshape(block_count, block_rows)))

    def cont_block(pieces):
        block_q, block_k, block_v, block_at = pieces
        joined_k = jnp.concatenate([prompt_k, block_k], axis=0)
        joined_v = jnp.concatenate([prompt_v, block_v], axis=0)
        joined_at = jnp.concatenate([prompt_at, block_at]).astype(jnp.int32)
        return attend_block(block_q, joined_k, joined_v, multiplicity(block_at, joined_at, seg_heads, rate_heads, head_ids))
    cont_out = lax.map(jax.checkpoint(cont_block), (cont_q, cont_k, cont_v, cont_at))
    attended = jnp.concatenate([prompt_out.reshape(GDEV, PDEV, D), cont_out.reshape(GDEV, KDEV * CONT, D)], axis=1).reshape(GDEV * TOK_DEV, D)
    attended = low_back(attended)
    sub_out = low(norm_rows(attended, sub_gain, sub_bias))
    branch = low_back(dense(sub_out, out_weight) + out_bias)
    mixed = rows_all + branch
    mid = low(norm_rows(mixed, mid_gain, mid_bias))
    inner = low_back(dense(mid, inner_weight) + inner_bias)
    activated = jax.nn.gelu(inner, approximate=False)
    ffn_out = low(norm_rows(activated, ffn_gain, ffn_bias))
    outer = low_back(dense(ffn_out, outer_weight) + outer_bias)
    return (mixed + outer).reshape(GDEV, TOK_DEV, D)

def layer_forward(inputs, params, prompt_start, cont_gap, seg_heads, rate_heads):
    grouped = inputs.reshape(GROUPS, GDEV, TOK_DEV, D)

    def scan_step(running, pieces):
        group_rows, start_at, gaps = pieces
        return (running, group_forward(params, group_rows, start_at, gaps, seg_heads, rate_heads))
    _, outputs = lax.scan(scan_step, jnp.zeros((), jnp.float32), (grouped, prompt_start, cont_gap))
    return outputs.reshape(TOKENS, D)

def reference(hidden_in, cotangent, prompt_start, cont_gap, seg_len, dilation_rate, pre_gain, pre_bias, query_weight, query_bias, key_weight, value_weight, value_bias, sub_gain, sub_bias, out_weight, out_bias, mid_gain, mid_bias, inner_weight, inner_bias, ffn_gain, ffn_bias, outer_weight, outer_bias):
    params = tuple((weight.astype(jnp.float32) for weight in (pre_gain, pre_bias, query_weight, query_bias, key_weight, value_weight, value_bias, sub_gain, sub_bias, out_weight, out_bias, mid_gain, mid_bias, inner_weight, inner_bias, ffn_gain, ffn_bias, outer_weight, outer_bias)))
    seg_heads = jnp.repeat(seg_len, 2, axis=0)
    rate_heads = jnp.repeat(dilation_rate, 2, axis=0)

    def closed(inputs, weights):
        return layer_forward(inputs, weights, prompt_start, cont_gap, seg_heads, rate_heads)
    result, pullback = jax.vjp(closed, hidden_in.astype(jnp.float32), params)
    input_grad, weight_grads = pullback(cotangent.astype(jnp.float32))
    return (result.astype(jnp.bfloat16), input_grad.astype(jnp.bfloat16), weight_grads[0], weight_grads[1], weight_grads[2], weight_grads[3], weight_grads[4], weight_grads[5], weight_grads[6], weight_grads[7], weight_grads[8], weight_grads[9], weight_grads[10], weight_grads[11], weight_grads[12], weight_grads[13], weight_grads[14], weight_grads[15], weight_grads[16], weight_grads[17], weight_grads[18])
```

```python
import jax
import jax.numpy as jnp
from jax import lax
from jax.experimental import pallas as pl
from jax.experimental.pallas import tpu as pltpu
from jax.sharding import PartitionSpec as P

HD = 64
PROMPT = 2048
CONT = 256
GDEV = 4
TILE = 256
CHUNK = PROMPT // GDEV
PTILES = CHUNK // TILE
LOG2E = 1.4426950408889634
BF = jnp.bfloat16
F32 = jnp.float32
TAB = 10


def dot_nt(a, b):
    return lax.dot_general(a, b, (((1,), (1,)), ((), ())), preferred_element_type=F32)


def dot_nn(a, b):
    return lax.dot_general(a, b, (((1,), (0,)), ((), ())), preferred_element_type=F32)


def low_half(rows):
    return lax.broadcasted_iota(jnp.int32, (rows, 128), 1) < HD


def codes(at, tab, pair, miss):
    def cell(i):
        return tab[pair * TAB + i]

    first = jnp.floor((at + 0.5) * cell(0))
    second = jnp.floor((at + 0.5) * cell(1))
    rest1 = at - cell(2) * jnp.floor((at + 0.5) * cell(3))
    rest2 = at - cell(4) * jnp.floor((at + 0.5) * cell(5))
    return [
        first,
        jnp.where(rest1 == cell(6), second, miss),
        jnp.where(rest1 == cell(7), second, miss),
        jnp.where(rest2 == cell(8), 1.0, 0.0),
        jnp.where(rest2 == cell(9), 1.0, 0.0),
    ]


def fwd_kernel(info, tab, q_ref, kp_ref, vp_ref, ko_ref, vo_ref, o_ref, e_ref, li_ref, t_s, kc_s):
    pair = pl.program_id(0)
    step = pl.program_id(1)
    member = info[0]
    low = low_half(TILE)
    q = q_ref[...]
    zero = jnp.zeros_like(q)
    qs = [jnp.where(low, q, zero), jnp.where(low, zero, q)]
    row = lax.broadcasted_iota(jnp.int32, (TILE, 128), 0).astype(F32)
    at_q = info[2 + step].astype(F32) + row
    qc = codes(at_q, tab, pair, -2.0)

    @pl.when(step == 0)
    def _():
        at_k = info[1].astype(F32) + lax.broadcasted_iota(jnp.int32, (8, PROMPT), 1).astype(F32)
        for i, c in enumerate(codes(at_k, tab, pair, -1.0)):
            kc_s[i] = c

    def logits(mx, keys, kc, causal, at, width):
        out = []
        for h in range(2):
            s = dot_nt(qs[h], keys)
            top = mx[h]
            for g in range(width // 128):
                lanes = slice(g * 128, (g + 1) * 128)
                w = jnp.where(qc[0] == kc[0][:, lanes], 1.0, 0.0)
                w = w + jnp.where(qc[1 + h] == kc[1 + h][:, lanes], 1.0, 0.0)
                w = w + qc[3 + h] * kc[3 + h][:, lanes]
                if causal is not None:
                    w = jnp.where(causal[:, lanes], w, 0.0)
                t = s[:, lanes] * LOG2E + jnp.log2(w)
                t_s[h, :, pl.ds(at + g * 128, 128)] = t
                top = jnp.maximum(top, t)
            out.append(top)
        return tuple(out)

    def weigh(carry, vals, m, at, width):
        sums, accs = carry
        ns, na = [], []
        for h in range(2):
            total = sums[h]
            parts = []
            for g in range(width // 128):
                e = jnp.exp2(t_s[h, :, pl.ds(at + g * 128, 128)] - m[h])
                total = total + e
                parts.append(e.astype(BF))
            el = jnp.concatenate(parts, axis=1)
            e_ref[h, :, pl.ds(at, width)] = el
            ns.append(total)
            na.append(accs[h] + dot_nn(el, vals))
        return (tuple(ns), tuple(na))

    def finish(carry):
        sums, accs = carry
        li = [1.0 / jnp.sum(s, axis=1, keepdims=True) for s in sums]
        lfull = jnp.where(low, li[0], li[1])
        li_ref[...] = lfull
        o_ref[...] = (jnp.where(low, accs[0], accs[1]) * lfull).astype(BF)

    def tops(mx):
        return [jnp.broadcast_to(jnp.max(x, axis=1, keepdims=True), (TILE, 128)) for x in mx]

    neg = jnp.full((TILE, 128), -jnp.inf, F32)
    zf = jnp.zeros((TILE, 128), F32)

    def key_codes(at, width):
        return [kc_s[i, 0:1, pl.ds(at, width)] for i in range(5)]

    @pl.when(step < PTILES)
    def _():
        def one(j, mx):
            at = pl.multiple_of(j * CHUNK, CHUNK)
            held = pl.multiple_of((j ^ member) * CHUNK, CHUNK)
            return logits(mx, kp_ref[pl.ds(held, CHUNK), :], key_codes(at, CHUNK), None, held, CHUNK)

        mx = lax.fori_loop(0, member, one, (neg, neg))
        at = pl.multiple_of(member * CHUNK, CHUNK)
        rows = lax.broadcasted_iota(jnp.int32, (TILE, CHUNK), 0) + step * TILE
        cols = lax.broadcasted_iota(jnp.int32, (TILE, CHUNK), 1)
        mx = logits(mx, kp_ref[0:CHUNK, :], key_codes(at, CHUNK), cols <= rows, 0, CHUNK)
        m = tops(mx)

        def two(j, carry):
            held = pl.multiple_of((j ^ member) * CHUNK, CHUNK)
            return weigh(carry, vp_ref[pl.ds(held, CHUNK), :], m, held, CHUNK)

        finish(lax.fori_loop(0, member + 1, two, ((zf, zf), (zf, zf))))

    @pl.when(step >= PTILES)
    def _():
        mx = (neg, neg)
        for j in range(GDEV):
            at = pl.multiple_of((j ^ member) * CHUNK, CHUNK)
            mx = logits(mx, kp_ref[j * CHUNK : (j + 1) * CHUNK, :], key_codes(at, CHUNK), None, j * CHUNK, CHUNK)
        rows = lax.broadcasted_iota(jnp.int32, (TILE, CONT), 0)
        cols = lax.broadcasted_iota(jnp.int32, (TILE, CONT), 1)
        at_k = info[2 + step].astype(F32) + lax.broadcasted_iota(jnp.int32, (8, CONT), 1).astype(F32)
        own = [c[0:1] for c in codes(at_k, tab, pair, -1.0)]
        mx = logits(mx, ko_ref[...], own, cols <= rows, PROMPT, CONT)
        m = tops(mx)
        carry = ((zf, zf), (zf, zf))
        for j in range(GDEV):
            carry = weigh(carry, vp_ref[j * CHUNK : (j + 1) * CHUNK, :], m, j * CHUNK, CHUNK)
        finish(weigh(carry, vo_ref[...], m, PROMPT, CONT))


def attend(info, tab, q, k, v, kp, vp):
    rows, width = q.shape
    pairs = width // 128
    span = PROMPT + CONT
    tile = pl.BlockSpec((TILE, 128), lambda a, t, s, f: (t, a))
    whole = pl.BlockSpec((PROMPT, 128), lambda a, t, s, f: (0, a))
    return pl.pallas_call(
        fwd_kernel,
        grid_spec=pltpu.PrefetchScalarGridSpec(
            num_scalar_prefetch=2,
            grid=(pairs, rows // TILE),
            in_specs=[tile, whole, whole, tile, tile],
            out_specs=[tile, pl.BlockSpec((2, TILE, span), lambda a, t, s, f: (a, t, 0)), tile],
            scratch_shapes=[pltpu.VMEM((2, TILE, span), F32), pltpu.VMEM((5, 8, PROMPT), F32)],
        ),
        out_shape=[
            jax.ShapeDtypeStruct((rows, width), BF),
            jax.ShapeDtypeStruct((2 * pairs, rows, span), BF),
            jax.ShapeDtypeStruct((rows, width), F32),
        ],
        compiler_params=pltpu.CompilerParams(vmem_limit_bytes=48 << 20),
        cost_estimate=pl.CostEstimate(flops=16 * 10**9, bytes_accessed=60 * 10**6, transcendentals=0),
        name="attend",
    )(info, tab, q, kp, vp, k, v)


def bwd_kernel(info, q_ref, kp_ref, vp_ref, ko_ref, vo_ref, o_ref, li_ref, g_ref, e_ref, dq_ref, dk_ref, dv_ref, dko_ref, dvo_ref, dk_s, dv_s):
    step = pl.program_id(1)
    member = info[0]
    low = low_half(TILE)
    g = g_ref[...].astype(F32) * li_ref[...]
    prod = g * o_ref[...].astype(F32)
    zf = jnp.zeros((TILE, 128), F32)
    deltas = [
        jnp.sum(jnp.where(low, prod, zf), axis=1, keepdims=True),
        jnp.sum(jnp.where(low, zf, prod), axis=1, keepdims=True),
    ]
    gs = [jnp.where(low, g, zf).astype(BF), jnp.where(low, zf, g).astype(BF)]
    gt = jnp.transpose(g).astype(BF)
    qt = jnp.transpose(q_ref[...].astype(F32)).astype(BF)

    def grads(dq, keys, vals, at, width):
        out, dks, dvs = [], [], []
        for h in range(2):
            e = e_ref[h, :, pl.ds(at, width)]
            dp = dot_nt(gs[h], vals)
            ds = (e.astype(F32) * (dp - deltas[h])).astype(BF)
            out.append(dq[h] + dot_nn(ds, keys))
            dks.append(dot_nn(qt[h * HD : (h + 1) * HD, :], ds))
            dvs.append(dot_nn(gt[h * HD : (h + 1) * HD, :], e))
        return tuple(out), dks, dvs

    @pl.when(step == 0)
    def _():
        dk_s[...] = jnp.zeros_like(dk_s)
        dv_s[...] = jnp.zeros_like(dv_s)

    def add(at, width, dks, dvs):
        for h in range(2):
            dk_s[h * HD : (h + 1) * HD, pl.ds(at, width)] += dks[h]
            dv_s[h * HD : (h + 1) * HD, pl.ds(at, width)] += dvs[h]

    def scaled(dq):
        return (jnp.where(low, dq[0], dq[1]).astype(BF).astype(F32) * 0.125).astype(BF)

    @pl.when(step < PTILES)
    def _():
        def one(j, dq):
            at = pl.multiple_of((j ^ member) * CHUNK, CHUNK)
            dq, dks, dvs = grads(dq, kp_ref[pl.ds(at, CHUNK), :], vp_ref[pl.ds(at, CHUNK), :], at, CHUNK)
            add(at, CHUNK, dks, dvs)
            return dq

        dq_ref[...] = scaled(lax.fori_loop(0, member + 1, one, (zf, zf)))
        dko_ref[...] = jnp.zeros_like(dko_ref)
        dvo_ref[...] = jnp.zeros_like(dvo_ref)

    @pl.when(step >= PTILES)
    def _():
        dq = (zf, zf)
        for j in range(GDEV):
            span = slice(j * CHUNK, (j + 1) * CHUNK)
            dq, dks, dvs = grads(dq, kp_ref[span, :], vp_ref[span, :], j * CHUNK, CHUNK)
            add(j * CHUNK, CHUNK, dks, dvs)
        dq, dks, dvs = grads(dq, ko_ref[...], vo_ref[...], PROMPT, CONT)
        dq_ref[...] = scaled(dq)
        dko_ref[...] = jnp.transpose(jnp.concatenate(dks, axis=0)).astype(BF)
        dvo_ref[...] = jnp.transpose(jnp.concatenate(dvs, axis=0)).astype(BF)

    @pl.when(step == pl.num_programs(1) - 1)
    def _():
        for j in range(GDEV):
            span = slice(j * CHUNK, (j + 1) * CHUNK)
            dk_ref[span, :] = jnp.transpose(dk_s[:, span]).astype(BF)
            dv_ref[span, :] = jnp.transpose(dv_s[:, span]).astype(BF)


def attend_back(info, q, k, v, kp, vp, o, li, g, e):
    rows, width = q.shape
    pairs = width // 128
    span = PROMPT + CONT
    tile = pl.BlockSpec((TILE, 128), lambda a, t, s: (t, a))
    whole = pl.BlockSpec((PROMPT, 128), lambda a, t, s: (0, a))
    return pl.pallas_call(
        bwd_kernel,
        grid_spec=pltpu.PrefetchScalarGridSpec(
            num_scalar_prefetch=1,
            grid=(pairs, rows // TILE),
            in_specs=[tile, whole, whole, tile, tile, tile, tile, tile, pl.BlockSpec((2, TILE, span), lambda a, t, s: (a, t, 0))],
            out_specs=[tile, whole, whole, tile, tile],
            scratch_shapes=[pltpu.VMEM((128, PROMPT), F32), pltpu.VMEM((128, PROMPT), F32)],
        ),
        out_shape=[
            jax.ShapeDtypeStruct((rows, width), BF),
            jax.ShapeDtypeStruct((PROMPT, width), BF),
            jax.ShapeDtypeStruct((PROMPT, width), BF),
            jax.ShapeDtypeStruct((rows, width), BF),
            jax.ShapeDtypeStruct((rows, width), BF),
        ],
        compiler_params=pltpu.CompilerParams(vmem_limit_bytes=48 << 20),
        cost_estimate=pl.CostEstimate(flops=30 * 10**9, bytes_accessed=60 * 10**6, transcendentals=0),
        name="attend_back",
    )(info, q, kp, vp, k, v, o, li, g, e)


D = 768
FF = 3072
EPSILON = 1e-05


def flip(value, axis, bit):
    return lax.ppermute(value, axis, [(i, i ^ (1 << bit)) for i in range(lax.axis_size(axis))])


def contract_rows(left, right):
    return lax.dot_general(left, right, (((0,), (0,)), ((), ())), preferred_element_type=F32)


def back_project(left, right):
    return lax.dot_general(left, right, (((1,), (1,)), ((), ())), preferred_element_type=F32)


def dense(left, right):
    return jnp.dot(left, right, preferred_element_type=F32)


def exact_gelu(values):
    return jax.nn.gelu(values, approximate=False)


def norm_rows(values, gain, bias):
    center = jnp.mean(values, axis=-1, keepdims=True)
    spread = jnp.mean(values * values, axis=-1, keepdims=True) - center * center
    scaled = lax.rsqrt(spread + EPSILON)
    unit_rows = (values - center) * scaled
    return (unit_rows * gain + bias, unit_rows, scaled)


def norm_back(grad_rows, gain, unit_rows, scaled):
    shaped = grad_rows * gain
    return scaled * (
        shaped
        - jnp.mean(shaped, axis=-1, keepdims=True)
        - unit_rows * jnp.mean(shaped * unit_rows, axis=-1, keepdims=True)
    )


def in_order(which, mine, other, axis):
    return jnp.where(
        which == 0,
        jnp.concatenate([mine, other], axis=axis),
        jnp.concatenate([other, mine], axis=axis),
    )


def fetch(weight, core, axis):
    half = weight.shape[axis] // 2
    sent = lax.dynamic_slice_in_dim(weight, core * half, half, axis)
    got = flip(sent, "tensor", 0)
    return in_order(core, got, flip(got, "dp", 0), axis)


def halving(value, device):
    bits = lax.axis_size("dp").bit_length() - 1
    rows, columns = value.shape
    current = value
    for bit in range(bits):
        upper = device // (1 << bit) % 2
        left = bits - bit
        view = current.reshape((1 << (left - 1), 2, -1, columns))
        kept = lax.dynamic_index_in_dim(view, upper, 1, keepdims=False)
        sent = lax.dynamic_index_in_dim(view, 1 - upper, 1, keepdims=False)
        got = flip(sent, "dp", bit)
        current = (kept.astype(F32) + got.astype(F32)).astype(BF)
    return current.reshape(rows >> bits, columns)


def body(
    hidden_in,
    cotangent,
    prompt_start,
    cont_gap,
    seg_len,
    dilation_rate,
    pre_gain,
    pre_bias,
    query_weight,
    query_bias,
    key_weight,
    value_weight,
    value_bias,
    sub_gain,
    sub_bias,
    out_weight,
    out_bias,
    mid_gain,
    mid_bias,
    inner_weight,
    inner_bias,
    ffn_gain,
    ffn_bias,
    outer_weight,
    outer_bias,
):
    device = lax.axis_index("dp")
    ranks = lax.axis_size("dp")
    group_id = device // GDEV
    member = device % GDEV
    tensor_id = lax.axis_index("tensor")
    core = device % 2
    width = query_weight.shape[1]
    units = inner_weight.shape[1]
    pairs = width // 128
    rows = hidden_in.shape[0]
    half = rows // 2
    prompt_rows = CHUNK
    cont_count = (rows - prompt_rows) // CONT

    start_at = lax.dynamic_index_in_dim(prompt_start, group_id, 0, keepdims=False)
    gap_row = lax.dynamic_index_in_dim(cont_gap, group_id, 0, keepdims=False)
    own_gaps = lax.dynamic_slice_in_dim(gap_row, member * cont_count, cont_count)
    info = jnp.concatenate(
        [
            jnp.stack([member, start_at]),
            start_at + member * prompt_rows + TILE * jnp.arange(PTILES),
            start_at + PROMPT + own_gaps,
        ]
    ).astype(jnp.int32)
    seg = lax.dynamic_slice_in_dim(seg_len, tensor_id * pairs, pairs, 0)
    rate = lax.dynamic_slice_in_dim(dilation_rate, tensor_id * pairs, pairs, 0)
    head = 2 * (tensor_id * pairs + jnp.arange(pairs))
    tab = jnp.stack(
        [
            1.0 / seg[:, 0].astype(F32),
            1.0 / seg[:, 1].astype(F32),
            rate[:, 1].astype(F32),
            1.0 / rate[:, 1].astype(F32),
            rate[:, 2].astype(F32),
            1.0 / rate[:, 2].astype(F32),
            (head % rate[:, 1]).astype(F32),
            ((head + 1) % rate[:, 1]).astype(F32),
            (head % rate[:, 2]).astype(F32),
            ((head + 1) % rate[:, 2]).astype(F32),
        ],
        axis=1,
    ).reshape(-1)

    inner_other = fetch(inner_weight, core, 1)
    outer_other = fetch(outer_weight, core, 0)
    out_other = fetch(out_weight, core, 0)
    vectors = jnp.concatenate([inner_bias, ffn_gain, ffn_bias, sub_gain, sub_bias])
    vectors_other = flip(vectors, "tensor", 0)
    splits = [units, 2 * units, 3 * units, 3 * units + width]
    ib_o, fg_o, fb_o, sg_o, sb_o = jnp.split(vectors_other, splits)
    both = lambda mine, other: jnp.concatenate([mine, other]).astype(F32)
    inner_bias_f = both(inner_bias, ib_o)
    ffn_gain_f, ffn_bias_f = both(ffn_gain, fg_o), both(ffn_bias, fb_o)
    sub_gain_f, sub_bias_f = both(sub_gain, sg_o), both(sub_bias, sb_o)
    inner_all = jnp.concatenate([inner_weight, inner_other], axis=1)
    outer_all = jnp.concatenate([outer_weight, outer_other], axis=0)
    out_all = jnp.concatenate([out_weight, out_other], axis=0)

    inputs = hidden_in.astype(F32)
    pre_gain_f = pre_gain.astype(F32)
    pre_normed, pre_unit, pre_scale = norm_rows(inputs, pre_gain_f, pre_bias.astype(F32))
    pre_low = pre_normed.astype(BF)
    keys = dense(pre_low, key_weight).astype(BF)
    values = (dense(pre_low, value_weight) + value_bias.astype(F32)).astype(BF)
    own_pair = jnp.stack([keys[:prompt_rows], values[:prompt_rows]])
    far = flip(own_pair, "dp", 1)
    near_own = flip(own_pair, "dp", 0)
    near_far = flip(far, "dp", 0)
    prompt_pair = jnp.concatenate([own_pair, near_own, far, near_far], axis=1)
    queries = ((dense(pre_low, query_weight) + query_bias.astype(F32)) * 0.125).astype(BF)
    attended, weighed, inverse = attend(info, tab, queries, keys, values, prompt_pair[0], prompt_pair[1])

    own_at = tensor_id * half
    other_at = (1 - tensor_id) * half
    att_mine = lax.dynamic_slice_in_dim(attended, own_at, half)
    att_got = flip(lax.dynamic_slice_in_dim(attended, other_at, half), "tensor", 0)
    att_rows = jnp.concatenate([att_mine, att_got], axis=1).astype(F32)
    hidden_rows = lax.dynamic_slice_in_dim(hidden_in, own_at, half).astype(F32)
    cot_rows = lax.dynamic_slice_in_dim(cotangent, own_at, half)

    sub_normed, sub_unit, sub_scale = norm_rows(att_rows, sub_gain_f, sub_bias_f)
    sub_low = sub_normed.astype(BF)
    mixed = hidden_rows + (dense(sub_low, out_all) + out_bias.astype(F32))
    mid_gain_f = mid_gain.astype(F32)
    mid_normed, mid_unit, mid_scale = norm_rows(mixed, mid_gain_f, mid_bias.astype(F32))
    mid_low = mid_normed.astype(BF)
    inner = dense(mid_low, inner_all) + inner_bias_f
    activated = exact_gelu(inner)
    ffn_normed, ffn_unit, ffn_scale = norm_rows(activated, ffn_gain_f, ffn_bias_f)
    ffn_low = ffn_normed.astype(BF)
    outer = dense(ffn_low, outer_all)
    out_half = (mixed + (outer + outer_bias.astype(F32))).astype(BF)

    grad_result = cot_rows.astype(F32)
    outer_bias_grad = jnp.sum(grad_result, axis=0)
    outer_t_grad = contract_rows(cot_rows, ffn_low)
    grad_ffn = back_project(cot_rows, outer_all)
    ffn_gain_grad = jnp.sum(grad_ffn * ffn_unit, axis=0)
    ffn_bias_grad = jnp.sum(grad_ffn, axis=0)
    grad_activated = norm_back(grad_ffn, ffn_gain_f, ffn_unit, ffn_scale)
    _, gelu_back = jax.vjp(exact_gelu, inner)
    grad_inner = gelu_back(grad_activated)[0].astype(BF)
    inner_bias_grad = jnp.sum(grad_inner.astype(F32), axis=0)
    inner_grad = contract_rows(mid_low, grad_inner)
    grad_mid = back_project(grad_inner, inner_all)
    mid_gain_grad = jnp.sum(grad_mid * mid_unit, axis=0)
    mid_bias_grad = jnp.sum(grad_mid, axis=0)
    grad_mixed = grad_result + norm_back(grad_mid, mid_gain_f, mid_unit, mid_scale)
    grad_branch = grad_mixed.astype(BF)
    out_bias_grad = jnp.sum(grad_branch.astype(F32), axis=0)
    out_t_grad = contract_rows(grad_branch, sub_low)
    grad_sub = back_project(grad_branch, out_all)
    sub_gain_grad = jnp.sum(grad_sub * sub_unit, axis=0)
    sub_bias_grad = jnp.sum(grad_sub, axis=0)
    grad_att = norm_back(grad_sub, sub_gain_f, sub_unit, sub_scale).astype(BF)

    grad_mine = grad_att[:, :width]
    grad_got = flip(grad_att[:, width:], "tensor", 0)
    grad_attended = in_order(tensor_id, grad_mine, grad_got, 0)

    def columns(vector):
        per = vector.shape[0] // ranks
        block = D // ranks
        count = -(-per // block)
        padded = jnp.pad(vector.reshape(ranks, per), ((0, 0), (0, count * block - per)))
        return padded.reshape(ranks, count, block).swapaxes(1, 2).reshape(D, count)

    def vector_of(cols, per):
        return cols.T.reshape(-1)[:per]

    shared = [out_bias_grad, mid_gain_grad, mid_bias_grad, outer_bias_grad]

    def pack(at, at_w):
        parts = [inner_grad[:, at : at + units], outer_t_grad[:, at : at + units], out_t_grad[:, at_w : at_w + width]]
        small = [v[at : at + units] for v in (ffn_gain_grad, ffn_bias_grad, inner_bias_grad)]
        small = small + [v[at_w : at_w + width] for v in (sub_gain_grad, sub_bias_grad)] + shared
        cols = [columns(v) for v in small]
        used = sum(c.shape[1] for c in cols)
        fill = -(-used // 128) * 128 - used
        return jnp.concatenate([p.astype(BF) for p in parts + cols] + [jnp.zeros((D, fill), BF)], axis=1)

    early = lax.psum_scatter(
        jnp.concatenate([pack(0, 0), pack(units, width)], axis=1), "dp", scatter_dimension=0, tiled=True
    )
    early_mine, early_other = jnp.split(early, 2, axis=1)
    early_sum = early_mine.astype(F32) + flip(early_other, "tensor", 0).astype(F32)
    big = 2 * units + width
    inner_weight_grad = early_sum[:, :units]
    outer_weight_grad = early_sum[:, units : 2 * units].T
    out_weight_grad = early_sum[:, 2 * units : big].T
    tail = early_sum[:, big:]
    block = D // ranks
    per_u, per_w = units // ranks, width // ranks
    cu, cw = -(-per_u // block), -(-per_w // block)
    ffn_gain_grad = vector_of(tail[:, 0:cu], per_u)
    ffn_bias_grad = vector_of(tail[:, cu : 2 * cu], per_u)
    inner_bias_grad = vector_of(tail[:, 2 * cu : 3 * cu], per_u)
    sub_gain_grad = vector_of(tail[:, 3 * cu : 3 * cu + cw], per_w)
    sub_bias_grad = vector_of(tail[:, 3 * cu + cw : 3 * cu + 2 * cw], per_w)
    out_bias_grad, mid_gain_grad, mid_bias_grad, outer_bias_grad = [
        tail[:, 3 * cu + 2 * cw + i] for i in range(4)
    ]

    output = in_order(tensor_id, out_half, flip(out_half, "tensor", 0), 0)

    grad_query_in, key_acc, value_acc, own_key_grad, own_value_grad = attend_back(
        info, queries, keys, values, prompt_pair[0], prompt_pair[1], attended, inverse, grad_attended, weighed
    )
    acc = jnp.stack([key_acc, value_acc]).reshape(2, GDEV, prompt_rows, width)
    near = acc[:, 0::2].astype(F32) + flip(acc[:, 1::2], "dp", 0).astype(F32)
    summed = (near[:, 0] + flip(near[:, 1].astype(BF), "dp", 1).astype(F32)).astype(BF)
    grad_keys = jnp.concatenate([summed[0], own_key_grad[prompt_rows:]], axis=0)
    grad_values = jnp.concatenate([summed[1], own_value_grad[prompt_rows:]], axis=0)

    query_weight_grad = contract_rows(pre_low, grad_query_in)
    key_weight_grad = contract_rows(pre_low, grad_keys)
    value_weight_grad = contract_rows(pre_low, grad_values)
    query_bias_grad = jnp.sum(grad_query_in.astype(F32), axis=0)
    value_bias_grad = jnp.sum(grad_values.astype(F32), axis=0)
    grad_normed_part = (
        back_project(grad_query_in, query_weight)
        + back_project(grad_keys, key_weight)
        + back_project(grad_values, value_weight)
    )
    grad_normed_low = grad_normed_part.astype(BF)
    grad_normed = grad_normed_low.astype(F32) + flip(grad_normed_low, "tensor", 0).astype(F32)
    pre_gain_grad = jnp.sum(grad_normed * pre_unit, axis=0)
    pre_bias_grad = jnp.sum(grad_normed, axis=0)
    grad_mixed_low = grad_mixed.astype(BF)
    grad_mixed_all = in_order(tensor_id, grad_mixed_low, flip(grad_mixed_low, "tensor", 0), 0).astype(F32)
    input_low = (grad_mixed_all + norm_back(grad_normed, pre_gain_f, pre_unit, pre_scale)).astype(BF)

    cols = [columns(v) for v in (query_bias_grad, value_bias_grad, pre_gain_grad, pre_bias_grad)]
    used = sum(c.shape[1] for c in cols)
    fill = -(-used // 128) * 128 - used
    late = halving(
        jnp.concatenate(
            [p.astype(BF) for p in [query_weight_grad, key_weight_grad, value_weight_grad] + cols]
            + [jnp.zeros((D, fill), BF)],
            axis=1,
        ),
        device,
    ).astype(F32)
    tail = late[:, 3 * width :]
    return (
        output,
        input_low,
        tail[:, 2 * cw],
        tail[:, 2 * cw + 1],
        late[:, :width],
        vector_of(tail[:, 0:cw], per_w),
        late[:, width : 2 * width],
        late[:, 2 * width : 3 * width],
        vector_of(tail[:, cw : 2 * cw], per_w),
        sub_gain_grad,
        sub_bias_grad,
        out_weight_grad,
        out_bias_grad,
        mid_gain_grad,
        mid_bias_grad,
        inner_weight_grad,
        inner_bias_grad,
        ffn_gain_grad,
        ffn_bias_grad,
        outer_weight_grad,
        outer_bias_grad,
    )


def solution(mesh):
    placed = (
        P("dp", None),
        P("dp", None),
        P(),
        P(),
        P(),
        P(),
        P(),
        P(),
        P(None, "tensor"),
        P("tensor"),
        P(None, "tensor"),
        P(None, "tensor"),
        P("tensor"),
        P("tensor"),
        P("tensor"),
        P("tensor", None),
        P(),
        P(),
        P(),
        P(None, "tensor"),
        P("tensor"),
        P("tensor"),
        P("tensor"),
        P("tensor", None),
        P(),
    )
    return jax.shard_map(
        body,
        mesh=mesh,
        in_specs=placed,
        out_specs=(
            P("dp", None),
            P("dp", None),
            P("dp"),
            P("dp"),
            P("dp", "tensor"),
            P(("tensor", "dp")),
            P("dp", "tensor"),
            P("dp", "tensor"),
            P(("tensor", "dp")),
            P(("tensor", "dp")),
            P(("tensor", "dp")),
            P("tensor", "dp"),
            P("dp"),
            P("dp"),
            P("dp"),
            P("dp", "tensor"),
            P(("tensor", "dp")),
            P(("tensor", "dp")),
            P(("tensor", "dp")),
            P("tensor", "dp"),
            P("dp"),
        ),
        check_vma=False,
    )
```

```python
import jax
import jax.numpy as jnp
from jax import lax
from jax.experimental import pallas as pl
from jax.experimental.pallas import tpu as pltpu
from jax.sharding import PartitionSpec as P

HD = 64
PROMPT = 2048
CONT = 256
GDEV = 4
TILE = 256
CHUNK = PROMPT // GDEV
PTILES = CHUNK // TILE
LOG2E = 1.4426950408889634
BF = jnp.bfloat16
F32 = jnp.float32
TAB = 10


def dot_nt(a, b):
    return lax.dot_general(a, b, (((1,), (1,)), ((), ())), preferred_element_type=F32)


def dot_nn(a, b):
    return lax.dot_general(a, b, (((1,), (0,)), ((), ())), preferred_element_type=F32)


def low_half(rows):
    return lax.broadcasted_iota(jnp.int32, (rows, 128), 1) < HD


def codes(at, tab, pair, miss):
    def cell(i):
        return tab[pair * TAB + i]

    first = jnp.floor((at + 0.5) * cell(0))
    second = jnp.floor((at + 0.5) * cell(1))
    rest1 = at - cell(2) * jnp.floor((at + 0.5) * cell(3))
    rest2 = at - cell(4) * jnp.floor((at + 0.5) * cell(5))
    return [
        first,
        jnp.where(rest1 == cell(6), second, miss),
        jnp.where(rest1 == cell(7), second, miss),
        jnp.where(rest2 == cell(8), 1.0, 0.0),
        jnp.where(rest2 == cell(9), 1.0, 0.0),
    ]


def fwd_kernel(info, tab, q_ref, kp_ref, vp_ref, ko_ref, vo_ref, o_ref, e_ref, li_ref, t_s, kc_s):
    pair = pl.program_id(0)
    step = pl.program_id(1)
    member = info[0]
    low = low_half(TILE)
    q = q_ref[...]
    zero = jnp.zeros_like(q)
    qs = [jnp.where(low, q, zero), jnp.where(low, zero, q)]
    row = lax.broadcasted_iota(jnp.int32, (TILE, 128), 0).astype(F32)
    at_q = info[2 + step].astype(F32) + row
    qc = codes(at_q, tab, pair, -2.0)

    @pl.when(step == 0)
    def _():
        at_k = info[1].astype(F32) + lax.broadcasted_iota(jnp.int32, (8, PROMPT), 1).astype(F32)
        for i, c in enumerate(codes(at_k, tab, pair, -1.0)):
            kc_s[i] = c

    def logits(mx, keys, kc, causal, at, width):
        out = []
        for h in range(2):
            s = dot_nt(qs[h], keys)
            top = mx[h]
            for g in range(width // 128):
                lanes = slice(g * 128, (g + 1) * 128)
                w = jnp.where(qc[0] == kc[0][:, lanes], 1.0, 0.0)
                w = w + jnp.where(qc[1 + h] == kc[1 + h][:, lanes], 1.0, 0.0)
                w = w + qc[3 + h] * kc[3 + h][:, lanes]
                if causal is not None:
                    w = jnp.where(causal[:, lanes], w, 0.0)
                t = s[:, lanes] * LOG2E + jnp.log2(w)
                t_s[h, :, pl.ds(at + g * 128, 128)] = t
                top = jnp.maximum(top, t)
            out.append(top)
        return tuple(out)

    def weigh(carry, vals, m, at, width):
        sums, accs = carry
        ns, na = [], []
        for h in range(2):
            total = sums[h]
            parts = []
            for g in range(width // 128):
                e = jnp.exp2(t_s[h, :, pl.ds(at + g * 128, 128)] - m[h])
                total = total + e
                parts.append(e.astype(BF))
            el = jnp.concatenate(parts, axis=1)
            e_ref[h, :, pl.ds(at, width)] = el
            ns.append(total)
            na.append(accs[h] + dot_nn(el, vals))
        return (tuple(ns), tuple(na))

    def finish(carry):
        sums, accs = carry
        li = [1.0 / jnp.sum(s, axis=1, keepdims=True) for s in sums]
        lfull = jnp.where(low, li[0], li[1])
        li_ref[...] = lfull
        o_ref[...] = (jnp.where(low, accs[0], accs[1]) * lfull).astype(BF)

    def tops(mx):
        return [jnp.broadcast_to(jnp.max(x, axis=1, keepdims=True), (TILE, 128)) for x in mx]

    neg = jnp.full((TILE, 128), -jnp.inf, F32)
    zf = jnp.zeros((TILE, 128), F32)

    def key_codes(at, width):
        return [kc_s[i, 0:1, pl.ds(at, width)] for i in range(5)]

    @pl.when(step < PTILES)
    def _():
        def one(j, mx):
            at = pl.multiple_of(j * CHUNK, CHUNK)
            held = pl.multiple_of((j ^ member) * CHUNK, CHUNK)
            return logits(mx, kp_ref[pl.ds(held, CHUNK), :], key_codes(at, CHUNK), None, held, CHUNK)

        mx = lax.fori_loop(0, member, one, (neg, neg))
        at = pl.multiple_of(member * CHUNK, CHUNK)
        rows = lax.broadcasted_iota(jnp.int32, (TILE, CHUNK), 0) + step * TILE
        cols = lax.broadcasted_iota(jnp.int32, (TILE, CHUNK), 1)
        mx = logits(mx, kp_ref[0:CHUNK, :], key_codes(at, CHUNK), cols <= rows, 0, CHUNK)
        m = tops(mx)

        def two(j, carry):
            held = pl.multiple_of((j ^ member) * CHUNK, CHUNK)
            return weigh(carry, vp_ref[pl.ds(held, CHUNK), :], m, held, CHUNK)

        finish(lax.fori_loop(0, member + 1, two, ((zf, zf), (zf, zf))))

    @pl.when(step >= PTILES)
    def _():
        mx = (neg, neg)
        for j in range(GDEV):
            at = pl.multiple_of((j ^ member) * CHUNK, CHUNK)
            mx = logits(mx, kp_ref[j * CHUNK : (j + 1) * CHUNK, :], key_codes(at, CHUNK), None, j * CHUNK, CHUNK)
        rows = lax.broadcasted_iota(jnp.int32, (TILE, CONT), 0)
        cols = lax.broadcasted_iota(jnp.int32, (TILE, CONT), 1)
        at_k = info[2 + step].astype(F32) + lax.broadcasted_iota(jnp.int32, (8, CONT), 1).astype(F32)
        own = [c[0:1] for c in codes(at_k, tab, pair, -1.0)]
        mx = logits(mx, ko_ref[...], own, cols <= rows, PROMPT, CONT)
        m = tops(mx)
        carry = ((zf, zf), (zf, zf))
        for j in range(GDEV):
            carry = weigh(carry, vp_ref[j * CHUNK : (j + 1) * CHUNK, :], m, j * CHUNK, CHUNK)
        finish(weigh(carry, vo_ref[...], m, PROMPT, CONT))


def attend(info, tab, q, k, v, kp, vp):
    rows, width = q.shape
    pairs = width // 128
    span = PROMPT + CONT
    tile = pl.BlockSpec((TILE, 128), lambda a, t, s, f: (t, a))
    whole = pl.BlockSpec((PROMPT, 128), lambda a, t, s, f: (0, a))
    return pl.pallas_call(
        fwd_kernel,
        grid_spec=pltpu.PrefetchScalarGridSpec(
            num_scalar_prefetch=2,
            grid=(pairs, rows // TILE),
            in_specs=[tile, whole, whole, tile, tile],
            out_specs=[tile, pl.BlockSpec((2, TILE, span), lambda a, t, s, f: (a, t, 0)), tile],
            scratch_shapes=[pltpu.VMEM((2, TILE, span), F32), pltpu.VMEM((5, 8, PROMPT), F32)],
        ),
        out_shape=[
            jax.ShapeDtypeStruct((rows, width), BF),
            jax.ShapeDtypeStruct((2 * pairs, rows, span), BF),
            jax.ShapeDtypeStruct((rows, width), F32),
        ],
        compiler_params=pltpu.CompilerParams(vmem_limit_bytes=48 << 20),
        cost_estimate=pl.CostEstimate(flops=16 * 10**9, bytes_accessed=60 * 10**6, transcendentals=0),
        name="attend",
    )(info, tab, q, kp, vp, k, v)


def bwd_kernel(info, q_ref, kp_ref, vp_ref, ko_ref, vo_ref, o_ref, li_ref, g_ref, e_ref, dq_ref, dk_ref, dv_ref, dko_ref, dvo_ref, dk_s, dv_s):
    step = pl.program_id(1)
    member = info[0]
    low = low_half(TILE)
    g = g_ref[...].astype(F32) * li_ref[...]
    prod = g * o_ref[...].astype(F32)
    zf = jnp.zeros((TILE, 128), F32)
    deltas = [
        jnp.sum(jnp.where(low, prod, zf), axis=1, keepdims=True),
        jnp.sum(jnp.where(low, zf, prod), axis=1, keepdims=True),
    ]
    gs = [jnp.where(low, g, zf).astype(BF), jnp.where(low, zf, g).astype(BF)]
    gt = jnp.transpose(g).astype(BF)
    qt = jnp.transpose(q_ref[...].astype(F32)).astype(BF)

    def grads(dq, keys, vals, at, width):
        out, dks, dvs = [], [], []
        for h in range(2):
            e = e_ref[h, :, pl.ds(at, width)]
            dp = dot_nt(gs[h], vals)
            ds = (e.astype(F32) * (dp - deltas[h])).astype(BF)
            out.append(dq[h] + dot_nn(ds, keys))
            dks.append(dot_nn(qt[h * HD : (h + 1) * HD, :], ds))
            dvs.append(dot_nn(gt[h * HD : (h + 1) * HD, :], e))
        return tuple(out), dks, dvs

    @pl.when(step == 0)
    def _():
        dk_s[...] = jnp.zeros_like(dk_s)
        dv_s[...] = jnp.zeros_like(dv_s)

    def add(at, width, dks, dvs):
        for h in range(2):
            dk_s[h * HD : (h + 1) * HD, pl.ds(at, width)] += dks[h]
            dv_s[h * HD : (h + 1) * HD, pl.ds(at, width)] += dvs[h]

    def scaled(dq):
        return (jnp.where(low, dq[0], dq[1]).astype(BF).astype(F32) * 0.125).astype(BF)

    @pl.when(step < PTILES)
    def _():
        def one(j, dq):
            at = pl.multiple_of((j ^ member) * CHUNK, CHUNK)
            dq, dks, dvs = grads(dq, kp_ref[pl.ds(at, CHUNK), :], vp_ref[pl.ds(at, CHUNK), :], at, CHUNK)
            add(at, CHUNK, dks, dvs)
            return dq

        dq_ref[...] = scaled(lax.fori_loop(0, member + 1, one, (zf, zf)))
        dko_ref[...] = jnp.zeros_like(dko_ref)
        dvo_ref[...] = jnp.zeros_like(dvo_ref)

    @pl.when(step >= PTILES)
    def _():
        dq = (zf, zf)
        for j in range(GDEV):
            span = slice(j * CHUNK, (j + 1) * CHUNK)
            dq, dks, dvs = grads(dq, kp_ref[span, :], vp_ref[span, :], j * CHUNK, CHUNK)
            add(j * CHUNK, CHUNK, dks, dvs)
        dq, dks, dvs = grads(dq, ko_ref[...], vo_ref[...], PROMPT, CONT)
        dq_ref[...] = scaled(dq)
        dko_ref[...] = jnp.transpose(jnp.concatenate(dks, axis=0)).astype(BF)
        dvo_ref[...] = jnp.transpose(jnp.concatenate(dvs, axis=0)).astype(BF)

    @pl.when(step == pl.num_programs(1) - 1)
    def _():
        for j in range(GDEV):
            span = slice(j * CHUNK, (j + 1) * CHUNK)
            dk_ref[span, :] = jnp.transpose(dk_s[:, span]).astype(BF)
            dv_ref[span, :] = jnp.transpose(dv_s[:, span]).astype(BF)


def attend_back(info, q, k, v, kp, vp, o, li, g, e):
    rows, width = q.shape
    pairs = width // 128
    span = PROMPT + CONT
    tile = pl.BlockSpec((TILE, 128), lambda a, t, s: (t, a))
    whole = pl.BlockSpec((PROMPT, 128), lambda a, t, s: (0, a))
    return pl.pallas_call(
        bwd_kernel,
        grid_spec=pltpu.PrefetchScalarGridSpec(
            num_scalar_prefetch=1,
            grid=(pairs, rows // TILE),
            in_specs=[tile, whole, whole, tile, tile, tile, tile, tile, pl.BlockSpec((2, TILE, span), lambda a, t, s: (a, t, 0))],
            out_specs=[tile, whole, whole, tile, tile],
            scratch_shapes=[pltpu.VMEM((128, PROMPT), F32), pltpu.VMEM((128, PROMPT), F32)],
        ),
        out_shape=[
            jax.ShapeDtypeStruct((rows, width), BF),
            jax.ShapeDtypeStruct((PROMPT, width), BF),
            jax.ShapeDtypeStruct((PROMPT, width), BF),
            jax.ShapeDtypeStruct((rows, width), BF),
            jax.ShapeDtypeStruct((rows, width), BF),
        ],
        compiler_params=pltpu.CompilerParams(vmem_limit_bytes=48 << 20),
        cost_estimate=pl.CostEstimate(flops=30 * 10**9, bytes_accessed=60 * 10**6, transcendentals=0),
        name="attend_back",
    )(info, q, kp, vp, k, v, o, li, g, e)


EPSILON = 1e-05
D = 768
UCH = 512


def polynomial(x, terms):
    out = jnp.full_like(x, terms[0])
    for term in terms[1:]:
        out = out * x + term
    return out


def error_function(x):
    x = jnp.clip(x, -3.832506856900711, 3.832506856900711)
    square = x * x
    top = polynomial(
        square,
        (0.00022905065861350646, 0.0034082910107109506, 0.050955695062380861, 0.18520832239976145, 1.128379143519084),
    )
    bottom = polynomial(
        square,
        (
            -1.1791602954361697e-7,
            0.000023547966471313185,
            0.0010179625278914885,
            0.014070470171167667,
            0.11098505178285362,
            0.49746925110067538,
            1.0,
        ),
    )
    return x * top / bottom


def gelu_pair(v):
    phi = 0.5 + 0.5 * error_function(v * 0.7071067811865476)
    density = jnp.exp(-0.5 * v * v) * 0.3989422804014327
    return v * phi, phi + v * density


def column_sum(x):
    return jnp.sum(x, axis=0, keepdims=True)


def mid_kernel(
    info, att_m, att_o, hid, cot, vec_u, vec_w, vec_d, w1_own, w1_got, w1_swap, w2_own, w2_got, w2_swap, wo_own, wo_got, wo_swap,
    out_ref, gatt_m, gatt_o, gmix_ref, packed, su_ref, sw_ref, sd_ref,
    w1, w2, wo, act_s, shp_s, dg_s, wide_s, acc_s, gmid_s, sub_s, mid_s, low_s, midt_s, cott_s, stage, sems, out_sems,
):
    core = info[0]
    units = w1_own.shape[1]
    width = wo_own.shape[0]
    rows = hid.shape[0]
    full = 2 * units
    half = units // 2
    half_w = width // 2
    here_u = pl.multiple_of(units + core * half, 128)
    there_u = pl.multiple_of(units + (1 - core) * half, 128)
    here_w = pl.multiple_of(width + core * half_w, 64)
    there_w = pl.multiple_of(width + (1 - core) * half_w, 64)
    loads = []
    for i, (src, dst) in enumerate(
        [
            (wo_own, wo.at[pl.ds(0, width), :]),
            (wo_got, wo.at[pl.ds(here_w, half_w), :]),
            (wo_swap, wo.at[pl.ds(there_w, half_w), :]),
            (w1_own, w1.at[:, pl.ds(0, units)]),
            (w1_got, w1.at[:, pl.ds(here_u, half)]),
            (w1_swap, w1.at[:, pl.ds(there_u, half)]),
            (w2_own, w2.at[pl.ds(0, units), :]),
            (w2_got, w2.at[pl.ds(here_u, half), :]),
            (w2_swap, w2.at[pl.ds(there_u, half), :]),
        ]
    ):
        copy = pltpu.make_async_copy(src, dst, sems.at[i])
        copy.start()
        loads.append(copy)

    a0 = att_m[...].astype(F32)
    a1 = att_o[...].astype(F32)
    center = (jnp.sum(a0, axis=1, keepdims=True) + jnp.sum(a1, axis=1, keepdims=True)) * (1.0 / D)
    square = (jnp.sum(a0 * a0, axis=1, keepdims=True) + jnp.sum(a1 * a1, axis=1, keepdims=True)) * (1.0 / D)
    sub_scale = lax.rsqrt(square - center * center + EPSILON)
    sub_s[:, 0:width] = (a0 - center) * sub_scale
    sub_s[:, width : 2 * width] = (a1 - center) * sub_scale
    sub_gain = vec_w[0:1, :]
    low_s[...] = (sub_s[...] * sub_gain + vec_w[1:2, :]).astype(BF)
    for copy in loads[0:3]:
        copy.wait()
    mixed = hid[...].astype(F32) + (dot_nn(low_s[...], wo[...]) + vec_d[0:1, :])
    wide_s[...] = mixed
    mean = jnp.mean(mixed, axis=1, keepdims=True)
    mid_scale = lax.rsqrt(jnp.mean(mixed * mixed, axis=1, keepdims=True) - mean * mean + EPSILON)
    mid_s[...] = (mixed - mean) * mid_scale
    mid_gain = vec_d[1:2, :]
    mid_full = mid_s[...] * mid_gain + vec_d[2:3, :]
    mid_low = mid_full.astype(BF)
    midt_s[...] = jnp.transpose(mid_full).astype(BF)
    cot_full = cot[...].astype(F32)
    cott_s[...] = jnp.transpose(cot_full).astype(BF)
    sd_ref[...] = jnp.zeros_like(sd_ref)
    sd_ref[3:4, :] = column_sum(cot_full)
    for copy in loads[3:6]:
        copy.wait()

    def lanes_sum(x):
        total = x[:, 0:128]
        for i in range(1, x.shape[1] // 128):
            total = total + x[:, i * 128 : (i + 1) * 128]
        return total

    def first(c, carry):
        at = pl.multiple_of(c * UCH, UCH)
        inner = dot_nn(mid_low, w1[:, pl.ds(at, UCH)]) + vec_u[2:3, pl.ds(at, UCH)]
        act, slope = gelu_pair(inner)
        act_s[:, pl.ds(at, UCH)] = act
        dg_s[:, pl.ds(at, UCH)] = slope.astype(BF)
        return carry[0] + lanes_sum(act), carry[1] + lanes_sum(act * act)

    zero = jnp.zeros((rows, 128), F32)
    act_sum, act_square = lax.fori_loop(0, full // UCH, first, (zero, zero))
    ffn_center = jnp.sum(act_sum, axis=1, keepdims=True) * (1.0 / full)
    ffn_scale = lax.rsqrt(
        jnp.sum(act_square, axis=1, keepdims=True) * (1.0 / full) - ffn_center * ffn_center + EPSILON
    )
    for copy in loads[6:9]:
        copy.wait()
    acc_s[...] = jnp.zeros_like(acc_s)
    per = units // UCH
    wide = 2 * units + width

    def column_of(c, extra):
        return pl.multiple_of((c // per) * wide + lax.rem(c, per) * UCH + extra, 128)

    def send(slot, column):
        return pltpu.make_async_copy(stage.at[slot], packed.at[:, pl.ds(column, UCH)], out_sems.at[slot])

    def put(c, value, extra):
        slot = lax.rem(c, 2)

        @pl.when(c >= 2)
        def _():
            send(slot, column_of(c - 2, extra)).wait()

        stage[slot] = value
        send(slot, column_of(c, extra)).start()

    def drain(extra):
        for c in range(full // UCH - 2, full // UCH):
            send(c % 2, column_of(c, extra)).wait()

    def second(c, carry):
        at = pl.multiple_of(c * UCH, UCH)
        unit = (act_s[:, pl.ds(at, UCH)] - ffn_center) * ffn_scale
        act_s[:, pl.ds(at, UCH)] = unit
        gain = vec_u[0:1, pl.ds(at, UCH)]
        low = (unit * gain + vec_u[1:2, pl.ds(at, UCH)]).astype(BF)
        acc_s[...] += dot_nn(low, w2[pl.ds(at, UCH), :])
        grad = dot_nt(cot[...], w2[pl.ds(at, UCH), :])
        cross = grad * unit
        su_ref[0:1, pl.ds(at, UCH)] = column_sum(cross)
        su_ref[1:2, pl.ds(at, UCH)] = column_sum(grad)
        shaped = grad * gain
        shp_s[:, pl.ds(at, UCH)] = shaped
        put(c, dot_nn(cott_s[...], low).astype(BF), units)
        return carry[0] + lanes_sum(shaped), carry[1] + lanes_sum(shaped * unit)

    su_ref[...] = jnp.zeros_like(su_ref)
    s_sum, s_cross = lax.fori_loop(0, full // UCH, second, (zero, zero))
    drain(units)
    shaped_mean = jnp.sum(s_sum, axis=1, keepdims=True) * (1.0 / full)
    cross_mean = jnp.sum(s_cross, axis=1, keepdims=True) * (1.0 / full)
    out_ref[...] = (wide_s[...] + (acc_s[...] + vec_d[3:4, :])).astype(BF)
    gmid_s[...] = jnp.zeros_like(gmid_s)

    def third(c, carry):
        at = pl.multiple_of(c * UCH, UCH)
        g = ffn_scale * (shp_s[:, pl.ds(at, UCH)] - shaped_mean - act_s[:, pl.ds(at, UCH)] * cross_mean)
        low = (g * dg_s[:, pl.ds(at, UCH)].astype(F32)).astype(BF)
        su_ref[2:3, pl.ds(at, UCH)] = column_sum(low.astype(F32))
        gmid_s[...] += dot_nt(low, w1[:, pl.ds(at, UCH)])
        put(c, dot_nn(midt_s[...], low).astype(BF), 0)
        return carry

    lax.fori_loop(0, full // UCH, third, 0)
    drain(0)

    grad_mid = gmid_s[...]
    unit = mid_s[...]
    sd_ref[1:2, :] = column_sum(grad_mid * unit)
    sd_ref[2:3, :] = column_sum(grad_mid)
    shaped = grad_mid * mid_gain
    grad_mixed = cot[...].astype(F32) + mid_scale * (
        shaped - jnp.mean(shaped, axis=1, keepdims=True) - unit * jnp.mean(shaped * unit, axis=1, keepdims=True)
    )
    branch = grad_mixed.astype(BF)
    gmix_ref[...] = branch
    branch_f = branch.astype(F32)
    sd_ref[0:1, :] = column_sum(branch_f)
    out_grad = dot_nn(jnp.transpose(branch_f).astype(BF), low_s[...]).astype(BF)
    stage[0, :, 0:width] = out_grad[:, 0:width]
    stage[1, :, 0:width] = out_grad[:, width : 2 * width]
    last = [
        pltpu.make_async_copy(stage.at[i, :, pl.ds(0, width)], packed.at[:, pl.ds(i * wide + 2 * units, width)], out_sems.at[i])
        for i in range(2)
    ]
    for copy in last:
        copy.start()
    grad_sub = dot_nt(branch, wo[...])
    unit = sub_s[...]
    cross = grad_sub * unit
    sw_ref[...] = jnp.zeros_like(sw_ref)
    sw_ref[0:1, :] = column_sum(cross)
    sw_ref[1:2, :] = column_sum(grad_sub)
    shaped = grad_sub * sub_gain
    grad_att = sub_scale * (
        shaped - jnp.mean(shaped, axis=1, keepdims=True) - unit * jnp.mean(shaped * unit, axis=1, keepdims=True)
    )
    gatt_m[...] = grad_att[:, 0:width].astype(BF)
    gatt_o[...] = grad_att[:, width : 2 * width].astype(BF)
    for copy in last:
        copy.wait()


def middle(core, att_m, att_o, hid, cot, vec_u, vec_w, vec_d, w1, w2, wo):
    rows = hid.shape[0]
    units = w1[0].shape[1]
    width = wo[0].shape[0]
    vmem = pl.BlockSpec(memory_space=pltpu.VMEM)
    hbm = pl.BlockSpec(memory_space=pl.ANY)
    shape = jax.ShapeDtypeStruct
    return pl.pallas_call(
        mid_kernel,
        in_specs=[pl.BlockSpec(memory_space=pltpu.SMEM)] + [vmem] * 7 + [hbm] * 9,
        out_specs=[vmem] * 4 + [hbm] + [vmem] * 3,
        out_shape=[
            shape((rows, D), BF),
            shape((rows, width), BF),
            shape((rows, width), BF),
            shape((rows, D), BF),
            shape((D, 2 * (2 * units + width)), BF),
            shape((8, 2 * units), F32),
            shape((8, 2 * width), F32),
            shape((8, D), F32),
        ],
        scratch_shapes=[
            pltpu.VMEM((D, 2 * units), BF),
            pltpu.VMEM((2 * units, D), BF),
            pltpu.VMEM((2 * width, D), BF),
            pltpu.VMEM((rows, 2 * units), F32),
            pltpu.VMEM((rows, 2 * units), F32),
            pltpu.VMEM((rows, 2 * units), BF),
            pltpu.VMEM((rows, D), F32),
            pltpu.VMEM((rows, D), F32),
            pltpu.VMEM((rows, D), F32),
            pltpu.VMEM((rows, 2 * width), F32),
            pltpu.VMEM((rows, D), F32),
            pltpu.VMEM((rows, 2 * width), BF),
            pltpu.VMEM((D, rows), BF),
            pltpu.VMEM((D, rows), BF),
            pltpu.VMEM((2, D, UCH), BF),
            pltpu.SemaphoreType.DMA((9,)),
            pltpu.SemaphoreType.DMA((2,)),
        ],
        compiler_params=pltpu.CompilerParams(vmem_limit_bytes=62 << 20),
        cost_estimate=pl.CostEstimate(flops=21 * 10**9, bytes_accessed=30 * 10**6, transcendentals=0),
        name="middle",
    )(core, att_m, att_o, hid, cot, vec_u, vec_w, vec_d, *w1, *w2, *wo)


def flip(value, axis, bit):
    return lax.ppermute(value, axis, [(i, i ^ (1 << bit)) for i in range(lax.axis_size(axis))])


def contract_rows(left, right):
    return lax.dot_general(left, right, (((0,), (0,)), ((), ())), preferred_element_type=F32)


def back_project(left, right):
    return lax.dot_general(left, right, (((1,), (1,)), ((), ())), preferred_element_type=F32)


def dense(left, right):
    return jnp.dot(left, right, preferred_element_type=F32)


def norm_rows(values, gain, bias):
    center = jnp.mean(values, axis=-1, keepdims=True)
    spread = jnp.mean(values * values, axis=-1, keepdims=True) - center * center
    scaled = lax.rsqrt(spread + EPSILON)
    unit_rows = (values - center) * scaled
    return (unit_rows * gain + bias, unit_rows, scaled)


def norm_back(grad_rows, gain, unit_rows, scaled):
    shaped = grad_rows * gain
    return scaled * (
        shaped
        - jnp.mean(shaped, axis=-1, keepdims=True)
        - unit_rows * jnp.mean(shaped * unit_rows, axis=-1, keepdims=True)
    )


def in_order(which, mine, other, axis):
    return jnp.where(
        which == 0,
        jnp.concatenate([mine, other], axis=axis),
        jnp.concatenate([other, mine], axis=axis),
    )


def fetch(weight, core, axis):
    half = weight.shape[axis] // 2
    got = flip(lax.dynamic_slice_in_dim(weight, core * half, half, axis), "tensor", 0)
    return (got, flip(got, "dp", 0))


def halving(value, device):
    bits = lax.axis_size("dp").bit_length() - 1
    rows, columns = value.shape
    current = value
    for bit in range(bits):
        upper = device // (1 << bit) % 2
        left = bits - bit
        view = current.reshape((1 << (left - 1), 2, -1, columns))
        kept = lax.dynamic_index_in_dim(view, upper, 1, keepdims=False)
        sent = lax.dynamic_index_in_dim(view, 1 - upper, 1, keepdims=False)
        got = flip(sent, "dp", bit)
        current = (kept.astype(F32) + got.astype(F32)).astype(BF)
    return current.reshape(rows >> bits, columns)


def body(
    hidden_in,
    cotangent,
    prompt_start,
    cont_gap,
    seg_len,
    dilation_rate,
    pre_gain,
    pre_bias,
    query_weight,
    query_bias,
    key_weight,
    value_weight,
    value_bias,
    sub_gain,
    sub_bias,
    out_weight,
    out_bias,
    mid_gain,
    mid_bias,
    inner_weight,
    inner_bias,
    ffn_gain,
    ffn_bias,
    outer_weight,
    outer_bias,
):
    device = lax.axis_index("dp")
    ranks = lax.axis_size("dp")
    group_id = device // GDEV
    member = device % GDEV
    tensor_id = lax.axis_index("tensor")
    core = device % 2
    width = query_weight.shape[1]
    units = inner_weight.shape[1]
    pairs = width // 128
    rows = hidden_in.shape[0]
    half = rows // 2
    prompt_rows = CHUNK
    cont_count = (rows - prompt_rows) // CONT

    start_at = lax.dynamic_index_in_dim(prompt_start, group_id, 0, keepdims=False)
    gap_row = lax.dynamic_index_in_dim(cont_gap, group_id, 0, keepdims=False)
    own_gaps = lax.dynamic_slice_in_dim(gap_row, member * cont_count, cont_count)
    info = jnp.concatenate(
        [
            jnp.stack([member, start_at]),
            start_at + member * prompt_rows + TILE * jnp.arange(PTILES),
            start_at + PROMPT + own_gaps,
        ]
    ).astype(jnp.int32)
    seg = lax.dynamic_slice_in_dim(seg_len, tensor_id * pairs, pairs, 0)
    rate = lax.dynamic_slice_in_dim(dilation_rate, tensor_id * pairs, pairs, 0)
    head = 2 * (tensor_id * pairs + jnp.arange(pairs))
    tab = jnp.stack(
        [
            1.0 / seg[:, 0].astype(F32),
            1.0 / seg[:, 1].astype(F32),
            rate[:, 1].astype(F32),
            1.0 / rate[:, 1].astype(F32),
            rate[:, 2].astype(F32),
            1.0 / rate[:, 2].astype(F32),
            (head % rate[:, 1]).astype(F32),
            ((head + 1) % rate[:, 1]).astype(F32),
            (head % rate[:, 2]).astype(F32),
            ((head + 1) % rate[:, 2]).astype(F32),
        ],
        axis=1,
    ).reshape(-1)

    inner_parts = (inner_weight,) + fetch(inner_weight, core, 1)
    outer_parts = (outer_weight,) + fetch(outer_weight, core, 0)
    out_parts = (out_weight,) + fetch(out_weight, core, 0)
    vectors = jnp.concatenate([ffn_gain, ffn_bias, inner_bias, sub_gain, sub_bias])
    vectors_other = flip(vectors, "tensor", 0)
    both = jnp.stack([vectors, vectors_other]).astype(F32)
    vec_u = both[:, : 3 * units].reshape(2, 3, units).swapaxes(0, 1).reshape(3, 2 * units)
    vec_w = both[:, 3 * units :].reshape(2, 2, width).swapaxes(0, 1).reshape(2, 2 * width)
    vec_d = jnp.stack([out_bias, mid_gain, mid_bias, outer_bias]).astype(F32)

    inputs = hidden_in.astype(F32)
    pre_gain_f = pre_gain.astype(F32)
    pre_normed, pre_unit, pre_scale = norm_rows(inputs, pre_gain_f, pre_bias.astype(F32))
    pre_low = pre_normed.astype(BF)
    keys = dense(pre_low, key_weight).astype(BF)
    values = (dense(pre_low, value_weight) + value_bias.astype(F32)).astype(BF)
    own_pair = jnp.stack([keys[:prompt_rows], values[:prompt_rows]])
    far = flip(own_pair, "dp", 1)
    near_own = flip(own_pair, "dp", 0)
    near_far = flip(far, "dp", 0)
    prompt_pair = jnp.concatenate([own_pair, near_own, far, near_far], axis=1)
    queries = ((dense(pre_low, query_weight) + query_bias.astype(F32)) * 0.125).astype(BF)
    attended, weighed, inverse = attend(info, tab, queries, keys, values, prompt_pair[0], prompt_pair[1])

    own_at = tensor_id * half
    other_at = (1 - tensor_id) * half
    att_mine = lax.dynamic_slice_in_dim(attended, own_at, half)
    att_got = flip(lax.dynamic_slice_in_dim(attended, other_at, half), "tensor", 0)
    hidden_rows = lax.dynamic_slice_in_dim(hidden_in, own_at, half)
    cot_rows = lax.dynamic_slice_in_dim(cotangent, own_at, half)
    out_half, grad_mine, grad_theirs, grad_mixed_low, packed, sum_u, sum_w, sum_d = middle(
        core[None].astype(jnp.int32), att_mine, att_got, hidden_rows, cot_rows, vec_u, vec_w, vec_d, inner_parts, outer_parts, out_parts
    )

    grad_got = flip(grad_theirs, "tensor", 0)
    grad_attended = in_order(tensor_id, grad_mine, grad_got, 0)

    early = lax.psum_scatter(packed, "dp", scatter_dimension=0, tiled=True)
    early_mine, early_other = jnp.split(early, 2, axis=1)
    early_sum = early_mine.astype(F32) + flip(early_other, "tensor", 0).astype(F32)
    inner_weight_grad = early_sum[:, :units]
    outer_weight_grad = early_sum[:, units : 2 * units].T
    out_weight_grad = early_sum[:, 2 * units :].T

    output = in_order(tensor_id, out_half, flip(out_half, "tensor", 0), 0)

    grad_query_in, key_acc, value_acc, own_key_grad, own_value_grad = attend_back(
        info, queries, keys, values, prompt_pair[0], prompt_pair[1], attended, inverse, grad_attended, weighed
    )
    acc = jnp.stack([key_acc, value_acc]).reshape(2, GDEV, prompt_rows, width)
    near = acc[:, 0::2].astype(F32) + flip(acc[:, 1::2], "dp", 0).astype(F32)
    summed = (near[:, 0] + flip(near[:, 1].astype(BF), "dp", 1).astype(F32)).astype(BF)
    grad_keys = jnp.concatenate([summed[0], own_key_grad[prompt_rows:]], axis=0)
    grad_values = jnp.concatenate([summed[1], own_value_grad[prompt_rows:]], axis=0)

    query_weight_grad = contract_rows(pre_low, grad_query_in)
    key_weight_grad = contract_rows(pre_low, grad_keys)
    value_weight_grad = contract_rows(pre_low, grad_values)
    query_bias_grad = jnp.sum(grad_query_in.astype(F32), axis=0)
    value_bias_grad = jnp.sum(grad_values.astype(F32), axis=0)
    grad_normed_part = (
        back_project(grad_query_in, query_weight)
        + back_project(grad_keys, key_weight)
        + back_project(grad_values, value_weight)
    )
    grad_normed_low = grad_normed_part.astype(BF)
    grad_normed = grad_normed_low.astype(F32) + flip(grad_normed_low, "tensor", 0).astype(F32)
    pre_gain_grad = jnp.sum(grad_normed * pre_unit, axis=0)
    pre_bias_grad = jnp.sum(grad_normed, axis=0)
    grad_mixed_all = in_order(tensor_id, grad_mixed_low, flip(grad_mixed_low, "tensor", 0), 0).astype(F32)
    input_low = (grad_mixed_all + norm_back(grad_normed, pre_gain_f, pre_unit, pre_scale)).astype(BF)

    per_u, per_w, per_d = units // ranks, width // ranks, D // ranks
    vec = jnp.concatenate(
        [
            sum_u[:3].reshape(3, 2, ranks, per_u).transpose(2, 1, 0, 3).reshape(ranks, 6 * per_u),
            sum_w[:2].reshape(2, 2, ranks, per_w).transpose(2, 1, 0, 3).reshape(ranks, 4 * per_w),
            sum_d[:4].reshape(4, ranks, per_d).swapaxes(0, 1).reshape(ranks, 4 * per_d),
            jnp.stack([query_bias_grad, value_bias_grad]).reshape(2, ranks, per_w).swapaxes(0, 1).reshape(ranks, 2 * per_w),
            jnp.stack([pre_gain_grad, pre_bias_grad]).reshape(2, ranks, per_d).swapaxes(0, 1).reshape(ranks, 2 * per_d),
        ],
        axis=1,
    )
    count = vec.shape[1]
    block = D // ranks
    vec = jnp.pad(vec, ((0, 0), (0, block * 128 - count))).reshape(D, 128)
    late = halving(
        jnp.concatenate(
            [p.astype(BF) for p in (query_weight_grad, key_weight_grad, value_weight_grad, vec)], axis=1
        ),
        device,
    )
    vec = late[:, 3 * width :].reshape(-1)[:count]
    late = late[:, : 3 * width].astype(F32)
    at_w = 6 * per_u
    at_d = at_w + 4 * per_w
    at_late = at_d + 4 * per_d
    got = flip(vec[:at_late], "tensor", 0).astype(F32)
    vec = vec.astype(F32)
    ffn_gain_grad, ffn_bias_grad, inner_bias_grad = (vec[: 3 * per_u] + got[3 * per_u : at_w]).reshape(3, per_u)
    sub_gain_grad, sub_bias_grad = (vec[at_w : at_w + 2 * per_w] + got[at_w + 2 * per_w : at_d]).reshape(2, per_w)
    out_bias_grad, mid_gain_grad, mid_bias_grad, outer_bias_grad = (vec[at_d:at_late] + got[at_d:]).reshape(4, per_d)
    query_bias_grad, value_bias_grad = vec[at_late : at_late + 2 * per_w].reshape(2, per_w)
    pre_gain_grad, pre_bias_grad = vec[at_late + 2 * per_w :].reshape(2, per_d)
    return (
        output,
        input_low,
        pre_gain_grad,
        pre_bias_grad,
        late[:, :width],
        query_bias_grad,
        late[:, width : 2 * width],
        late[:, 2 * width : 3 * width],
        value_bias_grad,
        sub_gain_grad,
        sub_bias_grad,
        out_weight_grad,
        out_bias_grad,
        mid_gain_grad,
        mid_bias_grad,
        inner_weight_grad,
        inner_bias_grad,
        ffn_gain_grad,
        ffn_bias_grad,
        outer_weight_grad,
        outer_bias_grad,
    )

def solution(mesh):
    placed = (
        P("dp", None),
        P("dp", None),
        P(),
        P(),
        P(),
        P(),
        P(),
        P(),
        P(None, "tensor"),
        P("tensor"),
        P(None, "tensor"),
        P(None, "tensor"),
        P("tensor"),
        P("tensor"),
        P("tensor"),
        P("tensor", None),
        P(),
        P(),
        P(),
        P(None, "tensor"),
        P("tensor"),
        P("tensor"),
        P("tensor"),
        P("tensor", None),
        P(),
    )
    return jax.shard_map(
        body,
        mesh=mesh,
        in_specs=placed,
        out_specs=(
            P("dp", None),
            P("dp", None),
            P("dp"),
            P("dp"),
            P("dp", "tensor"),
            P(("tensor", "dp")),
            P("dp", "tensor"),
            P("dp", "tensor"),
            P(("tensor", "dp")),
            P(("tensor", "dp")),
            P(("tensor", "dp")),
            P("tensor", "dp"),
            P("dp"),
            P("dp"),
            P("dp"),
            P("dp", "tensor"),
            P(("tensor", "dp")),
            P(("tensor", "dp")),
            P(("tensor", "dp")),
            P("tensor", "dp"),
            P("dp"),
        ),
        check_vma=False,
    )
```

```python
import functools

import jax
import jax.numpy as jnp
from jax import lax
from jax.experimental import pallas as pl
from jax.experimental.pallas import tpu as pltpu
from jax.sharding import PartitionSpec as P

HD = 64
PROMPT = 2048
CONT = 256
GDEV = 4
TILE = 256
CHUNK = PROMPT // GDEV
PTILES = CHUNK // TILE
LOG2E = 1.4426950408889634
BF = jnp.bfloat16
F32 = jnp.float32
TAB = 10


def dot_nt(a, b):
    return lax.dot_general(a, b, (((1,), (1,)), ((), ())), preferred_element_type=F32)


def dot_nn(a, b):
    return lax.dot_general(a, b, (((1,), (0,)), ((), ())), preferred_element_type=F32)


def low_half(rows):
    return lax.broadcasted_iota(jnp.int32, (rows, 128), 1) < HD


def codes(at, tab, pair, miss):
    def cell(i):
        return tab[pair * TAB + i]

    first = jnp.floor((at + 0.5) * cell(0))
    second = jnp.floor((at + 0.5) * cell(1))
    rest1 = at - cell(2) * jnp.floor((at + 0.5) * cell(3))
    rest2 = at - cell(4) * jnp.floor((at + 0.5) * cell(5))
    return [
        first,
        jnp.where(rest1 == cell(6), second, miss),
        jnp.where(rest1 == cell(7), second, miss),
        jnp.where(rest2 == cell(8), 1.0, 0.0),
        jnp.where(rest2 == cell(9), 1.0, 0.0),
    ]


def fwd_kernel(info, tab, q_ref, kp_ref, vp_ref, ko_ref, vo_ref, o_ref, e_ref, li_ref, t_s, kc_s):
    pair = pl.program_id(0)
    step = pl.program_id(1)
    member = info[0]
    low = low_half(TILE)
    q = q_ref[...]
    zero = jnp.zeros_like(q)
    qs = [jnp.where(low, q, zero), jnp.where(low, zero, q)]
    row = lax.broadcasted_iota(jnp.int32, (TILE, 128), 0).astype(F32)
    at_q = info[2 + step].astype(F32) + row
    qc = codes(at_q, tab, pair, -2.0)

    @pl.when(step == 0)
    def _():
        at_k = info[1].astype(F32) + lax.broadcasted_iota(jnp.int32, (8, PROMPT), 1).astype(F32)
        for i, c in enumerate(codes(at_k, tab, pair, -1.0)):
            kc_s[i] = c

    def logits(mx, keys, kc, causal, at, width):
        out = []
        for h in range(2):
            s = dot_nt(qs[h], keys)
            top = mx[h]
            for g in range(width // 128):
                lanes = slice(g * 128, (g + 1) * 128)
                w = jnp.where(qc[0] == kc[0][:, lanes], 1.0, 0.0)
                w = w + jnp.where(qc[1 + h] == kc[1 + h][:, lanes], 1.0, 0.0)
                w = w + qc[3 + h] * kc[3 + h][:, lanes]
                if causal is not None:
                    w = jnp.where(causal[:, lanes], w, 0.0)
                t = s[:, lanes] * LOG2E + jnp.log2(w)
                t_s[h, :, pl.ds(at + g * 128, 128)] = t
                top = jnp.maximum(top, t)
            out.append(top)
        return tuple(out)

    def weigh(carry, vals, m, at, width):
        sums, accs = carry
        ns, na = [], []
        for h in range(2):
            total = sums[h]
            parts = []
            for g in range(width // 128):
                e = jnp.exp2(t_s[h, :, pl.ds(at + g * 128, 128)] - m[h])
                total = total + e
                parts.append(e.astype(BF))
            el = jnp.concatenate(parts, axis=1)
            e_ref[h, :, pl.ds(at, width)] = el
            ns.append(total)
            na.append(accs[h] + dot_nn(el, vals))
        return (tuple(ns), tuple(na))

    def finish(carry):
        sums, accs = carry
        li = [1.0 / jnp.sum(s, axis=1, keepdims=True) for s in sums]
        lfull = jnp.where(low, li[0], li[1])
        li_ref[...] = lfull
        o_ref[...] = (jnp.where(low, accs[0], accs[1]) * lfull).astype(BF)

    def tops(mx):
        return [jnp.broadcast_to(jnp.max(x, axis=1, keepdims=True), (TILE, 128)) for x in mx]

    neg = jnp.full((TILE, 128), -jnp.inf, F32)
    zf = jnp.zeros((TILE, 128), F32)

    def key_codes(at, width):
        return [kc_s[i, 0:1, pl.ds(at, width)] for i in range(5)]

    @pl.when(step < PTILES)
    def _():
        def one(j, mx):
            at = pl.multiple_of(j * CHUNK, CHUNK)
            held = pl.multiple_of((j ^ member) * CHUNK, CHUNK)
            return logits(mx, kp_ref[pl.ds(held, CHUNK), :], key_codes(at, CHUNK), None, held, CHUNK)

        mx = lax.fori_loop(0, member, one, (neg, neg))
        at = pl.multiple_of(member * CHUNK, CHUNK)
        rows = lax.broadcasted_iota(jnp.int32, (TILE, CHUNK), 0) + step * TILE
        cols = lax.broadcasted_iota(jnp.int32, (TILE, CHUNK), 1)
        mx = logits(mx, kp_ref[0:CHUNK, :], key_codes(at, CHUNK), cols <= rows, 0, CHUNK)
        m = tops(mx)

        def two(j, carry):
            held = pl.multiple_of((j ^ member) * CHUNK, CHUNK)
            return weigh(carry, vp_ref[pl.ds(held, CHUNK), :], m, held, CHUNK)

        finish(lax.fori_loop(0, member + 1, two, ((zf, zf), (zf, zf))))

    @pl.when(step >= PTILES)
    def _():
        mx = (neg, neg)
        for j in range(GDEV):
            at = pl.multiple_of((j ^ member) * CHUNK, CHUNK)
            mx = logits(mx, kp_ref[j * CHUNK : (j + 1) * CHUNK, :], key_codes(at, CHUNK), None, j * CHUNK, CHUNK)
        rows = lax.broadcasted_iota(jnp.int32, (TILE, CONT), 0)
        cols = lax.broadcasted_iota(jnp.int32, (TILE, CONT), 1)
        at_k = info[2 + step].astype(F32) + lax.broadcasted_iota(jnp.int32, (8, CONT), 1).astype(F32)
        own = [c[0:1] for c in codes(at_k, tab, pair, -1.0)]
        mx = logits(mx, ko_ref[...], own, cols <= rows, PROMPT, CONT)
        m = tops(mx)
        carry = ((zf, zf), (zf, zf))
        for j in range(GDEV):
            carry = weigh(carry, vp_ref[j * CHUNK : (j + 1) * CHUNK, :], m, j * CHUNK, CHUNK)
        finish(weigh(carry, vo_ref[...], m, PROMPT, CONT))


def attend(info, tab, q, k, v, kp, vp):
    rows, width = q.shape
    pairs = width // 128
    span = PROMPT + CONT
    tile = pl.BlockSpec((TILE, 128), lambda a, t, s, f: (t, a))
    whole = pl.BlockSpec((PROMPT, 128), lambda a, t, s, f: (0, a))
    return pl.pallas_call(
        fwd_kernel,
        grid_spec=pltpu.PrefetchScalarGridSpec(
            num_scalar_prefetch=2,
            grid=(pairs, rows // TILE),
            in_specs=[tile, whole, whole, tile, tile],
            out_specs=[tile, pl.BlockSpec((2, TILE, span), lambda a, t, s, f: (a, t, 0)), tile],
            scratch_shapes=[pltpu.VMEM((2, TILE, span), F32), pltpu.VMEM((5, 8, PROMPT), F32)],
        ),
        out_shape=[
            jax.ShapeDtypeStruct((rows, width), BF),
            jax.ShapeDtypeStruct((2 * pairs, rows, span), BF),
            jax.ShapeDtypeStruct((rows, width), F32),
        ],
        compiler_params=pltpu.CompilerParams(vmem_limit_bytes=48 << 20),
        cost_estimate=pl.CostEstimate(flops=16 * 10**9, bytes_accessed=60 * 10**6, transcendentals=0),
        name="attend",
    )(info, tab, q, kp, vp, k, v)


def bwd_kernel(info, q_ref, kp_ref, vp_ref, ko_ref, vo_ref, o_ref, li_ref, g_ref, e_ref, dq_ref, dk_ref, dv_ref, dko_ref, dvo_ref, dk_s, dv_s):
    step = pl.program_id(1)
    member = info[0]
    low = low_half(TILE)
    g = g_ref[...].astype(F32) * li_ref[...]
    prod = g * o_ref[...].astype(F32)
    zf = jnp.zeros((TILE, 128), F32)
    deltas = [
        jnp.sum(jnp.where(low, prod, zf), axis=1, keepdims=True),
        jnp.sum(jnp.where(low, zf, prod), axis=1, keepdims=True),
    ]
    gs = [jnp.where(low, g, zf).astype(BF), jnp.where(low, zf, g).astype(BF)]
    gt = jnp.transpose(g).astype(BF)
    qt = jnp.transpose(q_ref[...].astype(F32)).astype(BF)

    def grads(dq, keys, vals, at, width):
        out, dks, dvs = [], [], []
        for h in range(2):
            e = e_ref[h, :, pl.ds(at, width)]
            dp = dot_nt(gs[h], vals)
            ds = (e.astype(F32) * (dp - deltas[h])).astype(BF)
            out.append(dq[h] + dot_nn(ds, keys))
            dks.append(dot_nn(qt[h * HD : (h + 1) * HD, :], ds))
            dvs.append(dot_nn(gt[h * HD : (h + 1) * HD, :], e))
        return tuple(out), dks, dvs

    @pl.when(step == 0)
    def _():
        dk_s[...] = jnp.zeros_like(dk_s)
        dv_s[...] = jnp.zeros_like(dv_s)

    def add(at, width, dks, dvs):
        for h in range(2):
            dk_s[h * HD : (h + 1) * HD, pl.ds(at, width)] += dks[h]
            dv_s[h * HD : (h + 1) * HD, pl.ds(at, width)] += dvs[h]

    def scaled(dq):
        return (jnp.where(low, dq[0], dq[1]).astype(BF).astype(F32) * 0.125).astype(BF)

    @pl.when(step < PTILES)
    def _():
        def one(j, dq):
            at = pl.multiple_of((j ^ member) * CHUNK, CHUNK)
            dq, dks, dvs = grads(dq, kp_ref[pl.ds(at, CHUNK), :], vp_ref[pl.ds(at, CHUNK), :], at, CHUNK)
            add(at, CHUNK, dks, dvs)
            return dq

        dq_ref[...] = scaled(lax.fori_loop(0, member + 1, one, (zf, zf)))
        dko_ref[...] = jnp.zeros_like(dko_ref)
        dvo_ref[...] = jnp.zeros_like(dvo_ref)

    @pl.when(step >= PTILES)
    def _():
        dq = (zf, zf)
        for j in range(GDEV):
            span = slice(j * CHUNK, (j + 1) * CHUNK)
            dq, dks, dvs = grads(dq, kp_ref[span, :], vp_ref[span, :], j * CHUNK, CHUNK)
            add(j * CHUNK, CHUNK, dks, dvs)
        dq, dks, dvs = grads(dq, ko_ref[...], vo_ref[...], PROMPT, CONT)
        dq_ref[...] = scaled(dq)
        dko_ref[...] = jnp.transpose(jnp.concatenate(dks, axis=0)).astype(BF)
        dvo_ref[...] = jnp.transpose(jnp.concatenate(dvs, axis=0)).astype(BF)

    @pl.when(step == pl.num_programs(1) - 1)
    def _():
        for j in range(GDEV):
            span = slice(j * CHUNK, (j + 1) * CHUNK)
            dk_ref[span, :] = jnp.transpose(dk_s[:, span]).astype(BF)
            dv_ref[span, :] = jnp.transpose(dv_s[:, span]).astype(BF)


def attend_back(info, q, k, v, kp, vp, o, li, g, e):
    rows, width = q.shape
    pairs = width // 128
    span = PROMPT + CONT
    tile = pl.BlockSpec((TILE, 128), lambda a, t, s: (t, a))
    whole = pl.BlockSpec((PROMPT, 128), lambda a, t, s: (0, a))
    return pl.pallas_call(
        bwd_kernel,
        grid_spec=pltpu.PrefetchScalarGridSpec(
            num_scalar_prefetch=1,
            grid=(pairs, rows // TILE),
            in_specs=[tile, whole, whole, tile, tile, tile, tile, tile, pl.BlockSpec((2, TILE, span), lambda a, t, s: (a, t, 0))],
            out_specs=[tile, whole, whole, tile, tile],
            scratch_shapes=[pltpu.VMEM((128, PROMPT), F32), pltpu.VMEM((128, PROMPT), F32)],
        ),
        out_shape=[
            jax.ShapeDtypeStruct((rows, width), BF),
            jax.ShapeDtypeStruct((PROMPT, width), BF),
            jax.ShapeDtypeStruct((PROMPT, width), BF),
            jax.ShapeDtypeStruct((rows, width), BF),
            jax.ShapeDtypeStruct((rows, width), BF),
        ],
        compiler_params=pltpu.CompilerParams(vmem_limit_bytes=48 << 20),
        cost_estimate=pl.CostEstimate(flops=30 * 10**9, bytes_accessed=60 * 10**6, transcendentals=0),
        name="attend_back",
    )(info, q, kp, vp, k, v, o, li, g, e)

MESH = pl.DeviceIdType.MESH


EPSILON = 1e-05
D = 768
UCH = 512


def polynomial(x, terms):
    out = jnp.full_like(x, terms[0])
    for term in terms[1:]:
        out = out * x + term
    return out


def error_function(x):
    x = jnp.clip(x, -3.832506856900711, 3.832506856900711)
    square = x * x
    top = polynomial(
        square,
        (0.00022905065861350646, 0.0034082910107109506, 0.050955695062380861, 0.18520832239976145, 1.128379143519084),
    )
    bottom = polynomial(
        square,
        (
            -1.1791602954361697e-7,
            0.000023547966471313185,
            0.0010179625278914885,
            0.014070470171167667,
            0.11098505178285362,
            0.49746925110067538,
            1.0,
        ),
    )
    return x * top / bottom


def gelu_pair(v):
    phi = 0.5 + 0.5 * error_function(v * 0.7071067811865476)
    density = jnp.exp(-0.5 * v * v) * 0.3989422804014327
    return v * phi, phi + v * density


def column_sum(x):
    return jnp.sum(x, axis=0, keepdims=True)


def mid_kernel(
    info, att_m, att_o, hid, cot, vec_own, vec_got, vec_d, w1_own, w1_got, w1_swap, w2_own, w2_got, w2_swap, wo_own, wo_got, wo_swap,
    out_ref, gatt_m, gatt_o, gmix_ref, packed, su_ref, sw_ref, sd_ref, ext_ref,
    vec_u, vec_w, w1, w2, wo, act_s, shp_s, dg_s, wide_s, acc_s, gmid_s, sub_s, mid_s, low_s, midt_s, cott_s, stage, sems, out_sems,
):
    core = info[0]
    units = w1_own.shape[1]
    width = wo_own.shape[0]
    rows = hid.shape[0]
    full = 2 * units
    half = units // 2
    half_w = width // 2
    here_u = pl.multiple_of(units + core * half, 128)
    there_u = pl.multiple_of(units + (1 - core) * half, 128)
    here_w = pl.multiple_of(width + core * half_w, 64)
    there_w = pl.multiple_of(width + (1 - core) * half_w, 64)
    loads = []
    for i, (src, dst) in enumerate(
        [
            (wo_own, wo.at[pl.ds(0, width), :]),
            (wo_got, wo.at[pl.ds(here_w, half_w), :]),
            (wo_swap, wo.at[pl.ds(there_w, half_w), :]),
            (w1_own, w1.at[:, pl.ds(0, units)]),
            (w1_got, w1.at[:, pl.ds(here_u, half)]),
            (w1_swap, w1.at[:, pl.ds(there_u, half)]),
            (w2_own, w2.at[pl.ds(0, units), :]),
            (w2_got, w2.at[pl.ds(here_u, half), :]),
            (w2_swap, w2.at[pl.ds(there_u, half), :]),
        ]
    ):
        copy = pltpu.make_async_copy(src, dst, sems.at[i])
        copy.start()
        loads.append(copy)

    for i in range(3):
        for j, vec in enumerate((vec_own, vec_got)):
            vec_u[i : i + 1, pl.ds(j * units, units)] = vec[0:1, pl.ds(i * units, units)]
    for i in range(2):
        for j, vec in enumerate((vec_own, vec_got)):
            vec_w[i : i + 1, pl.ds(j * width, width)] = vec[0:1, pl.ds(3 * units + i * width, width)]

    a0 = att_m[...].astype(F32)
    a1 = att_o[...].astype(F32)
    center = (jnp.sum(a0, axis=1, keepdims=True) + jnp.sum(a1, axis=1, keepdims=True)) * (1.0 / D)
    square = (jnp.sum(a0 * a0, axis=1, keepdims=True) + jnp.sum(a1 * a1, axis=1, keepdims=True)) * (1.0 / D)
    sub_scale = lax.rsqrt(square - center * center + EPSILON)
    sub_s[:, 0:width] = (a0 - center) * sub_scale
    sub_s[:, width : 2 * width] = (a1 - center) * sub_scale
    sub_gain = vec_w[0:1, :]
    low_s[...] = (sub_s[...] * sub_gain + vec_w[1:2, :]).astype(BF)
    for copy in loads[0:3]:
        copy.wait()
    mixed = hid[...].astype(F32) + (dot_nn(low_s[...], wo[...]) + vec_d[0:1, pl.ds(0, D)])
    wide_s[...] = mixed
    mean = jnp.mean(mixed, axis=1, keepdims=True)
    mid_scale = lax.rsqrt(jnp.mean(mixed * mixed, axis=1, keepdims=True) - mean * mean + EPSILON)
    mid_s[...] = (mixed - mean) * mid_scale
    mid_gain = vec_d[0:1, pl.ds(768, D)]
    mid_full = mid_s[...] * mid_gain + vec_d[0:1, pl.ds(1536, D)]
    mid_low = mid_full.astype(BF)
    midt_s[...] = jnp.transpose(mid_full).astype(BF)
    cot_full = cot[...].astype(F32)
    cott_s[...] = jnp.transpose(cot_full).astype(BF)
    sd_ref[...] = jnp.zeros_like(sd_ref)
    sd_ref[3:4, :] = column_sum(cot_full)
    for copy in loads[3:6]:
        copy.wait()

    def lanes_sum(x):
        total = x[:, 0:128]
        for i in range(1, x.shape[1] // 128):
            total = total + x[:, i * 128 : (i + 1) * 128]
        return total

    def first(c, carry):
        at = pl.multiple_of(c * UCH, UCH)
        inner = dot_nn(mid_low, w1[:, pl.ds(at, UCH)]) + vec_u[2:3, pl.ds(at, UCH)]
        act, slope = gelu_pair(inner)
        act_s[:, pl.ds(at, UCH)] = act
        dg_s[:, pl.ds(at, UCH)] = slope.astype(BF)
        return carry[0] + lanes_sum(act), carry[1] + lanes_sum(act * act)

    zero = jnp.zeros((rows, 128), F32)
    act_sum, act_square = lax.fori_loop(0, full // UCH, first, (zero, zero))
    ffn_center = jnp.sum(act_sum, axis=1, keepdims=True) * (1.0 / full)
    ffn_scale = lax.rsqrt(
        jnp.sum(act_square, axis=1, keepdims=True) * (1.0 / full) - ffn_center * ffn_center + EPSILON
    )
    for copy in loads[6:9]:
        copy.wait()
    acc_s[...] = jnp.zeros_like(acc_s)
    per = units // UCH
    wide = 2 * units + width

    def column_of(c, extra):
        return pl.multiple_of((c // per) * wide + lax.rem(c, per) * UCH + extra, 128)

    def send(slot, column):
        return pltpu.make_async_copy(stage.at[slot], packed.at[:, pl.ds(column, UCH)], out_sems.at[slot])

    def put(c, value, extra):
        slot = lax.rem(c, 2)

        @pl.when(c >= 2)
        def _():
            send(slot, column_of(c - 2, extra)).wait()

        stage[slot] = value
        send(slot, column_of(c, extra)).start()

    def drain(extra):
        for c in range(full // UCH - 2, full // UCH):
            send(c % 2, column_of(c, extra)).wait()

    def second(c, carry):
        at = pl.multiple_of(c * UCH, UCH)
        unit = (act_s[:, pl.ds(at, UCH)] - ffn_center) * ffn_scale
        act_s[:, pl.ds(at, UCH)] = unit
        gain = vec_u[0:1, pl.ds(at, UCH)]
        low = (unit * gain + vec_u[1:2, pl.ds(at, UCH)]).astype(BF)
        acc_s[...] += dot_nn(low, w2[pl.ds(at, UCH), :])
        grad = dot_nt(cot[...], w2[pl.ds(at, UCH), :])
        cross = grad * unit
        su_ref[0:1, pl.ds(at, UCH)] = column_sum(cross)
        su_ref[1:2, pl.ds(at, UCH)] = column_sum(grad)
        shaped = grad * gain
        shp_s[:, pl.ds(at, UCH)] = shaped
        put(c, dot_nn(cott_s[...], low).astype(BF), units)
        return carry[0] + lanes_sum(shaped), carry[1] + lanes_sum(shaped * unit)

    su_ref[...] = jnp.zeros_like(su_ref)
    s_sum, s_cross = lax.fori_loop(0, full // UCH, second, (zero, zero))
    drain(units)
    shaped_mean = jnp.sum(s_sum, axis=1, keepdims=True) * (1.0 / full)
    cross_mean = jnp.sum(s_cross, axis=1, keepdims=True) * (1.0 / full)
    out_ref[...] = (wide_s[...] + (acc_s[...] + vec_d[0:1, pl.ds(2304, D)])).astype(BF)
    gmid_s[...] = jnp.zeros_like(gmid_s)

    def third(c, carry):
        at = pl.multiple_of(c * UCH, UCH)
        g = ffn_scale * (shp_s[:, pl.ds(at, UCH)] - shaped_mean - act_s[:, pl.ds(at, UCH)] * cross_mean)
        low = (g * dg_s[:, pl.ds(at, UCH)].astype(F32)).astype(BF)
        su_ref[2:3, pl.ds(at, UCH)] = column_sum(low.astype(F32))
        gmid_s[...] += dot_nt(low, w1[:, pl.ds(at, UCH)])
        put(c, dot_nn(midt_s[...], low).astype(BF), 0)
        return carry

    lax.fori_loop(0, full // UCH, third, 0)
    drain(0)

    grad_mid = gmid_s[...]
    unit = mid_s[...]
    sd_ref[1:2, :] = column_sum(grad_mid * unit)
    sd_ref[2:3, :] = column_sum(grad_mid)
    shaped = grad_mid * mid_gain
    grad_mixed = cot[...].astype(F32) + mid_scale * (
        shaped - jnp.mean(shaped, axis=1, keepdims=True) - unit * jnp.mean(shaped * unit, axis=1, keepdims=True)
    )
    branch = grad_mixed.astype(BF)
    gmix_ref[...] = branch
    branch_f = branch.astype(F32)
    sd_ref[0:1, :] = column_sum(branch_f)
    out_grad = dot_nn(jnp.transpose(branch_f).astype(BF), low_s[...]).astype(BF)
    stage[0, :, 0:width] = out_grad[:, 0:width]
    stage[1, :, 0:width] = out_grad[:, width : 2 * width]
    last = [
        pltpu.make_async_copy(stage.at[i, :, pl.ds(0, width)], packed.at[:, pl.ds(i * wide + 2 * units, width)], out_sems.at[i])
        for i in range(2)
    ]
    for copy in last:
        copy.start()
    grad_sub = dot_nt(branch, wo[...])
    unit = sub_s[...]
    cross = grad_sub * unit
    sw_ref[...] = jnp.zeros_like(sw_ref)
    sw_ref[0:1, :] = column_sum(cross)
    sw_ref[1:2, :] = column_sum(grad_sub)
    shaped = grad_sub * sub_gain
    grad_att = sub_scale * (
        shaped - jnp.mean(shaped, axis=1, keepdims=True) - unit * jnp.mean(shaped * unit, axis=1, keepdims=True)
    )
    gatt_m[...] = grad_att[:, 0:width].astype(BF)
    gatt_o[...] = grad_att[:, width : 2 * width].astype(BF)
    parts = ext_ref.shape[0]
    if parts > 1:
        sums_u, sums_w, sums_d = su_ref[...], sw_ref[...], sd_ref[...]
        for i in range(parts):
            ext_ref[i] = jnp.concatenate(
                [
                    window(sums_u, i * (units // parts)),
                    window(sums_u, units + i * (units // parts)),
                    window(sums_w, i * (width // parts)),
                    window(sums_w, width + i * (width // parts)),
                    window(sums_d, i * (D // parts)),
                    jnp.zeros((8, 128), F32),
                ],
                axis=0,
            ).astype(BF)
    for copy in last:
        copy.wait()


def window(rows8, start):
    base = start // 128 * 128
    size = min(256, rows8.shape[1] - base)
    view = rows8[:, base : base + size]
    shift = start - base
    if shift:
        view = pltpu.roll(view, size - shift, 1)
    return view[:, 0:128]


def middle(core, att_m, att_o, hid, cot, vec_own, vec_got, vec_d, w1, w2, wo, parts):
    rows = hid.shape[0]
    units = w1[0].shape[1]
    width = wo[0].shape[0]
    vmem = pl.BlockSpec(memory_space=pltpu.VMEM)
    hbm = pl.BlockSpec(memory_space=pl.ANY)
    shape = jax.ShapeDtypeStruct
    return pl.pallas_call(
        mid_kernel,
        in_specs=[pl.BlockSpec(memory_space=pltpu.SMEM)] + [vmem] * 7 + [hbm] * 9,
        out_specs=[vmem] * 4 + [hbm] + [vmem] * 4,
        out_shape=[
            shape((rows, D), BF),
            shape((rows, width), BF),
            shape((rows, width), BF),
            shape((rows, D), BF),
            shape((D, 2 * (2 * units + width)), BF),
            shape((8, 2 * units), F32),
            shape((8, 2 * width), F32),
            shape((8, D), F32),
            shape((parts, 48, 128), BF),
        ],
        scratch_shapes=[
            pltpu.VMEM((8, 2 * units), F32),
            pltpu.VMEM((8, 2 * width), F32),
            pltpu.VMEM((D, 2 * units), BF),
            pltpu.VMEM((2 * units, D), BF),
            pltpu.VMEM((2 * width, D), BF),
            pltpu.VMEM((rows, 2 * units), F32),
            pltpu.VMEM((rows, 2 * units), F32),
            pltpu.VMEM((rows, 2 * units), BF),
            pltpu.VMEM((rows, D), F32),
            pltpu.VMEM((rows, D), F32),
            pltpu.VMEM((rows, D), F32),
            pltpu.VMEM((rows, 2 * width), F32),
            pltpu.VMEM((rows, D), F32),
            pltpu.VMEM((rows, 2 * width), BF),
            pltpu.VMEM((D, rows), BF),
            pltpu.VMEM((D, rows), BF),
            pltpu.VMEM((2, D, UCH), BF),
            pltpu.SemaphoreType.DMA((9,)),
            pltpu.SemaphoreType.DMA((2,)),
        ],
        compiler_params=pltpu.CompilerParams(vmem_limit_bytes=62 << 20),
        cost_estimate=pl.CostEstimate(flops=21 * 10**9, bytes_accessed=30 * 10**6, transcendentals=0),
        name="middle",
    )(core, att_m, att_o, hid, cot, vec_own, vec_got, vec_d, *w1, *w2, *wo)


def bit_peer(device, bit):
    step = 1 << bit
    return device + (1 - 2 * ((device // step) % 2)) * step


def greet(peers):
    barrier = pltpu.get_barrier_semaphore()
    for peer in peers:
        pl.semaphore_signal(barrier, inc=1, device_id=peer, device_id_type=MESH)
    pl.semaphore_wait(barrier, len(peers))


def final_kernel(
    bits, hid, gain, bias, dq, dk, dv, wq, wk, wv, gmix, ext, kp, vp,
    gin, late_out, vec_out,
    near_s, loc_s, relay_s, far_s, unit_s, mine_s, norm_s, send_c, recv_c, send_p, recv_p, give_c, give_p, late_s, small_s,
    vec_s, vec_r, sems_a, sems_b, loc_sems, *stage_refs,
):
    device = lax.axis_index("dp")
    side = lax.axis_index("tensor")
    across = {"dp": device, "tensor": 1 - side}
    peers = [{"dp": bit_peer(device, b), "tensor": side} for b in range(bits)]
    rows, width = dq.shape
    prompt = kp.shape[0] // GDEV
    conts = rows - prompt
    half_p, half_c = prompt // 2, conts // 2
    own_p = pl.multiple_of(side * half_p, 128)
    their_p = pl.multiple_of((1 - side) * half_p, 128)
    own_c = pl.multiple_of(prompt + side * half_c, 128)
    their_c = pl.multiple_of(prompt + (1 - side) * half_c, 128)
    lanes = 3 * width + 128

    greet(peers + [across])
    count = [0]

    def remote(src, dst, peer):
        i = count[0]
        count[0] += 1
        copy = pltpu.make_async_remote_copy(
            src_ref=src, dst_ref=dst, send_sem=sems_a.at[i], recv_sem=sems_b.at[i], device_id=peer, device_id_type=MESH
        )
        copy.start()
        return copy

    first = []
    for i, part in enumerate((kp, vp)):
        first.append(remote(part.at[pl.ds(3 * prompt, prompt), :], near_s.at[2 * i + 1], peers[0]))
        first.append(remote(part.at[pl.ds(prompt, prompt), :], near_s.at[2 * i], peers[0]))
    local = []
    for i, part in enumerate((kp, vp)):
        for j in range(2):
            copy = pltpu.make_async_copy(part.at[pl.ds(2 * j * prompt, prompt), :], loc_s.at[2 * i + j], loc_sems.at[2 * i + j])
            copy.start()
            local.append(copy)

    gain_f = gain[...]
    bias_f = bias[...]

    def unit_rows(at, size):
        x = hid[pl.ds(at, size), :].astype(F32)
        center = jnp.mean(x, axis=1, keepdims=True)
        scale = lax.rsqrt(jnp.mean(x * x, axis=1, keepdims=True) - center * center + EPSILON)
        return (x - center) * scale, scale

    def part_of(at, size, k_rows, v_rows):
        return dot_nt(dq[pl.ds(at, size), :], wq[...]) + dot_nt(k_rows, wk[...]) + dot_nt(v_rows, wv[...])

    def gather(part, unit):
        return column_sum(part * unit), column_sum(part)

    unit, _ = unit_rows(their_c, half_c)
    part = part_of(their_c, half_c, dk[pl.ds(their_c, half_c), :], dv[pl.ds(their_c, half_c), :])
    send_c[...] = part.astype(BF)
    y_cont = remote(send_c, recv_c, across)
    gain_grad, bias_grad = gather(part, unit)
    norm_s[:, pl.ds(their_c, half_c)] = jnp.transpose(unit * gain_f + bias_f).astype(BF)
    unit, scale_c = unit_rows(own_c, half_c)
    part = part_of(own_c, half_c, dk[pl.ds(own_c, half_c), :], dv[pl.ds(own_c, half_c), :])
    mine_s[pl.ds(half_p, half_c), :] = part
    unit_s[pl.ds(half_p, half_c), :] = unit
    g, b = gather(part, unit)
    gain_grad, bias_grad = gain_grad + g, bias_grad + b
    norm_s[:, pl.ds(own_c, half_c)] = jnp.transpose(unit * gain_f + bias_f).astype(BF)

    for copy in local:
        copy.wait()
    for copy in first:
        copy.wait_recv()
    second = []
    for i in range(2):
        relay_s[i] = (loc_s[2 * i + 1].astype(F32) + near_s[2 * i + 1].astype(F32)).astype(BF)
        second.append(remote(relay_s.at[i], far_s.at[i], peers[1]))

    unit, _ = unit_rows(their_p, half_p)
    norm_s[:, pl.ds(their_p, half_p)] = jnp.transpose(unit * gain_f + bias_f).astype(BF)
    unit, scale_p = unit_rows(own_p, half_p)
    unit_s[pl.ds(0, half_p), :] = unit
    norm_s[:, pl.ds(own_p, half_p)] = jnp.transpose(unit * gain_f + bias_f).astype(BF)

    blocks = 1 << bits
    block = D // blocks

    def keep(value, lane):
        low = value.astype(BF)
        for i in range(blocks):
            late_s[i // 2, i % 2, :, pl.ds(lane, width)] = low[i * block : (i + 1) * block, :]

    keep(dot_nn(norm_s[...], dq[...]), 0)
    q_bias = column_sum(dq[...].astype(F32))

    def norm_back(total, unit, scale, mixed):
        shaped = total * gain_f
        return mixed.astype(F32) + scale * (
            shaped - jnp.mean(shaped, axis=1, keepdims=True) - unit * jnp.mean(shaped * unit, axis=1, keepdims=True)
        )

    y_cont.wait_recv()
    total = mine_s[pl.ds(half_p, half_c), :] + recv_c[...].astype(F32)
    give_c[...] = norm_back(total, unit_s[pl.ds(half_p, half_c), :], scale_c, gmix[pl.ds(half_p, half_c), :]).astype(BF)
    back_c = remote(give_c, gin.at[pl.ds(own_c, half_c), :], across)
    keep_c = pltpu.make_async_copy(give_c, gin.at[pl.ds(own_c, half_c), :], loc_sems.at[4])
    keep_c.start()

    for copy in second:
        copy.wait_recv()
    for i in range(2):
        loc_s[2 * i] = (loc_s[2 * i].astype(F32) + near_s[2 * i].astype(F32) + far_s[i].astype(F32)).astype(BF)
    part = part_of(their_p, half_p, loc_s[0, pl.ds(their_p, half_p), :], loc_s[2, pl.ds(their_p, half_p), :])
    send_p[...] = part.astype(BF)
    y_prompt = remote(send_p, recv_p, across)
    unit, _ = unit_rows(their_p, half_p)
    g, b = gather(part, unit)
    gain_grad, bias_grad = gain_grad + g, bias_grad + b
    part = part_of(own_p, half_p, loc_s[0, pl.ds(own_p, half_p), :], loc_s[2, pl.ds(own_p, half_p), :])
    mine_s[pl.ds(0, half_p), :] = part
    g, b = gather(part, unit_s[pl.ds(0, half_p), :])
    gain_grad, bias_grad = gain_grad + g, bias_grad + b

    for i, rest in enumerate((dk, dv)):
        keep(
            dot_nn(norm_s[:, pl.ds(0, prompt)], loc_s[2 * i])
            + dot_nn(norm_s[:, pl.ds(prompt, conts)], rest[pl.ds(prompt, conts), :]),
            (i + 1) * width,
        )
    v_bias = column_sum(loc_s[2].astype(F32)) + column_sum(dv[pl.ds(prompt, conts), :].astype(F32))

    small_s[...] = jnp.zeros_like(small_s)
    small_s[0:1, pl.ds(0, width)] = q_bias
    small_s[1:2, pl.ds(0, width)] = v_bias
    small_s[2:3, pl.ds(0, D)] = gain_grad
    small_s[3:4, pl.ds(0, D)] = bias_grad
    small = small_s[...]
    row_id = lax.broadcasted_iota(jnp.int32, (8, 128), 0)
    for i in range(blocks):
        narrow = window(small, i * (width // blocks))
        broad = window(small, i * block)
        tail = jnp.concatenate([ext[i, pl.ds(32, 16), :].astype(F32)[0:8], jnp.where(row_id < 2, narrow, broad)], axis=0)
        late_s[i // 2, i % 2, pl.ds(0, 32), pl.ds(3 * width, 128)] = ext[i, pl.ds(0, 32), :]
        late_s[i // 2, i % 2, pl.ds(32, 16), pl.ds(3 * width, 128)] = tail.astype(BF)

    source = late_s
    stages = []
    for bit in range(bits):
        landing, kept = stage_refs[2 * bit], stage_refs[2 * bit + 1]
        mine = (device // (1 << bit)) % 2
        copy = remote(source.at[:, 1 - mine], landing, peers[bit])
        if bit == 0:
            y_prompt.wait_recv()
            total = mine_s[pl.ds(0, half_p), :] + recv_p[...].astype(F32)
            give_p[...] = norm_back(total, unit_s[pl.ds(0, half_p), :], scale_p, gmix[pl.ds(0, half_p), :]).astype(BF)
            back_p = remote(give_p, gin.at[pl.ds(own_p, half_p), :], across)
            keep_p = pltpu.make_async_copy(give_p, gin.at[pl.ds(own_p, half_p), :], loc_sems.at[5])
            keep_p.start()
        copy.wait_recv()
        stages.append(copy)
        for i in range(landing.shape[0]):
            kept[i // 2, i % 2] = (source[i, mine].astype(F32) + landing[i].astype(F32)).astype(BF)
        source = kept
    late_out[...] = source[0, 0, :, pl.ds(0, 3 * width)].astype(F32)
    vec_s[...] = source[0, 0, :, pl.ds(3 * width, 128)]
    swap = remote(vec_s, vec_r, across)
    swap.wait_recv()
    vec_out[0] = vec_s[...].astype(F32)
    vec_out[1] = vec_r[...].astype(F32)
    for copy in first + second + stages + [y_cont, y_prompt, swap]:
        copy.wait_send()
    for copy in (back_c, back_p):
        copy.wait_recv()
        copy.wait_send()
    keep_c.wait()
    keep_p.wait()


def finish(hid, gain, bias, dq, dk, dv, wq, wk, wv, gmix, ext, kp, vp):
    rows, width = dq.shape
    ranks = lax.axis_size("dp")
    bits = ranks.bit_length() - 1
    block = D // ranks
    prompt = kp.shape[0] // GDEV
    conts = rows - prompt
    lanes = 3 * width + 128
    vmem = pl.BlockSpec(memory_space=pltpu.VMEM)
    hbm = pl.BlockSpec(memory_space=pl.ANY)
    shape = jax.ShapeDtypeStruct
    copies = 11 + bits
    stages = []
    for bit in range(bits):
        left = ranks >> (bit + 1)
        stages.append(pltpu.VMEM((left, block, lanes), BF))
        stages.append(pltpu.VMEM((max(left // 2, 1), min(left, 2), block, lanes), BF))
    return pl.pallas_call(
        functools.partial(final_kernel, bits),
        in_specs=[vmem] * 11 + [hbm] * 2,
        out_specs=[hbm, vmem, vmem],
        out_shape=[shape((rows, D), BF), shape((block, 3 * width), F32), shape((2, block, 128), F32)],
        scratch_shapes=[
            pltpu.VMEM((4, prompt, width), BF),
            pltpu.VMEM((4, prompt, width), BF),
            pltpu.VMEM((2, prompt, width), BF),
            pltpu.VMEM((2, prompt, width), BF),
            pltpu.VMEM((rows // 2, D), F32),
            pltpu.VMEM((rows // 2, D), F32),
            pltpu.VMEM((D, rows), BF),
            pltpu.VMEM((conts // 2, D), BF),
            pltpu.VMEM((conts // 2, D), BF),
            pltpu.VMEM((prompt // 2, D), BF),
            pltpu.VMEM((prompt // 2, D), BF),
            pltpu.VMEM((conts // 2, D), BF),
            pltpu.VMEM((prompt // 2, D), BF),
            pltpu.VMEM((ranks // 2, 2, block, lanes), BF),
            pltpu.VMEM((8, D + 128), F32),
            pltpu.VMEM((block, 128), BF),
            pltpu.VMEM((block, 128), BF),
            pltpu.SemaphoreType.DMA((copies,)),
            pltpu.SemaphoreType.DMA((copies,)),
            pltpu.SemaphoreType.DMA((6,)),
        ]
        + stages,
        compiler_params=pltpu.CompilerParams(vmem_limit_bytes=56 << 20, collective_id=1, has_side_effects=True),
        cost_estimate=pl.CostEstimate(flops=5 * 10**9, bytes_accessed=20 * 10**6, transcendentals=0),
        name="finish",
    )(hid, gain, bias, dq, dk, dv, wq, wk, wv, gmix, ext, kp, vp)


def flip(value, axis, bit):
    return lax.ppermute(value, axis, [(i, i ^ (1 << bit)) for i in range(lax.axis_size(axis))])


def contract_rows(left, right):
    return lax.dot_general(left, right, (((0,), (0,)), ((), ())), preferred_element_type=F32)


def back_project(left, right):
    return lax.dot_general(left, right, (((1,), (1,)), ((), ())), preferred_element_type=F32)


def dense(left, right):
    return jnp.dot(left, right, preferred_element_type=F32)


def norm_rows(values, gain, bias):
    center = jnp.mean(values, axis=-1, keepdims=True)
    spread = jnp.mean(values * values, axis=-1, keepdims=True) - center * center
    scaled = lax.rsqrt(spread + EPSILON)
    unit_rows = (values - center) * scaled
    return (unit_rows * gain + bias, unit_rows, scaled)


def norm_back(grad_rows, gain, unit_rows, scaled):
    shaped = grad_rows * gain
    return scaled * (
        shaped
        - jnp.mean(shaped, axis=-1, keepdims=True)
        - unit_rows * jnp.mean(shaped * unit_rows, axis=-1, keepdims=True)
    )


def in_order(which, mine, other, axis):
    return jnp.where(
        which == 0,
        jnp.concatenate([mine, other], axis=axis),
        jnp.concatenate([other, mine], axis=axis),
    )


def fetch(weight, core, axis):
    half = weight.shape[axis] // 2
    got = flip(lax.dynamic_slice_in_dim(weight, core * half, half, axis), "tensor", 0)
    return (got, flip(got, "dp", 0))


def halving(value, device):
    bits = lax.axis_size("dp").bit_length() - 1
    rows, columns = value.shape
    current = value
    for bit in range(bits):
        upper = device // (1 << bit) % 2
        left = bits - bit
        view = current.reshape((1 << (left - 1), 2, -1, columns))
        kept = lax.dynamic_index_in_dim(view, upper, 1, keepdims=False)
        sent = lax.dynamic_index_in_dim(view, 1 - upper, 1, keepdims=False)
        got = flip(sent, "dp", bit)
        current = (kept.astype(F32) + got.astype(F32)).astype(BF)
    return current.reshape(rows >> bits, columns)


def half_of(value, which):
    prompt, conts = CHUNK // 2, (value.shape[0] - CHUNK) // 2
    return jnp.concatenate(
        [
            lax.dynamic_slice_in_dim(value, which * prompt, prompt),
            lax.dynamic_slice_in_dim(value, CHUNK + which * conts, conts),
        ]
    )


def joined(which, mine, other):
    prompt = CHUNK // 2
    low = jnp.where(which == 0, mine, other)
    high = jnp.where(which == 0, other, mine)
    return jnp.concatenate([low[:prompt], high[:prompt], low[prompt:], high[prompt:]])


def body(
    hidden_in,
    cotangent,
    prompt_start,
    cont_gap,
    seg_len,
    dilation_rate,
    pre_gain,
    pre_bias,
    query_weight,
    query_bias,
    key_weight,
    value_weight,
    value_bias,
    sub_gain,
    sub_bias,
    out_weight,
    out_bias,
    mid_gain,
    mid_bias,
    inner_weight,
    inner_bias,
    ffn_gain,
    ffn_bias,
    outer_weight,
    outer_bias,
):
    device = lax.axis_index("dp")
    ranks = lax.axis_size("dp")
    group_id = device // GDEV
    member = device % GDEV
    tensor_id = lax.axis_index("tensor")
    core = device % 2
    width = query_weight.shape[1]
    units = inner_weight.shape[1]
    pairs = width // 128
    rows = hidden_in.shape[0]
    prompt_rows = CHUNK
    cont_count = (rows - prompt_rows) // CONT

    start_at = lax.dynamic_index_in_dim(prompt_start, group_id, 0, keepdims=False)
    gap_row = lax.dynamic_index_in_dim(cont_gap, group_id, 0, keepdims=False)
    own_gaps = lax.dynamic_slice_in_dim(gap_row, member * cont_count, cont_count)
    info = jnp.concatenate(
        [
            jnp.stack([member, start_at]),
            start_at + member * prompt_rows + TILE * jnp.arange(PTILES),
            start_at + PROMPT + own_gaps,
        ]
    ).astype(jnp.int32)
    seg = lax.dynamic_slice_in_dim(seg_len, tensor_id * pairs, pairs, 0)
    rate = lax.dynamic_slice_in_dim(dilation_rate, tensor_id * pairs, pairs, 0)
    head = 2 * (tensor_id * pairs + jnp.arange(pairs))
    tab = jnp.stack(
        [
            1.0 / seg[:, 0].astype(F32),
            1.0 / seg[:, 1].astype(F32),
            rate[:, 1].astype(F32),
            1.0 / rate[:, 1].astype(F32),
            rate[:, 2].astype(F32),
            1.0 / rate[:, 2].astype(F32),
            (head % rate[:, 1]).astype(F32),
            ((head + 1) % rate[:, 1]).astype(F32),
            (head % rate[:, 2]).astype(F32),
            ((head + 1) % rate[:, 2]).astype(F32),
        ],
        axis=1,
    ).reshape(-1)

    inner_parts = (inner_weight,) + fetch(inner_weight, core, 1)
    outer_parts = (outer_weight,) + fetch(outer_weight, core, 0)
    out_parts = (out_weight,) + fetch(out_weight, core, 0)
    vectors = jnp.concatenate([ffn_gain, ffn_bias, inner_bias, sub_gain, sub_bias]).astype(F32)
    vectors_other = flip(vectors, "tensor", 0)
    shared = jnp.concatenate([out_bias, mid_gain, mid_bias, outer_bias]).astype(F32)[None]

    inputs = hidden_in.astype(F32)
    pre_gain_f = pre_gain.astype(F32)
    pre_normed, pre_unit, pre_scale = norm_rows(inputs, pre_gain_f, pre_bias.astype(F32))
    pre_low = pre_normed.astype(BF)
    keys = dense(pre_low, key_weight).astype(BF)
    values = (dense(pre_low, value_weight) + value_bias.astype(F32)).astype(BF)
    own_pair = jnp.stack([keys[:prompt_rows], values[:prompt_rows]])
    far = flip(own_pair, "dp", 1)
    near_own = flip(own_pair, "dp", 0)
    near_far = flip(far, "dp", 0)
    prompt_pair = jnp.concatenate([own_pair, near_own, far, near_far], axis=1)
    queries = ((dense(pre_low, query_weight) + query_bias.astype(F32)) * 0.125).astype(BF)
    attended, weighed, inverse = attend(info, tab, queries, keys, values, prompt_pair[0], prompt_pair[1])

    att_mine = half_of(attended, tensor_id)
    att_got = flip(half_of(attended, 1 - tensor_id), "tensor", 0)
    hidden_rows = half_of(hidden_in, tensor_id)
    cot_rows = half_of(cotangent, tensor_id)
    fused = D % (16 * ranks) == 0
    out_half, grad_mine, grad_theirs, grad_mixed_low, packed, sum_u, sum_w, sum_d, ext = middle(
        core[None].astype(jnp.int32),
        att_mine,
        att_got,
        hidden_rows,
        cot_rows,
        vectors[None],
        vectors_other[None],
        shared,
        inner_parts,
        outer_parts,
        out_parts,
        ranks if fused else 1,
    )

    grad_got = flip(grad_theirs, "tensor", 0)
    grad_attended = joined(tensor_id, grad_mine, grad_got)

    early = lax.psum_scatter(packed, "dp", scatter_dimension=0, tiled=True)
    early_mine, early_other = jnp.split(early, 2, axis=1)
    early_sum = early_mine.astype(F32) + flip(early_other, "tensor", 0).astype(F32)
    inner_weight_grad = early_sum[:, :units]
    outer_weight_grad = early_sum[:, units : 2 * units].T
    out_weight_grad = early_sum[:, 2 * units :].T

    output = joined(tensor_id, out_half, flip(out_half, "tensor", 0))

    grad_query_in, key_acc, value_acc, own_key_grad, own_value_grad = attend_back(
        info, queries, keys, values, prompt_pair[0], prompt_pair[1], attended, inverse, grad_attended, weighed
    )
    block = D // ranks
    per_u, per_w, per_d = units // ranks, width // ranks, D // ranks
    if fused:
        input_low, late, vec = finish(
            hidden_in,
            pre_gain_f[None],
            pre_bias.astype(F32)[None],
            grad_query_in,
            own_key_grad,
            own_value_grad,
            query_weight,
            key_weight,
            value_weight,
            grad_mixed_low,
            ext,
            key_acc,
            value_acc,
        )
        ffn_gain_grad, ffn_bias_grad, inner_bias_grad = [vec[0, i, :per_u] + vec[1, 8 + i, :per_u] for i in range(3)]
        sub_gain_grad, sub_bias_grad = [vec[0, 16 + i, :per_w] + vec[1, 24 + i, :per_w] for i in range(2)]
        out_bias_grad, mid_gain_grad, mid_bias_grad, outer_bias_grad = [
            vec[0, 32 + i, :per_d] + vec[1, 32 + i, :per_d] for i in range(4)
        ]
        query_bias_grad, value_bias_grad = [vec[0, 40 + i, :per_w] for i in range(2)]
        pre_gain_grad, pre_bias_grad = [vec[0, 42 + i, :per_d] + vec[1, 42 + i, :per_d] for i in range(2)]
    else:
        acc = jnp.stack([key_acc, value_acc]).reshape(2, GDEV, prompt_rows, width)
        near = acc[:, 0::2].astype(F32) + flip(acc[:, 1::2], "dp", 0).astype(F32)
        summed = (near[:, 0] + flip(near[:, 1].astype(BF), "dp", 1).astype(F32)).astype(BF)
        grad_keys = jnp.concatenate([summed[0], own_key_grad[prompt_rows:]], axis=0)
        grad_values = jnp.concatenate([summed[1], own_value_grad[prompt_rows:]], axis=0)

        query_weight_grad = contract_rows(pre_low, grad_query_in)
        key_weight_grad = contract_rows(pre_low, grad_keys)
        value_weight_grad = contract_rows(pre_low, grad_values)
        query_bias_grad = jnp.sum(grad_query_in.astype(F32), axis=0)
        value_bias_grad = jnp.sum(grad_values.astype(F32), axis=0)
        grad_normed_part = (
            back_project(grad_query_in, query_weight)
            + back_project(grad_keys, key_weight)
            + back_project(grad_values, value_weight)
        )
        grad_normed_low = grad_normed_part.astype(BF)
        grad_normed = grad_normed_low.astype(F32) + flip(grad_normed_low, "tensor", 0).astype(F32)
        pre_gain_grad = jnp.sum(grad_normed * pre_unit, axis=0)
        pre_bias_grad = jnp.sum(grad_normed, axis=0)
        grad_mixed_all = joined(tensor_id, grad_mixed_low, flip(grad_mixed_low, "tensor", 0)).astype(F32)
        input_low = (grad_mixed_all + norm_back(grad_normed, pre_gain_f, pre_unit, pre_scale)).astype(BF)

        vec = jnp.concatenate(
            [
                sum_u[:3].reshape(3, 2, ranks, per_u).transpose(2, 1, 0, 3).reshape(ranks, 6 * per_u),
                sum_w[:2].reshape(2, 2, ranks, per_w).transpose(2, 1, 0, 3).reshape(ranks, 4 * per_w),
                sum_d[:4].reshape(4, ranks, per_d).swapaxes(0, 1).reshape(ranks, 4 * per_d),
                jnp.stack([query_bias_grad, value_bias_grad]).reshape(2, ranks, per_w).swapaxes(0, 1).reshape(ranks, 2 * per_w),
                jnp.stack([pre_gain_grad, pre_bias_grad]).reshape(2, ranks, per_d).swapaxes(0, 1).reshape(ranks, 2 * per_d),
            ],
            axis=1,
        )
        count = vec.shape[1]
        vec = jnp.pad(vec, ((0, 0), (0, block * 128 - count))).reshape(D, 128)
        late = halving(
            jnp.concatenate(
                [p.astype(BF) for p in (query_weight_grad, key_weight_grad, value_weight_grad, vec)], axis=1
            ),
            device,
        )
        vec = late[:, 3 * width :].reshape(-1)[:count]
        late = late[:, : 3 * width].astype(F32)
        at_w = 6 * per_u
        at_d = at_w + 4 * per_w
        at_late = at_d + 4 * per_d
        got = flip(vec[:at_late], "tensor", 0).astype(F32)
        vec = vec.astype(F32)
        ffn_gain_grad, ffn_bias_grad, inner_bias_grad = (vec[: 3 * per_u] + got[3 * per_u : at_w]).reshape(3, per_u)
        sub_gain_grad, sub_bias_grad = (vec[at_w : at_w + 2 * per_w] + got[at_w + 2 * per_w : at_d]).reshape(2, per_w)
        out_bias_grad, mid_gain_grad, mid_bias_grad, outer_bias_grad = (vec[at_d:at_late] + got[at_d:]).reshape(4, per_d)
        query_bias_grad, value_bias_grad = vec[at_late : at_late + 2 * per_w].reshape(2, per_w)
        pre_gain_grad, pre_bias_grad = vec[at_late + 2 * per_w :].reshape(2, per_d)
    return (
        output,
        input_low,
        pre_gain_grad,
        pre_bias_grad,
        late[:, :width],
        query_bias_grad,
        late[:, width : 2 * width],
        late[:, 2 * width : 3 * width],
        value_bias_grad,
        sub_gain_grad,
        sub_bias_grad,
        out_weight_grad,
        out_bias_grad,
        mid_gain_grad,
        mid_bias_grad,
        inner_weight_grad,
        inner_bias_grad,
        ffn_gain_grad,
        ffn_bias_grad,
        outer_weight_grad,
        outer_bias_grad,
    )

def solution(mesh):
    placed = (
        P("dp", None),
        P("dp", None),
        P(),
        P(),
        P(),
        P(),
        P(),
        P(),
        P(None, "tensor"),
        P("tensor"),
        P(None, "tensor"),
        P(None, "tensor"),
        P("tensor"),
        P("tensor"),
        P("tensor"),
        P("tensor", None),
        P(),
        P(),
        P(),
        P(None, "tensor"),
        P("tensor"),
        P("tensor"),
        P("tensor"),
        P("tensor", None),
        P(),
    )
    return jax.shard_map(
        body,
        mesh=mesh,
        in_specs=placed,
        out_specs=(
            P("dp", None),
            P("dp", None),
            P("dp"),
            P("dp"),
            P("dp", "tensor"),
            P(("tensor", "dp")),
            P("dp", "tensor"),
            P("dp", "tensor"),
            P(("tensor", "dp")),
            P(("tensor", "dp")),
            P(("tensor", "dp")),
            P("tensor", "dp"),
            P("dp"),
            P("dp"),
            P("dp"),
            P("dp", "tensor"),
            P(("tensor", "dp")),
            P(("tensor", "dp")),
            P(("tensor", "dp")),
            P("tensor", "dp"),
            P("dp"),
        ),
        check_vma=False,
    )
```

```python
import functools

import jax
import jax.numpy as jnp
from jax import lax
from jax.experimental import pallas as pl
from jax.experimental.pallas import tpu as pltpu
from jax.sharding import PartitionSpec as P

HD = 64
PROMPT = 2048
CONT = 256
GDEV = 4
TILE = 256
CHUNK = PROMPT // GDEV
PTILES = CHUNK // TILE
LOG2E = 1.4426950408889634
BF = jnp.bfloat16
F32 = jnp.float32
TAB = 10
D = 768
EPSILON = 1e-05
MESH = pl.DeviceIdType.MESH


def dot_nt(a, b):
    return lax.dot_general(a, b, (((1,), (1,)), ((), ())), preferred_element_type=F32)


def dot_nn(a, b):
    return lax.dot_general(a, b, (((1,), (0,)), ((), ())), preferred_element_type=F32)


def low_half(rows):
    return lax.broadcasted_iota(jnp.int32, (rows, 128), 1) < HD


def codes(at, tab, pair, miss):
    def cell(i):
        return tab[pair * TAB + i]

    first = jnp.floor((at + 0.5) * cell(0))
    second = jnp.floor((at + 0.5) * cell(1))
    rest1 = at - cell(2) * jnp.floor((at + 0.5) * cell(3))
    rest2 = at - cell(4) * jnp.floor((at + 0.5) * cell(5))
    return [
        first,
        jnp.where(rest1 == cell(6), second, miss),
        jnp.where(rest1 == cell(7), second, miss),
        jnp.where(rest2 == cell(8), 1.0, 0.0),
        jnp.where(rest2 == cell(9), 1.0, 0.0),
    ]


def bit_peer(device, bit):
    step = 1 << bit
    return device + (1 - 2 * ((device // step) % 2)) * step


def greet(peers):
    barrier = pltpu.get_barrier_semaphore()
    for peer in peers:
        pl.semaphore_signal(barrier, inc=1, device_id=peer, device_id_type=MESH)
    pl.semaphore_wait(barrier, len(peers))


def xor_bits(a, b):
    return (a % 2 + b % 2) % 2 + 2 * ((a // 2 + b // 2) % 2)


def fwd_kernel(
    info, tab, hid, gain, bias, wq, wk, wv, qb, vb, w1, w2, wo, vec,
    e_ref, li_ref, q_out, k_out, v_out, kp_out, vp_out, o_out, mine_out, got_out,
    w1_got, w1_swap, w2_got, w2_swap, wo_got, wo_swap, vec_got,
    t_s, kc_s, kv_s, low_s, q_s, ko_s, vo_s, o_s, sems_a, sems_b, loc_sems,
):
    pair = pl.program_id(0)
    step = pl.program_id(1)
    pairs = pl.num_programs(0)
    device = lax.axis_index("dp")
    side = lax.axis_index("tensor")
    member = device % GDEV
    core = device % 2
    rows, width = q_s.shape
    n_pairs = width // 128
    last_pair = n_pairs - 1
    conts = rows - CHUNK
    near = {"dp": bit_peer(device, 0), "tensor": side}
    far = {"dp": bit_peer(device, 1), "tensor": side}
    across = {"dp": device, "tensor": 1 - side}
    half_u = w1.shape[1] // 2
    half_w = wo.shape[0] // 2
    half_p, half_c = CHUNK // 2, conts // 2
    sent_u = pl.multiple_of(core * half_u, 128)
    sent_w = pl.multiple_of(core * half_w, 64)

    def remote(i, src, dst, peer):
        return pltpu.make_async_remote_copy(
            src_ref=src, dst_ref=dst, send_sem=sems_a.at[i], recv_sem=sems_b.at[i], device_id=peer, device_id_type=MESH
        )

    def to_far(p):
        lanes = pl.ds(p * 128, 128)
        return remote(3 * p, kv_s.at[0, :, :, lanes], kv_s.at[2, :, :, lanes], far)

    def to_near(p):
        lanes = pl.ds(p * 128, 128)
        return remote(3 * p + 1, kv_s.at[0, :, :, lanes], kv_s.at[1, :, :, lanes], near)

    def relay(p):
        lanes = pl.ds(p * 128, 128)
        return remote(3 * p + 2, kv_s.at[2, :, :, lanes], kv_s.at[3, :, :, lanes], near)

    base = 3 * n_pairs
    fetch_y = [
        remote(base, wo.at[pl.ds(sent_w, half_w), :], wo_got, across),
        remote(base + 1, w1.at[:, pl.ds(sent_u, half_u)], w1_got, across),
        remote(base + 2, w2.at[pl.ds(sent_u, half_u), :], w2_got, across),
        remote(base + 3, vec, vec_got, across),
    ]
    fetch_core = [
        remote(base + 4, wo_got, wo_swap, near),
        remote(base + 5, w1_got, w1_swap, near),
        remote(base + 6, w2_got, w2_swap, near),
    ]

    def give(p):
        lanes = pl.ds(p * 128, 128)
        their_p = pl.multiple_of((1 - side) * half_p, 128)
        their_c = pl.multiple_of(CHUNK + (1 - side) * half_c, 128)
        return [
            remote(base + 7 + 2 * p, o_s.at[pl.ds(their_p, half_p), lanes], got_out.at[pl.ds(0, half_p), lanes], across),
            remote(base + 8 + 2 * p, o_s.at[pl.ds(their_c, half_c), lanes], got_out.at[pl.ds(half_p, half_c), lanes], across),
        ]

    def keeps():
        own_p = pl.multiple_of(side * half_p, 128)
        own_c = pl.multiple_of(CHUNK + side * half_c, 128)
        return [
            pltpu.make_async_copy(o_s, o_out, loc_sems.at[0]),
            pltpu.make_async_copy(o_s.at[pl.ds(own_p, half_p), :], mine_out.at[pl.ds(0, half_p), :], loc_sems.at[1]),
            pltpu.make_async_copy(o_s.at[pl.ds(own_c, half_c), :], mine_out.at[pl.ds(half_p, half_c), :], loc_sems.at[2]),
        ]

    def saves():
        out = [
            pltpu.make_async_copy(q_s, q_out, loc_sems.at[3]),
            pltpu.make_async_copy(ko_s, k_out, loc_sems.at[4]),
            pltpu.make_async_copy(vo_s, v_out, loc_sems.at[5]),
        ]
        for r in range(GDEV):
            span = pl.ds(r * CHUNK, CHUNK)
            out.append(pltpu.make_async_copy(kv_s.at[r, 0], kp_out.at[span, :], loc_sems.at[6 + 2 * r]))
            out.append(pltpu.make_async_copy(kv_s.at[r, 1], vp_out.at[span, :], loc_sems.at[7 + 2 * r]))
        return out

    @pl.when((pair == 0) & (step == 0))
    def _():
        greet([near, far, across])
        for copy in fetch_y:
            copy.start()
        gain_f, bias_f = gain[...], bias[...]

        def norm(at, size):
            x = hid[at : at + size, :].astype(F32)
            center = jnp.mean(x, axis=1, keepdims=True)
            scale = lax.rsqrt(jnp.mean(x * x, axis=1, keepdims=True) - center * center + EPSILON)
            low = ((x - center) * scale * gain_f + bias_f).astype(BF)
            low_s[at : at + size, :] = low
            return low

        low = norm(0, CHUNK)
        kv_s[0, 0] = dot_nn(low, wk[...]).astype(BF)
        kv_s[0, 1] = (dot_nn(low, wv[...]) + vb[...]).astype(BF)
        to_far(0).start()
        for p in range(n_pairs):
            to_near(p).start()
        for at in range(CHUNK, rows, TILE):
            low = norm(at, TILE)
            ko_s[at - CHUNK : at - CHUNK + TILE, :] = dot_nn(low, wk[...]).astype(BF)
            vo_s[at - CHUNK : at - CHUNK + TILE, :] = (dot_nn(low, wv[...]) + vb[...]).astype(BF)
        to_far(0).wait_send()
        for p in range(1, n_pairs):
            to_far(p).start()
        for at in range(0, rows, TILE):
            q_s[at : at + TILE, :] = ((dot_nn(low_s[at : at + TILE, :], wq[...]) + qb[...]) * 0.125).astype(BF)
        to_far(0).wait_recv()
        relay(0).start()

    for p in range(n_pairs):
        @pl.when((pair == p) & (step == 0))
        def _():
            to_near(p).wait_recv()
            relay(p).wait_recv()

        if p + 1 < n_pairs:
            @pl.when((pair == p) & (step == 3))
            def _():
                to_far(p + 1).wait_recv()
                relay(p + 1).start()

    lanes = pl.ds(pl.multiple_of(pair * 128, 128), 128)
    low = low_half(TILE)
    q = q_s[pl.ds(pl.multiple_of(step * TILE, TILE), TILE), lanes]
    zero = jnp.zeros_like(q)
    qs = [jnp.where(low, q, zero), jnp.where(low, zero, q)]
    row = lax.broadcasted_iota(jnp.int32, (TILE, 128), 0).astype(F32)
    at_q = info[2 + step].astype(F32) + row
    qc = codes(at_q, tab, pair, -2.0)

    @pl.when(step == 0)
    def _():
        at_k = info[1].astype(F32) + lax.broadcasted_iota(jnp.int32, (8, PROMPT), 1).astype(F32)
        for i, c in enumerate(codes(at_k, tab, pair, -1.0)):
            kc_s[i] = c

    def logits(mx, keys, kc, causal, at, span):
        out = []
        for h in range(2):
            s = dot_nt(qs[h], keys)
            top = mx[h]
            for g in range(span // 128):
                part = slice(g * 128, (g + 1) * 128)
                w = jnp.where(qc[0] == kc[0][:, part], 1.0, 0.0)
                w = w + jnp.where(qc[1 + h] == kc[1 + h][:, part], 1.0, 0.0)
                w = w + qc[3 + h] * kc[3 + h][:, part]
                if causal is not None:
                    w = jnp.where(causal[:, part], w, 0.0)
                t = s[:, part] * LOG2E + jnp.log2(w)
                t_s[h, :, pl.ds(at + g * 128, 128)] = t
                top = jnp.maximum(top, t)
            out.append(top)
        return tuple(out)

    def weigh(carry, vals, m, at, span):
        sums, accs = carry
        ns, na = [], []
        for h in range(2):
            total = sums[h]
            parts = []
            for g in range(span // 128):
                e = jnp.exp2(t_s[h, :, pl.ds(at + g * 128, 128)] - m[h])
                total = total + e
                parts.append(e.astype(BF))
            el = jnp.concatenate(parts, axis=1)
            e_ref[h, :, pl.ds(at, span)] = el
            ns.append(total)
            na.append(accs[h] + dot_nn(el, vals))
        return (tuple(ns), tuple(na))

    def finish_rows(carry):
        sums, accs = carry
        li = [1.0 / jnp.sum(s, axis=1, keepdims=True) for s in sums]
        lfull = jnp.where(low, li[0], li[1])
        li_ref[...] = lfull
        o_s[pl.ds(pl.multiple_of(step * TILE, TILE), TILE), lanes] = (jnp.where(low, accs[0], accs[1]) * lfull).astype(BF)

    def tops(mx):
        return [jnp.broadcast_to(jnp.max(x, axis=1, keepdims=True), (TILE, 128)) for x in mx]

    neg = jnp.full((TILE, 128), -jnp.inf, F32)
    zf = jnp.zeros((TILE, 128), F32)

    def key_codes(at, span):
        return [kc_s[i, 0:1, pl.ds(at, span)] for i in range(5)]

    @pl.when(step < PTILES)
    def _():
        def one(j, mx):
            at = pl.multiple_of(j * CHUNK, CHUNK)
            held = xor_bits(j, member)
            return logits(
                mx, kv_s[held, 0, :, lanes], key_codes(at, CHUNK), None, pl.multiple_of(held * CHUNK, CHUNK), CHUNK
            )

        mx = lax.fori_loop(0, member, one, (neg, neg))
        at = pl.multiple_of(member * CHUNK, CHUNK)
        rows_id = lax.broadcasted_iota(jnp.int32, (TILE, CHUNK), 0) + step * TILE
        cols = lax.broadcasted_iota(jnp.int32, (TILE, CHUNK), 1)
        mx = logits(mx, kv_s[0, 0, :, lanes], key_codes(at, CHUNK), cols <= rows_id, 0, CHUNK)
        m = tops(mx)

        def two(j, carry):
            held = xor_bits(j, member)
            return weigh(carry, kv_s[held, 1, :, lanes], m, pl.multiple_of(held * CHUNK, CHUNK), CHUNK)

        finish_rows(lax.fori_loop(0, member + 1, two, ((zf, zf), (zf, zf))))

    @pl.when(step >= PTILES)
    def _():
        own = pl.ds(pl.multiple_of((step - PTILES) * TILE, TILE), TILE)
        mx = (neg, neg)
        for j in range(GDEV):
            at = pl.multiple_of(xor_bits(j, member) * CHUNK, CHUNK)
            mx = logits(mx, kv_s[j, 0, :, lanes], key_codes(at, CHUNK), None, j * CHUNK, CHUNK)
        rows_id = lax.broadcasted_iota(jnp.int32, (TILE, CONT), 0)
        cols = lax.broadcasted_iota(jnp.int32, (TILE, CONT), 1)
        at_k = info[2 + step].astype(F32) + lax.broadcasted_iota(jnp.int32, (8, CONT), 1).astype(F32)
        own_codes = [c[0:1] for c in codes(at_k, tab, pair, -1.0)]
        mx = logits(mx, ko_s[own, lanes], own_codes, cols <= rows_id, PROMPT, CONT)
        m = tops(mx)
        carry = ((zf, zf), (zf, zf))
        for j in range(GDEV):
            carry = weigh(carry, kv_s[j, 1, :, lanes], m, j * CHUNK, CHUNK)
        finish_rows(weigh(carry, vo_s[own, lanes], m, PROMPT, CONT))

    end = pl.num_programs(1) - 1
    for p in range(n_pairs):
        @pl.when((pair == p) & (step == end))
        def _():
            for copy in give(p):
                copy.start()

    @pl.when((pair == last_pair - 1) & (step == 3))
    def _():
        for i in range(2):
            fetch_y[i].wait_recv()
            fetch_core[i].start()

    @pl.when((pair == last_pair) & (step == 0))
    def _():
        for copy in saves():
            copy.start()

    @pl.when((pair == last_pair) & (step == end))
    def _():
        for copy in keeps():
            copy.start()
        fetch_y[2].wait_recv()
        fetch_core[2].start()
        fetch_y[3].wait_recv()
        for copy in fetch_core:
            copy.wait_recv()
        for p in range(n_pairs):
            for copy in give(p):
                copy.wait_recv()
                copy.wait_send()
            if p > 0:
                to_far(p).wait_send()
            to_near(p).wait_send()
            relay(p).wait_send()
        for copy in fetch_y + fetch_core:
            copy.wait_send()
        for copy in keeps() + saves():
            copy.wait()


def attend(info, tab, hid, gain, bias, wq, wk, wv, qb, vb, w1, w2, wo, vec):
    rows = hid.shape[0]
    width = wq.shape[1]
    pairs = width // 128
    span = PROMPT + CONT
    conts = rows - CHUNK
    units = w1.shape[1]
    vmem = pl.BlockSpec(memory_space=pltpu.VMEM)
    hbm = pl.BlockSpec(memory_space=pl.ANY)
    shape = jax.ShapeDtypeStruct
    copies = 3 * pairs + 7 + 2 * pairs
    return pl.pallas_call(
        fwd_kernel,
        grid_spec=pltpu.PrefetchScalarGridSpec(
            num_scalar_prefetch=2,
            grid=(pairs, rows // TILE),
            in_specs=[vmem] * 8 + [hbm] * 4,
            out_specs=[
                pl.BlockSpec((2, TILE, span), lambda a, t, s, f: (a, t, 0)),
                pl.BlockSpec((TILE, 128), lambda a, t, s, f: (t, a)),
            ]
            + [hbm] * 15,
            scratch_shapes=[
                pltpu.VMEM((2, TILE, span), F32),
                pltpu.VMEM((5, 8, PROMPT), F32),
                pltpu.VMEM((GDEV, 2, CHUNK, width), BF),
                pltpu.VMEM((rows, D), BF),
                pltpu.VMEM((rows, width), BF),
                pltpu.VMEM((conts, width), BF),
                pltpu.VMEM((conts, width), BF),
                pltpu.VMEM((rows, width), BF),
                pltpu.SemaphoreType.DMA((copies,)),
                pltpu.SemaphoreType.DMA((copies,)),
                pltpu.SemaphoreType.DMA((6 + 2 * GDEV,)),
            ],
        ),
        out_shape=[
            shape((2 * pairs, rows, span), BF),
            shape((rows, width), F32),
            shape((rows, width), BF),
            shape((conts, width), BF),
            shape((conts, width), BF),
            shape((PROMPT, width), BF),
            shape((PROMPT, width), BF),
            shape((rows, width), BF),
            shape((rows // 2, width), BF),
            shape((rows // 2, width), BF),
            shape((D, units // 2), BF),
            shape((D, units // 2), BF),
            shape((units // 2, D), BF),
            shape((units // 2, D), BF),
            shape((width // 2, D), BF),
            shape((width // 2, D), BF),
            shape(vec.shape, F32),
        ],
        compiler_params=pltpu.CompilerParams(vmem_limit_bytes=56 << 20, collective_id=0, has_side_effects=True),
        cost_estimate=pl.CostEstimate(flops=20 * 10**9, bytes_accessed=60 * 10**6, transcendentals=0),
        name="attend",
    )(info, tab, hid, gain, bias, wq, wk, wv, qb, vb, w1, w2, wo, vec)


def bwd_kernel(info, q_ref, kp_ref, vp_ref, ko_ref, vo_ref, o_ref, li_ref, g_ref, e_ref, dq_ref, dk_ref, dv_ref, dko_ref, dvo_ref, dk_s, dv_s):
    step = pl.program_id(1)
    member = info[0]
    low = low_half(TILE)
    g = g_ref[...].astype(F32) * li_ref[...]
    prod = g * o_ref[...].astype(F32)
    zf = jnp.zeros((TILE, 128), F32)
    deltas = [
        jnp.sum(jnp.where(low, prod, zf), axis=1, keepdims=True),
        jnp.sum(jnp.where(low, zf, prod), axis=1, keepdims=True),
    ]
    gs = [jnp.where(low, g, zf).astype(BF), jnp.where(low, zf, g).astype(BF)]
    gt = jnp.transpose(g).astype(BF)
    qt = jnp.transpose(q_ref[...].astype(F32)).astype(BF)

    def grads(dq, keys, vals, at, width):
        out, dks, dvs = [], [], []
        for h in range(2):
            e = e_ref[h, :, pl.ds(at, width)]
            dp = dot_nt(gs[h], vals)
            ds = (e.astype(F32) * (dp - deltas[h])).astype(BF)
            out.append(dq[h] + dot_nn(ds, keys))
            dks.append(dot_nn(qt[h * HD : (h + 1) * HD, :], ds))
            dvs.append(dot_nn(gt[h * HD : (h + 1) * HD, :], e))
        return tuple(out), dks, dvs

    @pl.when(step == 0)
    def _():
        dk_s[...] = jnp.zeros_like(dk_s)
        dv_s[...] = jnp.zeros_like(dv_s)

    def add(at, width, dks, dvs):
        for h in range(2):
            dk_s[h * HD : (h + 1) * HD, pl.ds(at, width)] += dks[h]
            dv_s[h * HD : (h + 1) * HD, pl.ds(at, width)] += dvs[h]

    def scaled(dq):
        return (jnp.where(low, dq[0], dq[1]).astype(BF).astype(F32) * 0.125).astype(BF)

    @pl.when(step < PTILES)
    def _():
        def one(j, dq):
            at = pl.multiple_of((j ^ member) * CHUNK, CHUNK)
            dq, dks, dvs = grads(dq, kp_ref[pl.ds(at, CHUNK), :], vp_ref[pl.ds(at, CHUNK), :], at, CHUNK)
            add(at, CHUNK, dks, dvs)
            return dq

        dq_ref[...] = scaled(lax.fori_loop(0, member + 1, one, (zf, zf)))
        dko_ref[...] = jnp.zeros_like(dko_ref)
        dvo_ref[...] = jnp.zeros_like(dvo_ref)

    @pl.when(step >= PTILES)
    def _():
        dq = (zf, zf)
        for j in range(GDEV):
            span = slice(j * CHUNK, (j + 1) * CHUNK)
            dq, dks, dvs = grads(dq, kp_ref[span, :], vp_ref[span, :], j * CHUNK, CHUNK)
            add(j * CHUNK, CHUNK, dks, dvs)
        dq, dks, dvs = grads(dq, ko_ref[...], vo_ref[...], PROMPT, CONT)
        dq_ref[...] = scaled(dq)
        dko_ref[...] = jnp.transpose(jnp.concatenate(dks, axis=0)).astype(BF)
        dvo_ref[...] = jnp.transpose(jnp.concatenate(dvs, axis=0)).astype(BF)

    @pl.when(step == pl.num_programs(1) - 1)
    def _():
        for j in range(GDEV):
            span = slice(j * CHUNK, (j + 1) * CHUNK)
            dk_ref[span, :] = jnp.transpose(dk_s[:, span]).astype(BF)
            dv_ref[span, :] = jnp.transpose(dv_s[:, span]).astype(BF)


def attend_back(info, q, k, v, kp, vp, o, li, g, e):
    rows, width = q.shape
    pairs = width // 128
    span = PROMPT + CONT
    tile = pl.BlockSpec((TILE, 128), lambda a, t, s: (t, a))
    whole = pl.BlockSpec((PROMPT, 128), lambda a, t, s: (0, a))
    own = pl.BlockSpec((TILE, 128), lambda a, t, s: (jnp.maximum(t - PTILES, 0), a))
    return pl.pallas_call(
        bwd_kernel,
        grid_spec=pltpu.PrefetchScalarGridSpec(
            num_scalar_prefetch=1,
            grid=(pairs, rows // TILE),
            in_specs=[tile, whole, whole, own, own, tile, tile, tile, pl.BlockSpec((2, TILE, span), lambda a, t, s: (a, t, 0))],
            out_specs=[tile, whole, whole, tile, tile],
            scratch_shapes=[pltpu.VMEM((128, PROMPT), F32), pltpu.VMEM((128, PROMPT), F32)],
        ),
        out_shape=[
            jax.ShapeDtypeStruct((rows, width), BF),
            jax.ShapeDtypeStruct((PROMPT, width), BF),
            jax.ShapeDtypeStruct((PROMPT, width), BF),
            jax.ShapeDtypeStruct((rows, width), BF),
            jax.ShapeDtypeStruct((rows, width), BF),
        ],
        compiler_params=pltpu.CompilerParams(vmem_limit_bytes=48 << 20),
        cost_estimate=pl.CostEstimate(flops=30 * 10**9, bytes_accessed=60 * 10**6, transcendentals=0),
        name="attend_back",
    )(info, q, kp, vp, k, v, o, li, g, e)


UCH = 512


def polynomial(x, terms):
    out = jnp.full_like(x, terms[0])
    for term in terms[1:]:
        out = out * x + term
    return out


def error_function(x):
    x = jnp.clip(x, -3.832506856900711, 3.832506856900711)
    square = x * x
    top = polynomial(
        square,
        (0.00022905065861350646, 0.0034082910107109506, 0.050955695062380861, 0.18520832239976145, 1.128379143519084),
    )
    bottom = polynomial(
        square,
        (
            -1.1791602954361697e-7,
            0.000023547966471313185,
            0.0010179625278914885,
            0.014070470171167667,
            0.11098505178285362,
            0.49746925110067538,
            1.0,
        ),
    )
    return x * top / bottom


def gelu_pair(v):
    phi = 0.5 + 0.5 * error_function(v * 0.7071067811865476)
    density = jnp.exp(-0.5 * v * v) * 0.3989422804014327
    return v * phi, phi + v * density


def column_sum(x):
    return jnp.sum(x, axis=0, keepdims=True)


def mid_kernel(
    info, att_m, att_o, hid, cot, vec_own, vec_got, vec_d, w1_own, w1_got, w1_swap, w2_own, w2_got, w2_swap, wo_own, wo_got, wo_swap,
    out_ref, gatt_m, gatt_o, gmix_ref, packed, su_ref, sw_ref, sd_ref, ext_ref,
    vec_u, vec_w, w1, w2, wo, act_s, shp_s, dg_s, wide_s, acc_s, gmid_s, sub_s, mid_s, low_s, midt_s, cott_s, stage, sems, out_sems,
):
    core = info[0]
    units = w1_own.shape[1]
    width = wo_own.shape[0]
    rows = hid.shape[0]
    full = 2 * units
    half = units // 2
    half_w = width // 2
    here_u = pl.multiple_of(units + core * half, 128)
    there_u = pl.multiple_of(units + (1 - core) * half, 128)
    here_w = pl.multiple_of(width + core * half_w, 64)
    there_w = pl.multiple_of(width + (1 - core) * half_w, 64)
    loads = []
    for i, (src, dst) in enumerate(
        [
            (wo_own, wo.at[pl.ds(0, width), :]),
            (wo_got, wo.at[pl.ds(here_w, half_w), :]),
            (wo_swap, wo.at[pl.ds(there_w, half_w), :]),
            (w1_own, w1.at[:, pl.ds(0, units)]),
            (w1_got, w1.at[:, pl.ds(here_u, half)]),
            (w1_swap, w1.at[:, pl.ds(there_u, half)]),
            (w2_own, w2.at[pl.ds(0, units), :]),
            (w2_got, w2.at[pl.ds(here_u, half), :]),
            (w2_swap, w2.at[pl.ds(there_u, half), :]),
        ]
    ):
        copy = pltpu.make_async_copy(src, dst, sems.at[i])
        copy.start()
        loads.append(copy)

    for i in range(3):
        for j, vec in enumerate((vec_own, vec_got)):
            vec_u[i : i + 1, pl.ds(j * units, units)] = vec[0:1, pl.ds(i * units, units)]
    for i in range(2):
        for j, vec in enumerate((vec_own, vec_got)):
            vec_w[i : i + 1, pl.ds(j * width, width)] = vec[0:1, pl.ds(3 * units + i * width, width)]

    a0 = att_m[...].astype(F32)
    a1 = att_o[...].astype(F32)
    center = (jnp.sum(a0, axis=1, keepdims=True) + jnp.sum(a1, axis=1, keepdims=True)) * (1.0 / D)
    square = (jnp.sum(a0 * a0, axis=1, keepdims=True) + jnp.sum(a1 * a1, axis=1, keepdims=True)) * (1.0 / D)
    sub_scale = lax.rsqrt(square - center * center + EPSILON)
    sub_s[:, 0:width] = (a0 - center) * sub_scale
    sub_s[:, width : 2 * width] = (a1 - center) * sub_scale
    sub_gain = vec_w[0:1, :]
    low_s[...] = (sub_s[...] * sub_gain + vec_w[1:2, :]).astype(BF)
    for copy in loads[0:3]:
        copy.wait()
    mixed = hid[...].astype(F32) + (dot_nn(low_s[...], wo[...]) + vec_d[0:1, pl.ds(0, D)])
    wide_s[...] = mixed
    mean = jnp.mean(mixed, axis=1, keepdims=True)
    mid_scale = lax.rsqrt(jnp.mean(mixed * mixed, axis=1, keepdims=True) - mean * mean + EPSILON)
    mid_s[...] = (mixed - mean) * mid_scale
    mid_gain = vec_d[0:1, pl.ds(768, D)]
    mid_full = mid_s[...] * mid_gain + vec_d[0:1, pl.ds(1536, D)]
    mid_low = mid_full.astype(BF)
    midt_s[...] = jnp.transpose(mid_full).astype(BF)
    cot_full = cot[...].astype(F32)
    cott_s[...] = jnp.transpose(cot_full).astype(BF)
    sd_ref[...] = jnp.zeros_like(sd_ref)
    sd_ref[3:4, :] = column_sum(cot_full)
    for copy in loads[3:6]:
        copy.wait()

    def lanes_sum(x):
        total = x[:, 0:128]
        for i in range(1, x.shape[1] // 128):
            total = total + x[:, i * 128 : (i + 1) * 128]
        return total

    def first(c, carry):
        at = pl.multiple_of(c * UCH, UCH)
        inner = dot_nn(mid_low, w1[:, pl.ds(at, UCH)]) + vec_u[2:3, pl.ds(at, UCH)]
        act, slope = gelu_pair(inner)
        act_s[:, pl.ds(at, UCH)] = act
        dg_s[:, pl.ds(at, UCH)] = slope.astype(BF)
        return carry[0] + lanes_sum(act), carry[1] + lanes_sum(act * act)

    zero = jnp.zeros((rows, 128), F32)
    act_sum, act_square = lax.fori_loop(0, full // UCH, first, (zero, zero))
    ffn_center = jnp.sum(act_sum, axis=1, keepdims=True) * (1.0 / full)
    ffn_scale = lax.rsqrt(
        jnp.sum(act_square, axis=1, keepdims=True) * (1.0 / full) - ffn_center * ffn_center + EPSILON
    )
    for copy in loads[6:9]:
        copy.wait()
    acc_s[...] = jnp.zeros_like(acc_s)
    per = units // UCH
    wide = 2 * units + width

    def column_of(c, extra):
        return pl.multiple_of((c // per) * wide + lax.rem(c, per) * UCH + extra, 128)

    def send(slot, column):
        return pltpu.make_async_copy(stage.at[slot], packed.at[:, pl.ds(column, UCH)], out_sems.at[slot])

    def put(c, value, extra):
        slot = lax.rem(c, 2)

        @pl.when(c >= 2)
        def _():
            send(slot, column_of(c - 2, extra)).wait()

        stage[slot] = value
        send(slot, column_of(c, extra)).start()

    def drain(extra):
        for c in range(full // UCH - 2, full // UCH):
            send(c % 2, column_of(c, extra)).wait()

    def second(c, carry):
        at = pl.multiple_of(c * UCH, UCH)
        unit = (act_s[:, pl.ds(at, UCH)] - ffn_center) * ffn_scale
        act_s[:, pl.ds(at, UCH)] = unit
        gain = vec_u[0:1, pl.ds(at, UCH)]
        low = (unit * gain + vec_u[1:2, pl.ds(at, UCH)]).astype(BF)
        acc_s[...] += dot_nn(low, w2[pl.ds(at, UCH), :])
        grad = dot_nt(cot[...], w2[pl.ds(at, UCH), :])
        cross = grad * unit
        su_ref[0:1, pl.ds(at, UCH)] = column_sum(cross)
        su_ref[1:2, pl.ds(at, UCH)] = column_sum(grad)
        shaped = grad * gain
        shp_s[:, pl.ds(at, UCH)] = shaped
        put(c, dot_nn(cott_s[...], low).astype(BF), units)
        return carry[0] + lanes_sum(shaped), carry[1] + lanes_sum(shaped * unit)

    su_ref[...] = jnp.zeros_like(su_ref)
    s_sum, s_cross = lax.fori_loop(0, full // UCH, second, (zero, zero))
    drain(units)
    shaped_mean = jnp.sum(s_sum, axis=1, keepdims=True) * (1.0 / full)
    cross_mean = jnp.sum(s_cross, axis=1, keepdims=True) * (1.0 / full)
    out_ref[...] = (wide_s[...] + (acc_s[...] + vec_d[0:1, pl.ds(2304, D)])).astype(BF)
    gmid_s[...] = jnp.zeros_like(gmid_s)

    def third(c, carry):
        at = pl.multiple_of(c * UCH, UCH)
        g = ffn_scale * (shp_s[:, pl.ds(at, UCH)] - shaped_mean - act_s[:, pl.ds(at, UCH)] * cross_mean)
        low = (g * dg_s[:, pl.ds(at, UCH)].astype(F32)).astype(BF)
        su_ref[2:3, pl.ds(at, UCH)] = column_sum(low.astype(F32))
        gmid_s[...] += dot_nt(low, w1[:, pl.ds(at, UCH)])
        put(c, dot_nn(midt_s[...], low).astype(BF), 0)
        return carry

    lax.fori_loop(0, full // UCH, third, 0)
    drain(0)

    grad_mid = gmid_s[...]
    unit = mid_s[...]
    sd_ref[1:2, :] = column_sum(grad_mid * unit)
    sd_ref[2:3, :] = column_sum(grad_mid)
    shaped = grad_mid * mid_gain
    grad_mixed = cot[...].astype(F32) + mid_scale * (
        shaped - jnp.mean(shaped, axis=1, keepdims=True) - unit * jnp.mean(shaped * unit, axis=1, keepdims=True)
    )
    branch = grad_mixed.astype(BF)
    gmix_ref[...] = branch
    branch_f = branch.astype(F32)
    sd_ref[0:1, :] = column_sum(branch_f)
    out_grad = dot_nn(jnp.transpose(branch_f).astype(BF), low_s[...]).astype(BF)
    stage[0, :, 0:width] = out_grad[:, 0:width]
    stage[1, :, 0:width] = out_grad[:, width : 2 * width]
    last = [
        pltpu.make_async_copy(stage.at[i, :, pl.ds(0, width)], packed.at[:, pl.ds(i * wide + 2 * units, width)], out_sems.at[i])
        for i in range(2)
    ]
    for copy in last:
        copy.start()
    grad_sub = dot_nt(branch, wo[...])
    unit = sub_s[...]
    cross = grad_sub * unit
    sw_ref[...] = jnp.zeros_like(sw_ref)
    sw_ref[0:1, :] = column_sum(cross)
    sw_ref[1:2, :] = column_sum(grad_sub)
    shaped = grad_sub * sub_gain
    grad_att = sub_scale * (
        shaped - jnp.mean(shaped, axis=1, keepdims=True) - unit * jnp.mean(shaped * unit, axis=1, keepdims=True)
    )
    gatt_m[...] = grad_att[:, 0:width].astype(BF)
    gatt_o[...] = grad_att[:, width : 2 * width].astype(BF)
    parts = ext_ref.shape[0]
    if parts > 1:
        sums_u, sums_w, sums_d = su_ref[...], sw_ref[...], sd_ref[...]
        for i in range(parts):
            ext_ref[i] = jnp.concatenate(
                [
                    window(sums_u, i * (units // parts)),
                    window(sums_u, units + i * (units // parts)),
                    window(sums_w, i * (width // parts)),
                    window(sums_w, width + i * (width // parts)),
                    window(sums_d, i * (D // parts)),
                    jnp.zeros((8, 128), F32),
                ],
                axis=0,
            ).astype(BF)
    for copy in last:
        copy.wait()


def window(rows8, start):
    base = start // 128 * 128
    size = min(256, rows8.shape[1] - base)
    view = rows8[:, base : base + size]
    shift = start - base
    if shift:
        view = pltpu.roll(view, size - shift, 1)
    return view[:, 0:128]


def middle(core, att_m, att_o, hid, cot, vec_own, vec_got, vec_d, w1, w2, wo, parts):
    rows = hid.shape[0]
    units = w1[0].shape[1]
    width = wo[0].shape[0]
    vmem = pl.BlockSpec(memory_space=pltpu.VMEM)
    hbm = pl.BlockSpec(memory_space=pl.ANY)
    shape = jax.ShapeDtypeStruct
    return pl.pallas_call(
        mid_kernel,
        in_specs=[pl.BlockSpec(memory_space=pltpu.SMEM)] + [vmem] * 7 + [hbm] * 9,
        out_specs=[vmem] * 4 + [hbm] + [vmem] * 4,
        out_shape=[
            shape((rows, D), BF),
            shape((rows, width), BF),
            shape((rows, width), BF),
            shape((rows, D), BF),
            shape((D, 2 * (2 * units + width)), BF),
            shape((8, 2 * units), F32),
            shape((8, 2 * width), F32),
            shape((8, D), F32),
            shape((parts, 48, 128), BF),
        ],
        scratch_shapes=[
            pltpu.VMEM((8, 2 * units), F32),
            pltpu.VMEM((8, 2 * width), F32),
            pltpu.VMEM((D, 2 * units), BF),
            pltpu.VMEM((2 * units, D), BF),
            pltpu.VMEM((2 * width, D), BF),
            pltpu.VMEM((rows, 2 * units), F32),
            pltpu.VMEM((rows, 2 * units), F32),
            pltpu.VMEM((rows, 2 * units), BF),
            pltpu.VMEM((rows, D), F32),
            pltpu.VMEM((rows, D), F32),
            pltpu.VMEM((rows, D), F32),
            pltpu.VMEM((rows, 2 * width), F32),
            pltpu.VMEM((rows, D), F32),
            pltpu.VMEM((rows, 2 * width), BF),
            pltpu.VMEM((D, rows), BF),
            pltpu.VMEM((D, rows), BF),
            pltpu.VMEM((2, D, UCH), BF),
            pltpu.SemaphoreType.DMA((9,)),
            pltpu.SemaphoreType.DMA((2,)),
        ],
        compiler_params=pltpu.CompilerParams(vmem_limit_bytes=62 << 20),
        cost_estimate=pl.CostEstimate(flops=21 * 10**9, bytes_accessed=30 * 10**6, transcendentals=0),
        name="middle",
    )(core, att_m, att_o, hid, cot, vec_own, vec_got, vec_d, *w1, *w2, *wo)


def final_kernel(
    bits, hid, gain, bias, dq, dk, dv, wq, wk, wv, gmix, ext, kp, vp,
    gin, late_out, vec_out,
    near_s, loc_s, relay_s, far_s, unit_s, mine_s, norm_s, send_c, recv_c, send_p, recv_p, give_c, give_p, late_s, small_s,
    vec_s, vec_r, sems_a, sems_b, loc_sems, *stage_refs,
):
    device = lax.axis_index("dp")
    side = lax.axis_index("tensor")
    across = {"dp": device, "tensor": 1 - side}
    peers = [{"dp": bit_peer(device, b), "tensor": side} for b in range(bits)]
    rows, width = dq.shape
    prompt = kp.shape[0] // GDEV
    conts = rows - prompt
    half_p, half_c = prompt // 2, conts // 2
    own_p = pl.multiple_of(side * half_p, 128)
    their_p = pl.multiple_of((1 - side) * half_p, 128)
    own_c = pl.multiple_of(prompt + side * half_c, 128)
    their_c = pl.multiple_of(prompt + (1 - side) * half_c, 128)
    lanes = 3 * width + 128

    greet(peers + [across])
    count = [0]

    def remote(src, dst, peer):
        i = count[0]
        count[0] += 1
        copy = pltpu.make_async_remote_copy(
            src_ref=src, dst_ref=dst, send_sem=sems_a.at[i], recv_sem=sems_b.at[i], device_id=peer, device_id_type=MESH
        )
        copy.start()
        return copy

    first = []
    for i, part in enumerate((kp, vp)):
        first.append(remote(part.at[pl.ds(3 * prompt, prompt), :], near_s.at[2 * i + 1], peers[0]))
        first.append(remote(part.at[pl.ds(prompt, prompt), :], near_s.at[2 * i], peers[0]))
    local = []
    for i, part in enumerate((kp, vp)):
        for j in range(2):
            copy = pltpu.make_async_copy(part.at[pl.ds(2 * j * prompt, prompt), :], loc_s.at[2 * i + j], loc_sems.at[2 * i + j])
            copy.start()
            local.append(copy)

    gain_f = gain[...]
    bias_f = bias[...]

    def unit_rows(at, size):
        x = hid[pl.ds(at, size), :].astype(F32)
        center = jnp.mean(x, axis=1, keepdims=True)
        scale = lax.rsqrt(jnp.mean(x * x, axis=1, keepdims=True) - center * center + EPSILON)
        return (x - center) * scale, scale

    def part_of(at, size, k_rows, v_rows):
        return dot_nt(dq[pl.ds(at, size), :], wq[...]) + dot_nt(k_rows, wk[...]) + dot_nt(v_rows, wv[...])

    def gather(part, unit):
        return column_sum(part * unit), column_sum(part)

    unit, _ = unit_rows(their_c, half_c)
    part = part_of(their_c, half_c, dk[pl.ds(their_c, half_c), :], dv[pl.ds(their_c, half_c), :])
    send_c[...] = part.astype(BF)
    y_cont = remote(send_c, recv_c, across)
    gain_grad, bias_grad = gather(part, unit)
    norm_s[:, pl.ds(their_c, half_c)] = jnp.transpose(unit * gain_f + bias_f).astype(BF)
    unit, scale_c = unit_rows(own_c, half_c)
    part = part_of(own_c, half_c, dk[pl.ds(own_c, half_c), :], dv[pl.ds(own_c, half_c), :])
    mine_s[pl.ds(half_p, half_c), :] = part
    unit_s[pl.ds(half_p, half_c), :] = unit
    g, b = gather(part, unit)
    gain_grad, bias_grad = gain_grad + g, bias_grad + b
    norm_s[:, pl.ds(own_c, half_c)] = jnp.transpose(unit * gain_f + bias_f).astype(BF)

    for copy in local:
        copy.wait()
    for copy in first:
        copy.wait_recv()
    second = []
    for i in range(2):
        relay_s[i] = (loc_s[2 * i + 1].astype(F32) + near_s[2 * i + 1].astype(F32)).astype(BF)
        second.append(remote(relay_s.at[i], far_s.at[i], peers[1]))

    unit, _ = unit_rows(their_p, half_p)
    norm_s[:, pl.ds(their_p, half_p)] = jnp.transpose(unit * gain_f + bias_f).astype(BF)
    unit, scale_p = unit_rows(own_p, half_p)
    unit_s[pl.ds(0, half_p), :] = unit
    norm_s[:, pl.ds(own_p, half_p)] = jnp.transpose(unit * gain_f + bias_f).astype(BF)

    blocks = 1 << bits
    block = D // blocks

    def keep(value, lane):
        low = value.astype(BF)
        for i in range(blocks):
            late_s[i // 2, i % 2, :, pl.ds(lane, width)] = low[i * block : (i + 1) * block, :]

    keep(dot_nn(norm_s[...], dq[...]), 0)
    q_bias = column_sum(dq[...].astype(F32))

    def norm_back(total, unit, scale, mixed):
        shaped = total * gain_f
        return mixed.astype(F32) + scale * (
            shaped - jnp.mean(shaped, axis=1, keepdims=True) - unit * jnp.mean(shaped * unit, axis=1, keepdims=True)
        )

    y_cont.wait_recv()
    total = mine_s[pl.ds(half_p, half_c), :] + recv_c[...].astype(F32)
    give_c[...] = norm_back(total, unit_s[pl.ds(half_p, half_c), :], scale_c, gmix[pl.ds(half_p, half_c), :]).astype(BF)
    back_c = remote(give_c, gin.at[pl.ds(own_c, half_c), :], across)
    keep_c = pltpu.make_async_copy(give_c, gin.at[pl.ds(own_c, half_c), :], loc_sems.at[4])
    keep_c.start()

    for copy in second:
        copy.wait_recv()
    for i in range(2):
        loc_s[2 * i] = (loc_s[2 * i].astype(F32) + near_s[2 * i].astype(F32) + far_s[i].astype(F32)).astype(BF)
    part = part_of(their_p, half_p, loc_s[0, pl.ds(their_p, half_p), :], loc_s[2, pl.ds(their_p, half_p), :])
    send_p[...] = part.astype(BF)
    y_prompt = remote(send_p, recv_p, across)
    unit, _ = unit_rows(their_p, half_p)
    g, b = gather(part, unit)
    gain_grad, bias_grad = gain_grad + g, bias_grad + b
    part = part_of(own_p, half_p, loc_s[0, pl.ds(own_p, half_p), :], loc_s[2, pl.ds(own_p, half_p), :])
    mine_s[pl.ds(0, half_p), :] = part
    g, b = gather(part, unit_s[pl.ds(0, half_p), :])
    gain_grad, bias_grad = gain_grad + g, bias_grad + b

    for i, rest in enumerate((dk, dv)):
        keep(
            dot_nn(norm_s[:, pl.ds(0, prompt)], loc_s[2 * i])
            + dot_nn(norm_s[:, pl.ds(prompt, conts)], rest[pl.ds(prompt, conts), :]),
            (i + 1) * width,
        )
    v_bias = column_sum(loc_s[2].astype(F32)) + column_sum(dv[pl.ds(prompt, conts), :].astype(F32))

    small_s[...] = jnp.zeros_like(small_s)
    small_s[0:1, pl.ds(0, width)] = q_bias
    small_s[1:2, pl.ds(0, width)] = v_bias
    small_s[2:3, pl.ds(0, D)] = gain_grad
    small_s[3:4, pl.ds(0, D)] = bias_grad
    small = small_s[...]
    row_id = lax.broadcasted_iota(jnp.int32, (8, 128), 0)
    for i in range(blocks):
        narrow = window(small, i * (width // blocks))
        broad = window(small, i * block)
        tail = jnp.concatenate([ext[i, pl.ds(32, 16), :].astype(F32)[0:8], jnp.where(row_id < 2, narrow, broad)], axis=0)
        late_s[i // 2, i % 2, pl.ds(0, 32), pl.ds(3 * width, 128)] = ext[i, pl.ds(0, 32), :]
        late_s[i // 2, i % 2, pl.ds(32, 16), pl.ds(3 * width, 128)] = tail.astype(BF)

    source = late_s
    stages = []
    for bit in range(bits):
        landing, kept = stage_refs[2 * bit], stage_refs[2 * bit + 1]
        mine = (device // (1 << bit)) % 2
        copy = remote(source.at[:, 1 - mine], landing, peers[bit])
        if bit == 0:
            y_prompt.wait_recv()
            total = mine_s[pl.ds(0, half_p), :] + recv_p[...].astype(F32)
            give_p[...] = norm_back(total, unit_s[pl.ds(0, half_p), :], scale_p, gmix[pl.ds(0, half_p), :]).astype(BF)
            back_p = remote(give_p, gin.at[pl.ds(own_p, half_p), :], across)
            keep_p = pltpu.make_async_copy(give_p, gin.at[pl.ds(own_p, half_p), :], loc_sems.at[5])
            keep_p.start()
        copy.wait_recv()
        stages.append(copy)
        for i in range(landing.shape[0]):
            kept[i // 2, i % 2] = (source[i, mine].astype(F32) + landing[i].astype(F32)).astype(BF)
        source = kept
    late_out[...] = source[0, 0, :, pl.ds(0, 3 * width)].astype(F32)
    vec_s[...] = source[0, 0, :, pl.ds(3 * width, 128)]
    swap = remote(vec_s, vec_r, across)
    swap.wait_recv()
    vec_out[0] = vec_s[...].astype(F32)
    vec_out[1] = vec_r[...].astype(F32)
    for copy in first + second + stages + [y_cont, y_prompt, swap]:
        copy.wait_send()
    for copy in (back_c, back_p):
        copy.wait_recv()
        copy.wait_send()
    keep_c.wait()
    keep_p.wait()


def finish(hid, gain, bias, dq, dk, dv, wq, wk, wv, gmix, ext, kp, vp):
    rows, width = dq.shape
    ranks = lax.axis_size("dp")
    bits = ranks.bit_length() - 1
    block = D // ranks
    prompt = kp.shape[0] // GDEV
    conts = rows - prompt
    lanes = 3 * width + 128
    vmem = pl.BlockSpec(memory_space=pltpu.VMEM)
    hbm = pl.BlockSpec(memory_space=pl.ANY)
    shape = jax.ShapeDtypeStruct
    copies = 11 + bits
    stages = []
    for bit in range(bits):
        left = ranks >> (bit + 1)
        stages.append(pltpu.VMEM((left, block, lanes), BF))
        stages.append(pltpu.VMEM((max(left // 2, 1), min(left, 2), block, lanes), BF))
    return pl.pallas_call(
        functools.partial(final_kernel, bits),
        in_specs=[vmem] * 11 + [hbm] * 2,
        out_specs=[hbm, vmem, vmem],
        out_shape=[shape((rows, D), BF), shape((block, 3 * width), F32), shape((2, block, 128), F32)],
        scratch_shapes=[
            pltpu.VMEM((4, prompt, width), BF),
            pltpu.VMEM((4, prompt, width), BF),
            pltpu.VMEM((2, prompt, width), BF),
            pltpu.VMEM((2, prompt, width), BF),
            pltpu.VMEM((rows // 2, D), F32),
            pltpu.VMEM((rows // 2, D), F32),
            pltpu.VMEM((D, rows), BF),
            pltpu.VMEM((conts // 2, D), BF),
            pltpu.VMEM((conts // 2, D), BF),
            pltpu.VMEM((prompt // 2, D), BF),
            pltpu.VMEM((prompt // 2, D), BF),
            pltpu.VMEM((conts // 2, D), BF),
            pltpu.VMEM((prompt // 2, D), BF),
            pltpu.VMEM((ranks // 2, 2, block, lanes), BF),
            pltpu.VMEM((8, D + 128), F32),
            pltpu.VMEM((block, 128), BF),
            pltpu.VMEM((block, 128), BF),
            pltpu.SemaphoreType.DMA((copies,)),
            pltpu.SemaphoreType.DMA((copies,)),
            pltpu.SemaphoreType.DMA((6,)),
        ]
        + stages,
        compiler_params=pltpu.CompilerParams(vmem_limit_bytes=56 << 20, collective_id=1, has_side_effects=True),
        cost_estimate=pl.CostEstimate(flops=5 * 10**9, bytes_accessed=20 * 10**6, transcendentals=0),
        name="finish",
    )(hid, gain, bias, dq, dk, dv, wq, wk, wv, gmix, ext, kp, vp)


def flip(value, axis, bit):
    return lax.ppermute(value, axis, [(i, i ^ (1 << bit)) for i in range(lax.axis_size(axis))])


def contract_rows(left, right):
    return lax.dot_general(left, right, (((0,), (0,)), ((), ())), preferred_element_type=F32)


def back_project(left, right):
    return lax.dot_general(left, right, (((1,), (1,)), ((), ())), preferred_element_type=F32)


def norm_rows(values, gain, bias):
    center = jnp.mean(values, axis=-1, keepdims=True)
    spread = jnp.mean(values * values, axis=-1, keepdims=True) - center * center
    scaled = lax.rsqrt(spread + EPSILON)
    unit_rows = (values - center) * scaled
    return (unit_rows * gain + bias, unit_rows, scaled)


def norm_back(grad_rows, gain, unit_rows, scaled):
    shaped = grad_rows * gain
    return scaled * (
        shaped
        - jnp.mean(shaped, axis=-1, keepdims=True)
        - unit_rows * jnp.mean(shaped * unit_rows, axis=-1, keepdims=True)
    )


def in_order(which, mine, other, axis):
    return jnp.where(
        which == 0,
        jnp.concatenate([mine, other], axis=axis),
        jnp.concatenate([other, mine], axis=axis),
    )


def halving(value, device):
    bits = lax.axis_size("dp").bit_length() - 1
    rows, columns = value.shape
    current = value
    for bit in range(bits):
        upper = device // (1 << bit) % 2
        left = bits - bit
        view = current.reshape((1 << (left - 1), 2, -1, columns))
        kept = lax.dynamic_index_in_dim(view, upper, 1, keepdims=False)
        sent = lax.dynamic_index_in_dim(view, 1 - upper, 1, keepdims=False)
        got = flip(sent, "dp", bit)
        current = (kept.astype(F32) + got.astype(F32)).astype(BF)
    return current.reshape(rows >> bits, columns)


def half_of(value, which):
    prompt, conts = CHUNK // 2, (value.shape[0] - CHUNK) // 2
    return jnp.concatenate(
        [
            lax.dynamic_slice_in_dim(value, which * prompt, prompt),
            lax.dynamic_slice_in_dim(value, CHUNK + which * conts, conts),
        ]
    )


def joined(which, mine, other):
    prompt = CHUNK // 2
    low = jnp.where(which == 0, mine, other)
    high = jnp.where(which == 0, other, mine)
    return jnp.concatenate([low[:prompt], high[:prompt], low[prompt:], high[prompt:]])


def body(
    hidden_in,
    cotangent,
    prompt_start,
    cont_gap,
    seg_len,
    dilation_rate,
    pre_gain,
    pre_bias,
    query_weight,
    query_bias,
    key_weight,
    value_weight,
    value_bias,
    sub_gain,
    sub_bias,
    out_weight,
    out_bias,
    mid_gain,
    mid_bias,
    inner_weight,
    inner_bias,
    ffn_gain,
    ffn_bias,
    outer_weight,
    outer_bias,
):
    device = lax.axis_index("dp")
    ranks = lax.axis_size("dp")
    group_id = device // GDEV
    member = device % GDEV
    tensor_id = lax.axis_index("tensor")
    core = device % 2
    width = query_weight.shape[1]
    units = inner_weight.shape[1]
    pairs = width // 128
    rows = hidden_in.shape[0]
    prompt_rows = CHUNK
    cont_count = (rows - prompt_rows) // CONT

    start_at = lax.dynamic_index_in_dim(prompt_start, group_id, 0, keepdims=False)
    gap_row = lax.dynamic_index_in_dim(cont_gap, group_id, 0, keepdims=False)
    own_gaps = lax.dynamic_slice_in_dim(gap_row, member * cont_count, cont_count)
    info = jnp.concatenate(
        [
            jnp.stack([member, start_at]),
            start_at + member * prompt_rows + TILE * jnp.arange(PTILES),
            start_at + PROMPT + own_gaps,
        ]
    ).astype(jnp.int32)
    seg = lax.dynamic_slice_in_dim(seg_len, tensor_id * pairs, pairs, 0)
    rate = lax.dynamic_slice_in_dim(dilation_rate, tensor_id * pairs, pairs, 0)
    head = 2 * (tensor_id * pairs + jnp.arange(pairs))
    tab = jnp.stack(
        [
            1.0 / seg[:, 0].astype(F32),
            1.0 / seg[:, 1].astype(F32),
            rate[:, 1].astype(F32),
            1.0 / rate[:, 1].astype(F32),
            rate[:, 2].astype(F32),
            1.0 / rate[:, 2].astype(F32),
            (head % rate[:, 1]).astype(F32),
            ((head + 1) % rate[:, 1]).astype(F32),
            (head % rate[:, 2]).astype(F32),
            ((head + 1) % rate[:, 2]).astype(F32),
        ],
        axis=1,
    ).reshape(-1)

    vectors = jnp.concatenate([ffn_gain, ffn_bias, inner_bias, sub_gain, sub_bias]).astype(F32)[None]
    shared = jnp.concatenate([out_bias, mid_gain, mid_bias, outer_bias]).astype(F32)[None]
    pre_gain_f = pre_gain.astype(F32)

    (
        weighed,
        inverse,
        queries,
        keys,
        values,
        prompt_keys,
        prompt_values,
        attended,
        att_mine,
        att_got,
        *pieces,
        vectors_other,
    ) = attend(
        info,
        tab,
        hidden_in,
        pre_gain_f[None],
        pre_bias.astype(F32)[None],
        query_weight,
        key_weight,
        value_weight,
        query_bias.astype(F32)[None],
        value_bias.astype(F32)[None],
        inner_weight,
        outer_weight,
        out_weight,
        vectors,
    )
    inner_parts = (inner_weight, pieces[0], pieces[1])
    outer_parts = (outer_weight, pieces[2], pieces[3])
    out_parts = (out_weight, pieces[4], pieces[5])

    hidden_rows = half_of(hidden_in, tensor_id)
    cot_rows = half_of(cotangent, tensor_id)
    fused = D % (16 * ranks) == 0
    out_half, grad_mine, grad_theirs, grad_mixed_low, packed, sum_u, sum_w, sum_d, ext = middle(
        core[None].astype(jnp.int32),
        att_mine,
        att_got,
        hidden_rows,
        cot_rows,
        vectors,
        vectors_other,
        shared,
        inner_parts,
        outer_parts,
        out_parts,
        ranks if fused else 1,
    )

    grad_got = flip(grad_theirs, "tensor", 0)
    grad_attended = joined(tensor_id, grad_mine, grad_got)

    early = lax.psum_scatter(packed, "dp", scatter_dimension=0, tiled=True)
    early_mine, early_other = jnp.split(early, 2, axis=1)
    early_sum = early_mine.astype(F32) + flip(early_other, "tensor", 0).astype(F32)
    inner_weight_grad = early_sum[:, :units]
    outer_weight_grad = early_sum[:, units : 2 * units].T
    out_weight_grad = early_sum[:, 2 * units :].T

    output = joined(tensor_id, out_half, flip(out_half, "tensor", 0))

    grad_query_in, key_acc, value_acc, own_key_grad, own_value_grad = attend_back(
        info, queries, keys, values, prompt_keys, prompt_values, attended, inverse, grad_attended, weighed
    )
    block = D // ranks
    per_u, per_w, per_d = units // ranks, width // ranks, D // ranks
    if fused:
        input_low, late, vec = finish(
            hidden_in,
            pre_gain_f[None],
            pre_bias.astype(F32)[None],
            grad_query_in,
            own_key_grad,
            own_value_grad,
            query_weight,
            key_weight,
            value_weight,
            grad_mixed_low,
            ext,
            key_acc,
            value_acc,
        )
        ffn_gain_grad, ffn_bias_grad, inner_bias_grad = [vec[0, i, :per_u] + vec[1, 8 + i, :per_u] for i in range(3)]
        sub_gain_grad, sub_bias_grad = [vec[0, 16 + i, :per_w] + vec[1, 24 + i, :per_w] for i in range(2)]
        out_bias_grad, mid_gain_grad, mid_bias_grad, outer_bias_grad = [
            vec[0, 32 + i, :per_d] + vec[1, 32 + i, :per_d] for i in range(4)
        ]
        query_bias_grad, value_bias_grad = [vec[0, 40 + i, :per_w] for i in range(2)]
        pre_gain_grad, pre_bias_grad = [vec[0, 42 + i, :per_d] + vec[1, 42 + i, :per_d] for i in range(2)]
    else:
        pre_normed, pre_unit, pre_scale = norm_rows(hidden_in.astype(F32), pre_gain_f, pre_bias.astype(F32))
        pre_low = pre_normed.astype(BF)
        acc = jnp.stack([key_acc, value_acc]).reshape(2, GDEV, prompt_rows, width)
        near = acc[:, 0::2].astype(F32) + flip(acc[:, 1::2], "dp", 0).astype(F32)
        summed = (near[:, 0] + flip(near[:, 1].astype(BF), "dp", 1).astype(F32)).astype(BF)
        grad_keys = jnp.concatenate([summed[0], own_key_grad[prompt_rows:]], axis=0)
        grad_values = jnp.concatenate([summed[1], own_value_grad[prompt_rows:]], axis=0)

        query_weight_grad = contract_rows(pre_low, grad_query_in)
        key_weight_grad = contract_rows(pre_low, grad_keys)
        value_weight_grad = contract_rows(pre_low, grad_values)
        query_bias_grad = jnp.sum(grad_query_in.astype(F32), axis=0)
        value_bias_grad = jnp.sum(grad_values.astype(F32), axis=0)
        grad_normed_part = (
            back_project(grad_query_in, query_weight)
            + back_project(grad_keys, key_weight)
            + back_project(grad_values, value_weight)
        )
        grad_normed_low = grad_normed_part.astype(BF)
        grad_normed = grad_normed_low.astype(F32) + flip(grad_normed_low, "tensor", 0).astype(F32)
        pre_gain_grad = jnp.sum(grad_normed * pre_unit, axis=0)
        pre_bias_grad = jnp.sum(grad_normed, axis=0)
        grad_mixed_all = joined(tensor_id, grad_mixed_low, flip(grad_mixed_low, "tensor", 0)).astype(F32)
        input_low = (grad_mixed_all + norm_back(grad_normed, pre_gain_f, pre_unit, pre_scale)).astype(BF)

        vec = jnp.concatenate(
            [
                sum_u[:3].reshape(3, 2, ranks, per_u).transpose(2, 1, 0, 3).reshape(ranks, 6 * per_u),
                sum_w[:2].reshape(2, 2, ranks, per_w).transpose(2, 1, 0, 3).reshape(ranks, 4 * per_w),
                sum_d[:4].reshape(4, ranks, per_d).swapaxes(0, 1).reshape(ranks, 4 * per_d),
                jnp.stack([query_bias_grad, value_bias_grad]).reshape(2, ranks, per_w).swapaxes(0, 1).reshape(ranks, 2 * per_w),
                jnp.stack([pre_gain_grad, pre_bias_grad]).reshape(2, ranks, per_d).swapaxes(0, 1).reshape(ranks, 2 * per_d),
            ],
            axis=1,
        )
        count = vec.shape[1]
        vec = jnp.pad(vec, ((0, 0), (0, block * 128 - count))).reshape(D, 128)
        late = halving(
            jnp.concatenate(
                [p.astype(BF) for p in (query_weight_grad, key_weight_grad, value_weight_grad, vec)], axis=1
            ),
            device,
        )
        vec = late[:, 3 * width :].reshape(-1)[:count]
        late = late[:, : 3 * width].astype(F32)
        at_w = 6 * per_u
        at_d = at_w + 4 * per_w
        at_late = at_d + 4 * per_d
        got = flip(vec[:at_late], "tensor", 0).astype(F32)
        vec = vec.astype(F32)
        ffn_gain_grad, ffn_bias_grad, inner_bias_grad = (vec[: 3 * per_u] + got[3 * per_u : at_w]).reshape(3, per_u)
        sub_gain_grad, sub_bias_grad = (vec[at_w : at_w + 2 * per_w] + got[at_w + 2 * per_w : at_d]).reshape(2, per_w)
        out_bias_grad, mid_gain_grad, mid_bias_grad, outer_bias_grad = (vec[at_d:at_late] + got[at_d:]).reshape(4, per_d)
        query_bias_grad, value_bias_grad = vec[at_late : at_late + 2 * per_w].reshape(2, per_w)
        pre_gain_grad, pre_bias_grad = vec[at_late + 2 * per_w :].reshape(2, per_d)
    return (
        output,
        input_low,
        pre_gain_grad,
        pre_bias_grad,
        late[:, :width],
        query_bias_grad,
        late[:, width : 2 * width],
        late[:, 2 * width : 3 * width],
        value_bias_grad,
        sub_gain_grad,
        sub_bias_grad,
        out_weight_grad,
        out_bias_grad,
        mid_gain_grad,
        mid_bias_grad,
        inner_weight_grad,
        inner_bias_grad,
        ffn_gain_grad,
        ffn_bias_grad,
        outer_weight_grad,
        outer_bias_grad,
    )

def solution(mesh):
    placed = (
        P("dp", None),
        P("dp", None),
        P(),
        P(),
        P(),
        P(),
        P(),
        P(),
        P(None, "tensor"),
        P("tensor"),
        P(None, "tensor"),
        P(None, "tensor"),
        P("tensor"),
        P("tensor"),
        P("tensor"),
        P("tensor", None),
        P(),
        P(),
        P(),
        P(None, "tensor"),
        P("tensor"),
        P("tensor"),
        P("tensor"),
        P("tensor", None),
        P(),
    )
    return jax.shard_map(
        body,
        mesh=mesh,
        in_specs=placed,
        out_specs=(
            P("dp", None),
            P("dp", None),
            P("dp"),
            P("dp"),
            P("dp", "tensor"),
            P(("tensor", "dp")),
            P("dp", "tensor"),
            P("dp", "tensor"),
            P(("tensor", "dp")),
            P(("tensor", "dp")),
            P(("tensor", "dp")),
            P("tensor", "dp"),
            P("dp"),
            P("dp"),
            P("dp"),
            P("dp", "tensor"),
            P(("tensor", "dp")),
            P(("tensor", "dp")),
            P(("tensor", "dp")),
            P("tensor", "dp"),
            P("dp"),
        ),
        check_vma=False,
    )
```

```python
import functools

import jax
import jax.numpy as jnp
from jax import lax
from jax.experimental import pallas as pl
from jax.experimental.pallas import tpu as pltpu
from jax.sharding import PartitionSpec as P

HD = 64
PROMPT = 2048
CONT = 256
GDEV = 4
TILE = 256
CHUNK = PROMPT // GDEV
PTILES = CHUNK // TILE
LOG2E = 1.4426950408889634
BF = jnp.bfloat16
F32 = jnp.float32
TAB = 10
D = 768
EPSILON = 1e-05
MESH = pl.DeviceIdType.MESH


def dot_nt(a, b):
    return lax.dot_general(a, b, (((1,), (1,)), ((), ())), preferred_element_type=F32)


def dot_nn(a, b):
    return lax.dot_general(a, b, (((1,), (0,)), ((), ())), preferred_element_type=F32)


def low_half(rows):
    return lax.broadcasted_iota(jnp.int32, (rows, 128), 1) < HD


def codes(at, tab, pair, miss):
    def cell(i):
        return tab[pair * TAB + i]

    first = jnp.floor((at + 0.5) * cell(0))
    second = jnp.floor((at + 0.5) * cell(1))
    rest1 = at - cell(2) * jnp.floor((at + 0.5) * cell(3))
    rest2 = at - cell(4) * jnp.floor((at + 0.5) * cell(5))
    return [
        first,
        jnp.where(rest1 == cell(6), second, miss),
        jnp.where(rest1 == cell(7), second, miss),
        jnp.where(rest2 == cell(8), 1.0, 0.0),
        jnp.where(rest2 == cell(9), 1.0, 0.0),
    ]


def bit_peer(device, bit):
    step = 1 << bit
    return device + (1 - 2 * ((device // step) % 2)) * step


def greet(peers):
    barrier = pltpu.get_barrier_semaphore()
    for peer in peers:
        pl.semaphore_signal(barrier, inc=1, device_id=peer, device_id_type=MESH)
    pl.semaphore_wait(barrier, len(peers))


def xor_bits(a, b):
    return (a % 2 + b % 2) % 2 + 2 * ((a // 2 + b // 2) % 2)


def fwd_kernel(
    info, tab, hid, gain, bias, wq, wk, wv, qb, vb, w1, wo, vec,
    e_ref, li_ref, q_out, k_out, v_out, kp_out, vp_out, o_out, mine_out, got_out,
    w1_got, w1_swap, wo_got, wo_swap, vec_got,
    t_s, kc_s, kv_s, low_s, q_s, ko_s, vo_s, o_s, sems_a, sems_b, loc_sems,
):
    pair = pl.program_id(0)
    step = pl.program_id(1)
    pairs = pl.num_programs(0)
    device = lax.axis_index("dp")
    side = lax.axis_index("tensor")
    member = device % GDEV
    core = device % 2
    rows, width = q_s.shape
    n_pairs = width // 128
    last_pair = n_pairs - 1
    conts = rows - CHUNK
    near = {"dp": bit_peer(device, 0), "tensor": side}
    far = {"dp": bit_peer(device, 1), "tensor": side}
    across = {"dp": device, "tensor": 1 - side}
    half_u = w1.shape[1] // 2
    half_w = wo.shape[0] // 2
    half_p, half_c = CHUNK // 2, conts // 2
    sent_u = pl.multiple_of(core * half_u, 128)
    sent_w = pl.multiple_of(core * half_w, 64)

    def remote(i, src, dst, peer):
        return pltpu.make_async_remote_copy(
            src_ref=src, dst_ref=dst, send_sem=sems_a.at[i], recv_sem=sems_b.at[i], device_id=peer, device_id_type=MESH
        )

    def to_far(p):
        lanes = pl.ds(p * 128, 128)
        return remote(3 * p, kv_s.at[0, :, :, lanes], kv_s.at[2, :, :, lanes], far)

    def to_near(p):
        lanes = pl.ds(p * 128, 128)
        return remote(3 * p + 1, kv_s.at[0, :, :, lanes], kv_s.at[1, :, :, lanes], near)

    def relay(p):
        lanes = pl.ds(p * 128, 128)
        return remote(3 * p + 2, kv_s.at[2, :, :, lanes], kv_s.at[3, :, :, lanes], near)

    base = 3 * n_pairs
    fetch_y = [
        remote(base, wo.at[pl.ds(sent_w, half_w), :], wo_got, across),
        remote(base + 1, w1.at[:, pl.ds(sent_u, half_u)], w1_got, across),
        remote(base + 2, vec, vec_got, across),
    ]
    fetch_core = [
        remote(base + 3, wo_got, wo_swap, near),
        remote(base + 4, w1_got, w1_swap, near),
    ]

    def give(p):
        lanes = pl.ds(p * 128, 128)
        their_p = pl.multiple_of((1 - side) * half_p, 128)
        their_c = pl.multiple_of(CHUNK + (1 - side) * half_c, 128)
        return [
            remote(base + 5 + 2 * p, o_s.at[pl.ds(their_p, half_p), lanes], got_out.at[pl.ds(0, half_p), lanes], across),
            remote(base + 6 + 2 * p, o_s.at[pl.ds(their_c, half_c), lanes], got_out.at[pl.ds(half_p, half_c), lanes], across),
        ]

    def keeps():
        own_p = pl.multiple_of(side * half_p, 128)
        own_c = pl.multiple_of(CHUNK + side * half_c, 128)
        return [
            pltpu.make_async_copy(o_s, o_out, loc_sems.at[0]),
            pltpu.make_async_copy(o_s.at[pl.ds(own_p, half_p), :], mine_out.at[pl.ds(0, half_p), :], loc_sems.at[1]),
            pltpu.make_async_copy(o_s.at[pl.ds(own_c, half_c), :], mine_out.at[pl.ds(half_p, half_c), :], loc_sems.at[2]),
        ]

    def saves():
        out = [
            pltpu.make_async_copy(q_s, q_out, loc_sems.at[3]),
            pltpu.make_async_copy(ko_s, k_out, loc_sems.at[0]),
            pltpu.make_async_copy(vo_s, v_out, loc_sems.at[5]),
        ]
        for r in range(GDEV):
            span = pl.ds(r * CHUNK, CHUNK)
            out.append(pltpu.make_async_copy(kv_s.at[r, 0], kp_out.at[span, :], loc_sems.at[6 + 2 * r]))
            out.append(pltpu.make_async_copy(kv_s.at[r, 1], vp_out.at[span, :], loc_sems.at[7 + 2 * r]))
        return out

    @pl.when((pair == 0) & (step == 0))
    def _():
        greet([near, far, across])
        for copy in fetch_y:
            copy.start()
        gain_f, bias_f = gain[...], bias[...]

        def norm(at, size):
            x = hid[at : at + size, :].astype(F32)
            center = jnp.mean(x, axis=1, keepdims=True)
            scale = lax.rsqrt(jnp.mean(x * x, axis=1, keepdims=True) - center * center + EPSILON)
            low = ((x - center) * scale * gain_f + bias_f).astype(BF)
            low_s[at : at + size, :] = low
            return low

        low = norm(0, CHUNK)
        kv_s[0, 0] = dot_nn(low, wk[...]).astype(BF)
        kv_s[0, 1] = (dot_nn(low, wv[...]) + vb[...]).astype(BF)
        to_far(0).start()
        for p in range(n_pairs):
            to_near(p).start()
        for at in range(CHUNK, rows, TILE):
            low = norm(at, TILE)
            ko_s[at - CHUNK : at - CHUNK + TILE, :] = dot_nn(low, wk[...]).astype(BF)
            vo_s[at - CHUNK : at - CHUNK + TILE, :] = (dot_nn(low, wv[...]) + vb[...]).astype(BF)
        to_far(0).wait_send()
        for p in range(1, n_pairs):
            to_far(p).start()
        for at in range(0, rows, TILE):
            q_s[at : at + TILE, :] = ((dot_nn(low_s[at : at + TILE, :], wq[...]) + qb[...]) * 0.125).astype(BF)
        to_far(0).wait_recv()
        relay(0).start()

    for p in range(n_pairs):
        @pl.when((pair == p) & (step == 0))
        def _():
            to_near(p).wait_recv()
            relay(p).wait_recv()

        if p + 1 < n_pairs:
            @pl.when((pair == p) & (step == 3))
            def _():
                to_far(p + 1).wait_recv()
                relay(p + 1).start()

    lanes = pl.ds(pl.multiple_of(pair * 128, 128), 128)
    low = low_half(TILE)
    q = q_s[pl.ds(pl.multiple_of(step * TILE, TILE), TILE), lanes]
    zero = jnp.zeros_like(q)
    qs = [jnp.where(low, q, zero), jnp.where(low, zero, q)]
    row = lax.broadcasted_iota(jnp.int32, (TILE, 128), 0).astype(F32)
    at_q = info[2 + step].astype(F32) + row
    qc = codes(at_q, tab, pair, -2.0)

    @pl.when(step == 0)
    def _():
        at_k = info[1].astype(F32) + lax.broadcasted_iota(jnp.int32, (8, PROMPT), 1).astype(F32)
        for i, c in enumerate(codes(at_k, tab, pair, -1.0)):
            kc_s[i] = c

    def logits(mx, keys, kc, causal, at, span):
        out = []
        for h in range(2):
            s = dot_nt(qs[h], keys)
            top = mx[h]
            for g in range(span // 128):
                part = slice(g * 128, (g + 1) * 128)
                w = jnp.where(qc[0] == kc[0][:, part], 1.0, 0.0)
                w = w + jnp.where(qc[1 + h] == kc[1 + h][:, part], 1.0, 0.0)
                w = w + qc[3 + h] * kc[3 + h][:, part]
                if causal is not None:
                    w = jnp.where(causal[:, part], w, 0.0)
                t = s[:, part] * LOG2E + jnp.log2(w)
                t_s[h, :, pl.ds(at + g * 128, 128)] = t
                top = jnp.maximum(top, t)
            out.append(top)
        return tuple(out)

    def weigh(carry, vals, m, at, span):
        sums, accs = carry
        ns, na = [], []
        for h in range(2):
            total = sums[h]
            parts = []
            for g in range(span // 128):
                e = jnp.exp2(t_s[h, :, pl.ds(at + g * 128, 128)] - m[h])
                total = total + e
                parts.append(e.astype(BF))
            el = jnp.concatenate(parts, axis=1)
            e_ref[h, :, pl.ds(at, span)] = el
            ns.append(total)
            na.append(accs[h] + dot_nn(el, vals))
        return (tuple(ns), tuple(na))

    def finish_rows(carry):
        sums, accs = carry
        li = [1.0 / jnp.sum(s, axis=1, keepdims=True) for s in sums]
        lfull = jnp.where(low, li[0], li[1])
        li_ref[...] = lfull
        o_s[pl.ds(pl.multiple_of(step * TILE, TILE), TILE), lanes] = (jnp.where(low, accs[0], accs[1]) * lfull).astype(BF)

    def tops(mx):
        return [jnp.broadcast_to(jnp.max(x, axis=1, keepdims=True), (TILE, 128)) for x in mx]

    neg = jnp.full((TILE, 128), -jnp.inf, F32)
    zf = jnp.zeros((TILE, 128), F32)

    def key_codes(at, span):
        return [kc_s[i, 0:1, pl.ds(at, span)] for i in range(5)]

    @pl.when(step < PTILES)
    def _():
        def one(j, mx):
            at = pl.multiple_of(j * CHUNK, CHUNK)
            held = xor_bits(j, member)
            return logits(
                mx, kv_s[held, 0, :, lanes], key_codes(at, CHUNK), None, pl.multiple_of(held * CHUNK, CHUNK), CHUNK
            )

        mx = lax.fori_loop(0, member, one, (neg, neg))
        at = pl.multiple_of(member * CHUNK, CHUNK)
        rows_id = lax.broadcasted_iota(jnp.int32, (TILE, CHUNK), 0) + step * TILE
        cols = lax.broadcasted_iota(jnp.int32, (TILE, CHUNK), 1)
        mx = logits(mx, kv_s[0, 0, :, lanes], key_codes(at, CHUNK), cols <= rows_id, 0, CHUNK)
        m = tops(mx)

        def two(j, carry):
            held = xor_bits(j, member)
            return weigh(carry, kv_s[held, 1, :, lanes], m, pl.multiple_of(held * CHUNK, CHUNK), CHUNK)

        finish_rows(lax.fori_loop(0, member + 1, two, ((zf, zf), (zf, zf))))

    @pl.when(step >= PTILES)
    def _():
        own = pl.ds(pl.multiple_of((step - PTILES) * TILE, TILE), TILE)
        mx = (neg, neg)
        for j in range(GDEV):
            at = pl.multiple_of(xor_bits(j, member) * CHUNK, CHUNK)
            mx = logits(mx, kv_s[j, 0, :, lanes], key_codes(at, CHUNK), None, j * CHUNK, CHUNK)
        rows_id = lax.broadcasted_iota(jnp.int32, (TILE, CONT), 0)
        cols = lax.broadcasted_iota(jnp.int32, (TILE, CONT), 1)
        at_k = info[2 + step].astype(F32) + lax.broadcasted_iota(jnp.int32, (8, CONT), 1).astype(F32)
        own_codes = [c[0:1] for c in codes(at_k, tab, pair, -1.0)]
        mx = logits(mx, ko_s[own, lanes], own_codes, cols <= rows_id, PROMPT, CONT)
        m = tops(mx)
        carry = ((zf, zf), (zf, zf))
        for j in range(GDEV):
            carry = weigh(carry, kv_s[j, 1, :, lanes], m, j * CHUNK, CHUNK)
        finish_rows(weigh(carry, vo_s[own, lanes], m, PROMPT, CONT))

    end = pl.num_programs(1) - 1
    for p in range(n_pairs):
        @pl.when((pair == p) & (step == end))
        def _():
            for copy in give(p):
                copy.start()

    @pl.when((pair == last_pair - 1) & (step == 3))
    def _():
        for i in range(2):
            fetch_y[i].wait_recv()
            fetch_core[i].start()

    @pl.when((pair == last_pair) & (step == 0))
    def _():
        for copy in saves():
            copy.start()

    @pl.when((pair == last_pair) & (step == end))
    def _():
        for copy in keeps():
            copy.start()
        fetch_y[2].wait_recv()
        for copy in fetch_core:
            copy.wait_recv()
        for p in range(n_pairs):
            for copy in give(p):
                copy.wait_recv()
                copy.wait_send()
            if p > 0:
                to_far(p).wait_send()
            to_near(p).wait_send()
            relay(p).wait_send()
        for copy in fetch_y + fetch_core:
            copy.wait_send()
        for copy in keeps() + saves():
            copy.wait()


def attend(info, tab, hid, gain, bias, wq, wk, wv, qb, vb, w1, wo, vec):
    rows = hid.shape[0]
    width = wq.shape[1]
    pairs = width // 128
    span = PROMPT + CONT
    conts = rows - CHUNK
    units = w1.shape[1]
    vmem = pl.BlockSpec(memory_space=pltpu.VMEM)
    hbm = pl.BlockSpec(memory_space=pl.ANY)
    shape = jax.ShapeDtypeStruct
    copies = 3 * pairs + 5 + 2 * pairs
    return pl.pallas_call(
        fwd_kernel,
        grid_spec=pltpu.PrefetchScalarGridSpec(
            num_scalar_prefetch=2,
            grid=(pairs, rows // TILE),
            in_specs=[vmem] * 8 + [hbm] * 3,
            out_specs=[
                pl.BlockSpec((2, TILE, span), lambda a, t, s, f: (a, t, 0)),
                pl.BlockSpec((TILE, 128), lambda a, t, s, f: (t, a)),
            ]
            + [hbm] * 13,
            scratch_shapes=[
                pltpu.VMEM((2, TILE, span), F32),
                pltpu.VMEM((5, 8, PROMPT), F32),
                pltpu.VMEM((GDEV, 2, CHUNK, width), BF),
                pltpu.VMEM((rows, D), BF),
                pltpu.VMEM((rows, width), BF),
                pltpu.VMEM((conts, width), BF),
                pltpu.VMEM((conts, width), BF),
                pltpu.VMEM((rows, width), BF),
                pltpu.SemaphoreType.DMA((copies,)),
                pltpu.SemaphoreType.DMA((copies,)),
                pltpu.SemaphoreType.DMA((6 + 2 * GDEV,)),
            ],
        ),
        out_shape=[
            shape((2 * pairs, rows, span), BF),
            shape((rows, width), F32),
            shape((rows, width), BF),
            shape((conts, width), BF),
            shape((conts, width), BF),
            shape((PROMPT, width), BF),
            shape((PROMPT, width), BF),
            shape((rows, width), BF),
            shape((rows // 2, width), BF),
            shape((rows // 2, width), BF),
            shape((D, units // 2), BF),
            shape((D, units // 2), BF),
            shape((width // 2, D), BF),
            shape((width // 2, D), BF),
            shape(vec.shape, F32),
        ],
        compiler_params=pltpu.CompilerParams(vmem_limit_bytes=56 << 20, collective_id=0, has_side_effects=True),
        cost_estimate=pl.CostEstimate(flops=20 * 10**9, bytes_accessed=60 * 10**6, transcendentals=0),
        name="attend",
    )(info, tab, hid, gain, bias, wq, wk, wv, qb, vb, w1, wo, vec)


def bwd_kernel(
    q_ref, kp_ref, vp_ref, ko_ref, vo_ref, o_ref, li_ref, e_ref, g_mine, g_theirs, out_half,
    dq_ref, dko_ref, dvo_ref, sum_k, sum_v, relay_out, out_got,
    dk_s, dv_s, g_s, grad_s, near_s, relay_s, far_s, sems_a, sems_b, loc_sems,
):
    pair = pl.program_id(0)
    step = pl.program_id(1)
    device = lax.axis_index("dp")
    side = lax.axis_index("tensor")
    member = device % GDEV
    rows, width = g_s.shape
    n_pairs = width // 128
    conts = rows - CHUNK
    half_p, half_c = CHUNK // 2, conts // 2
    near = {"dp": bit_peer(device, 0), "tensor": side}
    far = {"dp": bit_peer(device, 1), "tensor": side}
    across = {"dp": device, "tensor": 1 - side}
    lanes = pl.ds(pl.multiple_of(pair * 128, 128), 128)
    mine_p = pl.ds(pl.multiple_of(side * half_p, 128), half_p)
    mine_c = pl.ds(pl.multiple_of(CHUNK + side * half_c, 128), half_c)

    def remote(i, src, dst, peer):
        return pltpu.make_async_remote_copy(
            src_ref=src, dst_ref=dst, send_sem=sems_a.at[i], recv_sem=sems_b.at[i], device_id=peer, device_id_type=MESH
        )

    def heads():
        return [
            remote(0, g_theirs.at[pl.ds(0, half_p), :], g_s.at[mine_p, :], across),
            remote(1, g_theirs.at[pl.ds(half_p, half_c), :], g_s.at[mine_c, :], across),
            remote(2, out_half, out_got, across),
        ]

    def local():
        return [
            pltpu.make_async_copy(g_mine.at[pl.ds(0, half_p), :], g_s.at[mine_p, :], loc_sems.at[0]),
            pltpu.make_async_copy(g_mine.at[pl.ds(half_p, half_c), :], g_s.at[mine_c, :], loc_sems.at[1]),
        ]

    def cores(p):
        part = pl.ds(p * 128, 128)
        return remote(3 + 2 * p, grad_s.at[:, :, 1, :, part], near_s.at[:, :, :, part], near)

    def chips(p):
        part = pl.ds(p * 128, 128)
        return remote(4 + 2 * p, relay_s.at[:, :, part], far_s.at[:, :, part], far)

    @pl.when((pair == 0) & (step == 0))
    def _():
        greet([near, far, across])
        for copy in heads() + local():
            copy.start()
        for copy in local():
            copy.wait()

    @pl.when((pair == 0) & (step == 1 - side))
    def _():
        heads()[0].wait_recv()

    @pl.when((pair == 0) & (step == 3 - side))
    def _():
        heads()[1].wait_recv()

    low = low_half(TILE)
    g = g_s[pl.ds(pl.multiple_of(step * TILE, TILE), TILE), lanes].astype(F32) * li_ref[...]
    prod = g * o_ref[...].astype(F32)
    zf = jnp.zeros((TILE, 128), F32)
    deltas = [
        jnp.sum(jnp.where(low, prod, zf), axis=1, keepdims=True),
        jnp.sum(jnp.where(low, zf, prod), axis=1, keepdims=True),
    ]
    gs = [jnp.where(low, g, zf).astype(BF), jnp.where(low, zf, g).astype(BF)]
    gt = jnp.transpose(g).astype(BF)
    qt = jnp.transpose(q_ref[...].astype(F32)).astype(BF)

    def grads(dq, keys, vals, at, width):
        out, dks, dvs = [], [], []
        for h in range(2):
            e = e_ref[h, :, pl.ds(at, width)]
            dp = dot_nt(gs[h], vals)
            ds = (e.astype(F32) * (dp - deltas[h])).astype(BF)
            out.append(dq[h] + dot_nn(ds, keys))
            dks.append(dot_nn(qt[h * HD : (h + 1) * HD, :], ds))
            dvs.append(dot_nn(gt[h * HD : (h + 1) * HD, :], e))
        return tuple(out), dks, dvs

    @pl.when(step == 0)
    def _():
        dk_s[...] = jnp.zeros_like(dk_s)
        dv_s[...] = jnp.zeros_like(dv_s)

    def add(at, width, dks, dvs):
        for h in range(2):
            dk_s[h * HD : (h + 1) * HD, pl.ds(at, width)] += dks[h]
            dv_s[h * HD : (h + 1) * HD, pl.ds(at, width)] += dvs[h]

    def scaled(dq):
        return (jnp.where(low, dq[0], dq[1]).astype(BF).astype(F32) * 0.125).astype(BF)

    @pl.when(step < PTILES)
    def _():
        def one(j, dq):
            at = pl.multiple_of(xor_bits(j, member) * CHUNK, CHUNK)
            dq, dks, dvs = grads(dq, kp_ref[pl.ds(at, CHUNK), :], vp_ref[pl.ds(at, CHUNK), :], at, CHUNK)
            add(at, CHUNK, dks, dvs)
            return dq

        dq_ref[...] = scaled(lax.fori_loop(0, member + 1, one, (zf, zf)))
        dko_ref[...] = jnp.zeros_like(dko_ref)
        dvo_ref[...] = jnp.zeros_like(dvo_ref)

    @pl.when(step >= PTILES)
    def _():
        dq = (zf, zf)
        for j in range(GDEV):
            span = slice(j * CHUNK, (j + 1) * CHUNK)
            dq, dks, dvs = grads(dq, kp_ref[span, :], vp_ref[span, :], j * CHUNK, CHUNK)
            add(j * CHUNK, CHUNK, dks, dvs)
        dq, dks, dvs = grads(dq, ko_ref[...], vo_ref[...], PROMPT, CONT)
        dq_ref[...] = scaled(dq)
        dko_ref[...] = jnp.transpose(jnp.concatenate(dks, axis=0)).astype(BF)
        dvo_ref[...] = jnp.transpose(jnp.concatenate(dvs, axis=0)).astype(BF)

    end = pl.num_programs(1) - 1

    @pl.when(step == end)
    def _():
        for j in range(GDEV):
            span = slice(j * CHUNK, (j + 1) * CHUNK)
            grad_s[0, j // 2, j % 2, :, lanes] = jnp.transpose(dk_s[:, span]).astype(BF)
            grad_s[1, j // 2, j % 2, :, lanes] = jnp.transpose(dv_s[:, span]).astype(BF)

    for p in range(n_pairs):
        @pl.when((pair == p) & (step == end))
        def _():
            cores(p).start()

        if p + 1 < n_pairs:
            @pl.when((pair == p + 1) & (step == 2))
            def _():
                part = pl.ds(p * 128, 128)
                cores(p).wait_recv()
                relay_s[:, :, part] = (
                    grad_s[:, 1, 0, :, part].astype(F32) + near_s[:, 1, :, part].astype(F32)
                ).astype(BF)
                chips(p).start()

    @pl.when((pair == n_pairs - 1) & (step == end))
    def _():
        last = n_pairs - 1
        sums = (sum_k, sum_v)
        for p in range(last):
            part = pl.ds(p * 128, 128)
            chips(p).wait_recv()
            for i in range(2):
                sums[i][:, part] = (
                    grad_s[i, 0, 0, :, part].astype(F32) + near_s[i, 0, :, part].astype(F32) + far_s[i, :, part].astype(F32)
                ).astype(BF)
        part = pl.ds(last * 128, 128)
        cores(last).wait_recv()
        for i in range(2):
            relay_out[i] = (grad_s[i, 1, 0, :, part].astype(F32) + near_s[i, 1, :, part].astype(F32)).astype(BF)
            sums[i][:, part] = (grad_s[i, 0, 0, :, part].astype(F32) + near_s[i, 0, :, part].astype(F32)).astype(BF)
        heads()[2].wait_recv()
        for copy in heads():
            copy.wait_send()
        for p in range(n_pairs):
            cores(p).wait_send()
            if p < last:
                chips(p).wait_send()


def attend_back(q, k, v, kp, vp, o, li, e, g_mine, g_theirs, out_half):
    rows, width = q.shape
    pairs = width // 128
    span = PROMPT + CONT
    tile = pl.BlockSpec((TILE, 128), lambda a, t: (t, a))
    whole = pl.BlockSpec((PROMPT, 128), lambda a, t: (0, a))
    own = pl.BlockSpec((TILE, 128), lambda a, t: (jnp.maximum(t - PTILES, 0), a))
    vmem = pl.BlockSpec(memory_space=pltpu.VMEM)
    hbm = pl.BlockSpec(memory_space=pl.ANY)
    shape = jax.ShapeDtypeStruct
    copies = 3 + 2 * pairs
    return pl.pallas_call(
        bwd_kernel,
        grid=(pairs, rows // TILE),
        in_specs=[tile, whole, whole, own, own, tile, tile, pl.BlockSpec((2, TILE, span), lambda a, t: (a, t, 0))]
        + [hbm] * 3,
        out_specs=[tile, tile, tile, vmem, vmem, vmem, hbm],
        out_shape=[
            shape((rows, width), BF),
            shape((rows, width), BF),
            shape((rows, width), BF),
            shape((CHUNK, width), BF),
            shape((CHUNK, width), BF),
            shape((2, CHUNK, 128), BF),
            shape(out_half.shape, BF),
        ],
        scratch_shapes=[
            pltpu.VMEM((128, PROMPT), F32),
            pltpu.VMEM((128, PROMPT), F32),
            pltpu.VMEM((rows, width), BF),
            pltpu.VMEM((2, 2, 2, CHUNK, width), BF),
            pltpu.VMEM((2, 2, CHUNK, width), BF),
            pltpu.VMEM((2, CHUNK, width), BF),
            pltpu.VMEM((2, CHUNK, width), BF),
            pltpu.SemaphoreType.DMA((copies,)),
            pltpu.SemaphoreType.DMA((copies,)),
            pltpu.SemaphoreType.DMA((2,)),
        ],
        compiler_params=pltpu.CompilerParams(vmem_limit_bytes=56 << 20, collective_id=2, has_side_effects=True),
        cost_estimate=pl.CostEstimate(flops=30 * 10**9, bytes_accessed=60 * 10**6, transcendentals=0),
        name="attend_back",
    )(q, kp, vp, k, v, o, li, e, g_mine, g_theirs, out_half)


UCH = 512


def polynomial(x, terms):
    out = jnp.full_like(x, terms[0])
    for term in terms[1:]:
        out = out * x + term
    return out


def error_function(x):
    x = jnp.clip(x, -3.832506856900711, 3.832506856900711)
    square = x * x
    top = polynomial(
        square,
        (0.00022905065861350646, 0.0034082910107109506, 0.050955695062380861, 0.18520832239976145, 1.128379143519084),
    )
    bottom = polynomial(
        square,
        (
            -1.1791602954361697e-7,
            0.000023547966471313185,
            0.0010179625278914885,
            0.014070470171167667,
            0.11098505178285362,
            0.49746925110067538,
            1.0,
        ),
    )
    return x * top / bottom


def gelu_pair(v):
    phi = 0.5 + 0.5 * error_function(v * 0.7071067811865476)
    density = jnp.exp(-0.5 * v * v) * 0.3989422804014327
    return v * phi, phi + v * density


def column_sum(x):
    return jnp.sum(x, axis=0, keepdims=True)


def mid_kernel(
    att_m, att_o, hid, cot, vec_own, vec_got, vec_d, w1_own, w1_got, w1_swap, wo_own, wo_got, wo_swap, w2_own,
    out_ref, gatt_m, gatt_o, gmix_ref, packed, su_ref, sw_ref, sd_ref, ext_ref,
    vec_u, vec_w, w1, w2, wo, act_s, shp_s, dg_s, wide_s, acc_s, gmid_s, sub_s, mid_s, low_s, midt_s, cott_s, stage, sems, out_sems, send_sems, recv_sems,
):
    device = lax.axis_index("dp")
    side = lax.axis_index("tensor")
    core = device % 2
    near = {"dp": bit_peer(device, 0), "tensor": side}
    across = {"dp": device, "tensor": 1 - side}
    units = w1_own.shape[1]
    width = wo_own.shape[0]
    rows = hid.shape[0]
    full = 2 * units
    half = units // 2
    half_w = width // 2
    here_u = pl.multiple_of(units + core * half, 128)
    there_u = pl.multiple_of(units + (1 - core) * half, 128)
    here_w = pl.multiple_of(width + core * half_w, 64)
    there_w = pl.multiple_of(width + (1 - core) * half_w, 64)
    loads = []
    for i, (src, dst) in enumerate(
        [
            (wo_own, wo.at[pl.ds(0, width), :]),
            (wo_got, wo.at[pl.ds(here_w, half_w), :]),
            (wo_swap, wo.at[pl.ds(there_w, half_w), :]),
            (w1_own, w1.at[:, pl.ds(0, units)]),
            (w1_got, w1.at[:, pl.ds(here_u, half)]),
            (w1_swap, w1.at[:, pl.ds(there_u, half)]),
            (w2_own, w2.at[pl.ds(0, units), :]),
        ]
    ):
        copy = pltpu.make_async_copy(src, dst, sems.at[i])
        copy.start()
        loads.append(copy)

    piece = half // 2
    greet([near, across])

    def remote(i, src, dst, peer):
        return pltpu.make_async_remote_copy(
            src_ref=src, dst_ref=dst, send_sem=send_sems.at[i], recv_sem=recv_sems.at[i], device_id=peer, device_id_type=MESH
        )

    over, passed = [], []
    for i in range(2):
        from_own = pl.ds(pl.multiple_of(core * half + i * piece, 128), piece)
        landed = w2.at[pl.ds(pl.multiple_of(units + core * half + i * piece, 128), piece), :]
        over.append(remote(i, w2_own.at[from_own, :], landed, across))
        passed.append(remote(2 + i, landed, landed, near))
        over[i].start()

    for i in range(3):
        for j, vec in enumerate((vec_own, vec_got)):
            vec_u[i : i + 1, pl.ds(j * units, units)] = vec[0:1, pl.ds(i * units, units)]
    for i in range(2):
        for j, vec in enumerate((vec_own, vec_got)):
            vec_w[i : i + 1, pl.ds(j * width, width)] = vec[0:1, pl.ds(3 * units + i * width, width)]

    a0 = att_m[...].astype(F32)
    a1 = att_o[...].astype(F32)
    center = (jnp.sum(a0, axis=1, keepdims=True) + jnp.sum(a1, axis=1, keepdims=True)) * (1.0 / D)
    square = (jnp.sum(a0 * a0, axis=1, keepdims=True) + jnp.sum(a1 * a1, axis=1, keepdims=True)) * (1.0 / D)
    sub_scale = lax.rsqrt(square - center * center + EPSILON)
    sub_s[:, 0:width] = (a0 - center) * sub_scale
    sub_s[:, width : 2 * width] = (a1 - center) * sub_scale
    sub_gain = vec_w[0:1, :]
    low_s[...] = (sub_s[...] * sub_gain + vec_w[1:2, :]).astype(BF)
    for copy in loads[0:3]:
        copy.wait()
    mixed = hid[...].astype(F32) + (dot_nn(low_s[...], wo[...]) + vec_d[0:1, pl.ds(0, D)])
    wide_s[...] = mixed
    mean = jnp.mean(mixed, axis=1, keepdims=True)
    mid_scale = lax.rsqrt(jnp.mean(mixed * mixed, axis=1, keepdims=True) - mean * mean + EPSILON)
    mid_s[...] = (mixed - mean) * mid_scale
    mid_gain = vec_d[0:1, pl.ds(768, D)]
    mid_full = mid_s[...] * mid_gain + vec_d[0:1, pl.ds(1536, D)]
    mid_low = mid_full.astype(BF)
    midt_s[...] = jnp.transpose(mid_full).astype(BF)
    cot_full = cot[...].astype(F32)
    cott_s[...] = jnp.transpose(cot_full).astype(BF)
    sd_ref[...] = jnp.zeros_like(sd_ref)
    sd_ref[3:4, :] = column_sum(cot_full)
    for copy in loads[3:6]:
        copy.wait()

    def lanes_sum(x):
        total = x[:, 0:128]
        for i in range(1, x.shape[1] // 128):
            total = total + x[:, i * 128 : (i + 1) * 128]
        return total

    def first(c, carry):
        at = pl.multiple_of(c * UCH, UCH)
        inner = dot_nn(mid_low, w1[:, pl.ds(at, UCH)]) + vec_u[2:3, pl.ds(at, UCH)]
        act, slope = gelu_pair(inner)
        act_s[:, pl.ds(at, UCH)] = act
        dg_s[:, pl.ds(at, UCH)] = slope.astype(BF)
        return carry[0] + lanes_sum(act), carry[1] + lanes_sum(act * act)

    zero = jnp.zeros((rows, 128), F32)
    act_sum, act_square = lax.fori_loop(0, full // UCH, first, (zero, zero))
    ffn_center = jnp.sum(act_sum, axis=1, keepdims=True) * (1.0 / full)
    ffn_scale = lax.rsqrt(
        jnp.sum(act_square, axis=1, keepdims=True) * (1.0 / full) - ffn_center * ffn_center + EPSILON
    )
    loads[6].wait()
    over[0].wait_recv()
    passed[0].start()
    acc_s[...] = jnp.zeros_like(acc_s)
    per = units // UCH
    wide = 2 * units + width

    def column_of(c, extra):
        return pl.multiple_of((c // per) * wide + lax.rem(c, per) * UCH + extra, 128)

    def send(slot, column):
        return pltpu.make_async_copy(stage.at[slot], packed.at[:, pl.ds(column, UCH)], out_sems.at[slot])

    def put(c, value, extra):
        slot = lax.rem(c, 2)

        @pl.when(c >= 2)
        def _():
            send(slot, column_of(c - 2, extra)).wait()

        stage[slot] = value
        send(slot, column_of(c, extra)).start()

    def drain(extra):
        for c in range(full // UCH - 2, full // UCH):
            send(c % 2, column_of(c, extra)).wait()

    def second(c, carry):
        at = pl.multiple_of(c * UCH, UCH)
        unit = (act_s[:, pl.ds(at, UCH)] - ffn_center) * ffn_scale
        act_s[:, pl.ds(at, UCH)] = unit
        gain = vec_u[0:1, pl.ds(at, UCH)]
        low = (unit * gain + vec_u[1:2, pl.ds(at, UCH)]).astype(BF)
        acc_s[...] += dot_nn(low, w2[pl.ds(at, UCH), :])
        grad = dot_nt(cot[...], w2[pl.ds(at, UCH), :])
        cross = grad * unit
        su_ref[0:1, pl.ds(at, UCH)] = column_sum(cross)
        su_ref[1:2, pl.ds(at, UCH)] = column_sum(grad)
        shaped = grad * gain
        shp_s[:, pl.ds(at, UCH)] = shaped
        put(c, dot_nn(cott_s[...], low).astype(BF), units)
        return carry[0] + lanes_sum(shaped), carry[1] + lanes_sum(shaped * unit)

    su_ref[...] = jnp.zeros_like(su_ref)
    sums = lax.fori_loop(0, per, second, (zero, zero))
    over[1].wait_recv()
    passed[1].start()
    for copy in passed:
        copy.wait_recv()
    s_sum, s_cross = lax.fori_loop(per, 2 * per, second, sums)
    drain(units)
    shaped_mean = jnp.sum(s_sum, axis=1, keepdims=True) * (1.0 / full)
    cross_mean = jnp.sum(s_cross, axis=1, keepdims=True) * (1.0 / full)
    out_ref[...] = (wide_s[...] + (acc_s[...] + vec_d[0:1, pl.ds(2304, D)])).astype(BF)
    gmid_s[...] = jnp.zeros_like(gmid_s)

    def third(c, carry):
        at = pl.multiple_of(c * UCH, UCH)
        g = ffn_scale * (shp_s[:, pl.ds(at, UCH)] - shaped_mean - act_s[:, pl.ds(at, UCH)] * cross_mean)
        low = (g * dg_s[:, pl.ds(at, UCH)].astype(F32)).astype(BF)
        su_ref[2:3, pl.ds(at, UCH)] = column_sum(low.astype(F32))
        gmid_s[...] += dot_nt(low, w1[:, pl.ds(at, UCH)])
        put(c, dot_nn(midt_s[...], low).astype(BF), 0)
        return carry

    lax.fori_loop(0, full // UCH, third, 0)
    drain(0)

    grad_mid = gmid_s[...]
    unit = mid_s[...]
    sd_ref[1:2, :] = column_sum(grad_mid * unit)
    sd_ref[2:3, :] = column_sum(grad_mid)
    shaped = grad_mid * mid_gain
    grad_mixed = cot[...].astype(F32) + mid_scale * (
        shaped - jnp.mean(shaped, axis=1, keepdims=True) - unit * jnp.mean(shaped * unit, axis=1, keepdims=True)
    )
    branch = grad_mixed.astype(BF)
    gmix_ref[...] = branch
    branch_f = branch.astype(F32)
    sd_ref[0:1, :] = column_sum(branch_f)
    out_grad = dot_nn(jnp.transpose(branch_f).astype(BF), low_s[...]).astype(BF)
    stage[0, :, 0:width] = out_grad[:, 0:width]
    stage[1, :, 0:width] = out_grad[:, width : 2 * width]
    last = [
        pltpu.make_async_copy(stage.at[i, :, pl.ds(0, width)], packed.at[:, pl.ds(i * wide + 2 * units, width)], out_sems.at[i])
        for i in range(2)
    ]
    for copy in last:
        copy.start()
    grad_sub = dot_nt(branch, wo[...])
    unit = sub_s[...]
    cross = grad_sub * unit
    sw_ref[...] = jnp.zeros_like(sw_ref)
    sw_ref[0:1, :] = column_sum(cross)
    sw_ref[1:2, :] = column_sum(grad_sub)
    shaped = grad_sub * sub_gain
    grad_att = sub_scale * (
        shaped - jnp.mean(shaped, axis=1, keepdims=True) - unit * jnp.mean(shaped * unit, axis=1, keepdims=True)
    )
    gatt_m[...] = grad_att[:, 0:width].astype(BF)
    gatt_o[...] = grad_att[:, width : 2 * width].astype(BF)
    parts = ext_ref.shape[0]
    if parts > 1:
        sums_u, sums_w, sums_d = su_ref[...], sw_ref[...], sd_ref[...]
        for i in range(parts):
            ext_ref[i] = jnp.concatenate(
                [
                    window(sums_u, i * (units // parts)),
                    window(sums_u, units + i * (units // parts)),
                    window(sums_w, i * (width // parts)),
                    window(sums_w, width + i * (width // parts)),
                    window(sums_d, i * (D // parts)),
                    jnp.zeros((8, 128), F32),
                ],
                axis=0,
            ).astype(BF)
    for copy in last:
        copy.wait()
    for copy in over + passed:
        copy.wait_send()


def window(rows8, start):
    base = start // 128 * 128
    size = min(256, rows8.shape[1] - base)
    view = rows8[:, base : base + size]
    shift = start - base
    if shift:
        view = pltpu.roll(view, size - shift, 1)
    return view[:, 0:128]


def middle(att_m, att_o, hid, cot, vec_own, vec_got, vec_d, w1, w2, wo, parts):
    rows = hid.shape[0]
    units = w2.shape[0]
    width = wo[0].shape[0]
    vmem = pl.BlockSpec(memory_space=pltpu.VMEM)
    hbm = pl.BlockSpec(memory_space=pl.ANY)
    shape = jax.ShapeDtypeStruct
    return pl.pallas_call(
        mid_kernel,
        in_specs=[vmem] * 7 + [hbm] * 7,
        out_specs=[vmem] * 4 + [hbm] + [vmem] * 4,
        out_shape=[
            shape((rows, D), BF),
            shape((rows, width), BF),
            shape((rows, width), BF),
            shape((rows, D), BF),
            shape((D, 2 * (2 * units + width)), BF),
            shape((8, 2 * units), F32),
            shape((8, 2 * width), F32),
            shape((8, D), F32),
            shape((parts, 48, 128), BF),
        ],
        scratch_shapes=[
            pltpu.VMEM((8, 2 * units), F32),
            pltpu.VMEM((8, 2 * width), F32),
            pltpu.VMEM((D, 2 * units), BF),
            pltpu.VMEM((2 * units, D), BF),
            pltpu.VMEM((2 * width, D), BF),
            pltpu.VMEM((rows, 2 * units), F32),
            pltpu.VMEM((rows, 2 * units), F32),
            pltpu.VMEM((rows, 2 * units), BF),
            pltpu.VMEM((rows, D), F32),
            pltpu.VMEM((rows, D), F32),
            pltpu.VMEM((rows, D), F32),
            pltpu.VMEM((rows, 2 * width), F32),
            pltpu.VMEM((rows, D), F32),
            pltpu.VMEM((rows, 2 * width), BF),
            pltpu.VMEM((D, rows), BF),
            pltpu.VMEM((D, rows), BF),
            pltpu.VMEM((2, D, UCH), BF),
            pltpu.SemaphoreType.DMA((7,)),
            pltpu.SemaphoreType.DMA((2,)),
            pltpu.SemaphoreType.DMA((4,)),
            pltpu.SemaphoreType.DMA((4,)),
        ],
        compiler_params=pltpu.CompilerParams(vmem_limit_bytes=62 << 20, collective_id=3, has_side_effects=True),
        cost_estimate=pl.CostEstimate(flops=21 * 10**9, bytes_accessed=30 * 10**6, transcendentals=0),
        name="middle",
    )(att_m, att_o, hid, cot, vec_own, vec_got, vec_d, *w1, *wo, w2)


def final_kernel(
    bits, hid, gain, bias, dq, dk, dv, wq, wk, wv, gmix, ext, sum_k, sum_v, relay,
    gin, late_out, vec_out,
    loc_s, far_s, unit_s, mine_s, norm_s, send_c, recv_c, send_p, recv_p, give_c, give_p, late_s, small_s,
    vec_s, vec_r, sems_a, sems_b, loc_sems, *stage_refs,
):
    device = lax.axis_index("dp")
    side = lax.axis_index("tensor")
    across = {"dp": device, "tensor": 1 - side}
    peers = [{"dp": bit_peer(device, b), "tensor": side} for b in range(bits)]
    rows, width = dq.shape
    prompt = sum_k.shape[0]
    conts = rows - prompt
    half_p, half_c = prompt // 2, conts // 2
    own_p = pl.multiple_of(side * half_p, 128)
    their_p = pl.multiple_of((1 - side) * half_p, 128)
    own_c = pl.multiple_of(prompt + side * half_c, 128)
    their_c = pl.multiple_of(prompt + (1 - side) * half_c, 128)
    lanes = 3 * width + 128

    greet(peers + [across])
    count = [0]

    def remote(src, dst, peer):
        i = count[0]
        count[0] += 1
        copy = pltpu.make_async_remote_copy(
            src_ref=src, dst_ref=dst, send_sem=sems_a.at[i], recv_sem=sems_b.at[i], device_id=peer, device_id_type=MESH
        )
        copy.start()
        return copy

    share = remote(relay, far_s, peers[1])

    gain_f = gain[...]
    bias_f = bias[...]

    def unit_rows(at, size):
        x = hid[pl.ds(at, size), :].astype(F32)
        center = jnp.mean(x, axis=1, keepdims=True)
        scale = lax.rsqrt(jnp.mean(x * x, axis=1, keepdims=True) - center * center + EPSILON)
        return (x - center) * scale, scale

    def part_of(at, size, k_rows, v_rows):
        return dot_nt(dq[pl.ds(at, size), :], wq[...]) + dot_nt(k_rows, wk[...]) + dot_nt(v_rows, wv[...])

    def gather(part, unit):
        return column_sum(part * unit), column_sum(part)

    unit, _ = unit_rows(their_c, half_c)
    part = part_of(their_c, half_c, dk[pl.ds(their_c, half_c), :], dv[pl.ds(their_c, half_c), :])
    send_c[...] = part.astype(BF)
    y_cont = remote(send_c, recv_c, across)
    gain_grad, bias_grad = gather(part, unit)
    norm_s[:, pl.ds(their_c, half_c)] = jnp.transpose(unit * gain_f + bias_f).astype(BF)
    unit, scale_c = unit_rows(own_c, half_c)
    part = part_of(own_c, half_c, dk[pl.ds(own_c, half_c), :], dv[pl.ds(own_c, half_c), :])
    mine_s[pl.ds(half_p, half_c), :] = part
    unit_s[pl.ds(half_p, half_c), :] = unit
    g, b = gather(part, unit)
    gain_grad, bias_grad = gain_grad + g, bias_grad + b
    norm_s[:, pl.ds(own_c, half_c)] = jnp.transpose(unit * gain_f + bias_f).astype(BF)

    unit, _ = unit_rows(their_p, half_p)
    norm_s[:, pl.ds(their_p, half_p)] = jnp.transpose(unit * gain_f + bias_f).astype(BF)
    unit, scale_p = unit_rows(own_p, half_p)
    unit_s[pl.ds(0, half_p), :] = unit
    norm_s[:, pl.ds(own_p, half_p)] = jnp.transpose(unit * gain_f + bias_f).astype(BF)

    blocks = 1 << bits
    block = D // blocks

    def keep(value, lane):
        low = value.astype(BF)
        for i in range(blocks):
            late_s[i // 2, i % 2, :, pl.ds(lane, width)] = low[i * block : (i + 1) * block, :]

    keep(dot_nn(norm_s[...], dq[...]), 0)
    q_bias = column_sum(dq[...].astype(F32))

    def norm_back(total, unit, scale, mixed):
        shaped = total * gain_f
        return mixed.astype(F32) + scale * (
            shaped - jnp.mean(shaped, axis=1, keepdims=True) - unit * jnp.mean(shaped * unit, axis=1, keepdims=True)
        )

    y_cont.wait_recv()
    total = mine_s[pl.ds(half_p, half_c), :] + recv_c[...].astype(F32)
    give_c[...] = norm_back(total, unit_s[pl.ds(half_p, half_c), :], scale_c, gmix[pl.ds(half_p, half_c), :]).astype(BF)
    back_c = remote(give_c, gin.at[pl.ds(own_c, half_c), :], across)
    keep_c = pltpu.make_async_copy(give_c, gin.at[pl.ds(own_c, half_c), :], loc_sems.at[0])
    keep_c.start()

    share.wait_recv()
    for i, total in enumerate((sum_k, sum_v)):
        loc_s[i, :, pl.ds(0, width - 128)] = total[:, pl.ds(0, width - 128)]
        loc_s[i, :, pl.ds(width - 128, 128)] = (
            total[:, pl.ds(width - 128, 128)].astype(F32) + far_s[i].astype(F32)
        ).astype(BF)
    part = part_of(their_p, half_p, loc_s[0, pl.ds(their_p, half_p), :], loc_s[1, pl.ds(their_p, half_p), :])
    send_p[...] = part.astype(BF)
    y_prompt = remote(send_p, recv_p, across)
    unit, _ = unit_rows(their_p, half_p)
    g, b = gather(part, unit)
    gain_grad, bias_grad = gain_grad + g, bias_grad + b
    part = part_of(own_p, half_p, loc_s[0, pl.ds(own_p, half_p), :], loc_s[1, pl.ds(own_p, half_p), :])
    mine_s[pl.ds(0, half_p), :] = part
    g, b = gather(part, unit_s[pl.ds(0, half_p), :])
    gain_grad, bias_grad = gain_grad + g, bias_grad + b

    for i, rest in enumerate((dk, dv)):
        keep(
            dot_nn(norm_s[:, pl.ds(0, prompt)], loc_s[i])
            + dot_nn(norm_s[:, pl.ds(prompt, conts)], rest[pl.ds(prompt, conts), :]),
            (i + 1) * width,
        )
    v_bias = column_sum(loc_s[1].astype(F32)) + column_sum(dv[pl.ds(prompt, conts), :].astype(F32))

    small_s[...] = jnp.zeros_like(small_s)
    small_s[0:1, pl.ds(0, width)] = q_bias
    small_s[1:2, pl.ds(0, width)] = v_bias
    small_s[2:3, pl.ds(0, D)] = gain_grad
    small_s[3:4, pl.ds(0, D)] = bias_grad
    small = small_s[...]
    row_id = lax.broadcasted_iota(jnp.int32, (8, 128), 0)
    for i in range(blocks):
        narrow = window(small, i * (width // blocks))
        broad = window(small, i * block)
        tail = jnp.concatenate([ext[i, pl.ds(32, 16), :].astype(F32)[0:8], jnp.where(row_id < 2, narrow, broad)], axis=0)
        late_s[i // 2, i % 2, pl.ds(0, 32), pl.ds(3 * width, 128)] = ext[i, pl.ds(0, 32), :]
        late_s[i // 2, i % 2, pl.ds(32, 16), pl.ds(3 * width, 128)] = tail.astype(BF)

    source = late_s
    stages = []
    for bit in range(bits):
        landing, kept = stage_refs[2 * bit], stage_refs[2 * bit + 1]
        mine = (device // (1 << bit)) % 2
        copy = remote(source.at[:, 1 - mine], landing, peers[bit])
        if bit == 0:
            y_prompt.wait_recv()
            total = mine_s[pl.ds(0, half_p), :] + recv_p[...].astype(F32)
            give_p[...] = norm_back(total, unit_s[pl.ds(0, half_p), :], scale_p, gmix[pl.ds(0, half_p), :]).astype(BF)
            back_p = remote(give_p, gin.at[pl.ds(own_p, half_p), :], across)
            keep_p = pltpu.make_async_copy(give_p, gin.at[pl.ds(own_p, half_p), :], loc_sems.at[1])
            keep_p.start()
        copy.wait_recv()
        stages.append(copy)
        for i in range(landing.shape[0]):
            kept[i // 2, i % 2] = (source[i, mine].astype(F32) + landing[i].astype(F32)).astype(BF)
        source = kept
    late_out[...] = source[0, 0, :, pl.ds(0, 3 * width)].astype(F32)
    vec_s[...] = source[0, 0, :, pl.ds(3 * width, 128)]
    swap = remote(vec_s, vec_r, across)
    swap.wait_recv()
    vec_out[0] = vec_s[...].astype(F32)
    vec_out[1] = vec_r[...].astype(F32)
    for copy in stages + [share, y_cont, y_prompt, swap]:
        copy.wait_send()
    for copy in (back_c, back_p):
        copy.wait_recv()
        copy.wait_send()
    keep_c.wait()
    keep_p.wait()


def finish(hid, gain, bias, dq, dk, dv, wq, wk, wv, gmix, ext, sum_k, sum_v, relay):
    rows, width = dq.shape
    ranks = lax.axis_size("dp")
    bits = ranks.bit_length() - 1
    block = D // ranks
    prompt = sum_k.shape[0]
    conts = rows - prompt
    lanes = 3 * width + 128
    vmem = pl.BlockSpec(memory_space=pltpu.VMEM)
    hbm = pl.BlockSpec(memory_space=pl.ANY)
    shape = jax.ShapeDtypeStruct
    copies = 6 + bits
    stages = []
    for bit in range(bits):
        left = ranks >> (bit + 1)
        stages.append(pltpu.VMEM((left, block, lanes), BF))
        stages.append(pltpu.VMEM((max(left // 2, 1), min(left, 2), block, lanes), BF))
    return pl.pallas_call(
        functools.partial(final_kernel, bits),
        in_specs=[vmem] * 14,
        out_specs=[hbm, vmem, vmem],
        out_shape=[shape((rows, D), BF), shape((block, 3 * width), F32), shape((2, block, 128), F32)],
        scratch_shapes=[
            pltpu.VMEM((2, prompt, width), BF),
            pltpu.VMEM((2, prompt, 128), BF),
            pltpu.VMEM((rows // 2, D), F32),
            pltpu.VMEM((rows // 2, D), F32),
            pltpu.VMEM((D, rows), BF),
            pltpu.VMEM((conts // 2, D), BF),
            pltpu.VMEM((conts // 2, D), BF),
            pltpu.VMEM((prompt // 2, D), BF),
            pltpu.VMEM((prompt // 2, D), BF),
            pltpu.VMEM((conts // 2, D), BF),
            pltpu.VMEM((prompt // 2, D), BF),
            pltpu.VMEM((ranks // 2, 2, block, lanes), BF),
            pltpu.VMEM((8, D + 128), F32),
            pltpu.VMEM((block, 128), BF),
            pltpu.VMEM((block, 128), BF),
            pltpu.SemaphoreType.DMA((copies,)),
            pltpu.SemaphoreType.DMA((copies,)),
            pltpu.SemaphoreType.DMA((2,)),
        ]
        + stages,
        compiler_params=pltpu.CompilerParams(vmem_limit_bytes=56 << 20, collective_id=1, has_side_effects=True),
        cost_estimate=pl.CostEstimate(flops=5 * 10**9, bytes_accessed=20 * 10**6, transcendentals=0),
        name="finish",
    )(hid, gain, bias, dq, dk, dv, wq, wk, wv, gmix, ext, sum_k, sum_v, relay)


def flip(value, axis, bit):
    return lax.ppermute(value, axis, [(i, i ^ (1 << bit)) for i in range(lax.axis_size(axis))])


def contract_rows(left, right):
    return lax.dot_general(left, right, (((0,), (0,)), ((), ())), preferred_element_type=F32)


def back_project(left, right):
    return lax.dot_general(left, right, (((1,), (1,)), ((), ())), preferred_element_type=F32)


def norm_rows(values, gain, bias):
    center = jnp.mean(values, axis=-1, keepdims=True)
    spread = jnp.mean(values * values, axis=-1, keepdims=True) - center * center
    scaled = lax.rsqrt(spread + EPSILON)
    unit_rows = (values - center) * scaled
    return (unit_rows * gain + bias, unit_rows, scaled)


def norm_back(grad_rows, gain, unit_rows, scaled):
    shaped = grad_rows * gain
    return scaled * (
        shaped
        - jnp.mean(shaped, axis=-1, keepdims=True)
        - unit_rows * jnp.mean(shaped * unit_rows, axis=-1, keepdims=True)
    )


def in_order(which, mine, other, axis):
    return jnp.where(
        which == 0,
        jnp.concatenate([mine, other], axis=axis),
        jnp.concatenate([other, mine], axis=axis),
    )


def halving(value, device):
    bits = lax.axis_size("dp").bit_length() - 1
    rows, columns = value.shape
    current = value
    for bit in range(bits):
        upper = device // (1 << bit) % 2
        left = bits - bit
        view = current.reshape((1 << (left - 1), 2, -1, columns))
        kept = lax.dynamic_index_in_dim(view, upper, 1, keepdims=False)
        sent = lax.dynamic_index_in_dim(view, 1 - upper, 1, keepdims=False)
        got = flip(sent, "dp", bit)
        current = (kept.astype(F32) + got.astype(F32)).astype(BF)
    return current.reshape(rows >> bits, columns)


def half_of(value, which):
    prompt, conts = CHUNK // 2, (value.shape[0] - CHUNK) // 2
    return jnp.concatenate(
        [
            lax.dynamic_slice_in_dim(value, which * prompt, prompt),
            lax.dynamic_slice_in_dim(value, CHUNK + which * conts, conts),
        ]
    )


def joined(which, mine, other):
    prompt = CHUNK // 2
    low = jnp.where(which == 0, mine, other)
    high = jnp.where(which == 0, other, mine)
    return jnp.concatenate([low[:prompt], high[:prompt], low[prompt:], high[prompt:]])


def body(
    hidden_in,
    cotangent,
    prompt_start,
    cont_gap,
    seg_len,
    dilation_rate,
    pre_gain,
    pre_bias,
    query_weight,
    query_bias,
    key_weight,
    value_weight,
    value_bias,
    sub_gain,
    sub_bias,
    out_weight,
    out_bias,
    mid_gain,
    mid_bias,
    inner_weight,
    inner_bias,
    ffn_gain,
    ffn_bias,
    outer_weight,
    outer_bias,
):
    device = lax.axis_index("dp")
    ranks = lax.axis_size("dp")
    group_id = device // GDEV
    member = device % GDEV
    tensor_id = lax.axis_index("tensor")
    core = device % 2
    width = query_weight.shape[1]
    units = inner_weight.shape[1]
    pairs = width // 128
    rows = hidden_in.shape[0]
    prompt_rows = CHUNK
    cont_count = (rows - prompt_rows) // CONT

    start_at = lax.dynamic_index_in_dim(prompt_start, group_id, 0, keepdims=False)
    gap_row = lax.dynamic_index_in_dim(cont_gap, group_id, 0, keepdims=False)
    own_gaps = lax.dynamic_slice_in_dim(gap_row, member * cont_count, cont_count)
    info = jnp.concatenate(
        [
            jnp.stack([member, start_at]),
            start_at + member * prompt_rows + TILE * jnp.arange(PTILES),
            start_at + PROMPT + own_gaps,
        ]
    ).astype(jnp.int32)
    seg = lax.dynamic_slice_in_dim(seg_len, tensor_id * pairs, pairs, 0)
    rate = lax.dynamic_slice_in_dim(dilation_rate, tensor_id * pairs, pairs, 0)
    head = 2 * (tensor_id * pairs + jnp.arange(pairs))
    tab = jnp.stack(
        [
            1.0 / seg[:, 0].astype(F32),
            1.0 / seg[:, 1].astype(F32),
            rate[:, 1].astype(F32),
            1.0 / rate[:, 1].astype(F32),
            rate[:, 2].astype(F32),
            1.0 / rate[:, 2].astype(F32),
            (head % rate[:, 1]).astype(F32),
            ((head + 1) % rate[:, 1]).astype(F32),
            (head % rate[:, 2]).astype(F32),
            ((head + 1) % rate[:, 2]).astype(F32),
        ],
        axis=1,
    ).reshape(-1)

    vectors = jnp.concatenate([ffn_gain, ffn_bias, inner_bias, sub_gain, sub_bias]).astype(F32)[None]
    shared = jnp.concatenate([out_bias, mid_gain, mid_bias, outer_bias]).astype(F32)[None]
    pre_gain_f = pre_gain.astype(F32)

    (
        weighed,
        inverse,
        queries,
        keys,
        values,
        prompt_keys,
        prompt_values,
        attended,
        att_mine,
        att_got,
        *pieces,
        vectors_other,
    ) = attend(
        info,
        tab,
        hidden_in,
        pre_gain_f[None],
        pre_bias.astype(F32)[None],
        query_weight,
        key_weight,
        value_weight,
        query_bias.astype(F32)[None],
        value_bias.astype(F32)[None],
        inner_weight,
        out_weight,
        vectors,
    )
    inner_parts = (inner_weight, pieces[0], pieces[1])
    out_parts = (out_weight, pieces[2], pieces[3])

    hidden_rows = half_of(hidden_in, tensor_id)
    cot_rows = half_of(cotangent, tensor_id)
    fused = D % (16 * ranks) == 0
    out_half, grad_mine, grad_theirs, grad_mixed_low, packed, sum_u, sum_w, sum_d, ext = middle(
        att_mine,
        att_got,
        hidden_rows,
        cot_rows,
        vectors,
        vectors_other,
        shared,
        inner_parts,
        outer_weight,
        out_parts,
        ranks if fused else 1,
    )

    early = lax.psum_scatter(packed, "dp", scatter_dimension=0, tiled=True)
    early_mine, early_other = jnp.split(early, 2, axis=1)
    early_sum = early_mine.astype(F32) + flip(early_other, "tensor", 0).astype(F32)
    inner_weight_grad = early_sum[:, :units]
    outer_weight_grad = early_sum[:, units : 2 * units].T
    out_weight_grad = early_sum[:, 2 * units :].T

    grad_query_in, own_key_grad, own_value_grad, key_sum, value_sum, relay, out_got = attend_back(
        queries,
        keys,
        values,
        prompt_keys,
        prompt_values,
        attended,
        inverse,
        weighed,
        grad_mine,
        grad_theirs,
        out_half,
    )
    output = joined(tensor_id, out_half, out_got)
    block = D // ranks
    per_u, per_w, per_d = units // ranks, width // ranks, D // ranks
    if fused:
        input_low, late, vec = finish(
            hidden_in,
            pre_gain_f[None],
            pre_bias.astype(F32)[None],
            grad_query_in,
            own_key_grad,
            own_value_grad,
            query_weight,
            key_weight,
            value_weight,
            grad_mixed_low,
            ext,
            key_sum,
            value_sum,
            relay,
        )
        ffn_gain_grad, ffn_bias_grad, inner_bias_grad = [vec[0, i, :per_u] + vec[1, 8 + i, :per_u] for i in range(3)]
        sub_gain_grad, sub_bias_grad = [vec[0, 16 + i, :per_w] + vec[1, 24 + i, :per_w] for i in range(2)]
        out_bias_grad, mid_gain_grad, mid_bias_grad, outer_bias_grad = [
            vec[0, 32 + i, :per_d] + vec[1, 32 + i, :per_d] for i in range(4)
        ]
        query_bias_grad, value_bias_grad = [vec[0, 40 + i, :per_w] for i in range(2)]
        pre_gain_grad, pre_bias_grad = [vec[0, 42 + i, :per_d] + vec[1, 42 + i, :per_d] for i in range(2)]
    else:
        pre_normed, pre_unit, pre_scale = norm_rows(hidden_in.astype(F32), pre_gain_f, pre_bias.astype(F32))
        pre_low = pre_normed.astype(BF)
        last = width - 128
        far = flip(relay, "dp", 1).astype(F32)
        summed = jnp.stack([key_sum, value_sum]).astype(F32)
        summed = jnp.concatenate([summed[:, :, :last], summed[:, :, last:] + far], axis=2).astype(BF)
        grad_keys = jnp.concatenate([summed[0], own_key_grad[prompt_rows:]], axis=0)
        grad_values = jnp.concatenate([summed[1], own_value_grad[prompt_rows:]], axis=0)

        query_weight_grad = contract_rows(pre_low, grad_query_in)
        key_weight_grad = contract_rows(pre_low, grad_keys)
        value_weight_grad = contract_rows(pre_low, grad_values)
        query_bias_grad = jnp.sum(grad_query_in.astype(F32), axis=0)
        value_bias_grad = jnp.sum(grad_values.astype(F32), axis=0)
        grad_normed_part = (
            back_project(grad_query_in, query_weight)
            + back_project(grad_keys, key_weight)
            + back_project(grad_values, value_weight)
        )
        grad_normed_low = grad_normed_part.astype(BF)
        grad_normed = grad_normed_low.astype(F32) + flip(grad_normed_low, "tensor", 0).astype(F32)
        pre_gain_grad = jnp.sum(grad_normed * pre_unit, axis=0)
        pre_bias_grad = jnp.sum(grad_normed, axis=0)
        grad_mixed_all = joined(tensor_id, grad_mixed_low, flip(grad_mixed_low, "tensor", 0)).astype(F32)
        input_low = (grad_mixed_all + norm_back(grad_normed, pre_gain_f, pre_unit, pre_scale)).astype(BF)

        vec = jnp.concatenate(
            [
                sum_u[:3].reshape(3, 2, ranks, per_u).transpose(2, 1, 0, 3).reshape(ranks, 6 * per_u),
                sum_w[:2].reshape(2, 2, ranks, per_w).transpose(2, 1, 0, 3).reshape(ranks, 4 * per_w),
                sum_d[:4].reshape(4, ranks, per_d).swapaxes(0, 1).reshape(ranks, 4 * per_d),
                jnp.stack([query_bias_grad, value_bias_grad]).reshape(2, ranks, per_w).swapaxes(0, 1).reshape(ranks, 2 * per_w),
                jnp.stack([pre_gain_grad, pre_bias_grad]).reshape(2, ranks, per_d).swapaxes(0, 1).reshape(ranks, 2 * per_d),
            ],
            axis=1,
        )
        count = vec.shape[1]
        vec = jnp.pad(vec, ((0, 0), (0, block * 128 - count))).reshape(D, 128)
        late = halving(
            jnp.concatenate(
                [p.astype(BF) for p in (query_weight_grad, key_weight_grad, value_weight_grad, vec)], axis=1
            ),
            device,
        )
        vec = late[:, 3 * width :].reshape(-1)[:count]
        late = late[:, : 3 * width].astype(F32)
        at_w = 6 * per_u
        at_d = at_w + 4 * per_w
        at_late = at_d + 4 * per_d
        got = flip(vec[:at_late], "tensor", 0).astype(F32)
        vec = vec.astype(F32)
        ffn_gain_grad, ffn_bias_grad, inner_bias_grad = (vec[: 3 * per_u] + got[3 * per_u : at_w]).reshape(3, per_u)
        sub_gain_grad, sub_bias_grad = (vec[at_w : at_w + 2 * per_w] + got[at_w + 2 * per_w : at_d]).reshape(2, per_w)
        out_bias_grad, mid_gain_grad, mid_bias_grad, outer_bias_grad = (vec[at_d:at_late] + got[at_d:]).reshape(4, per_d)
        query_bias_grad, value_bias_grad = vec[at_late : at_late + 2 * per_w].reshape(2, per_w)
        pre_gain_grad, pre_bias_grad = vec[at_late + 2 * per_w :].reshape(2, per_d)
    return (
        output,
        input_low,
        pre_gain_grad,
        pre_bias_grad,
        late[:, :width],
        query_bias_grad,
        late[:, width : 2 * width],
        late[:, 2 * width : 3 * width],
        value_bias_grad,
        sub_gain_grad,
        sub_bias_grad,
        out_weight_grad,
        out_bias_grad,
        mid_gain_grad,
        mid_bias_grad,
        inner_weight_grad,
        inner_bias_grad,
        ffn_gain_grad,
        ffn_bias_grad,
        outer_weight_grad,
        outer_bias_grad,
    )

def solution(mesh):
    placed = (
        P("dp", None),
        P("dp", None),
        P(),
        P(),
        P(),
        P(),
        P(),
        P(),
        P(None, "tensor"),
        P("tensor"),
        P(None, "tensor"),
        P(None, "tensor"),
        P("tensor"),
        P("tensor"),
        P("tensor"),
        P("tensor", None),
        P(),
        P(),
        P(),
        P(None, "tensor"),
        P("tensor"),
        P("tensor"),
        P("tensor"),
        P("tensor", None),
        P(),
    )
    return jax.shard_map(
        body,
        mesh=mesh,
        in_specs=placed,
        out_specs=(
            P("dp", None),
            P("dp", None),
            P("dp"),
            P("dp"),
            P("dp", "tensor"),
            P(("tensor", "dp")),
            P("dp", "tensor"),
            P("dp", "tensor"),
            P(("tensor", "dp")),
            P(("tensor", "dp")),
            P(("tensor", "dp")),
            P("tensor", "dp"),
            P("dp"),
            P("dp"),
            P("dp"),
            P("dp", "tensor"),
            P(("tensor", "dp")),
            P(("tensor", "dp")),
            P(("tensor", "dp")),
            P("tensor", "dp"),
            P("dp"),
        ),
        check_vma=False,
    )
```

```python
import functools

import jax
import jax.numpy as jnp
from jax import lax
from jax.experimental import pallas as pl
from jax.experimental.pallas import tpu as pltpu
from jax.sharding import PartitionSpec as P

HD = 64
PROMPT = 2048
CONT = 256
GDEV = 4
TILE = 256
CHUNK = PROMPT // GDEV
PTILES = CHUNK // TILE
LOG2E = 1.4426950408889634
BF = jnp.bfloat16
F32 = jnp.float32
D = 768
EPSILON = 1e-05
MESH = pl.DeviceIdType.MESH


def dot_nt(a, b):
    return lax.dot_general(a, b, (((1,), (1,)), ((), ())), preferred_element_type=F32)


def dot_nn(a, b):
    return lax.dot_general(a, b, (((1,), (0,)), ((), ())), preferred_element_type=F32)


def low_half(rows):
    return lax.broadcasted_iota(jnp.int32, (rows, 128), 1) < HD


def settings(seg, rate, pair):
    def row(value):
        return jnp.zeros((1, 128), F32) + value.astype(F32)

    def rest(number, period):
        return number - period * jnp.floor((number + 0.5) / period)

    second, third = row(rate[pair, 1]), row(rate[pair, 2])
    head = row(2 * pair)
    return (
        1.0 / row(seg[pair, 0]),
        1.0 / row(seg[pair, 1]),
        second,
        1.0 / second,
        third,
        1.0 / third,
        rest(head, second),
        rest(head + 1.0, second),
        rest(head, third),
        rest(head + 1.0, third),
    )


def codes(at, cells, miss):
    first = jnp.floor((at + 0.5) * cells[0])
    second = jnp.floor((at + 0.5) * cells[1])
    rest1 = at - cells[2] * jnp.floor((at + 0.5) * cells[3])
    rest2 = at - cells[4] * jnp.floor((at + 0.5) * cells[5])
    return [
        first,
        jnp.where(rest1 == cells[6], second, miss),
        jnp.where(rest1 == cells[7], second, miss),
        jnp.where(rest2 == cells[8], 1.0, 0.0),
        jnp.where(rest2 == cells[9], 1.0, 0.0),
    ]


def bit_peer(device, bit):
    step = 1 << bit
    return device + (1 - 2 * ((device // step) % 2)) * step


def greet(peers):
    barrier = pltpu.get_barrier_semaphore()
    for peer in peers:
        pl.semaphore_signal(barrier, inc=1, device_id=peer, device_id_type=MESH)
    pl.semaphore_wait(barrier, len(peers))


def xor_bits(a, b):
    return (a % 2 + b % 2) % 2 + 2 * ((a // 2 + b // 2) % 2)


def fwd_kernel(
    starts, gaps, seg, rate, hid, vec, wq, wk, wv, w1, wo, vec_hbm,
    e_ref, li_ref, q_out, k_out, v_out, kp_out, vp_out, o_out, mine_out, got_out,
    w1_got, w1_swap, wo_got, wo_swap, vec_got,
    t_s, kc_s, kv_s, low_s, q_s, ko_s, vo_s, o_s, sems_a, sems_b, loc_sems,
):
    pair = pl.program_id(0)
    step = pl.program_id(1)
    pairs = pl.num_programs(0)
    device = lax.axis_index("dp")
    side = lax.axis_index("tensor")
    member = device % GDEV
    core = device % 2
    rows, width = q_s.shape
    n_pairs = width // 128
    last_pair = n_pairs - 1
    conts = rows - CHUNK
    near = {"dp": bit_peer(device, 0), "tensor": side}
    far = {"dp": bit_peer(device, 1), "tensor": side}
    across = {"dp": device, "tensor": 1 - side}
    half_u = w1.shape[1] // 2
    half_w = wo.shape[0] // 2
    half_p, half_c = CHUNK // 2, conts // 2
    sent_u = pl.multiple_of(core * half_u, 128)
    shared_at = 2 * D + 2 * width
    sent_w = pl.multiple_of(core * half_w, 64)

    def remote(i, src, dst, peer):
        return pltpu.make_async_remote_copy(
            src_ref=src, dst_ref=dst, send_sem=sems_a.at[i], recv_sem=sems_b.at[i], device_id=peer, device_id_type=MESH
        )

    def to_far(p):
        lanes = pl.ds(p * 128, 128)
        return remote(3 * p, kv_s.at[0, :, :, lanes], kv_s.at[2, :, :, lanes], far)

    def to_near(p):
        lanes = pl.ds(p * 128, 128)
        return remote(3 * p + 1, kv_s.at[0, :, :, lanes], kv_s.at[1, :, :, lanes], near)

    def relay(p):
        lanes = pl.ds(p * 128, 128)
        return remote(3 * p + 2, kv_s.at[2, :, :, lanes], kv_s.at[3, :, :, lanes], near)

    base = 3 * n_pairs
    fetch_y = [
        remote(base, wo.at[pl.ds(sent_w, half_w), :], wo_got, across),
        remote(base + 1, w1.at[:, pl.ds(sent_u, half_u)], w1_got, across),
        remote(base + 2, vec_hbm.at[:, pl.ds(shared_at, vec_got.shape[1])], vec_got, across),
    ]
    fetch_core = [
        remote(base + 3, wo_got, wo_swap, near),
        remote(base + 4, w1_got, w1_swap, near),
    ]

    def give(p, piece):
        lanes = pl.ds(p * 128, 128)
        their_p = pl.multiple_of((1 - side) * half_p, 128)
        their_c = pl.multiple_of(CHUNK + (1 - side) * half_c, 128)
        third = half_c // 3
        if piece == 0:
            source, target = pl.ds(their_p, half_p), pl.ds(0, half_p)
        else:
            source = pl.ds(pl.multiple_of(their_c + (piece - 1) * third, 128), third)
            target = pl.ds(half_p + (piece - 1) * third, third)
        return remote(base + 5 + 4 * p + piece, o_s.at[source, lanes], got_out.at[target, lanes], across)

    def keeps():
        own_p = pl.multiple_of(side * half_p, 128)
        own_c = pl.multiple_of(CHUNK + side * half_c, 128)
        return [
            pltpu.make_async_copy(o_s, o_out, loc_sems.at[0]),
            pltpu.make_async_copy(o_s.at[pl.ds(own_p, half_p), :], mine_out.at[pl.ds(0, half_p), :], loc_sems.at[1]),
            pltpu.make_async_copy(o_s.at[pl.ds(own_c, half_c), :], mine_out.at[pl.ds(half_p, half_c), :], loc_sems.at[2]),
        ]

    def saves():
        out = [
            pltpu.make_async_copy(q_s, q_out, loc_sems.at[3]),
            pltpu.make_async_copy(ko_s, k_out, loc_sems.at[0]),
            pltpu.make_async_copy(vo_s, v_out, loc_sems.at[5]),
        ]
        for r in range(GDEV):
            span = pl.ds(r * CHUNK, CHUNK)
            out.append(pltpu.make_async_copy(kv_s.at[r, 0], kp_out.at[span, :], loc_sems.at[6 + 2 * r]))
            out.append(pltpu.make_async_copy(kv_s.at[r, 1], vp_out.at[span, :], loc_sems.at[7 + 2 * r]))
        return out

    @pl.when((pair == 0) & (step == 0))
    def _():
        greet([near, far, across])
        for copy in fetch_y:
            copy.start()
        gain_f, bias_f = vec[:, pl.ds(0, D)], vec[:, pl.ds(D, D)]
        query_bias = vec[:, pl.ds(2 * D, width)]
        value_bias = vec[:, pl.ds(2 * D + width, width)]

        def norm(at, size):
            x = hid[at : at + size, :].astype(F32)
            center = jnp.mean(x, axis=1, keepdims=True)
            scale = lax.rsqrt(jnp.mean(x * x, axis=1, keepdims=True) - center * center + EPSILON)
            low = ((x - center) * scale * gain_f + bias_f).astype(BF)
            low_s[at : at + size, :] = low
            return low

        low = norm(0, CHUNK)
        kv_s[0, 0] = dot_nn(low, wk[...]).astype(BF)
        kv_s[0, 1] = (dot_nn(low, wv[...]) + value_bias).astype(BF)
        to_far(0).start()
        for p in range(n_pairs):
            to_near(p).start()
        for at in range(CHUNK, rows, TILE):
            low = norm(at, TILE)
            ko_s[at - CHUNK : at - CHUNK + TILE, :] = dot_nn(low, wk[...]).astype(BF)
            vo_s[at - CHUNK : at - CHUNK + TILE, :] = (dot_nn(low, wv[...]) + value_bias).astype(BF)
        to_far(0).wait_send()
        for p in range(1, n_pairs):
            to_far(p).start()
        for at in range(0, rows, TILE):
            q_s[at : at + TILE, :] = ((dot_nn(low_s[at : at + TILE, :], wq[...]) + query_bias) * 0.125).astype(BF)
        to_far(0).wait_recv()
        relay(0).start()

    for p in range(n_pairs):
        @pl.when((pair == p) & (step == 0))
        def _():
            to_near(p).wait_recv()
            relay(p).wait_recv()

        if p + 1 < n_pairs:
            @pl.when((pair == p) & (step == 3))
            def _():
                to_far(p + 1).wait_recv()
                relay(p + 1).start()

    lanes = pl.ds(pl.multiple_of(pair * 128, 128), 128)
    low = low_half(TILE)
    q = q_s[pl.ds(pl.multiple_of(step * TILE, TILE), TILE), lanes]
    zero = jnp.zeros_like(q)
    qs = [jnp.where(low, q, zero), jnp.where(low, zero, q)]
    row = lax.broadcasted_iota(jnp.int32, (TILE, 128), 0).astype(F32)
    group = device // GDEV
    start = starts[group]
    first_cont = member * (conts // CONT)
    own_gap = gaps[group, first_cont + jnp.maximum(step - PTILES, 0)]
    base_q = start + jnp.where(step < PTILES, member * CHUNK + step * TILE, PROMPT + own_gap)
    cells = settings(seg, rate, side * n_pairs + pair)
    at_q = base_q.astype(F32) + row
    qc = codes(at_q, cells, -2.0)

    @pl.when(step == 0)
    def _():
        ahead = lax.broadcasted_iota(jnp.int32, (8, 128), 1).astype(F32) + start.astype(F32)
        for j in range(PROMPT // 128):
            for i, c in enumerate(codes(ahead + j * 128.0, cells, -1.0)):
                kc_s[i, :, j * 128 : (j + 1) * 128] = c

    def logits(mx, keys, kc, causal, at, span):
        out = []
        for h in range(2):
            s = dot_nt(qs[h], keys)
            top = mx[h]
            for g in range(span // 128):
                part = slice(g * 128, (g + 1) * 128)
                w = jnp.where(qc[0] == kc[0][:, part], 1.0, 0.0)
                w = w + jnp.where(qc[1 + h] == kc[1 + h][:, part], 1.0, 0.0)
                w = w + qc[3 + h] * kc[3 + h][:, part]
                if causal is not None:
                    w = jnp.where(causal[:, part], w, 0.0)
                t = s[:, part] * LOG2E + jnp.log2(w)
                t_s[h, :, pl.ds(at + g * 128, 128)] = t
                top = jnp.maximum(top, t)
            out.append(top)
        return tuple(out)

    def weigh(carry, vals, m, at, span):
        sums, accs = carry
        ns, na = [], []
        for h in range(2):
            total = sums[h]
            parts = []
            for g in range(span // 128):
                e = jnp.exp2(t_s[h, :, pl.ds(at + g * 128, 128)] - m[h])
                total = total + e
                parts.append(e.astype(BF))
            el = jnp.concatenate(parts, axis=1)
            e_ref[h, :, pl.ds(at, span)] = el
            ns.append(total)
            na.append(accs[h] + dot_nn(el, vals))
        return (tuple(ns), tuple(na))

    def finish_rows(carry):
        sums, accs = carry
        li = [1.0 / jnp.sum(s, axis=1, keepdims=True) for s in sums]
        lfull = jnp.where(low, li[0], li[1])
        li_ref[...] = lfull
        o_s[pl.ds(pl.multiple_of(step * TILE, TILE), TILE), lanes] = (jnp.where(low, accs[0], accs[1]) * lfull).astype(BF)

    def tops(mx):
        return [jnp.broadcast_to(jnp.max(x, axis=1, keepdims=True), (TILE, 128)) for x in mx]

    neg = jnp.full((TILE, 128), -jnp.inf, F32)
    zf = jnp.zeros((TILE, 128), F32)

    def key_codes(at, span):
        return [kc_s[i, 0:1, pl.ds(at, span)] for i in range(5)]

    @pl.when(step < PTILES)
    def _():
        def one(j, mx):
            at = pl.multiple_of(j * CHUNK, CHUNK)
            held = xor_bits(j, member)
            return logits(
                mx, kv_s[held, 0, :, lanes], key_codes(at, CHUNK), None, pl.multiple_of(held * CHUNK, CHUNK), CHUNK
            )

        mx = lax.fori_loop(0, member, one, (neg, neg))
        at = pl.multiple_of(member * CHUNK, CHUNK)
        rows_id = lax.broadcasted_iota(jnp.int32, (TILE, CHUNK), 0) + step * TILE
        cols = lax.broadcasted_iota(jnp.int32, (TILE, CHUNK), 1)
        mx = logits(mx, kv_s[0, 0, :, lanes], key_codes(at, CHUNK), cols <= rows_id, 0, CHUNK)
        m = tops(mx)

        def two(j, carry):
            held = xor_bits(j, member)
            return weigh(carry, kv_s[held, 1, :, lanes], m, pl.multiple_of(held * CHUNK, CHUNK), CHUNK)

        finish_rows(lax.fori_loop(0, member + 1, two, ((zf, zf), (zf, zf))))

    @pl.when(step >= PTILES)
    def _():
        own = pl.ds(pl.multiple_of((step - PTILES) * TILE, TILE), TILE)
        mx = (neg, neg)
        for j in range(GDEV):
            at = pl.multiple_of(xor_bits(j, member) * CHUNK, CHUNK)
            mx = logits(mx, kv_s[j, 0, :, lanes], key_codes(at, CHUNK), None, j * CHUNK, CHUNK)
        rows_id = lax.broadcasted_iota(jnp.int32, (TILE, CONT), 0)
        cols = lax.broadcasted_iota(jnp.int32, (TILE, CONT), 1)
        ahead = lax.broadcasted_iota(jnp.int32, (8, 128), 1).astype(F32) + base_q.astype(F32)
        parts = [codes(ahead + j * 128.0, cells, -1.0) for j in range(CONT // 128)]
        own_codes = [jnp.concatenate([part[i] for part in parts], axis=1)[0:1] for i in range(5)]
        mx = logits(mx, ko_s[own, lanes], own_codes, cols <= rows_id, PROMPT, CONT)
        m = tops(mx)
        carry = ((zf, zf), (zf, zf))
        for j in range(GDEV):
            carry = weigh(carry, kv_s[j, 1, :, lanes], m, j * CHUNK, CHUNK)
        finish_rows(weigh(carry, vo_s[own, lanes], m, PROMPT, CONT))

    end = pl.num_programs(1) - 1
    for p in range(n_pairs):
        @pl.when((pair == p) & (step == 1 - side))
        def _():
            give(p, 0).start()

        for unit in range(6):
            @pl.when((pair == p) & (step == PTILES + unit // 2) & (side == 1 - unit // 3))
            def _():
                give(p, 1 + unit % 3).start()

    @pl.when((pair == last_pair - 1) & (step == 3))
    def _():
        for i in range(2):
            fetch_y[i].wait_recv()
            fetch_core[i].start()

    @pl.when((pair == last_pair) & (step == 0))
    def _():
        for copy in saves():
            copy.start()

    @pl.when((pair == last_pair) & (step == end))
    def _():
        for copy in keeps():
            copy.start()
        fetch_y[2].wait_recv()
        for copy in fetch_core:
            copy.wait_recv()
        for p in range(n_pairs):
            for piece in range(4):
                copy = give(p, piece)
                copy.wait_recv()
                copy.wait_send()
            if p > 0:
                to_far(p).wait_send()
            to_near(p).wait_send()
            relay(p).wait_send()
        for copy in fetch_y + fetch_core:
            copy.wait_send()
        for copy in keeps() + saves():
            copy.wait()


def attend(starts, gaps, seg, rate, hid, vec, wq, wk, wv, w1, wo):
    rows = hid.shape[0]
    width = wq.shape[1]
    pairs = width // 128
    span = PROMPT + CONT
    conts = rows - CHUNK
    units = w1.shape[1]
    vmem = pl.BlockSpec(memory_space=pltpu.VMEM)
    hbm = pl.BlockSpec(memory_space=pl.ANY)
    shape = jax.ShapeDtypeStruct
    copies = 3 * pairs + 5 + 4 * pairs
    shared = 3 * units + 2 * width
    smem = pl.BlockSpec(memory_space=pltpu.SMEM)
    return pl.pallas_call(
        fwd_kernel,
        grid_spec=pltpu.PrefetchScalarGridSpec(
            num_scalar_prefetch=0,
            grid=(pairs, rows // TILE),
            in_specs=[smem] * 4 + [vmem] * 5 + [hbm] * 3,
            out_specs=[
                pl.BlockSpec((2, TILE, span), lambda a, t: (a, t, 0)),
                pl.BlockSpec((TILE, 128), lambda a, t: (t, a)),
            ]
            + [hbm] * 13,
            scratch_shapes=[
                pltpu.VMEM((2, TILE, span), F32),
                pltpu.VMEM((5, 8, PROMPT), F32),
                pltpu.VMEM((GDEV, 2, CHUNK, width), BF),
                pltpu.VMEM((rows, D), BF),
                pltpu.VMEM((rows, width), BF),
                pltpu.VMEM((conts, width), BF),
                pltpu.VMEM((conts, width), BF),
                pltpu.VMEM((rows, width), BF),
                pltpu.SemaphoreType.DMA((copies,)),
                pltpu.SemaphoreType.DMA((copies,)),
                pltpu.SemaphoreType.DMA((6 + 2 * GDEV,)),
            ],
        ),
        out_shape=[
            shape((2 * pairs, rows, span), BF),
            shape((rows, width), F32),
            shape((rows, width), BF),
            shape((conts, width), BF),
            shape((conts, width), BF),
            shape((PROMPT, width), BF),
            shape((PROMPT, width), BF),
            shape((rows, width), BF),
            shape((rows // 2, width), BF),
            shape((rows // 2, width), BF),
            shape((D, units // 2), BF),
            shape((D, units // 2), BF),
            shape((width // 2, D), BF),
            shape((width // 2, D), BF),
            shape((1, shared), F32),
        ],
        compiler_params=pltpu.CompilerParams(vmem_limit_bytes=56 << 20, collective_id=0, has_side_effects=True),
        cost_estimate=pl.CostEstimate(flops=20 * 10**9, bytes_accessed=60 * 10**6, transcendentals=0),
        name="attend",
    )(starts, gaps, seg, rate, hid, vec, wq, wk, wv, w1, wo, vec)


def bwd_kernel(
    q_ref, kp_ref, vp_ref, ko_ref, vo_ref, o_ref, li_ref, e_ref, g_mine, g_theirs, out_half,
    dq_ref, dko_ref, dvo_ref, sum_k, sum_v, relay_out, out_got,
    dk_s, dv_s, g_s, grad_s, near_s, relay_s, far_s, sems_a, sems_b, loc_sems,
):
    pair = pl.program_id(0)
    step = pl.program_id(1)
    device = lax.axis_index("dp")
    side = lax.axis_index("tensor")
    member = device % GDEV
    rows, width = g_s.shape
    n_pairs = width // 128
    conts = rows - CHUNK
    half_p, half_c = CHUNK // 2, conts // 2
    near = {"dp": bit_peer(device, 0), "tensor": side}
    far = {"dp": bit_peer(device, 1), "tensor": side}
    across = {"dp": device, "tensor": 1 - side}
    lanes = pl.ds(pl.multiple_of(pair * 128, 128), 128)
    mine_p = pl.ds(pl.multiple_of(side * half_p, 128), half_p)
    mine_c = pl.ds(pl.multiple_of(CHUNK + side * half_c, 128), half_c)

    def remote(i, src, dst, peer):
        return pltpu.make_async_remote_copy(
            src_ref=src, dst_ref=dst, send_sem=sems_a.at[i], recv_sem=sems_b.at[i], device_id=peer, device_id_type=MESH
        )

    def heads():
        return [
            remote(0, g_theirs.at[pl.ds(0, half_p), :], g_s.at[mine_p, :], across),
            remote(1, g_theirs.at[pl.ds(half_p, half_c), :], g_s.at[mine_c, :], across),
            remote(2, out_half, out_got, across),
        ]

    def local():
        return [
            pltpu.make_async_copy(g_mine.at[pl.ds(0, half_p), :], g_s.at[mine_p, :], loc_sems.at[0]),
            pltpu.make_async_copy(g_mine.at[pl.ds(half_p, half_c), :], g_s.at[mine_c, :], loc_sems.at[1]),
        ]

    def cores(p):
        part = pl.ds(p * 128, 128)
        return remote(3 + 2 * p, grad_s.at[:, :, 1, :, part], near_s.at[:, :, :, part], near)

    def chips(p):
        part = pl.ds(p * 128, 128)
        return remote(4 + 2 * p, relay_s.at[:, :, part], far_s.at[:, :, part], far)

    @pl.when((pair == 0) & (step == 0))
    def _():
        greet([near, far, across])
        for copy in heads() + local():
            copy.start()
        for copy in local():
            copy.wait()

    @pl.when((pair == 0) & (step == 1 - side))
    def _():
        heads()[0].wait_recv()

    @pl.when((pair == 0) & (step == 3 - side))
    def _():
        heads()[1].wait_recv()

    low = low_half(TILE)
    g = g_s[pl.ds(pl.multiple_of(step * TILE, TILE), TILE), lanes].astype(F32) * li_ref[...]
    prod = g * o_ref[...].astype(F32)
    zf = jnp.zeros((TILE, 128), F32)
    deltas = [
        jnp.sum(jnp.where(low, prod, zf), axis=1, keepdims=True),
        jnp.sum(jnp.where(low, zf, prod), axis=1, keepdims=True),
    ]
    gs = [jnp.where(low, g, zf).astype(BF), jnp.where(low, zf, g).astype(BF)]
    gt = jnp.transpose(g).astype(BF)
    qt = jnp.transpose(q_ref[...].astype(F32)).astype(BF)

    def grads(dq, keys, vals, at, width):
        out, dks, dvs = [], [], []
        for h in range(2):
            e = e_ref[h, :, pl.ds(at, width)]
            dp = dot_nt(gs[h], vals)
            ds = (e.astype(F32) * (dp - deltas[h])).astype(BF)
            out.append(dq[h] + dot_nn(ds, keys))
            dks.append(dot_nn(qt[h * HD : (h + 1) * HD, :], ds))
            dvs.append(dot_nn(gt[h * HD : (h + 1) * HD, :], e))
        return tuple(out), dks, dvs

    @pl.when(step == 0)
    def _():
        dk_s[...] = jnp.zeros_like(dk_s)
        dv_s[...] = jnp.zeros_like(dv_s)

    def add(at, width, dks, dvs):
        for h in range(2):
            dk_s[h * HD : (h + 1) * HD, pl.ds(at, width)] += dks[h]
            dv_s[h * HD : (h + 1) * HD, pl.ds(at, width)] += dvs[h]

    def scaled(dq):
        return (jnp.where(low, dq[0], dq[1]).astype(BF).astype(F32) * 0.125).astype(BF)

    @pl.when(step < PTILES)
    def _():
        def one(j, dq):
            at = pl.multiple_of(xor_bits(j, member) * CHUNK, CHUNK)
            dq, dks, dvs = grads(dq, kp_ref[pl.ds(at, CHUNK), :], vp_ref[pl.ds(at, CHUNK), :], at, CHUNK)
            add(at, CHUNK, dks, dvs)
            return dq

        dq_ref[...] = scaled(lax.fori_loop(0, member + 1, one, (zf, zf)))
        dko_ref[...] = jnp.zeros_like(dko_ref)
        dvo_ref[...] = jnp.zeros_like(dvo_ref)

    @pl.when(step >= PTILES)
    def _():
        dq = (zf, zf)
        for j in range(GDEV):
            span = slice(j * CHUNK, (j + 1) * CHUNK)
            dq, dks, dvs = grads(dq, kp_ref[span, :], vp_ref[span, :], j * CHUNK, CHUNK)
            add(j * CHUNK, CHUNK, dks, dvs)
        dq, dks, dvs = grads(dq, ko_ref[...], vo_ref[...], PROMPT, CONT)
        dq_ref[...] = scaled(dq)
        dko_ref[...] = jnp.transpose(jnp.concatenate(dks, axis=0)).astype(BF)
        dvo_ref[...] = jnp.transpose(jnp.concatenate(dvs, axis=0)).astype(BF)

    end = pl.num_programs(1) - 1

    @pl.when(step == end)
    def _():
        for j in range(GDEV):
            span = slice(j * CHUNK, (j + 1) * CHUNK)
            grad_s[0, j // 2, j % 2, :, lanes] = jnp.transpose(dk_s[:, span]).astype(BF)
            grad_s[1, j // 2, j % 2, :, lanes] = jnp.transpose(dv_s[:, span]).astype(BF)

    for p in range(n_pairs):
        @pl.when((pair == p) & (step == end))
        def _():
            cores(p).start()

        if p + 1 < n_pairs:
            @pl.when((pair == p + 1) & (step == 2))
            def _():
                part = pl.ds(p * 128, 128)
                cores(p).wait_recv()
                relay_s[:, :, part] = (
                    grad_s[:, 1, 0, :, part].astype(F32) + near_s[:, 1, :, part].astype(F32)
                ).astype(BF)
                chips(p).start()

    @pl.when((pair == n_pairs - 1) & (step == end))
    def _():
        last = n_pairs - 1
        sums = (sum_k, sum_v)
        for p in range(last):
            part = pl.ds(p * 128, 128)
            chips(p).wait_recv()
            for i in range(2):
                sums[i][:, part] = (
                    grad_s[i, 0, 0, :, part].astype(F32) + near_s[i, 0, :, part].astype(F32) + far_s[i, :, part].astype(F32)
                ).astype(BF)
        part = pl.ds(last * 128, 128)
        cores(last).wait_recv()
        for i in range(2):
            relay_out[i] = (grad_s[i, 1, 0, :, part].astype(F32) + near_s[i, 1, :, part].astype(F32)).astype(BF)
            sums[i][:, part] = (grad_s[i, 0, 0, :, part].astype(F32) + near_s[i, 0, :, part].astype(F32)).astype(BF)
        heads()[2].wait_recv()
        for copy in heads():
            copy.wait_send()
        for p in range(n_pairs):
            cores(p).wait_send()
            if p < last:
                chips(p).wait_send()


def attend_back(q, k, v, kp, vp, o, li, e, g_mine, g_theirs, out_half):
    rows, width = q.shape
    pairs = width // 128
    span = PROMPT + CONT
    tile = pl.BlockSpec((TILE, 128), lambda a, t: (t, a))
    whole = pl.BlockSpec((PROMPT, 128), lambda a, t: (0, a))
    own = pl.BlockSpec((TILE, 128), lambda a, t: (jnp.maximum(t - PTILES, 0), a))
    vmem = pl.BlockSpec(memory_space=pltpu.VMEM)
    hbm = pl.BlockSpec(memory_space=pl.ANY)
    shape = jax.ShapeDtypeStruct
    copies = 3 + 2 * pairs
    return pl.pallas_call(
        bwd_kernel,
        grid=(pairs, rows // TILE),
        in_specs=[tile, whole, whole, own, own, tile, tile, pl.BlockSpec((2, TILE, span), lambda a, t: (a, t, 0))]
        + [hbm] * 3,
        out_specs=[tile, tile, tile, vmem, vmem, vmem, hbm],
        out_shape=[
            shape((rows, width), BF),
            shape((rows, width), BF),
            shape((rows, width), BF),
            shape((CHUNK, width), BF),
            shape((CHUNK, width), BF),
            shape((2, CHUNK, 128), BF),
            shape(out_half.shape, BF),
        ],
        scratch_shapes=[
            pltpu.VMEM((128, PROMPT), F32),
            pltpu.VMEM((128, PROMPT), F32),
            pltpu.VMEM((rows, width), BF),
            pltpu.VMEM((2, 2, 2, CHUNK, width), BF),
            pltpu.VMEM((2, 2, CHUNK, width), BF),
            pltpu.VMEM((2, CHUNK, width), BF),
            pltpu.VMEM((2, CHUNK, width), BF),
            pltpu.SemaphoreType.DMA((copies,)),
            pltpu.SemaphoreType.DMA((copies,)),
            pltpu.SemaphoreType.DMA((2,)),
        ],
        compiler_params=pltpu.CompilerParams(vmem_limit_bytes=56 << 20, collective_id=2, has_side_effects=True),
        cost_estimate=pl.CostEstimate(flops=30 * 10**9, bytes_accessed=60 * 10**6, transcendentals=0),
        name="attend_back",
    )(q, kp, vp, k, v, o, li, e, g_mine, g_theirs, out_half)


UCH = 512


def polynomial(x, terms):
    out = jnp.full_like(x, terms[0])
    for term in terms[1:]:
        out = out * x + term
    return out


def error_function(x):
    x = jnp.clip(x, -3.832506856900711, 3.832506856900711)
    square = x * x
    top = polynomial(
        square,
        (0.00022905065861350646, 0.0034082910107109506, 0.050955695062380861, 0.18520832239976145, 1.128379143519084),
    )
    bottom = polynomial(
        square,
        (
            -1.1791602954361697e-7,
            0.000023547966471313185,
            0.0010179625278914885,
            0.014070470171167667,
            0.11098505178285362,
            0.49746925110067538,
            1.0,
        ),
    )
    return x * top / bottom


def gelu_pair(v):
    phi = 0.5 + 0.5 * error_function(v * 0.7071067811865476)
    density = jnp.exp(-0.5 * v * v) * 0.3989422804014327
    return v * phi, phi + v * density


def column_sum(x):
    return jnp.sum(x, axis=0, keepdims=True)


def mid_kernel(
    att_m, att_o, vec_all, vec_got, hid_all, cot_all, w1_own, w1_got, w1_swap, wo_own, wo_got, wo_swap, w2_own,
    out_ref, gatt_m, gatt_o, gmix_ref, packed, su_ref, sw_ref, sd_ref, ext_ref,
    vec_u, vec_w, w1, w2, wo, act_s, shp_s, dg_s, wide_s, acc_s, gmid_s, sub_s, mid_s, low_s, midt_s, cott_s, stage, hid, cot, sems, out_sems, send_sems, recv_sems,
):
    device = lax.axis_index("dp")
    side = lax.axis_index("tensor")
    core = device % 2
    near = {"dp": bit_peer(device, 0), "tensor": side}
    across = {"dp": device, "tensor": 1 - side}
    units = w1_own.shape[1]
    width = wo_own.shape[0]
    rows = hid.shape[0]
    full = 2 * units
    half = units // 2
    half_w = width // 2
    here_u = pl.multiple_of(units + core * half, 128)
    there_u = pl.multiple_of(units + (1 - core) * half, 128)
    here_w = pl.multiple_of(width + core * half_w, 64)
    there_w = pl.multiple_of(width + (1 - core) * half_w, 64)
    prompt, conts = CHUNK // 2, (hid_all.shape[0] - CHUNK) // 2
    own_p = pl.ds(pl.multiple_of(side * prompt, 128), prompt)
    own_c = pl.ds(pl.multiple_of(CHUNK + side * conts, 128), conts)
    at_own = 2 * D + 2 * width
    vec_own = vec_all.at[:, pl.ds(at_own, 3 * units + 2 * width)]
    vec_d = vec_all.at[:, pl.ds(at_own + 3 * units + 2 * width, 4 * D)]
    rows_in = []
    for i, (all_rows, held) in enumerate(((hid_all, hid), (cot_all, cot))):
        for j, (span, at, size) in enumerate(((own_p, 0, prompt), (own_c, prompt, conts))):
            copy = pltpu.make_async_copy(all_rows.at[span, :], held.at[pl.ds(at, size), :], sems.at[7 + 2 * i + j])
            copy.start()
            rows_in.append(copy)
    loads = []
    for i, (src, dst) in enumerate(
        [
            (wo_own, wo.at[pl.ds(0, width), :]),
            (wo_got, wo.at[pl.ds(here_w, half_w), :]),
            (wo_swap, wo.at[pl.ds(there_w, half_w), :]),
            (w1_own, w1.at[:, pl.ds(0, units)]),
            (w1_got, w1.at[:, pl.ds(here_u, half)]),
            (w1_swap, w1.at[:, pl.ds(there_u, half)]),
            (w2_own, w2.at[pl.ds(0, units), :]),
        ]
    ):
        copy = pltpu.make_async_copy(src, dst, sems.at[i])
        copy.start()
        loads.append(copy)

    piece = half // 2
    greet([near, across])

    def remote(i, src, dst, peer):
        return pltpu.make_async_remote_copy(
            src_ref=src, dst_ref=dst, send_sem=send_sems.at[i], recv_sem=recv_sems.at[i], device_id=peer, device_id_type=MESH
        )

    over, passed = [], []
    for i in range(2):
        from_own = pl.ds(pl.multiple_of(core * half + i * piece, 128), piece)
        landed = w2.at[pl.ds(pl.multiple_of(units + core * half + i * piece, 128), piece), :]
        over.append(remote(i, w2_own.at[from_own, :], landed, across))
        passed.append(remote(2 + i, landed, landed, near))
        over[i].start()

    for i in range(3):
        for j, vec in enumerate((vec_own, vec_got)):
            vec_u[i : i + 1, pl.ds(j * units, units)] = vec[0:1, pl.ds(i * units, units)]
    for i in range(2):
        for j, vec in enumerate((vec_own, vec_got)):
            vec_w[i : i + 1, pl.ds(j * width, width)] = vec[0:1, pl.ds(3 * units + i * width, width)]

    a0 = att_m[...].astype(F32)
    a1 = att_o[...].astype(F32)
    center = (jnp.sum(a0, axis=1, keepdims=True) + jnp.sum(a1, axis=1, keepdims=True)) * (1.0 / D)
    square = (jnp.sum(a0 * a0, axis=1, keepdims=True) + jnp.sum(a1 * a1, axis=1, keepdims=True)) * (1.0 / D)
    sub_scale = lax.rsqrt(square - center * center + EPSILON)
    sub_s[:, 0:width] = (a0 - center) * sub_scale
    sub_s[:, width : 2 * width] = (a1 - center) * sub_scale
    sub_gain = vec_w[0:1, :]
    low_s[...] = (sub_s[...] * sub_gain + vec_w[1:2, :]).astype(BF)
    for copy in loads[0:3] + rows_in:
        copy.wait()
    mixed = hid[...].astype(F32) + (dot_nn(low_s[...], wo[...]) + vec_d[0:1, pl.ds(0, D)])
    wide_s[...] = mixed
    mean = jnp.mean(mixed, axis=1, keepdims=True)
    mid_scale = lax.rsqrt(jnp.mean(mixed * mixed, axis=1, keepdims=True) - mean * mean + EPSILON)
    mid_s[...] = (mixed - mean) * mid_scale
    mid_gain = vec_d[0:1, pl.ds(768, D)]
    mid_full = mid_s[...] * mid_gain + vec_d[0:1, pl.ds(1536, D)]
    mid_low = mid_full.astype(BF)
    midt_s[...] = jnp.transpose(mid_full).astype(BF)
    cot_full = cot[...].astype(F32)
    cott_s[...] = jnp.transpose(cot_full).astype(BF)
    sd_ref[...] = jnp.zeros_like(sd_ref)
    sd_ref[3:4, :] = column_sum(cot_full)
    for copy in loads[3:6]:
        copy.wait()

    def lanes_sum(x):
        total = x[:, 0:128]
        for i in range(1, x.shape[1] // 128):
            total = total + x[:, i * 128 : (i + 1) * 128]
        return total

    def first(c, carry):
        at = pl.multiple_of(c * UCH, UCH)
        inner = dot_nn(mid_low, w1[:, pl.ds(at, UCH)]) + vec_u[2:3, pl.ds(at, UCH)]
        act, slope = gelu_pair(inner)
        act_s[:, pl.ds(at, UCH)] = act
        dg_s[:, pl.ds(at, UCH)] = slope.astype(BF)
        return carry[0] + lanes_sum(act), carry[1] + lanes_sum(act * act)

    zero = jnp.zeros((rows, 128), F32)
    act_sum, act_square = lax.fori_loop(0, full // UCH, first, (zero, zero))
    ffn_center = jnp.sum(act_sum, axis=1, keepdims=True) * (1.0 / full)
    ffn_scale = lax.rsqrt(
        jnp.sum(act_square, axis=1, keepdims=True) * (1.0 / full) - ffn_center * ffn_center + EPSILON
    )
    loads[6].wait()
    over[0].wait_recv()
    passed[0].start()
    acc_s[...] = jnp.zeros_like(acc_s)
    per = units // UCH
    wide = 2 * units + width

    def column_of(c, extra):
        return pl.multiple_of((c // per) * wide + lax.rem(c, per) * UCH + extra, 128)

    def send(slot, column):
        return pltpu.make_async_copy(stage.at[slot], packed.at[:, pl.ds(column, UCH)], out_sems.at[slot])

    def put(c, value, extra):
        slot = lax.rem(c, 2)

        @pl.when(c >= 2)
        def _():
            send(slot, column_of(c - 2, extra)).wait()

        stage[slot] = value
        send(slot, column_of(c, extra)).start()

    def drain(extra):
        for c in range(full // UCH - 2, full // UCH):
            send(c % 2, column_of(c, extra)).wait()

    def second(c, carry):
        at = pl.multiple_of(c * UCH, UCH)
        unit = (act_s[:, pl.ds(at, UCH)] - ffn_center) * ffn_scale
        act_s[:, pl.ds(at, UCH)] = unit
        gain = vec_u[0:1, pl.ds(at, UCH)]
        low = (unit * gain + vec_u[1:2, pl.ds(at, UCH)]).astype(BF)
        acc_s[...] += dot_nn(low, w2[pl.ds(at, UCH), :])
        grad = dot_nt(cot[...], w2[pl.ds(at, UCH), :])
        cross = grad * unit
        su_ref[0:1, pl.ds(at, UCH)] = column_sum(cross)
        su_ref[1:2, pl.ds(at, UCH)] = column_sum(grad)
        shaped = grad * gain
        shp_s[:, pl.ds(at, UCH)] = shaped
        put(c, dot_nn(cott_s[...], low).astype(BF), units)
        return carry[0] + lanes_sum(shaped), carry[1] + lanes_sum(shaped * unit)

    su_ref[...] = jnp.zeros_like(su_ref)
    sums = lax.fori_loop(0, per, second, (zero, zero))
    over[1].wait_recv()
    passed[1].start()
    for copy in passed:
        copy.wait_recv()
    s_sum, s_cross = lax.fori_loop(per, 2 * per, second, sums)
    drain(units)
    shaped_mean = jnp.sum(s_sum, axis=1, keepdims=True) * (1.0 / full)
    cross_mean = jnp.sum(s_cross, axis=1, keepdims=True) * (1.0 / full)
    out_ref[...] = (wide_s[...] + (acc_s[...] + vec_d[0:1, pl.ds(2304, D)])).astype(BF)
    gmid_s[...] = jnp.zeros_like(gmid_s)

    def third(c, carry):
        at = pl.multiple_of(c * UCH, UCH)
        g = ffn_scale * (shp_s[:, pl.ds(at, UCH)] - shaped_mean - act_s[:, pl.ds(at, UCH)] * cross_mean)
        low = (g * dg_s[:, pl.ds(at, UCH)].astype(F32)).astype(BF)
        su_ref[2:3, pl.ds(at, UCH)] = column_sum(low.astype(F32))
        gmid_s[...] += dot_nt(low, w1[:, pl.ds(at, UCH)])
        put(c, dot_nn(midt_s[...], low).astype(BF), 0)
        return carry

    lax.fori_loop(0, full // UCH, third, 0)
    drain(0)

    grad_mid = gmid_s[...]
    unit = mid_s[...]
    sd_ref[1:2, :] = column_sum(grad_mid * unit)
    sd_ref[2:3, :] = column_sum(grad_mid)
    shaped = grad_mid * mid_gain
    grad_mixed = cot[...].astype(F32) + mid_scale * (
        shaped - jnp.mean(shaped, axis=1, keepdims=True) - unit * jnp.mean(shaped * unit, axis=1, keepdims=True)
    )
    branch = grad_mixed.astype(BF)
    gmix_ref[...] = branch
    branch_f = branch.astype(F32)
    sd_ref[0:1, :] = column_sum(branch_f)
    out_grad = dot_nn(jnp.transpose(branch_f).astype(BF), low_s[...]).astype(BF)
    stage[0, :, 0:width] = out_grad[:, 0:width]
    stage[1, :, 0:width] = out_grad[:, width : 2 * width]
    last = [
        pltpu.make_async_copy(stage.at[i, :, pl.ds(0, width)], packed.at[:, pl.ds(i * wide + 2 * units, width)], out_sems.at[i])
        for i in range(2)
    ]
    for copy in last:
        copy.start()
    grad_sub = dot_nt(branch, wo[...])
    unit = sub_s[...]
    cross = grad_sub * unit
    sw_ref[...] = jnp.zeros_like(sw_ref)
    sw_ref[0:1, :] = column_sum(cross)
    sw_ref[1:2, :] = column_sum(grad_sub)
    shaped = grad_sub * sub_gain
    grad_att = sub_scale * (
        shaped - jnp.mean(shaped, axis=1, keepdims=True) - unit * jnp.mean(shaped * unit, axis=1, keepdims=True)
    )
    gatt_m[...] = grad_att[:, 0:width].astype(BF)
    gatt_o[...] = grad_att[:, width : 2 * width].astype(BF)
    parts = ext_ref.shape[0]
    if parts > 1:
        sums_u, sums_w, sums_d = su_ref[...], sw_ref[...], sd_ref[...]
        for i in range(parts):
            ext_ref[i] = jnp.concatenate(
                [
                    window(sums_u, i * (units // parts)),
                    window(sums_u, units + i * (units // parts)),
                    window(sums_w, i * (width // parts)),
                    window(sums_w, width + i * (width // parts)),
                    window(sums_d, i * (D // parts)),
                    jnp.zeros((8, 128), F32),
                ],
                axis=0,
            ).astype(BF)
    for copy in last:
        copy.wait()
    for copy in over + passed:
        copy.wait_send()


def window(rows8, start):
    base = start // 128 * 128
    size = min(256, rows8.shape[1] - base)
    view = rows8[:, base : base + size]
    shift = start - base
    if shift:
        view = pltpu.roll(view, size - shift, 1)
    return view[:, 0:128]


def middle(att_m, att_o, hid, cot, vec_all, vec_got, w1, w2, wo, parts):
    rows = att_m.shape[0]
    units = w2.shape[0]
    width = wo[0].shape[0]
    vmem = pl.BlockSpec(memory_space=pltpu.VMEM)
    hbm = pl.BlockSpec(memory_space=pl.ANY)
    shape = jax.ShapeDtypeStruct
    return pl.pallas_call(
        mid_kernel,
        in_specs=[vmem] * 4 + [hbm] * 9,
        out_specs=[vmem] * 4 + [hbm] + [vmem] * 4,
        out_shape=[
            shape((rows, D), BF),
            shape((rows, width), BF),
            shape((rows, width), BF),
            shape((rows, D), BF),
            shape((D, 2 * (2 * units + width)), BF),
            shape((8, 2 * units), F32),
            shape((8, 2 * width), F32),
            shape((8, D), F32),
            shape((parts, 48, 128), BF),
        ],
        scratch_shapes=[
            pltpu.VMEM((8, 2 * units), F32),
            pltpu.VMEM((8, 2 * width), F32),
            pltpu.VMEM((D, 2 * units), BF),
            pltpu.VMEM((2 * units, D), BF),
            pltpu.VMEM((2 * width, D), BF),
            pltpu.VMEM((rows, 2 * units), F32),
            pltpu.VMEM((rows, 2 * units), F32),
            pltpu.VMEM((rows, 2 * units), BF),
            pltpu.VMEM((rows, D), F32),
            pltpu.VMEM((rows, D), F32),
            pltpu.VMEM((rows, D), F32),
            pltpu.VMEM((rows, 2 * width), F32),
            pltpu.VMEM((rows, D), F32),
            pltpu.VMEM((rows, 2 * width), BF),
            pltpu.VMEM((D, rows), BF),
            pltpu.VMEM((D, rows), BF),
            pltpu.VMEM((2, D, UCH), BF),
            pltpu.VMEM((rows, D), BF),
            pltpu.VMEM((rows, D), BF),
            pltpu.SemaphoreType.DMA((11,)),
            pltpu.SemaphoreType.DMA((2,)),
            pltpu.SemaphoreType.DMA((4,)),
            pltpu.SemaphoreType.DMA((4,)),
        ],
        compiler_params=pltpu.CompilerParams(vmem_limit_bytes=62 << 20, collective_id=3, has_side_effects=True),
        cost_estimate=pl.CostEstimate(flops=21 * 10**9, bytes_accessed=30 * 10**6, transcendentals=0),
        name="middle",
    )(att_m, att_o, vec_all, vec_got, hid, cot, *w1, *wo, w2)


def final_kernel(
    bits, hid, vec_all, dq, dk, dv, wq, wk, wv, gmix, ext, sum_k, sum_v, relay,
    gin, late_out, vec_out,
    loc_s, far_s, unit_s, mine_s, norm_s, send_c, recv_c, send_p, recv_p, give_c, give_p, late_s, small_s,
    vec_s, vec_r, sems_a, sems_b, loc_sems, *stage_refs,
):
    device = lax.axis_index("dp")
    side = lax.axis_index("tensor")
    across = {"dp": device, "tensor": 1 - side}
    peers = [{"dp": bit_peer(device, b), "tensor": side} for b in range(bits)]
    rows, width = dq.shape
    prompt = sum_k.shape[0]
    conts = rows - prompt
    half_p, half_c = prompt // 2, conts // 2
    own_p = pl.multiple_of(side * half_p, 128)
    their_p = pl.multiple_of((1 - side) * half_p, 128)
    own_c = pl.multiple_of(prompt + side * half_c, 128)
    their_c = pl.multiple_of(prompt + (1 - side) * half_c, 128)
    lanes = 3 * width + 128

    greet(peers + [across])
    count = [0]

    def remote(src, dst, peer):
        i = count[0]
        count[0] += 1
        copy = pltpu.make_async_remote_copy(
            src_ref=src, dst_ref=dst, send_sem=sems_a.at[i], recv_sem=sems_b.at[i], device_id=peer, device_id_type=MESH
        )
        copy.start()
        return copy

    share = remote(relay, far_s, peers[1])

    gain_f = vec_all[:, pl.ds(0, D)]
    bias_f = vec_all[:, pl.ds(D, D)]

    def unit_rows(at, size):
        x = hid[pl.ds(at, size), :].astype(F32)
        center = jnp.mean(x, axis=1, keepdims=True)
        scale = lax.rsqrt(jnp.mean(x * x, axis=1, keepdims=True) - center * center + EPSILON)
        return (x - center) * scale, scale

    def part_of(at, size, k_rows, v_rows):
        return dot_nt(dq[pl.ds(at, size), :], wq[...]) + dot_nt(k_rows, wk[...]) + dot_nt(v_rows, wv[...])

    def gather(part, unit):
        return column_sum(part * unit), column_sum(part)

    def normed_rows(at, size, unit):
        norm_s[:, pl.ds(at, size)] = jnp.transpose(unit * gain_f + bias_f).astype(BF)

    part = part_of(their_c, half_c, dk[pl.ds(their_c, half_c), :], dv[pl.ds(their_c, half_c), :])
    send_c[...] = part.astype(BF)
    y_cont = remote(send_c, recv_c, across)
    unit, _ = unit_rows(their_c, half_c)
    gain_grad, bias_grad = gather(part, unit)
    normed_rows(their_c, half_c, unit)
    unit, scale_c = unit_rows(own_c, half_c)
    part = part_of(own_c, half_c, dk[pl.ds(own_c, half_c), :], dv[pl.ds(own_c, half_c), :])
    mine_s[pl.ds(half_p, half_c), :] = part
    unit_s[pl.ds(half_p, half_c), :] = unit
    g, b = gather(part, unit)
    gain_grad, bias_grad = gain_grad + g, bias_grad + b
    normed_rows(own_c, half_c, unit)

    share.wait_recv()
    for i, total in enumerate((sum_k, sum_v)):
        loc_s[i, :, pl.ds(0, width - 128)] = total[:, pl.ds(0, width - 128)]
        loc_s[i, :, pl.ds(width - 128, 128)] = (
            total[:, pl.ds(width - 128, 128)].astype(F32) + far_s[i].astype(F32)
        ).astype(BF)
    part = part_of(their_p, half_p, loc_s[0, pl.ds(their_p, half_p), :], loc_s[1, pl.ds(their_p, half_p), :])
    send_p[...] = part.astype(BF)
    y_prompt = remote(send_p, recv_p, across)
    unit, _ = unit_rows(their_p, half_p)
    normed_rows(their_p, half_p, unit)
    g, b = gather(part, unit)
    gain_grad, bias_grad = gain_grad + g, bias_grad + b
    unit, scale_p = unit_rows(own_p, half_p)
    unit_s[pl.ds(0, half_p), :] = unit
    normed_rows(own_p, half_p, unit)
    part = part_of(own_p, half_p, loc_s[0, pl.ds(own_p, half_p), :], loc_s[1, pl.ds(own_p, half_p), :])
    mine_s[pl.ds(0, half_p), :] = part
    g, b = gather(part, unit)
    gain_grad, bias_grad = gain_grad + g, bias_grad + b

    blocks = 1 << bits
    block = D // blocks

    def keep(value, lane):
        low = value.astype(BF)
        for i in range(blocks):
            late_s[i // 2, i % 2, :, pl.ds(lane, width)] = low[i * block : (i + 1) * block, :]

    keep(dot_nn(norm_s[...], dq[...]), 0)
    q_bias = column_sum(dq[...].astype(F32))
    for i, rest in enumerate((dk, dv)):
        keep(
            dot_nn(norm_s[:, pl.ds(0, prompt)], loc_s[i])
            + dot_nn(norm_s[:, pl.ds(prompt, conts)], rest[pl.ds(prompt, conts), :]),
            (i + 1) * width,
        )
    v_bias = column_sum(loc_s[1].astype(F32)) + column_sum(dv[pl.ds(prompt, conts), :].astype(F32))

    def norm_back(total, unit, scale, mixed):
        shaped = total * gain_f
        return mixed.astype(F32) + scale * (
            shaped - jnp.mean(shaped, axis=1, keepdims=True) - unit * jnp.mean(shaped * unit, axis=1, keepdims=True)
        )

    small_s[...] = jnp.zeros_like(small_s)
    small_s[0:1, pl.ds(0, width)] = q_bias
    small_s[1:2, pl.ds(0, width)] = v_bias
    small_s[2:3, pl.ds(0, D)] = gain_grad
    small_s[3:4, pl.ds(0, D)] = bias_grad
    small = small_s[...]
    row_id = lax.broadcasted_iota(jnp.int32, (8, 128), 0)
    for i in range(blocks):
        narrow = window(small, i * (width // blocks))
        broad = window(small, i * block)
        tail = jnp.concatenate([ext[i, pl.ds(32, 16), :].astype(F32)[0:8], jnp.where(row_id < 2, narrow, broad)], axis=0)
        late_s[i // 2, i % 2, pl.ds(0, 32), pl.ds(3 * width, 128)] = ext[i, pl.ds(0, 32), :]
        late_s[i // 2, i % 2, pl.ds(32, 16), pl.ds(3 * width, 128)] = tail.astype(BF)

    def input_rows(arrived, at, size, scale, held, rows_at, sem):
        arrived[0].wait_recv()
        here = pl.ds(at, size)
        total = mine_s[here, :] + arrived[1][...].astype(F32)
        held[...] = norm_back(total, unit_s[here, :], scale, gmix[here, :]).astype(BF)
        back = remote(held, gin.at[pl.ds(rows_at, size), :], across)
        kept = pltpu.make_async_copy(held, gin.at[pl.ds(rows_at, size), :], loc_sems.at[sem])
        kept.start()
        return back, kept

    source = late_s
    stages = []
    for bit in range(bits):
        landing, kept = stage_refs[2 * bit], stage_refs[2 * bit + 1]
        mine = (device // (1 << bit)) % 2
        copy = remote(source.at[:, 1 - mine], landing, peers[bit])
        if bit == 0:
            back_c, keep_c = input_rows((y_cont, recv_c), half_p, half_c, scale_c, give_c, own_c, 0)
        if bit == 1:
            back_p, keep_p = input_rows((y_prompt, recv_p), 0, half_p, scale_p, give_p, own_p, 1)
        copy.wait_recv()
        stages.append(copy)
        for i in range(landing.shape[0]):
            kept[i // 2, i % 2] = (source[i, mine].astype(F32) + landing[i].astype(F32)).astype(BF)
        source = kept
    late_out[...] = source[0, 0, :, pl.ds(0, 3 * width)].astype(F32)
    vec_s[...] = source[0, 0, :, pl.ds(3 * width, 128)]
    swap = remote(vec_s, vec_r, across)
    swap.wait_recv()
    vec_out[0] = vec_s[...].astype(F32)
    vec_out[1] = vec_r[...].astype(F32)
    for copy in stages + [share, y_cont, y_prompt, swap]:
        copy.wait_send()
    for copy in (back_c, back_p):
        copy.wait_recv()
        copy.wait_send()
    keep_c.wait()
    keep_p.wait()


def finish(hid, vec_all, dq, dk, dv, wq, wk, wv, gmix, ext, sum_k, sum_v, relay):
    rows, width = dq.shape
    ranks = lax.axis_size("dp")
    bits = ranks.bit_length() - 1
    block = D // ranks
    prompt = sum_k.shape[0]
    conts = rows - prompt
    lanes = 3 * width + 128
    vmem = pl.BlockSpec(memory_space=pltpu.VMEM)
    hbm = pl.BlockSpec(memory_space=pl.ANY)
    shape = jax.ShapeDtypeStruct
    copies = 6 + bits
    stages = []
    for bit in range(bits):
        left = ranks >> (bit + 1)
        stages.append(pltpu.VMEM((left, block, lanes), BF))
        stages.append(pltpu.VMEM((max(left // 2, 1), min(left, 2), block, lanes), BF))
    return pl.pallas_call(
        functools.partial(final_kernel, bits),
        in_specs=[vmem] * 13,
        out_specs=[hbm, vmem, vmem],
        out_shape=[shape((rows, D), BF), shape((block, 3 * width), F32), shape((2, block, 128), F32)],
        scratch_shapes=[
            pltpu.VMEM((2, prompt, width), BF),
            pltpu.VMEM((2, prompt, 128), BF),
            pltpu.VMEM((rows // 2, D), F32),
            pltpu.VMEM((rows // 2, D), F32),
            pltpu.VMEM((D, rows), BF),
            pltpu.VMEM((conts // 2, D), BF),
            pltpu.VMEM((conts // 2, D), BF),
            pltpu.VMEM((prompt // 2, D), BF),
            pltpu.VMEM((prompt // 2, D), BF),
            pltpu.VMEM((conts // 2, D), BF),
            pltpu.VMEM((prompt // 2, D), BF),
            pltpu.VMEM((ranks // 2, 2, block, lanes), BF),
            pltpu.VMEM((8, D + 128), F32),
            pltpu.VMEM((block, 128), BF),
            pltpu.VMEM((block, 128), BF),
            pltpu.SemaphoreType.DMA((copies,)),
            pltpu.SemaphoreType.DMA((copies,)),
            pltpu.SemaphoreType.DMA((2,)),
        ]
        + stages,
        compiler_params=pltpu.CompilerParams(vmem_limit_bytes=56 << 20, collective_id=1, has_side_effects=True),
        cost_estimate=pl.CostEstimate(flops=5 * 10**9, bytes_accessed=20 * 10**6, transcendentals=0),
        name="finish",
    )(hid, vec_all, dq, dk, dv, wq, wk, wv, gmix, ext, sum_k, sum_v, relay)


def flip(value, axis, bit):
    return lax.ppermute(value, axis, [(i, i ^ (1 << bit)) for i in range(lax.axis_size(axis))])


def contract_rows(left, right):
    return lax.dot_general(left, right, (((0,), (0,)), ((), ())), preferred_element_type=F32)


def back_project(left, right):
    return lax.dot_general(left, right, (((1,), (1,)), ((), ())), preferred_element_type=F32)


def norm_rows(values, gain, bias):
    center = jnp.mean(values, axis=-1, keepdims=True)
    spread = jnp.mean(values * values, axis=-1, keepdims=True) - center * center
    scaled = lax.rsqrt(spread + EPSILON)
    unit_rows = (values - center) * scaled
    return (unit_rows * gain + bias, unit_rows, scaled)


def norm_back(grad_rows, gain, unit_rows, scaled):
    shaped = grad_rows * gain
    return scaled * (
        shaped
        - jnp.mean(shaped, axis=-1, keepdims=True)
        - unit_rows * jnp.mean(shaped * unit_rows, axis=-1, keepdims=True)
    )


def in_order(which, mine, other, axis):
    return jnp.where(
        which == 0,
        jnp.concatenate([mine, other], axis=axis),
        jnp.concatenate([other, mine], axis=axis),
    )


def halving(value, device):
    bits = lax.axis_size("dp").bit_length() - 1
    rows, columns = value.shape
    current = value
    for bit in range(bits):
        upper = device // (1 << bit) % 2
        left = bits - bit
        view = current.reshape((1 << (left - 1), 2, -1, columns))
        kept = lax.dynamic_index_in_dim(view, upper, 1, keepdims=False)
        sent = lax.dynamic_index_in_dim(view, 1 - upper, 1, keepdims=False)
        got = flip(sent, "dp", bit)
        current = (kept.astype(F32) + got.astype(F32)).astype(BF)
    return current.reshape(rows >> bits, columns)


def half_of(value, which):
    prompt, conts = CHUNK // 2, (value.shape[0] - CHUNK) // 2
    return jnp.concatenate(
        [
            lax.dynamic_slice_in_dim(value, which * prompt, prompt),
            lax.dynamic_slice_in_dim(value, CHUNK + which * conts, conts),
        ]
    )


def joined(which, mine, other):
    prompt = CHUNK // 2
    low = jnp.where(which == 0, mine, other)
    high = jnp.where(which == 0, other, mine)
    return jnp.concatenate([low[:prompt], high[:prompt], low[prompt:], high[prompt:]])


def body(
    hidden_in,
    cotangent,
    prompt_start,
    cont_gap,
    seg_len,
    dilation_rate,
    pre_gain,
    pre_bias,
    query_weight,
    query_bias,
    key_weight,
    value_weight,
    value_bias,
    sub_gain,
    sub_bias,
    out_weight,
    out_bias,
    mid_gain,
    mid_bias,
    inner_weight,
    inner_bias,
    ffn_gain,
    ffn_bias,
    outer_weight,
    outer_bias,
):
    device = lax.axis_index("dp")
    ranks = lax.axis_size("dp")
    group_id = device // GDEV
    member = device % GDEV
    tensor_id = lax.axis_index("tensor")
    core = device % 2
    width = query_weight.shape[1]
    units = inner_weight.shape[1]
    pairs = width // 128
    rows = hidden_in.shape[0]
    prompt_rows = CHUNK
    cont_count = (rows - prompt_rows) // CONT

    vectors = jnp.concatenate(
        [
            pre_gain,
            pre_bias,
            query_bias,
            value_bias,
            ffn_gain,
            ffn_bias,
            inner_bias,
            sub_gain,
            sub_bias,
            out_bias,
            mid_gain,
            mid_bias,
            outer_bias,
        ]
    ).astype(F32)[None]
    pre_gain_f = pre_gain.astype(F32)

    (
        weighed,
        inverse,
        queries,
        keys,
        values,
        prompt_keys,
        prompt_values,
        attended,
        att_mine,
        att_got,
        *pieces,
        vectors_other,
    ) = attend(
        prompt_start,
        cont_gap,
        seg_len,
        dilation_rate,
        hidden_in,
        vectors,
        query_weight,
        key_weight,
        value_weight,
        inner_weight,
        out_weight,
    )
    inner_parts = (inner_weight, pieces[0], pieces[1])
    out_parts = (out_weight, pieces[2], pieces[3])

    fused = D % (16 * ranks) == 0
    out_half, grad_mine, grad_theirs, grad_mixed_low, packed, sum_u, sum_w, sum_d, ext = middle(
        att_mine,
        att_got,
        hidden_in,
        cotangent,
        vectors,
        vectors_other,
        inner_parts,
        outer_weight,
        out_parts,
        ranks if fused else 1,
    )

    early = lax.psum_scatter(packed, "dp", scatter_dimension=0, tiled=True)
    early_mine, early_other = jnp.split(early, 2, axis=1)
    early_sum = early_mine.astype(F32) + flip(early_other, "tensor", 0).astype(F32)
    inner_weight_grad = early_sum[:, :units]
    outer_weight_grad = early_sum[:, units : 2 * units].T
    out_weight_grad = early_sum[:, 2 * units :].T

    grad_query_in, own_key_grad, own_value_grad, key_sum, value_sum, relay, out_got = attend_back(
        queries,
        keys,
        values,
        prompt_keys,
        prompt_values,
        attended,
        inverse,
        weighed,
        grad_mine,
        grad_theirs,
        out_half,
    )
    output = joined(tensor_id, out_half, out_got)
    block = D // ranks
    per_u, per_w, per_d = units // ranks, width // ranks, D // ranks
    if fused:
        input_low, late, vec = finish(
            hidden_in,
            vectors,
            grad_query_in,
            own_key_grad,
            own_value_grad,
            query_weight,
            key_weight,
            value_weight,
            grad_mixed_low,
            ext,
            key_sum,
            value_sum,
            relay,
        )
        ffn_gain_grad, ffn_bias_grad, inner_bias_grad = [vec[0, i, :per_u] + vec[1, 8 + i, :per_u] for i in range(3)]
        sub_gain_grad, sub_bias_grad = [vec[0, 16 + i, :per_w] + vec[1, 24 + i, :per_w] for i in range(2)]
        out_bias_grad, mid_gain_grad, mid_bias_grad, outer_bias_grad = [
            vec[0, 32 + i, :per_d] + vec[1, 32 + i, :per_d] for i in range(4)
        ]
        query_bias_grad, value_bias_grad = [vec[0, 40 + i, :per_w] for i in range(2)]
        pre_gain_grad, pre_bias_grad = [vec[0, 42 + i, :per_d] + vec[1, 42 + i, :per_d] for i in range(2)]
    else:
        pre_normed, pre_unit, pre_scale = norm_rows(hidden_in.astype(F32), pre_gain_f, pre_bias.astype(F32))
        pre_low = pre_normed.astype(BF)
        last = width - 128
        far = flip(relay, "dp", 1).astype(F32)
        summed = jnp.stack([key_sum, value_sum]).astype(F32)
        summed = jnp.concatenate([summed[:, :, :last], summed[:, :, last:] + far], axis=2).astype(BF)
        grad_keys = jnp.concatenate([summed[0], own_key_grad[prompt_rows:]], axis=0)
        grad_values = jnp.concatenate([summed[1], own_value_grad[prompt_rows:]], axis=0)

        query_weight_grad = contract_rows(pre_low, grad_query_in)
        key_weight_grad = contract_rows(pre_low, grad_keys)
        value_weight_grad = contract_rows(pre_low, grad_values)
        query_bias_grad = jnp.sum(grad_query_in.astype(F32), axis=0)
        value_bias_grad = jnp.sum(grad_values.astype(F32), axis=0)
        grad_normed_part = (
            back_project(grad_query_in, query_weight)
            + back_project(grad_keys, key_weight)
            + back_project(grad_values, value_weight)
        )
        grad_normed_low = grad_normed_part.astype(BF)
        grad_normed = grad_normed_low.astype(F32) + flip(grad_normed_low, "tensor", 0).astype(F32)
        pre_gain_grad = jnp.sum(grad_normed * pre_unit, axis=0)
        pre_bias_grad = jnp.sum(grad_normed, axis=0)
        grad_mixed_all = joined(tensor_id, grad_mixed_low, flip(grad_mixed_low, "tensor", 0)).astype(F32)
        input_low = (grad_mixed_all + norm_back(grad_normed, pre_gain_f, pre_unit, pre_scale)).astype(BF)

        vec = jnp.concatenate(
            [
                sum_u[:3].reshape(3, 2, ranks, per_u).transpose(2, 1, 0, 3).reshape(ranks, 6 * per_u),
                sum_w[:2].reshape(2, 2, ranks, per_w).transpose(2, 1, 0, 3).reshape(ranks, 4 * per_w),
                sum_d[:4].reshape(4, ranks, per_d).swapaxes(0, 1).reshape(ranks, 4 * per_d),
                jnp.stack([query_bias_grad, value_bias_grad]).reshape(2, ranks, per_w).swapaxes(0, 1).reshape(ranks, 2 * per_w),
                jnp.stack([pre_gain_grad, pre_bias_grad]).reshape(2, ranks, per_d).swapaxes(0, 1).reshape(ranks, 2 * per_d),
            ],
            axis=1,
        )
        count = vec.shape[1]
        vec = jnp.pad(vec, ((0, 0), (0, block * 128 - count))).reshape(D, 128)
        late = halving(
            jnp.concatenate(
                [p.astype(BF) for p in (query_weight_grad, key_weight_grad, value_weight_grad, vec)], axis=1
            ),
            device,
        )
        vec = late[:, 3 * width :].reshape(-1)[:count]
        late = late[:, : 3 * width].astype(F32)
        at_w = 6 * per_u
        at_d = at_w + 4 * per_w
        at_late = at_d + 4 * per_d
        got = flip(vec[:at_late], "tensor", 0).astype(F32)
        vec = vec.astype(F32)
        ffn_gain_grad, ffn_bias_grad, inner_bias_grad = (vec[: 3 * per_u] + got[3 * per_u : at_w]).reshape(3, per_u)
        sub_gain_grad, sub_bias_grad = (vec[at_w : at_w + 2 * per_w] + got[at_w + 2 * per_w : at_d]).reshape(2, per_w)
        out_bias_grad, mid_gain_grad, mid_bias_grad, outer_bias_grad = (vec[at_d:at_late] + got[at_d:]).reshape(4, per_d)
        query_bias_grad, value_bias_grad = vec[at_late : at_late + 2 * per_w].reshape(2, per_w)
        pre_gain_grad, pre_bias_grad = vec[at_late + 2 * per_w :].reshape(2, per_d)
    return (
        output,
        input_low,
        pre_gain_grad,
        pre_bias_grad,
        late[:, :width],
        query_bias_grad,
        late[:, width : 2 * width],
        late[:, 2 * width : 3 * width],
        value_bias_grad,
        sub_gain_grad,
        sub_bias_grad,
        out_weight_grad,
        out_bias_grad,
        mid_gain_grad,
        mid_bias_grad,
        inner_weight_grad,
        inner_bias_grad,
        ffn_gain_grad,
        ffn_bias_grad,
        outer_weight_grad,
        outer_bias_grad,
    )

def solution(mesh):
    placed = (
        P("dp", None),
        P("dp", None),
        P(),
        P(),
        P(),
        P(),
        P(),
        P(),
        P(None, "tensor"),
        P("tensor"),
        P(None, "tensor"),
        P(None, "tensor"),
        P("tensor"),
        P("tensor"),
        P("tensor"),
        P("tensor", None),
        P(),
        P(),
        P(),
        P(None, "tensor"),
        P("tensor"),
        P("tensor"),
        P("tensor"),
        P("tensor", None),
        P(),
    )
    return jax.shard_map(
        body,
        mesh=mesh,
        in_specs=placed,
        out_specs=(
            P("dp", None),
            P("dp", None),
            P("dp"),
            P("dp"),
            P("dp", "tensor"),
            P(("tensor", "dp")),
            P("dp", "tensor"),
            P("dp", "tensor"),
            P(("tensor", "dp")),
            P(("tensor", "dp")),
            P(("tensor", "dp")),
            P("tensor", "dp"),
            P("dp"),
            P("dp"),
            P("dp"),
            P("dp", "tensor"),
            P(("tensor", "dp")),
            P(("tensor", "dp")),
            P(("tensor", "dp")),
            P("tensor", "dp"),
            P("dp"),
        ),
        check_vma=False,
    )
```

```python
import functools

import jax
import jax.numpy as jnp
from jax import lax
from jax.experimental import pallas as pl
from jax.experimental.pallas import tpu as pltpu
from jax.sharding import PartitionSpec as P

HD = 64
PROMPT = 2048
CONT = 256
GDEV = 4
TILE = 256
CHUNK = PROMPT // GDEV
PTILES = CHUNK // TILE
LOG2E = 1.4426950408889634
BF = jnp.bfloat16
F32 = jnp.float32
D = 768
EPSILON = 1e-05
MESH = pl.DeviceIdType.MESH


def dot_nt(a, b):
    return lax.dot_general(a, b, (((1,), (1,)), ((), ())), preferred_element_type=F32)


def dot_nn(a, b):
    return lax.dot_general(a, b, (((1,), (0,)), ((), ())), preferred_element_type=F32)


def low_half(rows):
    return lax.broadcasted_iota(jnp.int32, (rows, 128), 1) < HD


def settings(seg, rate, pair):
    def row(value):
        return jnp.zeros((1, 128), F32) + value.astype(F32)

    def rest(number, period):
        return number - period * jnp.floor((number + 0.5) / period)

    second, third = row(rate[pair, 1]), row(rate[pair, 2])
    head = row(2 * pair)
    return (
        1.0 / row(seg[pair, 0]),
        1.0 / row(seg[pair, 1]),
        second,
        1.0 / second,
        third,
        1.0 / third,
        rest(head, second),
        rest(head + 1.0, second),
        rest(head, third),
        rest(head + 1.0, third),
    )


def codes(at, cells, miss):
    first = jnp.floor((at + 0.5) * cells[0])
    second = jnp.floor((at + 0.5) * cells[1])
    rest1 = at - cells[2] * jnp.floor((at + 0.5) * cells[3])
    rest2 = at - cells[4] * jnp.floor((at + 0.5) * cells[5])
    return [
        first,
        jnp.where(rest1 == cells[6], second, miss),
        jnp.where(rest1 == cells[7], second, miss),
        jnp.where(rest2 == cells[8], 1.0, 0.0),
        jnp.where(rest2 == cells[9], 1.0, 0.0),
    ]


def bit_peer(device, bit):
    step = 1 << bit
    return device + (1 - 2 * ((device // step) % 2)) * step


def greet(peers):
    barrier = pltpu.get_barrier_semaphore()
    for peer in peers:
        pl.semaphore_signal(barrier, inc=1, device_id=peer, device_id_type=MESH)
    pl.semaphore_wait(barrier, len(peers))


def xor_bits(a, b):
    return (a % 2 + b % 2) % 2 + 2 * ((a // 2 + b // 2) % 2)


def fwd_kernel(
    starts, gaps, seg, rate, hid, vec, wq, wk, wv, w1, wo, vec_hbm,
    e_ref, li_ref, q_out, k_out, v_out, kp_out, vp_out, o_out, mine_out, got_out,
    w1_got, w1_swap, wo_got, wo_swap, vec_got,
    t_s, kc_s, kv_s, low_s, q_s, ko_s, vo_s, o_s, sems_a, sems_b, loc_sems,
):
    pair = pl.program_id(0)
    step = pl.program_id(1)
    pairs = pl.num_programs(0)
    device = lax.axis_index("dp")
    side = lax.axis_index("tensor")
    member = device % GDEV
    core = device % 2
    rows, width = q_s.shape
    n_pairs = width // 128
    last_pair = n_pairs - 1
    conts = rows - CHUNK
    near = {"dp": bit_peer(device, 0), "tensor": side}
    far = {"dp": bit_peer(device, 1), "tensor": side}
    across = {"dp": device, "tensor": 1 - side}
    half_u = w1.shape[1] // 2
    half_w = wo.shape[0] // 2
    half_p, half_c = CHUNK // 2, conts // 2
    sent_u = pl.multiple_of(core * half_u, 128)
    shared_at = 2 * D + 2 * width
    sent_w = pl.multiple_of(core * half_w, 64)

    def remote(i, src, dst, peer):
        return pltpu.make_async_remote_copy(
            src_ref=src, dst_ref=dst, send_sem=sems_a.at[i], recv_sem=sems_b.at[i], device_id=peer, device_id_type=MESH
        )

    def to_far(p):
        lanes = pl.ds(p * 128, 128)
        return remote(3 * p, kv_s.at[0, :, :, lanes], kv_s.at[2, :, :, lanes], far)

    def to_near(p):
        lanes = pl.ds(p * 128, 128)
        return remote(3 * p + 1, kv_s.at[0, :, :, lanes], kv_s.at[1, :, :, lanes], near)

    def relay(p):
        lanes = pl.ds(p * 128, 128)
        return remote(3 * p + 2, kv_s.at[2, :, :, lanes], kv_s.at[3, :, :, lanes], near)

    base = 3 * n_pairs
    fetch_y = [
        remote(base, wo.at[pl.ds(sent_w, half_w), :], wo_got, across),
        remote(base + 1, w1.at[:, pl.ds(sent_u, half_u)], w1_got, across),
        remote(base + 2, vec_hbm.at[:, pl.ds(shared_at, vec_got.shape[1])], vec_got, across),
    ]
    fetch_core = [
        remote(base + 3, wo_got, wo_swap, near),
        remote(base + 4, w1_got, w1_swap, near),
    ]

    def give(p, piece):
        lanes = pl.ds(p * 128, 128)
        their_p = pl.multiple_of((1 - side) * half_p, 128)
        their_c = pl.multiple_of(CHUNK + (1 - side) * half_c, 128)
        third = half_c // 3
        if piece == 0:
            source, target = pl.ds(their_p, half_p), pl.ds(0, half_p)
        else:
            source = pl.ds(pl.multiple_of(their_c + (piece - 1) * third, 128), third)
            target = pl.ds(half_p + (piece - 1) * third, third)
        return remote(base + 5 + 4 * p + piece, o_s.at[source, lanes], got_out.at[target, lanes], across)

    def keeps():
        own_p = pl.multiple_of(side * half_p, 128)
        own_c = pl.multiple_of(CHUNK + side * half_c, 128)
        return [
            pltpu.make_async_copy(o_s, o_out, loc_sems.at[0]),
            pltpu.make_async_copy(o_s.at[pl.ds(own_p, half_p), :], mine_out.at[pl.ds(0, half_p), :], loc_sems.at[1]),
            pltpu.make_async_copy(o_s.at[pl.ds(own_c, half_c), :], mine_out.at[pl.ds(half_p, half_c), :], loc_sems.at[2]),
        ]

    def saves():
        out = [
            pltpu.make_async_copy(q_s, q_out, loc_sems.at[3]),
            pltpu.make_async_copy(ko_s, k_out, loc_sems.at[0]),
            pltpu.make_async_copy(vo_s, v_out, loc_sems.at[5]),
        ]
        for r in range(GDEV):
            span = pl.ds(r * CHUNK, CHUNK)
            out.append(pltpu.make_async_copy(kv_s.at[r, 0], kp_out.at[span, :], loc_sems.at[6 + 2 * r]))
            out.append(pltpu.make_async_copy(kv_s.at[r, 1], vp_out.at[span, :], loc_sems.at[7 + 2 * r]))
        return out

    @pl.when((pair == 0) & (step == 0))
    def _():
        greet([near, far, across])
        for copy in fetch_y:
            copy.start()
        gain_f, bias_f = vec[:, pl.ds(0, D)], vec[:, pl.ds(D, D)]
        query_bias = vec[:, pl.ds(2 * D, width)]
        value_bias = vec[:, pl.ds(2 * D + width, width)]

        def norm(at, size):
            x = hid[at : at + size, :].astype(F32)
            center = jnp.mean(x, axis=1, keepdims=True)
            scale = lax.rsqrt(jnp.mean(x * x, axis=1, keepdims=True) - center * center + EPSILON)
            low = ((x - center) * scale * gain_f + bias_f).astype(BF)
            low_s[at : at + size, :] = low
            return low

        low = norm(0, CHUNK)
        kv_s[0, 0] = dot_nn(low, wk[...]).astype(BF)
        kv_s[0, 1] = (dot_nn(low, wv[...]) + value_bias).astype(BF)
        to_far(0).start()
        for p in range(n_pairs):
            to_near(p).start()
        for at in range(CHUNK, rows, TILE):
            low = norm(at, TILE)
            ko_s[at - CHUNK : at - CHUNK + TILE, :] = dot_nn(low, wk[...]).astype(BF)
            vo_s[at - CHUNK : at - CHUNK + TILE, :] = (dot_nn(low, wv[...]) + value_bias).astype(BF)
        to_far(0).wait_send()
        for p in range(1, n_pairs):
            to_far(p).start()
        for at in range(0, rows, TILE):
            q_s[at : at + TILE, :] = ((dot_nn(low_s[at : at + TILE, :], wq[...]) + query_bias) * 0.125).astype(BF)
        to_far(0).wait_recv()
        relay(0).start()

    for p in range(n_pairs):
        @pl.when((pair == p) & (step == 0))
        def _():
            to_near(p).wait_recv()
            relay(p).wait_recv()

        if p + 1 < n_pairs:
            @pl.when((pair == p) & (step == 3))
            def _():
                to_far(p + 1).wait_recv()
                relay(p + 1).start()

    lanes = pl.ds(pl.multiple_of(pair * 128, 128), 128)
    low = low_half(TILE)
    q = q_s[pl.ds(pl.multiple_of(step * TILE, TILE), TILE), lanes]
    zero = jnp.zeros_like(q)
    qs = [jnp.where(low, q, zero), jnp.where(low, zero, q)]
    row = lax.broadcasted_iota(jnp.int32, (TILE, 128), 0).astype(F32)
    group = device // GDEV
    start = starts[group]
    first_cont = member * (conts // CONT)
    own_gap = gaps[group, first_cont + jnp.maximum(step - PTILES, 0)]
    base_q = start + jnp.where(step < PTILES, member * CHUNK + step * TILE, PROMPT + own_gap)
    cells = settings(seg, rate, side * n_pairs + pair)
    at_q = base_q.astype(F32) + row
    qc = codes(at_q, cells, -2.0)

    @pl.when(step == 0)
    def _():
        ahead = lax.broadcasted_iota(jnp.int32, (8, 128), 1).astype(F32) + start.astype(F32)
        for j in range(PROMPT // 128):
            for i, c in enumerate(codes(ahead + j * 128.0, cells, -1.0)):
                kc_s[i, :, j * 128 : (j + 1) * 128] = c

    def logits(mx, keys, kc, causal, at, span):
        out = []
        for h in range(2):
            s = dot_nt(qs[h], keys)
            top = mx[h]
            for g in range(span // 128):
                part = slice(g * 128, (g + 1) * 128)
                w = jnp.where(qc[0] == kc[0][:, part], 1.0, 0.0)
                w = w + jnp.where(qc[1 + h] == kc[1 + h][:, part], 1.0, 0.0)
                w = w + qc[3 + h] * kc[3 + h][:, part]
                if causal is not None:
                    w = jnp.where(causal[:, part], w, 0.0)
                t = s[:, part] * LOG2E + jnp.log2(w)
                t_s[h, :, pl.ds(at + g * 128, 128)] = t
                top = jnp.maximum(top, t)
            out.append(top)
        return tuple(out)

    def weigh(carry, vals, m, at, span):
        sums, accs = carry
        ns, na = [], []
        for h in range(2):
            total = sums[h]
            parts = []
            for g in range(span // 128):
                e = jnp.exp2(t_s[h, :, pl.ds(at + g * 128, 128)] - m[h])
                total = total + e
                parts.append(e.astype(BF))
            el = jnp.concatenate(parts, axis=1)
            e_ref[h, :, pl.ds(at, span)] = el
            ns.append(total)
            na.append(accs[h] + dot_nn(el, vals))
        return (tuple(ns), tuple(na))

    def finish_rows(carry):
        sums, accs = carry
        li = [1.0 / jnp.sum(s, axis=1, keepdims=True) for s in sums]
        lfull = jnp.where(low, li[0], li[1])
        li_ref[...] = lfull
        o_s[pl.ds(pl.multiple_of(step * TILE, TILE), TILE), lanes] = (jnp.where(low, accs[0], accs[1]) * lfull).astype(BF)

    def tops(mx):
        return [jnp.broadcast_to(jnp.max(x, axis=1, keepdims=True), (TILE, 128)) for x in mx]

    neg = jnp.full((TILE, 128), -jnp.inf, F32)
    zf = jnp.zeros((TILE, 128), F32)

    def key_codes(at, span):
        return [kc_s[i, 0:1, pl.ds(at, span)] for i in range(5)]

    @pl.when(step < PTILES)
    def _():
        def one(j, mx):
            at = pl.multiple_of(j * CHUNK, CHUNK)
            held = xor_bits(j, member)
            return logits(
                mx, kv_s[held, 0, :, lanes], key_codes(at, CHUNK), None, pl.multiple_of(held * CHUNK, CHUNK), CHUNK
            )

        mx = lax.fori_loop(0, member, one, (neg, neg))
        at = pl.multiple_of(member * CHUNK, CHUNK)
        rows_id = lax.broadcasted_iota(jnp.int32, (TILE, CHUNK), 0) + step * TILE
        cols = lax.broadcasted_iota(jnp.int32, (TILE, CHUNK), 1)
        mx = logits(mx, kv_s[0, 0, :, lanes], key_codes(at, CHUNK), cols <= rows_id, 0, CHUNK)
        m = tops(mx)

        def two(j, carry):
            held = xor_bits(j, member)
            return weigh(carry, kv_s[held, 1, :, lanes], m, pl.multiple_of(held * CHUNK, CHUNK), CHUNK)

        finish_rows(lax.fori_loop(0, member + 1, two, ((zf, zf), (zf, zf))))

    @pl.when(step >= PTILES)
    def _():
        own = pl.ds(pl.multiple_of((step - PTILES) * TILE, TILE), TILE)
        mx = (neg, neg)
        for j in range(GDEV):
            at = pl.multiple_of(xor_bits(j, member) * CHUNK, CHUNK)
            mx = logits(mx, kv_s[j, 0, :, lanes], key_codes(at, CHUNK), None, j * CHUNK, CHUNK)
        rows_id = lax.broadcasted_iota(jnp.int32, (TILE, CONT), 0)
        cols = lax.broadcasted_iota(jnp.int32, (TILE, CONT), 1)
        ahead = lax.broadcasted_iota(jnp.int32, (8, 128), 1).astype(F32) + base_q.astype(F32)
        parts = [codes(ahead + j * 128.0, cells, -1.0) for j in range(CONT // 128)]
        own_codes = [jnp.concatenate([part[i] for part in parts], axis=1)[0:1] for i in range(5)]
        mx = logits(mx, ko_s[own, lanes], own_codes, cols <= rows_id, PROMPT, CONT)
        m = tops(mx)
        carry = ((zf, zf), (zf, zf))
        for j in range(GDEV):
            carry = weigh(carry, kv_s[j, 1, :, lanes], m, j * CHUNK, CHUNK)
        finish_rows(weigh(carry, vo_s[own, lanes], m, PROMPT, CONT))

    end = pl.num_programs(1) - 1
    for p in range(n_pairs):
        @pl.when((pair == p) & (step == 1 - side))
        def _():
            give(p, 0).start()

        for unit in range(6):
            @pl.when((pair == p) & (step == PTILES + unit // 2) & (side == 1 - unit // 3))
            def _():
                give(p, 1 + unit % 3).start()

    @pl.when((pair == last_pair - 1) & (step == 3))
    def _():
        for i in range(2):
            fetch_y[i].wait_recv()
            fetch_core[i].start()

    @pl.when((pair == last_pair) & (step == 0))
    def _():
        for copy in saves():
            copy.start()

    @pl.when((pair == last_pair) & (step == end))
    def _():
        for copy in keeps():
            copy.start()
        fetch_y[2].wait_recv()
        for copy in fetch_core:
            copy.wait_recv()
        for p in range(n_pairs):
            for piece in range(4):
                copy = give(p, piece)
                copy.wait_recv()
                copy.wait_send()
            if p > 0:
                to_far(p).wait_send()
            to_near(p).wait_send()
            relay(p).wait_send()
        for copy in fetch_y + fetch_core:
            copy.wait_send()
        for copy in keeps() + saves():
            copy.wait()


def attend(starts, gaps, seg, rate, hid, vec, wq, wk, wv, w1, wo):
    rows = hid.shape[0]
    width = wq.shape[1]
    pairs = width // 128
    span = PROMPT + CONT
    conts = rows - CHUNK
    units = w1.shape[1]
    vmem = pl.BlockSpec(memory_space=pltpu.VMEM)
    hbm = pl.BlockSpec(memory_space=pl.ANY)
    shape = jax.ShapeDtypeStruct
    copies = 3 * pairs + 5 + 4 * pairs
    shared = 3 * units + 2 * width
    smem = pl.BlockSpec(memory_space=pltpu.SMEM)
    return pl.pallas_call(
        fwd_kernel,
        grid_spec=pltpu.PrefetchScalarGridSpec(
            num_scalar_prefetch=0,
            grid=(pairs, rows // TILE),
            in_specs=[smem] * 4 + [vmem] * 5 + [hbm] * 3,
            out_specs=[
                pl.BlockSpec((2, TILE, span), lambda a, t: (a, t, 0)),
                pl.BlockSpec((TILE, 128), lambda a, t: (t, a)),
            ]
            + [hbm] * 13,
            scratch_shapes=[
                pltpu.VMEM((2, TILE, span), F32),
                pltpu.VMEM((5, 8, PROMPT), F32),
                pltpu.VMEM((GDEV, 2, CHUNK, width), BF),
                pltpu.VMEM((rows, D), BF),
                pltpu.VMEM((rows, width), BF),
                pltpu.VMEM((conts, width), BF),
                pltpu.VMEM((conts, width), BF),
                pltpu.VMEM((rows, width), BF),
                pltpu.SemaphoreType.DMA((copies,)),
                pltpu.SemaphoreType.DMA((copies,)),
                pltpu.SemaphoreType.DMA((6 + 2 * GDEV,)),
            ],
        ),
        out_shape=[
            shape((2 * pairs, rows, span), BF),
            shape((rows, width), F32),
            shape((rows, width), BF),
            shape((conts, width), BF),
            shape((conts, width), BF),
            shape((PROMPT, width), BF),
            shape((PROMPT, width), BF),
            shape((rows, width), BF),
            shape((rows // 2, width), BF),
            shape((rows // 2, width), BF),
            shape((D, units // 2), BF),
            shape((D, units // 2), BF),
            shape((width // 2, D), BF),
            shape((width // 2, D), BF),
            shape((1, shared), F32),
        ],
        compiler_params=pltpu.CompilerParams(vmem_limit_bytes=56 << 20, collective_id=0, has_side_effects=True),
        cost_estimate=pl.CostEstimate(flops=20 * 10**9, bytes_accessed=60 * 10**6, transcendentals=0),
        name="attend",
    )(starts, gaps, seg, rate, hid, vec, wq, wk, wv, w1, wo, vec)


def bwd_kernel(
    fused, q_ref, kp_ref, vp_ref, ko_ref, vo_ref, o_ref, li_ref, e_ref, g_mine, g_theirs, out_half, *refs
):
    packed = refs[0] if fused else None
    refs = refs[1:] if fused else refs
    dq_ref, dko_ref, dvo_ref, sum_k, sum_v, relay_out, out_got = refs[:7]
    early_out = refs[7] if fused else None
    refs = refs[8:] if fused else refs[7:]
    dk_s, dv_s, g_s, grad_s, near_s, relay_s, far_s, sems_a, sems_b, loc_sems = refs[:10]
    pair = pl.program_id(0)
    step = pl.program_id(1)
    device = lax.axis_index("dp")
    side = lax.axis_index("tensor")
    member = device % GDEV
    rows, width = g_s.shape
    n_pairs = width // 128
    conts = rows - CHUNK
    half_p, half_c = CHUNK // 2, conts // 2
    near = {"dp": bit_peer(device, 0), "tensor": side}
    far = {"dp": bit_peer(device, 1), "tensor": side}
    across = {"dp": device, "tensor": 1 - side}
    lanes = pl.ds(pl.multiple_of(pair * 128, 128), 128)
    mine_p = pl.ds(pl.multiple_of(side * half_p, 128), half_p)
    mine_c = pl.ds(pl.multiple_of(CHUNK + side * half_c, 128), half_c)

    def remote(i, src, dst, peer):
        return pltpu.make_async_remote_copy(
            src_ref=src, dst_ref=dst, send_sem=sems_a.at[i], recv_sem=sems_b.at[i], device_id=peer, device_id_type=MESH
        )

    def heads():
        return [
            remote(0, g_theirs.at[pl.ds(0, half_p), :], g_s.at[mine_p, :], across),
            remote(1, g_theirs.at[pl.ds(half_p, half_c), :], g_s.at[mine_c, :], across),
            remote(2, out_half, out_got, across),
        ]

    def local():
        return [
            pltpu.make_async_copy(g_mine.at[pl.ds(0, half_p), :], g_s.at[mine_p, :], loc_sems.at[0]),
            pltpu.make_async_copy(g_mine.at[pl.ds(half_p, half_c), :], g_s.at[mine_c, :], loc_sems.at[1]),
        ]

    def cores(p):
        part = pl.ds(p * 128, 128)
        return remote(3 + 2 * p, grad_s.at[:, :, 1, :, part], near_s.at[:, :, :, part], near)

    def chips(p):
        part = pl.ds(p * 128, 128)
        return remote(4 + 2 * p, relay_s.at[:, :, part], far_s.at[:, :, part], far)

    if fused:
        held, got0, got1, held1, got2, held2, got3, done_s, other_s, early_a, early_b, early_l = refs[10:]
        bit = [(device // (1 << b)) % 2 for b in range(4)]
        peers = [{"dp": bit_peer(device, b), "tensor": side} for b in range(4)]
        early_columns = packed.shape[-1]
        span_e = held.shape[-1]
        chunks = early_columns // span_e

        def passing(c, stage, source, target, peer):
            return pltpu.make_async_remote_copy(
                src_ref=source,
                dst_ref=target,
                send_sem=early_a.at[4 * c + stage],
                recv_sem=early_b.at[4 * c + stage],
                device_id=peer,
                device_id_type=MESH,
            )

        def columns_of(c):
            return pl.ds(pl.multiple_of((chunks - 1 - c) * span_e, 128), span_e)

        def own_half(c):
            return pltpu.make_async_copy(packed.at[:, :, :, bit[0], :, columns_of(c)], held.at[c], early_l.at[c])

        def stage0(c):
            return passing(c, 0, packed.at[:, :, :, 1 - bit[0], :, columns_of(c)], got0.at[c], peers[0])

        def stage1(c, odd):
            if odd:
                return passing(c, 1, held.at[c, :, 1 - bit[2]], got1.at[c], peers[2])
            return passing(c, 1, held.at[c, :, :, 1 - bit[1]], got1.at[c], peers[1])

        def stage2(c, odd):
            b = 1 if odd else 2
            return passing(c, 2, held1.at[c, :, 1 - bit[b]], got2.at[c], peers[b])

        def stage3(c):
            return passing(c, 3, held2.at[c, 1 - bit[3]], got3.at[c], peers[3])

        def begin(c):
            own_half(c).start()
            stage0(c).start()

        def after0(c):
            own_half(c).wait()
            stage0(c).wait_recv()
            held[c] = held[c] + got0[c]
            for odd in range(2):
                @pl.when(c % 2 == odd)
                def _():
                    stage1(c, odd).start()

        def after1(c):
            for odd in range(2):
                @pl.when(c % 2 == odd)
                def _():
                    stage1(c, odd).wait_recv()
                    kept = held[c, :, bit[2]] if odd else held[c, :, :, bit[1]]
                    held1[c] = kept + got1[c]
                    stage2(c, odd).start()

        def after2(c):
            for odd in range(2):
                @pl.when(c % 2 == odd)
                def _():
                    stage2(c, odd).wait_recv()
                    held2[c] = held1[c, :, bit[1 if odd else 2]] + got2[c]
            stage3(c).start()

        def after3(c):
            stage3(c).wait_recv()
            done_s[:, columns_of(c)] = held2[c, bit[3]] + got3[c]

        half_e = early_columns // 2
        swap = pltpu.make_async_remote_copy(
            src_ref=done_s.at[:, pl.ds(half_e, half_e)],
            dst_ref=other_s,
            send_sem=early_a.at[4 * chunks],
            recv_sem=early_b.at[4 * chunks],
            device_id=across,
            device_id_type=MESH,
        )
        tick = pair * pl.num_programs(1) + step

    @pl.when((pair == 0) & (step == 0))
    def _():
        greet([near, far, across] + (peers[2:] if fused else []))
        for copy in heads() + local():
            copy.start()
        for copy in local():
            copy.wait()

    if fused:
        for late, act in ((0, begin), (1, after0), (3, after1), (4, after2), (5, after3)):
            since = tick - late
            @pl.when((since >= 0) & (since % 4 != 3) & (since - since // 4 < chunks))
            def _():
                act(since - since // 4)

        @pl.when(tick == 12)
        def _():
            swap.start()

    @pl.when((pair == 0) & (step == 1 - side))
    def _():
        heads()[0].wait_recv()

    @pl.when((pair == 0) & (step == 3 - side))
    def _():
        heads()[1].wait_recv()

    low = low_half(TILE)
    g = g_s[pl.ds(pl.multiple_of(step * TILE, TILE), TILE), lanes].astype(F32) * li_ref[...]
    prod = g * o_ref[...].astype(F32)
    zf = jnp.zeros((TILE, 128), F32)
    deltas = [
        jnp.sum(jnp.where(low, prod, zf), axis=1, keepdims=True),
        jnp.sum(jnp.where(low, zf, prod), axis=1, keepdims=True),
    ]
    gs = [jnp.where(low, g, zf).astype(BF), jnp.where(low, zf, g).astype(BF)]
    gt = jnp.transpose(g).astype(BF)
    qt = jnp.transpose(q_ref[...].astype(F32)).astype(BF)

    def grads(dq, keys, vals, at, width):
        out, dks, dvs = [], [], []
        for h in range(2):
            e = e_ref[h, :, pl.ds(at, width)]
            dp = dot_nt(gs[h], vals)
            ds = (e.astype(F32) * (dp - deltas[h])).astype(BF)
            out.append(dq[h] + dot_nn(ds, keys))
            dks.append(dot_nn(qt[h * HD : (h + 1) * HD, :], ds))
            dvs.append(dot_nn(gt[h * HD : (h + 1) * HD, :], e))
        return tuple(out), dks, dvs

    @pl.when(step == 0)
    def _():
        dk_s[...] = jnp.zeros_like(dk_s)
        dv_s[...] = jnp.zeros_like(dv_s)

    def add(at, width, dks, dvs):
        for h in range(2):
            dk_s[h * HD : (h + 1) * HD, pl.ds(at, width)] += dks[h]
            dv_s[h * HD : (h + 1) * HD, pl.ds(at, width)] += dvs[h]

    def scaled(dq):
        return (jnp.where(low, dq[0], dq[1]).astype(BF).astype(F32) * 0.125).astype(BF)

    @pl.when(step < PTILES)
    def _():
        def one(j, dq):
            at = pl.multiple_of(xor_bits(j, member) * CHUNK, CHUNK)
            dq, dks, dvs = grads(dq, kp_ref[pl.ds(at, CHUNK), :], vp_ref[pl.ds(at, CHUNK), :], at, CHUNK)
            add(at, CHUNK, dks, dvs)
            return dq

        dq_ref[...] = scaled(lax.fori_loop(0, member + 1, one, (zf, zf)))
        dko_ref[...] = jnp.zeros_like(dko_ref)
        dvo_ref[...] = jnp.zeros_like(dvo_ref)

    @pl.when(step >= PTILES)
    def _():
        dq = (zf, zf)
        for j in range(GDEV):
            span = slice(j * CHUNK, (j + 1) * CHUNK)
            dq, dks, dvs = grads(dq, kp_ref[span, :], vp_ref[span, :], j * CHUNK, CHUNK)
            add(j * CHUNK, CHUNK, dks, dvs)
        dq, dks, dvs = grads(dq, ko_ref[...], vo_ref[...], PROMPT, CONT)
        dq_ref[...] = scaled(dq)
        dko_ref[...] = jnp.transpose(jnp.concatenate(dks, axis=0)).astype(BF)
        dvo_ref[...] = jnp.transpose(jnp.concatenate(dvs, axis=0)).astype(BF)

    end = pl.num_programs(1) - 1

    @pl.when(step == end)
    def _():
        for j in range(GDEV):
            span = slice(j * CHUNK, (j + 1) * CHUNK)
            grad_s[0, j // 2, j % 2, :, lanes] = jnp.transpose(dk_s[:, span]).astype(BF)
            grad_s[1, j // 2, j % 2, :, lanes] = jnp.transpose(dv_s[:, span]).astype(BF)

    for p in range(n_pairs):
        @pl.when((pair == p) & (step == end))
        def _():
            cores(p).start()

        if p + 1 < n_pairs:
            @pl.when((pair == p + 1) & (step == 2))
            def _():
                part = pl.ds(p * 128, 128)
                cores(p).wait_recv()
                relay_s[:, :, part] = (
                    grad_s[:, 1, 0, :, part].astype(F32) + near_s[:, 1, :, part].astype(F32)
                ).astype(BF)
                chips(p).start()

    @pl.when((pair == n_pairs - 1) & (step == end))
    def _():
        last = n_pairs - 1
        sums = (sum_k, sum_v)
        for p in range(last):
            part = pl.ds(p * 128, 128)
            chips(p).wait_recv()
            for i in range(2):
                sums[i][:, part] = (
                    grad_s[i, 0, 0, :, part].astype(F32) + near_s[i, 0, :, part].astype(F32) + far_s[i, :, part].astype(F32)
                ).astype(BF)
        part = pl.ds(last * 128, 128)
        cores(last).wait_recv()
        for i in range(2):
            relay_out[i] = (grad_s[i, 1, 0, :, part].astype(F32) + near_s[i, 1, :, part].astype(F32)).astype(BF)
            sums[i][:, part] = (grad_s[i, 0, 0, :, part].astype(F32) + near_s[i, 0, :, part].astype(F32)).astype(BF)
        if fused:
            after3(chunks - 1)
            swap.wait_recv()
            early_out[...] = done_s[:, pl.ds(0, half_e)].astype(F32) + other_s[...].astype(F32)
            for c in range(chunks):
                stage0(c).wait_send()
                stage1(c, c % 2).wait_send()
                stage2(c, c % 2).wait_send()
                stage3(c).wait_send()
            swap.wait_send()
        heads()[2].wait_recv()
        for copy in heads():
            copy.wait_send()
        for p in range(n_pairs):
            cores(p).wait_send()
            if p < last:
                chips(p).wait_send()


def attend_back(q, k, v, kp, vp, o, li, e, g_mine, g_theirs, out_half, packed):
    rows, width = q.shape
    pairs = width // 128
    span = PROMPT + CONT
    tile = pl.BlockSpec((TILE, 128), lambda a, t: (t, a))
    whole = pl.BlockSpec((PROMPT, 128), lambda a, t: (0, a))
    own = pl.BlockSpec((TILE, 128), lambda a, t: (jnp.maximum(t - PTILES, 0), a))
    vmem = pl.BlockSpec(memory_space=pltpu.VMEM)
    hbm = pl.BlockSpec(memory_space=pl.ANY)
    shape = jax.ShapeDtypeStruct
    copies = 3 + 2 * pairs
    fused = packed is not None
    more_in, more_out, more_scratch = [], [], []
    if fused:
        block, columns = packed.shape[-2:]
        chunks = 9
        cut = columns // chunks
        more_in = [packed]
        more_out = [shape((block, columns // 2), F32)]
        more_scratch = [
            pltpu.VMEM((chunks, 2, 2, 2, block, cut), BF),
            pltpu.VMEM((chunks, 2, 2, 2, block, cut), BF),
            pltpu.VMEM((chunks, 2, 2, block, cut), BF),
            pltpu.VMEM((chunks, 2, 2, block, cut), BF),
            pltpu.VMEM((chunks, 2, block, cut), BF),
            pltpu.VMEM((chunks, 2, block, cut), BF),
            pltpu.VMEM((chunks, block, cut), BF),
            pltpu.VMEM((block, columns), BF),
            pltpu.VMEM((block, columns // 2), BF),
            pltpu.SemaphoreType.DMA((4 * chunks + 1,)),
            pltpu.SemaphoreType.DMA((4 * chunks + 1,)),
            pltpu.SemaphoreType.DMA((chunks,)),
        ]
    return pl.pallas_call(
        functools.partial(bwd_kernel, fused),
        grid=(pairs, rows // TILE),
        in_specs=[tile, whole, whole, own, own, tile, tile, pl.BlockSpec((2, TILE, span), lambda a, t: (a, t, 0))]
        + [hbm] * (3 + len(more_in)),
        out_specs=[tile, tile, tile, vmem, vmem, vmem, hbm] + [vmem] * len(more_out),
        out_shape=[
            shape((rows, width), BF),
            shape((rows, width), BF),
            shape((rows, width), BF),
            shape((CHUNK, width), BF),
            shape((CHUNK, width), BF),
            shape((2, CHUNK, 128), BF),
            shape(out_half.shape, BF),
        ]
        + more_out,
        scratch_shapes=[
            pltpu.VMEM((128, PROMPT), F32),
            pltpu.VMEM((128, PROMPT), F32),
            pltpu.VMEM((rows, width), BF),
            pltpu.VMEM((2, 2, 2, CHUNK, width), BF),
            pltpu.VMEM((2, 2, CHUNK, width), BF),
            pltpu.VMEM((2, CHUNK, width), BF),
            pltpu.VMEM((2, CHUNK, width), BF),
            pltpu.SemaphoreType.DMA((copies,)),
            pltpu.SemaphoreType.DMA((copies,)),
            pltpu.SemaphoreType.DMA((2,)),
        ]
        + more_scratch,
        compiler_params=pltpu.CompilerParams(vmem_limit_bytes=60 << 20, collective_id=2, has_side_effects=True),
        cost_estimate=pl.CostEstimate(flops=30 * 10**9, bytes_accessed=60 * 10**6, transcendentals=0),
        name="attend_back",
    )(q, kp, vp, k, v, o, li, e, g_mine, g_theirs, out_half, *more_in)


UCH = 512


def polynomial(x, terms):
    out = jnp.full_like(x, terms[0])
    for term in terms[1:]:
        out = out * x + term
    return out


def error_function(x):
    x = jnp.clip(x, -3.832506856900711, 3.832506856900711)
    square = x * x
    top = polynomial(
        square,
        (0.00022905065861350646, 0.0034082910107109506, 0.050955695062380861, 0.18520832239976145, 1.128379143519084),
    )
    bottom = polynomial(
        square,
        (
            -1.1791602954361697e-7,
            0.000023547966471313185,
            0.0010179625278914885,
            0.014070470171167667,
            0.11098505178285362,
            0.49746925110067538,
            1.0,
        ),
    )
    return x * top / bottom


def gelu_pair(v):
    phi = 0.5 + 0.5 * error_function(v * 0.7071067811865476)
    density = jnp.exp(-0.5 * v * v) * 0.3989422804014327
    return v * phi, phi + v * density


def column_sum(x):
    return jnp.sum(x, axis=0, keepdims=True)


def mid_kernel(
    att_m, att_o, vec_all, vec_got, hid_all, cot_all, w1_own, w1_got, w1_swap, wo_own, wo_got, wo_swap, w2_own,
    out_ref, gatt_m, gatt_o, gmix_ref, packed, su_ref, sw_ref, sd_ref, ext_ref,
    vec_u, vec_w, w1, w2, wo, act_s, shp_s, dg_s, wide_s, acc_s, gmid_s, sub_s, mid_s, low_s, midt_s, cott_s, stage, hid, cot, sems, out_sems, send_sems, recv_sems,
):
    device = lax.axis_index("dp")
    side = lax.axis_index("tensor")
    core = device % 2
    near = {"dp": bit_peer(device, 0), "tensor": side}
    across = {"dp": device, "tensor": 1 - side}
    units = w1_own.shape[1]
    width = wo_own.shape[0]
    rows = hid.shape[0]
    full = 2 * units
    half = units // 2
    half_w = width // 2
    here_u = pl.multiple_of(units + core * half, 128)
    there_u = pl.multiple_of(units + (1 - core) * half, 128)
    here_w = pl.multiple_of(width + core * half_w, 64)
    there_w = pl.multiple_of(width + (1 - core) * half_w, 64)
    prompt, conts = CHUNK // 2, (hid_all.shape[0] - CHUNK) // 2
    own_p = pl.ds(pl.multiple_of(side * prompt, 128), prompt)
    own_c = pl.ds(pl.multiple_of(CHUNK + side * conts, 128), conts)
    at_own = 2 * D + 2 * width
    vec_own = vec_all.at[:, pl.ds(at_own, 3 * units + 2 * width)]
    vec_d = vec_all.at[:, pl.ds(at_own + 3 * units + 2 * width, 4 * D)]
    rows_in = []
    for i, (all_rows, held) in enumerate(((hid_all, hid), (cot_all, cot))):
        for j, (span, at, size) in enumerate(((own_p, 0, prompt), (own_c, prompt, conts))):
            copy = pltpu.make_async_copy(all_rows.at[span, :], held.at[pl.ds(at, size), :], sems.at[7 + 2 * i + j])
            copy.start()
            rows_in.append(copy)
    loads = []
    for i, (src, dst) in enumerate(
        [
            (wo_own, wo.at[pl.ds(0, width), :]),
            (wo_got, wo.at[pl.ds(here_w, half_w), :]),
            (wo_swap, wo.at[pl.ds(there_w, half_w), :]),
            (w1_own, w1.at[:, pl.ds(0, units)]),
            (w1_got, w1.at[:, pl.ds(here_u, half)]),
            (w1_swap, w1.at[:, pl.ds(there_u, half)]),
            (w2_own, w2.at[pl.ds(0, units), :]),
        ]
    ):
        copy = pltpu.make_async_copy(src, dst, sems.at[i])
        copy.start()
        loads.append(copy)

    piece = half // 2
    greet([near, across])

    def remote(i, src, dst, peer):
        return pltpu.make_async_remote_copy(
            src_ref=src, dst_ref=dst, send_sem=send_sems.at[i], recv_sem=recv_sems.at[i], device_id=peer, device_id_type=MESH
        )

    over, passed = [], []
    for i in range(2):
        from_own = pl.ds(pl.multiple_of(core * half + i * piece, 128), piece)
        landed = w2.at[pl.ds(pl.multiple_of(units + core * half + i * piece, 128), piece), :]
        over.append(remote(i, w2_own.at[from_own, :], landed, across))
        passed.append(remote(2 + i, landed, landed, near))
        over[i].start()

    for i in range(3):
        for j, vec in enumerate((vec_own, vec_got)):
            vec_u[i : i + 1, pl.ds(j * units, units)] = vec[0:1, pl.ds(i * units, units)]
    for i in range(2):
        for j, vec in enumerate((vec_own, vec_got)):
            vec_w[i : i + 1, pl.ds(j * width, width)] = vec[0:1, pl.ds(3 * units + i * width, width)]

    a0 = att_m[...].astype(F32)
    a1 = att_o[...].astype(F32)
    center = (jnp.sum(a0, axis=1, keepdims=True) + jnp.sum(a1, axis=1, keepdims=True)) * (1.0 / D)
    square = (jnp.sum(a0 * a0, axis=1, keepdims=True) + jnp.sum(a1 * a1, axis=1, keepdims=True)) * (1.0 / D)
    sub_scale = lax.rsqrt(square - center * center + EPSILON)
    sub_s[:, 0:width] = (a0 - center) * sub_scale
    sub_s[:, width : 2 * width] = (a1 - center) * sub_scale
    sub_gain = vec_w[0:1, :]
    low_s[...] = (sub_s[...] * sub_gain + vec_w[1:2, :]).astype(BF)
    for copy in loads[0:3] + rows_in:
        copy.wait()
    mixed = hid[...].astype(F32) + (dot_nn(low_s[...], wo[...]) + vec_d[0:1, pl.ds(0, D)])
    wide_s[...] = mixed
    mean = jnp.mean(mixed, axis=1, keepdims=True)
    mid_scale = lax.rsqrt(jnp.mean(mixed * mixed, axis=1, keepdims=True) - mean * mean + EPSILON)
    mid_s[...] = (mixed - mean) * mid_scale
    mid_gain = vec_d[0:1, pl.ds(768, D)]
    mid_full = mid_s[...] * mid_gain + vec_d[0:1, pl.ds(1536, D)]
    mid_low = mid_full.astype(BF)
    midt_s[...] = jnp.transpose(mid_full).astype(BF)
    cot_full = cot[...].astype(F32)
    cott_s[...] = jnp.transpose(cot_full).astype(BF)
    sd_ref[...] = jnp.zeros_like(sd_ref)
    sd_ref[3:4, :] = column_sum(cot_full)
    for copy in loads[3:6]:
        copy.wait()

    def lanes_sum(x):
        total = x[:, 0:128]
        for i in range(1, x.shape[1] // 128):
            total = total + x[:, i * 128 : (i + 1) * 128]
        return total

    def first(c, carry):
        at = pl.multiple_of(c * UCH, UCH)
        inner = dot_nn(mid_low, w1[:, pl.ds(at, UCH)]) + vec_u[2:3, pl.ds(at, UCH)]
        act, slope = gelu_pair(inner)
        act_s[:, pl.ds(at, UCH)] = act
        dg_s[:, pl.ds(at, UCH)] = slope.astype(BF)
        return carry[0] + lanes_sum(act), carry[1] + lanes_sum(act * act)

    zero = jnp.zeros((rows, 128), F32)
    act_sum, act_square = lax.fori_loop(0, full // UCH, first, (zero, zero))
    ffn_center = jnp.sum(act_sum, axis=1, keepdims=True) * (1.0 / full)
    ffn_scale = lax.rsqrt(
        jnp.sum(act_square, axis=1, keepdims=True) * (1.0 / full) - ffn_center * ffn_center + EPSILON
    )
    loads[6].wait()
    over[0].wait_recv()
    passed[0].start()
    acc_s[...] = jnp.zeros_like(acc_s)
    per = units // UCH
    wide = 2 * units + width

    def column_of(c, extra):
        return pl.multiple_of((c // per) * wide + lax.rem(c, per) * UCH + extra, 128)

    def send(slot, column):
        return pltpu.make_async_copy(stage.at[slot], packed.at[:, pl.ds(column, UCH)], out_sems.at[slot])

    def put(c, value, extra):
        slot = lax.rem(c, 2)

        @pl.when(c >= 2)
        def _():
            send(slot, column_of(c - 2, extra)).wait()

        stage[slot] = value
        send(slot, column_of(c, extra)).start()

    def drain(extra):
        for c in range(full // UCH - 2, full // UCH):
            send(c % 2, column_of(c, extra)).wait()

    def second(c, carry):
        at = pl.multiple_of(c * UCH, UCH)
        unit = (act_s[:, pl.ds(at, UCH)] - ffn_center) * ffn_scale
        act_s[:, pl.ds(at, UCH)] = unit
        gain = vec_u[0:1, pl.ds(at, UCH)]
        low = (unit * gain + vec_u[1:2, pl.ds(at, UCH)]).astype(BF)
        acc_s[...] += dot_nn(low, w2[pl.ds(at, UCH), :])
        grad = dot_nt(cot[...], w2[pl.ds(at, UCH), :])
        cross = grad * unit
        su_ref[0:1, pl.ds(at, UCH)] = column_sum(cross)
        su_ref[1:2, pl.ds(at, UCH)] = column_sum(grad)
        shaped = grad * gain
        shp_s[:, pl.ds(at, UCH)] = shaped
        put(c, dot_nn(cott_s[...], low).astype(BF), units)
        return carry[0] + lanes_sum(shaped), carry[1] + lanes_sum(shaped * unit)

    su_ref[...] = jnp.zeros_like(su_ref)
    sums = lax.fori_loop(0, per, second, (zero, zero))
    over[1].wait_recv()
    passed[1].start()
    for copy in passed:
        copy.wait_recv()
    s_sum, s_cross = lax.fori_loop(per, 2 * per, second, sums)
    drain(units)
    shaped_mean = jnp.sum(s_sum, axis=1, keepdims=True) * (1.0 / full)
    cross_mean = jnp.sum(s_cross, axis=1, keepdims=True) * (1.0 / full)
    out_ref[...] = (wide_s[...] + (acc_s[...] + vec_d[0:1, pl.ds(2304, D)])).astype(BF)
    gmid_s[...] = jnp.zeros_like(gmid_s)

    def third(c, carry):
        at = pl.multiple_of(c * UCH, UCH)
        g = ffn_scale * (shp_s[:, pl.ds(at, UCH)] - shaped_mean - act_s[:, pl.ds(at, UCH)] * cross_mean)
        low = (g * dg_s[:, pl.ds(at, UCH)].astype(F32)).astype(BF)
        su_ref[2:3, pl.ds(at, UCH)] = column_sum(low.astype(F32))
        gmid_s[...] += dot_nt(low, w1[:, pl.ds(at, UCH)])
        put(c, dot_nn(midt_s[...], low).astype(BF), 0)
        return carry

    lax.fori_loop(0, full // UCH, third, 0)
    drain(0)

    grad_mid = gmid_s[...]
    unit = mid_s[...]
    sd_ref[1:2, :] = column_sum(grad_mid * unit)
    sd_ref[2:3, :] = column_sum(grad_mid)
    shaped = grad_mid * mid_gain
    grad_mixed = cot[...].astype(F32) + mid_scale * (
        shaped - jnp.mean(shaped, axis=1, keepdims=True) - unit * jnp.mean(shaped * unit, axis=1, keepdims=True)
    )
    branch = grad_mixed.astype(BF)
    gmix_ref[...] = branch
    branch_f = branch.astype(F32)
    sd_ref[0:1, :] = column_sum(branch_f)
    out_grad = dot_nn(jnp.transpose(branch_f).astype(BF), low_s[...]).astype(BF)
    stage[0, :, 0:width] = out_grad[:, 0:width]
    stage[1, :, 0:width] = out_grad[:, width : 2 * width]
    last = [
        pltpu.make_async_copy(stage.at[i, :, pl.ds(0, width)], packed.at[:, pl.ds(i * wide + 2 * units, width)], out_sems.at[i])
        for i in range(2)
    ]
    for copy in last:
        copy.start()
    grad_sub = dot_nt(branch, wo[...])
    unit = sub_s[...]
    cross = grad_sub * unit
    sw_ref[...] = jnp.zeros_like(sw_ref)
    sw_ref[0:1, :] = column_sum(cross)
    sw_ref[1:2, :] = column_sum(grad_sub)
    shaped = grad_sub * sub_gain
    grad_att = sub_scale * (
        shaped - jnp.mean(shaped, axis=1, keepdims=True) - unit * jnp.mean(shaped * unit, axis=1, keepdims=True)
    )
    gatt_m[...] = grad_att[:, 0:width].astype(BF)
    gatt_o[...] = grad_att[:, width : 2 * width].astype(BF)
    parts = ext_ref.shape[0]
    if parts > 1:
        sums_u, sums_w, sums_d = su_ref[...], sw_ref[...], sd_ref[...]
        for i in range(parts):
            ext_ref[i] = jnp.concatenate(
                [
                    window(sums_u, i * (units // parts)),
                    window(sums_u, units + i * (units // parts)),
                    window(sums_w, i * (width // parts)),
                    window(sums_w, width + i * (width // parts)),
                    window(sums_d, i * (D // parts)),
                    jnp.zeros((8, 128), F32),
                ],
                axis=0,
            ).astype(BF)
    for copy in last:
        copy.wait()
    for copy in over + passed:
        copy.wait_send()


def window(rows8, start):
    base = start // 128 * 128
    size = min(256, rows8.shape[1] - base)
    view = rows8[:, base : base + size]
    shift = start - base
    if shift:
        view = pltpu.roll(view, size - shift, 1)
    return view[:, 0:128]


def middle(att_m, att_o, hid, cot, vec_all, vec_got, w1, w2, wo, parts):
    rows = att_m.shape[0]
    units = w2.shape[0]
    width = wo[0].shape[0]
    vmem = pl.BlockSpec(memory_space=pltpu.VMEM)
    hbm = pl.BlockSpec(memory_space=pl.ANY)
    shape = jax.ShapeDtypeStruct
    return pl.pallas_call(
        mid_kernel,
        in_specs=[vmem] * 4 + [hbm] * 9,
        out_specs=[vmem] * 4 + [hbm] + [vmem] * 4,
        out_shape=[
            shape((rows, D), BF),
            shape((rows, width), BF),
            shape((rows, width), BF),
            shape((rows, D), BF),
            shape((D, 2 * (2 * units + width)), BF),
            shape((8, 2 * units), F32),
            shape((8, 2 * width), F32),
            shape((8, D), F32),
            shape((parts, 48, 128), BF),
        ],
        scratch_shapes=[
            pltpu.VMEM((8, 2 * units), F32),
            pltpu.VMEM((8, 2 * width), F32),
            pltpu.VMEM((D, 2 * units), BF),
            pltpu.VMEM((2 * units, D), BF),
            pltpu.VMEM((2 * width, D), BF),
            pltpu.VMEM((rows, 2 * units), F32),
            pltpu.VMEM((rows, 2 * units), F32),
            pltpu.VMEM((rows, 2 * units), BF),
            pltpu.VMEM((rows, D), F32),
            pltpu.VMEM((rows, D), F32),
            pltpu.VMEM((rows, D), F32),
            pltpu.VMEM((rows, 2 * width), F32),
            pltpu.VMEM((rows, D), F32),
            pltpu.VMEM((rows, 2 * width), BF),
            pltpu.VMEM((D, rows), BF),
            pltpu.VMEM((D, rows), BF),
            pltpu.VMEM((2, D, UCH), BF),
            pltpu.VMEM((rows, D), BF),
            pltpu.VMEM((rows, D), BF),
            pltpu.SemaphoreType.DMA((11,)),
            pltpu.SemaphoreType.DMA((2,)),
            pltpu.SemaphoreType.DMA((4,)),
            pltpu.SemaphoreType.DMA((4,)),
        ],
        compiler_params=pltpu.CompilerParams(vmem_limit_bytes=62 << 20, collective_id=3, has_side_effects=True),
        cost_estimate=pl.CostEstimate(flops=21 * 10**9, bytes_accessed=30 * 10**6, transcendentals=0),
        name="middle",
    )(att_m, att_o, vec_all, vec_got, hid, cot, *w1, *wo, w2)


def final_kernel(
    bits, hid, vec_all, dq, dk, dv, wq, wk, wv, gmix, ext, sum_k, sum_v, relay,
    gin, late_out, vec_out,
    loc_s, far_s, unit_s, mine_s, norm_s, send_c, recv_c, send_p, recv_p, give_c, give_p, late_s, small_s,
    vec_s, vec_r, sems_a, sems_b, loc_sems, *stage_refs,
):
    device = lax.axis_index("dp")
    side = lax.axis_index("tensor")
    across = {"dp": device, "tensor": 1 - side}
    peers = [{"dp": bit_peer(device, b), "tensor": side} for b in range(bits)]
    rows, width = dq.shape
    prompt = sum_k.shape[0]
    conts = rows - prompt
    half_p, half_c = prompt // 2, conts // 2
    own_p = pl.multiple_of(side * half_p, 128)
    their_p = pl.multiple_of((1 - side) * half_p, 128)
    own_c = pl.multiple_of(prompt + side * half_c, 128)
    their_c = pl.multiple_of(prompt + (1 - side) * half_c, 128)
    lanes = 3 * width + 128

    greet(peers + [across])
    count = [0]

    def remote(src, dst, peer):
        i = count[0]
        count[0] += 1
        copy = pltpu.make_async_remote_copy(
            src_ref=src, dst_ref=dst, send_sem=sems_a.at[i], recv_sem=sems_b.at[i], device_id=peer, device_id_type=MESH
        )
        copy.start()
        return copy

    share = remote(relay, far_s, peers[1])

    gain_f = vec_all[:, pl.ds(0, D)]
    bias_f = vec_all[:, pl.ds(D, D)]

    def unit_rows(at, size):
        x = hid[pl.ds(at, size), :].astype(F32)
        center = jnp.mean(x, axis=1, keepdims=True)
        scale = lax.rsqrt(jnp.mean(x * x, axis=1, keepdims=True) - center * center + EPSILON)
        return (x - center) * scale, scale

    def part_of(at, size, k_rows, v_rows):
        return dot_nt(dq[pl.ds(at, size), :], wq[...]) + dot_nt(k_rows, wk[...]) + dot_nt(v_rows, wv[...])

    def gather(part, unit):
        return column_sum(part * unit), column_sum(part)

    def normed_rows(at, size, unit):
        norm_s[:, pl.ds(at, size)] = jnp.transpose(unit * gain_f + bias_f).astype(BF)

    part = part_of(their_c, half_c, dk[pl.ds(their_c, half_c), :], dv[pl.ds(their_c, half_c), :])
    send_c[...] = part.astype(BF)
    y_cont = remote(send_c, recv_c, across)
    unit, _ = unit_rows(their_c, half_c)
    gain_grad, bias_grad = gather(part, unit)
    normed_rows(their_c, half_c, unit)
    unit, scale_c = unit_rows(own_c, half_c)
    part = part_of(own_c, half_c, dk[pl.ds(own_c, half_c), :], dv[pl.ds(own_c, half_c), :])
    mine_s[pl.ds(half_p, half_c), :] = part
    unit_s[pl.ds(half_p, half_c), :] = unit
    g, b = gather(part, unit)
    gain_grad, bias_grad = gain_grad + g, bias_grad + b
    normed_rows(own_c, half_c, unit)

    share.wait_recv()
    for i, total in enumerate((sum_k, sum_v)):
        loc_s[i, :, pl.ds(0, width - 128)] = total[:, pl.ds(0, width - 128)]
        loc_s[i, :, pl.ds(width - 128, 128)] = (
            total[:, pl.ds(width - 128, 128)].astype(F32) + far_s[i].astype(F32)
        ).astype(BF)
    part = part_of(their_p, half_p, loc_s[0, pl.ds(their_p, half_p), :], loc_s[1, pl.ds(their_p, half_p), :])
    send_p[...] = part.astype(BF)
    y_prompt = remote(send_p, recv_p, across)
    unit, _ = unit_rows(their_p, half_p)
    normed_rows(their_p, half_p, unit)
    g, b = gather(part, unit)
    gain_grad, bias_grad = gain_grad + g, bias_grad + b
    unit, scale_p = unit_rows(own_p, half_p)
    unit_s[pl.ds(0, half_p), :] = unit
    normed_rows(own_p, half_p, unit)
    part = part_of(own_p, half_p, loc_s[0, pl.ds(own_p, half_p), :], loc_s[1, pl.ds(own_p, half_p), :])
    mine_s[pl.ds(0, half_p), :] = part
    g, b = gather(part, unit)
    gain_grad, bias_grad = gain_grad + g, bias_grad + b

    blocks = 1 << bits
    block = D // blocks

    def keep(value, lane):
        low = value.astype(BF)
        for i in range(blocks):
            late_s[i // 2, i % 2, :, pl.ds(lane, width)] = low[i * block : (i + 1) * block, :]

    keep(dot_nn(norm_s[...], dq[...]), 0)
    q_bias = column_sum(dq[...].astype(F32))
    for i, rest in enumerate((dk, dv)):
        keep(
            dot_nn(norm_s[:, pl.ds(0, prompt)], loc_s[i])
            + dot_nn(norm_s[:, pl.ds(prompt, conts)], rest[pl.ds(prompt, conts), :]),
            (i + 1) * width,
        )
    v_bias = column_sum(loc_s[1].astype(F32)) + column_sum(dv[pl.ds(prompt, conts), :].astype(F32))

    def norm_back(total, unit, scale, mixed):
        shaped = total * gain_f
        return mixed.astype(F32) + scale * (
            shaped - jnp.mean(shaped, axis=1, keepdims=True) - unit * jnp.mean(shaped * unit, axis=1, keepdims=True)
        )

    small_s[...] = jnp.zeros_like(small_s)
    small_s[0:1, pl.ds(0, width)] = q_bias
    small_s[1:2, pl.ds(0, width)] = v_bias
    small_s[2:3, pl.ds(0, D)] = gain_grad
    small_s[3:4, pl.ds(0, D)] = bias_grad
    small = small_s[...]
    row_id = lax.broadcasted_iota(jnp.int32, (8, 128), 0)
    for i in range(blocks):
        narrow = window(small, i * (width // blocks))
        broad = window(small, i * block)
        tail = jnp.concatenate([ext[i, pl.ds(32, 16), :].astype(F32)[0:8], jnp.where(row_id < 2, narrow, broad)], axis=0)
        late_s[i // 2, i % 2, pl.ds(0, 32), pl.ds(3 * width, 128)] = ext[i, pl.ds(0, 32), :]
        late_s[i // 2, i % 2, pl.ds(32, 16), pl.ds(3 * width, 128)] = tail.astype(BF)

    def input_rows(arrived, at, size, scale, held, rows_at, sem):
        arrived[0].wait_recv()
        here = pl.ds(at, size)
        total = mine_s[here, :] + arrived[1][...].astype(F32)
        held[...] = norm_back(total, unit_s[here, :], scale, gmix[here, :]).astype(BF)
        back = remote(held, gin.at[pl.ds(rows_at, size), :], across)
        kept = pltpu.make_async_copy(held, gin.at[pl.ds(rows_at, size), :], loc_sems.at[sem])
        kept.start()
        return back, kept

    source = late_s
    stages = []
    for bit in range(bits):
        landing, kept = stage_refs[2 * bit], stage_refs[2 * bit + 1]
        mine = (device // (1 << bit)) % 2
        copy = remote(source.at[:, 1 - mine], landing, peers[bit])
        if bit == 0:
            back_c, keep_c = input_rows((y_cont, recv_c), half_p, half_c, scale_c, give_c, own_c, 0)
        if bit == 1:
            back_p, keep_p = input_rows((y_prompt, recv_p), 0, half_p, scale_p, give_p, own_p, 1)
        copy.wait_recv()
        stages.append(copy)
        for i in range(landing.shape[0]):
            kept[i // 2, i % 2] = (source[i, mine].astype(F32) + landing[i].astype(F32)).astype(BF)
        source = kept
    late_out[...] = source[0, 0, :, pl.ds(0, 3 * width)].astype(F32)
    vec_s[...] = source[0, 0, :, pl.ds(3 * width, 128)]
    swap = remote(vec_s, vec_r, across)
    swap.wait_recv()
    vec_out[0] = vec_s[...].astype(F32)
    vec_out[1] = vec_r[...].astype(F32)
    for copy in stages + [share, y_cont, y_prompt, swap]:
        copy.wait_send()
    for copy in (back_c, back_p):
        copy.wait_recv()
        copy.wait_send()
    keep_c.wait()
    keep_p.wait()


def finish(hid, vec_all, dq, dk, dv, wq, wk, wv, gmix, ext, sum_k, sum_v, relay):
    rows, width = dq.shape
    ranks = lax.axis_size("dp")
    bits = ranks.bit_length() - 1
    block = D // ranks
    prompt = sum_k.shape[0]
    conts = rows - prompt
    lanes = 3 * width + 128
    vmem = pl.BlockSpec(memory_space=pltpu.VMEM)
    hbm = pl.BlockSpec(memory_space=pl.ANY)
    shape = jax.ShapeDtypeStruct
    copies = 6 + bits
    stages = []
    for bit in range(bits):
        left = ranks >> (bit + 1)
        stages.append(pltpu.VMEM((left, block, lanes), BF))
        stages.append(pltpu.VMEM((max(left // 2, 1), min(left, 2), block, lanes), BF))
    return pl.pallas_call(
        functools.partial(final_kernel, bits),
        in_specs=[vmem] * 13,
        out_specs=[hbm, vmem, vmem],
        out_shape=[shape((rows, D), BF), shape((block, 3 * width), F32), shape((2, block, 128), F32)],
        scratch_shapes=[
            pltpu.VMEM((2, prompt, width), BF),
            pltpu.VMEM((2, prompt, 128), BF),
            pltpu.VMEM((rows // 2, D), F32),
            pltpu.VMEM((rows // 2, D), F32),
            pltpu.VMEM((D, rows), BF),
            pltpu.VMEM((conts // 2, D), BF),
            pltpu.VMEM((conts // 2, D), BF),
            pltpu.VMEM((prompt // 2, D), BF),
            pltpu.VMEM((prompt // 2, D), BF),
            pltpu.VMEM((conts // 2, D), BF),
            pltpu.VMEM((prompt // 2, D), BF),
            pltpu.VMEM((ranks // 2, 2, block, lanes), BF),
            pltpu.VMEM((8, D + 128), F32),
            pltpu.VMEM((block, 128), BF),
            pltpu.VMEM((block, 128), BF),
            pltpu.SemaphoreType.DMA((copies,)),
            pltpu.SemaphoreType.DMA((copies,)),
            pltpu.SemaphoreType.DMA((2,)),
        ]
        + stages,
        compiler_params=pltpu.CompilerParams(vmem_limit_bytes=56 << 20, collective_id=1, has_side_effects=True),
        cost_estimate=pl.CostEstimate(flops=5 * 10**9, bytes_accessed=20 * 10**6, transcendentals=0),
        name="finish",
    )(hid, vec_all, dq, dk, dv, wq, wk, wv, gmix, ext, sum_k, sum_v, relay)


def flip(value, axis, bit):
    return lax.ppermute(value, axis, [(i, i ^ (1 << bit)) for i in range(lax.axis_size(axis))])


def contract_rows(left, right):
    return lax.dot_general(left, right, (((0,), (0,)), ((), ())), preferred_element_type=F32)


def back_project(left, right):
    return lax.dot_general(left, right, (((1,), (1,)), ((), ())), preferred_element_type=F32)


def norm_rows(values, gain, bias):
    center = jnp.mean(values, axis=-1, keepdims=True)
    spread = jnp.mean(values * values, axis=-1, keepdims=True) - center * center
    scaled = lax.rsqrt(spread + EPSILON)
    unit_rows = (values - center) * scaled
    return (unit_rows * gain + bias, unit_rows, scaled)


def norm_back(grad_rows, gain, unit_rows, scaled):
    shaped = grad_rows * gain
    return scaled * (
        shaped
        - jnp.mean(shaped, axis=-1, keepdims=True)
        - unit_rows * jnp.mean(shaped * unit_rows, axis=-1, keepdims=True)
    )


def in_order(which, mine, other, axis):
    return jnp.where(
        which == 0,
        jnp.concatenate([mine, other], axis=axis),
        jnp.concatenate([other, mine], axis=axis),
    )


def halving(value, device):
    bits = lax.axis_size("dp").bit_length() - 1
    rows, columns = value.shape
    current = value
    for bit in range(bits):
        upper = device // (1 << bit) % 2
        left = bits - bit
        view = current.reshape((1 << (left - 1), 2, -1, columns))
        kept = lax.dynamic_index_in_dim(view, upper, 1, keepdims=False)
        sent = lax.dynamic_index_in_dim(view, 1 - upper, 1, keepdims=False)
        got = flip(sent, "dp", bit)
        current = (kept.astype(F32) + got.astype(F32)).astype(BF)
    return current.reshape(rows >> bits, columns)


def half_of(value, which):
    prompt, conts = CHUNK // 2, (value.shape[0] - CHUNK) // 2
    return jnp.concatenate(
        [
            lax.dynamic_slice_in_dim(value, which * prompt, prompt),
            lax.dynamic_slice_in_dim(value, CHUNK + which * conts, conts),
        ]
    )


def joined(which, mine, other):
    prompt = CHUNK // 2
    low = jnp.where(which == 0, mine, other)
    high = jnp.where(which == 0, other, mine)
    return jnp.concatenate([low[:prompt], high[:prompt], low[prompt:], high[prompt:]])


def body(
    hidden_in,
    cotangent,
    prompt_start,
    cont_gap,
    seg_len,
    dilation_rate,
    pre_gain,
    pre_bias,
    query_weight,
    query_bias,
    key_weight,
    value_weight,
    value_bias,
    sub_gain,
    sub_bias,
    out_weight,
    out_bias,
    mid_gain,
    mid_bias,
    inner_weight,
    inner_bias,
    ffn_gain,
    ffn_bias,
    outer_weight,
    outer_bias,
):
    device = lax.axis_index("dp")
    ranks = lax.axis_size("dp")
    group_id = device // GDEV
    member = device % GDEV
    tensor_id = lax.axis_index("tensor")
    core = device % 2
    width = query_weight.shape[1]
    units = inner_weight.shape[1]
    pairs = width // 128
    rows = hidden_in.shape[0]
    prompt_rows = CHUNK
    cont_count = (rows - prompt_rows) // CONT

    vectors = jnp.concatenate(
        [
            pre_gain,
            pre_bias,
            query_bias,
            value_bias,
            ffn_gain,
            ffn_bias,
            inner_bias,
            sub_gain,
            sub_bias,
            out_bias,
            mid_gain,
            mid_bias,
            outer_bias,
        ]
    ).astype(F32)[None]
    pre_gain_f = pre_gain.astype(F32)

    (
        weighed,
        inverse,
        queries,
        keys,
        values,
        prompt_keys,
        prompt_values,
        attended,
        att_mine,
        att_got,
        *pieces,
        vectors_other,
    ) = attend(
        prompt_start,
        cont_gap,
        seg_len,
        dilation_rate,
        hidden_in,
        vectors,
        query_weight,
        key_weight,
        value_weight,
        inner_weight,
        out_weight,
    )
    inner_parts = (inner_weight, pieces[0], pieces[1])
    out_parts = (out_weight, pieces[2], pieces[3])

    fused = ranks == 16
    out_half, grad_mine, grad_theirs, grad_mixed_low, packed, sum_u, sum_w, sum_d, ext = middle(
        att_mine,
        att_got,
        hidden_in,
        cotangent,
        vectors,
        vectors_other,
        inner_parts,
        outer_weight,
        out_parts,
        ranks if fused else 1,
    )

    grad_query_in, own_key_grad, own_value_grad, key_sum, value_sum, relay, out_got, *early = attend_back(
        queries,
        keys,
        values,
        prompt_keys,
        prompt_values,
        attended,
        inverse,
        weighed,
        grad_mine,
        grad_theirs,
        out_half,
        packed.reshape(2, 2, 2, 2, D // ranks, -1) if fused else None,
    )
    if fused:
        early_sum = early[0]
    else:
        early = lax.psum_scatter(packed, "dp", scatter_dimension=0, tiled=True)
        early_mine, early_other = jnp.split(early, 2, axis=1)
        early_sum = early_mine.astype(F32) + flip(early_other, "tensor", 0).astype(F32)
    inner_weight_grad = early_sum[:, :units]
    outer_weight_grad = early_sum[:, units : 2 * units].T
    out_weight_grad = early_sum[:, 2 * units :].T
    output = joined(tensor_id, out_half, out_got)
    block = D // ranks
    per_u, per_w, per_d = units // ranks, width // ranks, D // ranks
    if fused:
        input_low, late, vec = finish(
            hidden_in,
            vectors,
            grad_query_in,
            own_key_grad,
            own_value_grad,
            query_weight,
            key_weight,
            value_weight,
            grad_mixed_low,
            ext,
            key_sum,
            value_sum,
            relay,
        )
        ffn_gain_grad, ffn_bias_grad, inner_bias_grad = [vec[0, i, :per_u] + vec[1, 8 + i, :per_u] for i in range(3)]
        sub_gain_grad, sub_bias_grad = [vec[0, 16 + i, :per_w] + vec[1, 24 + i, :per_w] for i in range(2)]
        out_bias_grad, mid_gain_grad, mid_bias_grad, outer_bias_grad = [
            vec[0, 32 + i, :per_d] + vec[1, 32 + i, :per_d] for i in range(4)
        ]
        query_bias_grad, value_bias_grad = [vec[0, 40 + i, :per_w] for i in range(2)]
        pre_gain_grad, pre_bias_grad = [vec[0, 42 + i, :per_d] + vec[1, 42 + i, :per_d] for i in range(2)]
    else:
        pre_normed, pre_unit, pre_scale = norm_rows(hidden_in.astype(F32), pre_gain_f, pre_bias.astype(F32))
        pre_low = pre_normed.astype(BF)
        last = width - 128
        far = flip(relay, "dp", 1).astype(F32)
        summed = jnp.stack([key_sum, value_sum]).astype(F32)
        summed = jnp.concatenate([summed[:, :, :last], summed[:, :, last:] + far], axis=2).astype(BF)
        grad_keys = jnp.concatenate([summed[0], own_key_grad[prompt_rows:]], axis=0)
        grad_values = jnp.concatenate([summed[1], own_value_grad[prompt_rows:]], axis=0)

        query_weight_grad = contract_rows(pre_low, grad_query_in)
        key_weight_grad = contract_rows(pre_low, grad_keys)
        value_weight_grad = contract_rows(pre_low, grad_values)
        query_bias_grad = jnp.sum(grad_query_in.astype(F32), axis=0)
        value_bias_grad = jnp.sum(grad_values.astype(F32), axis=0)
        grad_normed_part = (
            back_project(grad_query_in, query_weight)
            + back_project(grad_keys, key_weight)
            + back_project(grad_values, value_weight)
        )
        grad_normed_low = grad_normed_part.astype(BF)
        grad_normed = grad_normed_low.astype(F32) + flip(grad_normed_low, "tensor", 0).astype(F32)
        pre_gain_grad = jnp.sum(grad_normed * pre_unit, axis=0)
        pre_bias_grad = jnp.sum(grad_normed, axis=0)
        grad_mixed_all = joined(tensor_id, grad_mixed_low, flip(grad_mixed_low, "tensor", 0)).astype(F32)
        input_low = (grad_mixed_all + norm_back(grad_normed, pre_gain_f, pre_unit, pre_scale)).astype(BF)

        vec = jnp.concatenate(
            [
                sum_u[:3].reshape(3, 2, ranks, per_u).transpose(2, 1, 0, 3).reshape(ranks, 6 * per_u),
                sum_w[:2].reshape(2, 2, ranks, per_w).transpose(2, 1, 0, 3).reshape(ranks, 4 * per_w),
                sum_d[:4].reshape(4, ranks, per_d).swapaxes(0, 1).reshape(ranks, 4 * per_d),
                jnp.stack([query_bias_grad, value_bias_grad]).reshape(2, ranks, per_w).swapaxes(0, 1).reshape(ranks, 2 * per_w),
                jnp.stack([pre_gain_grad, pre_bias_grad]).reshape(2, ranks, per_d).swapaxes(0, 1).reshape(ranks, 2 * per_d),
            ],
            axis=1,
        )
        count = vec.shape[1]
        vec = jnp.pad(vec, ((0, 0), (0, block * 128 - count))).reshape(D, 128)
        late = halving(
            jnp.concatenate(
                [p.astype(BF) for p in (query_weight_grad, key_weight_grad, value_weight_grad, vec)], axis=1
            ),
            device,
        )
        vec = late[:, 3 * width :].reshape(-1)[:count]
        late = late[:, : 3 * width].astype(F32)
        at_w = 6 * per_u
        at_d = at_w + 4 * per_w
        at_late = at_d + 4 * per_d
        got = flip(vec[:at_late], "tensor", 0).astype(F32)
        vec = vec.astype(F32)
        ffn_gain_grad, ffn_bias_grad, inner_bias_grad = (vec[: 3 * per_u] + got[3 * per_u : at_w]).reshape(3, per_u)
        sub_gain_grad, sub_bias_grad = (vec[at_w : at_w + 2 * per_w] + got[at_w + 2 * per_w : at_d]).reshape(2, per_w)
        out_bias_grad, mid_gain_grad, mid_bias_grad, outer_bias_grad = (vec[at_d:at_late] + got[at_d:]).reshape(4, per_d)
        query_bias_grad, value_bias_grad = vec[at_late : at_late + 2 * per_w].reshape(2, per_w)
        pre_gain_grad, pre_bias_grad = vec[at_late + 2 * per_w :].reshape(2, per_d)
    return (
        output,
        input_low,
        pre_gain_grad,
        pre_bias_grad,
        late[:, :width],
        query_bias_grad,
        late[:, width : 2 * width],
        late[:, 2 * width : 3 * width],
        value_bias_grad,
        sub_gain_grad,
        sub_bias_grad,
        out_weight_grad,
        out_bias_grad,
        mid_gain_grad,
        mid_bias_grad,
        inner_weight_grad,
        inner_bias_grad,
        ffn_gain_grad,
        ffn_bias_grad,
        outer_weight_grad,
        outer_bias_grad,
    )

def solution(mesh):
    placed = (
        P("dp", None),
        P("dp", None),
        P(),
        P(),
        P(),
        P(),
        P(),
        P(),
        P(None, "tensor"),
        P("tensor"),
        P(None, "tensor"),
        P(None, "tensor"),
        P("tensor"),
        P("tensor"),
        P("tensor"),
        P("tensor", None),
        P(),
        P(),
        P(),
        P(None, "tensor"),
        P("tensor"),
        P("tensor"),
        P("tensor"),
        P("tensor", None),
        P(),
    )
    return jax.shard_map(
        body,
        mesh=mesh,
        in_specs=placed,
        out_specs=(
            P("dp", None),
            P("dp", None),
            P("dp"),
            P("dp"),
            P("dp", "tensor"),
            P(("tensor", "dp")),
            P("dp", "tensor"),
            P("dp", "tensor"),
            P(("tensor", "dp")),
            P(("tensor", "dp")),
            P(("tensor", "dp")),
            P("tensor", "dp"),
            P("dp"),
            P("dp"),
            P("dp"),
            P("dp", "tensor"),
            P(("tensor", "dp")),
            P(("tensor", "dp")),
            P(("tensor", "dp")),
            P("tensor", "dp"),
            P("dp"),
        ),
        check_vma=False,
    )
```

```python
import functools

import jax
import jax.numpy as jnp
from jax import lax
from jax.experimental import pallas as pl
from jax.experimental.pallas import tpu as pltpu
from jax.sharding import PartitionSpec as P

HD = 64
PROMPT = 2048
CONT = 256
GDEV = 4
TILE = 256
CHUNK = PROMPT // GDEV
PTILES = CHUNK // TILE
LOG2E = 1.4426950408889634
BF = jnp.bfloat16
F32 = jnp.float32
D = 768
EPSILON = 1e-05
MESH = pl.DeviceIdType.MESH


def dot_nt(a, b):
    return lax.dot_general(a, b, (((1,), (1,)), ((), ())), preferred_element_type=F32)


def dot_nn(a, b):
    return lax.dot_general(a, b, (((1,), (0,)), ((), ())), preferred_element_type=F32)


def low_half(rows):
    return lax.broadcasted_iota(jnp.int32, (rows, 128), 1) < HD


def settings(seg, rate, pair):
    def row(value):
        return jnp.broadcast_to(value, (1, 128)).astype(F32)

    def rest(number, period):
        return number - period * jnp.floor((number + 0.5) / period)

    at = pl.ds(pair, 1)
    second, third = row(rate[at, 1:2]), row(rate[at, 2:3])
    head = jnp.full((1, 128), 2 * pair, jnp.int32).astype(F32)
    return (
        1.0 / row(seg[at, 0:1]),
        1.0 / row(seg[at, 1:2]),
        second,
        1.0 / second,
        third,
        1.0 / third,
        rest(head, second),
        rest(head + 1.0, second),
        rest(head, third),
        rest(head + 1.0, third),
    )


def codes(at, cells, miss):
    first = jnp.floor((at + 0.5) * cells[0])
    second = jnp.floor((at + 0.5) * cells[1])
    rest1 = at - cells[2] * jnp.floor((at + 0.5) * cells[3])
    rest2 = at - cells[4] * jnp.floor((at + 0.5) * cells[5])
    return [
        first,
        jnp.where(rest1 == cells[6], second, miss),
        jnp.where(rest1 == cells[7], second, miss),
        jnp.where(rest2 == cells[8], 1.0, 0.0),
        jnp.where(rest2 == cells[9], 1.0, 0.0),
    ]


def bit_peer(device, bit):
    step = 1 << bit
    return device + (1 - 2 * ((device // step) % 2)) * step


def greet(peers):
    barrier = pltpu.get_barrier_semaphore()
    for peer in peers:
        pl.semaphore_signal(barrier, inc=1, device_id=peer, device_id_type=MESH)
    pl.semaphore_wait(barrier, len(peers))


def xor_bits(a, b):
    return (a % 2 + b % 2) % 2 + 2 * ((a // 2 + b // 2) % 2)


def fwd_kernel(
    starts, gaps, seg, rate, hid, vec, wq, wk, wv, w1, wo, vec_hbm,
    e_ref, li_ref, q_out, k_out, v_out, kp_out, vp_out, o_out, mine_out, got_out,
    w1_got, w1_swap, wo_got, wo_swap, vec_got,
    t_s, kc_s, kv_s, low_s, q_s, ko_s, vo_s, o_s, sems_a, sems_b, loc_sems,
):
    pair = pl.program_id(0)
    step = pl.program_id(1)
    pairs = pl.num_programs(0)
    device = lax.axis_index("dp")
    side = lax.axis_index("tensor")
    member = device % GDEV
    core = device % 2
    rows, width = q_s.shape
    n_pairs = width // 128
    last_pair = n_pairs - 1
    conts = rows - CHUNK
    near = {"dp": bit_peer(device, 0), "tensor": side}
    far = {"dp": bit_peer(device, 1), "tensor": side}
    across = {"dp": device, "tensor": 1 - side}
    half_u = w1.shape[1] // 2
    half_w = wo.shape[0] // 2
    half_p, half_c = CHUNK // 2, conts // 2
    sent_u = pl.multiple_of(core * half_u, 128)
    shared_at = 2 * D + 2 * width
    sent_w = pl.multiple_of(core * half_w, 64)

    def remote(i, src, dst, peer):
        return pltpu.make_async_remote_copy(
            src_ref=src, dst_ref=dst, send_sem=sems_a.at[i], recv_sem=sems_b.at[i], device_id=peer, device_id_type=MESH
        )

    def to_far(p):
        lanes = pl.ds(p * 128, 128)
        return remote(3 * p, kv_s.at[0, :, :, lanes], kv_s.at[2, :, :, lanes], far)

    def to_near(p):
        lanes = pl.ds(p * 128, 128)
        return remote(3 * p + 1, kv_s.at[0, :, :, lanes], kv_s.at[1, :, :, lanes], near)

    def relay(p):
        lanes = pl.ds(p * 128, 128)
        return remote(3 * p + 2, kv_s.at[2, :, :, lanes], kv_s.at[3, :, :, lanes], near)

    base = 3 * n_pairs
    fetch_y = [
        remote(base, wo.at[pl.ds(sent_w, half_w), :], wo_got, across),
        remote(base + 1, w1.at[:, pl.ds(sent_u, half_u)], w1_got, across),
        remote(base + 2, vec_hbm.at[:, pl.ds(shared_at, vec_got.shape[1])], vec_got, across),
    ]
    fetch_core = [
        remote(base + 3, wo_got, wo_swap, near),
        remote(base + 4, w1_got, w1_swap, near),
    ]

    def give(p, piece):
        lanes = pl.ds(p * 128, 128)
        their_p = pl.multiple_of((1 - side) * half_p, 128)
        their_c = pl.multiple_of(CHUNK + (1 - side) * half_c, 128)
        third = half_c // 3
        if piece == 0:
            source, target = pl.ds(their_p, half_p), pl.ds(0, half_p)
        else:
            source = pl.ds(pl.multiple_of(their_c + (piece - 1) * third, 128), third)
            target = pl.ds(half_p + (piece - 1) * third, third)
        return remote(base + 5 + 4 * p + piece, o_s.at[source, lanes], got_out.at[target, lanes], across)

    def keeps():
        own_p = pl.multiple_of(side * half_p, 128)
        own_c = pl.multiple_of(CHUNK + side * half_c, 128)
        return [
            pltpu.make_async_copy(o_s, o_out, loc_sems.at[0]),
            pltpu.make_async_copy(o_s.at[pl.ds(own_p, half_p), :], mine_out.at[pl.ds(0, half_p), :], loc_sems.at[1]),
            pltpu.make_async_copy(o_s.at[pl.ds(own_c, half_c), :], mine_out.at[pl.ds(half_p, half_c), :], loc_sems.at[2]),
        ]

    def saves():
        out = [
            pltpu.make_async_copy(q_s, q_out, loc_sems.at[3]),
            pltpu.make_async_copy(ko_s, k_out, loc_sems.at[0]),
            pltpu.make_async_copy(vo_s, v_out, loc_sems.at[5]),
        ]
        for r in range(GDEV):
            span = pl.ds(r * CHUNK, CHUNK)
            out.append(pltpu.make_async_copy(kv_s.at[r, 0], kp_out.at[span, :], loc_sems.at[6 + 2 * r]))
            out.append(pltpu.make_async_copy(kv_s.at[r, 1], vp_out.at[span, :], loc_sems.at[7 + 2 * r]))
        return out

    @pl.when((pair == 0) & (step == 0))
    def _():
        greet([near, far, across])
        for copy in fetch_y:
            copy.start()
        gain_f, bias_f = vec[:, pl.ds(0, D)], vec[:, pl.ds(D, D)]
        query_bias = vec[:, pl.ds(2 * D, width)]
        value_bias = vec[:, pl.ds(2 * D + width, width)]

        def norm(at, size):
            x = hid[at : at + size, :].astype(F32)
            center = jnp.mean(x, axis=1, keepdims=True)
            scale = lax.rsqrt(jnp.mean(x * x, axis=1, keepdims=True) - center * center + EPSILON)
            low = ((x - center) * scale * gain_f + bias_f).astype(BF)
            low_s[at : at + size, :] = low
            return low

        low = norm(0, CHUNK)
        kv_s[0, 0] = dot_nn(low, wk[...]).astype(BF)
        kv_s[0, 1] = (dot_nn(low, wv[...]) + value_bias).astype(BF)
        to_far(0).start()
        for p in range(n_pairs):
            to_near(p).start()
        for at in range(CHUNK, rows, TILE):
            low = norm(at, TILE)
            ko_s[at - CHUNK : at - CHUNK + TILE, :] = dot_nn(low, wk[...]).astype(BF)
            vo_s[at - CHUNK : at - CHUNK + TILE, :] = (dot_nn(low, wv[...]) + value_bias).astype(BF)
        to_far(0).wait_send()
        for p in range(1, n_pairs):
            to_far(p).start()
        for at in range(0, rows, TILE):
            q_s[at : at + TILE, :] = ((dot_nn(low_s[at : at + TILE, :], wq[...]) + query_bias) * 0.125).astype(BF)
        to_far(0).wait_recv()
        relay(0).start()

    for p in range(n_pairs):
        @pl.when((pair == p) & (step == 0))
        def _():
            to_near(p).wait_recv()
            relay(p).wait_recv()

        if p + 1 < n_pairs:
            @pl.when((pair == p) & (step == 3))
            def _():
                to_far(p + 1).wait_recv()
                relay(p + 1).start()

    lanes = pl.ds(pl.multiple_of(pair * 128, 128), 128)
    low = low_half(TILE)
    q = q_s[pl.ds(pl.multiple_of(step * TILE, TILE), TILE), lanes]
    zero = jnp.zeros_like(q)
    qs = [jnp.where(low, q, zero), jnp.where(low, zero, q)]
    row = lax.broadcasted_iota(jnp.int32, (TILE, 128), 0).astype(F32)
    group = device // GDEV
    start = starts[group]
    first_cont = member * (conts // CONT)
    own_gap = gaps[group, first_cont + jnp.maximum(step - PTILES, 0)]
    base_q = start + jnp.where(step < PTILES, member * CHUNK + step * TILE, PROMPT + own_gap)
    cells = settings(seg, rate, side * n_pairs + pair)
    at_q = base_q.astype(F32) + row
    qc = codes(at_q, cells, -2.0)

    @pl.when(step == 0)
    def _():
        ahead = lax.broadcasted_iota(jnp.int32, (8, 128), 1).astype(F32) + start.astype(F32)
        for j in range(PROMPT // 128):
            for i, c in enumerate(codes(ahead + j * 128.0, cells, -1.0)):
                kc_s[i, :, j * 128 : (j + 1) * 128] = c

    def logits(mx, keys, kc, causal, at, span):
        out = []
        for h in range(2):
            s = dot_nt(qs[h], keys)
            top = mx[h]
            for g in range(span // 128):
                part = slice(g * 128, (g + 1) * 128)
                w = jnp.where(qc[0] == kc[0][:, part], 1.0, 0.0)
                w = w + jnp.where(qc[1 + h] == kc[1 + h][:, part], 1.0, 0.0)
                w = w + qc[3 + h] * kc[3 + h][:, part]
                if causal is not None:
                    w = jnp.where(causal[:, part], w, 0.0)
                t = s[:, part] * LOG2E + jnp.log2(w)
                t_s[h, :, pl.ds(at + g * 128, 128)] = t
                top = jnp.maximum(top, t)
            out.append(top)
        return tuple(out)

    def weigh(carry, vals, m, at, span):
        sums, accs = carry
        ns, na = [], []
        for h in range(2):
            total = sums[h]
            parts = []
            for g in range(span // 128):
                e = jnp.exp2(t_s[h, :, pl.ds(at + g * 128, 128)] - m[h])
                total = total + e
                parts.append(e.astype(BF))
            el = jnp.concatenate(parts, axis=1)
            e_ref[h, :, pl.ds(at, span)] = el
            ns.append(total)
            na.append(accs[h] + dot_nn(el, vals))
        return (tuple(ns), tuple(na))

    def finish_rows(carry):
        sums, accs = carry
        li = [1.0 / jnp.sum(s, axis=1, keepdims=True) for s in sums]
        lfull = jnp.where(low, li[0], li[1])
        li_ref[...] = lfull
        o_s[pl.ds(pl.multiple_of(step * TILE, TILE), TILE), lanes] = (jnp.where(low, accs[0], accs[1]) * lfull).astype(BF)

    def tops(mx):
        return [jnp.broadcast_to(jnp.max(x, axis=1, keepdims=True), (TILE, 128)) for x in mx]

    neg = jnp.full((TILE, 128), -jnp.inf, F32)
    zf = jnp.zeros((TILE, 128), F32)

    def key_codes(at, span):
        return [kc_s[i, 0:1, pl.ds(at, span)] for i in range(5)]

    @pl.when(step < PTILES)
    def _():
        def one(j, mx):
            at = pl.multiple_of(j * CHUNK, CHUNK)
            held = xor_bits(j, member)
            return logits(
                mx, kv_s[held, 0, :, lanes], key_codes(at, CHUNK), None, pl.multiple_of(held * CHUNK, CHUNK), CHUNK
            )

        mx = lax.fori_loop(0, member, one, (neg, neg))
        at = pl.multiple_of(member * CHUNK, CHUNK)
        rows_id = lax.broadcasted_iota(jnp.int32, (TILE, CHUNK), 0) + step * TILE
        cols = lax.broadcasted_iota(jnp.int32, (TILE, CHUNK), 1)
        mx = logits(mx, kv_s[0, 0, :, lanes], key_codes(at, CHUNK), cols <= rows_id, 0, CHUNK)
        m = tops(mx)

        def two(j, carry):
            held = xor_bits(j, member)
            return weigh(carry, kv_s[held, 1, :, lanes], m, pl.multiple_of(held * CHUNK, CHUNK), CHUNK)

        finish_rows(lax.fori_loop(0, member + 1, two, ((zf, zf), (zf, zf))))

    @pl.when(step >= PTILES)
    def _():
        own = pl.ds(pl.multiple_of((step - PTILES) * TILE, TILE), TILE)
        mx = (neg, neg)
        for j in range(GDEV):
            at = pl.multiple_of(xor_bits(j, member) * CHUNK, CHUNK)
            mx = logits(mx, kv_s[j, 0, :, lanes], key_codes(at, CHUNK), None, j * CHUNK, CHUNK)
        rows_id = lax.broadcasted_iota(jnp.int32, (TILE, CONT), 0)
        cols = lax.broadcasted_iota(jnp.int32, (TILE, CONT), 1)
        ahead = lax.broadcasted_iota(jnp.int32, (8, 128), 1).astype(F32) + base_q.astype(F32)
        parts = [codes(ahead + j * 128.0, cells, -1.0) for j in range(CONT // 128)]
        own_codes = [jnp.concatenate([part[i] for part in parts], axis=1)[0:1] for i in range(5)]
        mx = logits(mx, ko_s[own, lanes], own_codes, cols <= rows_id, PROMPT, CONT)
        m = tops(mx)
        carry = ((zf, zf), (zf, zf))
        for j in range(GDEV):
            carry = weigh(carry, kv_s[j, 1, :, lanes], m, j * CHUNK, CHUNK)
        finish_rows(weigh(carry, vo_s[own, lanes], m, PROMPT, CONT))

    end = pl.num_programs(1) - 1
    for p in range(n_pairs):
        @pl.when((pair == p) & (step == 1 - side))
        def _():
            give(p, 0).start()

        for unit in range(6):
            @pl.when((pair == p) & (step == PTILES + unit // 2) & (side == 1 - unit // 3))
            def _():
                give(p, 1 + unit % 3).start()

    @pl.when((pair == last_pair - 1) & (step == 3))
    def _():
        for i in range(2):
            fetch_y[i].wait_recv()
            fetch_core[i].start()

    @pl.when((pair == last_pair) & (step == 0))
    def _():
        for copy in saves():
            copy.start()

    @pl.when((pair == last_pair) & (step == end))
    def _():
        for copy in keeps():
            copy.start()
        fetch_y[2].wait_recv()
        for copy in fetch_core:
            copy.wait_recv()
        for p in range(n_pairs):
            for piece in range(4):
                copy = give(p, piece)
                copy.wait_recv()
                copy.wait_send()
            if p > 0:
                to_far(p).wait_send()
            to_near(p).wait_send()
            relay(p).wait_send()
        for copy in fetch_y + fetch_core:
            copy.wait_send()
        for copy in keeps() + saves():
            copy.wait()


def attend(starts, gaps, seg, rate, hid, vec, wq, wk, wv, w1, wo):
    rows = hid.shape[0]
    width = wq.shape[1]
    pairs = width // 128
    span = PROMPT + CONT
    conts = rows - CHUNK
    units = w1.shape[1]
    vmem = pl.BlockSpec(memory_space=pltpu.VMEM)
    hbm = pl.BlockSpec(memory_space=pl.ANY)
    shape = jax.ShapeDtypeStruct
    copies = 3 * pairs + 5 + 4 * pairs
    shared = 3 * units + 2 * width
    smem = pl.BlockSpec(memory_space=pltpu.SMEM)
    return pl.pallas_call(
        fwd_kernel,
        grid_spec=pltpu.PrefetchScalarGridSpec(
            num_scalar_prefetch=0,
            grid=(pairs, rows // TILE),
            in_specs=[smem] * 2 + [vmem] * 7 + [hbm] * 3,
            out_specs=[
                pl.BlockSpec((2, TILE, span), lambda a, t: (a, t, 0)),
                pl.BlockSpec((TILE, 128), lambda a, t: (t, a)),
            ]
            + [hbm] * 13,
            scratch_shapes=[
                pltpu.VMEM((2, TILE, span), F32),
                pltpu.VMEM((5, 8, PROMPT), F32),
                pltpu.VMEM((GDEV, 2, CHUNK, width), BF),
                pltpu.VMEM((rows, D), BF),
                pltpu.VMEM((rows, width), BF),
                pltpu.VMEM((conts, width), BF),
                pltpu.VMEM((conts, width), BF),
                pltpu.VMEM((rows, width), BF),
                pltpu.SemaphoreType.DMA((copies,)),
                pltpu.SemaphoreType.DMA((copies,)),
                pltpu.SemaphoreType.DMA((6 + 2 * GDEV,)),
            ],
        ),
        out_shape=[
            shape((2 * pairs, rows, span), BF),
            shape((rows, width), F32),
            shape((rows, width), BF),
            shape((conts, width), BF),
            shape((conts, width), BF),
            shape((PROMPT, width), BF),
            shape((PROMPT, width), BF),
            shape((rows, width), BF),
            shape((rows // 2, width), BF),
            shape((rows // 2, width), BF),
            shape((D, units // 2), BF),
            shape((D, units // 2), BF),
            shape((width // 2, D), BF),
            shape((width // 2, D), BF),
            shape((1, shared), F32),
        ],
        compiler_params=pltpu.CompilerParams(vmem_limit_bytes=56 << 20, collective_id=0, has_side_effects=True),
        cost_estimate=pl.CostEstimate(flops=20 * 10**9, bytes_accessed=60 * 10**6, transcendentals=0),
        name="attend",
    )(starts, gaps, seg, rate, hid, vec, wq, wk, wv, w1, wo, vec)


CHUNKS = 9
IN_FIRST = 5


def reducer_scratch(count, block, cut):
    return [
        pltpu.VMEM((count, 2, 2, 2, block, cut), BF),
        pltpu.VMEM((count, 2, 2, 2, block, cut), BF),
        pltpu.VMEM((count, 2, 2, block, cut), BF),
        pltpu.VMEM((count, 2, 2, block, cut), BF),
        pltpu.VMEM((count, 2, block, cut), BF),
        pltpu.VMEM((count, 2, block, cut), BF),
        pltpu.VMEM((count, block, cut), BF),
        pltpu.SemaphoreType.DMA((4 * count,)),
        pltpu.SemaphoreType.DMA((4 * count,)),
        pltpu.SemaphoreType.DMA((count,)),
    ]


def reducer(packed, device, side, count, top, refs, done):
    held, got0, got1, held1, got2, held2, got3, sems_a, sems_b, sems_l = refs
    bit = [(device // (1 << b)) % 2 for b in range(4)]
    peers = [{"dp": bit_peer(device, b), "tensor": side} for b in range(4)]
    cut = held.shape[-1]

    def either(c, act):
        if isinstance(c, int):
            act(c % 2)
            return
        for odd in range(2):
            @pl.when(c % 2 == odd)
            def _():
                act(odd)

    def passing(c, stage, source, target, peer):
        return pltpu.make_async_remote_copy(
            src_ref=source,
            dst_ref=target,
            send_sem=sems_a.at[4 * c + stage],
            recv_sem=sems_b.at[4 * c + stage],
            device_id=peer,
            device_id_type=MESH,
        )

    def columns_of(c, first):
        at = (first - c) * cut
        return pl.ds(at if isinstance(c, int) else pl.multiple_of(at, 128), cut)

    def own_half(c):
        return pltpu.make_async_copy(packed.at[:, :, :, bit[0], :, columns_of(c, top)], held.at[c], sems_l.at[c])

    def stage0(c):
        return passing(c, 0, packed.at[:, :, :, 1 - bit[0], :, columns_of(c, top)], got0.at[c], peers[0])

    def stage1(c, odd):
        if odd:
            return passing(c, 1, held.at[c, :, 1 - bit[2]], got1.at[c], peers[2])
        return passing(c, 1, held.at[c, :, :, 1 - bit[1]], got1.at[c], peers[1])

    def stage2(c, odd):
        b = 1 if odd else 2
        return passing(c, 2, held1.at[c, :, 1 - bit[b]], got2.at[c], peers[b])

    def stage3(c):
        return passing(c, 3, held2.at[c, 1 - bit[3]], got3.at[c], peers[3])

    def begin(c):
        own_half(c).start()
        stage0(c).start()

    def after0(c):
        own_half(c).wait()
        stage0(c).wait_recv()
        held[c] = held[c] + got0[c]
        either(c, lambda odd: stage1(c, odd).start())

    def after1(c):
        def act(odd):
            stage1(c, odd).wait_recv()
            kept = held[c, :, bit[2]] if odd else held[c, :, :, bit[1]]
            held1[c] = kept + got1[c]
            stage2(c, odd).start()

        either(c, act)

    def after2(c):
        def act(odd):
            stage2(c, odd).wait_recv()
            held2[c] = held1[c, :, bit[1 if odd else 2]] + got2[c]

        either(c, act)
        stage3(c).start()

    def after3(c):
        stage3(c).wait_recv()
        done[:, columns_of(c, count - 1)] = held2[c, bit[3]] + got3[c]

    def settle():
        for c in range(count):
            for copy in (stage0(c), stage1(c, c % 2), stage2(c, c % 2), stage3(c)):
                copy.wait_send()

    return begin, after0, after1, after2, after3, settle


def bwd_kernel(
    fused, q_ref, kp_ref, vp_ref, ko_ref, vo_ref, o_ref, li_ref, e_ref, g_mine, g_theirs, out_half, *refs
):
    packed = refs[0] if fused else None
    refs = refs[1:] if fused else refs
    dq_ref, dko_ref, dvo_ref, sum_k, sum_v, relay_out, out_got = refs[:7]
    done_out, other_out = refs[7:9] if fused else (None, None)
    refs = refs[9:] if fused else refs[7:]
    dk_s, dv_s, g_s, grad_s, near_s, relay_s, far_s, sems_a, sems_b, loc_sems = refs[:10]
    pair = pl.program_id(0)
    step = pl.program_id(1)
    device = lax.axis_index("dp")
    side = lax.axis_index("tensor")
    member = device % GDEV
    rows, width = g_s.shape
    n_pairs = width // 128
    conts = rows - CHUNK
    half_p, half_c = CHUNK // 2, conts // 2
    near = {"dp": bit_peer(device, 0), "tensor": side}
    far = {"dp": bit_peer(device, 1), "tensor": side}
    across = {"dp": device, "tensor": 1 - side}
    lanes = pl.ds(pl.multiple_of(pair * 128, 128), 128)
    mine_p = pl.ds(pl.multiple_of(side * half_p, 128), half_p)
    mine_c = pl.ds(pl.multiple_of(CHUNK + side * half_c, 128), half_c)

    def remote(i, src, dst, peer):
        return pltpu.make_async_remote_copy(
            src_ref=src, dst_ref=dst, send_sem=sems_a.at[i], recv_sem=sems_b.at[i], device_id=peer, device_id_type=MESH
        )

    def heads():
        return [
            remote(0, g_theirs.at[pl.ds(0, half_p), :], g_s.at[mine_p, :], across),
            remote(1, g_theirs.at[pl.ds(half_p, half_c), :], g_s.at[mine_c, :], across),
            remote(2, out_half, out_got, across),
        ]

    def local():
        return [
            pltpu.make_async_copy(g_mine.at[pl.ds(0, half_p), :], g_s.at[mine_p, :], loc_sems.at[0]),
            pltpu.make_async_copy(g_mine.at[pl.ds(half_p, half_c), :], g_s.at[mine_c, :], loc_sems.at[1]),
        ]

    def cores(p):
        part = pl.ds(p * 128, 128)
        return remote(3 + 2 * p, grad_s.at[:, :, 1, :, part], near_s.at[:, :, :, part], near)

    def chips(p):
        part = pl.ds(p * 128, 128)
        return remote(4 + 2 * p, relay_s.at[:, :, part], far_s.at[:, :, part], far)

    if fused:
        *early_refs, done_s, other_a, early_sems = refs[10:]
        begin, after0, after1, after2, after3, settle = reducer(packed, device, side, IN_FIRST, CHUNKS - 1, early_refs, done_s)
        span_e = packed.shape[-1] // CHUNKS
        peers = [{"dp": bit_peer(device, b), "tensor": side} for b in range(4)]
        sent_e = (IN_FIRST - 1) * span_e
        swap = pltpu.make_async_remote_copy(
            src_ref=done_s.at[:, pl.ds(span_e, sent_e)],
            dst_ref=other_a,
            send_sem=early_sems.at[0],
            recv_sem=early_sems.at[1],
            device_id=across,
            device_id_type=MESH,
        )
        tick = pair * pl.num_programs(1) + step

    @pl.when((pair == 0) & (step == 0))
    def _():
        greet([near, far, across] + (peers[2:] if fused else []))
        for copy in heads() + local():
            copy.start()
        for copy in local():
            copy.wait()

    if fused:
        for late, act in ((0, begin), (1, after0), (3, after1), (5, after2), (6, after3)):
            since = tick - late
            @pl.when((since >= 0) & (since % 2 == 0) & (since // 2 < IN_FIRST))
            def _():
                act(since // 2)

        @pl.when(tick == 12)
        def _():
            swap.start()

    @pl.when((pair == 0) & (step == 1 - side))
    def _():
        heads()[0].wait_recv()

    @pl.when((pair == 0) & (step == 3 - side))
    def _():
        heads()[1].wait_recv()

    low = low_half(TILE)
    g = g_s[pl.ds(pl.multiple_of(step * TILE, TILE), TILE), lanes].astype(F32) * li_ref[...]
    prod = g * o_ref[...].astype(F32)
    zf = jnp.zeros((TILE, 128), F32)
    deltas = [
        jnp.sum(jnp.where(low, prod, zf), axis=1, keepdims=True),
        jnp.sum(jnp.where(low, zf, prod), axis=1, keepdims=True),
    ]
    gs = [jnp.where(low, g, zf).astype(BF), jnp.where(low, zf, g).astype(BF)]
    gt = jnp.transpose(g).astype(BF)
    qt = jnp.transpose(q_ref[...].astype(F32)).astype(BF)

    def grads(dq, keys, vals, at, width):
        out, dks, dvs = [], [], []
        for h in range(2):
            e = e_ref[h, :, pl.ds(at, width)]
            dp = dot_nt(gs[h], vals)
            ds = (e.astype(F32) * (dp - deltas[h])).astype(BF)
            out.append(dq[h] + dot_nn(ds, keys))
            dks.append(dot_nn(qt[h * HD : (h + 1) * HD, :], ds))
            dvs.append(dot_nn(gt[h * HD : (h + 1) * HD, :], e))
        return tuple(out), dks, dvs

    @pl.when(step == 0)
    def _():
        dk_s[...] = jnp.zeros_like(dk_s)
        dv_s[...] = jnp.zeros_like(dv_s)

    def add(at, width, dks, dvs):
        for h in range(2):
            dk_s[h * HD : (h + 1) * HD, pl.ds(at, width)] += dks[h]
            dv_s[h * HD : (h + 1) * HD, pl.ds(at, width)] += dvs[h]

    def scaled(dq):
        return (jnp.where(low, dq[0], dq[1]).astype(BF).astype(F32) * 0.125).astype(BF)

    @pl.when(step < PTILES)
    def _():
        def one(j, dq):
            at = pl.multiple_of(xor_bits(j, member) * CHUNK, CHUNK)
            dq, dks, dvs = grads(dq, kp_ref[pl.ds(at, CHUNK), :], vp_ref[pl.ds(at, CHUNK), :], at, CHUNK)
            add(at, CHUNK, dks, dvs)
            return dq

        dq_ref[...] = scaled(lax.fori_loop(0, member + 1, one, (zf, zf)))
        dko_ref[...] = jnp.zeros_like(dko_ref)
        dvo_ref[...] = jnp.zeros_like(dvo_ref)

    @pl.when(step >= PTILES)
    def _():
        dq = (zf, zf)
        for j in range(GDEV):
            span = slice(j * CHUNK, (j + 1) * CHUNK)
            dq, dks, dvs = grads(dq, kp_ref[span, :], vp_ref[span, :], j * CHUNK, CHUNK)
            add(j * CHUNK, CHUNK, dks, dvs)
        dq, dks, dvs = grads(dq, ko_ref[...], vo_ref[...], PROMPT, CONT)
        dq_ref[...] = scaled(dq)
        dko_ref[...] = jnp.transpose(jnp.concatenate(dks, axis=0)).astype(BF)
        dvo_ref[...] = jnp.transpose(jnp.concatenate(dvs, axis=0)).astype(BF)

    end = pl.num_programs(1) - 1

    @pl.when(step == end)
    def _():
        for j in range(GDEV):
            span = slice(j * CHUNK, (j + 1) * CHUNK)
            grad_s[0, j // 2, j % 2, :, lanes] = jnp.transpose(dk_s[:, span]).astype(BF)
            grad_s[1, j // 2, j % 2, :, lanes] = jnp.transpose(dv_s[:, span]).astype(BF)

    for p in range(n_pairs):
        @pl.when((pair == p) & (step == end))
        def _():
            cores(p).start()

        if p + 1 < n_pairs:
            @pl.when((pair == p + 1) & (step == 2))
            def _():
                part = pl.ds(p * 128, 128)
                cores(p).wait_recv()
                relay_s[:, :, part] = (
                    grad_s[:, 1, 0, :, part].astype(F32) + near_s[:, 1, :, part].astype(F32)
                ).astype(BF)
                chips(p).start()

    @pl.when((pair == n_pairs - 1) & (step == end))
    def _():
        last = n_pairs - 1
        sums = (sum_k, sum_v)
        for p in range(last):
            part = pl.ds(p * 128, 128)
            chips(p).wait_recv()
            for i in range(2):
                sums[i][:, part] = (
                    grad_s[i, 0, 0, :, part].astype(F32) + near_s[i, 0, :, part].astype(F32) + far_s[i, :, part].astype(F32)
                ).astype(BF)
        part = pl.ds(last * 128, 128)
        cores(last).wait_recv()
        for i in range(2):
            relay_out[i] = (grad_s[i, 1, 0, :, part].astype(F32) + near_s[i, 1, :, part].astype(F32)).astype(BF)
            sums[i][:, part] = (grad_s[i, 0, 0, :, part].astype(F32) + near_s[i, 0, :, part].astype(F32)).astype(BF)
        if fused:
            swap.wait_recv()
            done_out[...] = done_s[:, pl.ds(0, span_e)]
            other_out[...] = other_a[...]
            settle()
            swap.wait_send()
        heads()[2].wait_recv()
        for copy in heads():
            copy.wait_send()
        for p in range(n_pairs):
            cores(p).wait_send()
            if p < last:
                chips(p).wait_send()


def attend_back(q, k, v, kp, vp, o, li, e, g_mine, g_theirs, out_half, packed):
    rows, width = q.shape
    pairs = width // 128
    span = PROMPT + CONT
    tile = pl.BlockSpec((TILE, 128), lambda a, t: (t, a))
    whole = pl.BlockSpec((PROMPT, 128), lambda a, t: (0, a))
    own = pl.BlockSpec((TILE, 128), lambda a, t: (jnp.maximum(t - PTILES, 0), a))
    vmem = pl.BlockSpec(memory_space=pltpu.VMEM)
    hbm = pl.BlockSpec(memory_space=pl.ANY)
    shape = jax.ShapeDtypeStruct
    copies = 3 + 2 * pairs
    fused = packed is not None
    more_in, more_out, more_scratch = [], [], []
    if fused:
        block, cut = packed.shape[-2], packed.shape[-1] // CHUNKS
        more_in = [packed]
        more_out = [shape((block, cut), BF), shape((block, (IN_FIRST - 1) * cut), BF)]
        more_scratch = reducer_scratch(IN_FIRST, block, cut) + [
            pltpu.VMEM((block, IN_FIRST * cut), BF),
            pltpu.VMEM((block, (IN_FIRST - 1) * cut), BF),
            pltpu.SemaphoreType.DMA((2,)),
        ]
    return pl.pallas_call(
        functools.partial(bwd_kernel, fused),
        grid=(pairs, rows // TILE),
        in_specs=[tile, whole, whole, own, own, tile, tile, pl.BlockSpec((2, TILE, span), lambda a, t: (a, t, 0))]
        + [hbm] * (3 + len(more_in)),
        out_specs=[tile, tile, tile, vmem, vmem, vmem, hbm] + [vmem] * len(more_out),
        out_shape=[
            shape((rows, width), BF),
            shape((rows, width), BF),
            shape((rows, width), BF),
            shape((CHUNK, width), BF),
            shape((CHUNK, width), BF),
            shape((2, CHUNK, 128), BF),
            shape(out_half.shape, BF),
        ]
        + more_out,
        scratch_shapes=[
            pltpu.VMEM((128, PROMPT), F32),
            pltpu.VMEM((128, PROMPT), F32),
            pltpu.VMEM((rows, width), BF),
            pltpu.VMEM((2, 2, 2, CHUNK, width), BF),
            pltpu.VMEM((2, 2, CHUNK, width), BF),
            pltpu.VMEM((2, CHUNK, width), BF),
            pltpu.VMEM((2, CHUNK, width), BF),
            pltpu.SemaphoreType.DMA((copies,)),
            pltpu.SemaphoreType.DMA((copies,)),
            pltpu.SemaphoreType.DMA((2,)),
        ]
        + more_scratch,
        compiler_params=pltpu.CompilerParams(vmem_limit_bytes=60 << 20, collective_id=2, has_side_effects=True),
        cost_estimate=pl.CostEstimate(flops=30 * 10**9, bytes_accessed=60 * 10**6, transcendentals=0),
        name="attend_back",
    )(q, kp, vp, k, v, o, li, e, g_mine, g_theirs, out_half, *more_in)


UCH = 512


def polynomial(x, terms):
    out = jnp.full_like(x, terms[0])
    for term in terms[1:]:
        out = out * x + term
    return out


def error_function(x):
    x = jnp.clip(x, -3.832506856900711, 3.832506856900711)
    square = x * x
    top = polynomial(
        square,
        (0.00022905065861350646, 0.0034082910107109506, 0.050955695062380861, 0.18520832239976145, 1.128379143519084),
    )
    bottom = polynomial(
        square,
        (
            -1.1791602954361697e-7,
            0.000023547966471313185,
            0.0010179625278914885,
            0.014070470171167667,
            0.11098505178285362,
            0.49746925110067538,
            1.0,
        ),
    )
    return x * top / bottom


def gelu_pair(v):
    phi = 0.5 + 0.5 * error_function(v * 0.7071067811865476)
    density = jnp.exp(-0.5 * v * v) * 0.3989422804014327
    return v * phi, phi + v * density


def column_sum(x):
    return jnp.sum(x, axis=0, keepdims=True)


def mid_kernel(
    att_m, att_o, vec_all, vec_got, hid_all, cot_all, w1_own, w1_got, w1_swap, wo_own, wo_got, wo_swap, w2_own,
    out_ref, gatt_m, gatt_o, gmix_ref, packed, su_ref, sw_ref, sd_ref, ext_ref,
    vec_u, vec_w, w1, w2, wo, act_s, shp_s, dg_s, wide_s, acc_s, gmid_s, sub_s, mid_s, low_s, midt_s, cott_s, stage, hid, cot, sems, out_sems, send_sems, recv_sems,
):
    device = lax.axis_index("dp")
    side = lax.axis_index("tensor")
    core = device % 2
    near = {"dp": bit_peer(device, 0), "tensor": side}
    across = {"dp": device, "tensor": 1 - side}
    units = w1_own.shape[1]
    width = wo_own.shape[0]
    rows = hid.shape[0]
    full = 2 * units
    half = units // 2
    half_w = width // 2
    here_u = pl.multiple_of(units + core * half, 128)
    there_u = pl.multiple_of(units + (1 - core) * half, 128)
    here_w = pl.multiple_of(width + core * half_w, 64)
    there_w = pl.multiple_of(width + (1 - core) * half_w, 64)
    prompt, conts = CHUNK // 2, (hid_all.shape[0] - CHUNK) // 2
    own_p = pl.ds(pl.multiple_of(side * prompt, 128), prompt)
    own_c = pl.ds(pl.multiple_of(CHUNK + side * conts, 128), conts)
    at_own = 2 * D + 2 * width
    vec_own = vec_all.at[:, pl.ds(at_own, 3 * units + 2 * width)]
    vec_d = vec_all.at[:, pl.ds(at_own + 3 * units + 2 * width, 4 * D)]
    rows_in = []
    for i, (all_rows, held) in enumerate(((hid_all, hid), (cot_all, cot))):
        for j, (span, at, size) in enumerate(((own_p, 0, prompt), (own_c, prompt, conts))):
            copy = pltpu.make_async_copy(all_rows.at[span, :], held.at[pl.ds(at, size), :], sems.at[7 + 2 * i + j])
            copy.start()
            rows_in.append(copy)
    loads = []
    for i, (src, dst) in enumerate(
        [
            (wo_own, wo.at[pl.ds(0, width), :]),
            (wo_got, wo.at[pl.ds(here_w, half_w), :]),
            (wo_swap, wo.at[pl.ds(there_w, half_w), :]),
            (w1_own, w1.at[:, pl.ds(0, units)]),
            (w1_got, w1.at[:, pl.ds(here_u, half)]),
            (w1_swap, w1.at[:, pl.ds(there_u, half)]),
            (w2_own, w2.at[pl.ds(0, units), :]),
        ]
    ):
        copy = pltpu.make_async_copy(src, dst, sems.at[i])
        copy.start()
        loads.append(copy)

    piece = half // 2
    greet([near, across])

    def remote(i, src, dst, peer):
        return pltpu.make_async_remote_copy(
            src_ref=src, dst_ref=dst, send_sem=send_sems.at[i], recv_sem=recv_sems.at[i], device_id=peer, device_id_type=MESH
        )

    over, passed = [], []
    for i in range(2):
        from_own = pl.ds(pl.multiple_of(core * half + i * piece, 128), piece)
        landed = w2.at[pl.ds(pl.multiple_of(units + core * half + i * piece, 128), piece), :]
        over.append(remote(i, w2_own.at[from_own, :], landed, across))
        passed.append(remote(2 + i, landed, landed, near))
        over[i].start()

    for i in range(3):
        for j, vec in enumerate((vec_own, vec_got)):
            vec_u[i : i + 1, pl.ds(j * units, units)] = vec[0:1, pl.ds(i * units, units)]
    for i in range(2):
        for j, vec in enumerate((vec_own, vec_got)):
            vec_w[i : i + 1, pl.ds(j * width, width)] = vec[0:1, pl.ds(3 * units + i * width, width)]

    a0 = att_m[...].astype(F32)
    a1 = att_o[...].astype(F32)
    center = (jnp.sum(a0, axis=1, keepdims=True) + jnp.sum(a1, axis=1, keepdims=True)) * (1.0 / D)
    square = (jnp.sum(a0 * a0, axis=1, keepdims=True) + jnp.sum(a1 * a1, axis=1, keepdims=True)) * (1.0 / D)
    sub_scale = lax.rsqrt(square - center * center + EPSILON)
    sub_s[:, 0:width] = (a0 - center) * sub_scale
    sub_s[:, width : 2 * width] = (a1 - center) * sub_scale
    sub_gain = vec_w[0:1, :]
    low_s[...] = (sub_s[...] * sub_gain + vec_w[1:2, :]).astype(BF)
    for copy in loads[0:3] + rows_in:
        copy.wait()
    mixed = hid[...].astype(F32) + (dot_nn(low_s[...], wo[...]) + vec_d[0:1, pl.ds(0, D)])
    wide_s[...] = mixed
    mean = jnp.mean(mixed, axis=1, keepdims=True)
    mid_scale = lax.rsqrt(jnp.mean(mixed * mixed, axis=1, keepdims=True) - mean * mean + EPSILON)
    mid_s[...] = (mixed - mean) * mid_scale
    mid_gain = vec_d[0:1, pl.ds(768, D)]
    mid_full = mid_s[...] * mid_gain + vec_d[0:1, pl.ds(1536, D)]
    mid_low = mid_full.astype(BF)
    midt_s[...] = jnp.transpose(mid_full).astype(BF)
    cot_full = cot[...].astype(F32)
    cott_s[...] = jnp.transpose(cot_full).astype(BF)
    sd_ref[...] = jnp.zeros_like(sd_ref)
    sd_ref[3:4, :] = column_sum(cot_full)
    for copy in loads[3:6]:
        copy.wait()

    def lanes_sum(x):
        total = x[:, 0:128]
        for i in range(1, x.shape[1] // 128):
            total = total + x[:, i * 128 : (i + 1) * 128]
        return total

    def first(c, carry):
        at = pl.multiple_of(c * UCH, UCH)
        inner = dot_nn(mid_low, w1[:, pl.ds(at, UCH)]) + vec_u[2:3, pl.ds(at, UCH)]
        act, slope = gelu_pair(inner)
        act_s[:, pl.ds(at, UCH)] = act
        dg_s[:, pl.ds(at, UCH)] = slope.astype(BF)
        return carry[0] + lanes_sum(act), carry[1] + lanes_sum(act * act)

    zero = jnp.zeros((rows, 128), F32)
    act_sum, act_square = lax.fori_loop(0, full // UCH, first, (zero, zero))
    ffn_center = jnp.sum(act_sum, axis=1, keepdims=True) * (1.0 / full)
    ffn_scale = lax.rsqrt(
        jnp.sum(act_square, axis=1, keepdims=True) * (1.0 / full) - ffn_center * ffn_center + EPSILON
    )
    loads[6].wait()
    over[0].wait_recv()
    passed[0].start()
    acc_s[...] = jnp.zeros_like(acc_s)
    per = units // UCH
    wide = 2 * units + width

    def column_of(c, extra):
        return pl.multiple_of((c // per) * wide + lax.rem(c, per) * UCH + extra, 128)

    def send(slot, column):
        return pltpu.make_async_copy(stage.at[slot], packed.at[:, pl.ds(column, UCH)], out_sems.at[slot])

    def put(c, value, extra):
        slot = lax.rem(c, 2)

        @pl.when(c >= 2)
        def _():
            send(slot, column_of(c - 2, extra)).wait()

        stage[slot] = value
        send(slot, column_of(c, extra)).start()

    def drain(extra):
        for c in range(full // UCH - 2, full // UCH):
            send(c % 2, column_of(c, extra)).wait()

    def second(c, carry):
        at = pl.multiple_of(c * UCH, UCH)
        unit = (act_s[:, pl.ds(at, UCH)] - ffn_center) * ffn_scale
        act_s[:, pl.ds(at, UCH)] = unit
        gain = vec_u[0:1, pl.ds(at, UCH)]
        low = (unit * gain + vec_u[1:2, pl.ds(at, UCH)]).astype(BF)
        acc_s[...] += dot_nn(low, w2[pl.ds(at, UCH), :])
        grad = dot_nt(cot[...], w2[pl.ds(at, UCH), :])
        cross = grad * unit
        su_ref[0:1, pl.ds(at, UCH)] = column_sum(cross)
        su_ref[1:2, pl.ds(at, UCH)] = column_sum(grad)
        shaped = grad * gain
        shp_s[:, pl.ds(at, UCH)] = shaped
        put(c, dot_nn(cott_s[...], low).astype(BF), units)
        return carry[0] + lanes_sum(shaped), carry[1] + lanes_sum(shaped * unit)

    su_ref[...] = jnp.zeros_like(su_ref)
    sums = lax.fori_loop(0, per, second, (zero, zero))
    over[1].wait_recv()
    passed[1].start()
    for copy in passed:
        copy.wait_recv()
    s_sum, s_cross = lax.fori_loop(per, 2 * per, second, sums)
    drain(units)
    shaped_mean = jnp.sum(s_sum, axis=1, keepdims=True) * (1.0 / full)
    cross_mean = jnp.sum(s_cross, axis=1, keepdims=True) * (1.0 / full)
    out_ref[...] = (wide_s[...] + (acc_s[...] + vec_d[0:1, pl.ds(2304, D)])).astype(BF)
    gmid_s[...] = jnp.zeros_like(gmid_s)

    def third(c, carry):
        at = pl.multiple_of(c * UCH, UCH)
        g = ffn_scale * (shp_s[:, pl.ds(at, UCH)] - shaped_mean - act_s[:, pl.ds(at, UCH)] * cross_mean)
        low = (g * dg_s[:, pl.ds(at, UCH)].astype(F32)).astype(BF)
        su_ref[2:3, pl.ds(at, UCH)] = column_sum(low.astype(F32))
        gmid_s[...] += dot_nt(low, w1[:, pl.ds(at, UCH)])
        put(c, dot_nn(midt_s[...], low).astype(BF), 0)
        return carry

    lax.fori_loop(0, full // UCH, third, 0)
    drain(0)

    grad_mid = gmid_s[...]
    unit = mid_s[...]
    sd_ref[1:2, :] = column_sum(grad_mid * unit)
    sd_ref[2:3, :] = column_sum(grad_mid)
    shaped = grad_mid * mid_gain
    grad_mixed = cot[...].astype(F32) + mid_scale * (
        shaped - jnp.mean(shaped, axis=1, keepdims=True) - unit * jnp.mean(shaped * unit, axis=1, keepdims=True)
    )
    branch = grad_mixed.astype(BF)
    gmix_ref[...] = branch
    branch_f = branch.astype(F32)
    sd_ref[0:1, :] = column_sum(branch_f)
    out_grad = dot_nn(jnp.transpose(branch_f).astype(BF), low_s[...]).astype(BF)
    stage[0, :, 0:width] = out_grad[:, 0:width]
    stage[1, :, 0:width] = out_grad[:, width : 2 * width]
    last = [
        pltpu.make_async_copy(stage.at[i, :, pl.ds(0, width)], packed.at[:, pl.ds(i * wide + 2 * units, width)], out_sems.at[i])
        for i in range(2)
    ]
    for copy in last:
        copy.start()
    grad_sub = dot_nt(branch, wo[...])
    unit = sub_s[...]
    cross = grad_sub * unit
    sw_ref[...] = jnp.zeros_like(sw_ref)
    sw_ref[0:1, :] = column_sum(cross)
    sw_ref[1:2, :] = column_sum(grad_sub)
    shaped = grad_sub * sub_gain
    grad_att = sub_scale * (
        shaped - jnp.mean(shaped, axis=1, keepdims=True) - unit * jnp.mean(shaped * unit, axis=1, keepdims=True)
    )
    gatt_m[...] = grad_att[:, 0:width].astype(BF)
    gatt_o[...] = grad_att[:, width : 2 * width].astype(BF)
    parts = ext_ref.shape[0]
    if parts > 1:
        sums_u, sums_w, sums_d = su_ref[...], sw_ref[...], sd_ref[...]
        for i in range(parts):
            ext_ref[i] = jnp.concatenate(
                [
                    window(sums_u, i * (units // parts)),
                    window(sums_u, units + i * (units // parts)),
                    window(sums_w, i * (width // parts)),
                    window(sums_w, width + i * (width // parts)),
                    window(sums_d, i * (D // parts)),
                    jnp.zeros((8, 128), F32),
                ],
                axis=0,
            ).astype(BF)
    for copy in last:
        copy.wait()
    for copy in over + passed:
        copy.wait_send()


def window(rows8, start):
    base = start // 128 * 128
    size = min(256, rows8.shape[1] - base)
    view = rows8[:, base : base + size]
    shift = start - base
    if shift:
        view = pltpu.roll(view, size - shift, 1)
    return view[:, 0:128]


def middle(att_m, att_o, hid, cot, vec_all, vec_got, w1, w2, wo, parts):
    rows = att_m.shape[0]
    units = w2.shape[0]
    width = wo[0].shape[0]
    vmem = pl.BlockSpec(memory_space=pltpu.VMEM)
    hbm = pl.BlockSpec(memory_space=pl.ANY)
    shape = jax.ShapeDtypeStruct
    return pl.pallas_call(
        mid_kernel,
        in_specs=[vmem] * 4 + [hbm] * 9,
        out_specs=[vmem] * 4 + [hbm] + [vmem] * 4,
        out_shape=[
            shape((rows, D), BF),
            shape((rows, width), BF),
            shape((rows, width), BF),
            shape((rows, D), BF),
            shape((D, 2 * (2 * units + width)), BF),
            shape((8, 2 * units), F32),
            shape((8, 2 * width), F32),
            shape((8, D), F32),
            shape((parts, 48, 128), BF),
        ],
        scratch_shapes=[
            pltpu.VMEM((8, 2 * units), F32),
            pltpu.VMEM((8, 2 * width), F32),
            pltpu.VMEM((D, 2 * units), BF),
            pltpu.VMEM((2 * units, D), BF),
            pltpu.VMEM((2 * width, D), BF),
            pltpu.VMEM((rows, 2 * units), F32),
            pltpu.VMEM((rows, 2 * units), F32),
            pltpu.VMEM((rows, 2 * units), BF),
            pltpu.VMEM((rows, D), F32),
            pltpu.VMEM((rows, D), F32),
            pltpu.VMEM((rows, D), F32),
            pltpu.VMEM((rows, 2 * width), F32),
            pltpu.VMEM((rows, D), F32),
            pltpu.VMEM((rows, 2 * width), BF),
            pltpu.VMEM((D, rows), BF),
            pltpu.VMEM((D, rows), BF),
            pltpu.VMEM((2, D, UCH), BF),
            pltpu.VMEM((rows, D), BF),
            pltpu.VMEM((rows, D), BF),
            pltpu.SemaphoreType.DMA((11,)),
            pltpu.SemaphoreType.DMA((2,)),
            pltpu.SemaphoreType.DMA((4,)),
            pltpu.SemaphoreType.DMA((4,)),
        ],
        compiler_params=pltpu.CompilerParams(vmem_limit_bytes=62 << 20, collective_id=3, has_side_effects=True),
        cost_estimate=pl.CostEstimate(flops=21 * 10**9, bytes_accessed=30 * 10**6, transcendentals=0),
        name="middle",
    )(att_m, att_o, vec_all, vec_got, hid, cot, *w1, *wo, w2)


def final_kernel(
    bits, hid, vec_all, dq, dk, dv, wq, wk, wv, gmix, ext, sum_k, sum_v, relay, first_done, first_other, packed,
    gin, late_out, vec_out, early_out,
    loc_s, far_s, unit_s, mine_s, norm_s, send_c, recv_c, send_p, recv_p, give_c, give_p, late_s, small_s,
    vec_s, vec_r, done_s, other_b, sems_a, sems_b, loc_sems, *stage_refs,
):
    device = lax.axis_index("dp")
    side = lax.axis_index("tensor")
    across = {"dp": device, "tensor": 1 - side}
    peers = [{"dp": bit_peer(device, b), "tensor": side} for b in range(bits)]
    rows, width = dq.shape
    prompt = sum_k.shape[0]
    conts = rows - prompt
    half_p, half_c = prompt // 2, conts // 2
    own_p = pl.multiple_of(side * half_p, 128)
    their_p = pl.multiple_of((1 - side) * half_p, 128)
    own_c = pl.multiple_of(prompt + side * half_c, 128)
    their_c = pl.multiple_of(prompt + (1 - side) * half_c, 128)
    lanes = 3 * width + 128

    greet(peers + [across])
    count = [0]

    def remote(src, dst, peer):
        i = count[0]
        count[0] += 1
        copy = pltpu.make_async_remote_copy(
            src_ref=src, dst_ref=dst, send_sem=sems_a.at[i], recv_sem=sems_b.at[i], device_id=peer, device_id_type=MESH
        )
        copy.start()
        return copy

    share = remote(relay, far_s, peers[1])

    in_last = CHUNKS - IN_FIRST
    begin, after0, after1, after2, after3, settle = reducer(packed, device, side, in_last, in_last - 1, stage_refs[-10:], done_s)
    cut = packed.shape[-1] // CHUNKS
    half_cut = cut // 2
    swap_e = remote(first_done.at[:, pl.ds(half_cut, half_cut)], other_b, across)

    def each(act):
        for c in range(in_last):
            act(c)

    each(begin)

    gain_f = vec_all[:, pl.ds(0, D)]
    bias_f = vec_all[:, pl.ds(D, D)]

    def unit_rows(at, size):
        x = hid[pl.ds(at, size), :].astype(F32)
        center = jnp.mean(x, axis=1, keepdims=True)
        scale = lax.rsqrt(jnp.mean(x * x, axis=1, keepdims=True) - center * center + EPSILON)
        return (x - center) * scale, scale

    def part_of(at, size, k_rows, v_rows):
        return dot_nt(dq[pl.ds(at, size), :], wq[...]) + dot_nt(k_rows, wk[...]) + dot_nt(v_rows, wv[...])

    def gather(part, unit):
        return column_sum(part * unit), column_sum(part)

    def normed_rows(at, size, unit):
        norm_s[:, pl.ds(at, size)] = jnp.transpose(unit * gain_f + bias_f).astype(BF)

    part = part_of(their_c, half_c, dk[pl.ds(their_c, half_c), :], dv[pl.ds(their_c, half_c), :])
    send_c[...] = part.astype(BF)
    y_cont = remote(send_c, recv_c, across)
    unit, _ = unit_rows(their_c, half_c)
    gain_grad, bias_grad = gather(part, unit)
    normed_rows(their_c, half_c, unit)
    unit, scale_c = unit_rows(own_c, half_c)
    part = part_of(own_c, half_c, dk[pl.ds(own_c, half_c), :], dv[pl.ds(own_c, half_c), :])
    mine_s[pl.ds(half_p, half_c), :] = part
    unit_s[pl.ds(half_p, half_c), :] = unit
    g, b = gather(part, unit)
    gain_grad, bias_grad = gain_grad + g, bias_grad + b
    normed_rows(own_c, half_c, unit)

    each(after0)
    share.wait_recv()
    for i, total in enumerate((sum_k, sum_v)):
        loc_s[i, :, pl.ds(0, width - 128)] = total[:, pl.ds(0, width - 128)]
        loc_s[i, :, pl.ds(width - 128, 128)] = (
            total[:, pl.ds(width - 128, 128)].astype(F32) + far_s[i].astype(F32)
        ).astype(BF)
    part = part_of(their_p, half_p, loc_s[0, pl.ds(their_p, half_p), :], loc_s[1, pl.ds(their_p, half_p), :])
    send_p[...] = part.astype(BF)
    y_prompt = remote(send_p, recv_p, across)
    unit, _ = unit_rows(their_p, half_p)
    normed_rows(their_p, half_p, unit)
    g, b = gather(part, unit)
    gain_grad, bias_grad = gain_grad + g, bias_grad + b
    unit, scale_p = unit_rows(own_p, half_p)
    unit_s[pl.ds(0, half_p), :] = unit
    normed_rows(own_p, half_p, unit)
    part = part_of(own_p, half_p, loc_s[0, pl.ds(own_p, half_p), :], loc_s[1, pl.ds(own_p, half_p), :])
    mine_s[pl.ds(0, half_p), :] = part
    g, b = gather(part, unit)
    gain_grad, bias_grad = gain_grad + g, bias_grad + b

    blocks = 1 << bits
    block = D // blocks

    def keep(value, lane):
        low = value.astype(BF)
        for i in range(blocks):
            late_s[i // 2, i % 2, :, pl.ds(lane, width)] = low[i * block : (i + 1) * block, :]

    keep(dot_nn(norm_s[...], dq[...]), 0)
    q_bias = column_sum(dq[...].astype(F32))
    for i, rest in enumerate((dk, dv)):
        keep(
            dot_nn(norm_s[:, pl.ds(0, prompt)], loc_s[i])
            + dot_nn(norm_s[:, pl.ds(prompt, conts)], rest[pl.ds(prompt, conts), :]),
            (i + 1) * width,
        )
    v_bias = column_sum(loc_s[1].astype(F32)) + column_sum(dv[pl.ds(prompt, conts), :].astype(F32))

    def norm_back(total, unit, scale, mixed):
        shaped = total * gain_f
        return mixed.astype(F32) + scale * (
            shaped - jnp.mean(shaped, axis=1, keepdims=True) - unit * jnp.mean(shaped * unit, axis=1, keepdims=True)
        )

    small_s[...] = jnp.zeros_like(small_s)
    small_s[0:1, pl.ds(0, width)] = q_bias
    small_s[1:2, pl.ds(0, width)] = v_bias
    small_s[2:3, pl.ds(0, D)] = gain_grad
    small_s[3:4, pl.ds(0, D)] = bias_grad
    small = small_s[...]
    row_id = lax.broadcasted_iota(jnp.int32, (8, 128), 0)
    for i in range(blocks):
        narrow = window(small, i * (width // blocks))
        broad = window(small, i * block)
        tail = jnp.concatenate([ext[i, pl.ds(32, 16), :].astype(F32)[0:8], jnp.where(row_id < 2, narrow, broad)], axis=0)
        late_s[i // 2, i % 2, pl.ds(0, 32), pl.ds(3 * width, 128)] = ext[i, pl.ds(0, 32), :]
        late_s[i // 2, i % 2, pl.ds(32, 16), pl.ds(3 * width, 128)] = tail.astype(BF)

    def input_rows(arrived, at, size, scale, held, rows_at, sem):
        arrived[0].wait_recv()
        here = pl.ds(at, size)
        total = mine_s[here, :] + arrived[1][...].astype(F32)
        held[...] = norm_back(total, unit_s[here, :], scale, gmix[here, :]).astype(BF)
        back = remote(held, gin.at[pl.ds(rows_at, size), :], across)
        kept = pltpu.make_async_copy(held, gin.at[pl.ds(rows_at, size), :], loc_sems.at[sem])
        kept.start()
        return back, kept

    source = late_s
    stages = []
    for bit in range(bits):
        landing, kept = stage_refs[2 * bit], stage_refs[2 * bit + 1]
        mine = (device // (1 << bit)) % 2
        copy = remote(source.at[:, 1 - mine], landing, peers[bit])
        if bit == 0:
            back_c, keep_c = input_rows((y_cont, recv_c), half_p, half_c, scale_c, give_c, own_c, 0)
        if bit == 1:
            each(after1)
            back_p, keep_p = input_rows((y_prompt, recv_p), 0, half_p, scale_p, give_p, own_p, 1)
        if bit == 2:
            each(after2)
        if bit == 3:
            each(after3)
        copy.wait_recv()
        stages.append(copy)
        for i in range(landing.shape[0]):
            kept[i // 2, i % 2] = (source[i, mine].astype(F32) + landing[i].astype(F32)).astype(BF)
        source = kept
    late_out[...] = source[0, 0, :, pl.ds(0, 3 * width)].astype(F32)
    vec_s[...] = source[0, 0, :, pl.ds(3 * width, 128)]
    swap = remote(vec_s, vec_r, across)
    swap_e.wait_recv()
    last_e = in_last * cut
    early_out[:, pl.ds(0, half_cut)] = done_s[:, pl.ds(0, half_cut)].astype(F32) + other_b[...].astype(F32)
    early_out[:, pl.ds(half_cut, last_e - half_cut)] = done_s[:, pl.ds(half_cut, last_e - half_cut)].astype(
        F32
    ) + first_other[:, pl.ds(0, last_e - half_cut)].astype(F32)
    early_out[:, pl.ds(last_e, half_cut)] = first_done[:, pl.ds(0, half_cut)].astype(F32) + first_other[
        :, pl.ds(last_e - half_cut, half_cut)
    ].astype(F32)
    settle()
    swap.wait_recv()
    vec_out[0] = vec_s[...].astype(F32)
    vec_out[1] = vec_r[...].astype(F32)
    for copy in stages + [share, swap_e, y_cont, y_prompt, swap]:
        copy.wait_send()
    for copy in (back_c, back_p):
        copy.wait_recv()
        copy.wait_send()
    keep_c.wait()
    keep_p.wait()


def finish(hid, vec_all, dq, dk, dv, wq, wk, wv, gmix, ext, sum_k, sum_v, relay, first_done, first_other, packed):
    rows, width = dq.shape
    ranks = lax.axis_size("dp")
    bits = ranks.bit_length() - 1
    block = D // ranks
    prompt = sum_k.shape[0]
    conts = rows - prompt
    lanes = 3 * width + 128
    vmem = pl.BlockSpec(memory_space=pltpu.VMEM)
    hbm = pl.BlockSpec(memory_space=pl.ANY)
    shape = jax.ShapeDtypeStruct
    copies = 7 + bits
    cut = packed.shape[-1] // CHUNKS
    stages = []
    for bit in range(bits):
        left = ranks >> (bit + 1)
        stages.append(pltpu.VMEM((left, block, lanes), BF))
        stages.append(pltpu.VMEM((max(left // 2, 1), min(left, 2), block, lanes), BF))
    return pl.pallas_call(
        functools.partial(final_kernel, bits),
        in_specs=[vmem] * 15 + [hbm],
        out_specs=[hbm, vmem, vmem, vmem],
        out_shape=[shape((rows, D), BF), shape((block, 3 * width), F32), shape((2, block, 128), F32), shape((block, packed.shape[-1] // 2), F32)],
        scratch_shapes=[
            pltpu.VMEM((2, prompt, width), BF),
            pltpu.VMEM((2, prompt, 128), BF),
            pltpu.VMEM((rows // 2, D), F32),
            pltpu.VMEM((rows // 2, D), F32),
            pltpu.VMEM((D, rows), BF),
            pltpu.VMEM((conts // 2, D), BF),
            pltpu.VMEM((conts // 2, D), BF),
            pltpu.VMEM((prompt // 2, D), BF),
            pltpu.VMEM((prompt // 2, D), BF),
            pltpu.VMEM((conts // 2, D), BF),
            pltpu.VMEM((prompt // 2, D), BF),
            pltpu.VMEM((ranks // 2, 2, block, lanes), BF),
            pltpu.VMEM((8, D + 128), F32),
            pltpu.VMEM((block, 128), BF),
            pltpu.VMEM((block, 128), BF),
            pltpu.VMEM((block, (CHUNKS - IN_FIRST) * cut), BF),
            pltpu.VMEM((block, cut // 2), BF),
            pltpu.SemaphoreType.DMA((copies,)),
            pltpu.SemaphoreType.DMA((copies,)),
            pltpu.SemaphoreType.DMA((2,)),
        ]
        + stages
        + reducer_scratch(CHUNKS - IN_FIRST, block, cut),
        compiler_params=pltpu.CompilerParams(vmem_limit_bytes=56 << 20, collective_id=1, has_side_effects=True),
        cost_estimate=pl.CostEstimate(flops=5 * 10**9, bytes_accessed=20 * 10**6, transcendentals=0),
        name="finish",
    )(hid, vec_all, dq, dk, dv, wq, wk, wv, gmix, ext, sum_k, sum_v, relay, first_done, first_other, packed)


def flip(value, axis, bit):
    return lax.ppermute(value, axis, [(i, i ^ (1 << bit)) for i in range(lax.axis_size(axis))])


def contract_rows(left, right):
    return lax.dot_general(left, right, (((0,), (0,)), ((), ())), preferred_element_type=F32)


def back_project(left, right):
    return lax.dot_general(left, right, (((1,), (1,)), ((), ())), preferred_element_type=F32)


def norm_rows(values, gain, bias):
    center = jnp.mean(values, axis=-1, keepdims=True)
    spread = jnp.mean(values * values, axis=-1, keepdims=True) - center * center
    scaled = lax.rsqrt(spread + EPSILON)
    unit_rows = (values - center) * scaled
    return (unit_rows * gain + bias, unit_rows, scaled)


def norm_back(grad_rows, gain, unit_rows, scaled):
    shaped = grad_rows * gain
    return scaled * (
        shaped
        - jnp.mean(shaped, axis=-1, keepdims=True)
        - unit_rows * jnp.mean(shaped * unit_rows, axis=-1, keepdims=True)
    )


def in_order(which, mine, other, axis):
    return jnp.where(
        which == 0,
        jnp.concatenate([mine, other], axis=axis),
        jnp.concatenate([other, mine], axis=axis),
    )


def halving(value, device):
    bits = lax.axis_size("dp").bit_length() - 1
    rows, columns = value.shape
    current = value
    for bit in range(bits):
        upper = device // (1 << bit) % 2
        left = bits - bit
        view = current.reshape((1 << (left - 1), 2, -1, columns))
        kept = lax.dynamic_index_in_dim(view, upper, 1, keepdims=False)
        sent = lax.dynamic_index_in_dim(view, 1 - upper, 1, keepdims=False)
        got = flip(sent, "dp", bit)
        current = (kept.astype(F32) + got.astype(F32)).astype(BF)
    return current.reshape(rows >> bits, columns)


def side_by_side(parts):
    total = sum(part.shape[0] for part in parts)
    row, at = jnp.zeros((1, total), F32), 0
    for part in parts:
        size = part.shape[0]
        row = row + jnp.pad(part.astype(F32)[None], ((0, 0), (at, total - at - size)))
        at += size
    return row


def half_of(value, which):
    prompt, conts = CHUNK // 2, (value.shape[0] - CHUNK) // 2
    return jnp.concatenate(
        [
            lax.dynamic_slice_in_dim(value, which * prompt, prompt),
            lax.dynamic_slice_in_dim(value, CHUNK + which * conts, conts),
        ]
    )


def joined(which, mine, other):
    prompt = CHUNK // 2
    low = jnp.where(which == 0, mine, other)
    high = jnp.where(which == 0, other, mine)
    return jnp.concatenate([low[:prompt], high[:prompt], low[prompt:], high[prompt:]])


def body(
    hidden_in,
    cotangent,
    prompt_start,
    cont_gap,
    seg_len,
    dilation_rate,
    pre_gain,
    pre_bias,
    query_weight,
    query_bias,
    key_weight,
    value_weight,
    value_bias,
    sub_gain,
    sub_bias,
    out_weight,
    out_bias,
    mid_gain,
    mid_bias,
    inner_weight,
    inner_bias,
    ffn_gain,
    ffn_bias,
    outer_weight,
    outer_bias,
):
    device = lax.axis_index("dp")
    ranks = lax.axis_size("dp")
    group_id = device // GDEV
    member = device % GDEV
    tensor_id = lax.axis_index("tensor")
    core = device % 2
    width = query_weight.shape[1]
    units = inner_weight.shape[1]
    pairs = width // 128
    rows = hidden_in.shape[0]
    prompt_rows = CHUNK
    cont_count = (rows - prompt_rows) // CONT

    vectors = side_by_side(
        [
            pre_gain,
            pre_bias,
            query_bias,
            value_bias,
            ffn_gain,
            ffn_bias,
            inner_bias,
            sub_gain,
            sub_bias,
            out_bias,
            mid_gain,
            mid_bias,
            outer_bias,
        ]
    )
    pre_gain_f = pre_gain.astype(F32)

    (
        weighed,
        inverse,
        queries,
        keys,
        values,
        prompt_keys,
        prompt_values,
        attended,
        att_mine,
        att_got,
        *pieces,
        vectors_other,
    ) = attend(
        prompt_start,
        cont_gap,
        seg_len,
        dilation_rate,
        hidden_in,
        vectors,
        query_weight,
        key_weight,
        value_weight,
        inner_weight,
        out_weight,
    )
    inner_parts = (inner_weight, pieces[0], pieces[1])
    out_parts = (out_weight, pieces[2], pieces[3])

    fused = ranks == 16
    out_half, grad_mine, grad_theirs, grad_mixed_low, packed, sum_u, sum_w, sum_d, ext = middle(
        att_mine,
        att_got,
        hidden_in,
        cotangent,
        vectors,
        vectors_other,
        inner_parts,
        outer_weight,
        out_parts,
        ranks if fused else 1,
    )

    grad_query_in, own_key_grad, own_value_grad, key_sum, value_sum, relay, out_got, *early = attend_back(
        queries,
        keys,
        values,
        prompt_keys,
        prompt_values,
        attended,
        inverse,
        weighed,
        grad_mine,
        grad_theirs,
        out_half,
        packed.reshape(2, 2, 2, 2, D // ranks, -1) if fused else None,
    )
    if not fused:
        early = lax.psum_scatter(packed, "dp", scatter_dimension=0, tiled=True)
        early_mine, early_other = jnp.split(early, 2, axis=1)
        early_sum = early_mine.astype(F32) + flip(early_other, "tensor", 0).astype(F32)
    output = joined(tensor_id, out_half, out_got)
    block = D // ranks
    per_u, per_w, per_d = units // ranks, width // ranks, D // ranks
    if fused:
        input_low, late, vec, early_sum = finish(
            hidden_in,
            vectors,
            grad_query_in,
            own_key_grad,
            own_value_grad,
            query_weight,
            key_weight,
            value_weight,
            grad_mixed_low,
            ext,
            key_sum,
            value_sum,
            relay,
            *early,
            packed.reshape(2, 2, 2, 2, D // ranks, -1),
        )
        ffn_gain_grad, ffn_bias_grad, inner_bias_grad = [vec[0, i, :per_u] + vec[1, 8 + i, :per_u] for i in range(3)]
        sub_gain_grad, sub_bias_grad = [vec[0, 16 + i, :per_w] + vec[1, 24 + i, :per_w] for i in range(2)]
        out_bias_grad, mid_gain_grad, mid_bias_grad, outer_bias_grad = [
            vec[0, 32 + i, :per_d] + vec[1, 32 + i, :per_d] for i in range(4)
        ]
        query_bias_grad, value_bias_grad = [vec[0, 40 + i, :per_w] for i in range(2)]
        pre_gain_grad, pre_bias_grad = [vec[0, 42 + i, :per_d] + vec[1, 42 + i, :per_d] for i in range(2)]
    else:
        pre_normed, pre_unit, pre_scale = norm_rows(hidden_in.astype(F32), pre_gain_f, pre_bias.astype(F32))
        pre_low = pre_normed.astype(BF)
        last = width - 128
        far = flip(relay, "dp", 1).astype(F32)
        summed = jnp.stack([key_sum, value_sum]).astype(F32)
        summed = jnp.concatenate([summed[:, :, :last], summed[:, :, last:] + far], axis=2).astype(BF)
        grad_keys = jnp.concatenate([summed[0], own_key_grad[prompt_rows:]], axis=0)
        grad_values = jnp.concatenate([summed[1], own_value_grad[prompt_rows:]], axis=0)

        query_weight_grad = contract_rows(pre_low, grad_query_in)
        key_weight_grad = contract_rows(pre_low, grad_keys)
        value_weight_grad = contract_rows(pre_low, grad_values)
        query_bias_grad = jnp.sum(grad_query_in.astype(F32), axis=0)
        value_bias_grad = jnp.sum(grad_values.astype(F32), axis=0)
        grad_normed_part = (
            back_project(grad_query_in, query_weight)
            + back_project(grad_keys, key_weight)
            + back_project(grad_values, value_weight)
        )
        grad_normed_low = grad_normed_part.astype(BF)
        grad_normed = grad_normed_low.astype(F32) + flip(grad_normed_low, "tensor", 0).astype(F32)
        pre_gain_grad = jnp.sum(grad_normed * pre_unit, axis=0)
        pre_bias_grad = jnp.sum(grad_normed, axis=0)
        grad_mixed_all = joined(tensor_id, grad_mixed_low, flip(grad_mixed_low, "tensor", 0)).astype(F32)
        input_low = (grad_mixed_all + norm_back(grad_normed, pre_gain_f, pre_unit, pre_scale)).astype(BF)

        vec = jnp.concatenate(
            [
                sum_u[:3].reshape(3, 2, ranks, per_u).transpose(2, 1, 0, 3).reshape(ranks, 6 * per_u),
                sum_w[:2].reshape(2, 2, ranks, per_w).transpose(2, 1, 0, 3).reshape(ranks, 4 * per_w),
                sum_d[:4].reshape(4, ranks, per_d).swapaxes(0, 1).reshape(ranks, 4 * per_d),
                jnp.stack([query_bias_grad, value_bias_grad]).reshape(2, ranks, per_w).swapaxes(0, 1).reshape(ranks, 2 * per_w),
                jnp.stack([pre_gain_grad, pre_bias_grad]).reshape(2, ranks, per_d).swapaxes(0, 1).reshape(ranks, 2 * per_d),
            ],
            axis=1,
        )
        count = vec.shape[1]
        vec = jnp.pad(vec, ((0, 0), (0, block * 128 - count))).reshape(D, 128)
        late = halving(
            jnp.concatenate(
                [p.astype(BF) for p in (query_weight_grad, key_weight_grad, value_weight_grad, vec)], axis=1
            ),
            device,
        )
        vec = late[:, 3 * width :].reshape(-1)[:count]
        late = late[:, : 3 * width].astype(F32)
        at_w = 6 * per_u
        at_d = at_w + 4 * per_w
        at_late = at_d + 4 * per_d
        got = flip(vec[:at_late], "tensor", 0).astype(F32)
        vec = vec.astype(F32)
        ffn_gain_grad, ffn_bias_grad, inner_bias_grad = (vec[: 3 * per_u] + got[3 * per_u : at_w]).reshape(3, per_u)
        sub_gain_grad, sub_bias_grad = (vec[at_w : at_w + 2 * per_w] + got[at_w + 2 * per_w : at_d]).reshape(2, per_w)
        out_bias_grad, mid_gain_grad, mid_bias_grad, outer_bias_grad = (vec[at_d:at_late] + got[at_d:]).reshape(4, per_d)
        query_bias_grad, value_bias_grad = vec[at_late : at_late + 2 * per_w].reshape(2, per_w)
        pre_gain_grad, pre_bias_grad = vec[at_late + 2 * per_w :].reshape(2, per_d)
    inner_weight_grad = early_sum[:, :units]
    outer_weight_grad = early_sum[:, units : 2 * units].T
    out_weight_grad = early_sum[:, 2 * units :].T
    return (
        output,
        input_low,
        pre_gain_grad,
        pre_bias_grad,
        late[:, :width],
        query_bias_grad,
        late[:, width : 2 * width],
        late[:, 2 * width : 3 * width],
        value_bias_grad,
        sub_gain_grad,
        sub_bias_grad,
        out_weight_grad,
        out_bias_grad,
        mid_gain_grad,
        mid_bias_grad,
        inner_weight_grad,
        inner_bias_grad,
        ffn_gain_grad,
        ffn_bias_grad,
        outer_weight_grad,
        outer_bias_grad,
    )

def solution(mesh):
    placed = (
        P("dp", None),
        P("dp", None),
        P(),
        P(),
        P(),
        P(),
        P(),
        P(),
        P(None, "tensor"),
        P("tensor"),
        P(None, "tensor"),
        P(None, "tensor"),
        P("tensor"),
        P("tensor"),
        P("tensor"),
        P("tensor", None),
        P(),
        P(),
        P(),
        P(None, "tensor"),
        P("tensor"),
        P("tensor"),
        P("tensor"),
        P("tensor", None),
        P(),
    )
    return jax.shard_map(
        body,
        mesh=mesh,
        in_specs=placed,
        out_specs=(
            P("dp", None),
            P("dp", None),
            P("dp"),
            P("dp"),
            P("dp", "tensor"),
            P(("tensor", "dp")),
            P("dp", "tensor"),
            P("dp", "tensor"),
            P(("tensor", "dp")),
            P(("tensor", "dp")),
            P(("tensor", "dp")),
            P("tensor", "dp"),
            P("dp"),
            P("dp"),
            P("dp"),
            P("dp", "tensor"),
            P(("tensor", "dp")),
            P(("tensor", "dp")),
            P(("tensor", "dp")),
            P("tensor", "dp"),
            P("dp"),
        ),
        check_vma=False,
    )
```

```python
import functools

import jax
import jax.numpy as jnp
from jax import lax
from jax.experimental import pallas as pl
from jax.experimental.pallas import tpu as pltpu
from jax.sharding import PartitionSpec as P

HD = 64
PROMPT = 2048
CONT = 256
GDEV = 4
TILE = 256
CHUNK = PROMPT // GDEV
PTILES = CHUNK // TILE
LOG2E = 1.4426950408889634
BF = jnp.bfloat16
F32 = jnp.float32
D = 768
EPSILON = 1e-05
MESH = pl.DeviceIdType.MESH


def dot_nt(a, b):
    return lax.dot_general(a, b, (((1,), (1,)), ((), ())), preferred_element_type=F32)


def dot_nn(a, b):
    return lax.dot_general(a, b, (((1,), (0,)), ((), ())), preferred_element_type=F32)


def low_half(rows):
    return lax.broadcasted_iota(jnp.int32, (rows, 128), 1) < HD


def settings(seg, rate, pair):
    def row(value):
        return jnp.full((1, 128), value, jnp.int32).astype(F32)

    def rest(number, period):
        return number - period * jnp.floor((number + 0.5) / period)

    second, third = row(rate[1, pair]), row(rate[2, pair])
    head = row(2 * pair)
    return (
        1.0 / row(seg[0, pair]),
        1.0 / row(seg[1, pair]),
        second,
        1.0 / second,
        third,
        1.0 / third,
        rest(head, second),
        rest(head + 1.0, second),
        rest(head, third),
        rest(head + 1.0, third),
    )


def codes(at, cells, miss):
    first = jnp.floor((at + 0.5) * cells[0])
    second = jnp.floor((at + 0.5) * cells[1])
    rest1 = at - cells[2] * jnp.floor((at + 0.5) * cells[3])
    rest2 = at - cells[4] * jnp.floor((at + 0.5) * cells[5])
    return [
        first,
        jnp.where(rest1 == cells[6], second, miss),
        jnp.where(rest1 == cells[7], second, miss),
        jnp.where(rest2 == cells[8], 1.0, 0.0),
        jnp.where(rest2 == cells[9], 1.0, 0.0),
    ]


def bit_peer(device, bit):
    step = 1 << bit
    return device + (1 - 2 * ((device // step) % 2)) * step


def greet(peers):
    barrier = pltpu.get_barrier_semaphore()
    for peer in peers:
        pl.semaphore_signal(barrier, inc=1, device_id=peer, device_id_type=MESH)
    pl.semaphore_wait(barrier, len(peers))


def xor_bits(a, b):
    return (a % 2 + b % 2) % 2 + 2 * ((a // 2 + b // 2) % 2)


def fwd_kernel(
    starts, gaps, seg, rate, hid, vec, wq, wk, wv, w1, wo, vec_hbm,
    e_ref, li_ref, q_out, k_out, v_out, kp_out, vp_out, o_out, mine_out, got_out,
    w1_got, w1_swap, wo_got, wo_swap, vec_got,
    t_s, kc_s, kv_s, low_s, q_s, ko_s, vo_s, o_s, sems_a, sems_b, loc_sems,
):
    pair = pl.program_id(0)
    step = pl.program_id(1)
    pairs = pl.num_programs(0)
    device = lax.axis_index("dp")
    side = lax.axis_index("tensor")
    member = device % GDEV
    core = device % 2
    rows, width = q_s.shape
    n_pairs = width // 128
    last_pair = n_pairs - 1
    conts = rows - CHUNK
    near = {"dp": bit_peer(device, 0), "tensor": side}
    far = {"dp": bit_peer(device, 1), "tensor": side}
    across = {"dp": device, "tensor": 1 - side}
    half_u = w1.shape[1] // 2
    half_w = wo.shape[0] // 2
    half_p, half_c = CHUNK // 2, conts // 2
    sent_u = pl.multiple_of(core * half_u, 128)
    shared_at = 2 * D + 2 * width
    sent_w = pl.multiple_of(core * half_w, 64)

    def remote(i, src, dst, peer):
        return pltpu.make_async_remote_copy(
            src_ref=src, dst_ref=dst, send_sem=sems_a.at[i], recv_sem=sems_b.at[i], device_id=peer, device_id_type=MESH
        )

    def to_far(p):
        lanes = pl.ds(p * 128, 128)
        return remote(3 * p, kv_s.at[0, :, :, lanes], kv_s.at[2, :, :, lanes], far)

    def to_near(p):
        lanes = pl.ds(p * 128, 128)
        return remote(3 * p + 1, kv_s.at[0, :, :, lanes], kv_s.at[1, :, :, lanes], near)

    def relay(p):
        lanes = pl.ds(p * 128, 128)
        return remote(3 * p + 2, kv_s.at[2, :, :, lanes], kv_s.at[3, :, :, lanes], near)

    base = 3 * n_pairs
    fetch_y = [
        remote(base, wo.at[pl.ds(sent_w, half_w), :], wo_got, across),
        remote(base + 1, w1.at[:, pl.ds(sent_u, half_u)], w1_got, across),
        remote(base + 2, vec_hbm.at[:, pl.ds(shared_at, vec_got.shape[1])], vec_got, across),
    ]
    fetch_core = [
        remote(base + 3, wo_got, wo_swap, near),
        remote(base + 4, w1_got, w1_swap, near),
    ]

    def give(p, piece):
        lanes = pl.ds(p * 128, 128)
        their_p = pl.multiple_of((1 - side) * half_p, 128)
        their_c = pl.multiple_of(CHUNK + (1 - side) * half_c, 128)
        third = half_c // 3
        if piece == 0:
            source, target = pl.ds(their_p, half_p), pl.ds(0, half_p)
        else:
            source = pl.ds(pl.multiple_of(their_c + (piece - 1) * third, 128), third)
            target = pl.ds(half_p + (piece - 1) * third, third)
        return remote(base + 5 + 4 * p + piece, o_s.at[source, lanes], got_out.at[target, lanes], across)

    def keeps():
        own_p = pl.multiple_of(side * half_p, 128)
        own_c = pl.multiple_of(CHUNK + side * half_c, 128)
        return [
            pltpu.make_async_copy(o_s, o_out, loc_sems.at[0]),
            pltpu.make_async_copy(o_s.at[pl.ds(own_p, half_p), :], mine_out.at[pl.ds(0, half_p), :], loc_sems.at[1]),
            pltpu.make_async_copy(o_s.at[pl.ds(own_c, half_c), :], mine_out.at[pl.ds(half_p, half_c), :], loc_sems.at[2]),
        ]

    def saves():
        out = [
            pltpu.make_async_copy(q_s, q_out, loc_sems.at[3]),
            pltpu.make_async_copy(ko_s, k_out, loc_sems.at[0]),
            pltpu.make_async_copy(vo_s, v_out, loc_sems.at[5]),
        ]
        for r in range(GDEV):
            span = pl.ds(r * CHUNK, CHUNK)
            out.append(pltpu.make_async_copy(kv_s.at[r, 0], kp_out.at[span, :], loc_sems.at[6 + 2 * r]))
            out.append(pltpu.make_async_copy(kv_s.at[r, 1], vp_out.at[span, :], loc_sems.at[7 + 2 * r]))
        return out

    @pl.when((pair == 0) & (step == 0))
    def _():
        greet([near, far, across])
        for copy in fetch_y:
            copy.start()
        gain_f, bias_f = vec[:, pl.ds(0, D)], vec[:, pl.ds(D, D)]
        query_bias = vec[:, pl.ds(2 * D, width)]
        value_bias = vec[:, pl.ds(2 * D + width, width)]

        def norm(at, size):
            x = hid[at : at + size, :].astype(F32)
            center = jnp.mean(x, axis=1, keepdims=True)
            scale = lax.rsqrt(jnp.mean(x * x, axis=1, keepdims=True) - center * center + EPSILON)
            low = ((x - center) * scale * gain_f + bias_f).astype(BF)
            low_s[at : at + size, :] = low
            return low

        low = norm(0, CHUNK)
        kv_s[0, 0] = dot_nn(low, wk[...]).astype(BF)
        kv_s[0, 1] = (dot_nn(low, wv[...]) + value_bias).astype(BF)
        to_far(0).start()
        for p in range(n_pairs):
            to_near(p).start()
        for at in range(CHUNK, rows, TILE):
            low = norm(at, TILE)
            ko_s[at - CHUNK : at - CHUNK + TILE, :] = dot_nn(low, wk[...]).astype(BF)
            vo_s[at - CHUNK : at - CHUNK + TILE, :] = (dot_nn(low, wv[...]) + value_bias).astype(BF)
        to_far(0).wait_send()
        for p in range(1, n_pairs):
            to_far(p).start()
        for at in range(0, rows, TILE):
            q_s[at : at + TILE, :] = ((dot_nn(low_s[at : at + TILE, :], wq[...]) + query_bias) * 0.125).astype(BF)
        to_far(0).wait_recv()
        relay(0).start()

    for p in range(n_pairs):
        @pl.when((pair == p) & (step == 0))
        def _():
            to_near(p).wait_recv()
            relay(p).wait_recv()

        if p + 1 < n_pairs:
            @pl.when((pair == p) & (step == 3))
            def _():
                to_far(p + 1).wait_recv()
                relay(p + 1).start()

    lanes = pl.ds(pl.multiple_of(pair * 128, 128), 128)
    low = low_half(TILE)
    q = q_s[pl.ds(pl.multiple_of(step * TILE, TILE), TILE), lanes]
    zero = jnp.zeros_like(q)
    qs = [jnp.where(low, q, zero), jnp.where(low, zero, q)]
    row = lax.broadcasted_iota(jnp.int32, (TILE, 128), 0).astype(F32)
    group = device // GDEV
    start = starts[group]
    first_cont = member * (conts // CONT)
    own_gap = gaps[group, first_cont + jnp.maximum(step - PTILES, 0)]
    base_q = start + jnp.where(step < PTILES, member * CHUNK + step * TILE, PROMPT + own_gap)
    cells = settings(seg, rate, side * n_pairs + pair)
    at_q = base_q.astype(F32) + row
    qc = codes(at_q, cells, -2.0)

    @pl.when(step == 0)
    def _():
        ahead = lax.broadcasted_iota(jnp.int32, (8, 128), 1).astype(F32) + start.astype(F32)
        for j in range(PROMPT // 128):
            for i, c in enumerate(codes(ahead + j * 128.0, cells, -1.0)):
                kc_s[i, :, j * 128 : (j + 1) * 128] = c

    def logits(mx, keys, kc, causal, at, span):
        out = []
        for h in range(2):
            s = dot_nt(qs[h], keys)
            top = mx[h]
            for g in range(span // 128):
                part = slice(g * 128, (g + 1) * 128)
                w = jnp.where(qc[0] == kc[0][:, part], 1.0, 0.0)
                w = w + jnp.where(qc[1 + h] == kc[1 + h][:, part], 1.0, 0.0)
                w = w + qc[3 + h] * kc[3 + h][:, part]
                if causal is not None:
                    w = jnp.where(causal[:, part], w, 0.0)
                t = s[:, part] * LOG2E + jnp.log2(w)
                t_s[h, :, pl.ds(at + g * 128, 128)] = t
                top = jnp.maximum(top, t)
            out.append(top)
        return tuple(out)

    def weigh(carry, vals, m, at, span):
        sums, accs = carry
        ns, na = [], []
        for h in range(2):
            total = sums[h]
            parts = []
            for g in range(span // 128):
                e = jnp.exp2(t_s[h, :, pl.ds(at + g * 128, 128)] - m[h])
                total = total + e
                parts.append(e.astype(BF))
            el = jnp.concatenate(parts, axis=1)
            e_ref[h, :, pl.ds(at, span)] = el
            ns.append(total)
            na.append(accs[h] + dot_nn(el, vals))
        return (tuple(ns), tuple(na))

    def finish_rows(carry):
        sums, accs = carry
        li = [1.0 / jnp.sum(s, axis=1, keepdims=True) for s in sums]
        lfull = jnp.where(low, li[0], li[1])
        li_ref[...] = lfull
        o_s[pl.ds(pl.multiple_of(step * TILE, TILE), TILE), lanes] = (jnp.where(low, accs[0], accs[1]) * lfull).astype(BF)

    def tops(mx):
        return [jnp.broadcast_to(jnp.max(x, axis=1, keepdims=True), (TILE, 128)) for x in mx]

    neg = jnp.full((TILE, 128), -jnp.inf, F32)
    zf = jnp.zeros((TILE, 128), F32)

    def key_codes(at, span):
        return [kc_s[i, 0:1, pl.ds(at, span)] for i in range(5)]

    @pl.when(step < PTILES)
    def _():
        def one(j, mx):
            at = pl.multiple_of(j * CHUNK, CHUNK)
            held = xor_bits(j, member)
            return logits(
                mx, kv_s[held, 0, :, lanes], key_codes(at, CHUNK), None, pl.multiple_of(held * CHUNK, CHUNK), CHUNK
            )

        mx = lax.fori_loop(0, member, one, (neg, neg))
        at = pl.multiple_of(member * CHUNK, CHUNK)
        rows_id = lax.broadcasted_iota(jnp.int32, (TILE, CHUNK), 0) + step * TILE
        cols = lax.broadcasted_iota(jnp.int32, (TILE, CHUNK), 1)
        mx = logits(mx, kv_s[0, 0, :, lanes], key_codes(at, CHUNK), cols <= rows_id, 0, CHUNK)
        m = tops(mx)

        def two(j, carry):
            held = xor_bits(j, member)
            return weigh(carry, kv_s[held, 1, :, lanes], m, pl.multiple_of(held * CHUNK, CHUNK), CHUNK)

        finish_rows(lax.fori_loop(0, member + 1, two, ((zf, zf), (zf, zf))))

    @pl.when(step >= PTILES)
    def _():
        own = pl.ds(pl.multiple_of((step - PTILES) * TILE, TILE), TILE)
        mx = (neg, neg)
        for j in range(GDEV):
            at = pl.multiple_of(xor_bits(j, member) * CHUNK, CHUNK)
            mx = logits(mx, kv_s[j, 0, :, lanes], key_codes(at, CHUNK), None, j * CHUNK, CHUNK)
        rows_id = lax.broadcasted_iota(jnp.int32, (TILE, CONT), 0)
        cols = lax.broadcasted_iota(jnp.int32, (TILE, CONT), 1)
        ahead = lax.broadcasted_iota(jnp.int32, (8, 128), 1).astype(F32) + base_q.astype(F32)
        parts = [codes(ahead + j * 128.0, cells, -1.0) for j in range(CONT // 128)]
        own_codes = [jnp.concatenate([part[i] for part in parts], axis=1)[0:1] for i in range(5)]
        mx = logits(mx, ko_s[own, lanes], own_codes, cols <= rows_id, PROMPT, CONT)
        m = tops(mx)
        carry = ((zf, zf), (zf, zf))
        for j in range(GDEV):
            carry = weigh(carry, kv_s[j, 1, :, lanes], m, j * CHUNK, CHUNK)
        finish_rows(weigh(carry, vo_s[own, lanes], m, PROMPT, CONT))

    end = pl.num_programs(1) - 1
    for p in range(n_pairs):
        @pl.when((pair == p) & (step == 1 - side))
        def _():
            give(p, 0).start()

        for unit in range(6):
            @pl.when((pair == p) & (step == PTILES + unit // 2) & (side == 1 - unit // 3))
            def _():
                give(p, 1 + unit % 3).start()

    @pl.when((pair == last_pair - 1) & (step == 3))
    def _():
        for i in range(2):
            fetch_y[i].wait_recv()
            fetch_core[i].start()

    @pl.when((pair == last_pair) & (step == 0))
    def _():
        for copy in saves():
            copy.start()

    @pl.when((pair == last_pair) & (step == end))
    def _():
        for copy in keeps():
            copy.start()
        fetch_y[2].wait_recv()
        for copy in fetch_core:
            copy.wait_recv()
        for p in range(n_pairs):
            for piece in range(4):
                copy = give(p, piece)
                copy.wait_recv()
                copy.wait_send()
            if p > 0:
                to_far(p).wait_send()
            to_near(p).wait_send()
            relay(p).wait_send()
        for copy in fetch_y + fetch_core:
            copy.wait_send()
        for copy in keeps() + saves():
            copy.wait()


def attend(starts, gaps, seg, rate, hid, vec, wq, wk, wv, w1, wo):
    rows = hid.shape[0]
    width = wq.shape[1]
    pairs = width // 128
    span = PROMPT + CONT
    conts = rows - CHUNK
    units = w1.shape[1]
    vmem = pl.BlockSpec(memory_space=pltpu.VMEM)
    hbm = pl.BlockSpec(memory_space=pl.ANY)
    shape = jax.ShapeDtypeStruct
    copies = 3 * pairs + 5 + 4 * pairs
    shared = 3 * units + 2 * width
    smem = pl.BlockSpec(memory_space=pltpu.SMEM)
    return pl.pallas_call(
        fwd_kernel,
        grid_spec=pltpu.PrefetchScalarGridSpec(
            num_scalar_prefetch=0,
            grid=(pairs, rows // TILE),
            in_specs=[smem] * 4 + [vmem] * 5 + [hbm] * 3,
            out_specs=[
                pl.BlockSpec((2, TILE, span), lambda a, t: (a, t, 0)),
                pl.BlockSpec((TILE, 128), lambda a, t: (t, a)),
            ]
            + [hbm] * 13,
            scratch_shapes=[
                pltpu.VMEM((2, TILE, span), F32),
                pltpu.VMEM((5, 8, PROMPT), F32),
                pltpu.VMEM((GDEV, 2, CHUNK, width), BF),
                pltpu.VMEM((rows, D), BF),
                pltpu.VMEM((rows, width), BF),
                pltpu.VMEM((conts, width), BF),
                pltpu.VMEM((conts, width), BF),
                pltpu.VMEM((rows, width), BF),
                pltpu.SemaphoreType.DMA((copies,)),
                pltpu.SemaphoreType.DMA((copies,)),
                pltpu.SemaphoreType.DMA((6 + 2 * GDEV,)),
            ],
        ),
        out_shape=[
            shape((2 * pairs, rows, span), BF),
            shape((rows, width), F32),
            shape((rows, width), BF),
            shape((conts, width), BF),
            shape((conts, width), BF),
            shape((PROMPT, width), BF),
            shape((PROMPT, width), BF),
            shape((rows, width), BF),
            shape((rows // 2, width), BF),
            shape((rows // 2, width), BF),
            shape((D, units // 2), BF),
            shape((D, units // 2), BF),
            shape((width // 2, D), BF),
            shape((width // 2, D), BF),
            shape((1, shared), F32),
        ],
        compiler_params=pltpu.CompilerParams(vmem_limit_bytes=56 << 20, collective_id=0, has_side_effects=True),
        cost_estimate=pl.CostEstimate(flops=20 * 10**9, bytes_accessed=60 * 10**6, transcendentals=0),
        name="attend",
    )(starts, gaps, seg, rate, hid, vec, wq, wk, wv, w1, wo, vec)


EARLY = 2
FIRST_CUT = 1920


def reducer_scratch(count, block, cut):
    return [
        pltpu.VMEM((count, 2, 2, 2, block, cut), BF),
        pltpu.VMEM((count, 2, 2, 2, block, cut), BF),
        pltpu.VMEM((count, 2, 2, block, cut), BF),
        pltpu.VMEM((count, 2, 2, block, cut), BF),
        pltpu.VMEM((count, 2, block, cut), BF),
        pltpu.VMEM((count, 2, block, cut), BF),
        pltpu.VMEM((count, block, cut), BF),
        pltpu.SemaphoreType.DMA((4 * count,)),
        pltpu.SemaphoreType.DMA((4 * count,)),
        pltpu.SemaphoreType.DMA((count,)),
    ]


def reducer(packed, device, side, base, refs, done):
    held, got0, got1, held1, got2, held2, got3, sems_a, sems_b, sems_l = refs
    bit = [(device // (1 << b)) % 2 for b in range(4)]
    peers = [{"dp": bit_peer(device, b), "tensor": side} for b in range(4)]
    cut = held.shape[-1]

    def passing(c, stage, source, target, peer):
        return pltpu.make_async_remote_copy(
            src_ref=source,
            dst_ref=target,
            send_sem=sems_a.at[4 * c + stage],
            recv_sem=sems_b.at[4 * c + stage],
            device_id=peer,
            device_id_type=MESH,
        )

    count = held.shape[0]

    def columns_of(c, first):
        return pl.ds(first + (count - 1 - c) * cut, cut)

    def own_half(c):
        return pltpu.make_async_copy(packed.at[:, :, :, bit[0], :, columns_of(c, base)], held.at[c], sems_l.at[c])

    def stage0(c):
        return passing(c, 0, packed.at[:, :, :, 1 - bit[0], :, columns_of(c, base)], got0.at[c], peers[0])

    def stage1(c):
        if c % 2:
            return passing(c, 1, held.at[c, :, 1 - bit[2]], got1.at[c], peers[2])
        return passing(c, 1, held.at[c, :, :, 1 - bit[1]], got1.at[c], peers[1])

    def stage2(c):
        b = 1 if c % 2 else 2
        return passing(c, 2, held1.at[c, :, 1 - bit[b]], got2.at[c], peers[b])

    def stage3(c):
        return passing(c, 3, held2.at[c, 1 - bit[3]], got3.at[c], peers[3])

    def begin(c):
        own_half(c).start()
        stage0(c).start()

    def after0(c):
        own_half(c).wait()
        stage0(c).wait_recv()
        held[c] = held[c] + got0[c]
        stage1(c).start()

    def after1(c):
        stage1(c).wait_recv()
        kept = held[c, :, bit[2]] if c % 2 else held[c, :, :, bit[1]]
        held1[c] = kept + got1[c]
        stage2(c).start()

    def after2(c):
        stage2(c).wait_recv()
        held2[c] = held1[c, :, bit[1 if c % 2 else 2]] + got2[c]
        stage3(c).start()

    def after3(c):
        stage3(c).wait_recv()
        done[:, columns_of(c, 0)] = held2[c, bit[3]] + got3[c]

    def settle():
        for c in range(count):
            for copy in (stage0(c), stage1(c), stage2(c), stage3(c)):
                copy.wait_send()

    return begin, after0, after1, after2, after3, settle


def bwd_kernel(
    fused, q_ref, kp_ref, vp_ref, ko_ref, vo_ref, o_ref, li_ref, e_ref, g_mine, g_theirs, out_half, *refs
):
    packed = refs[0] if fused else None
    refs = refs[1:] if fused else refs
    dq_ref, dko_ref, dvo_ref, sum_k, sum_v, relay_out, out_got = refs[:7]
    done_out, other_out = refs[7:9] if fused else (None, None)
    refs = refs[9:] if fused else refs[7:]
    dk_s, dv_s, g_s, grad_s, near_s, relay_s, far_s, sems_a, sems_b, loc_sems = refs[:10]
    pair = pl.program_id(0)
    step = pl.program_id(1)
    device = lax.axis_index("dp")
    side = lax.axis_index("tensor")
    member = device % GDEV
    rows, width = g_s.shape
    n_pairs = width // 128
    conts = rows - CHUNK
    half_p, half_c = CHUNK // 2, conts // 2
    near = {"dp": bit_peer(device, 0), "tensor": side}
    far = {"dp": bit_peer(device, 1), "tensor": side}
    across = {"dp": device, "tensor": 1 - side}
    lanes = pl.ds(pl.multiple_of(pair * 128, 128), 128)
    mine_p = pl.ds(pl.multiple_of(side * half_p, 128), half_p)
    mine_c = pl.ds(pl.multiple_of(CHUNK + side * half_c, 128), half_c)

    def remote(i, src, dst, peer):
        return pltpu.make_async_remote_copy(
            src_ref=src, dst_ref=dst, send_sem=sems_a.at[i], recv_sem=sems_b.at[i], device_id=peer, device_id_type=MESH
        )

    def heads():
        return [
            remote(0, g_theirs.at[pl.ds(0, half_p), :], g_s.at[mine_p, :], across),
            remote(1, g_theirs.at[pl.ds(half_p, half_c), :], g_s.at[mine_c, :], across),
            remote(2, out_half, out_got, across),
        ]

    def local():
        return [
            pltpu.make_async_copy(g_mine.at[pl.ds(0, half_p), :], g_s.at[mine_p, :], loc_sems.at[0]),
            pltpu.make_async_copy(g_mine.at[pl.ds(half_p, half_c), :], g_s.at[mine_c, :], loc_sems.at[1]),
        ]

    def cores(p):
        part = pl.ds(p * 128, 128)
        return remote(3 + 2 * p, grad_s.at[:, :, 1, :, part], near_s.at[:, :, :, part], near)

    def chips(p):
        part = pl.ds(p * 128, 128)
        return remote(4 + 2 * p, relay_s.at[:, :, part], far_s.at[:, :, part], far)

    if fused:
        *early_refs, done_s, other_a, early_sems = refs[10:]
        begin, after0, after1, after2, after3, settle = reducer(
            packed, device, side, packed.shape[-1] - EARLY * FIRST_CUT, early_refs, done_s
        )
        half_e = packed.shape[-1] // 2
        tail_e = EARLY * FIRST_CUT - half_e
        peers = [{"dp": bit_peer(device, b), "tensor": side} for b in range(4)]
        swap = pltpu.make_async_remote_copy(
            src_ref=done_s.at[:, pl.ds(tail_e, half_e)],
            dst_ref=other_a,
            send_sem=early_sems.at[0],
            recv_sem=early_sems.at[1],
            device_id=across,
            device_id_type=MESH,
        )
        tick = pair * pl.num_programs(1) + step

    @pl.when((pair == 0) & (step == 0))
    def _():
        greet([near, far, across] + (peers[2:] if fused else []))
        for copy in heads() + local():
            copy.start()
        for copy in local():
            copy.wait()

    if fused:
        for c in range(EARLY):
            for at, act in ((0, begin), (1 + c, after0), (5 + c, after1), (8 + c, after2), (12, after3)):
                @pl.when(tick == at)
                def _():
                    act(c)

        @pl.when(tick == 12)
        def _():
            swap.start()

    @pl.when((pair == 0) & (step == 1 - side))
    def _():
        heads()[0].wait_recv()

    @pl.when((pair == 0) & (step == 3 - side))
    def _():
        heads()[1].wait_recv()

    low = low_half(TILE)
    g = g_s[pl.ds(pl.multiple_of(step * TILE, TILE), TILE), lanes].astype(F32) * li_ref[...]
    prod = g * o_ref[...].astype(F32)
    zf = jnp.zeros((TILE, 128), F32)
    deltas = [
        jnp.sum(jnp.where(low, prod, zf), axis=1, keepdims=True),
        jnp.sum(jnp.where(low, zf, prod), axis=1, keepdims=True),
    ]
    gs = [jnp.where(low, g, zf).astype(BF), jnp.where(low, zf, g).astype(BF)]
    gt = jnp.transpose(g).astype(BF)
    qt = jnp.transpose(q_ref[...].astype(F32)).astype(BF)

    def grads(dq, keys, vals, at, width):
        out, dks, dvs = [], [], []
        for h in range(2):
            e = e_ref[h, :, pl.ds(at, width)]
            dp = dot_nt(gs[h], vals)
            ds = (e.astype(F32) * (dp - deltas[h])).astype(BF)
            out.append(dq[h] + dot_nn(ds, keys))
            dks.append(dot_nn(qt[h * HD : (h + 1) * HD, :], ds))
            dvs.append(dot_nn(gt[h * HD : (h + 1) * HD, :], e))
        return tuple(out), dks, dvs

    @pl.when(step == 0)
    def _():
        dk_s[...] = jnp.zeros_like(dk_s)
        dv_s[...] = jnp.zeros_like(dv_s)

    def add(at, width, dks, dvs):
        for h in range(2):
            dk_s[h * HD : (h + 1) * HD, pl.ds(at, width)] += dks[h]
            dv_s[h * HD : (h + 1) * HD, pl.ds(at, width)] += dvs[h]

    def scaled(dq):
        return (jnp.where(low, dq[0], dq[1]).astype(BF).astype(F32) * 0.125).astype(BF)

    @pl.when(step < PTILES)
    def _():
        def one(j, dq):
            at = pl.multiple_of(xor_bits(j, member) * CHUNK, CHUNK)
            dq, dks, dvs = grads(dq, kp_ref[pl.ds(at, CHUNK), :], vp_ref[pl.ds(at, CHUNK), :], at, CHUNK)
            add(at, CHUNK, dks, dvs)
            return dq

        dq_ref[...] = scaled(lax.fori_loop(0, member + 1, one, (zf, zf)))
        dko_ref[...] = jnp.zeros_like(dko_ref)
        dvo_ref[...] = jnp.zeros_like(dvo_ref)

    @pl.when(step >= PTILES)
    def _():
        dq = (zf, zf)
        for j in range(GDEV):
            span = slice(j * CHUNK, (j + 1) * CHUNK)
            dq, dks, dvs = grads(dq, kp_ref[span, :], vp_ref[span, :], j * CHUNK, CHUNK)
            add(j * CHUNK, CHUNK, dks, dvs)
        dq, dks, dvs = grads(dq, ko_ref[...], vo_ref[...], PROMPT, CONT)
        dq_ref[...] = scaled(dq)
        dko_ref[...] = jnp.transpose(jnp.concatenate(dks, axis=0)).astype(BF)
        dvo_ref[...] = jnp.transpose(jnp.concatenate(dvs, axis=0)).astype(BF)

    end = pl.num_programs(1) - 1

    @pl.when(step == end)
    def _():
        for j in range(GDEV):
            span = slice(j * CHUNK, (j + 1) * CHUNK)
            grad_s[0, j // 2, j % 2, :, lanes] = jnp.transpose(dk_s[:, span]).astype(BF)
            grad_s[1, j // 2, j % 2, :, lanes] = jnp.transpose(dv_s[:, span]).astype(BF)

    for p in range(n_pairs):
        @pl.when((pair == p) & (step == end))
        def _():
            cores(p).start()

        if p + 1 < n_pairs:
            @pl.when((pair == p + 1) & (step == 2))
            def _():
                part = pl.ds(p * 128, 128)
                cores(p).wait_recv()
                relay_s[:, :, part] = (
                    grad_s[:, 1, 0, :, part].astype(F32) + near_s[:, 1, :, part].astype(F32)
                ).astype(BF)
                chips(p).start()

    @pl.when((pair == n_pairs - 1) & (step == end))
    def _():
        last = n_pairs - 1
        sums = (sum_k, sum_v)
        for p in range(last):
            part = pl.ds(p * 128, 128)
            chips(p).wait_recv()
            for i in range(2):
                sums[i][:, part] = (
                    grad_s[i, 0, 0, :, part].astype(F32) + near_s[i, 0, :, part].astype(F32) + far_s[i, :, part].astype(F32)
                ).astype(BF)
        part = pl.ds(last * 128, 128)
        cores(last).wait_recv()
        for i in range(2):
            relay_out[i] = (grad_s[i, 1, 0, :, part].astype(F32) + near_s[i, 1, :, part].astype(F32)).astype(BF)
            sums[i][:, part] = (grad_s[i, 0, 0, :, part].astype(F32) + near_s[i, 0, :, part].astype(F32)).astype(BF)
        if fused:
            swap.wait_recv()
            done_out[...] = done_s[:, pl.ds(0, tail_e)]
            other_out[...] = other_a[...]
            settle()
            swap.wait_send()
        heads()[2].wait_recv()
        for copy in heads():
            copy.wait_send()
        for p in range(n_pairs):
            cores(p).wait_send()
            if p < last:
                chips(p).wait_send()


def attend_back(q, k, v, kp, vp, o, li, e, g_mine, g_theirs, out_half, packed):
    rows, width = q.shape
    pairs = width // 128
    span = PROMPT + CONT
    tile = pl.BlockSpec((TILE, 128), lambda a, t: (t, a))
    whole = pl.BlockSpec((PROMPT, 128), lambda a, t: (0, a))
    own = pl.BlockSpec((TILE, 128), lambda a, t: (jnp.maximum(t - PTILES, 0), a))
    vmem = pl.BlockSpec(memory_space=pltpu.VMEM)
    hbm = pl.BlockSpec(memory_space=pl.ANY)
    shape = jax.ShapeDtypeStruct
    copies = 3 + 2 * pairs
    fused = packed is not None
    more_in, more_out, more_scratch = [], [], []
    if fused:
        block, half_e = packed.shape[-2], packed.shape[-1] // 2
        more_in = [packed]
        more_out = [shape((block, EARLY * FIRST_CUT - half_e), BF), shape((block, half_e), BF)]
        more_scratch = reducer_scratch(EARLY, block, FIRST_CUT) + [
            pltpu.VMEM((block, EARLY * FIRST_CUT), BF),
            pltpu.VMEM((block, half_e), BF),
            pltpu.SemaphoreType.DMA((2,)),
        ]
    return pl.pallas_call(
        functools.partial(bwd_kernel, fused),
        grid=(pairs, rows // TILE),
        in_specs=[tile, whole, whole, own, own, tile, tile, pl.BlockSpec((2, TILE, span), lambda a, t: (a, t, 0))]
        + [hbm] * (3 + len(more_in)),
        out_specs=[tile, tile, tile, vmem, vmem, vmem, hbm] + [vmem] * len(more_out),
        out_shape=[
            shape((rows, width), BF),
            shape((rows, width), BF),
            shape((rows, width), BF),
            shape((CHUNK, width), BF),
            shape((CHUNK, width), BF),
            shape((2, CHUNK, 128), BF),
            shape(out_half.shape, BF),
        ]
        + more_out,
        scratch_shapes=[
            pltpu.VMEM((128, PROMPT), F32),
            pltpu.VMEM((128, PROMPT), F32),
            pltpu.VMEM((rows, width), BF),
            pltpu.VMEM((2, 2, 2, CHUNK, width), BF),
            pltpu.VMEM((2, 2, CHUNK, width), BF),
            pltpu.VMEM((2, CHUNK, width), BF),
            pltpu.VMEM((2, CHUNK, width), BF),
            pltpu.SemaphoreType.DMA((copies,)),
            pltpu.SemaphoreType.DMA((copies,)),
            pltpu.SemaphoreType.DMA((2,)),
        ]
        + more_scratch,
        compiler_params=pltpu.CompilerParams(vmem_limit_bytes=60 << 20, collective_id=2, has_side_effects=True),
        cost_estimate=pl.CostEstimate(flops=30 * 10**9, bytes_accessed=60 * 10**6, transcendentals=0),
        name="attend_back",
    )(q, kp, vp, k, v, o, li, e, g_mine, g_theirs, out_half, *more_in)


UCH = 512


def polynomial(x, terms):
    out = jnp.full_like(x, terms[0])
    for term in terms[1:]:
        out = out * x + term
    return out


def error_function(x):
    x = jnp.clip(x, -3.832506856900711, 3.832506856900711)
    square = x * x
    top = polynomial(
        square,
        (0.00022905065861350646, 0.0034082910107109506, 0.050955695062380861, 0.18520832239976145, 1.128379143519084),
    )
    bottom = polynomial(
        square,
        (
            -1.1791602954361697e-7,
            0.000023547966471313185,
            0.0010179625278914885,
            0.014070470171167667,
            0.11098505178285362,
            0.49746925110067538,
            1.0,
        ),
    )
    return x * top / bottom


def gelu_pair(v):
    phi = 0.5 + 0.5 * error_function(v * 0.7071067811865476)
    density = jnp.exp(-0.5 * v * v) * 0.3989422804014327
    return v * phi, phi + v * density


def column_sum(x):
    return jnp.sum(x, axis=0, keepdims=True)


def mid_kernel(
    att_m, att_o, vec_all, vec_got, hid_all, cot_all, w1_own, w1_got, w1_swap, wo_own, wo_got, wo_swap, w2_own,
    out_ref, gatt_m, gatt_o, gmix_ref, packed, su_ref, sw_ref, sd_ref, ext_ref,
    vec_u, vec_w, w1, w2, wo, act_s, shp_s, dg_s, wide_s, acc_s, gmid_s, sub_s, mid_s, low_s, midt_s, cott_s, stage, hid, cot, sems, out_sems, send_sems, recv_sems,
):
    device = lax.axis_index("dp")
    side = lax.axis_index("tensor")
    core = device % 2
    near = {"dp": bit_peer(device, 0), "tensor": side}
    across = {"dp": device, "tensor": 1 - side}
    units = w1_own.shape[1]
    width = wo_own.shape[0]
    rows = hid.shape[0]
    full = 2 * units
    half = units // 2
    half_w = width // 2
    here_u = pl.multiple_of(units + core * half, 128)
    there_u = pl.multiple_of(units + (1 - core) * half, 128)
    here_w = pl.multiple_of(width + core * half_w, 64)
    there_w = pl.multiple_of(width + (1 - core) * half_w, 64)
    prompt, conts = CHUNK // 2, (hid_all.shape[0] - CHUNK) // 2
    own_p = pl.ds(pl.multiple_of(side * prompt, 128), prompt)
    own_c = pl.ds(pl.multiple_of(CHUNK + side * conts, 128), conts)
    at_own = 2 * D + 2 * width
    vec_own = vec_all.at[:, pl.ds(at_own, 3 * units + 2 * width)]
    vec_d = vec_all.at[:, pl.ds(at_own + 3 * units + 2 * width, 4 * D)]
    rows_in = []
    for i, (all_rows, held) in enumerate(((hid_all, hid), (cot_all, cot))):
        for j, (span, at, size) in enumerate(((own_p, 0, prompt), (own_c, prompt, conts))):
            copy = pltpu.make_async_copy(all_rows.at[span, :], held.at[pl.ds(at, size), :], sems.at[7 + 2 * i + j])
            copy.start()
            rows_in.append(copy)
    loads = []
    for i, (src, dst) in enumerate(
        [
            (wo_own, wo.at[pl.ds(0, width), :]),
            (wo_got, wo.at[pl.ds(here_w, half_w), :]),
            (wo_swap, wo.at[pl.ds(there_w, half_w), :]),
            (w1_own, w1.at[:, pl.ds(0, units)]),
            (w1_got, w1.at[:, pl.ds(here_u, half)]),
            (w1_swap, w1.at[:, pl.ds(there_u, half)]),
            (w2_own, w2.at[pl.ds(0, units), :]),
        ]
    ):
        copy = pltpu.make_async_copy(src, dst, sems.at[i])
        copy.start()
        loads.append(copy)

    piece = half // 2
    greet([near, across])

    def remote(i, src, dst, peer):
        return pltpu.make_async_remote_copy(
            src_ref=src, dst_ref=dst, send_sem=send_sems.at[i], recv_sem=recv_sems.at[i], device_id=peer, device_id_type=MESH
        )

    over, passed = [], []
    for i in range(2):
        from_own = pl.ds(pl.multiple_of(core * half + i * piece, 128), piece)
        landed = w2.at[pl.ds(pl.multiple_of(units + core * half + i * piece, 128), piece), :]
        over.append(remote(i, w2_own.at[from_own, :], landed, across))
        passed.append(remote(2 + i, landed, landed, near))
        over[i].start()

    for i in range(3):
        for j, vec in enumerate((vec_own, vec_got)):
            vec_u[i : i + 1, pl.ds(j * units, units)] = vec[0:1, pl.ds(i * units, units)]
    for i in range(2):
        for j, vec in enumerate((vec_own, vec_got)):
            vec_w[i : i + 1, pl.ds(j * width, width)] = vec[0:1, pl.ds(3 * units + i * width, width)]

    a0 = att_m[...].astype(F32)
    a1 = att_o[...].astype(F32)
    center = (jnp.sum(a0, axis=1, keepdims=True) + jnp.sum(a1, axis=1, keepdims=True)) * (1.0 / D)
    square = (jnp.sum(a0 * a0, axis=1, keepdims=True) + jnp.sum(a1 * a1, axis=1, keepdims=True)) * (1.0 / D)
    sub_scale = lax.rsqrt(square - center * center + EPSILON)
    sub_s[:, 0:width] = (a0 - center) * sub_scale
    sub_s[:, width : 2 * width] = (a1 - center) * sub_scale
    sub_gain = vec_w[0:1, :]
    low_s[...] = (sub_s[...] * sub_gain + vec_w[1:2, :]).astype(BF)
    for copy in loads[0:3] + rows_in:
        copy.wait()
    mixed = hid[...].astype(F32) + (dot_nn(low_s[...], wo[...]) + vec_d[0:1, pl.ds(0, D)])
    wide_s[...] = mixed
    mean = jnp.mean(mixed, axis=1, keepdims=True)
    mid_scale = lax.rsqrt(jnp.mean(mixed * mixed, axis=1, keepdims=True) - mean * mean + EPSILON)
    mid_s[...] = (mixed - mean) * mid_scale
    mid_gain = vec_d[0:1, pl.ds(768, D)]
    mid_full = mid_s[...] * mid_gain + vec_d[0:1, pl.ds(1536, D)]
    mid_low = mid_full.astype(BF)
    midt_s[...] = jnp.transpose(mid_full).astype(BF)
    cot_full = cot[...].astype(F32)
    cott_s[...] = jnp.transpose(cot_full).astype(BF)
    sd_ref[...] = jnp.zeros_like(sd_ref)
    sd_ref[3:4, :] = column_sum(cot_full)
    for copy in loads[3:6]:
        copy.wait()

    def lanes_sum(x):
        total = x[:, 0:128]
        for i in range(1, x.shape[1] // 128):
            total = total + x[:, i * 128 : (i + 1) * 128]
        return total

    def first(c, carry):
        at = pl.multiple_of(c * UCH, UCH)
        inner = dot_nn(mid_low, w1[:, pl.ds(at, UCH)]) + vec_u[2:3, pl.ds(at, UCH)]
        act, slope = gelu_pair(inner)
        act_s[:, pl.ds(at, UCH)] = act
        dg_s[:, pl.ds(at, UCH)] = slope.astype(BF)
        return carry[0] + lanes_sum(act), carry[1] + lanes_sum(act * act)

    zero = jnp.zeros((rows, 128), F32)
    act_sum, act_square = lax.fori_loop(0, full // UCH, first, (zero, zero))
    ffn_center = jnp.sum(act_sum, axis=1, keepdims=True) * (1.0 / full)
    ffn_scale = lax.rsqrt(
        jnp.sum(act_square, axis=1, keepdims=True) * (1.0 / full) - ffn_center * ffn_center + EPSILON
    )
    loads[6].wait()
    over[0].wait_recv()
    passed[0].start()
    acc_s[...] = jnp.zeros_like(acc_s)
    per = units // UCH
    wide = 2 * units + width

    def column_of(c, extra):
        return pl.multiple_of((c // per) * wide + lax.rem(c, per) * UCH + extra, 128)

    def send(slot, column):
        return pltpu.make_async_copy(stage.at[slot], packed.at[:, pl.ds(column, UCH)], out_sems.at[slot])

    def put(c, value, extra):
        slot = lax.rem(c, 2)

        @pl.when(c >= 2)
        def _():
            send(slot, column_of(c - 2, extra)).wait()

        stage[slot] = value
        send(slot, column_of(c, extra)).start()

    def drain(extra):
        for c in range(full // UCH - 2, full // UCH):
            send(c % 2, column_of(c, extra)).wait()

    def second(c, carry):
        at = pl.multiple_of(c * UCH, UCH)
        unit = (act_s[:, pl.ds(at, UCH)] - ffn_center) * ffn_scale
        act_s[:, pl.ds(at, UCH)] = unit
        gain = vec_u[0:1, pl.ds(at, UCH)]
        low = (unit * gain + vec_u[1:2, pl.ds(at, UCH)]).astype(BF)
        acc_s[...] += dot_nn(low, w2[pl.ds(at, UCH), :])
        grad = dot_nt(cot[...], w2[pl.ds(at, UCH), :])
        cross = grad * unit
        su_ref[0:1, pl.ds(at, UCH)] = column_sum(cross)
        su_ref[1:2, pl.ds(at, UCH)] = column_sum(grad)
        shaped = grad * gain
        shp_s[:, pl.ds(at, UCH)] = shaped
        put(c, dot_nn(cott_s[...], low).astype(BF), units)
        return carry[0] + lanes_sum(shaped), carry[1] + lanes_sum(shaped * unit)

    su_ref[...] = jnp.zeros_like(su_ref)
    sums = lax.fori_loop(0, per, second, (zero, zero))
    over[1].wait_recv()
    passed[1].start()
    for copy in passed:
        copy.wait_recv()
    s_sum, s_cross = lax.fori_loop(per, 2 * per, second, sums)
    drain(units)
    shaped_mean = jnp.sum(s_sum, axis=1, keepdims=True) * (1.0 / full)
    cross_mean = jnp.sum(s_cross, axis=1, keepdims=True) * (1.0 / full)
    out_ref[...] = (wide_s[...] + (acc_s[...] + vec_d[0:1, pl.ds(2304, D)])).astype(BF)
    gmid_s[...] = jnp.zeros_like(gmid_s)

    def third(c, carry):
        at = pl.multiple_of(c * UCH, UCH)
        g = ffn_scale * (shp_s[:, pl.ds(at, UCH)] - shaped_mean - act_s[:, pl.ds(at, UCH)] * cross_mean)
        low = (g * dg_s[:, pl.ds(at, UCH)].astype(F32)).astype(BF)
        su_ref[2:3, pl.ds(at, UCH)] = column_sum(low.astype(F32))
        gmid_s[...] += dot_nt(low, w1[:, pl.ds(at, UCH)])
        put(c, dot_nn(midt_s[...], low).astype(BF), 0)
        return carry

    lax.fori_loop(0, full // UCH, third, 0)
    drain(0)

    grad_mid = gmid_s[...]
    unit = mid_s[...]
    sd_ref[1:2, :] = column_sum(grad_mid * unit)
    sd_ref[2:3, :] = column_sum(grad_mid)
    shaped = grad_mid * mid_gain
    grad_mixed = cot[...].astype(F32) + mid_scale * (
        shaped - jnp.mean(shaped, axis=1, keepdims=True) - unit * jnp.mean(shaped * unit, axis=1, keepdims=True)
    )
    branch = grad_mixed.astype(BF)
    gmix_ref[...] = branch
    branch_f = branch.astype(F32)
    sd_ref[0:1, :] = column_sum(branch_f)
    out_grad = dot_nn(jnp.transpose(branch_f).astype(BF), low_s[...]).astype(BF)
    stage[0, :, 0:width] = out_grad[:, 0:width]
    stage[1, :, 0:width] = out_grad[:, width : 2 * width]
    last = [
        pltpu.make_async_copy(stage.at[i, :, pl.ds(0, width)], packed.at[:, pl.ds(i * wide + 2 * units, width)], out_sems.at[i])
        for i in range(2)
    ]
    for copy in last:
        copy.start()
    grad_sub = dot_nt(branch, wo[...])
    unit = sub_s[...]
    cross = grad_sub * unit
    sw_ref[...] = jnp.zeros_like(sw_ref)
    sw_ref[0:1, :] = column_sum(cross)
    sw_ref[1:2, :] = column_sum(grad_sub)
    shaped = grad_sub * sub_gain
    grad_att = sub_scale * (
        shaped - jnp.mean(shaped, axis=1, keepdims=True) - unit * jnp.mean(shaped * unit, axis=1, keepdims=True)
    )
    gatt_m[...] = grad_att[:, 0:width].astype(BF)
    gatt_o[...] = grad_att[:, width : 2 * width].astype(BF)
    parts = ext_ref.shape[0]
    if parts > 1:
        sums_u, sums_w, sums_d = su_ref[...], sw_ref[...], sd_ref[...]
        for i in range(parts):
            ext_ref[i] = jnp.concatenate(
                [
                    window(sums_u, i * (units // parts)),
                    window(sums_u, units + i * (units // parts)),
                    window(sums_w, i * (width // parts)),
                    window(sums_w, width + i * (width // parts)),
                    window(sums_d, i * (D // parts)),
                    jnp.zeros((8, 128), F32),
                ],
                axis=0,
            ).astype(BF)
    for copy in last:
        copy.wait()
    for copy in over + passed:
        copy.wait_send()


def window(rows8, start):
    base = start // 128 * 128
    size = min(256, rows8.shape[1] - base)
    view = rows8[:, base : base + size]
    shift = start - base
    if shift:
        view = pltpu.roll(view, size - shift, 1)
    return view[:, 0:128]


def middle(att_m, att_o, hid, cot, vec_all, vec_got, w1, w2, wo, parts):
    rows = att_m.shape[0]
    units = w2.shape[0]
    width = wo[0].shape[0]
    vmem = pl.BlockSpec(memory_space=pltpu.VMEM)
    hbm = pl.BlockSpec(memory_space=pl.ANY)
    shape = jax.ShapeDtypeStruct
    return pl.pallas_call(
        mid_kernel,
        in_specs=[vmem] * 4 + [hbm] * 9,
        out_specs=[vmem] * 4 + [hbm] + [vmem] * 4,
        out_shape=[
            shape((rows, D), BF),
            shape((rows, width), BF),
            shape((rows, width), BF),
            shape((rows, D), BF),
            shape((D, 2 * (2 * units + width)), BF),
            shape((8, 2 * units), F32),
            shape((8, 2 * width), F32),
            shape((8, D), F32),
            shape((parts, 48, 128), BF),
        ],
        scratch_shapes=[
            pltpu.VMEM((8, 2 * units), F32),
            pltpu.VMEM((8, 2 * width), F32),
            pltpu.VMEM((D, 2 * units), BF),
            pltpu.VMEM((2 * units, D), BF),
            pltpu.VMEM((2 * width, D), BF),
            pltpu.VMEM((rows, 2 * units), F32),
            pltpu.VMEM((rows, 2 * units), F32),
            pltpu.VMEM((rows, 2 * units), BF),
            pltpu.VMEM((rows, D), F32),
            pltpu.VMEM((rows, D), F32),
            pltpu.VMEM((rows, D), F32),
            pltpu.VMEM((rows, 2 * width), F32),
            pltpu.VMEM((rows, D), F32),
            pltpu.VMEM((rows, 2 * width), BF),
            pltpu.VMEM((D, rows), BF),
            pltpu.VMEM((D, rows), BF),
            pltpu.VMEM((2, D, UCH), BF),
            pltpu.VMEM((rows, D), BF),
            pltpu.VMEM((rows, D), BF),
            pltpu.SemaphoreType.DMA((11,)),
            pltpu.SemaphoreType.DMA((2,)),
            pltpu.SemaphoreType.DMA((4,)),
            pltpu.SemaphoreType.DMA((4,)),
        ],
        compiler_params=pltpu.CompilerParams(vmem_limit_bytes=62 << 20, collective_id=3, has_side_effects=True),
        cost_estimate=pl.CostEstimate(flops=21 * 10**9, bytes_accessed=30 * 10**6, transcendentals=0),
        name="middle",
    )(att_m, att_o, vec_all, vec_got, hid, cot, *w1, *wo, w2)


def final_kernel(
    bits, hid, vec_all, dq, dk, dv, wq, wk, wv, gmix, ext, sum_k, sum_v, relay, first_done, first_other, packed,
    gin, late_out, vec_out, early_out,
    loc_s, far_s, unit_s, mine_s, norm_s, send_c, recv_c, send_p, recv_p, give_c, give_p, late_s, small_s,
    vec_s, vec_r, done_s, sems_a, sems_b, loc_sems, *stage_refs,
):
    device = lax.axis_index("dp")
    side = lax.axis_index("tensor")
    across = {"dp": device, "tensor": 1 - side}
    peers = [{"dp": bit_peer(device, b), "tensor": side} for b in range(bits)]
    rows, width = dq.shape
    prompt = sum_k.shape[0]
    conts = rows - prompt
    half_p, half_c = prompt // 2, conts // 2
    own_p = pl.multiple_of(side * half_p, 128)
    their_p = pl.multiple_of((1 - side) * half_p, 128)
    own_c = pl.multiple_of(prompt + side * half_c, 128)
    their_c = pl.multiple_of(prompt + (1 - side) * half_c, 128)
    lanes = 3 * width + 128

    greet(peers + [across])
    count = [0]

    def remote(src, dst, peer):
        i = count[0]
        count[0] += 1
        copy = pltpu.make_async_remote_copy(
            src_ref=src, dst_ref=dst, send_sem=sems_a.at[i], recv_sem=sems_b.at[i], device_id=peer, device_id_type=MESH
        )
        copy.start()
        return copy

    share = remote(relay, far_s, peers[1])

    begin, after0, after1, after2, after3, settle = reducer(packed, device, side, 0, stage_refs[-10:], done_s)

    def each(act):
        for c in range(EARLY):
            act(c)

    each(begin)

    gain_f = vec_all[:, pl.ds(0, D)]
    bias_f = vec_all[:, pl.ds(D, D)]

    def unit_rows(at, size):
        x = hid[pl.ds(at, size), :].astype(F32)
        center = jnp.mean(x, axis=1, keepdims=True)
        scale = lax.rsqrt(jnp.mean(x * x, axis=1, keepdims=True) - center * center + EPSILON)
        return (x - center) * scale, scale

    def part_of(at, size, k_rows, v_rows):
        return dot_nt(dq[pl.ds(at, size), :], wq[...]) + dot_nt(k_rows, wk[...]) + dot_nt(v_rows, wv[...])

    def gather(part, unit):
        return column_sum(part * unit), column_sum(part)

    def normed_rows(at, size, unit):
        norm_s[:, pl.ds(at, size)] = jnp.transpose(unit * gain_f + bias_f).astype(BF)

    part = part_of(their_c, half_c, dk[pl.ds(their_c, half_c), :], dv[pl.ds(their_c, half_c), :])
    send_c[...] = part.astype(BF)
    y_cont = remote(send_c, recv_c, across)
    unit, _ = unit_rows(their_c, half_c)
    gain_grad, bias_grad = gather(part, unit)
    normed_rows(their_c, half_c, unit)
    unit, scale_c = unit_rows(own_c, half_c)
    part = part_of(own_c, half_c, dk[pl.ds(own_c, half_c), :], dv[pl.ds(own_c, half_c), :])
    mine_s[pl.ds(half_p, half_c), :] = part
    unit_s[pl.ds(half_p, half_c), :] = unit
    g, b = gather(part, unit)
    gain_grad, bias_grad = gain_grad + g, bias_grad + b
    normed_rows(own_c, half_c, unit)

    each(after0)
    share.wait_recv()
    for i, total in enumerate((sum_k, sum_v)):
        loc_s[i, :, pl.ds(0, width - 128)] = total[:, pl.ds(0, width - 128)]
        loc_s[i, :, pl.ds(width - 128, 128)] = (
            total[:, pl.ds(width - 128, 128)].astype(F32) + far_s[i].astype(F32)
        ).astype(BF)
    part = part_of(their_p, half_p, loc_s[0, pl.ds(their_p, half_p), :], loc_s[1, pl.ds(their_p, half_p), :])
    send_p[...] = part.astype(BF)
    y_prompt = remote(send_p, recv_p, across)
    unit, _ = unit_rows(their_p, half_p)
    normed_rows(their_p, half_p, unit)
    g, b = gather(part, unit)
    gain_grad, bias_grad = gain_grad + g, bias_grad + b
    unit, scale_p = unit_rows(own_p, half_p)
    unit_s[pl.ds(0, half_p), :] = unit
    normed_rows(own_p, half_p, unit)
    part = part_of(own_p, half_p, loc_s[0, pl.ds(own_p, half_p), :], loc_s[1, pl.ds(own_p, half_p), :])
    mine_s[pl.ds(0, half_p), :] = part
    g, b = gather(part, unit)
    gain_grad, bias_grad = gain_grad + g, bias_grad + b

    blocks = 1 << bits
    block = D // blocks

    def keep(value, lane):
        low = value.astype(BF)
        for i in range(blocks):
            late_s[i // 2, i % 2, :, pl.ds(lane, width)] = low[i * block : (i + 1) * block, :]

    keep(dot_nn(norm_s[...], dq[...]), 0)
    q_bias = column_sum(dq[...].astype(F32))
    for i, rest in enumerate((dk, dv)):
        keep(
            dot_nn(norm_s[:, pl.ds(0, prompt)], loc_s[i])
            + dot_nn(norm_s[:, pl.ds(prompt, conts)], rest[pl.ds(prompt, conts), :]),
            (i + 1) * width,
        )
    v_bias = column_sum(loc_s[1].astype(F32)) + column_sum(dv[pl.ds(prompt, conts), :].astype(F32))

    def norm_back(total, unit, scale, mixed):
        shaped = total * gain_f
        return mixed.astype(F32) + scale * (
            shaped - jnp.mean(shaped, axis=1, keepdims=True) - unit * jnp.mean(shaped * unit, axis=1, keepdims=True)
        )

    small_s[...] = jnp.zeros_like(small_s)
    small_s[0:1, pl.ds(0, width)] = q_bias
    small_s[1:2, pl.ds(0, width)] = v_bias
    small_s[2:3, pl.ds(0, D)] = gain_grad
    small_s[3:4, pl.ds(0, D)] = bias_grad
    small = small_s[...]
    row_id = lax.broadcasted_iota(jnp.int32, (8, 128), 0)
    for i in range(blocks):
        narrow = window(small, i * (width // blocks))
        broad = window(small, i * block)
        tail = jnp.concatenate([ext[i, pl.ds(32, 16), :].astype(F32)[0:8], jnp.where(row_id < 2, narrow, broad)], axis=0)
        late_s[i // 2, i % 2, pl.ds(0, 32), pl.ds(3 * width, 128)] = ext[i, pl.ds(0, 32), :]
        late_s[i // 2, i % 2, pl.ds(32, 16), pl.ds(3 * width, 128)] = tail.astype(BF)

    def input_rows(arrived, at, size, scale, held, rows_at, sem):
        arrived[0].wait_recv()
        here = pl.ds(at, size)
        total = mine_s[here, :] + arrived[1][...].astype(F32)
        held[...] = norm_back(total, unit_s[here, :], scale, gmix[here, :]).astype(BF)
        back = remote(held, gin.at[pl.ds(rows_at, size), :], across)
        kept = pltpu.make_async_copy(held, gin.at[pl.ds(rows_at, size), :], loc_sems.at[sem])
        kept.start()
        return back, kept

    source = late_s
    stages = []
    for bit in range(bits):
        landing, kept = stage_refs[2 * bit], stage_refs[2 * bit + 1]
        mine = (device // (1 << bit)) % 2
        copy = remote(source.at[:, 1 - mine], landing, peers[bit])
        if bit == 0:
            back_c, keep_c = input_rows((y_cont, recv_c), half_p, half_c, scale_c, give_c, own_c, 0)
        if bit == 1:
            each(after1)
            back_p, keep_p = input_rows((y_prompt, recv_p), 0, half_p, scale_p, give_p, own_p, 1)
        if bit == 2:
            each(after2)
        if bit == 3:
            each(after3)
        copy.wait_recv()
        stages.append(copy)
        for i in range(landing.shape[0]):
            kept[i // 2, i % 2] = (source[i, mine].astype(F32) + landing[i].astype(F32)).astype(BF)
        source = kept
    late_out[...] = source[0, 0, :, pl.ds(0, 3 * width)].astype(F32)
    vec_s[...] = source[0, 0, :, pl.ds(3 * width, 128)]
    swap = remote(vec_s, vec_r, across)
    last_e = done_s.shape[1]
    early_out[:, pl.ds(0, last_e)] = done_s[...].astype(F32) + first_other[:, pl.ds(0, last_e)].astype(F32)
    rest_e = first_done.shape[1]
    early_out[:, pl.ds(last_e, rest_e)] = first_done[...].astype(F32) + first_other[:, pl.ds(last_e, rest_e)].astype(F32)
    settle()
    swap.wait_recv()
    own_v, got_v = vec_s[...].astype(F32), vec_r[...].astype(F32)
    vec_out[0:8, :] = own_v[0:8] + got_v[8:16]
    vec_out[8:16, :] = own_v[16:24] + got_v[24:32]
    vec_out[16:24, :] = own_v[32:40] + got_v[32:40]
    vec_out[24:32, :] = own_v[40:48] + jnp.where(row_id < 2, 0.0, got_v[40:48])
    for copy in stages + [share, y_cont, y_prompt, swap]:
        copy.wait_send()
    for copy in (back_c, back_p):
        copy.wait_recv()
        copy.wait_send()
    keep_c.wait()
    keep_p.wait()


def finish(hid, vec_all, dq, dk, dv, wq, wk, wv, gmix, ext, sum_k, sum_v, relay, first_done, first_other, packed):
    rows, width = dq.shape
    ranks = lax.axis_size("dp")
    bits = ranks.bit_length() - 1
    block = D // ranks
    prompt = sum_k.shape[0]
    conts = rows - prompt
    lanes = 3 * width + 128
    vmem = pl.BlockSpec(memory_space=pltpu.VMEM)
    hbm = pl.BlockSpec(memory_space=pl.ANY)
    shape = jax.ShapeDtypeStruct
    copies = 6 + bits
    cut = (packed.shape[-1] - EARLY * FIRST_CUT) // EARLY
    stages = []
    for bit in range(bits):
        left = ranks >> (bit + 1)
        stages.append(pltpu.VMEM((left, block, lanes), BF))
        stages.append(pltpu.VMEM((max(left // 2, 1), min(left, 2), block, lanes), BF))
    return pl.pallas_call(
        functools.partial(final_kernel, bits),
        in_specs=[vmem] * 15 + [hbm],
        out_specs=[hbm, vmem, vmem, vmem],
        out_shape=[shape((rows, D), BF), shape((block, 3 * width), F32), shape((32, 128), F32), shape((block, packed.shape[-1] // 2), F32)],
        scratch_shapes=[
            pltpu.VMEM((2, prompt, width), BF),
            pltpu.VMEM((2, prompt, 128), BF),
            pltpu.VMEM((rows // 2, D), F32),
            pltpu.VMEM((rows // 2, D), F32),
            pltpu.VMEM((D, rows), BF),
            pltpu.VMEM((conts // 2, D), BF),
            pltpu.VMEM((conts // 2, D), BF),
            pltpu.VMEM((prompt // 2, D), BF),
            pltpu.VMEM((prompt // 2, D), BF),
            pltpu.VMEM((conts // 2, D), BF),
            pltpu.VMEM((prompt // 2, D), BF),
            pltpu.VMEM((ranks // 2, 2, block, lanes), BF),
            pltpu.VMEM((8, D + 128), F32),
            pltpu.VMEM((block, 128), BF),
            pltpu.VMEM((block, 128), BF),
            pltpu.VMEM((block, EARLY * cut), BF),
            pltpu.SemaphoreType.DMA((copies,)),
            pltpu.SemaphoreType.DMA((copies,)),
            pltpu.SemaphoreType.DMA((2,)),
        ]
        + stages
        + reducer_scratch(EARLY, block, cut),
        compiler_params=pltpu.CompilerParams(vmem_limit_bytes=56 << 20, collective_id=1, has_side_effects=True),
        cost_estimate=pl.CostEstimate(flops=5 * 10**9, bytes_accessed=20 * 10**6, transcendentals=0),
        name="finish",
    )(hid, vec_all, dq, dk, dv, wq, wk, wv, gmix, ext, sum_k, sum_v, relay, first_done, first_other, packed)


def flip(value, axis, bit):
    return lax.ppermute(value, axis, [(i, i ^ (1 << bit)) for i in range(lax.axis_size(axis))])


def contract_rows(left, right):
    return lax.dot_general(left, right, (((0,), (0,)), ((), ())), preferred_element_type=F32)


def back_project(left, right):
    return lax.dot_general(left, right, (((1,), (1,)), ((), ())), preferred_element_type=F32)


def norm_rows(values, gain, bias):
    center = jnp.mean(values, axis=-1, keepdims=True)
    spread = jnp.mean(values * values, axis=-1, keepdims=True) - center * center
    scaled = lax.rsqrt(spread + EPSILON)
    unit_rows = (values - center) * scaled
    return (unit_rows * gain + bias, unit_rows, scaled)


def norm_back(grad_rows, gain, unit_rows, scaled):
    shaped = grad_rows * gain
    return scaled * (
        shaped
        - jnp.mean(shaped, axis=-1, keepdims=True)
        - unit_rows * jnp.mean(shaped * unit_rows, axis=-1, keepdims=True)
    )


def in_order(which, mine, other, axis):
    return jnp.where(
        which == 0,
        jnp.concatenate([mine, other], axis=axis),
        jnp.concatenate([other, mine], axis=axis),
    )


def halving(value, device):
    bits = lax.axis_size("dp").bit_length() - 1
    rows, columns = value.shape
    current = value
    for bit in range(bits):
        upper = device // (1 << bit) % 2
        left = bits - bit
        view = current.reshape((1 << (left - 1), 2, -1, columns))
        kept = lax.dynamic_index_in_dim(view, upper, 1, keepdims=False)
        sent = lax.dynamic_index_in_dim(view, 1 - upper, 1, keepdims=False)
        got = flip(sent, "dp", bit)
        current = (kept.astype(F32) + got.astype(F32)).astype(BF)
    return current.reshape(rows >> bits, columns)


def side_by_side(parts):
    total = sum(part.shape[0] for part in parts)
    row, at = jnp.zeros((total,), F32), 0
    for part in parts:
        size = part.shape[0]
        row = row + jnp.pad(part.astype(F32), (at, total - at - size))
        at += size
    return row[None]


def half_of(value, which):
    prompt, conts = CHUNK // 2, (value.shape[0] - CHUNK) // 2
    return jnp.concatenate(
        [
            lax.dynamic_slice_in_dim(value, which * prompt, prompt),
            lax.dynamic_slice_in_dim(value, CHUNK + which * conts, conts),
        ]
    )


def joined(which, mine, other):
    prompt = CHUNK // 2
    low = jnp.where(which == 0, mine, other)
    high = jnp.where(which == 0, other, mine)
    return jnp.concatenate([low[:prompt], high[:prompt], low[prompt:], high[prompt:]])


def body(
    hidden_in,
    cotangent,
    prompt_start,
    cont_gap,
    seg_len,
    dilation_rate,
    pre_gain,
    pre_bias,
    query_weight,
    query_bias,
    key_weight,
    value_weight,
    value_bias,
    sub_gain,
    sub_bias,
    out_weight,
    out_bias,
    mid_gain,
    mid_bias,
    inner_weight,
    inner_bias,
    ffn_gain,
    ffn_bias,
    outer_weight,
    outer_bias,
):
    device = lax.axis_index("dp")
    ranks = lax.axis_size("dp")
    group_id = device // GDEV
    member = device % GDEV
    tensor_id = lax.axis_index("tensor")
    core = device % 2
    width = query_weight.shape[1]
    units = inner_weight.shape[1]
    pairs = width // 128
    rows = hidden_in.shape[0]
    prompt_rows = CHUNK
    cont_count = (rows - prompt_rows) // CONT

    vectors = side_by_side(
        [
            pre_gain,
            pre_bias,
            query_bias,
            value_bias,
            ffn_gain,
            ffn_bias,
            inner_bias,
            sub_gain,
            sub_bias,
            out_bias,
            mid_gain,
            mid_bias,
            outer_bias,
        ]
    )
    pre_gain_f = pre_gain.astype(F32)

    (
        weighed,
        inverse,
        queries,
        keys,
        values,
        prompt_keys,
        prompt_values,
        attended,
        att_mine,
        att_got,
        *pieces,
        vectors_other,
    ) = attend(
        prompt_start,
        cont_gap,
        seg_len.T,
        dilation_rate.T,
        hidden_in,
        vectors,
        query_weight,
        key_weight,
        value_weight,
        inner_weight,
        out_weight,
    )
    inner_parts = (inner_weight, pieces[0], pieces[1])
    out_parts = (out_weight, pieces[2], pieces[3])

    fused = ranks == 16
    out_half, grad_mine, grad_theirs, grad_mixed_low, packed, sum_u, sum_w, sum_d, ext = middle(
        att_mine,
        att_got,
        hidden_in,
        cotangent,
        vectors,
        vectors_other,
        inner_parts,
        outer_weight,
        out_parts,
        ranks if fused else 1,
    )

    grad_query_in, own_key_grad, own_value_grad, key_sum, value_sum, relay, out_got, *early = attend_back(
        queries,
        keys,
        values,
        prompt_keys,
        prompt_values,
        attended,
        inverse,
        weighed,
        grad_mine,
        grad_theirs,
        out_half,
        packed.reshape(2, 2, 2, 2, D // ranks, -1) if fused else None,
    )
    if not fused:
        early = lax.psum_scatter(packed, "dp", scatter_dimension=0, tiled=True)
        early_mine, early_other = jnp.split(early, 2, axis=1)
        early_sum = early_mine.astype(F32) + flip(early_other, "tensor", 0).astype(F32)
    output = joined(tensor_id, out_half, out_got)
    block = D // ranks
    per_u, per_w, per_d = units // ranks, width // ranks, D // ranks
    if fused:
        input_low, late, vec, early_sum = finish(
            hidden_in,
            vectors,
            grad_query_in,
            own_key_grad,
            own_value_grad,
            query_weight,
            key_weight,
            value_weight,
            grad_mixed_low,
            ext,
            key_sum,
            value_sum,
            relay,
            *early,
            packed.reshape(2, 2, 2, 2, D // ranks, -1),
        )
        ffn_gain_grad, ffn_bias_grad, inner_bias_grad = [vec[i, :per_u] for i in range(3)]
        sub_gain_grad, sub_bias_grad = [vec[8 + i, :per_w] for i in range(2)]
        out_bias_grad, mid_gain_grad, mid_bias_grad, outer_bias_grad = [vec[16 + i, :per_d] for i in range(4)]
        query_bias_grad, value_bias_grad = [vec[24 + i, :per_w] for i in range(2)]
        pre_gain_grad, pre_bias_grad = [vec[26 + i, :per_d] for i in range(2)]
    else:
        pre_normed, pre_unit, pre_scale = norm_rows(hidden_in.astype(F32), pre_gain_f, pre_bias.astype(F32))
        pre_low = pre_normed.astype(BF)
        last = width - 128
        far = flip(relay, "dp", 1).astype(F32)
        summed = jnp.stack([key_sum, value_sum]).astype(F32)
        summed = jnp.concatenate([summed[:, :, :last], summed[:, :, last:] + far], axis=2).astype(BF)
        grad_keys = jnp.concatenate([summed[0], own_key_grad[prompt_rows:]], axis=0)
        grad_values = jnp.concatenate([summed[1], own_value_grad[prompt_rows:]], axis=0)

        query_weight_grad = contract_rows(pre_low, grad_query_in)
        key_weight_grad = contract_rows(pre_low, grad_keys)
        value_weight_grad = contract_rows(pre_low, grad_values)
        query_bias_grad = jnp.sum(grad_query_in.astype(F32), axis=0)
        value_bias_grad = jnp.sum(grad_values.astype(F32), axis=0)
        grad_normed_part = (
            back_project(grad_query_in, query_weight)
            + back_project(grad_keys, key_weight)
            + back_project(grad_values, value_weight)
        )
        grad_normed_low = grad_normed_part.astype(BF)
        grad_normed = grad_normed_low.astype(F32) + flip(grad_normed_low, "tensor", 0).astype(F32)
        pre_gain_grad = jnp.sum(grad_normed * pre_unit, axis=0)
        pre_bias_grad = jnp.sum(grad_normed, axis=0)
        grad_mixed_all = joined(tensor_id, grad_mixed_low, flip(grad_mixed_low, "tensor", 0)).astype(F32)
        input_low = (grad_mixed_all + norm_back(grad_normed, pre_gain_f, pre_unit, pre_scale)).astype(BF)

        vec = jnp.concatenate(
            [
                sum_u[:3].reshape(3, 2, ranks, per_u).transpose(2, 1, 0, 3).reshape(ranks, 6 * per_u),
                sum_w[:2].reshape(2, 2, ranks, per_w).transpose(2, 1, 0, 3).reshape(ranks, 4 * per_w),
                sum_d[:4].reshape(4, ranks, per_d).swapaxes(0, 1).reshape(ranks, 4 * per_d),
                jnp.stack([query_bias_grad, value_bias_grad]).reshape(2, ranks, per_w).swapaxes(0, 1).reshape(ranks, 2 * per_w),
                jnp.stack([pre_gain_grad, pre_bias_grad]).reshape(2, ranks, per_d).swapaxes(0, 1).reshape(ranks, 2 * per_d),
            ],
            axis=1,
        )
        count = vec.shape[1]
        vec = jnp.pad(vec, ((0, 0), (0, block * 128 - count))).reshape(D, 128)
        late = halving(
            jnp.concatenate(
                [p.astype(BF) for p in (query_weight_grad, key_weight_grad, value_weight_grad, vec)], axis=1
            ),
            device,
        )
        vec = late[:, 3 * width :].reshape(-1)[:count]
        late = late[:, : 3 * width].astype(F32)
        at_w = 6 * per_u
        at_d = at_w + 4 * per_w
        at_late = at_d + 4 * per_d
        got = flip(vec[:at_late], "tensor", 0).astype(F32)
        vec = vec.astype(F32)
        ffn_gain_grad, ffn_bias_grad, inner_bias_grad = (vec[: 3 * per_u] + got[3 * per_u : at_w]).reshape(3, per_u)
        sub_gain_grad, sub_bias_grad = (vec[at_w : at_w + 2 * per_w] + got[at_w + 2 * per_w : at_d]).reshape(2, per_w)
        out_bias_grad, mid_gain_grad, mid_bias_grad, outer_bias_grad = (vec[at_d:at_late] + got[at_d:]).reshape(4, per_d)
        query_bias_grad, value_bias_grad = vec[at_late : at_late + 2 * per_w].reshape(2, per_w)
        pre_gain_grad, pre_bias_grad = vec[at_late + 2 * per_w :].reshape(2, per_d)
    inner_weight_grad = early_sum[:, :units]
    outer_weight_grad = early_sum[:, units : 2 * units].T
    out_weight_grad = early_sum[:, 2 * units :].T
    return (
        output,
        input_low,
        pre_gain_grad,
        pre_bias_grad,
        late[:, :width],
        query_bias_grad,
        late[:, width : 2 * width],
        late[:, 2 * width : 3 * width],
        value_bias_grad,
        sub_gain_grad,
        sub_bias_grad,
        out_weight_grad,
        out_bias_grad,
        mid_gain_grad,
        mid_bias_grad,
        inner_weight_grad,
        inner_bias_grad,
        ffn_gain_grad,
        ffn_bias_grad,
        outer_weight_grad,
        outer_bias_grad,
    )

def solution(mesh):
    placed = (
        P("dp", None),
        P("dp", None),
        P(),
        P(),
        P(),
        P(),
        P(),
        P(),
        P(None, "tensor"),
        P("tensor"),
        P(None, "tensor"),
        P(None, "tensor"),
        P("tensor"),
        P("tensor"),
        P("tensor"),
        P("tensor", None),
        P(),
        P(),
        P(),
        P(None, "tensor"),
        P("tensor"),
        P("tensor"),
        P("tensor"),
        P("tensor", None),
        P(),
    )
    return jax.shard_map(
        body,
        mesh=mesh,
        in_specs=placed,
        out_specs=(
            P("dp", None),
            P("dp", None),
            P("dp"),
            P("dp"),
            P("dp", "tensor"),
            P(("tensor", "dp")),
            P("dp", "tensor"),
            P("dp", "tensor"),
            P(("tensor", "dp")),
            P(("tensor", "dp")),
            P(("tensor", "dp")),
            P("tensor", "dp"),
            P("dp"),
            P("dp"),
            P("dp"),
            P("dp", "tensor"),
            P(("tensor", "dp")),
            P(("tensor", "dp")),
            P(("tensor", "dp")),
            P("tensor", "dp"),
            P("dp"),
        ),
        check_vma=False,
    )
```

```python
import functools

import jax
import jax.numpy as jnp
from jax import lax
from jax.experimental import pallas as pl
from jax.experimental.pallas import tpu as pltpu
from jax.sharding import PartitionSpec as P

HD = 64
PROMPT = 2048
CONT = 256
GDEV = 4
TILE = 256
CHUNK = PROMPT // GDEV
PTILES = CHUNK // TILE
LOG2E = 1.4426950408889634
BF = jnp.bfloat16
F32 = jnp.float32
D = 768
EPSILON = 1e-05
MESH = pl.DeviceIdType.MESH


def dot_nt(a, b):
    return lax.dot_general(a, b, (((1,), (1,)), ((), ())), preferred_element_type=F32)


def dot_nn(a, b):
    return lax.dot_general(a, b, (((1,), (0,)), ((), ())), preferred_element_type=F32)


def low_half(rows):
    return lax.broadcasted_iota(jnp.int32, (rows, 128), 1) < HD


MASKED = -1e30
CLASSES = 36


def lane_classes(head):
    lane = lax.broadcasted_iota(jnp.int32, (8, 128), 1) - (HD if head == 0 else 0)
    number = lane.astype(F32)
    main = lane < CLASSES
    number = jnp.where(main, number, 4.0 * (number - CLASSES) + 3.0)
    number = jnp.where((lane >= 0) & (lane < CLASSES + CLASSES // 4), number, -5.0)
    combo = jnp.floor((number + 0.5) * 0.25)
    step0 = jnp.floor((combo + 0.5) * (1.0 / 3.0))
    step1 = combo - 3.0 * step0
    rest = number - 4.0 * combo
    flag1 = jnp.where(rest > 1.5, 1.0, 0.0)
    return number, step0, step1, flag1, rest - 2.0 * flag1, jnp.where(main, 0.0, 1.0)


def key_side(keys, first, cells, classes):
    size = keys.shape[0]
    at = first + lax.broadcasted_iota(jnp.int32, (8, size), 1).astype(F32)
    base = jnp.full((8, size), 0.0, F32) + first
    row = lax.broadcasted_iota(jnp.int32, (8, size), 0)

    def cell(i):
        return cells[i][:, 0:1]

    step0 = jnp.floor((at + 0.5) * cell(0)) - jnp.floor((base + 0.5) * cell(0))
    step1 = jnp.floor((at + 0.5) * cell(1)) - jnp.floor((base + 0.5) * cell(1))
    rest1 = at - cell(2) * jnp.floor((at + 0.5) * cell(3))
    rest2 = at - cell(4) * jnp.floor((at + 0.5) * cell(5))
    flag1 = jnp.where(rest1 == jnp.where(row == 0, cell(6), cell(7)), 2.0, 0.0)
    flag2 = jnp.where(rest2 == jnp.where(row == 0, cell(8), cell(9)), 1.0, 0.0)
    columns = jnp.transpose(4.0 * (3.0 * step0 + step1) + flag1 + flag2)
    low = low_half(size)
    hot = [jnp.where(columns[:, h : h + 1] == classes[h][0][0:1], 1.0, 0.0).astype(BF) for h in range(2)]
    return [jnp.where(low, keys, hot[0]), jnp.where(low, hot[1], keys)]


def query_side(head, queries, qc, first, cells, lanes, low):
    _, step0, step1, flag1, flag2, small = lanes
    base = jnp.zeros((8, 128), F32) + first
    kc0 = (jnp.floor((base + 0.5) * cells[0]) + step0)[0:1]
    kc1 = jnp.where(flag1 > 0.5, jnp.floor((base + 0.5) * cells[1]) + step1, -1.0)[0:1]
    weight = jnp.where(qc[0] == kc0, 1.0, 0.0) + jnp.where(qc[1 + head] == kc1, 1.0, 0.0)
    weight = weight + qc[3 + head] * flag2[0:1]
    logs = jnp.maximum(jnp.log2(weight), MASKED)
    logs = jnp.where(small[0:1] > 0.5, logs - logs.astype(BF).astype(F32), logs).astype(BF)
    return jnp.where(low, queries, logs) if head == 0 else jnp.where(low, logs, queries)


def settings(seg, rate, pair):
    def row(value):
        return jnp.full((1, 128), value, jnp.int32).astype(F32)

    def rest(number, period):
        return number - period * jnp.floor((number + 0.5) / period)

    second, third = row(rate[1, pair]), row(rate[2, pair])
    head = row(2 * pair)
    return (
        1.0 / row(seg[0, pair]),
        1.0 / row(seg[1, pair]),
        second,
        1.0 / second,
        third,
        1.0 / third,
        rest(head, second),
        rest(head + 1.0, second),
        rest(head, third),
        rest(head + 1.0, third),
    )


def codes(at, cells, miss):
    first = jnp.floor((at + 0.5) * cells[0])
    second = jnp.floor((at + 0.5) * cells[1])
    rest1 = at - cells[2] * jnp.floor((at + 0.5) * cells[3])
    rest2 = at - cells[4] * jnp.floor((at + 0.5) * cells[5])
    return [
        first,
        jnp.where(rest1 == cells[6], second, miss),
        jnp.where(rest1 == cells[7], second, miss),
        jnp.where(rest2 == cells[8], 1.0, 0.0),
        jnp.where(rest2 == cells[9], 1.0, 0.0),
    ]


def bit_peer(device, bit):
    step = 1 << bit
    return device + (1 - 2 * ((device // step) % 2)) * step


def greet(peers):
    barrier = pltpu.get_barrier_semaphore()
    for peer in peers:
        pl.semaphore_signal(barrier, inc=1, device_id=peer, device_id_type=MESH)
    pl.semaphore_wait(barrier, len(peers))


def xor_bits(a, b):
    return (a % 2 + b % 2) % 2 + 2 * ((a // 2 + b // 2) % 2)


def fwd_kernel(
    starts, gaps, seg, rate, hid, vec, wq, wk, wv, w1, wo, vec_hbm,
    e_ref, li_ref, q_out, k_out, v_out, kp_out, vp_out, o_out, mine_out, got_out,
    w1_got, w1_swap, wo_got, wo_swap, vec_got,
    t_s, ka_s, kv_s, low_s, q_s, qe_s, ko_s, vo_s, o_s, sems_a, sems_b, loc_sems,
):
    pair = pl.program_id(0)
    step = pl.program_id(1)
    pairs = pl.num_programs(0)
    device = lax.axis_index("dp")
    side = lax.axis_index("tensor")
    member = device % GDEV
    core = device % 2
    rows, width = q_s.shape
    n_pairs = width // 128
    last_pair = n_pairs - 1
    conts = rows - CHUNK
    near = {"dp": bit_peer(device, 0), "tensor": side}
    far = {"dp": bit_peer(device, 1), "tensor": side}
    across = {"dp": device, "tensor": 1 - side}
    half_u = w1.shape[1] // 2
    half_w = wo.shape[0] // 2
    half_p, half_c = CHUNK // 2, conts // 2
    sent_u = pl.multiple_of(core * half_u, 128)
    shared_at = 2 * D + 2 * width
    sent_w = pl.multiple_of(core * half_w, 64)

    def remote(i, src, dst, peer):
        return pltpu.make_async_remote_copy(
            src_ref=src, dst_ref=dst, send_sem=sems_a.at[i], recv_sem=sems_b.at[i], device_id=peer, device_id_type=MESH
        )

    def to_far(p):
        lanes = pl.ds(p * 128, 128)
        return remote(3 * p, kv_s.at[0, :, :, lanes], kv_s.at[2, :, :, lanes], far)

    def to_near(p):
        lanes = pl.ds(p * 128, 128)
        return remote(3 * p + 1, kv_s.at[0, :, :, lanes], kv_s.at[1, :, :, lanes], near)

    def relay(p):
        lanes = pl.ds(p * 128, 128)
        return remote(3 * p + 2, kv_s.at[2, :, :, lanes], kv_s.at[3, :, :, lanes], near)

    base = 3 * n_pairs
    fetch_y = [
        remote(base, wo.at[pl.ds(sent_w, half_w), :], wo_got, across),
        remote(base + 1, w1.at[:, pl.ds(sent_u, half_u)], w1_got, across),
        remote(base + 2, vec_hbm.at[:, pl.ds(shared_at, vec_got.shape[1])], vec_got, across),
    ]
    fetch_core = [
        remote(base + 3, wo_got, wo_swap, near),
        remote(base + 4, w1_got, w1_swap, near),
    ]

    def give(p, piece):
        lanes = pl.ds(p * 128, 128)
        their_p = pl.multiple_of((1 - side) * half_p, 128)
        their_c = pl.multiple_of(CHUNK + (1 - side) * half_c, 128)
        third = half_c // 3
        if piece == 0:
            source, target = pl.ds(their_p, half_p), pl.ds(0, half_p)
        else:
            source = pl.ds(pl.multiple_of(their_c + (piece - 1) * third, 128), third)
            target = pl.ds(half_p + (piece - 1) * third, third)
        return remote(base + 5 + 4 * p + piece, o_s.at[source, lanes], got_out.at[target, lanes], across)

    def keeps():
        own_p = pl.multiple_of(side * half_p, 128)
        own_c = pl.multiple_of(CHUNK + side * half_c, 128)
        return [
            pltpu.make_async_copy(o_s, o_out, loc_sems.at[0]),
            pltpu.make_async_copy(o_s.at[pl.ds(own_p, half_p), :], mine_out.at[pl.ds(0, half_p), :], loc_sems.at[1]),
            pltpu.make_async_copy(o_s.at[pl.ds(own_c, half_c), :], mine_out.at[pl.ds(half_p, half_c), :], loc_sems.at[2]),
        ]

    def saves():
        out = [
            pltpu.make_async_copy(q_s, q_out, loc_sems.at[3]),
            pltpu.make_async_copy(ko_s, k_out, loc_sems.at[0]),
            pltpu.make_async_copy(vo_s, v_out, loc_sems.at[5]),
        ]
        for r in range(GDEV):
            span = pl.ds(r * CHUNK, CHUNK)
            out.append(pltpu.make_async_copy(kv_s.at[r, 0], kp_out.at[span, :], loc_sems.at[6 + 2 * r]))
            out.append(pltpu.make_async_copy(kv_s.at[r, 1], vp_out.at[span, :], loc_sems.at[7 + 2 * r]))
        return out

    @pl.when((pair == 0) & (step == 0))
    def _():
        greet([near, far, across])
        for copy in fetch_y:
            copy.start()
        gain_f, bias_f = vec[:, pl.ds(0, D)], vec[:, pl.ds(D, D)]
        query_bias = vec[:, pl.ds(2 * D, width)]
        value_bias = vec[:, pl.ds(2 * D + width, width)]

        def norm(at, size):
            x = hid[at : at + size, :].astype(F32)
            center = jnp.mean(x, axis=1, keepdims=True)
            scale = lax.rsqrt(jnp.mean(x * x, axis=1, keepdims=True) - center * center + EPSILON)
            low = ((x - center) * scale * gain_f + bias_f).astype(BF)
            low_s[at : at + size, :] = low
            return low

        low = norm(0, CHUNK)
        kv_s[0, 0] = dot_nn(low, wk[...]).astype(BF)
        kv_s[0, 1] = (dot_nn(low, wv[...]) + value_bias).astype(BF)
        to_far(0).start()
        for p in range(n_pairs):
            to_near(p).start()
        for at in range(CHUNK, rows, TILE):
            low = norm(at, TILE)
            ko_s[at - CHUNK : at - CHUNK + TILE, :] = dot_nn(low, wk[...]).astype(BF)
            vo_s[at - CHUNK : at - CHUNK + TILE, :] = (dot_nn(low, wv[...]) + value_bias).astype(BF)
        to_far(0).wait_send()
        for p in range(1, n_pairs):
            to_far(p).start()
        for at in range(0, rows, TILE):
            scaled = (dot_nn(low_s[at : at + TILE, :], wq[...]) + query_bias) * 0.125
            q_s[at : at + TILE, :] = scaled.astype(BF)
            qe_s[at : at + TILE, :] = (scaled * LOG2E).astype(BF)
        to_far(0).wait_recv()
        relay(0).start()

    for p in range(n_pairs):
        @pl.when((pair == p) & (step == 0))
        def _():
            to_near(p).wait_recv()
            relay(p).wait_recv()

        if p + 1 < n_pairs:
            @pl.when((pair == p) & (step == 3))
            def _():
                to_far(p + 1).wait_recv()
                relay(p + 1).start()

    lanes = pl.ds(pl.multiple_of(pair * 128, 128), 128)
    low = low_half(TILE)
    q = qe_s[pl.ds(pl.multiple_of(step * TILE, TILE), TILE), lanes]
    row = lax.broadcasted_iota(jnp.int32, (TILE, 128), 0).astype(F32)
    group = device // GDEV
    start = starts[group]
    first_cont = member * (conts // CONT)
    own_gap = gaps[group, first_cont + jnp.maximum(step - PTILES, 0)]
    base_q = start + jnp.where(step < PTILES, member * CHUNK + step * TILE, PROMPT + own_gap)
    cells = settings(seg, rate, side * n_pairs + pair)
    at_q = base_q.astype(F32) + row
    qc = codes(at_q, cells, -2.0)
    classes = [lane_classes(h) for h in range(2)]
    first_at = start.astype(F32)

    @pl.when(step == 0)
    def _():
        for j in range(GDEV):
            first = first_at + (xor_bits(j, member) * CHUNK).astype(F32)
            for h, made in enumerate(key_side(kv_s[j, 0, :, lanes], first, cells, classes)):
                ka_s[h, j * CHUNK : (j + 1) * CHUNK, :] = made

    def logits(h, top, keys, first, causal, at, width):
        t = dot_nt(query_side(h, q, qc, first, cells, classes[h], low), keys)
        if causal is not None:
            t = jnp.where(causal, t, MASKED)
        t_s[h, :, pl.ds(at, width)] = t
        for g in range(width // 128):
            top = jnp.maximum(top, t[:, g * 128 : (g + 1) * 128])
        return top

    def weigh(h, carry, vals, m, at, width):
        total, acc = carry
        parts = []
        for g in range(width // 128):
            e = jnp.exp2(t_s[h, :, pl.ds(at + g * 128, 128)] - m)
            total = total + e
            parts.append(e.astype(BF))
        el = jnp.concatenate(parts, axis=1)
        e_ref[h, :, pl.ds(at, width)] = el
        return total, acc + dot_nn(el, vals)

    def finish_rows(carry):
        (sums0, acc0), (sums1, acc1) = carry
        sums, accs = (sums0, sums1), (acc0, acc1)
        li = [1.0 / jnp.sum(s, axis=1, keepdims=True) for s in sums]
        lfull = jnp.where(low, li[0], li[1])
        li_ref[...] = lfull
        o_s[pl.ds(pl.multiple_of(step * TILE, TILE), TILE), lanes] = (jnp.where(low, accs[0], accs[1]) * lfull).astype(BF)

    def tops(mx):
        return jnp.broadcast_to(jnp.max(mx, axis=1, keepdims=True), (TILE, 128))

    neg = jnp.full((TILE, 128), -jnp.inf, F32)
    zf = jnp.zeros((TILE, 128), F32)

    def held_keys(h, at):
        return ka_s[h, pl.ds(at, CHUNK), :]

    @pl.when(step < PTILES)
    def _():
        rows_id = lax.broadcasted_iota(jnp.int32, (TILE, CHUNK), 0) + step * TILE
        cols = lax.broadcasted_iota(jnp.int32, (TILE, CHUNK), 1)
        here = first_at + (member * CHUNK).astype(F32)

        def place(j):
            return pl.multiple_of(xor_bits(j, member) * CHUNK, CHUNK)

        def score(h, j, top):
            return logits(h, top, held_keys(h, place(j)), first_at + (j * CHUNK).astype(F32), None, place(j), CHUNK)

        def spread(h, j, m, carry):
            return weigh(h, carry, kv_s[xor_bits(j, member), 1, :, lanes], m, place(j), CHUNK)

        top = lax.fori_loop(0, member, lambda j, top: score(0, j, top), neg)
        m0 = tops(logits(0, top, held_keys(0, 0), here, cols <= rows_id, 0, CHUNK))

        def both(j, carry):
            return spread(0, j, m0, carry[0]), score(1, j, carry[1])

        first, top = lax.fori_loop(0, member, both, ((zf, zf), neg))
        first = weigh(0, first, kv_s[0, 1, :, lanes], m0, 0, CHUNK)
        m1 = tops(logits(1, top, held_keys(1, 0), here, cols <= rows_id, 0, CHUNK))
        finish_rows((first, lax.fori_loop(0, member + 1, lambda j, carry: spread(1, j, m1, carry), (zf, zf))))

    @pl.when(step >= PTILES)
    def _():
        own_rows = pl.ds(pl.multiple_of((step - PTILES) * TILE, TILE), TILE)
        rows_id = lax.broadcasted_iota(jnp.int32, (TILE, CONT), 0)
        cols = lax.broadcasted_iota(jnp.int32, (TILE, CONT), 1)
        own_at = base_q.astype(F32)
        own = key_side(ko_s[own_rows, lanes], own_at, cells, classes)

        def score(h, j, top):
            if j == GDEV:
                return logits(h, top, own[h], own_at, cols <= rows_id, PROMPT, CONT)
            first = first_at + (xor_bits(j, member) * CHUNK).astype(F32)
            return logits(h, top, held_keys(h, j * CHUNK), first, None, j * CHUNK, CHUNK)

        def spread(h, j, m, carry):
            if j == GDEV:
                return weigh(h, carry, vo_s[own_rows, lanes], m, PROMPT, CONT)
            return weigh(h, carry, kv_s[j, 1, :, lanes], m, j * CHUNK, CHUNK)

        top = neg
        for j in range(GDEV + 1):
            top = score(0, j, top)
        m0, top, first, second = tops(top), neg, (zf, zf), (zf, zf)
        for j in range(GDEV + 1):
            first = spread(0, j, m0, first)
            top = score(1, j, top)
        m1 = tops(top)
        for j in range(GDEV + 1):
            second = spread(1, j, m1, second)
        finish_rows((first, second))

    end = pl.num_programs(1) - 1
    for p in range(n_pairs):
        @pl.when((pair == p) & (step == 1 - side))
        def _():
            give(p, 0).start()

        for unit in range(6):
            @pl.when((pair == p) & (step == PTILES + unit // 2) & (side == 1 - unit // 3))
            def _():
                give(p, 1 + unit % 3).start()

    @pl.when((pair == last_pair - 1) & (step == 3))
    def _():
        for i in range(2):
            fetch_y[i].wait_recv()
            fetch_core[i].start()

    @pl.when((pair == last_pair) & (step == 0))
    def _():
        for copy in saves():
            copy.start()

    @pl.when((pair == last_pair) & (step == end))
    def _():
        for copy in keeps():
            copy.start()
        fetch_y[2].wait_recv()
        for copy in fetch_core:
            copy.wait_recv()
        for p in range(n_pairs):
            for piece in range(4):
                copy = give(p, piece)
                copy.wait_recv()
                copy.wait_send()
            if p > 0:
                to_far(p).wait_send()
            to_near(p).wait_send()
            relay(p).wait_send()
        for copy in fetch_y + fetch_core:
            copy.wait_send()
        for copy in keeps() + saves():
            copy.wait()


def attend(starts, gaps, seg, rate, hid, vec, wq, wk, wv, w1, wo):
    rows = hid.shape[0]
    width = wq.shape[1]
    pairs = width // 128
    span = PROMPT + CONT
    conts = rows - CHUNK
    units = w1.shape[1]
    vmem = pl.BlockSpec(memory_space=pltpu.VMEM)
    hbm = pl.BlockSpec(memory_space=pl.ANY)
    shape = jax.ShapeDtypeStruct
    copies = 3 * pairs + 5 + 4 * pairs
    shared = 3 * units + 2 * width
    smem = pl.BlockSpec(memory_space=pltpu.SMEM)
    return pl.pallas_call(
        fwd_kernel,
        grid_spec=pltpu.PrefetchScalarGridSpec(
            num_scalar_prefetch=0,
            grid=(pairs, rows // TILE),
            in_specs=[smem] * 4 + [vmem] * 5 + [hbm] * 3,
            out_specs=[
                pl.BlockSpec((2, TILE, span), lambda a, t: (a, t, 0)),
                pl.BlockSpec((TILE, 128), lambda a, t: (t, a)),
            ]
            + [hbm] * 13,
            scratch_shapes=[
                pltpu.VMEM((2, TILE, span), F32),
                pltpu.VMEM((2, PROMPT, 128), BF),
                pltpu.VMEM((GDEV, 2, CHUNK, width), BF),
                pltpu.VMEM((rows, D), BF),
                pltpu.VMEM((rows, width), BF),
                pltpu.VMEM((rows, width), BF),
                pltpu.VMEM((conts, width), BF),
                pltpu.VMEM((conts, width), BF),
                pltpu.VMEM((rows, width), BF),
                pltpu.SemaphoreType.DMA((copies,)),
                pltpu.SemaphoreType.DMA((copies,)),
                pltpu.SemaphoreType.DMA((6 + 2 * GDEV,)),
            ],
        ),
        out_shape=[
            shape((2 * pairs, rows, span), BF),
            shape((rows, width), F32),
            shape((rows, width), BF),
            shape((conts, width), BF),
            shape((conts, width), BF),
            shape((PROMPT, width), BF),
            shape((PROMPT, width), BF),
            shape((rows, width), BF),
            shape((rows // 2, width), BF),
            shape((rows // 2, width), BF),
            shape((D, units // 2), BF),
            shape((D, units // 2), BF),
            shape((width // 2, D), BF),
            shape((width // 2, D), BF),
            shape((1, shared), F32),
        ],
        compiler_params=pltpu.CompilerParams(vmem_limit_bytes=56 << 20, collective_id=0, has_side_effects=True),
        cost_estimate=pl.CostEstimate(flops=20 * 10**9, bytes_accessed=60 * 10**6, transcendentals=0),
        name="attend",
    )(starts, gaps, seg, rate, hid, vec, wq, wk, wv, w1, wo, vec)


EARLY = 2
FIRST_CUT = 1920


def reducer_scratch(count, block, cut):
    return [
        pltpu.VMEM((count, 2, 2, 2, block, cut), BF),
        pltpu.VMEM((count, 2, 2, 2, block, cut), BF),
        pltpu.VMEM((count, 2, 2, block, cut), BF),
        pltpu.VMEM((count, 2, 2, block, cut), BF),
        pltpu.VMEM((count, 2, block, cut), BF),
        pltpu.VMEM((count, 2, block, cut), BF),
        pltpu.VMEM((count, block, cut), BF),
        pltpu.SemaphoreType.DMA((4 * count,)),
        pltpu.SemaphoreType.DMA((4 * count,)),
        pltpu.SemaphoreType.DMA((count,)),
    ]


def reducer(packed, device, side, base, refs, done):
    held, got0, got1, held1, got2, held2, got3, sems_a, sems_b, sems_l = refs
    bit = [(device // (1 << b)) % 2 for b in range(4)]
    peers = [{"dp": bit_peer(device, b), "tensor": side} for b in range(4)]
    cut = held.shape[-1]

    def passing(c, stage, source, target, peer):
        return pltpu.make_async_remote_copy(
            src_ref=source,
            dst_ref=target,
            send_sem=sems_a.at[4 * c + stage],
            recv_sem=sems_b.at[4 * c + stage],
            device_id=peer,
            device_id_type=MESH,
        )

    count = held.shape[0]

    def columns_of(c, first):
        return pl.ds(first + (count - 1 - c) * cut, cut)

    def own_half(c):
        return pltpu.make_async_copy(packed.at[:, :, :, bit[0], :, columns_of(c, base)], held.at[c], sems_l.at[c])

    def stage0(c):
        return passing(c, 0, packed.at[:, :, :, 1 - bit[0], :, columns_of(c, base)], got0.at[c], peers[0])

    def stage1(c):
        if c % 2:
            return passing(c, 1, held.at[c, :, 1 - bit[2]], got1.at[c], peers[2])
        return passing(c, 1, held.at[c, :, :, 1 - bit[1]], got1.at[c], peers[1])

    def stage2(c):
        b = 1 if c % 2 else 2
        return passing(c, 2, held1.at[c, :, 1 - bit[b]], got2.at[c], peers[b])

    def stage3(c):
        return passing(c, 3, held2.at[c, 1 - bit[3]], got3.at[c], peers[3])

    def begin(c):
        own_half(c).start()
        stage0(c).start()

    def after0(c):
        own_half(c).wait()
        stage0(c).wait_recv()
        held[c] = held[c] + got0[c]
        stage1(c).start()

    def after1(c):
        stage1(c).wait_recv()
        kept = held[c, :, bit[2]] if c % 2 else held[c, :, :, bit[1]]
        held1[c] = kept + got1[c]
        stage2(c).start()

    def after2(c):
        stage2(c).wait_recv()
        held2[c] = held1[c, :, bit[1 if c % 2 else 2]] + got2[c]
        stage3(c).start()

    def after3(c):
        stage3(c).wait_recv()
        done[:, columns_of(c, 0)] = held2[c, bit[3]] + got3[c]

    def settle():
        for c in range(count):
            for copy in (stage0(c), stage1(c), stage2(c), stage3(c)):
                copy.wait_send()

    return begin, after0, after1, after2, after3, settle


def bwd_kernel(
    fused, q_ref, kp_ref, vp_ref, ko_ref, vo_ref, o_ref, li_ref, e_ref, g_mine, g_theirs, out_half, *refs
):
    packed = refs[0] if fused else None
    refs = refs[1:] if fused else refs
    dq_ref, dko_ref, dvo_ref, sum_k, sum_v, relay_out, out_got = refs[:7]
    done_out, other_out = refs[7:9] if fused else (None, None)
    refs = refs[9:] if fused else refs[7:]
    dk_s, dv_s, g_s, grad_s, near_s, relay_s, far_s, sems_a, sems_b, loc_sems = refs[:10]
    pair = pl.program_id(0)
    step = pl.program_id(1)
    device = lax.axis_index("dp")
    side = lax.axis_index("tensor")
    member = device % GDEV
    rows, width = g_s.shape
    n_pairs = width // 128
    conts = rows - CHUNK
    half_p, half_c = CHUNK // 2, conts // 2
    near = {"dp": bit_peer(device, 0), "tensor": side}
    far = {"dp": bit_peer(device, 1), "tensor": side}
    across = {"dp": device, "tensor": 1 - side}
    lanes = pl.ds(pl.multiple_of(pair * 128, 128), 128)
    mine_p = pl.ds(pl.multiple_of(side * half_p, 128), half_p)
    mine_c = pl.ds(pl.multiple_of(CHUNK + side * half_c, 128), half_c)

    def remote(i, src, dst, peer):
        return pltpu.make_async_remote_copy(
            src_ref=src, dst_ref=dst, send_sem=sems_a.at[i], recv_sem=sems_b.at[i], device_id=peer, device_id_type=MESH
        )

    def heads():
        return [
            remote(0, g_theirs.at[pl.ds(0, half_p), :], g_s.at[mine_p, :], across),
            remote(1, g_theirs.at[pl.ds(half_p, half_c), :], g_s.at[mine_c, :], across),
            remote(2, out_half, out_got, across),
        ]

    def local():
        return [
            pltpu.make_async_copy(g_mine.at[pl.ds(0, half_p), :], g_s.at[mine_p, :], loc_sems.at[0]),
            pltpu.make_async_copy(g_mine.at[pl.ds(half_p, half_c), :], g_s.at[mine_c, :], loc_sems.at[1]),
        ]

    def cores(p):
        part = pl.ds(p * 128, 128)
        return remote(3 + 2 * p, grad_s.at[:, :, 1, :, part], near_s.at[:, :, :, part], near)

    def chips(p):
        part = pl.ds(p * 128, 128)
        return remote(4 + 2 * p, relay_s.at[:, :, part], far_s.at[:, :, part], far)

    if fused:
        *early_refs, done_s, other_a, early_sems = refs[10:]
        begin, after0, after1, after2, after3, settle = reducer(
            packed, device, side, packed.shape[-1] - EARLY * FIRST_CUT, early_refs, done_s
        )
        half_e = packed.shape[-1] // 2
        tail_e = EARLY * FIRST_CUT - half_e
        peers = [{"dp": bit_peer(device, b), "tensor": side} for b in range(4)]
        swap = pltpu.make_async_remote_copy(
            src_ref=done_s.at[:, pl.ds(tail_e, half_e)],
            dst_ref=other_a,
            send_sem=early_sems.at[0],
            recv_sem=early_sems.at[1],
            device_id=across,
            device_id_type=MESH,
        )
        tick = pair * pl.num_programs(1) + step

    @pl.when((pair == 0) & (step == 0))
    def _():
        greet([near, far, across] + (peers[2:] if fused else []))
        for copy in heads() + local():
            copy.start()
        for copy in local():
            copy.wait()

    if fused:
        for c in range(EARLY):
            for at, act in ((0, begin), (1 + c, after0), (5 + c, after1), (8 + c, after2), (12, after3)):
                @pl.when(tick == at)
                def _():
                    act(c)

        @pl.when(tick == 12)
        def _():
            swap.start()

    @pl.when((pair == 0) & (step == 1 - side))
    def _():
        heads()[0].wait_recv()

    @pl.when((pair == 0) & (step == 3 - side))
    def _():
        heads()[1].wait_recv()

    low = low_half(TILE)
    g = g_s[pl.ds(pl.multiple_of(step * TILE, TILE), TILE), lanes].astype(F32) * li_ref[...]
    prod = g * o_ref[...].astype(F32)
    zf = jnp.zeros((TILE, 128), F32)
    deltas = [
        jnp.sum(jnp.where(low, prod, zf), axis=1, keepdims=True),
        jnp.sum(jnp.where(low, zf, prod), axis=1, keepdims=True),
    ]
    gs = [jnp.where(low, g, zf).astype(BF), jnp.where(low, zf, g).astype(BF)]
    gt = jnp.transpose(g).astype(BF)
    qt = jnp.transpose(q_ref[...].astype(F32)).astype(BF)

    def grads(dq, keys, vals, at, width):
        out, dks, dvs = [], [], []
        for h in range(2):
            e = e_ref[h, :, pl.ds(at, width)]
            dp = dot_nt(gs[h], vals)
            ds = (e.astype(F32) * (dp - deltas[h])).astype(BF)
            out.append(dq[h] + dot_nn(ds, keys))
            dks.append(dot_nn(qt[h * HD : (h + 1) * HD, :], ds))
            dvs.append(dot_nn(gt[h * HD : (h + 1) * HD, :], e))
        return tuple(out), dks, dvs

    @pl.when(step == 0)
    def _():
        dk_s[...] = jnp.zeros_like(dk_s)
        dv_s[...] = jnp.zeros_like(dv_s)

    def add(at, width, dks, dvs):
        for h in range(2):
            dk_s[h * HD : (h + 1) * HD, pl.ds(at, width)] += dks[h]
            dv_s[h * HD : (h + 1) * HD, pl.ds(at, width)] += dvs[h]

    def scaled(dq):
        return (jnp.where(low, dq[0], dq[1]).astype(BF).astype(F32) * 0.125).astype(BF)

    @pl.when(step < PTILES)
    def _():
        def one(j, dq):
            at = pl.multiple_of(xor_bits(j, member) * CHUNK, CHUNK)
            dq, dks, dvs = grads(dq, kp_ref[pl.ds(at, CHUNK), :], vp_ref[pl.ds(at, CHUNK), :], at, CHUNK)
            add(at, CHUNK, dks, dvs)
            return dq

        dq_ref[...] = scaled(lax.fori_loop(0, member + 1, one, (zf, zf)))
        dko_ref[...] = jnp.zeros_like(dko_ref)
        dvo_ref[...] = jnp.zeros_like(dvo_ref)

    @pl.when(step >= PTILES)
    def _():
        dq = (zf, zf)
        for j in range(GDEV):
            span = slice(j * CHUNK, (j + 1) * CHUNK)
            dq, dks, dvs = grads(dq, kp_ref[span, :], vp_ref[span, :], j * CHUNK, CHUNK)
            add(j * CHUNK, CHUNK, dks, dvs)
        dq, dks, dvs = grads(dq, ko_ref[...], vo_ref[...], PROMPT, CONT)
        dq_ref[...] = scaled(dq)
        dko_ref[...] = jnp.transpose(jnp.concatenate(dks, axis=0)).astype(BF)
        dvo_ref[...] = jnp.transpose(jnp.concatenate(dvs, axis=0)).astype(BF)

    end = pl.num_programs(1) - 1

    @pl.when(step == end)
    def _():
        for j in range(GDEV):
            span = slice(j * CHUNK, (j + 1) * CHUNK)
            grad_s[0, j // 2, j % 2, :, lanes] = jnp.transpose(dk_s[:, span]).astype(BF)
            grad_s[1, j // 2, j % 2, :, lanes] = jnp.transpose(dv_s[:, span]).astype(BF)

    for p in range(n_pairs):
        @pl.when((pair == p) & (step == end))
        def _():
            cores(p).start()

        if p + 1 < n_pairs:
            @pl.when((pair == p + 1) & (step == 2))
            def _():
                part = pl.ds(p * 128, 128)
                cores(p).wait_recv()
                relay_s[:, :, part] = (
                    grad_s[:, 1, 0, :, part].astype(F32) + near_s[:, 1, :, part].astype(F32)
                ).astype(BF)
                chips(p).start()

    @pl.when((pair == n_pairs - 1) & (step == end))
    def _():
        last = n_pairs - 1
        sums = (sum_k, sum_v)
        for p in range(last):
            part = pl.ds(p * 128, 128)
            chips(p).wait_recv()
            for i in range(2):
                sums[i][:, part] = (
                    grad_s[i, 0, 0, :, part].astype(F32) + near_s[i, 0, :, part].astype(F32) + far_s[i, :, part].astype(F32)
                ).astype(BF)
        part = pl.ds(last * 128, 128)
        cores(last).wait_recv()
        for i in range(2):
            relay_out[i] = (grad_s[i, 1, 0, :, part].astype(F32) + near_s[i, 1, :, part].astype(F32)).astype(BF)
            sums[i][:, part] = (grad_s[i, 0, 0, :, part].astype(F32) + near_s[i, 0, :, part].astype(F32)).astype(BF)
        if fused:
            swap.wait_recv()
            done_out[...] = done_s[:, pl.ds(0, tail_e)]
            other_out[...] = other_a[...]
            settle()
            swap.wait_send()
        heads()[2].wait_recv()
        for copy in heads():
            copy.wait_send()
        for p in range(n_pairs):
            cores(p).wait_send()
            if p < last:
                chips(p).wait_send()


def attend_back(q, k, v, kp, vp, o, li, e, g_mine, g_theirs, out_half, packed):
    rows, width = q.shape
    pairs = width // 128
    span = PROMPT + CONT
    tile = pl.BlockSpec((TILE, 128), lambda a, t: (t, a))
    whole = pl.BlockSpec((PROMPT, 128), lambda a, t: (0, a))
    own = pl.BlockSpec((TILE, 128), lambda a, t: (jnp.maximum(t - PTILES, 0), a))
    vmem = pl.BlockSpec(memory_space=pltpu.VMEM)
    hbm = pl.BlockSpec(memory_space=pl.ANY)
    shape = jax.ShapeDtypeStruct
    copies = 3 + 2 * pairs
    fused = packed is not None
    more_in, more_out, more_scratch = [], [], []
    if fused:
        block, half_e = packed.shape[-2], packed.shape[-1] // 2
        more_in = [packed]
        more_out = [shape((block, EARLY * FIRST_CUT - half_e), BF), shape((block, half_e), BF)]
        more_scratch = reducer_scratch(EARLY, block, FIRST_CUT) + [
            pltpu.VMEM((block, EARLY * FIRST_CUT), BF),
            pltpu.VMEM((block, half_e), BF),
            pltpu.SemaphoreType.DMA((2,)),
        ]
    return pl.pallas_call(
        functools.partial(bwd_kernel, fused),
        grid=(pairs, rows // TILE),
        in_specs=[tile, whole, whole, own, own, tile, tile, pl.BlockSpec((2, TILE, span), lambda a, t: (a, t, 0))]
        + [hbm] * (3 + len(more_in)),
        out_specs=[tile, tile, tile, vmem, vmem, vmem, hbm] + [vmem] * len(more_out),
        out_shape=[
            shape((rows, width), BF),
            shape((rows, width), BF),
            shape((rows, width), BF),
            shape((CHUNK, width), BF),
            shape((CHUNK, width), BF),
            shape((2, CHUNK, 128), BF),
            shape(out_half.shape, BF),
        ]
        + more_out,
        scratch_shapes=[
            pltpu.VMEM((128, PROMPT), F32),
            pltpu.VMEM((128, PROMPT), F32),
            pltpu.VMEM((rows, width), BF),
            pltpu.VMEM((2, 2, 2, CHUNK, width), BF),
            pltpu.VMEM((2, 2, CHUNK, width), BF),
            pltpu.VMEM((2, CHUNK, width), BF),
            pltpu.VMEM((2, CHUNK, width), BF),
            pltpu.SemaphoreType.DMA((copies,)),
            pltpu.SemaphoreType.DMA((copies,)),
            pltpu.SemaphoreType.DMA((2,)),
        ]
        + more_scratch,
        compiler_params=pltpu.CompilerParams(vmem_limit_bytes=60 << 20, collective_id=2, has_side_effects=True),
        cost_estimate=pl.CostEstimate(flops=30 * 10**9, bytes_accessed=60 * 10**6, transcendentals=0),
        name="attend_back",
    )(q, kp, vp, k, v, o, li, e, g_mine, g_theirs, out_half, *more_in)


UCH = 512


def polynomial(x, terms):
    out = jnp.full_like(x, terms[0])
    for term in terms[1:]:
        out = out * x + term
    return out


def error_function(x):
    x = jnp.clip(x, -3.832506856900711, 3.832506856900711)
    square = x * x
    top = polynomial(
        square,
        (0.00022905065861350646, 0.0034082910107109506, 0.050955695062380861, 0.18520832239976145, 1.128379143519084),
    )
    bottom = polynomial(
        square,
        (
            -1.1791602954361697e-7,
            0.000023547966471313185,
            0.0010179625278914885,
            0.014070470171167667,
            0.11098505178285362,
            0.49746925110067538,
            1.0,
        ),
    )
    return x * top / bottom


def gelu_pair(v):
    phi = 0.5 + 0.5 * error_function(v * 0.7071067811865476)
    density = jnp.exp(-0.5 * v * v) * 0.3989422804014327
    return v * phi, phi + v * density


def column_sum(x):
    return jnp.sum(x, axis=0, keepdims=True)


def mid_kernel(
    att_m, att_o, vec_all, vec_got, hid_all, cot_all, w1_own, w1_got, w1_swap, wo_own, wo_got, wo_swap, w2_own,
    out_ref, gatt_m, gatt_o, gmix_ref, packed, su_ref, sw_ref, sd_ref, ext_ref,
    vec_u, vec_w, w1, w2, wo, act_s, shp_s, dg_s, wide_s, acc_s, gmid_s, sub_s, mid_s, low_s, midt_s, cott_s, stage, hid, cot, sems, out_sems, send_sems, recv_sems,
):
    device = lax.axis_index("dp")
    side = lax.axis_index("tensor")
    core = device % 2
    near = {"dp": bit_peer(device, 0), "tensor": side}
    across = {"dp": device, "tensor": 1 - side}
    units = w1_own.shape[1]
    width = wo_own.shape[0]
    rows = hid.shape[0]
    full = 2 * units
    half = units // 2
    half_w = width // 2
    here_u = pl.multiple_of(units + core * half, 128)
    there_u = pl.multiple_of(units + (1 - core) * half, 128)
    here_w = pl.multiple_of(width + core * half_w, 64)
    there_w = pl.multiple_of(width + (1 - core) * half_w, 64)
    prompt, conts = CHUNK // 2, (hid_all.shape[0] - CHUNK) // 2
    own_p = pl.ds(pl.multiple_of(side * prompt, 128), prompt)
    own_c = pl.ds(pl.multiple_of(CHUNK + side * conts, 128), conts)
    at_own = 2 * D + 2 * width
    vec_own = vec_all.at[:, pl.ds(at_own, 3 * units + 2 * width)]
    vec_d = vec_all.at[:, pl.ds(at_own + 3 * units + 2 * width, 4 * D)]
    rows_in = []
    for i, (all_rows, held) in enumerate(((hid_all, hid), (cot_all, cot))):
        for j, (span, at, size) in enumerate(((own_p, 0, prompt), (own_c, prompt, conts))):
            copy = pltpu.make_async_copy(all_rows.at[span, :], held.at[pl.ds(at, size), :], sems.at[7 + 2 * i + j])
            copy.start()
            rows_in.append(copy)
    loads = []
    for i, (src, dst) in enumerate(
        [
            (wo_own, wo.at[pl.ds(0, width), :]),
            (wo_got, wo.at[pl.ds(here_w, half_w), :]),
            (wo_swap, wo.at[pl.ds(there_w, half_w), :]),
            (w1_own, w1.at[:, pl.ds(0, units)]),
            (w1_got, w1.at[:, pl.ds(here_u, half)]),
            (w1_swap, w1.at[:, pl.ds(there_u, half)]),
            (w2_own, w2.at[pl.ds(0, units), :]),
        ]
    ):
        copy = pltpu.make_async_copy(src, dst, sems.at[i])
        copy.start()
        loads.append(copy)

    piece = half // 2
    greet([near, across])

    def remote(i, src, dst, peer):
        return pltpu.make_async_remote_copy(
            src_ref=src, dst_ref=dst, send_sem=send_sems.at[i], recv_sem=recv_sems.at[i], device_id=peer, device_id_type=MESH
        )

    over, passed = [], []
    for i in range(2):
        from_own = pl.ds(pl.multiple_of(core * half + i * piece, 128), piece)
        landed = w2.at[pl.ds(pl.multiple_of(units + core * half + i * piece, 128), piece), :]
        over.append(remote(i, w2_own.at[from_own, :], landed, across))
        passed.append(remote(2 + i, landed, landed, near))
        over[i].start()

    for i in range(3):
        for j, vec in enumerate((vec_own, vec_got)):
            vec_u[i : i + 1, pl.ds(j * units, units)] = vec[0:1, pl.ds(i * units, units)]
    for i in range(2):
        for j, vec in enumerate((vec_own, vec_got)):
            vec_w[i : i + 1, pl.ds(j * width, width)] = vec[0:1, pl.ds(3 * units + i * width, width)]

    a0 = att_m[...].astype(F32)
    a1 = att_o[...].astype(F32)
    center = (jnp.sum(a0, axis=1, keepdims=True) + jnp.sum(a1, axis=1, keepdims=True)) * (1.0 / D)
    square = (jnp.sum(a0 * a0, axis=1, keepdims=True) + jnp.sum(a1 * a1, axis=1, keepdims=True)) * (1.0 / D)
    sub_scale = lax.rsqrt(square - center * center + EPSILON)
    sub_s[:, 0:width] = (a0 - center) * sub_scale
    sub_s[:, width : 2 * width] = (a1 - center) * sub_scale
    sub_gain = vec_w[0:1, :]
    low_s[...] = (sub_s[...] * sub_gain + vec_w[1:2, :]).astype(BF)
    for copy in loads[0:3] + rows_in:
        copy.wait()
    mixed = hid[...].astype(F32) + (dot_nn(low_s[...], wo[...]) + vec_d[0:1, pl.ds(0, D)])
    wide_s[...] = mixed
    mean = jnp.mean(mixed, axis=1, keepdims=True)
    mid_scale = lax.rsqrt(jnp.mean(mixed * mixed, axis=1, keepdims=True) - mean * mean + EPSILON)
    mid_s[...] = (mixed - mean) * mid_scale
    mid_gain = vec_d[0:1, pl.ds(768, D)]
    mid_full = mid_s[...] * mid_gain + vec_d[0:1, pl.ds(1536, D)]
    mid_low = mid_full.astype(BF)
    midt_s[...] = jnp.transpose(mid_full).astype(BF)
    cot_full = cot[...].astype(F32)
    cott_s[...] = jnp.transpose(cot_full).astype(BF)
    sd_ref[...] = jnp.zeros_like(sd_ref)
    sd_ref[3:4, :] = column_sum(cot_full)
    for copy in loads[3:6]:
        copy.wait()

    def lanes_sum(x):
        total = x[:, 0:128]
        for i in range(1, x.shape[1] // 128):
            total = total + x[:, i * 128 : (i + 1) * 128]
        return total

    def first(c, carry):
        at = pl.multiple_of(c * UCH, UCH)
        inner = dot_nn(mid_low, w1[:, pl.ds(at, UCH)]) + vec_u[2:3, pl.ds(at, UCH)]
        act, slope = gelu_pair(inner)
        act_s[:, pl.ds(at, UCH)] = act
        dg_s[:, pl.ds(at, UCH)] = slope.astype(BF)
        return carry[0] + lanes_sum(act), carry[1] + lanes_sum(act * act)

    zero = jnp.zeros((rows, 128), F32)
    act_sum, act_square = lax.fori_loop(0, full // UCH, first, (zero, zero))
    ffn_center = jnp.sum(act_sum, axis=1, keepdims=True) * (1.0 / full)
    ffn_scale = lax.rsqrt(
        jnp.sum(act_square, axis=1, keepdims=True) * (1.0 / full) - ffn_center * ffn_center + EPSILON
    )
    loads[6].wait()
    over[0].wait_recv()
    passed[0].start()
    acc_s[...] = jnp.zeros_like(acc_s)
    per = units // UCH
    wide = 2 * units + width

    def column_of(c, extra):
        return pl.multiple_of((c // per) * wide + lax.rem(c, per) * UCH + extra, 128)

    def send(slot, column):
        return pltpu.make_async_copy(stage.at[slot], packed.at[:, pl.ds(column, UCH)], out_sems.at[slot])

    def put(c, value, extra):
        slot = lax.rem(c, 2)

        @pl.when(c >= 2)
        def _():
            send(slot, column_of(c - 2, extra)).wait()

        stage[slot] = value
        send(slot, column_of(c, extra)).start()

    def drain(extra):
        for c in range(full // UCH - 2, full // UCH):
            send(c % 2, column_of(c, extra)).wait()

    def second(c, carry):
        at = pl.multiple_of(c * UCH, UCH)
        unit = (act_s[:, pl.ds(at, UCH)] - ffn_center) * ffn_scale
        act_s[:, pl.ds(at, UCH)] = unit
        gain = vec_u[0:1, pl.ds(at, UCH)]
        low = (unit * gain + vec_u[1:2, pl.ds(at, UCH)]).astype(BF)
        acc_s[...] += dot_nn(low, w2[pl.ds(at, UCH), :])
        grad = dot_nt(cot[...], w2[pl.ds(at, UCH), :])
        cross = grad * unit
        su_ref[0:1, pl.ds(at, UCH)] = column_sum(cross)
        su_ref[1:2, pl.ds(at, UCH)] = column_sum(grad)
        shaped = grad * gain
        shp_s[:, pl.ds(at, UCH)] = shaped
        put(c, dot_nn(cott_s[...], low).astype(BF), units)
        return carry[0] + lanes_sum(shaped), carry[1] + lanes_sum(shaped * unit)

    su_ref[...] = jnp.zeros_like(su_ref)
    sums = lax.fori_loop(0, per, second, (zero, zero))
    over[1].wait_recv()
    passed[1].start()
    for copy in passed:
        copy.wait_recv()
    s_sum, s_cross = lax.fori_loop(per, 2 * per, second, sums)
    drain(units)
    shaped_mean = jnp.sum(s_sum, axis=1, keepdims=True) * (1.0 / full)
    cross_mean = jnp.sum(s_cross, axis=1, keepdims=True) * (1.0 / full)
    out_ref[...] = (wide_s[...] + (acc_s[...] + vec_d[0:1, pl.ds(2304, D)])).astype(BF)
    gmid_s[...] = jnp.zeros_like(gmid_s)

    def third(c, carry):
        at = pl.multiple_of(c * UCH, UCH)
        g = ffn_scale * (shp_s[:, pl.ds(at, UCH)] - shaped_mean - act_s[:, pl.ds(at, UCH)] * cross_mean)
        low = (g * dg_s[:, pl.ds(at, UCH)].astype(F32)).astype(BF)
        su_ref[2:3, pl.ds(at, UCH)] = column_sum(low.astype(F32))
        gmid_s[...] += dot_nt(low, w1[:, pl.ds(at, UCH)])
        put(c, dot_nn(midt_s[...], low).astype(BF), 0)
        return carry

    lax.fori_loop(0, full // UCH, third, 0)
    drain(0)

    grad_mid = gmid_s[...]
    unit = mid_s[...]
    sd_ref[1:2, :] = column_sum(grad_mid * unit)
    sd_ref[2:3, :] = column_sum(grad_mid)
    shaped = grad_mid * mid_gain
    grad_mixed = cot[...].astype(F32) + mid_scale * (
        shaped - jnp.mean(shaped, axis=1, keepdims=True) - unit * jnp.mean(shaped * unit, axis=1, keepdims=True)
    )
    branch = grad_mixed.astype(BF)
    gmix_ref[...] = branch
    branch_f = branch.astype(F32)
    sd_ref[0:1, :] = column_sum(branch_f)
    out_grad = dot_nn(jnp.transpose(branch_f).astype(BF), low_s[...]).astype(BF)
    stage[0, :, 0:width] = out_grad[:, 0:width]
    stage[1, :, 0:width] = out_grad[:, width : 2 * width]
    last = [
        pltpu.make_async_copy(stage.at[i, :, pl.ds(0, width)], packed.at[:, pl.ds(i * wide + 2 * units, width)], out_sems.at[i])
        for i in range(2)
    ]
    for copy in last:
        copy.start()
    grad_sub = dot_nt(branch, wo[...])
    unit = sub_s[...]
    cross = grad_sub * unit
    sw_ref[...] = jnp.zeros_like(sw_ref)
    sw_ref[0:1, :] = column_sum(cross)
    sw_ref[1:2, :] = column_sum(grad_sub)
    shaped = grad_sub * sub_gain
    grad_att = sub_scale * (
        shaped - jnp.mean(shaped, axis=1, keepdims=True) - unit * jnp.mean(shaped * unit, axis=1, keepdims=True)
    )
    gatt_m[...] = grad_att[:, 0:width].astype(BF)
    gatt_o[...] = grad_att[:, width : 2 * width].astype(BF)
    parts = ext_ref.shape[0]
    if parts > 1:
        sums_u, sums_w, sums_d = su_ref[...], sw_ref[...], sd_ref[...]
        for i in range(parts):
            ext_ref[i] = jnp.concatenate(
                [
                    window(sums_u, i * (units // parts)),
                    window(sums_u, units + i * (units // parts)),
                    window(sums_w, i * (width // parts)),
                    window(sums_w, width + i * (width // parts)),
                    window(sums_d, i * (D // parts)),
                    jnp.zeros((8, 128), F32),
                ],
                axis=0,
            ).astype(BF)
    for copy in last:
        copy.wait()
    for copy in over + passed:
        copy.wait_send()


def window(rows8, start):
    base = start // 128 * 128
    size = min(256, rows8.shape[1] - base)
    view = rows8[:, base : base + size]
    shift = start - base
    if shift:
        view = pltpu.roll(view, size - shift, 1)
    return view[:, 0:128]


def middle(att_m, att_o, hid, cot, vec_all, vec_got, w1, w2, wo, parts):
    rows = att_m.shape[0]
    units = w2.shape[0]
    width = wo[0].shape[0]
    vmem = pl.BlockSpec(memory_space=pltpu.VMEM)
    hbm = pl.BlockSpec(memory_space=pl.ANY)
    shape = jax.ShapeDtypeStruct
    return pl.pallas_call(
        mid_kernel,
        in_specs=[vmem] * 4 + [hbm] * 9,
        out_specs=[vmem] * 4 + [hbm] + [vmem] * 4,
        out_shape=[
            shape((rows, D), BF),
            shape((rows, width), BF),
            shape((rows, width), BF),
            shape((rows, D), BF),
            shape((D, 2 * (2 * units + width)), BF),
            shape((8, 2 * units), F32),
            shape((8, 2 * width), F32),
            shape((8, D), F32),
            shape((parts, 48, 128), BF),
        ],
        scratch_shapes=[
            pltpu.VMEM((8, 2 * units), F32),
            pltpu.VMEM((8, 2 * width), F32),
            pltpu.VMEM((D, 2 * units), BF),
            pltpu.VMEM((2 * units, D), BF),
            pltpu.VMEM((2 * width, D), BF),
            pltpu.VMEM((rows, 2 * units), F32),
            pltpu.VMEM((rows, 2 * units), F32),
            pltpu.VMEM((rows, 2 * units), BF),
            pltpu.VMEM((rows, D), F32),
            pltpu.VMEM((rows, D), F32),
            pltpu.VMEM((rows, D), F32),
            pltpu.VMEM((rows, 2 * width), F32),
            pltpu.VMEM((rows, D), F32),
            pltpu.VMEM((rows, 2 * width), BF),
            pltpu.VMEM((D, rows), BF),
            pltpu.VMEM((D, rows), BF),
            pltpu.VMEM((2, D, UCH), BF),
            pltpu.VMEM((rows, D), BF),
            pltpu.VMEM((rows, D), BF),
            pltpu.SemaphoreType.DMA((11,)),
            pltpu.SemaphoreType.DMA((2,)),
            pltpu.SemaphoreType.DMA((4,)),
            pltpu.SemaphoreType.DMA((4,)),
        ],
        compiler_params=pltpu.CompilerParams(vmem_limit_bytes=62 << 20, collective_id=3, has_side_effects=True),
        cost_estimate=pl.CostEstimate(flops=21 * 10**9, bytes_accessed=30 * 10**6, transcendentals=0),
        name="middle",
    )(att_m, att_o, vec_all, vec_got, hid, cot, *w1, *wo, w2)


def final_kernel(
    bits, hid, vec_all, dq, dk, dv, wq, wk, wv, gmix, ext, sum_k, sum_v, relay, first_done, first_other, packed,
    gin, late_out, vec_out, early_out,
    loc_s, far_s, unit_s, mine_s, norm_s, send_c, recv_c, send_p, recv_p, give_c, give_p, late_s, small_s,
    vec_s, vec_r, done_s, sems_a, sems_b, loc_sems, *stage_refs,
):
    device = lax.axis_index("dp")
    side = lax.axis_index("tensor")
    across = {"dp": device, "tensor": 1 - side}
    peers = [{"dp": bit_peer(device, b), "tensor": side} for b in range(bits)]
    rows, width = dq.shape
    prompt = sum_k.shape[0]
    conts = rows - prompt
    half_p, half_c = prompt // 2, conts // 2
    own_p = pl.multiple_of(side * half_p, 128)
    their_p = pl.multiple_of((1 - side) * half_p, 128)
    own_c = pl.multiple_of(prompt + side * half_c, 128)
    their_c = pl.multiple_of(prompt + (1 - side) * half_c, 128)
    lanes = 3 * width + 128

    greet(peers + [across])
    count = [0]

    def remote(src, dst, peer):
        i = count[0]
        count[0] += 1
        copy = pltpu.make_async_remote_copy(
            src_ref=src, dst_ref=dst, send_sem=sems_a.at[i], recv_sem=sems_b.at[i], device_id=peer, device_id_type=MESH
        )
        copy.start()
        return copy

    share = remote(relay, far_s, peers[1])

    begin, after0, after1, after2, after3, settle = reducer(packed, device, side, 0, stage_refs[-10:], done_s)

    def each(act):
        for c in range(EARLY):
            act(c)

    each(begin)

    gain_f = vec_all[:, pl.ds(0, D)]
    bias_f = vec_all[:, pl.ds(D, D)]

    def unit_rows(at, size):
        x = hid[pl.ds(at, size), :].astype(F32)
        center = jnp.mean(x, axis=1, keepdims=True)
        scale = lax.rsqrt(jnp.mean(x * x, axis=1, keepdims=True) - center * center + EPSILON)
        return (x - center) * scale, scale

    def part_of(at, size, k_rows, v_rows):
        return dot_nt(dq[pl.ds(at, size), :], wq[...]) + dot_nt(k_rows, wk[...]) + dot_nt(v_rows, wv[...])

    def gather(part, unit):
        return column_sum(part * unit), column_sum(part)

    def normed_rows(at, size, unit):
        norm_s[:, pl.ds(at, size)] = jnp.transpose(unit * gain_f + bias_f).astype(BF)

    part = part_of(their_c, half_c, dk[pl.ds(their_c, half_c), :], dv[pl.ds(their_c, half_c), :])
    send_c[...] = part.astype(BF)
    y_cont = remote(send_c, recv_c, across)
    unit, _ = unit_rows(their_c, half_c)
    gain_grad, bias_grad = gather(part, unit)
    normed_rows(their_c, half_c, unit)
    unit, scale_c = unit_rows(own_c, half_c)
    part = part_of(own_c, half_c, dk[pl.ds(own_c, half_c), :], dv[pl.ds(own_c, half_c), :])
    mine_s[pl.ds(half_p, half_c), :] = part
    unit_s[pl.ds(half_p, half_c), :] = unit
    g, b = gather(part, unit)
    gain_grad, bias_grad = gain_grad + g, bias_grad + b
    normed_rows(own_c, half_c, unit)

    each(after0)
    share.wait_recv()
    for i, total in enumerate((sum_k, sum_v)):
        loc_s[i, :, pl.ds(0, width - 128)] = total[:, pl.ds(0, width - 128)]
        loc_s[i, :, pl.ds(width - 128, 128)] = (
            total[:, pl.ds(width - 128, 128)].astype(F32) + far_s[i].astype(F32)
        ).astype(BF)
    part = part_of(their_p, half_p, loc_s[0, pl.ds(their_p, half_p), :], loc_s[1, pl.ds(their_p, half_p), :])
    send_p[...] = part.astype(BF)
    y_prompt = remote(send_p, recv_p, across)
    unit, _ = unit_rows(their_p, half_p)
    normed_rows(their_p, half_p, unit)
    g, b = gather(part, unit)
    gain_grad, bias_grad = gain_grad + g, bias_grad + b
    unit, scale_p = unit_rows(own_p, half_p)
    unit_s[pl.ds(0, half_p), :] = unit
    normed_rows(own_p, half_p, unit)
    part = part_of(own_p, half_p, loc_s[0, pl.ds(own_p, half_p), :], loc_s[1, pl.ds(own_p, half_p), :])
    mine_s[pl.ds(0, half_p), :] = part
    g, b = gather(part, unit)
    gain_grad, bias_grad = gain_grad + g, bias_grad + b

    blocks = 1 << bits
    block = D // blocks

    def keep(value, lane):
        low = value.astype(BF)
        for i in range(blocks):
            late_s[i // 2, i % 2, :, pl.ds(lane, width)] = low[i * block : (i + 1) * block, :]

    keep(dot_nn(norm_s[...], dq[...]), 0)
    q_bias = column_sum(dq[...].astype(F32))
    for i, rest in enumerate((dk, dv)):
        keep(
            dot_nn(norm_s[:, pl.ds(0, prompt)], loc_s[i])
            + dot_nn(norm_s[:, pl.ds(prompt, conts)], rest[pl.ds(prompt, conts), :]),
            (i + 1) * width,
        )
    v_bias = column_sum(loc_s[1].astype(F32)) + column_sum(dv[pl.ds(prompt, conts), :].astype(F32))

    def norm_back(total, unit, scale, mixed):
        shaped = total * gain_f
        return mixed.astype(F32) + scale * (
            shaped - jnp.mean(shaped, axis=1, keepdims=True) - unit * jnp.mean(shaped * unit, axis=1, keepdims=True)
        )

    small_s[...] = jnp.zeros_like(small_s)
    small_s[0:1, pl.ds(0, width)] = q_bias
    small_s[1:2, pl.ds(0, width)] = v_bias
    small_s[2:3, pl.ds(0, D)] = gain_grad
    small_s[3:4, pl.ds(0, D)] = bias_grad
    small = small_s[...]
    row_id = lax.broadcasted_iota(jnp.int32, (8, 128), 0)
    for i in range(blocks):
        narrow = window(small, i * (width // blocks))
        broad = window(small, i * block)
        tail = jnp.concatenate([ext[i, pl.ds(32, 16), :].astype(F32)[0:8], jnp.where(row_id < 2, narrow, broad)], axis=0)
        late_s[i // 2, i % 2, pl.ds(0, 32), pl.ds(3 * width, 128)] = ext[i, pl.ds(0, 32), :]
        late_s[i // 2, i % 2, pl.ds(32, 16), pl.ds(3 * width, 128)] = tail.astype(BF)

    def input_rows(arrived, at, size, scale, held, rows_at, sem):
        arrived[0].wait_recv()
        here = pl.ds(at, size)
        total = mine_s[here, :] + arrived[1][...].astype(F32)
        held[...] = norm_back(total, unit_s[here, :], scale, gmix[here, :]).astype(BF)
        back = remote(held, gin.at[pl.ds(rows_at, size), :], across)
        kept = pltpu.make_async_copy(held, gin.at[pl.ds(rows_at, size), :], loc_sems.at[sem])
        kept.start()
        return back, kept

    source = late_s
    stages = []
    for bit in range(bits):
        landing, kept = stage_refs[2 * bit], stage_refs[2 * bit + 1]
        mine = (device // (1 << bit)) % 2
        copy = remote(source.at[:, 1 - mine], landing, peers[bit])
        if bit == 0:
            back_c, keep_c = input_rows((y_cont, recv_c), half_p, half_c, scale_c, give_c, own_c, 0)
        if bit == 1:
            each(after1)
            back_p, keep_p = input_rows((y_prompt, recv_p), 0, half_p, scale_p, give_p, own_p, 1)
        if bit == 2:
            each(after2)
        if bit == 3:
            each(after3)
        copy.wait_recv()
        stages.append(copy)
        for i in range(landing.shape[0]):
            kept[i // 2, i % 2] = (source[i, mine].astype(F32) + landing[i].astype(F32)).astype(BF)
        source = kept
    late_out[...] = source[0, 0, :, pl.ds(0, 3 * width)].astype(F32)
    vec_s[...] = source[0, 0, :, pl.ds(3 * width, 128)]
    swap = remote(vec_s, vec_r, across)
    last_e = done_s.shape[1]
    early_out[:, pl.ds(0, last_e)] = done_s[...].astype(F32) + first_other[:, pl.ds(0, last_e)].astype(F32)
    rest_e = first_done.shape[1]
    early_out[:, pl.ds(last_e, rest_e)] = first_done[...].astype(F32) + first_other[:, pl.ds(last_e, rest_e)].astype(F32)
    settle()
    swap.wait_recv()
    own_v, got_v = vec_s[...].astype(F32), vec_r[...].astype(F32)
    vec_out[0:8, :] = own_v[0:8] + got_v[8:16]
    vec_out[8:16, :] = own_v[16:24] + got_v[24:32]
    vec_out[16:24, :] = own_v[32:40] + got_v[32:40]
    vec_out[24:32, :] = own_v[40:48] + jnp.where(row_id < 2, 0.0, got_v[40:48])
    for copy in stages + [share, y_cont, y_prompt, swap]:
        copy.wait_send()
    for copy in (back_c, back_p):
        copy.wait_recv()
        copy.wait_send()
    keep_c.wait()
    keep_p.wait()


def finish(hid, vec_all, dq, dk, dv, wq, wk, wv, gmix, ext, sum_k, sum_v, relay, first_done, first_other, packed):
    rows, width = dq.shape
    ranks = lax.axis_size("dp")
    bits = ranks.bit_length() - 1
    block = D // ranks
    prompt = sum_k.shape[0]
    conts = rows - prompt
    lanes = 3 * width + 128
    vmem = pl.BlockSpec(memory_space=pltpu.VMEM)
    hbm = pl.BlockSpec(memory_space=pl.ANY)
    shape = jax.ShapeDtypeStruct
    copies = 6 + bits
    cut = (packed.shape[-1] - EARLY * FIRST_CUT) // EARLY
    stages = []
    for bit in range(bits):
        left = ranks >> (bit + 1)
        stages.append(pltpu.VMEM((left, block, lanes), BF))
        stages.append(pltpu.VMEM((max(left // 2, 1), min(left, 2), block, lanes), BF))
    return pl.pallas_call(
        functools.partial(final_kernel, bits),
        in_specs=[vmem] * 15 + [hbm],
        out_specs=[hbm, vmem, vmem, vmem],
        out_shape=[shape((rows, D), BF), shape((block, 3 * width), F32), shape((32, 128), F32), shape((block, packed.shape[-1] // 2), F32)],
        scratch_shapes=[
            pltpu.VMEM((2, prompt, width), BF),
            pltpu.VMEM((2, prompt, 128), BF),
            pltpu.VMEM((rows // 2, D), F32),
            pltpu.VMEM((rows // 2, D), F32),
            pltpu.VMEM((D, rows), BF),
            pltpu.VMEM((conts // 2, D), BF),
            pltpu.VMEM((conts // 2, D), BF),
            pltpu.VMEM((prompt // 2, D), BF),
            pltpu.VMEM((prompt // 2, D), BF),
            pltpu.VMEM((conts // 2, D), BF),
            pltpu.VMEM((prompt // 2, D), BF),
            pltpu.VMEM((ranks // 2, 2, block, lanes), BF),
            pltpu.VMEM((8, D + 128), F32),
            pltpu.VMEM((block, 128), BF),
            pltpu.VMEM((block, 128), BF),
            pltpu.VMEM((block, EARLY * cut), BF),
            pltpu.SemaphoreType.DMA((copies,)),
            pltpu.SemaphoreType.DMA((copies,)),
            pltpu.SemaphoreType.DMA((2,)),
        ]
        + stages
        + reducer_scratch(EARLY, block, cut),
        compiler_params=pltpu.CompilerParams(vmem_limit_bytes=56 << 20, collective_id=1, has_side_effects=True),
        cost_estimate=pl.CostEstimate(flops=5 * 10**9, bytes_accessed=20 * 10**6, transcendentals=0),
        name="finish",
    )(hid, vec_all, dq, dk, dv, wq, wk, wv, gmix, ext, sum_k, sum_v, relay, first_done, first_other, packed)


def flip(value, axis, bit):
    return lax.ppermute(value, axis, [(i, i ^ (1 << bit)) for i in range(lax.axis_size(axis))])


def contract_rows(left, right):
    return lax.dot_general(left, right, (((0,), (0,)), ((), ())), preferred_element_type=F32)


def back_project(left, right):
    return lax.dot_general(left, right, (((1,), (1,)), ((), ())), preferred_element_type=F32)


def norm_rows(values, gain, bias):
    center = jnp.mean(values, axis=-1, keepdims=True)
    spread = jnp.mean(values * values, axis=-1, keepdims=True) - center * center
    scaled = lax.rsqrt(spread + EPSILON)
    unit_rows = (values - center) * scaled
    return (unit_rows * gain + bias, unit_rows, scaled)


def norm_back(grad_rows, gain, unit_rows, scaled):
    shaped = grad_rows * gain
    return scaled * (
        shaped
        - jnp.mean(shaped, axis=-1, keepdims=True)
        - unit_rows * jnp.mean(shaped * unit_rows, axis=-1, keepdims=True)
    )


def in_order(which, mine, other, axis):
    return jnp.where(
        which == 0,
        jnp.concatenate([mine, other], axis=axis),
        jnp.concatenate([other, mine], axis=axis),
    )


def halving(value, device):
    bits = lax.axis_size("dp").bit_length() - 1
    rows, columns = value.shape
    current = value
    for bit in range(bits):
        upper = device // (1 << bit) % 2
        left = bits - bit
        view = current.reshape((1 << (left - 1), 2, -1, columns))
        kept = lax.dynamic_index_in_dim(view, upper, 1, keepdims=False)
        sent = lax.dynamic_index_in_dim(view, 1 - upper, 1, keepdims=False)
        got = flip(sent, "dp", bit)
        current = (kept.astype(F32) + got.astype(F32)).astype(BF)
    return current.reshape(rows >> bits, columns)


def side_by_side(parts):
    total = sum(part.shape[0] for part in parts)
    row, at = jnp.zeros((total,), F32), 0
    for part in parts:
        size = part.shape[0]
        row = row + jnp.pad(part.astype(F32), (at, total - at - size))
        at += size
    return row[None]


def half_of(value, which):
    prompt, conts = CHUNK // 2, (value.shape[0] - CHUNK) // 2
    return jnp.concatenate(
        [
            lax.dynamic_slice_in_dim(value, which * prompt, prompt),
            lax.dynamic_slice_in_dim(value, CHUNK + which * conts, conts),
        ]
    )


def joined(which, mine, other):
    prompt = CHUNK // 2
    low = jnp.where(which == 0, mine, other)
    high = jnp.where(which == 0, other, mine)
    return jnp.concatenate([low[:prompt], high[:prompt], low[prompt:], high[prompt:]])


def body(
    hidden_in,
    cotangent,
    prompt_start,
    cont_gap,
    seg_len,
    dilation_rate,
    pre_gain,
    pre_bias,
    query_weight,
    query_bias,
    key_weight,
    value_weight,
    value_bias,
    sub_gain,
    sub_bias,
    out_weight,
    out_bias,
    mid_gain,
    mid_bias,
    inner_weight,
    inner_bias,
    ffn_gain,
    ffn_bias,
    outer_weight,
    outer_bias,
):
    device = lax.axis_index("dp")
    ranks = lax.axis_size("dp")
    group_id = device // GDEV
    member = device % GDEV
    tensor_id = lax.axis_index("tensor")
    core = device % 2
    width = query_weight.shape[1]
    units = inner_weight.shape[1]
    pairs = width // 128
    rows = hidden_in.shape[0]
    prompt_rows = CHUNK
    cont_count = (rows - prompt_rows) // CONT

    vectors = side_by_side(
        [
            pre_gain,
            pre_bias,
            query_bias,
            value_bias,
            ffn_gain,
            ffn_bias,
            inner_bias,
            sub_gain,
            sub_bias,
            out_bias,
            mid_gain,
            mid_bias,
            outer_bias,
        ]
    )
    pre_gain_f = pre_gain.astype(F32)

    (
        weighed,
        inverse,
        queries,
        keys,
        values,
        prompt_keys,
        prompt_values,
        attended,
        att_mine,
        att_got,
        *pieces,
        vectors_other,
    ) = attend(
        prompt_start,
        cont_gap,
        seg_len.T,
        dilation_rate.T,
        hidden_in,
        vectors,
        query_weight,
        key_weight,
        value_weight,
        inner_weight,
        out_weight,
    )
    inner_parts = (inner_weight, pieces[0], pieces[1])
    out_parts = (out_weight, pieces[2], pieces[3])

    fused = ranks == 16
    out_half, grad_mine, grad_theirs, grad_mixed_low, packed, sum_u, sum_w, sum_d, ext = middle(
        att_mine,
        att_got,
        hidden_in,
        cotangent,
        vectors,
        vectors_other,
        inner_parts,
        outer_weight,
        out_parts,
        ranks if fused else 1,
    )

    grad_query_in, own_key_grad, own_value_grad, key_sum, value_sum, relay, out_got, *early = attend_back(
        queries,
        keys,
        values,
        prompt_keys,
        prompt_values,
        attended,
        inverse,
        weighed,
        grad_mine,
        grad_theirs,
        out_half,
        packed.reshape(2, 2, 2, 2, D // ranks, -1) if fused else None,
    )
    if not fused:
        early = lax.psum_scatter(packed, "dp", scatter_dimension=0, tiled=True)
        early_mine, early_other = jnp.split(early, 2, axis=1)
        early_sum = early_mine.astype(F32) + flip(early_other, "tensor", 0).astype(F32)
    output = joined(tensor_id, out_half, out_got)
    block = D // ranks
    per_u, per_w, per_d = units // ranks, width // ranks, D // ranks
    if fused:
        input_low, late, vec, early_sum = finish(
            hidden_in,
            vectors,
            grad_query_in,
            own_key_grad,
            own_value_grad,
            query_weight,
            key_weight,
            value_weight,
            grad_mixed_low,
            ext,
            key_sum,
            value_sum,
            relay,
            *early,
            packed.reshape(2, 2, 2, 2, D // ranks, -1),
        )
        ffn_gain_grad, ffn_bias_grad, inner_bias_grad = [vec[i, :per_u] for i in range(3)]
        sub_gain_grad, sub_bias_grad = [vec[8 + i, :per_w] for i in range(2)]
        out_bias_grad, mid_gain_grad, mid_bias_grad, outer_bias_grad = [vec[16 + i, :per_d] for i in range(4)]
        query_bias_grad, value_bias_grad = [vec[24 + i, :per_w] for i in range(2)]
        pre_gain_grad, pre_bias_grad = [vec[26 + i, :per_d] for i in range(2)]
    else:
        pre_normed, pre_unit, pre_scale = norm_rows(hidden_in.astype(F32), pre_gain_f, pre_bias.astype(F32))
        pre_low = pre_normed.astype(BF)
        last = width - 128
        far = flip(relay, "dp", 1).astype(F32)
        summed = jnp.stack([key_sum, value_sum]).astype(F32)
        summed = jnp.concatenate([summed[:, :, :last], summed[:, :, last:] + far], axis=2).astype(BF)
        grad_keys = jnp.concatenate([summed[0], own_key_grad[prompt_rows:]], axis=0)
        grad_values = jnp.concatenate([summed[1], own_value_grad[prompt_rows:]], axis=0)

        query_weight_grad = contract_rows(pre_low, grad_query_in)
        key_weight_grad = contract_rows(pre_low, grad_keys)
        value_weight_grad = contract_rows(pre_low, grad_values)
        query_bias_grad = jnp.sum(grad_query_in.astype(F32), axis=0)
        value_bias_grad = jnp.sum(grad_values.astype(F32), axis=0)
        grad_normed_part = (
            back_project(grad_query_in, query_weight)
            + back_project(grad_keys, key_weight)
            + back_project(grad_values, value_weight)
        )
        grad_normed_low = grad_normed_part.astype(BF)
        grad_normed = grad_normed_low.astype(F32) + flip(grad_normed_low, "tensor", 0).astype(F32)
        pre_gain_grad = jnp.sum(grad_normed * pre_unit, axis=0)
        pre_bias_grad = jnp.sum(grad_normed, axis=0)
        grad_mixed_all = joined(tensor_id, grad_mixed_low, flip(grad_mixed_low, "tensor", 0)).astype(F32)
        input_low = (grad_mixed_all + norm_back(grad_normed, pre_gain_f, pre_unit, pre_scale)).astype(BF)

        vec = jnp.concatenate(
            [
                sum_u[:3].reshape(3, 2, ranks, per_u).transpose(2, 1, 0, 3).reshape(ranks, 6 * per_u),
                sum_w[:2].reshape(2, 2, ranks, per_w).transpose(2, 1, 0, 3).reshape(ranks, 4 * per_w),
                sum_d[:4].reshape(4, ranks, per_d).swapaxes(0, 1).reshape(ranks, 4 * per_d),
                jnp.stack([query_bias_grad, value_bias_grad]).reshape(2, ranks, per_w).swapaxes(0, 1).reshape(ranks, 2 * per_w),
                jnp.stack([pre_gain_grad, pre_bias_grad]).reshape(2, ranks, per_d).swapaxes(0, 1).reshape(ranks, 2 * per_d),
            ],
            axis=1,
        )
        count = vec.shape[1]
        vec = jnp.pad(vec, ((0, 0), (0, block * 128 - count))).reshape(D, 128)
        late = halving(
            jnp.concatenate(
                [p.astype(BF) for p in (query_weight_grad, key_weight_grad, value_weight_grad, vec)], axis=1
            ),
            device,
        )
        vec = late[:, 3 * width :].reshape(-1)[:count]
        late = late[:, : 3 * width].astype(F32)
        at_w = 6 * per_u
        at_d = at_w + 4 * per_w
        at_late = at_d + 4 * per_d
        got = flip(vec[:at_late], "tensor", 0).astype(F32)
        vec = vec.astype(F32)
        ffn_gain_grad, ffn_bias_grad, inner_bias_grad = (vec[: 3 * per_u] + got[3 * per_u : at_w]).reshape(3, per_u)
        sub_gain_grad, sub_bias_grad = (vec[at_w : at_w + 2 * per_w] + got[at_w + 2 * per_w : at_d]).reshape(2, per_w)
        out_bias_grad, mid_gain_grad, mid_bias_grad, outer_bias_grad = (vec[at_d:at_late] + got[at_d:]).reshape(4, per_d)
        query_bias_grad, value_bias_grad = vec[at_late : at_late + 2 * per_w].reshape(2, per_w)
        pre_gain_grad, pre_bias_grad = vec[at_late + 2 * per_w :].reshape(2, per_d)
    inner_weight_grad = early_sum[:, :units]
    outer_weight_grad = early_sum[:, units : 2 * units].T
    out_weight_grad = early_sum[:, 2 * units :].T
    return (
        output,
        input_low,
        pre_gain_grad,
        pre_bias_grad,
        late[:, :width],
        query_bias_grad,
        late[:, width : 2 * width],
        late[:, 2 * width : 3 * width],
        value_bias_grad,
        sub_gain_grad,
        sub_bias_grad,
        out_weight_grad,
        out_bias_grad,
        mid_gain_grad,
        mid_bias_grad,
        inner_weight_grad,
        inner_bias_grad,
        ffn_gain_grad,
        ffn_bias_grad,
        outer_weight_grad,
        outer_bias_grad,
    )

def solution(mesh):
    placed = (
        P("dp", None),
        P("dp", None),
        P(),
        P(),
        P(),
        P(),
        P(),
        P(),
        P(None, "tensor"),
        P("tensor"),
        P(None, "tensor"),
        P(None, "tensor"),
        P("tensor"),
        P("tensor"),
        P("tensor"),
        P("tensor", None),
        P(),
        P(),
        P(),
        P(None, "tensor"),
        P("tensor"),
        P("tensor"),
        P("tensor"),
        P("tensor", None),
        P(),
    )
    return jax.shard_map(
        body,
        mesh=mesh,
        in_specs=placed,
        out_specs=(
            P("dp", None),
            P("dp", None),
            P("dp"),
            P("dp"),
            P("dp", "tensor"),
            P(("tensor", "dp")),
            P("dp", "tensor"),
            P("dp", "tensor"),
            P(("tensor", "dp")),
            P(("tensor", "dp")),
            P(("tensor", "dp")),
            P("tensor", "dp"),
            P("dp"),
            P("dp"),
            P("dp"),
            P("dp", "tensor"),
            P(("tensor", "dp")),
            P(("tensor", "dp")),
            P(("tensor", "dp")),
            P("tensor", "dp"),
            P("dp"),
        ),
        check_vma=False,
    )
```

```python
import functools

import jax
import jax.numpy as jnp
from jax import lax
from jax.experimental import pallas as pl
from jax.experimental.pallas import tpu as pltpu
from jax.sharding import PartitionSpec as P

HD = 64
PROMPT = 2048
CONT = 256
GDEV = 4
TILE = 256
CHUNK = PROMPT // GDEV
PTILES = CHUNK // TILE
LOG2E = 1.4426950408889634
BF = jnp.bfloat16
F32 = jnp.float32
D = 768
EPSILON = 1e-05
MESH = pl.DeviceIdType.MESH


def dot_nt(a, b):
    return lax.dot_general(a, b, (((1,), (1,)), ((), ())), preferred_element_type=F32)


def dot_nn(a, b):
    return lax.dot_general(a, b, (((1,), (0,)), ((), ())), preferred_element_type=F32)


def low_half(rows):
    return lax.broadcasted_iota(jnp.int32, (rows, 128), 1) < HD


MASKED = -1e30
CLASSES = 36


def lane_classes(head):
    lane = lax.broadcasted_iota(jnp.int32, (8, 128), 1) - (HD if head == 0 else 0)
    number = lane.astype(F32)
    main = lane < CLASSES
    number = jnp.where(main, number, 4.0 * (number - CLASSES) + 3.0)
    number = jnp.where((lane >= 0) & (lane < CLASSES + CLASSES // 4), number, -5.0)
    combo = jnp.floor((number + 0.5) * 0.25)
    step0 = jnp.floor((combo + 0.5) * (1.0 / 3.0))
    step1 = combo - 3.0 * step0
    rest = number - 4.0 * combo
    flag1 = jnp.where(rest > 1.5, 1.0, 0.0)
    return number, step0, step1, flag1, rest - 2.0 * flag1, jnp.where(main, 0.0, 1.0)


def key_side(keys, first, cells, classes):
    size = keys.shape[0]
    at = first + lax.broadcasted_iota(jnp.int32, (8, size), 1).astype(F32)
    base = jnp.full((8, size), 0.0, F32) + first
    row = lax.broadcasted_iota(jnp.int32, (8, size), 0)

    def cell(i):
        return cells[i][:, 0:1]

    step0 = jnp.floor((at + 0.5) * cell(0)) - jnp.floor((base + 0.5) * cell(0))
    step1 = jnp.floor((at + 0.5) * cell(1)) - jnp.floor((base + 0.5) * cell(1))
    rest1 = at - cell(2) * jnp.floor((at + 0.5) * cell(3))
    rest2 = at - cell(4) * jnp.floor((at + 0.5) * cell(5))
    flag1 = jnp.where(rest1 == jnp.where(row == 0, cell(6), cell(7)), 2.0, 0.0)
    flag2 = jnp.where(rest2 == jnp.where(row == 0, cell(8), cell(9)), 1.0, 0.0)
    columns = jnp.transpose(4.0 * (3.0 * step0 + step1) + flag1 + flag2)
    low = low_half(size)
    hot = [jnp.where(columns[:, h : h + 1] == classes[h][0][0:1], 1.0, 0.0).astype(BF) for h in range(2)]
    return [jnp.where(low, keys, hot[0]), jnp.where(low, hot[1], keys)]


def query_side(head, queries, qc, first, cells, lanes, low):
    _, step0, step1, flag1, flag2, small = lanes
    base = jnp.zeros((8, 128), F32) + first
    kc0 = (jnp.floor((base + 0.5) * cells[0]) + step0)[0:1]
    kc1 = jnp.where(flag1 > 0.5, jnp.floor((base + 0.5) * cells[1]) + step1, -1.0)[0:1]
    weight = jnp.where(qc[0] == kc0, 1.0, 0.0) + jnp.where(qc[1 + head] == kc1, 1.0, 0.0)
    weight = weight + qc[3 + head] * flag2[0:1]
    logs = jnp.maximum(jnp.log2(weight), MASKED)
    logs = jnp.where(small[0:1] > 0.5, logs - logs.astype(BF).astype(F32), logs).astype(BF)
    return jnp.where(low, queries, logs) if head == 0 else jnp.where(low, logs, queries)


def settings(seg, rate, pair):
    def row(value):
        return jnp.full((1, 128), value, jnp.int32).astype(F32)

    def rest(number, period):
        return number - period * jnp.floor((number + 0.5) / period)

    second, third = row(rate[1, pair]), row(rate[2, pair])
    head = row(2 * pair)
    return (
        1.0 / row(seg[0, pair]),
        1.0 / row(seg[1, pair]),
        second,
        1.0 / second,
        third,
        1.0 / third,
        rest(head, second),
        rest(head + 1.0, second),
        rest(head, third),
        rest(head + 1.0, third),
    )


def codes(at, cells, miss):
    first = jnp.floor((at + 0.5) * cells[0])
    second = jnp.floor((at + 0.5) * cells[1])
    rest1 = at - cells[2] * jnp.floor((at + 0.5) * cells[3])
    rest2 = at - cells[4] * jnp.floor((at + 0.5) * cells[5])
    return [
        first,
        jnp.where(rest1 == cells[6], second, miss),
        jnp.where(rest1 == cells[7], second, miss),
        jnp.where(rest2 == cells[8], 1.0, 0.0),
        jnp.where(rest2 == cells[9], 1.0, 0.0),
    ]


def bit_peer(device, bit):
    step = 1 << bit
    return device + (1 - 2 * ((device // step) % 2)) * step


def greet(peers):
    barrier = pltpu.get_barrier_semaphore()
    for peer in peers:
        pl.semaphore_signal(barrier, inc=1, device_id=peer, device_id_type=MESH)
    pl.semaphore_wait(barrier, len(peers))


def xor_bits(a, b):
    return (a % 2 + b % 2) % 2 + 2 * ((a // 2 + b // 2) % 2)


def fwd_kernel(
    starts, gaps, seg, rate, hid, vec, wq, wk, wv, w1, wo, vec_hbm,
    e_ref, li_ref, q_out, k_out, v_out, kp_out, vp_out, o_out, mine_out, got_out,
    w1_got, w1_swap, wo_got, wo_swap, vec_got,
    t_s, ka_s, kv_s, low_s, q_s, qe_s, ko_s, vo_s, o_s, sems_a, sems_b, loc_sems,
):
    pair = pl.program_id(0)
    step = pl.program_id(1)
    pairs = pl.num_programs(0)
    device = lax.axis_index("dp")
    side = lax.axis_index("tensor")
    member = device % GDEV
    core = device % 2
    rows, width = q_s.shape
    n_pairs = width // 128
    last_pair = n_pairs - 1
    conts = rows - CHUNK
    near = {"dp": bit_peer(device, 0), "tensor": side}
    far = {"dp": bit_peer(device, 1), "tensor": side}
    across = {"dp": device, "tensor": 1 - side}
    half_u = w1.shape[1] // 2
    half_w = wo.shape[0] // 2
    half_p, half_c = CHUNK // 2, conts // 2
    sent_u = pl.multiple_of(core * half_u, 128)
    shared_at = 2 * D + 2 * width
    sent_w = pl.multiple_of(core * half_w, 64)

    def remote(i, src, dst, peer):
        return pltpu.make_async_remote_copy(
            src_ref=src, dst_ref=dst, send_sem=sems_a.at[i], recv_sem=sems_b.at[i], device_id=peer, device_id_type=MESH
        )

    def to_far(p):
        lanes = pl.ds(p * 128, 128)
        return remote(3 * p, kv_s.at[0, :, :, lanes], kv_s.at[2, :, :, lanes], far)

    def to_near(p):
        lanes = pl.ds(p * 128, 128)
        return remote(3 * p + 1, kv_s.at[0, :, :, lanes], kv_s.at[1, :, :, lanes], near)

    def relay(p):
        lanes = pl.ds(p * 128, 128)
        return remote(3 * p + 2, kv_s.at[2, :, :, lanes], kv_s.at[3, :, :, lanes], near)

    base = 3 * n_pairs
    fetch_y = [
        remote(base, wo.at[pl.ds(sent_w, half_w), :], wo_got, across),
        remote(base + 1, w1.at[:, pl.ds(sent_u, half_u)], w1_got, across),
        remote(base + 2, vec_hbm.at[:, pl.ds(shared_at, vec_got.shape[1])], vec_got, across),
    ]
    fetch_core = [
        remote(base + 3, wo_got, wo_swap, near),
        remote(base + 4, w1_got, w1_swap, near),
    ]

    def give(p, piece):
        lanes = pl.ds(p * 128, 128)
        their_p = pl.multiple_of((1 - side) * half_p, 128)
        their_c = pl.multiple_of(CHUNK + (1 - side) * half_c, 128)
        third = half_c // 3
        if piece == 0:
            source, target = pl.ds(their_p, half_p), pl.ds(0, half_p)
        else:
            source = pl.ds(pl.multiple_of(their_c + (piece - 1) * third, 128), third)
            target = pl.ds(half_p + (piece - 1) * third, third)
        return remote(base + 5 + 4 * p + piece, o_s.at[source, lanes], got_out.at[target, lanes], across)

    def keeps():
        own_p = pl.multiple_of(side * half_p, 128)
        own_c = pl.multiple_of(CHUNK + side * half_c, 128)
        return [
            pltpu.make_async_copy(o_s, o_out, loc_sems.at[0]),
            pltpu.make_async_copy(o_s.at[pl.ds(own_p, half_p), :], mine_out.at[pl.ds(0, half_p), :], loc_sems.at[1]),
            pltpu.make_async_copy(o_s.at[pl.ds(own_c, half_c), :], mine_out.at[pl.ds(half_p, half_c), :], loc_sems.at[2]),
        ]

    def saves():
        out = [
            pltpu.make_async_copy(q_s, q_out, loc_sems.at[3]),
            pltpu.make_async_copy(ko_s, k_out, loc_sems.at[0]),
            pltpu.make_async_copy(vo_s, v_out, loc_sems.at[5]),
        ]
        for r in range(GDEV):
            span = pl.ds(r * CHUNK, CHUNK)
            out.append(pltpu.make_async_copy(kv_s.at[r, 0], kp_out.at[span, :], loc_sems.at[6 + 2 * r]))
            out.append(pltpu.make_async_copy(kv_s.at[r, 1], vp_out.at[span, :], loc_sems.at[7 + 2 * r]))
        return out

    @pl.when((pair == 0) & (step == 0))
    def _():
        greet([near, far, across])
        for copy in fetch_y:
            copy.start()
        gain_f, bias_f = vec[:, pl.ds(0, D)], vec[:, pl.ds(D, D)]
        query_bias = vec[:, pl.ds(2 * D, width)]
        value_bias = vec[:, pl.ds(2 * D + width, width)]

        def norm(at, size):
            x = hid[at : at + size, :].astype(F32)
            center = jnp.mean(x, axis=1, keepdims=True)
            scale = lax.rsqrt(jnp.mean(x * x, axis=1, keepdims=True) - center * center + EPSILON)
            low = ((x - center) * scale * gain_f + bias_f).astype(BF)
            low_s[at : at + size, :] = low
            return low

        low = norm(0, CHUNK)
        kv_s[0, 0] = dot_nn(low, wk[...]).astype(BF)
        kv_s[0, 1] = (dot_nn(low, wv[...]) + value_bias).astype(BF)
        to_far(0).start()
        for p in range(n_pairs):
            to_near(p).start()
        for at in range(CHUNK, rows, TILE):
            low = norm(at, TILE)
            ko_s[at - CHUNK : at - CHUNK + TILE, :] = dot_nn(low, wk[...]).astype(BF)
            vo_s[at - CHUNK : at - CHUNK + TILE, :] = (dot_nn(low, wv[...]) + value_bias).astype(BF)
        to_far(0).wait_send()
        for p in range(1, n_pairs):
            to_far(p).start()
        for at in range(0, rows, TILE):
            scaled = (dot_nn(low_s[at : at + TILE, :], wq[...]) + query_bias) * 0.125
            q_s[at : at + TILE, :] = scaled.astype(BF)
            qe_s[at : at + TILE, :] = (scaled * LOG2E).astype(BF)
        to_far(0).wait_recv()
        relay(0).start()

    for p in range(n_pairs):
        @pl.when((pair == p) & (step == 0))
        def _():
            to_near(p).wait_recv()
            relay(p).wait_recv()

        if p + 1 < n_pairs:
            @pl.when((pair == p) & (step == 3))
            def _():
                to_far(p + 1).wait_recv()
                relay(p + 1).start()

    lanes = pl.ds(pl.multiple_of(pair * 128, 128), 128)
    low = low_half(TILE)
    q = qe_s[pl.ds(pl.multiple_of(step * TILE, TILE), TILE), lanes]
    row = lax.broadcasted_iota(jnp.int32, (TILE, 128), 0).astype(F32)
    group = device // GDEV
    start = starts[group]
    first_cont = member * (conts // CONT)
    own_gap = gaps[group, first_cont + jnp.maximum(step - PTILES, 0)]
    base_q = start + jnp.where(step < PTILES, member * CHUNK + step * TILE, PROMPT + own_gap)
    cells = settings(seg, rate, side * n_pairs + pair)
    at_q = base_q.astype(F32) + row
    qc = codes(at_q, cells, -2.0)
    classes = [lane_classes(h) for h in range(2)]
    first_at = start.astype(F32)

    @pl.when(step == 0)
    def _():
        for j in range(GDEV):
            first = first_at + (xor_bits(j, member) * CHUNK).astype(F32)
            for h, made in enumerate(key_side(kv_s[j, 0, :, lanes], first, cells, classes)):
                ka_s[h, j * CHUNK : (j + 1) * CHUNK, :] = made

    def logits(h, top, keys, first, causal, at, width):
        t = dot_nt(query_side(h, q, qc, first, cells, classes[h], low), keys)
        if causal is not None:
            t = jnp.where(causal, t, MASKED)
        t_s[h, :, pl.ds(at, width)] = t
        for g in range(width // 128):
            top = jnp.maximum(top, t[:, g * 128 : (g + 1) * 128])
        return top

    def weigh(h, carry, vals, m, at, width):
        total, acc = carry
        parts = []
        for g in range(width // 128):
            e = jnp.exp2(t_s[h, :, pl.ds(at + g * 128, 128)] - m)
            total = total + e
            parts.append(e.astype(BF))
        el = jnp.concatenate(parts, axis=1)
        e_ref[h, :, pl.ds(at, width)] = el
        return total, acc + dot_nn(el, vals)

    def finish_rows(carry):
        (sums0, acc0), (sums1, acc1) = carry
        sums, accs = (sums0, sums1), (acc0, acc1)
        li = [1.0 / jnp.sum(s, axis=1, keepdims=True) for s in sums]
        lfull = jnp.where(low, li[0], li[1])
        li_ref[...] = lfull
        o_s[pl.ds(pl.multiple_of(step * TILE, TILE), TILE), lanes] = (jnp.where(low, accs[0], accs[1]) * lfull).astype(BF)

    def tops(mx):
        return jnp.broadcast_to(jnp.max(mx, axis=1, keepdims=True), (TILE, 128))

    neg = jnp.full((TILE, 128), -jnp.inf, F32)
    zf = jnp.zeros((TILE, 128), F32)

    def held_keys(h, at):
        return ka_s[h, pl.ds(at, CHUNK), :]

    @pl.when(step < PTILES)
    def _():
        rows_id = lax.broadcasted_iota(jnp.int32, (TILE, CHUNK), 0) + step * TILE
        cols = lax.broadcasted_iota(jnp.int32, (TILE, CHUNK), 1)
        here = first_at + (member * CHUNK).astype(F32)

        def place(j):
            return pl.multiple_of(xor_bits(j, member) * CHUNK, CHUNK)

        def score(h, j, top):
            return logits(h, top, held_keys(h, place(j)), first_at + (j * CHUNK).astype(F32), None, place(j), CHUNK)

        def spread(h, j, m, carry):
            return weigh(h, carry, kv_s[xor_bits(j, member), 1, :, lanes], m, place(j), CHUNK)

        top = lax.fori_loop(0, member, lambda j, top: score(0, j, top), neg)
        m0 = tops(logits(0, top, held_keys(0, 0), here, cols <= rows_id, 0, CHUNK))

        def both(j, carry):
            return spread(0, j, m0, carry[0]), score(1, j, carry[1])

        first, top = lax.fori_loop(0, member, both, ((zf, zf), neg))
        first = weigh(0, first, kv_s[0, 1, :, lanes], m0, 0, CHUNK)
        m1 = tops(logits(1, top, held_keys(1, 0), here, cols <= rows_id, 0, CHUNK))
        finish_rows((first, lax.fori_loop(0, member + 1, lambda j, carry: spread(1, j, m1, carry), (zf, zf))))

    @pl.when(step >= PTILES)
    def _():
        own_rows = pl.ds(pl.multiple_of((step - PTILES) * TILE, TILE), TILE)
        rows_id = lax.broadcasted_iota(jnp.int32, (TILE, CONT), 0)
        cols = lax.broadcasted_iota(jnp.int32, (TILE, CONT), 1)
        own_at = base_q.astype(F32)
        own = key_side(ko_s[own_rows, lanes], own_at, cells, classes)

        def score(h, j, top):
            if j == GDEV:
                return logits(h, top, own[h], own_at, cols <= rows_id, PROMPT, CONT)
            first = first_at + (xor_bits(j, member) * CHUNK).astype(F32)
            return logits(h, top, held_keys(h, j * CHUNK), first, None, j * CHUNK, CHUNK)

        def spread(h, j, m, carry):
            if j == GDEV:
                return weigh(h, carry, vo_s[own_rows, lanes], m, PROMPT, CONT)
            return weigh(h, carry, kv_s[j, 1, :, lanes], m, j * CHUNK, CHUNK)

        top = neg
        for j in range(GDEV + 1):
            top = score(0, j, top)
        m0, top, first, second = tops(top), neg, (zf, zf), (zf, zf)
        for j in range(GDEV + 1):
            first = spread(0, j, m0, first)
            top = score(1, j, top)
        m1 = tops(top)
        for j in range(GDEV + 1):
            second = spread(1, j, m1, second)
        finish_rows((first, second))

    end = pl.num_programs(1) - 1
    for p in range(n_pairs):
        @pl.when((pair == p) & (step == 1 - side))
        def _():
            give(p, 0).start()

        for unit in range(6):
            @pl.when((pair == p) & (step == PTILES + unit // 2) & (side == 1 - unit // 3))
            def _():
                give(p, 1 + unit % 3).start()

    @pl.when((pair == last_pair - 1) & (step == 3))
    def _():
        for i in range(2):
            fetch_y[i].wait_recv()
            fetch_core[i].start()

    @pl.when((pair == last_pair) & (step == 0))
    def _():
        for copy in saves():
            copy.start()

    @pl.when((pair == last_pair) & (step == end))
    def _():
        for copy in keeps():
            copy.start()
        fetch_y[2].wait_recv()
        for copy in fetch_core:
            copy.wait_recv()
        for p in range(n_pairs):
            for piece in range(4):
                copy = give(p, piece)
                copy.wait_recv()
                copy.wait_send()
            if p > 0:
                to_far(p).wait_send()
            to_near(p).wait_send()
            relay(p).wait_send()
        for copy in fetch_y + fetch_core:
            copy.wait_send()
        for copy in keeps() + saves():
            copy.wait()


def attend(starts, gaps, seg, rate, hid, vec, wq, wk, wv, w1, wo):
    rows = hid.shape[0]
    width = wq.shape[1]
    pairs = width // 128
    span = PROMPT + CONT
    conts = rows - CHUNK
    units = w1.shape[1]
    vmem = pl.BlockSpec(memory_space=pltpu.VMEM)
    hbm = pl.BlockSpec(memory_space=pl.ANY)
    shape = jax.ShapeDtypeStruct
    copies = 3 * pairs + 5 + 4 * pairs
    shared = 3 * units + 2 * width
    smem = pl.BlockSpec(memory_space=pltpu.SMEM)
    return pl.pallas_call(
        fwd_kernel,
        grid_spec=pltpu.PrefetchScalarGridSpec(
            num_scalar_prefetch=0,
            grid=(pairs, rows // TILE),
            in_specs=[smem] * 4 + [vmem] * 5 + [hbm] * 3,
            out_specs=[
                pl.BlockSpec((2, TILE, span), lambda a, t: (a, t, 0)),
                pl.BlockSpec((TILE, 128), lambda a, t: (t, a)),
            ]
            + [hbm] * 13,
            scratch_shapes=[
                pltpu.VMEM((2, TILE, span), F32),
                pltpu.VMEM((2, PROMPT, 128), BF),
                pltpu.VMEM((GDEV, 2, CHUNK, width), BF),
                pltpu.VMEM((rows, D), BF),
                pltpu.VMEM((rows, width), BF),
                pltpu.VMEM((rows, width), BF),
                pltpu.VMEM((conts, width), BF),
                pltpu.VMEM((conts, width), BF),
                pltpu.VMEM((rows, width), BF),
                pltpu.SemaphoreType.DMA((copies,)),
                pltpu.SemaphoreType.DMA((copies,)),
                pltpu.SemaphoreType.DMA((6 + 2 * GDEV,)),
            ],
        ),
        out_shape=[
            shape((2 * pairs, rows, span), BF),
            shape((rows, width), F32),
            shape((rows, width), BF),
            shape((conts, width), BF),
            shape((conts, width), BF),
            shape((PROMPT, width), BF),
            shape((PROMPT, width), BF),
            shape((rows, width), BF),
            shape((rows // 2, width), BF),
            shape((rows // 2, width), BF),
            shape((D, units // 2), BF),
            shape((D, units // 2), BF),
            shape((width // 2, D), BF),
            shape((width // 2, D), BF),
            shape((1, shared), F32),
        ],
        compiler_params=pltpu.CompilerParams(vmem_limit_bytes=56 << 20, collective_id=0, has_side_effects=True),
        cost_estimate=pl.CostEstimate(flops=20 * 10**9, bytes_accessed=60 * 10**6, transcendentals=0),
        name="attend",
    )(starts, gaps, seg, rate, hid, vec, wq, wk, wv, w1, wo, vec)


EARLY = 2
FIRST_CUT = 1920


def reducer_scratch(count, block, cut):
    return [
        pltpu.VMEM((count, 2, 2, 2, block, cut), BF),
        pltpu.VMEM((count, 2, 2, 2, block, cut), BF),
        pltpu.VMEM((count, 2, 2, block, cut), BF),
        pltpu.VMEM((count, 2, 2, block, cut), BF),
        pltpu.VMEM((count, 2, block, cut), BF),
        pltpu.VMEM((count, 2, block, cut), BF),
        pltpu.VMEM((count, block, cut), BF),
        pltpu.SemaphoreType.DMA((4 * count,)),
        pltpu.SemaphoreType.DMA((4 * count,)),
        pltpu.SemaphoreType.DMA((count,)),
    ]


def reducer(packed, device, side, base, refs, done):
    held, got0, got1, held1, got2, held2, got3, sems_a, sems_b, sems_l = refs
    bit = [(device // (1 << b)) % 2 for b in range(4)]
    peers = [{"dp": bit_peer(device, b), "tensor": side} for b in range(4)]
    cut = held.shape[-1]

    def passing(c, stage, source, target, peer):
        return pltpu.make_async_remote_copy(
            src_ref=source,
            dst_ref=target,
            send_sem=sems_a.at[4 * c + stage],
            recv_sem=sems_b.at[4 * c + stage],
            device_id=peer,
            device_id_type=MESH,
        )

    count = held.shape[0]

    def columns_of(c, first):
        return pl.ds(first + (count - 1 - c) * cut, cut)

    def own_half(c):
        return pltpu.make_async_copy(packed.at[:, :, :, bit[0], :, columns_of(c, base)], held.at[c], sems_l.at[c])

    def stage0(c):
        return passing(c, 0, packed.at[:, :, :, 1 - bit[0], :, columns_of(c, base)], got0.at[c], peers[0])

    def stage1(c):
        if c % 2:
            return passing(c, 1, held.at[c, :, 1 - bit[2]], got1.at[c], peers[2])
        return passing(c, 1, held.at[c, :, :, 1 - bit[1]], got1.at[c], peers[1])

    def stage2(c):
        b = 1 if c % 2 else 2
        return passing(c, 2, held1.at[c, :, 1 - bit[b]], got2.at[c], peers[b])

    def stage3(c):
        return passing(c, 3, held2.at[c, 1 - bit[3]], got3.at[c], peers[3])

    def begin(c):
        own_half(c).start()
        stage0(c).start()

    def after0(c):
        own_half(c).wait()
        stage0(c).wait_recv()
        held[c] = held[c] + got0[c]
        stage1(c).start()

    def after1(c):
        stage1(c).wait_recv()
        kept = held[c, :, bit[2]] if c % 2 else held[c, :, :, bit[1]]
        held1[c] = kept + got1[c]
        stage2(c).start()

    def after2(c):
        stage2(c).wait_recv()
        held2[c] = held1[c, :, bit[1 if c % 2 else 2]] + got2[c]
        stage3(c).start()

    def after3(c):
        stage3(c).wait_recv()
        done[:, columns_of(c, 0)] = held2[c, bit[3]] + got3[c]

    def settle():
        for c in range(count):
            for copy in (stage0(c), stage1(c), stage2(c), stage3(c)):
                copy.wait_send()

    return begin, after0, after1, after2, after3, settle


def bwd_kernel(
    fused, q_ref, kp_ref, vp_ref, ko_ref, vo_ref, o_ref, li_ref, e_ref, g_mine, g_theirs, out_half, *refs
):
    packed = refs[0] if fused else None
    refs = refs[1:] if fused else refs
    dq_ref, dko_ref, dvo_ref, sum_k, sum_v, relay_out, out_got = refs[:7]
    done_out, other_out = refs[7:9] if fused else (None, None)
    refs = refs[9:] if fused else refs[7:]
    dk_s, dv_s, g_s, grad_s, near_s, relay_s, far_s, sems_a, sems_b, loc_sems = refs[:10]
    pair = pl.program_id(0)
    step = pl.program_id(1)
    device = lax.axis_index("dp")
    side = lax.axis_index("tensor")
    member = device % GDEV
    rows, width = g_s.shape
    n_pairs = width // 128
    conts = rows - CHUNK
    half_p, half_c = CHUNK // 2, conts // 2
    near = {"dp": bit_peer(device, 0), "tensor": side}
    far = {"dp": bit_peer(device, 1), "tensor": side}
    across = {"dp": device, "tensor": 1 - side}
    lanes = pl.ds(pl.multiple_of(pair * 128, 128), 128)
    mine_p = pl.ds(pl.multiple_of(side * half_p, 128), half_p)
    mine_c = pl.ds(pl.multiple_of(CHUNK + side * half_c, 128), half_c)

    def remote(i, src, dst, peer):
        return pltpu.make_async_remote_copy(
            src_ref=src, dst_ref=dst, send_sem=sems_a.at[i], recv_sem=sems_b.at[i], device_id=peer, device_id_type=MESH
        )

    def heads():
        return [
            remote(0, g_theirs.at[pl.ds(0, half_p), :], g_s.at[mine_p, :], across),
            remote(1, g_theirs.at[pl.ds(half_p, half_c), :], g_s.at[mine_c, :], across),
            remote(2, out_half, out_got, across),
        ]

    def local():
        return [
            pltpu.make_async_copy(g_mine.at[pl.ds(0, half_p), :], g_s.at[mine_p, :], loc_sems.at[0]),
            pltpu.make_async_copy(g_mine.at[pl.ds(half_p, half_c), :], g_s.at[mine_c, :], loc_sems.at[1]),
        ]

    def cores(p):
        part = pl.ds(p * 128, 128)
        return remote(3 + 2 * p, grad_s.at[:, :, 1, :, part], near_s.at[:, :, :, part], near)

    def chips(p):
        part = pl.ds(p * 128, 128)
        return remote(4 + 2 * p, relay_s.at[:, :, part], far_s.at[:, :, part], far)

    if fused:
        *early_refs, done_s, other_a, early_sems = refs[10:]
        begin, after0, after1, after2, after3, settle = reducer(
            packed, device, side, packed.shape[-1] - EARLY * FIRST_CUT, early_refs, done_s
        )
        half_e = packed.shape[-1] // 2
        tail_e = EARLY * FIRST_CUT - half_e
        peers = [{"dp": bit_peer(device, b), "tensor": side} for b in range(4)]
        swap = pltpu.make_async_remote_copy(
            src_ref=done_s.at[:, pl.ds(tail_e, half_e)],
            dst_ref=other_a,
            send_sem=early_sems.at[0],
            recv_sem=early_sems.at[1],
            device_id=across,
            device_id_type=MESH,
        )
        tick = pair * pl.num_programs(1) + step

    @pl.when((pair == 0) & (step == 0))
    def _():
        greet([near, far, across] + (peers[2:] if fused else []))
        for copy in heads() + local():
            copy.start()
        for copy in local():
            copy.wait()

    if fused:
        for c in range(EARLY):
            for at, act in ((0, begin), (1 + c, after0), (5 + c, after1), (8 + c, after2), (12, after3)):
                @pl.when(tick == at)
                def _():
                    act(c)

        @pl.when(tick == 12)
        def _():
            swap.start()

    @pl.when((pair == 0) & (step == 1 - side))
    def _():
        heads()[0].wait_recv()

    @pl.when((pair == 0) & (step == 3 - side))
    def _():
        heads()[1].wait_recv()

    low = low_half(TILE)
    g = g_s[pl.ds(pl.multiple_of(step * TILE, TILE), TILE), lanes].astype(F32) * li_ref[...]
    prod = g * o_ref[...].astype(F32)
    zf = jnp.zeros((TILE, 128), F32)
    deltas = [
        jnp.sum(jnp.where(low, prod, zf), axis=1, keepdims=True),
        jnp.sum(jnp.where(low, zf, prod), axis=1, keepdims=True),
    ]
    gs = [jnp.where(low, g, zf).astype(BF), jnp.where(low, zf, g).astype(BF)]
    gt = jnp.transpose(g).astype(BF)
    qt = jnp.transpose(q_ref[...].astype(F32)).astype(BF)

    def grads(dq, keys, vals, at, width):
        out, dks, dvs = [], [], []
        for h in range(2):
            e = e_ref[h, :, pl.ds(at, width)]
            dp = dot_nt(gs[h], vals)
            ds = (e.astype(F32) * (dp - deltas[h])).astype(BF)
            out.append(dq[h] + dot_nn(ds, keys))
            dks.append(dot_nn(qt[h * HD : (h + 1) * HD, :], ds))
            dvs.append(dot_nn(gt[h * HD : (h + 1) * HD, :], e))
        return tuple(out), dks, dvs

    @pl.when(step == 0)
    def _():
        dk_s[...] = jnp.zeros_like(dk_s)
        dv_s[...] = jnp.zeros_like(dv_s)

    def add(at, width, dks, dvs):
        for h in range(2):
            dk_s[h * HD : (h + 1) * HD, pl.ds(at, width)] += dks[h]
            dv_s[h * HD : (h + 1) * HD, pl.ds(at, width)] += dvs[h]

    def scaled(dq):
        return (jnp.where(low, dq[0], dq[1]).astype(BF).astype(F32) * 0.125).astype(BF)

    @pl.when(step < PTILES)
    def _():
        def one(j, dq):
            at = pl.multiple_of(xor_bits(j, member) * CHUNK, CHUNK)
            dq, dks, dvs = grads(dq, kp_ref[pl.ds(at, CHUNK), :], vp_ref[pl.ds(at, CHUNK), :], at, CHUNK)
            add(at, CHUNK, dks, dvs)
            return dq

        dq_ref[...] = scaled(lax.fori_loop(0, member + 1, one, (zf, zf)))
        dko_ref[...] = jnp.zeros_like(dko_ref)
        dvo_ref[...] = jnp.zeros_like(dvo_ref)

    @pl.when(step >= PTILES)
    def _():
        dq = (zf, zf)
        for j in range(GDEV):
            span = slice(j * CHUNK, (j + 1) * CHUNK)
            dq, dks, dvs = grads(dq, kp_ref[span, :], vp_ref[span, :], j * CHUNK, CHUNK)
            add(j * CHUNK, CHUNK, dks, dvs)
        dq, dks, dvs = grads(dq, ko_ref[...], vo_ref[...], PROMPT, CONT)
        dq_ref[...] = scaled(dq)
        dko_ref[...] = jnp.transpose(jnp.concatenate(dks, axis=0)).astype(BF)
        dvo_ref[...] = jnp.transpose(jnp.concatenate(dvs, axis=0)).astype(BF)

    end = pl.num_programs(1) - 1

    @pl.when(step == end)
    def _():
        for j in range(GDEV):
            span = slice(j * CHUNK, (j + 1) * CHUNK)
            grad_s[0, j // 2, j % 2, :, lanes] = jnp.transpose(dk_s[:, span]).astype(BF)
            grad_s[1, j // 2, j % 2, :, lanes] = jnp.transpose(dv_s[:, span]).astype(BF)

    for p in range(n_pairs):
        @pl.when((pair == p) & (step == end))
        def _():
            cores(p).start()

        if p + 1 < n_pairs:
            @pl.when((pair == p + 1) & (step == 2))
            def _():
                part = pl.ds(p * 128, 128)
                cores(p).wait_recv()
                relay_s[:, :, part] = (
                    grad_s[:, 1, 0, :, part].astype(F32) + near_s[:, 1, :, part].astype(F32)
                ).astype(BF)
                chips(p).start()

    @pl.when((pair == n_pairs - 1) & (step == end))
    def _():
        last = n_pairs - 1
        sums = (sum_k, sum_v)
        for p in range(last):
            part = pl.ds(p * 128, 128)
            chips(p).wait_recv()
            for i in range(2):
                sums[i][:, part] = (
                    grad_s[i, 0, 0, :, part].astype(F32) + near_s[i, 0, :, part].astype(F32) + far_s[i, :, part].astype(F32)
                ).astype(BF)
        part = pl.ds(last * 128, 128)
        cores(last).wait_recv()
        for i in range(2):
            relay_out[i] = (grad_s[i, 1, 0, :, part].astype(F32) + near_s[i, 1, :, part].astype(F32)).astype(BF)
            sums[i][:, part] = (grad_s[i, 0, 0, :, part].astype(F32) + near_s[i, 0, :, part].astype(F32)).astype(BF)
        if fused:
            swap.wait_recv()
            done_out[...] = done_s[:, pl.ds(0, tail_e)]
            other_out[...] = other_a[...]
            settle()
            swap.wait_send()
        heads()[2].wait_recv()
        for copy in heads():
            copy.wait_send()
        for p in range(n_pairs):
            cores(p).wait_send()
            if p < last:
                chips(p).wait_send()


def attend_back(q, k, v, kp, vp, o, li, e, g_mine, g_theirs, out_half, packed):
    rows, width = q.shape
    pairs = width // 128
    span = PROMPT + CONT
    tile = pl.BlockSpec((TILE, 128), lambda a, t: (t, a))
    whole = pl.BlockSpec((PROMPT, 128), lambda a, t: (0, a))
    own = pl.BlockSpec((TILE, 128), lambda a, t: (jnp.maximum(t - PTILES, 0), a))
    vmem = pl.BlockSpec(memory_space=pltpu.VMEM)
    hbm = pl.BlockSpec(memory_space=pl.ANY)
    shape = jax.ShapeDtypeStruct
    copies = 3 + 2 * pairs
    fused = packed is not None
    more_in, more_out, more_scratch = [], [], []
    if fused:
        block, half_e = packed.shape[-2], packed.shape[-1] // 2
        more_in = [packed]
        more_out = [shape((block, EARLY * FIRST_CUT - half_e), BF), shape((block, half_e), BF)]
        more_scratch = reducer_scratch(EARLY, block, FIRST_CUT) + [
            pltpu.VMEM((block, EARLY * FIRST_CUT), BF),
            pltpu.VMEM((block, half_e), BF),
            pltpu.SemaphoreType.DMA((2,)),
        ]
    return pl.pallas_call(
        functools.partial(bwd_kernel, fused),
        grid=(pairs, rows // TILE),
        in_specs=[tile, whole, whole, own, own, tile, tile, pl.BlockSpec((2, TILE, span), lambda a, t: (a, t, 0))]
        + [hbm] * (3 + len(more_in)),
        out_specs=[tile, tile, tile, vmem, vmem, vmem, hbm] + [vmem] * len(more_out),
        out_shape=[
            shape((rows, width), BF),
            shape((rows, width), BF),
            shape((rows, width), BF),
            shape((CHUNK, width), BF),
            shape((CHUNK, width), BF),
            shape((2, CHUNK, 128), BF),
            shape(out_half.shape, BF),
        ]
        + more_out,
        scratch_shapes=[
            pltpu.VMEM((128, PROMPT), F32),
            pltpu.VMEM((128, PROMPT), F32),
            pltpu.VMEM((rows, width), BF),
            pltpu.VMEM((2, 2, 2, CHUNK, width), BF),
            pltpu.VMEM((2, 2, CHUNK, width), BF),
            pltpu.VMEM((2, CHUNK, width), BF),
            pltpu.VMEM((2, CHUNK, width), BF),
            pltpu.SemaphoreType.DMA((copies,)),
            pltpu.SemaphoreType.DMA((copies,)),
            pltpu.SemaphoreType.DMA((2,)),
        ]
        + more_scratch,
        compiler_params=pltpu.CompilerParams(vmem_limit_bytes=60 << 20, collective_id=2, has_side_effects=True),
        cost_estimate=pl.CostEstimate(flops=30 * 10**9, bytes_accessed=60 * 10**6, transcendentals=0),
        name="attend_back",
    )(q, kp, vp, k, v, o, li, e, g_mine, g_theirs, out_half, *more_in)


UCH = 768


def polynomial(x, terms):
    out = jnp.full_like(x, terms[0])
    for term in terms[1:]:
        out = out * x + term
    return out


def gelu_pair(v):
    bell = jnp.exp(-0.5 * v * v)
    t = 1.0 / (1.0 + (0.3275911 * 0.7071067811865476) * jnp.abs(v))
    terms = (0.5307027145, -0.7265760135, 0.7107068705, -0.142248368, 0.127414796)
    half = polynomial(t, terms) * t * bell
    phi = jnp.where(v < 0.0, half, 1.0 - half)
    return v * phi, phi + v * (bell * 0.3989422804014327)


def column_sum(x):
    return jnp.sum(x, axis=0, keepdims=True)


def mid_kernel(
    att_m, att_o, vec_all, vec_got, hid_all, cot_all, w1_own, w1_got, w1_swap, wo_own, wo_got, wo_swap, w2_own,
    out_ref, gatt_m, gatt_o, gmix_ref, packed, su_ref, sw_ref, sd_ref, ext_ref,
    vec_u, vec_w, w1, w2, wo, act_s, shp_s, dg_s, wide_s, acc_s, gmid_s, sub_s, mid_s, low_s, midt_s, cott_s, stage, hid, cot, sems, out_sems, send_sems, recv_sems,
):
    device = lax.axis_index("dp")
    side = lax.axis_index("tensor")
    core = device % 2
    near = {"dp": bit_peer(device, 0), "tensor": side}
    across = {"dp": device, "tensor": 1 - side}
    units = w1_own.shape[1]
    width = wo_own.shape[0]
    rows = hid.shape[0]
    full = 2 * units
    half = units // 2
    half_w = width // 2
    here_u = pl.multiple_of(units + core * half, 128)
    there_u = pl.multiple_of(units + (1 - core) * half, 128)
    here_w = pl.multiple_of(width + core * half_w, 64)
    there_w = pl.multiple_of(width + (1 - core) * half_w, 64)
    prompt, conts = CHUNK // 2, (hid_all.shape[0] - CHUNK) // 2
    own_p = pl.ds(pl.multiple_of(side * prompt, 128), prompt)
    own_c = pl.ds(pl.multiple_of(CHUNK + side * conts, 128), conts)
    at_own = 2 * D + 2 * width
    vec_own = vec_all.at[:, pl.ds(at_own, 3 * units + 2 * width)]
    vec_d = vec_all.at[:, pl.ds(at_own + 3 * units + 2 * width, 4 * D)]
    rows_in = []
    for i, (all_rows, held) in enumerate(((hid_all, hid), (cot_all, cot))):
        for j, (span, at, size) in enumerate(((own_p, 0, prompt), (own_c, prompt, conts))):
            copy = pltpu.make_async_copy(all_rows.at[span, :], held.at[pl.ds(at, size), :], sems.at[7 + 2 * i + j])
            copy.start()
            rows_in.append(copy)
    loads = []
    for i, (src, dst) in enumerate(
        [
            (wo_own, wo.at[pl.ds(0, width), :]),
            (wo_got, wo.at[pl.ds(here_w, half_w), :]),
            (wo_swap, wo.at[pl.ds(there_w, half_w), :]),
            (w1_own, w1.at[:, pl.ds(0, units)]),
            (w1_got, w1.at[:, pl.ds(here_u, half)]),
            (w1_swap, w1.at[:, pl.ds(there_u, half)]),
            (w2_own, w2.at[pl.ds(0, units), :]),
        ]
    ):
        copy = pltpu.make_async_copy(src, dst, sems.at[i])
        copy.start()
        loads.append(copy)

    piece = half // 2
    greet([near, across])

    def remote(i, src, dst, peer):
        return pltpu.make_async_remote_copy(
            src_ref=src, dst_ref=dst, send_sem=send_sems.at[i], recv_sem=recv_sems.at[i], device_id=peer, device_id_type=MESH
        )

    over, passed = [], []
    for i in range(2):
        from_own = pl.ds(pl.multiple_of(core * half + i * piece, 128), piece)
        landed = w2.at[pl.ds(pl.multiple_of(units + core * half + i * piece, 128), piece), :]
        over.append(remote(i, w2_own.at[from_own, :], landed, across))
        passed.append(remote(2 + i, landed, landed, near))
        over[i].start()

    for i in range(3):
        for j, vec in enumerate((vec_own, vec_got)):
            vec_u[i : i + 1, pl.ds(j * units, units)] = vec[0:1, pl.ds(i * units, units)]
    for i in range(2):
        for j, vec in enumerate((vec_own, vec_got)):
            vec_w[i : i + 1, pl.ds(j * width, width)] = vec[0:1, pl.ds(3 * units + i * width, width)]

    a0 = att_m[...].astype(F32)
    a1 = att_o[...].astype(F32)
    center = (jnp.sum(a0, axis=1, keepdims=True) + jnp.sum(a1, axis=1, keepdims=True)) * (1.0 / D)
    square = (jnp.sum(a0 * a0, axis=1, keepdims=True) + jnp.sum(a1 * a1, axis=1, keepdims=True)) * (1.0 / D)
    sub_scale = lax.rsqrt(square - center * center + EPSILON)
    sub_s[:, 0:width] = (a0 - center) * sub_scale
    sub_s[:, width : 2 * width] = (a1 - center) * sub_scale
    sub_gain = vec_w[0:1, :]
    low_s[...] = (sub_s[...] * sub_gain + vec_w[1:2, :]).astype(BF)
    for copy in loads[0:3] + rows_in:
        copy.wait()
    mixed = hid[...].astype(F32) + (dot_nn(low_s[...], wo[...]) + vec_d[0:1, pl.ds(0, D)])
    wide_s[...] = mixed
    mean = jnp.mean(mixed, axis=1, keepdims=True)
    mid_scale = lax.rsqrt(jnp.mean(mixed * mixed, axis=1, keepdims=True) - mean * mean + EPSILON)
    mid_s[...] = (mixed - mean) * mid_scale
    mid_gain = vec_d[0:1, pl.ds(768, D)]
    mid_full = mid_s[...] * mid_gain + vec_d[0:1, pl.ds(1536, D)]
    mid_low = mid_full.astype(BF)
    midt_s[...] = jnp.transpose(mid_full).astype(BF)
    cot_full = cot[...].astype(F32)
    cott_s[...] = jnp.transpose(cot_full).astype(BF)
    sd_ref[...] = jnp.zeros_like(sd_ref)
    sd_ref[3:4, :] = column_sum(cot_full)
    for copy in loads[3:6]:
        copy.wait()

    def unrolled(low, high, step, carry):
        for c in range(low, high):
            carry = step(c, carry)
        return carry

    def lanes_sum(x):
        total = x[:, 0:128]
        for i in range(1, x.shape[1] // 128):
            total = total + x[:, i * 128 : (i + 1) * 128]
        return total

    zero = jnp.zeros((rows, 128), F32)
    act_sum, act_square = zero, zero

    def inner_of(c):
        at = c * UCH
        shp_s[:, at : at + UCH] = dot_nn(mid_low, w1[:, at : at + UCH]) + vec_u[2:3, at : at + UCH]

    inner_of(0)
    for c in range(full // UCH):
        at = c * UCH
        if c + 1 < full // UCH:
            inner_of(c + 1)
        act, slope = gelu_pair(shp_s[:, at : at + UCH])
        act_s[:, at : at + UCH] = act
        dg_s[:, at : at + UCH] = slope.astype(BF)
        act_sum, act_square = act_sum + lanes_sum(act), act_square + lanes_sum(act * act)
    ffn_center = jnp.sum(act_sum, axis=1, keepdims=True) * (1.0 / full)
    ffn_scale = lax.rsqrt(
        jnp.sum(act_square, axis=1, keepdims=True) * (1.0 / full) - ffn_center * ffn_center + EPSILON
    )
    loads[6].wait()
    over[0].wait_recv()
    passed[0].start()
    acc_s[...] = jnp.zeros_like(acc_s)
    per = units // UCH
    wide = 2 * units + width

    def column_of(c, extra):
        return pl.multiple_of((c // per) * wide + (c % per) * UCH + extra, 128)

    def send(slot, column):
        return pltpu.make_async_copy(stage.at[slot], packed.at[:, pl.ds(column, UCH)], out_sems.at[slot])

    def put(c, value, extra):
        slot = c % 2

        @pl.when(c >= 2)
        def _():
            send(slot, column_of(c - 2, extra)).wait()

        stage[slot] = value
        send(slot, column_of(c, extra)).start()

    def drain(extra):
        for c in range(full // UCH - 2, full // UCH):
            send(c % 2, column_of(c, extra)).wait()

    def second(c, carry):
        at = pl.multiple_of(c * UCH, UCH)
        unit = (act_s[:, pl.ds(at, UCH)] - ffn_center) * ffn_scale
        act_s[:, pl.ds(at, UCH)] = unit
        gain = vec_u[0:1, pl.ds(at, UCH)]
        low = (unit * gain + vec_u[1:2, pl.ds(at, UCH)]).astype(BF)
        acc_s[...] += dot_nn(low, w2[pl.ds(at, UCH), :])
        grad = dot_nt(cot[...], w2[pl.ds(at, UCH), :])
        cross = grad * unit
        su_ref[0:1, pl.ds(at, UCH)] = column_sum(cross)
        su_ref[1:2, pl.ds(at, UCH)] = column_sum(grad)
        shaped = grad * gain
        shp_s[:, pl.ds(at, UCH)] = shaped
        put(c, dot_nn(cott_s[...], low).astype(BF), units)
        return carry[0] + lanes_sum(shaped), carry[1] + lanes_sum(shaped * unit)

    su_ref[...] = jnp.zeros_like(su_ref)
    sums = unrolled(0, per, second, (zero, zero))
    over[1].wait_recv()
    passed[1].start()
    for copy in passed:
        copy.wait_recv()
    s_sum, s_cross = unrolled(per, 2 * per, second, sums)
    drain(units)
    shaped_mean = jnp.sum(s_sum, axis=1, keepdims=True) * (1.0 / full)
    cross_mean = jnp.sum(s_cross, axis=1, keepdims=True) * (1.0 / full)
    out_ref[...] = (wide_s[...] + (acc_s[...] + vec_d[0:1, pl.ds(2304, D)])).astype(BF)
    gmid_s[...] = jnp.zeros_like(gmid_s)

    def third(c, carry):
        at = pl.multiple_of(c * UCH, UCH)
        g = ffn_scale * (shp_s[:, pl.ds(at, UCH)] - shaped_mean - act_s[:, pl.ds(at, UCH)] * cross_mean)
        low = (g * dg_s[:, pl.ds(at, UCH)].astype(F32)).astype(BF)
        su_ref[2:3, pl.ds(at, UCH)] = column_sum(low.astype(F32))
        gmid_s[...] += dot_nt(low, w1[:, pl.ds(at, UCH)])
        put(c, dot_nn(midt_s[...], low).astype(BF), 0)
        return carry

    unrolled(0, 2 * per, third, 0)
    drain(0)

    grad_mid = gmid_s[...]
    unit = mid_s[...]
    sd_ref[1:2, :] = column_sum(grad_mid * unit)
    sd_ref[2:3, :] = column_sum(grad_mid)
    shaped = grad_mid * mid_gain
    grad_mixed = cot[...].astype(F32) + mid_scale * (
        shaped - jnp.mean(shaped, axis=1, keepdims=True) - unit * jnp.mean(shaped * unit, axis=1, keepdims=True)
    )
    branch = grad_mixed.astype(BF)
    gmix_ref[...] = branch
    branch_f = branch.astype(F32)
    sd_ref[0:1, :] = column_sum(branch_f)
    out_grad = dot_nn(jnp.transpose(branch_f).astype(BF), low_s[...]).astype(BF)
    stage[0, :, 0:width] = out_grad[:, 0:width]
    stage[1, :, 0:width] = out_grad[:, width : 2 * width]
    last = [
        pltpu.make_async_copy(stage.at[i, :, pl.ds(0, width)], packed.at[:, pl.ds(i * wide + 2 * units, width)], out_sems.at[i])
        for i in range(2)
    ]
    for copy in last:
        copy.start()
    grad_sub = dot_nt(branch, wo[...])
    unit = sub_s[...]
    cross = grad_sub * unit
    sw_ref[...] = jnp.zeros_like(sw_ref)
    sw_ref[0:1, :] = column_sum(cross)
    sw_ref[1:2, :] = column_sum(grad_sub)
    shaped = grad_sub * sub_gain
    grad_att = sub_scale * (
        shaped - jnp.mean(shaped, axis=1, keepdims=True) - unit * jnp.mean(shaped * unit, axis=1, keepdims=True)
    )
    gatt_m[...] = grad_att[:, 0:width].astype(BF)
    gatt_o[...] = grad_att[:, width : 2 * width].astype(BF)
    parts = ext_ref.shape[0]
    if parts > 1:
        sums_u, sums_w, sums_d = su_ref[...], sw_ref[...], sd_ref[...]
        for i in range(parts):
            ext_ref[i] = jnp.concatenate(
                [
                    window(sums_u, i * (units // parts)),
                    window(sums_u, units + i * (units // parts)),
                    window(sums_w, i * (width // parts)),
                    window(sums_w, width + i * (width // parts)),
                    window(sums_d, i * (D // parts)),
                    jnp.zeros((8, 128), F32),
                ],
                axis=0,
            ).astype(BF)
    for copy in last:
        copy.wait()
    for copy in over + passed:
        copy.wait_send()


def window(rows8, start):
    base = start // 128 * 128
    size = min(256, rows8.shape[1] - base)
    view = rows8[:, base : base + size]
    shift = start - base
    if shift:
        view = pltpu.roll(view, size - shift, 1)
    return view[:, 0:128]


def middle(att_m, att_o, hid, cot, vec_all, vec_got, w1, w2, wo, parts):
    rows = att_m.shape[0]
    units = w2.shape[0]
    width = wo[0].shape[0]
    vmem = pl.BlockSpec(memory_space=pltpu.VMEM)
    hbm = pl.BlockSpec(memory_space=pl.ANY)
    shape = jax.ShapeDtypeStruct
    return pl.pallas_call(
        mid_kernel,
        in_specs=[vmem] * 4 + [hbm] * 9,
        out_specs=[vmem] * 4 + [hbm] + [vmem] * 4,
        out_shape=[
            shape((rows, D), BF),
            shape((rows, width), BF),
            shape((rows, width), BF),
            shape((rows, D), BF),
            shape((D, 2 * (2 * units + width)), BF),
            shape((8, 2 * units), F32),
            shape((8, 2 * width), F32),
            shape((8, D), F32),
            shape((parts, 48, 128), BF),
        ],
        scratch_shapes=[
            pltpu.VMEM((8, 2 * units), F32),
            pltpu.VMEM((8, 2 * width), F32),
            pltpu.VMEM((D, 2 * units), BF),
            pltpu.VMEM((2 * units, D), BF),
            pltpu.VMEM((2 * width, D), BF),
            pltpu.VMEM((rows, 2 * units), F32),
            pltpu.VMEM((rows, 2 * units), F32),
            pltpu.VMEM((rows, 2 * units), BF),
            pltpu.VMEM((rows, D), F32),
            pltpu.VMEM((rows, D), F32),
            pltpu.VMEM((rows, D), F32),
            pltpu.VMEM((rows, 2 * width), F32),
            pltpu.VMEM((rows, D), F32),
            pltpu.VMEM((rows, 2 * width), BF),
            pltpu.VMEM((D, rows), BF),
            pltpu.VMEM((D, rows), BF),
            pltpu.VMEM((2, D, UCH), BF),
            pltpu.VMEM((rows, D), BF),
            pltpu.VMEM((rows, D), BF),
            pltpu.SemaphoreType.DMA((11,)),
            pltpu.SemaphoreType.DMA((2,)),
            pltpu.SemaphoreType.DMA((4,)),
            pltpu.SemaphoreType.DMA((4,)),
        ],
        compiler_params=pltpu.CompilerParams(vmem_limit_bytes=62 << 20, collective_id=3, has_side_effects=True),
        cost_estimate=pl.CostEstimate(flops=21 * 10**9, bytes_accessed=30 * 10**6, transcendentals=0),
        name="middle",
    )(att_m, att_o, vec_all, vec_got, hid, cot, *w1, *wo, w2)


def final_kernel(
    bits, hid, vec_all, dq, dk, dv, wq, wk, wv, gmix, ext, sum_k, sum_v, relay, first_done, first_other, packed,
    gin, late_out, vec_out, early_out,
    loc_s, far_s, unit_s, mine_s, norm_s, send_c, recv_c, send_p, recv_p, give_c, give_p, late_s, small_s,
    vec_s, vec_r, done_s, sems_a, sems_b, loc_sems, *stage_refs,
):
    device = lax.axis_index("dp")
    side = lax.axis_index("tensor")
    across = {"dp": device, "tensor": 1 - side}
    peers = [{"dp": bit_peer(device, b), "tensor": side} for b in range(bits)]
    rows, width = dq.shape
    prompt = sum_k.shape[0]
    conts = rows - prompt
    half_p, half_c = prompt // 2, conts // 2
    own_p = pl.multiple_of(side * half_p, 128)
    their_p = pl.multiple_of((1 - side) * half_p, 128)
    own_c = pl.multiple_of(prompt + side * half_c, 128)
    their_c = pl.multiple_of(prompt + (1 - side) * half_c, 128)
    lanes = 3 * width + 128

    greet(peers + [across])
    count = [0]

    def remote(src, dst, peer):
        i = count[0]
        count[0] += 1
        copy = pltpu.make_async_remote_copy(
            src_ref=src, dst_ref=dst, send_sem=sems_a.at[i], recv_sem=sems_b.at[i], device_id=peer, device_id_type=MESH
        )
        copy.start()
        return copy

    share = remote(relay, far_s, peers[1])

    begin, after0, after1, after2, after3, settle = reducer(packed, device, side, 0, stage_refs[-10:], done_s)

    def each(act):
        for c in range(EARLY):
            act(c)

    each(begin)

    gain_f = vec_all[:, pl.ds(0, D)]
    bias_f = vec_all[:, pl.ds(D, D)]

    def unit_rows(at, size):
        x = hid[pl.ds(at, size), :].astype(F32)
        center = jnp.mean(x, axis=1, keepdims=True)
        scale = lax.rsqrt(jnp.mean(x * x, axis=1, keepdims=True) - center * center + EPSILON)
        return (x - center) * scale, scale

    def part_of(at, size, k_rows, v_rows):
        return dot_nt(dq[pl.ds(at, size), :], wq[...]) + dot_nt(k_rows, wk[...]) + dot_nt(v_rows, wv[...])

    def gather(part, unit):
        return column_sum(part * unit), column_sum(part)

    def normed_rows(at, size, unit):
        norm_s[:, pl.ds(at, size)] = jnp.transpose(unit * gain_f + bias_f).astype(BF)

    part = part_of(their_c, half_c, dk[pl.ds(their_c, half_c), :], dv[pl.ds(their_c, half_c), :])
    send_c[...] = part.astype(BF)
    y_cont = remote(send_c, recv_c, across)
    unit, _ = unit_rows(their_c, half_c)
    gain_grad, bias_grad = gather(part, unit)
    normed_rows(their_c, half_c, unit)
    unit, scale_c = unit_rows(own_c, half_c)
    part = part_of(own_c, half_c, dk[pl.ds(own_c, half_c), :], dv[pl.ds(own_c, half_c), :])
    mine_s[pl.ds(half_p, half_c), :] = part
    unit_s[pl.ds(half_p, half_c), :] = unit
    g, b = gather(part, unit)
    gain_grad, bias_grad = gain_grad + g, bias_grad + b
    normed_rows(own_c, half_c, unit)

    each(after0)
    share.wait_recv()
    for i, total in enumerate((sum_k, sum_v)):
        loc_s[i, :, pl.ds(0, width - 128)] = total[:, pl.ds(0, width - 128)]
        loc_s[i, :, pl.ds(width - 128, 128)] = (
            total[:, pl.ds(width - 128, 128)].astype(F32) + far_s[i].astype(F32)
        ).astype(BF)
    part = part_of(their_p, half_p, loc_s[0, pl.ds(their_p, half_p), :], loc_s[1, pl.ds(their_p, half_p), :])
    send_p[...] = part.astype(BF)
    y_prompt = remote(send_p, recv_p, across)
    unit, _ = unit_rows(their_p, half_p)
    normed_rows(their_p, half_p, unit)
    g, b = gather(part, unit)
    gain_grad, bias_grad = gain_grad + g, bias_grad + b
    unit, scale_p = unit_rows(own_p, half_p)
    unit_s[pl.ds(0, half_p), :] = unit
    normed_rows(own_p, half_p, unit)
    part = part_of(own_p, half_p, loc_s[0, pl.ds(own_p, half_p), :], loc_s[1, pl.ds(own_p, half_p), :])
    mine_s[pl.ds(0, half_p), :] = part
    g, b = gather(part, unit)
    gain_grad, bias_grad = gain_grad + g, bias_grad + b

    blocks = 1 << bits
    block = D // blocks

    def keep(value, lane):
        low = value.astype(BF)
        for i in range(blocks):
            late_s[i // 2, i % 2, :, pl.ds(lane, width)] = low[i * block : (i + 1) * block, :]

    keep(dot_nn(norm_s[...], dq[...]), 0)
    q_bias = column_sum(dq[...].astype(F32))
    for i, rest in enumerate((dk, dv)):
        keep(
            dot_nn(norm_s[:, pl.ds(0, prompt)], loc_s[i])
            + dot_nn(norm_s[:, pl.ds(prompt, conts)], rest[pl.ds(prompt, conts), :]),
            (i + 1) * width,
        )
    v_bias = column_sum(loc_s[1].astype(F32)) + column_sum(dv[pl.ds(prompt, conts), :].astype(F32))

    def norm_back(total, unit, scale, mixed):
        shaped = total * gain_f
        return mixed.astype(F32) + scale * (
            shaped - jnp.mean(shaped, axis=1, keepdims=True) - unit * jnp.mean(shaped * unit, axis=1, keepdims=True)
        )

    small_s[...] = jnp.zeros_like(small_s)
    small_s[0:1, pl.ds(0, width)] = q_bias
    small_s[1:2, pl.ds(0, width)] = v_bias
    small_s[2:3, pl.ds(0, D)] = gain_grad
    small_s[3:4, pl.ds(0, D)] = bias_grad
    small = small_s[...]
    row_id = lax.broadcasted_iota(jnp.int32, (8, 128), 0)
    for i in range(blocks):
        narrow = window(small, i * (width // blocks))
        broad = window(small, i * block)
        tail = jnp.concatenate([ext[i, pl.ds(32, 16), :].astype(F32)[0:8], jnp.where(row_id < 2, narrow, broad)], axis=0)
        late_s[i // 2, i % 2, pl.ds(0, 32), pl.ds(3 * width, 128)] = ext[i, pl.ds(0, 32), :]
        late_s[i // 2, i % 2, pl.ds(32, 16), pl.ds(3 * width, 128)] = tail.astype(BF)

    def input_rows(arrived, at, size, scale, held, rows_at, sem):
        arrived[0].wait_recv()
        here = pl.ds(at, size)
        total = mine_s[here, :] + arrived[1][...].astype(F32)
        held[...] = norm_back(total, unit_s[here, :], scale, gmix[here, :]).astype(BF)
        back = remote(held, gin.at[pl.ds(rows_at, size), :], across)
        kept = pltpu.make_async_copy(held, gin.at[pl.ds(rows_at, size), :], loc_sems.at[sem])
        kept.start()
        return back, kept

    source = late_s
    stages = []
    for bit in range(bits):
        landing, kept = stage_refs[2 * bit], stage_refs[2 * bit + 1]
        mine = (device // (1 << bit)) % 2
        copy = remote(source.at[:, 1 - mine], landing, peers[bit])
        if bit == 0:
            back_c, keep_c = input_rows((y_cont, recv_c), half_p, half_c, scale_c, give_c, own_c, 0)
        if bit == 1:
            each(after1)
            back_p, keep_p = input_rows((y_prompt, recv_p), 0, half_p, scale_p, give_p, own_p, 1)
        if bit == 2:
            each(after2)
        if bit == 3:
            each(after3)
        copy.wait_recv()
        stages.append(copy)
        for i in range(landing.shape[0]):
            kept[i // 2, i % 2] = (source[i, mine].astype(F32) + landing[i].astype(F32)).astype(BF)
        source = kept
    late_out[...] = source[0, 0, :, pl.ds(0, 3 * width)].astype(F32)
    vec_s[...] = source[0, 0, :, pl.ds(3 * width, 128)]
    swap = remote(vec_s, vec_r, across)
    last_e = done_s.shape[1]
    early_out[:, pl.ds(0, last_e)] = done_s[...].astype(F32) + first_other[:, pl.ds(0, last_e)].astype(F32)
    rest_e = first_done.shape[1]
    early_out[:, pl.ds(last_e, rest_e)] = first_done[...].astype(F32) + first_other[:, pl.ds(last_e, rest_e)].astype(F32)
    settle()
    swap.wait_recv()
    own_v, got_v = vec_s[...].astype(F32), vec_r[...].astype(F32)
    vec_out[0:8, :] = own_v[0:8] + got_v[8:16]
    vec_out[8:16, :] = own_v[16:24] + got_v[24:32]
    vec_out[16:24, :] = own_v[32:40] + got_v[32:40]
    vec_out[24:32, :] = own_v[40:48] + jnp.where(row_id < 2, 0.0, got_v[40:48])
    for copy in stages + [share, y_cont, y_prompt, swap]:
        copy.wait_send()
    for copy in (back_c, back_p):
        copy.wait_recv()
        copy.wait_send()
    keep_c.wait()
    keep_p.wait()


def finish(hid, vec_all, dq, dk, dv, wq, wk, wv, gmix, ext, sum_k, sum_v, relay, first_done, first_other, packed):
    rows, width = dq.shape
    ranks = lax.axis_size("dp")
    bits = ranks.bit_length() - 1
    block = D // ranks
    prompt = sum_k.shape[0]
    conts = rows - prompt
    lanes = 3 * width + 128
    vmem = pl.BlockSpec(memory_space=pltpu.VMEM)
    hbm = pl.BlockSpec(memory_space=pl.ANY)
    shape = jax.ShapeDtypeStruct
    copies = 6 + bits
    cut = (packed.shape[-1] - EARLY * FIRST_CUT) // EARLY
    stages = []
    for bit in range(bits):
        left = ranks >> (bit + 1)
        stages.append(pltpu.VMEM((left, block, lanes), BF))
        stages.append(pltpu.VMEM((max(left // 2, 1), min(left, 2), block, lanes), BF))
    return pl.pallas_call(
        functools.partial(final_kernel, bits),
        in_specs=[vmem] * 15 + [hbm],
        out_specs=[hbm, vmem, vmem, vmem],
        out_shape=[shape((rows, D), BF), shape((block, 3 * width), F32), shape((32, 128), F32), shape((block, packed.shape[-1] // 2), F32)],
        scratch_shapes=[
            pltpu.VMEM((2, prompt, width), BF),
            pltpu.VMEM((2, prompt, 128), BF),
            pltpu.VMEM((rows // 2, D), F32),
            pltpu.VMEM((rows // 2, D), F32),
            pltpu.VMEM((D, rows), BF),
            pltpu.VMEM((conts // 2, D), BF),
            pltpu.VMEM((conts // 2, D), BF),
            pltpu.VMEM((prompt // 2, D), BF),
            pltpu.VMEM((prompt // 2, D), BF),
            pltpu.VMEM((conts // 2, D), BF),
            pltpu.VMEM((prompt // 2, D), BF),
            pltpu.VMEM((ranks // 2, 2, block, lanes), BF),
            pltpu.VMEM((8, D + 128), F32),
            pltpu.VMEM((block, 128), BF),
            pltpu.VMEM((block, 128), BF),
            pltpu.VMEM((block, EARLY * cut), BF),
            pltpu.SemaphoreType.DMA((copies,)),
            pltpu.SemaphoreType.DMA((copies,)),
            pltpu.SemaphoreType.DMA((2,)),
        ]
        + stages
        + reducer_scratch(EARLY, block, cut),
        compiler_params=pltpu.CompilerParams(vmem_limit_bytes=56 << 20, collective_id=1, has_side_effects=True),
        cost_estimate=pl.CostEstimate(flops=5 * 10**9, bytes_accessed=20 * 10**6, transcendentals=0),
        name="finish",
    )(hid, vec_all, dq, dk, dv, wq, wk, wv, gmix, ext, sum_k, sum_v, relay, first_done, first_other, packed)


def flip(value, axis, bit):
    return lax.ppermute(value, axis, [(i, i ^ (1 << bit)) for i in range(lax.axis_size(axis))])


def contract_rows(left, right):
    return lax.dot_general(left, right, (((0,), (0,)), ((), ())), preferred_element_type=F32)


def back_project(left, right):
    return lax.dot_general(left, right, (((1,), (1,)), ((), ())), preferred_element_type=F32)


def norm_rows(values, gain, bias):
    center = jnp.mean(values, axis=-1, keepdims=True)
    spread = jnp.mean(values * values, axis=-1, keepdims=True) - center * center
    scaled = lax.rsqrt(spread + EPSILON)
    unit_rows = (values - center) * scaled
    return (unit_rows * gain + bias, unit_rows, scaled)


def norm_back(grad_rows, gain, unit_rows, scaled):
    shaped = grad_rows * gain
    return scaled * (
        shaped
        - jnp.mean(shaped, axis=-1, keepdims=True)
        - unit_rows * jnp.mean(shaped * unit_rows, axis=-1, keepdims=True)
    )


def in_order(which, mine, other, axis):
    return jnp.where(
        which == 0,
        jnp.concatenate([mine, other], axis=axis),
        jnp.concatenate([other, mine], axis=axis),
    )


def halving(value, device):
    bits = lax.axis_size("dp").bit_length() - 1
    rows, columns = value.shape
    current = value
    for bit in range(bits):
        upper = device // (1 << bit) % 2
        left = bits - bit
        view = current.reshape((1 << (left - 1), 2, -1, columns))
        kept = lax.dynamic_index_in_dim(view, upper, 1, keepdims=False)
        sent = lax.dynamic_index_in_dim(view, 1 - upper, 1, keepdims=False)
        got = flip(sent, "dp", bit)
        current = (kept.astype(F32) + got.astype(F32)).astype(BF)
    return current.reshape(rows >> bits, columns)


def side_by_side(parts):
    total = sum(part.shape[0] for part in parts)
    row, at = jnp.zeros((total,), F32), 0
    for part in parts:
        size = part.shape[0]
        row = row + jnp.pad(part.astype(F32), (at, total - at - size))
        at += size
    return row[None]


def half_of(value, which):
    prompt, conts = CHUNK // 2, (value.shape[0] - CHUNK) // 2
    return jnp.concatenate(
        [
            lax.dynamic_slice_in_dim(value, which * prompt, prompt),
            lax.dynamic_slice_in_dim(value, CHUNK + which * conts, conts),
        ]
    )


def joined(which, mine, other):
    prompt = CHUNK // 2
    low = jnp.where(which == 0, mine, other)
    high = jnp.where(which == 0, other, mine)
    return jnp.concatenate([low[:prompt], high[:prompt], low[prompt:], high[prompt:]])


def body(
    hidden_in,
    cotangent,
    prompt_start,
    cont_gap,
    seg_len,
    dilation_rate,
    pre_gain,
    pre_bias,
    query_weight,
    query_bias,
    key_weight,
    value_weight,
    value_bias,
    sub_gain,
    sub_bias,
    out_weight,
    out_bias,
    mid_gain,
    mid_bias,
    inner_weight,
    inner_bias,
    ffn_gain,
    ffn_bias,
    outer_weight,
    outer_bias,
):
    device = lax.axis_index("dp")
    ranks = lax.axis_size("dp")
    group_id = device // GDEV
    member = device % GDEV
    tensor_id = lax.axis_index("tensor")
    core = device % 2
    width = query_weight.shape[1]
    units = inner_weight.shape[1]
    pairs = width // 128
    rows = hidden_in.shape[0]
    prompt_rows = CHUNK
    cont_count = (rows - prompt_rows) // CONT

    vectors = side_by_side(
        [
            pre_gain,
            pre_bias,
            query_bias,
            value_bias,
            ffn_gain,
            ffn_bias,
            inner_bias,
            sub_gain,
            sub_bias,
            out_bias,
            mid_gain,
            mid_bias,
            outer_bias,
        ]
    )
    pre_gain_f = pre_gain.astype(F32)

    (
        weighed,
        inverse,
        queries,
        keys,
        values,
        prompt_keys,
        prompt_values,
        attended,
        att_mine,
        att_got,
        *pieces,
        vectors_other,
    ) = attend(
        prompt_start,
        cont_gap,
        seg_len.T,
        dilation_rate.T,
        hidden_in,
        vectors,
        query_weight,
        key_weight,
        value_weight,
        inner_weight,
        out_weight,
    )
    inner_parts = (inner_weight, pieces[0], pieces[1])
    out_parts = (out_weight, pieces[2], pieces[3])

    fused = ranks == 16
    out_half, grad_mine, grad_theirs, grad_mixed_low, packed, sum_u, sum_w, sum_d, ext = middle(
        att_mine,
        att_got,
        hidden_in,
        cotangent,
        vectors,
        vectors_other,
        inner_parts,
        outer_weight,
        out_parts,
        ranks if fused else 1,
    )

    grad_query_in, own_key_grad, own_value_grad, key_sum, value_sum, relay, out_got, *early = attend_back(
        queries,
        keys,
        values,
        prompt_keys,
        prompt_values,
        attended,
        inverse,
        weighed,
        grad_mine,
        grad_theirs,
        out_half,
        packed.reshape(2, 2, 2, 2, D // ranks, -1) if fused else None,
    )
    if not fused:
        early = lax.psum_scatter(packed, "dp", scatter_dimension=0, tiled=True)
        early_mine, early_other = jnp.split(early, 2, axis=1)
        early_sum = early_mine.astype(F32) + flip(early_other, "tensor", 0).astype(F32)
    output = joined(tensor_id, out_half, out_got)
    block = D // ranks
    per_u, per_w, per_d = units // ranks, width // ranks, D // ranks
    if fused:
        input_low, late, vec, early_sum = finish(
            hidden_in,
            vectors,
            grad_query_in,
            own_key_grad,
            own_value_grad,
            query_weight,
            key_weight,
            value_weight,
            grad_mixed_low,
            ext,
            key_sum,
            value_sum,
            relay,
            *early,
            packed.reshape(2, 2, 2, 2, D // ranks, -1),
        )
        ffn_gain_grad, ffn_bias_grad, inner_bias_grad = [vec[i, :per_u] for i in range(3)]
        sub_gain_grad, sub_bias_grad = [vec[8 + i, :per_w] for i in range(2)]
        out_bias_grad, mid_gain_grad, mid_bias_grad, outer_bias_grad = [vec[16 + i, :per_d] for i in range(4)]
        query_bias_grad, value_bias_grad = [vec[24 + i, :per_w] for i in range(2)]
        pre_gain_grad, pre_bias_grad = [vec[26 + i, :per_d] for i in range(2)]
    else:
        pre_normed, pre_unit, pre_scale = norm_rows(hidden_in.astype(F32), pre_gain_f, pre_bias.astype(F32))
        pre_low = pre_normed.astype(BF)
        last = width - 128
        far = flip(relay, "dp", 1).astype(F32)
        summed = jnp.stack([key_sum, value_sum]).astype(F32)
        summed = jnp.concatenate([summed[:, :, :last], summed[:, :, last:] + far], axis=2).astype(BF)
        grad_keys = jnp.concatenate([summed[0], own_key_grad[prompt_rows:]], axis=0)
        grad_values = jnp.concatenate([summed[1], own_value_grad[prompt_rows:]], axis=0)

        query_weight_grad = contract_rows(pre_low, grad_query_in)
        key_weight_grad = contract_rows(pre_low, grad_keys)
        value_weight_grad = contract_rows(pre_low, grad_values)
        query_bias_grad = jnp.sum(grad_query_in.astype(F32), axis=0)
        value_bias_grad = jnp.sum(grad_values.astype(F32), axis=0)
        grad_normed_part = (
            back_project(grad_query_in, query_weight)
            + back_project(grad_keys, key_weight)
            + back_project(grad_values, value_weight)
        )
        grad_normed_low = grad_normed_part.astype(BF)
        grad_normed = grad_normed_low.astype(F32) + flip(grad_normed_low, "tensor", 0).astype(F32)
        pre_gain_grad = jnp.sum(grad_normed * pre_unit, axis=0)
        pre_bias_grad = jnp.sum(grad_normed, axis=0)
        grad_mixed_all = joined(tensor_id, grad_mixed_low, flip(grad_mixed_low, "tensor", 0)).astype(F32)
        input_low = (grad_mixed_all + norm_back(grad_normed, pre_gain_f, pre_unit, pre_scale)).astype(BF)

        vec = jnp.concatenate(
            [
                sum_u[:3].reshape(3, 2, ranks, per_u).transpose(2, 1, 0, 3).reshape(ranks, 6 * per_u),
                sum_w[:2].reshape(2, 2, ranks, per_w).transpose(2, 1, 0, 3).reshape(ranks, 4 * per_w),
                sum_d[:4].reshape(4, ranks, per_d).swapaxes(0, 1).reshape(ranks, 4 * per_d),
                jnp.stack([query_bias_grad, value_bias_grad]).reshape(2, ranks, per_w).swapaxes(0, 1).reshape(ranks, 2 * per_w),
                jnp.stack([pre_gain_grad, pre_bias_grad]).reshape(2, ranks, per_d).swapaxes(0, 1).reshape(ranks, 2 * per_d),
            ],
            axis=1,
        )
        count = vec.shape[1]
        vec = jnp.pad(vec, ((0, 0), (0, block * 128 - count))).reshape(D, 128)
        late = halving(
            jnp.concatenate(
                [p.astype(BF) for p in (query_weight_grad, key_weight_grad, value_weight_grad, vec)], axis=1
            ),
            device,
        )
        vec = late[:, 3 * width :].reshape(-1)[:count]
        late = late[:, : 3 * width].astype(F32)
        at_w = 6 * per_u
        at_d = at_w + 4 * per_w
        at_late = at_d + 4 * per_d
        got = flip(vec[:at_late], "tensor", 0).astype(F32)
        vec = vec.astype(F32)
        ffn_gain_grad, ffn_bias_grad, inner_bias_grad = (vec[: 3 * per_u] + got[3 * per_u : at_w]).reshape(3, per_u)
        sub_gain_grad, sub_bias_grad = (vec[at_w : at_w + 2 * per_w] + got[at_w + 2 * per_w : at_d]).reshape(2, per_w)
        out_bias_grad, mid_gain_grad, mid_bias_grad, outer_bias_grad = (vec[at_d:at_late] + got[at_d:]).reshape(4, per_d)
        query_bias_grad, value_bias_grad = vec[at_late : at_late + 2 * per_w].reshape(2, per_w)
        pre_gain_grad, pre_bias_grad = vec[at_late + 2 * per_w :].reshape(2, per_d)
    inner_weight_grad = early_sum[:, :units]
    outer_weight_grad = early_sum[:, units : 2 * units].T
    out_weight_grad = early_sum[:, 2 * units :].T
    return (
        output,
        input_low,
        pre_gain_grad,
        pre_bias_grad,
        late[:, :width],
        query_bias_grad,
        late[:, width : 2 * width],
        late[:, 2 * width : 3 * width],
        value_bias_grad,
        sub_gain_grad,
        sub_bias_grad,
        out_weight_grad,
        out_bias_grad,
        mid_gain_grad,
        mid_bias_grad,
        inner_weight_grad,
        inner_bias_grad,
        ffn_gain_grad,
        ffn_bias_grad,
        outer_weight_grad,
        outer_bias_grad,
    )

def solution(mesh):
    placed = (
        P("dp", None),
        P("dp", None),
        P(),
        P(),
        P(),
        P(),
        P(),
        P(),
        P(None, "tensor"),
        P("tensor"),
        P(None, "tensor"),
        P(None, "tensor"),
        P("tensor"),
        P("tensor"),
        P("tensor"),
        P("tensor", None),
        P(),
        P(),
        P(),
        P(None, "tensor"),
        P("tensor"),
        P("tensor"),
        P("tensor"),
        P("tensor", None),
        P(),
    )
    return jax.shard_map(
        body,
        mesh=mesh,
        in_specs=placed,
        out_specs=(
            P("dp", None),
            P("dp", None),
            P("dp"),
            P("dp"),
            P("dp", "tensor"),
            P(("tensor", "dp")),
            P("dp", "tensor"),
            P("dp", "tensor"),
            P(("tensor", "dp")),
            P(("tensor", "dp")),
            P(("tensor", "dp")),
            P("tensor", "dp"),
            P("dp"),
            P("dp"),
            P("dp"),
            P("dp", "tensor"),
            P(("tensor", "dp")),
            P(("tensor", "dp")),
            P(("tensor", "dp")),
            P("tensor", "dp"),
            P("dp"),
        ),
        check_vma=False,
    )
```

```python
import functools

import jax
import jax.numpy as jnp
from jax import lax
from jax.experimental import pallas as pl
from jax.experimental.pallas import tpu as pltpu
from jax.sharding import PartitionSpec as P

HD = 64
PROMPT = 2048
CONT = 256
GDEV = 4
TILE = 256
CHUNK = PROMPT // GDEV
PTILES = CHUNK // TILE
LOG2E = 1.4426950408889634
BF = jnp.bfloat16
F32 = jnp.float32
D = 768
EPSILON = 1e-05
MESH = pl.DeviceIdType.MESH


def dot_nt(a, b):
    return lax.dot_general(a, b, (((1,), (1,)), ((), ())), preferred_element_type=F32)


def dot_nn(a, b):
    return lax.dot_general(a, b, (((1,), (0,)), ((), ())), preferred_element_type=F32)


def low_half(rows):
    return lax.broadcasted_iota(jnp.int32, (rows, 128), 1) < HD


MASKED = -1e30
CLASSES = 36


def lane_classes(head):
    lane = lax.broadcasted_iota(jnp.int32, (8, 128), 1) - (HD if head == 0 else 0)
    number = lane.astype(F32)
    main = lane < CLASSES
    number = jnp.where(main, number, 4.0 * (number - CLASSES) + 3.0)
    number = jnp.where((lane >= 0) & (lane < CLASSES + CLASSES // 4), number, -5.0)
    combo = jnp.floor((number + 0.5) * 0.25)
    step0 = jnp.floor((combo + 0.5) * (1.0 / 3.0))
    step1 = combo - 3.0 * step0
    rest = number - 4.0 * combo
    flag1 = jnp.where(rest > 1.5, 1.0, 0.0)
    return number, step0, step1, flag1, rest - 2.0 * flag1, jnp.where(main, 0.0, 1.0)


def key_side(keys, first, cells, classes):
    size = keys.shape[0]
    at = first + lax.broadcasted_iota(jnp.int32, (8, size), 1).astype(F32)
    base = jnp.full((8, size), 0.0, F32) + first
    row = lax.broadcasted_iota(jnp.int32, (8, size), 0)

    def cell(i):
        return cells[i][:, 0:1]

    step0 = jnp.floor((at + 0.5) * cell(0)) - jnp.floor((base + 0.5) * cell(0))
    step1 = jnp.floor((at + 0.5) * cell(1)) - jnp.floor((base + 0.5) * cell(1))
    rest1 = at - cell(2) * jnp.floor((at + 0.5) * cell(3))
    rest2 = at - cell(4) * jnp.floor((at + 0.5) * cell(5))
    flag1 = jnp.where(rest1 == jnp.where(row == 0, cell(6), cell(7)), 2.0, 0.0)
    flag2 = jnp.where(rest2 == jnp.where(row == 0, cell(8), cell(9)), 1.0, 0.0)
    columns = jnp.transpose(4.0 * (3.0 * step0 + step1) + flag1 + flag2)
    low = low_half(size)
    hot = [jnp.where(columns[:, h : h + 1] == classes[h][0][0:1], 1.0, 0.0).astype(BF) for h in range(2)]
    return [jnp.where(low, keys, hot[0]), jnp.where(low, hot[1], keys)]


def query_side(head, queries, qc, first, cells, lanes, low):
    _, step0, step1, flag1, flag2, small = lanes
    base = jnp.zeros((8, 128), F32) + first
    kc0 = (jnp.floor((base + 0.5) * cells[0]) + step0)[0:1]
    kc1 = jnp.where(flag1 > 0.5, jnp.floor((base + 0.5) * cells[1]) + step1, -1.0)[0:1]
    weight = jnp.where(qc[0] == kc0, 1.0, 0.0) + jnp.where(qc[1 + head] == kc1, 1.0, 0.0)
    weight = weight + qc[3 + head] * flag2[0:1]
    logs = jnp.maximum(jnp.log2(weight), MASKED)
    logs = jnp.where(small[0:1] > 0.5, logs - logs.astype(BF).astype(F32), logs).astype(BF)
    return jnp.where(low, queries, logs) if head == 0 else jnp.where(low, logs, queries)


def settings(seg, rate, pair):
    def row(value):
        return jnp.full((1, 128), value, jnp.int32).astype(F32)

    def rest(number, period):
        return number - period * jnp.floor((number + 0.5) / period)

    second, third = row(rate[1, pair]), row(rate[2, pair])
    head = row(2 * pair)
    return (
        1.0 / row(seg[0, pair]),
        1.0 / row(seg[1, pair]),
        second,
        1.0 / second,
        third,
        1.0 / third,
        rest(head, second),
        rest(head + 1.0, second),
        rest(head, third),
        rest(head + 1.0, third),
    )


def codes(at, cells, miss):
    first = jnp.floor((at + 0.5) * cells[0])
    second = jnp.floor((at + 0.5) * cells[1])
    rest1 = at - cells[2] * jnp.floor((at + 0.5) * cells[3])
    rest2 = at - cells[4] * jnp.floor((at + 0.5) * cells[5])
    return [
        first,
        jnp.where(rest1 == cells[6], second, miss),
        jnp.where(rest1 == cells[7], second, miss),
        jnp.where(rest2 == cells[8], 1.0, 0.0),
        jnp.where(rest2 == cells[9], 1.0, 0.0),
    ]


def bit_peer(device, bit):
    step = 1 << bit
    return device + (1 - 2 * ((device // step) % 2)) * step


def greet(peers):
    barrier = pltpu.get_barrier_semaphore()
    for peer in peers:
        pl.semaphore_signal(barrier, inc=1, device_id=peer, device_id_type=MESH)
    pl.semaphore_wait(barrier, len(peers))


def xor_bits(a, b):
    return (a % 2 + b % 2) % 2 + 2 * ((a // 2 + b // 2) % 2)


def fwd_kernel(
    starts, gaps, seg, rate, hid, vec, wq, wk, wv, w1, wo, w2, vec_hbm,
    e_ref, li_ref, q_out, k_out, v_out, kp_out, vp_out, o_out, mine_out, got_out,
    w1_got, w1_swap, wo_got, wo_swap, w2_got, w2_swap, vec_got,
    t_s, ka_s, kv_s, low_s, q_s, qe_s, ko_s, vo_s, o_s, sems_a, sems_b, loc_sems,
):
    pair = pl.program_id(0)
    step = pl.program_id(1)
    pairs = pl.num_programs(0)
    device = lax.axis_index("dp")
    side = lax.axis_index("tensor")
    member = device % GDEV
    core = device % 2
    rows, width = q_s.shape
    n_pairs = width // 128
    last_pair = n_pairs - 1
    conts = rows - CHUNK
    near = {"dp": bit_peer(device, 0), "tensor": side}
    far = {"dp": bit_peer(device, 1), "tensor": side}
    across = {"dp": device, "tensor": 1 - side}
    half_u = w1.shape[1] // 2
    half_w = wo.shape[0] // 2
    half_p, half_c = CHUNK // 2, conts // 2
    sent_u = pl.multiple_of(core * half_u, 128)
    shared_at = 2 * D + 2 * width
    sent_w = pl.multiple_of(core * half_w, 64)

    def remote(i, src, dst, peer):
        return pltpu.make_async_remote_copy(
            src_ref=src, dst_ref=dst, send_sem=sems_a.at[i], recv_sem=sems_b.at[i], device_id=peer, device_id_type=MESH
        )

    def to_far(p):
        lanes = pl.ds(p * 128, 128)
        return remote(3 * p, kv_s.at[0, :, :, lanes], kv_s.at[2, :, :, lanes], far)

    def to_near(p):
        lanes = pl.ds(p * 128, 128)
        return remote(3 * p + 1, kv_s.at[0, :, :, lanes], kv_s.at[1, :, :, lanes], near)

    def relay(p):
        lanes = pl.ds(p * 128, 128)
        return remote(3 * p + 2, kv_s.at[2, :, :, lanes], kv_s.at[3, :, :, lanes], near)

    base = 3 * n_pairs
    fetch_y = [
        remote(base, wo.at[pl.ds(sent_w, half_w), :], wo_got, across),
        remote(base + 1, w1.at[:, pl.ds(sent_u, half_u)], w1_got, across),
        remote(base + 2, vec_hbm.at[:, pl.ds(shared_at, vec_got.shape[1])], vec_got, across),
        remote(base + 3, w2.at[pl.ds(sent_u, half_u // 2), :], w2_got, across),
    ]
    fetch_core = [
        remote(base + 4, wo_got, wo_swap, near),
        remote(base + 5, w1_got, w1_swap, near),
        remote(base + 6, w2_got, w2_swap, near),
    ]

    def give(p, piece):
        lanes = pl.ds(p * 128, 128)
        their_p = pl.multiple_of((1 - side) * half_p, 128)
        their_c = pl.multiple_of(CHUNK + (1 - side) * half_c, 128)
        third = half_c // 3
        if piece == 0:
            source, target = pl.ds(their_p, half_p), pl.ds(0, half_p)
        else:
            source = pl.ds(pl.multiple_of(their_c + (piece - 1) * third, 128), third)
            target = pl.ds(half_p + (piece - 1) * third, third)
        return remote(base + 7 + 4 * p + piece, o_s.at[source, lanes], got_out.at[target, lanes], across)

    def keeps():
        own_p = pl.multiple_of(side * half_p, 128)
        own_c = pl.multiple_of(CHUNK + side * half_c, 128)
        return [
            pltpu.make_async_copy(o_s, o_out, loc_sems.at[0]),
            pltpu.make_async_copy(o_s.at[pl.ds(own_p, half_p), :], mine_out.at[pl.ds(0, half_p), :], loc_sems.at[1]),
            pltpu.make_async_copy(o_s.at[pl.ds(own_c, half_c), :], mine_out.at[pl.ds(half_p, half_c), :], loc_sems.at[2]),
        ]

    def saves():
        out = [
            pltpu.make_async_copy(q_s, q_out, loc_sems.at[3]),
            pltpu.make_async_copy(ko_s, k_out, loc_sems.at[0]),
            pltpu.make_async_copy(vo_s, v_out, loc_sems.at[5]),
        ]
        for r in range(GDEV):
            span = pl.ds(r * CHUNK, CHUNK)
            out.append(pltpu.make_async_copy(kv_s.at[r, 0], kp_out.at[span, :], loc_sems.at[6 + 2 * r]))
            out.append(pltpu.make_async_copy(kv_s.at[r, 1], vp_out.at[span, :], loc_sems.at[7 + 2 * r]))
        return out

    @pl.when((pair == 0) & (step == 0))
    def _():
        greet([near, far, across])
        for copy in fetch_y:
            copy.start()
        gain_f, bias_f = vec[:, pl.ds(0, D)], vec[:, pl.ds(D, D)]
        query_bias = vec[:, pl.ds(2 * D, width)]
        value_bias = vec[:, pl.ds(2 * D + width, width)]

        def norm(at, size):
            x = hid[at : at + size, :].astype(F32)
            center = jnp.mean(x, axis=1, keepdims=True)
            scale = lax.rsqrt(jnp.mean(x * x, axis=1, keepdims=True) - center * center + EPSILON)
            low = ((x - center) * scale * gain_f + bias_f).astype(BF)
            low_s[at : at + size, :] = low
            return low

        low = norm(0, CHUNK)
        kv_s[0, 0] = dot_nn(low, wk[...]).astype(BF)
        kv_s[0, 1] = (dot_nn(low, wv[...]) + value_bias).astype(BF)
        to_far(0).start()
        for p in range(n_pairs):
            to_near(p).start()
        for at in range(CHUNK, rows, TILE):
            low = norm(at, TILE)
            ko_s[at - CHUNK : at - CHUNK + TILE, :] = dot_nn(low, wk[...]).astype(BF)
            vo_s[at - CHUNK : at - CHUNK + TILE, :] = (dot_nn(low, wv[...]) + value_bias).astype(BF)
        to_far(0).wait_send()
        for p in range(1, n_pairs):
            to_far(p).start()
        for at in range(0, rows, TILE):
            scaled = (dot_nn(low_s[at : at + TILE, :], wq[...]) + query_bias) * 0.125
            q_s[at : at + TILE, :] = scaled.astype(BF)
            qe_s[at : at + TILE, :] = (scaled * LOG2E).astype(BF)
        to_far(0).wait_recv()
        relay(0).start()

    for p in range(n_pairs):
        @pl.when((pair == p) & (step == 0))
        def _():
            to_near(p).wait_recv()
            relay(p).wait_recv()

        if p + 1 < n_pairs:
            @pl.when((pair == p) & (step == 3))
            def _():
                to_far(p + 1).wait_recv()
                relay(p + 1).start()

    lanes = pl.ds(pl.multiple_of(pair * 128, 128), 128)
    low = low_half(TILE)
    q = qe_s[pl.ds(pl.multiple_of(step * TILE, TILE), TILE), lanes]
    row = lax.broadcasted_iota(jnp.int32, (TILE, 128), 0).astype(F32)
    group = device // GDEV
    start = starts[group]
    first_cont = member * (conts // CONT)
    own_gap = gaps[group, first_cont + jnp.maximum(step - PTILES, 0)]
    base_q = start + jnp.where(step < PTILES, member * CHUNK + step * TILE, PROMPT + own_gap)
    cells = settings(seg, rate, side * n_pairs + pair)
    at_q = base_q.astype(F32) + row
    qc = codes(at_q, cells, -2.0)
    classes = [lane_classes(h) for h in range(2)]
    first_at = start.astype(F32)

    @pl.when(step == 0)
    def _():
        for j in range(GDEV):
            first = first_at + (xor_bits(j, member) * CHUNK).astype(F32)
            for h, made in enumerate(key_side(kv_s[j, 0, :, lanes], first, cells, classes)):
                ka_s[h, j * CHUNK : (j + 1) * CHUNK, :] = made

    def logits(h, top, keys, first, causal, at, width):
        t = dot_nt(query_side(h, q, qc, first, cells, classes[h], low), keys)
        if causal is not None:
            t = jnp.where(causal, t, MASKED)
        t_s[h, :, pl.ds(at, width)] = t
        for g in range(width // 128):
            top = jnp.maximum(top, t[:, g * 128 : (g + 1) * 128])
        return top

    def weigh(h, carry, vals, m, at, width):
        total, acc = carry
        parts = []
        for g in range(width // 128):
            e = jnp.exp2(t_s[h, :, pl.ds(at + g * 128, 128)] - m)
            total = total + e
            parts.append(e.astype(BF))
        el = jnp.concatenate(parts, axis=1)
        e_ref[h, :, pl.ds(at, width)] = el
        return total, acc + dot_nn(el, vals)

    def finish_rows(carry):
        (sums0, acc0), (sums1, acc1) = carry
        sums, accs = (sums0, sums1), (acc0, acc1)
        li = [1.0 / jnp.sum(s, axis=1, keepdims=True) for s in sums]
        lfull = jnp.where(low, li[0], li[1])
        li_ref[...] = lfull
        o_s[pl.ds(pl.multiple_of(step * TILE, TILE), TILE), lanes] = (jnp.where(low, accs[0], accs[1]) * lfull).astype(BF)

    def tops(mx):
        return jnp.broadcast_to(jnp.max(mx, axis=1, keepdims=True), (TILE, 128))

    neg = jnp.full((TILE, 128), -jnp.inf, F32)
    zf = jnp.zeros((TILE, 128), F32)

    def held_keys(h, at):
        return ka_s[h, pl.ds(at, CHUNK), :]

    @pl.when(step < PTILES)
    def _():
        rows_id = lax.broadcasted_iota(jnp.int32, (TILE, CHUNK), 0) + step * TILE
        cols = lax.broadcasted_iota(jnp.int32, (TILE, CHUNK), 1)
        here = first_at + (member * CHUNK).astype(F32)

        def place(j):
            return pl.multiple_of(xor_bits(j, member) * CHUNK, CHUNK)

        def score(h, j, top):
            return logits(h, top, held_keys(h, place(j)), first_at + (j * CHUNK).astype(F32), None, place(j), CHUNK)

        def spread(h, j, m, carry):
            return weigh(h, carry, kv_s[xor_bits(j, member), 1, :, lanes], m, place(j), CHUNK)

        top = lax.fori_loop(0, member, lambda j, top: score(0, j, top), neg)
        m0 = tops(logits(0, top, held_keys(0, 0), here, cols <= rows_id, 0, CHUNK))

        def both(j, carry):
            return spread(0, j, m0, carry[0]), score(1, j, carry[1])

        first, top = lax.fori_loop(0, member, both, ((zf, zf), neg))
        first = weigh(0, first, kv_s[0, 1, :, lanes], m0, 0, CHUNK)
        m1 = tops(logits(1, top, held_keys(1, 0), here, cols <= rows_id, 0, CHUNK))
        finish_rows((first, lax.fori_loop(0, member + 1, lambda j, carry: spread(1, j, m1, carry), (zf, zf))))

    @pl.when(step >= PTILES)
    def _():
        own_rows = pl.ds(pl.multiple_of((step - PTILES) * TILE, TILE), TILE)
        rows_id = lax.broadcasted_iota(jnp.int32, (TILE, CONT), 0)
        cols = lax.broadcasted_iota(jnp.int32, (TILE, CONT), 1)
        own_at = base_q.astype(F32)
        own = key_side(ko_s[own_rows, lanes], own_at, cells, classes)

        def score(h, j, top):
            if j == GDEV:
                return logits(h, top, own[h], own_at, cols <= rows_id, PROMPT, CONT)
            first = first_at + (xor_bits(j, member) * CHUNK).astype(F32)
            return logits(h, top, held_keys(h, j * CHUNK), first, None, j * CHUNK, CHUNK)

        def spread(h, j, m, carry):
            if j == GDEV:
                return weigh(h, carry, vo_s[own_rows, lanes], m, PROMPT, CONT)
            return weigh(h, carry, kv_s[j, 1, :, lanes], m, j * CHUNK, CHUNK)

        top = neg
        for j in range(GDEV + 1):
            top = score(0, j, top)
        m0, top, first, second = tops(top), neg, (zf, zf), (zf, zf)
        for j in range(GDEV + 1):
            first = spread(0, j, m0, first)
            top = score(1, j, top)
        m1 = tops(top)
        for j in range(GDEV + 1):
            second = spread(1, j, m1, second)
        finish_rows((first, second))

    end = pl.num_programs(1) - 1
    for p in range(n_pairs):
        @pl.when((pair == p) & (step == 1 - side))
        def _():
            give(p, 0).start()

        for unit in range(6):
            @pl.when((pair == p) & (step == PTILES + unit // 2) & (side == 1 - unit // 3))
            def _():
                give(p, 1 + unit % 3).start()

    @pl.when((pair == last_pair - 1) & (step == 3))
    def _():
        for i in range(2):
            fetch_y[i].wait_recv()
            fetch_core[i].start()

    @pl.when((pair == last_pair) & (step == 3))
    def _():
        fetch_y[3].wait_recv()
        fetch_core[2].start()

    @pl.when((pair == last_pair) & (step == 0))
    def _():
        for copy in saves():
            copy.start()

    @pl.when((pair == last_pair) & (step == end))
    def _():
        for copy in keeps():
            copy.start()
        fetch_y[2].wait_recv()
        for copy in fetch_core:
            copy.wait_recv()
        for p in range(n_pairs):
            for piece in range(4):
                copy = give(p, piece)
                copy.wait_recv()
                copy.wait_send()
            if p > 0:
                to_far(p).wait_send()
            to_near(p).wait_send()
            relay(p).wait_send()
        for copy in fetch_y + fetch_core:
            copy.wait_send()
        for copy in keeps() + saves():
            copy.wait()


def attend(starts, gaps, seg, rate, hid, vec, wq, wk, wv, w1, wo, w2):
    rows = hid.shape[0]
    width = wq.shape[1]
    pairs = width // 128
    span = PROMPT + CONT
    conts = rows - CHUNK
    units = w1.shape[1]
    vmem = pl.BlockSpec(memory_space=pltpu.VMEM)
    hbm = pl.BlockSpec(memory_space=pl.ANY)
    shape = jax.ShapeDtypeStruct
    copies = 3 * pairs + 7 + 4 * pairs
    shared = 3 * units + 2 * width
    smem = pl.BlockSpec(memory_space=pltpu.SMEM)
    return pl.pallas_call(
        fwd_kernel,
        grid_spec=pltpu.PrefetchScalarGridSpec(
            num_scalar_prefetch=0,
            grid=(pairs, rows // TILE),
            in_specs=[smem] * 4 + [vmem] * 5 + [hbm] * 4,
            out_specs=[
                pl.BlockSpec((2, TILE, span), lambda a, t: (a, t, 0)),
                pl.BlockSpec((TILE, 128), lambda a, t: (t, a)),
            ]
            + [hbm] * 15,
            scratch_shapes=[
                pltpu.VMEM((2, TILE, span), F32),
                pltpu.VMEM((2, PROMPT, 128), BF),
                pltpu.VMEM((GDEV, 2, CHUNK, width), BF),
                pltpu.VMEM((rows, D), BF),
                pltpu.VMEM((rows, width), BF),
                pltpu.VMEM((rows, width), BF),
                pltpu.VMEM((conts, width), BF),
                pltpu.VMEM((conts, width), BF),
                pltpu.VMEM((rows, width), BF),
                pltpu.SemaphoreType.DMA((copies,)),
                pltpu.SemaphoreType.DMA((copies,)),
                pltpu.SemaphoreType.DMA((6 + 2 * GDEV,)),
            ],
        ),
        out_shape=[
            shape((2 * pairs, rows, span), BF),
            shape((rows, width), F32),
            shape((rows, width), BF),
            shape((conts, width), BF),
            shape((conts, width), BF),
            shape((PROMPT, width), BF),
            shape((PROMPT, width), BF),
            shape((rows, width), BF),
            shape((rows // 2, width), BF),
            shape((rows // 2, width), BF),
            shape((D, units // 2), BF),
            shape((D, units // 2), BF),
            shape((width // 2, D), BF),
            shape((width // 2, D), BF),
            shape((units // 4, D), BF),
            shape((units // 4, D), BF),
            shape((1, shared), F32),
        ],
        compiler_params=pltpu.CompilerParams(vmem_limit_bytes=56 << 20, collective_id=0, has_side_effects=True),
        cost_estimate=pl.CostEstimate(flops=20 * 10**9, bytes_accessed=60 * 10**6, transcendentals=0),
        name="attend",
    )(starts, gaps, seg, rate, hid, vec, wq, wk, wv, w1, wo, w2, vec)


EARLY = 2
FIRST_CUT = 1920


def reducer_scratch(count, block, cut):
    return [
        pltpu.VMEM((count, 2, 2, 2, block, cut), BF),
        pltpu.VMEM((count, 2, 2, 2, block, cut), BF),
        pltpu.VMEM((count, 2, 2, block, cut), BF),
        pltpu.VMEM((count, 2, 2, block, cut), BF),
        pltpu.VMEM((count, 2, block, cut), BF),
        pltpu.VMEM((count, 2, block, cut), BF),
        pltpu.VMEM((count, block, cut), BF),
        pltpu.SemaphoreType.DMA((4 * count,)),
        pltpu.SemaphoreType.DMA((4 * count,)),
        pltpu.SemaphoreType.DMA((count,)),
    ]


def reducer(packed, device, side, base, refs, done):
    held, got0, got1, held1, got2, held2, got3, sems_a, sems_b, sems_l = refs
    bit = [(device // (1 << b)) % 2 for b in range(4)]
    peers = [{"dp": bit_peer(device, b), "tensor": side} for b in range(4)]
    cut = held.shape[-1]

    def passing(c, stage, source, target, peer):
        return pltpu.make_async_remote_copy(
            src_ref=source,
            dst_ref=target,
            send_sem=sems_a.at[4 * c + stage],
            recv_sem=sems_b.at[4 * c + stage],
            device_id=peer,
            device_id_type=MESH,
        )

    count = held.shape[0]

    def columns_of(c, first):
        return pl.ds(first + (count - 1 - c) * cut, cut)

    def own_half(c):
        return pltpu.make_async_copy(packed.at[:, :, :, bit[0], :, columns_of(c, base)], held.at[c], sems_l.at[c])

    def stage0(c):
        return passing(c, 0, packed.at[:, :, :, 1 - bit[0], :, columns_of(c, base)], got0.at[c], peers[0])

    def stage1(c):
        if c % 2:
            return passing(c, 1, held.at[c, :, 1 - bit[2]], got1.at[c], peers[2])
        return passing(c, 1, held.at[c, :, :, 1 - bit[1]], got1.at[c], peers[1])

    def stage2(c):
        b = 1 if c % 2 else 2
        return passing(c, 2, held1.at[c, :, 1 - bit[b]], got2.at[c], peers[b])

    def stage3(c):
        return passing(c, 3, held2.at[c, 1 - bit[3]], got3.at[c], peers[3])

    def begin(c):
        own_half(c).start()
        stage0(c).start()

    def after0(c):
        own_half(c).wait()
        stage0(c).wait_recv()
        held[c] = held[c] + got0[c]
        stage1(c).start()

    def after1(c):
        stage1(c).wait_recv()
        kept = held[c, :, bit[2]] if c % 2 else held[c, :, :, bit[1]]
        held1[c] = kept + got1[c]
        stage2(c).start()

    def after2(c):
        stage2(c).wait_recv()
        held2[c] = held1[c, :, bit[1 if c % 2 else 2]] + got2[c]
        stage3(c).start()

    def after3(c):
        stage3(c).wait_recv()
        done[:, columns_of(c, 0)] = held2[c, bit[3]] + got3[c]

    def settle():
        for c in range(count):
            for copy in (stage0(c), stage1(c), stage2(c), stage3(c)):
                copy.wait_send()

    return begin, after0, after1, after2, after3, settle


def bwd_kernel(
    fused, q_ref, kp_ref, vp_ref, ko_ref, vo_ref, o_ref, li_ref, e_ref, g_mine, g_theirs, out_half, *refs
):
    packed = refs[0] if fused else None
    refs = refs[1:] if fused else refs
    dq_ref, dko_ref, dvo_ref, sum_k, sum_v, relay_out, out_got = refs[:7]
    done_out, other_out = refs[7:9] if fused else (None, None)
    refs = refs[9:] if fused else refs[7:]
    dk_s, dv_s, g_s, grad_s, near_s, relay_s, far_s, sems_a, sems_b, loc_sems = refs[:10]
    pair = pl.program_id(0)
    step = pl.program_id(1)
    device = lax.axis_index("dp")
    side = lax.axis_index("tensor")
    member = device % GDEV
    rows, width = g_s.shape
    n_pairs = width // 128
    conts = rows - CHUNK
    half_p, half_c = CHUNK // 2, conts // 2
    near = {"dp": bit_peer(device, 0), "tensor": side}
    far = {"dp": bit_peer(device, 1), "tensor": side}
    across = {"dp": device, "tensor": 1 - side}
    lanes = pl.ds(pl.multiple_of(pair * 128, 128), 128)
    mine_p = pl.ds(pl.multiple_of(side * half_p, 128), half_p)
    mine_c = pl.ds(pl.multiple_of(CHUNK + side * half_c, 128), half_c)

    def remote(i, src, dst, peer):
        return pltpu.make_async_remote_copy(
            src_ref=src, dst_ref=dst, send_sem=sems_a.at[i], recv_sem=sems_b.at[i], device_id=peer, device_id_type=MESH
        )

    def heads():
        return [
            remote(0, g_theirs.at[pl.ds(0, half_p), :], g_s.at[mine_p, :], across),
            remote(1, g_theirs.at[pl.ds(half_p, half_c), :], g_s.at[mine_c, :], across),
            remote(2, out_half, out_got, across),
        ]

    def local():
        return [
            pltpu.make_async_copy(g_mine.at[pl.ds(0, half_p), :], g_s.at[mine_p, :], loc_sems.at[0]),
            pltpu.make_async_copy(g_mine.at[pl.ds(half_p, half_c), :], g_s.at[mine_c, :], loc_sems.at[1]),
        ]

    def cores(p):
        part = pl.ds(p * 128, 128)
        return remote(3 + 2 * p, grad_s.at[:, :, 1, :, part], near_s.at[:, :, :, part], near)

    def chips(p):
        part = pl.ds(p * 128, 128)
        return remote(4 + 2 * p, relay_s.at[:, :, part], far_s.at[:, :, part], far)

    if fused:
        *early_refs, done_s, other_a, early_sems = refs[10:]
        begin, after0, after1, after2, after3, settle = reducer(
            packed, device, side, packed.shape[-1] - EARLY * FIRST_CUT, early_refs, done_s
        )
        half_e = packed.shape[-1] // 2
        tail_e = EARLY * FIRST_CUT - half_e
        peers = [{"dp": bit_peer(device, b), "tensor": side} for b in range(4)]
        swap = pltpu.make_async_remote_copy(
            src_ref=done_s.at[:, pl.ds(tail_e, half_e)],
            dst_ref=other_a,
            send_sem=early_sems.at[0],
            recv_sem=early_sems.at[1],
            device_id=across,
            device_id_type=MESH,
        )
        tick = pair * pl.num_programs(1) + step

    @pl.when((pair == 0) & (step == 0))
    def _():
        greet([near, far, across] + (peers[2:] if fused else []))
        for copy in heads() + local():
            copy.start()
        for copy in local():
            copy.wait()

    if fused:
        for c in range(EARLY):
            for at, act in ((0, begin), (1 + c, after0), (5 + c, after1), (8 + c, after2), (12, after3)):
                @pl.when(tick == at)
                def _():
                    act(c)

        @pl.when(tick == 12)
        def _():
            swap.start()

    @pl.when((pair == 0) & (step == 1 - side))
    def _():
        heads()[0].wait_recv()

    @pl.when((pair == 0) & (step == 3 - side))
    def _():
        heads()[1].wait_recv()

    low = low_half(TILE)
    g = g_s[pl.ds(pl.multiple_of(step * TILE, TILE), TILE), lanes].astype(F32) * li_ref[...]
    prod = g * o_ref[...].astype(F32)
    zf = jnp.zeros((TILE, 128), F32)
    deltas = [
        jnp.sum(jnp.where(low, prod, zf), axis=1, keepdims=True),
        jnp.sum(jnp.where(low, zf, prod), axis=1, keepdims=True),
    ]
    gs = [jnp.where(low, g, zf).astype(BF), jnp.where(low, zf, g).astype(BF)]
    gt = jnp.transpose(g).astype(BF)
    qt = jnp.transpose(q_ref[...].astype(F32)).astype(BF)

    def grads(dq, keys, vals, at, width):
        out, dks, dvs = [], [], []
        for h in range(2):
            e = e_ref[h, :, pl.ds(at, width)]
            dp = dot_nt(gs[h], vals)
            ds = (e.astype(F32) * (dp - deltas[h])).astype(BF)
            out.append(dq[h] + dot_nn(ds, keys))
            dks.append(dot_nn(qt[h * HD : (h + 1) * HD, :], ds))
            dvs.append(dot_nn(gt[h * HD : (h + 1) * HD, :], e))
        return tuple(out), dks, dvs

    @pl.when(step == 0)
    def _():
        dk_s[...] = jnp.zeros_like(dk_s)
        dv_s[...] = jnp.zeros_like(dv_s)

    def add(at, width, dks, dvs):
        for h in range(2):
            dk_s[h * HD : (h + 1) * HD, pl.ds(at, width)] += dks[h]
            dv_s[h * HD : (h + 1) * HD, pl.ds(at, width)] += dvs[h]

    def scaled(dq):
        return (jnp.where(low, dq[0], dq[1]).astype(BF).astype(F32) * 0.125).astype(BF)

    @pl.when(step < PTILES)
    def _():
        def one(j, dq):
            at = pl.multiple_of(xor_bits(j, member) * CHUNK, CHUNK)
            dq, dks, dvs = grads(dq, kp_ref[pl.ds(at, CHUNK), :], vp_ref[pl.ds(at, CHUNK), :], at, CHUNK)
            add(at, CHUNK, dks, dvs)
            return dq

        dq_ref[...] = scaled(lax.fori_loop(0, member + 1, one, (zf, zf)))
        dko_ref[...] = jnp.zeros_like(dko_ref)
        dvo_ref[...] = jnp.zeros_like(dvo_ref)

    @pl.when(step >= PTILES)
    def _():
        dq = (zf, zf)
        for j in range(GDEV):
            span = slice(j * CHUNK, (j + 1) * CHUNK)
            dq, dks, dvs = grads(dq, kp_ref[span, :], vp_ref[span, :], j * CHUNK, CHUNK)
            add(j * CHUNK, CHUNK, dks, dvs)
        dq, dks, dvs = grads(dq, ko_ref[...], vo_ref[...], PROMPT, CONT)
        dq_ref[...] = scaled(dq)
        dko_ref[...] = jnp.transpose(jnp.concatenate(dks, axis=0)).astype(BF)
        dvo_ref[...] = jnp.transpose(jnp.concatenate(dvs, axis=0)).astype(BF)

    end = pl.num_programs(1) - 1

    @pl.when(step == end)
    def _():
        for j in range(GDEV):
            span = slice(j * CHUNK, (j + 1) * CHUNK)
            grad_s[0, j // 2, j % 2, :, lanes] = jnp.transpose(dk_s[:, span]).astype(BF)
            grad_s[1, j // 2, j % 2, :, lanes] = jnp.transpose(dv_s[:, span]).astype(BF)

    for p in range(n_pairs):
        @pl.when((pair == p) & (step == end))
        def _():
            cores(p).start()

        if p + 1 < n_pairs:
            @pl.when((pair == p + 1) & (step == 2))
            def _():
                part = pl.ds(p * 128, 128)
                cores(p).wait_recv()
                relay_s[:, :, part] = (
                    grad_s[:, 1, 0, :, part].astype(F32) + near_s[:, 1, :, part].astype(F32)
                ).astype(BF)
                chips(p).start()

    @pl.when((pair == n_pairs - 1) & (step == end))
    def _():
        last = n_pairs - 1
        sums = (sum_k, sum_v)
        for p in range(last):
            part = pl.ds(p * 128, 128)
            chips(p).wait_recv()
            for i in range(2):
                sums[i][:, part] = (
                    grad_s[i, 0, 0, :, part].astype(F32) + near_s[i, 0, :, part].astype(F32) + far_s[i, :, part].astype(F32)
                ).astype(BF)
        part = pl.ds(last * 128, 128)
        cores(last).wait_recv()
        for i in range(2):
            relay_out[i] = (grad_s[i, 1, 0, :, part].astype(F32) + near_s[i, 1, :, part].astype(F32)).astype(BF)
            sums[i][:, part] = (grad_s[i, 0, 0, :, part].astype(F32) + near_s[i, 0, :, part].astype(F32)).astype(BF)
        if fused:
            swap.wait_recv()
            done_out[...] = done_s[:, pl.ds(0, tail_e)]
            other_out[...] = other_a[...]
            settle()
            swap.wait_send()
        heads()[2].wait_recv()
        for copy in heads():
            copy.wait_send()
        for p in range(n_pairs):
            cores(p).wait_send()
            if p < last:
                chips(p).wait_send()


def attend_back(q, k, v, kp, vp, o, li, e, g_mine, g_theirs, out_half, packed):
    rows, width = q.shape
    pairs = width // 128
    span = PROMPT + CONT
    tile = pl.BlockSpec((TILE, 128), lambda a, t: (t, a))
    whole = pl.BlockSpec((PROMPT, 128), lambda a, t: (0, a))
    own = pl.BlockSpec((TILE, 128), lambda a, t: (jnp.maximum(t - PTILES, 0), a))
    vmem = pl.BlockSpec(memory_space=pltpu.VMEM)
    hbm = pl.BlockSpec(memory_space=pl.ANY)
    shape = jax.ShapeDtypeStruct
    copies = 3 + 2 * pairs
    fused = packed is not None
    more_in, more_out, more_scratch = [], [], []
    if fused:
        block, half_e = packed.shape[-2], packed.shape[-1] // 2
        more_in = [packed]
        more_out = [shape((block, EARLY * FIRST_CUT - half_e), BF), shape((block, half_e), BF)]
        more_scratch = reducer_scratch(EARLY, block, FIRST_CUT) + [
            pltpu.VMEM((block, EARLY * FIRST_CUT), BF),
            pltpu.VMEM((block, half_e), BF),
            pltpu.SemaphoreType.DMA((2,)),
        ]
    return pl.pallas_call(
        functools.partial(bwd_kernel, fused),
        grid=(pairs, rows // TILE),
        in_specs=[tile, whole, whole, own, own, tile, tile, pl.BlockSpec((2, TILE, span), lambda a, t: (a, t, 0))]
        + [hbm] * (3 + len(more_in)),
        out_specs=[tile, tile, tile, vmem, vmem, vmem, hbm] + [vmem] * len(more_out),
        out_shape=[
            shape((rows, width), BF),
            shape((rows, width), BF),
            shape((rows, width), BF),
            shape((CHUNK, width), BF),
            shape((CHUNK, width), BF),
            shape((2, CHUNK, 128), BF),
            shape(out_half.shape, BF),
        ]
        + more_out,
        scratch_shapes=[
            pltpu.VMEM((128, PROMPT), F32),
            pltpu.VMEM((128, PROMPT), F32),
            pltpu.VMEM((rows, width), BF),
            pltpu.VMEM((2, 2, 2, CHUNK, width), BF),
            pltpu.VMEM((2, 2, CHUNK, width), BF),
            pltpu.VMEM((2, CHUNK, width), BF),
            pltpu.VMEM((2, CHUNK, width), BF),
            pltpu.SemaphoreType.DMA((copies,)),
            pltpu.SemaphoreType.DMA((copies,)),
            pltpu.SemaphoreType.DMA((2,)),
        ]
        + more_scratch,
        compiler_params=pltpu.CompilerParams(vmem_limit_bytes=60 << 20, collective_id=2, has_side_effects=True),
        cost_estimate=pl.CostEstimate(flops=30 * 10**9, bytes_accessed=60 * 10**6, transcendentals=0),
        name="attend_back",
    )(q, kp, vp, k, v, o, li, e, g_mine, g_theirs, out_half, *more_in)


UCH = 768


def polynomial(x, terms):
    out = jnp.full_like(x, terms[0])
    for term in terms[1:]:
        out = out * x + term
    return out


def gelu_pair(v):
    bell = jnp.exp(-0.5 * v * v)
    t = 1.0 / (1.0 + (0.3275911 * 0.7071067811865476) * jnp.abs(v))
    terms = (0.5307027145, -0.7265760135, 0.7107068705, -0.142248368, 0.127414796)
    half = polynomial(t, terms) * t * bell
    phi = jnp.where(v < 0.0, half, 1.0 - half)
    return v * phi, phi + v * (bell * 0.3989422804014327)


def column_sum(x):
    return jnp.sum(x, axis=0, keepdims=True)


def mid_kernel(
    att_m, att_o, vec_all, vec_got, hid_all, cot_all, w1_own, w1_got, w1_swap, wo_own, wo_got, wo_swap, w2_own, w2_got, w2_swap,
    out_ref, gatt_m, gatt_o, gmix_ref, packed, su_ref, sw_ref, sd_ref, ext_ref,
    vec_u, vec_w, w1, w2, wo, act_s, shp_s, dg_s, wide_s, acc_s, gmid_s, sub_s, mid_s, low_s, midt_s, cott_s, stage, hid, cot, sems, out_sems, send_sems, recv_sems,
):
    device = lax.axis_index("dp")
    side = lax.axis_index("tensor")
    core = device % 2
    near = {"dp": bit_peer(device, 0), "tensor": side}
    across = {"dp": device, "tensor": 1 - side}
    units = w1_own.shape[1]
    width = wo_own.shape[0]
    rows = hid.shape[0]
    full = 2 * units
    half = units // 2
    half_w = width // 2
    here_u = pl.multiple_of(units + core * half, 128)
    there_u = pl.multiple_of(units + (1 - core) * half, 128)
    here_w = pl.multiple_of(width + core * half_w, 64)
    there_w = pl.multiple_of(width + (1 - core) * half_w, 64)
    prompt, conts = CHUNK // 2, (hid_all.shape[0] - CHUNK) // 2
    own_p = pl.ds(pl.multiple_of(side * prompt, 128), prompt)
    own_c = pl.ds(pl.multiple_of(CHUNK + side * conts, 128), conts)
    at_own = 2 * D + 2 * width
    vec_own = vec_all.at[:, pl.ds(at_own, 3 * units + 2 * width)]
    vec_d = vec_all.at[:, pl.ds(at_own + 3 * units + 2 * width, 4 * D)]
    rows_in = []
    for i, (all_rows, held) in enumerate(((hid_all, hid), (cot_all, cot))):
        for j, (span, at, size) in enumerate(((own_p, 0, prompt), (own_c, prompt, conts))):
            copy = pltpu.make_async_copy(all_rows.at[span, :], held.at[pl.ds(at, size), :], sems.at[9 + 2 * i + j])
            copy.start()
            rows_in.append(copy)
    loads = []
    for i, (src, dst) in enumerate(
        [
            (wo_own, wo.at[pl.ds(0, width), :]),
            (wo_got, wo.at[pl.ds(here_w, half_w), :]),
            (wo_swap, wo.at[pl.ds(there_w, half_w), :]),
            (w1_own, w1.at[:, pl.ds(0, units)]),
            (w1_got, w1.at[:, pl.ds(here_u, half)]),
            (w1_swap, w1.at[:, pl.ds(there_u, half)]),
            (w2_own, w2.at[pl.ds(0, units), :]),
            (w2_got, w2.at[pl.ds(here_u, half // 2), :]),
            (w2_swap, w2.at[pl.ds(there_u, half // 2), :]),
        ]
    ):
        copy = pltpu.make_async_copy(src, dst, sems.at[i])
        copy.start()
        loads.append(copy)

    piece = half // 2
    greet([near, across])

    def remote(i, src, dst, peer):
        return pltpu.make_async_remote_copy(
            src_ref=src, dst_ref=dst, send_sem=send_sems.at[i], recv_sem=recv_sems.at[i], device_id=peer, device_id_type=MESH
        )

    from_own = pl.ds(pl.multiple_of(core * half + piece, 128), piece)
    landed = w2.at[pl.ds(pl.multiple_of(units + core * half + piece, 128), piece), :]
    over = remote(0, w2_own.at[from_own, :], landed, across)
    passed = remote(1, landed, landed, near)
    over.start()

    for i in range(3):
        for j, vec in enumerate((vec_own, vec_got)):
            vec_u[i : i + 1, pl.ds(j * units, units)] = vec[0:1, pl.ds(i * units, units)]
    for i in range(2):
        for j, vec in enumerate((vec_own, vec_got)):
            vec_w[i : i + 1, pl.ds(j * width, width)] = vec[0:1, pl.ds(3 * units + i * width, width)]

    a0 = att_m[...].astype(F32)
    a1 = att_o[...].astype(F32)
    center = (jnp.sum(a0, axis=1, keepdims=True) + jnp.sum(a1, axis=1, keepdims=True)) * (1.0 / D)
    square = (jnp.sum(a0 * a0, axis=1, keepdims=True) + jnp.sum(a1 * a1, axis=1, keepdims=True)) * (1.0 / D)
    sub_scale = lax.rsqrt(square - center * center + EPSILON)
    sub_s[:, 0:width] = (a0 - center) * sub_scale
    sub_s[:, width : 2 * width] = (a1 - center) * sub_scale
    sub_gain = vec_w[0:1, :]
    low_s[...] = (sub_s[...] * sub_gain + vec_w[1:2, :]).astype(BF)
    for copy in loads[0:3] + rows_in:
        copy.wait()
    mixed = hid[...].astype(F32) + (dot_nn(low_s[...], wo[...]) + vec_d[0:1, pl.ds(0, D)])
    wide_s[...] = mixed
    mean = jnp.mean(mixed, axis=1, keepdims=True)
    mid_scale = lax.rsqrt(jnp.mean(mixed * mixed, axis=1, keepdims=True) - mean * mean + EPSILON)
    mid_s[...] = (mixed - mean) * mid_scale
    mid_gain = vec_d[0:1, pl.ds(768, D)]
    mid_full = mid_s[...] * mid_gain + vec_d[0:1, pl.ds(1536, D)]
    mid_low = mid_full.astype(BF)
    midt_s[...] = jnp.transpose(mid_full).astype(BF)
    cot_full = cot[...].astype(F32)
    cott_s[...] = jnp.transpose(cot_full).astype(BF)
    sd_ref[...] = jnp.zeros_like(sd_ref)
    sd_ref[3:4, :] = column_sum(cot_full)
    for copy in loads[3:6]:
        copy.wait()

    def unrolled(low, high, step, carry):
        for c in range(low, high):
            carry = step(c, carry)
        return carry

    def lanes_sum(x):
        total = x[:, 0:128]
        for i in range(1, x.shape[1] // 128):
            total = total + x[:, i * 128 : (i + 1) * 128]
        return total

    zero = jnp.zeros((rows, 128), F32)
    act_sum, act_square = zero, zero

    def inner_of(c):
        at = c * UCH
        shp_s[:, at : at + UCH] = dot_nn(mid_low, w1[:, at : at + UCH]) + vec_u[2:3, at : at + UCH]

    inner_of(0)
    for c in range(full // UCH):
        at = c * UCH
        if c + 1 < full // UCH:
            inner_of(c + 1)
        act, slope = gelu_pair(shp_s[:, at : at + UCH])
        act_s[:, at : at + UCH] = act
        dg_s[:, at : at + UCH] = slope.astype(BF)
        act_sum, act_square = act_sum + lanes_sum(act), act_square + lanes_sum(act * act)
    ffn_center = jnp.sum(act_sum, axis=1, keepdims=True) * (1.0 / full)
    ffn_scale = lax.rsqrt(
        jnp.sum(act_square, axis=1, keepdims=True) * (1.0 / full) - ffn_center * ffn_center + EPSILON
    )
    for copy in loads[6:9]:
        copy.wait()
    over.wait_recv()
    passed.start()
    acc_s[...] = jnp.zeros_like(acc_s)
    per = units // UCH
    wide = 2 * units + width

    def column_of(c, extra):
        return pl.multiple_of((c // per) * wide + (c % per) * UCH + extra, 128)

    def send(slot, column):
        return pltpu.make_async_copy(stage.at[slot], packed.at[:, pl.ds(column, UCH)], out_sems.at[slot])

    def put(c, value, extra):
        slot = c % 2

        @pl.when(c >= 2)
        def _():
            send(slot, column_of(c - 2, extra)).wait()

        stage[slot] = value
        send(slot, column_of(c, extra)).start()

    def drain(extra):
        for c in range(full // UCH - 2, full // UCH):
            send(c % 2, column_of(c, extra)).wait()

    def second(c, carry):
        at = pl.multiple_of(c * UCH, UCH)
        unit = (act_s[:, pl.ds(at, UCH)] - ffn_center) * ffn_scale
        act_s[:, pl.ds(at, UCH)] = unit
        gain = vec_u[0:1, pl.ds(at, UCH)]
        low = (unit * gain + vec_u[1:2, pl.ds(at, UCH)]).astype(BF)
        acc_s[...] += dot_nn(low, w2[pl.ds(at, UCH), :])
        grad = dot_nt(cot[...], w2[pl.ds(at, UCH), :])
        cross = grad * unit
        su_ref[0:1, pl.ds(at, UCH)] = column_sum(cross)
        su_ref[1:2, pl.ds(at, UCH)] = column_sum(grad)
        shaped = grad * gain
        shp_s[:, pl.ds(at, UCH)] = shaped
        put(c, dot_nn(cott_s[...], low).astype(BF), units)
        return carry[0] + lanes_sum(shaped), carry[1] + lanes_sum(shaped * unit)

    su_ref[...] = jnp.zeros_like(su_ref)
    sums = unrolled(0, per, second, (zero, zero))
    passed.wait_recv()
    s_sum, s_cross = unrolled(per, 2 * per, second, sums)
    drain(units)
    shaped_mean = jnp.sum(s_sum, axis=1, keepdims=True) * (1.0 / full)
    cross_mean = jnp.sum(s_cross, axis=1, keepdims=True) * (1.0 / full)
    out_ref[...] = (wide_s[...] + (acc_s[...] + vec_d[0:1, pl.ds(2304, D)])).astype(BF)
    gmid_s[...] = jnp.zeros_like(gmid_s)

    def third(c, carry):
        at = pl.multiple_of(c * UCH, UCH)
        g = ffn_scale * (shp_s[:, pl.ds(at, UCH)] - shaped_mean - act_s[:, pl.ds(at, UCH)] * cross_mean)
        low = (g * dg_s[:, pl.ds(at, UCH)].astype(F32)).astype(BF)
        su_ref[2:3, pl.ds(at, UCH)] = column_sum(low.astype(F32))
        gmid_s[...] += dot_nt(low, w1[:, pl.ds(at, UCH)])
        put(c, dot_nn(midt_s[...], low).astype(BF), 0)
        return carry

    unrolled(0, 2 * per, third, 0)
    drain(0)

    grad_mid = gmid_s[...]
    unit = mid_s[...]
    sd_ref[1:2, :] = column_sum(grad_mid * unit)
    sd_ref[2:3, :] = column_sum(grad_mid)
    shaped = grad_mid * mid_gain
    grad_mixed = cot[...].astype(F32) + mid_scale * (
        shaped - jnp.mean(shaped, axis=1, keepdims=True) - unit * jnp.mean(shaped * unit, axis=1, keepdims=True)
    )
    branch = grad_mixed.astype(BF)
    gmix_ref[...] = branch
    branch_f = branch.astype(F32)
    sd_ref[0:1, :] = column_sum(branch_f)
    out_grad = dot_nn(jnp.transpose(branch_f).astype(BF), low_s[...]).astype(BF)
    stage[0, :, 0:width] = out_grad[:, 0:width]
    stage[1, :, 0:width] = out_grad[:, width : 2 * width]
    last = [
        pltpu.make_async_copy(stage.at[i, :, pl.ds(0, width)], packed.at[:, pl.ds(i * wide + 2 * units, width)], out_sems.at[i])
        for i in range(2)
    ]
    for copy in last:
        copy.start()
    grad_sub = dot_nt(branch, wo[...])
    unit = sub_s[...]
    cross = grad_sub * unit
    sw_ref[...] = jnp.zeros_like(sw_ref)
    sw_ref[0:1, :] = column_sum(cross)
    sw_ref[1:2, :] = column_sum(grad_sub)
    shaped = grad_sub * sub_gain
    grad_att = sub_scale * (
        shaped - jnp.mean(shaped, axis=1, keepdims=True) - unit * jnp.mean(shaped * unit, axis=1, keepdims=True)
    )
    gatt_m[...] = grad_att[:, 0:width].astype(BF)
    gatt_o[...] = grad_att[:, width : 2 * width].astype(BF)
    parts = ext_ref.shape[0]
    if parts > 1:
        sums_u, sums_w, sums_d = su_ref[...], sw_ref[...], sd_ref[...]
        for i in range(parts):
            ext_ref[i] = jnp.concatenate(
                [
                    window(sums_u, i * (units // parts)),
                    window(sums_u, units + i * (units // parts)),
                    window(sums_w, i * (width // parts)),
                    window(sums_w, width + i * (width // parts)),
                    window(sums_d, i * (D // parts)),
                    jnp.zeros((8, 128), F32),
                ],
                axis=0,
            ).astype(BF)
    for copy in last:
        copy.wait()
    over.wait_send()
    passed.wait_send()


def window(rows8, start):
    base = start // 128 * 128
    size = min(256, rows8.shape[1] - base)
    view = rows8[:, base : base + size]
    shift = start - base
    if shift:
        view = pltpu.roll(view, size - shift, 1)
    return view[:, 0:128]


def middle(att_m, att_o, hid, cot, vec_all, vec_got, w1, w2, wo, parts):
    rows = att_m.shape[0]
    units = w2[0].shape[0]
    width = wo[0].shape[0]
    vmem = pl.BlockSpec(memory_space=pltpu.VMEM)
    hbm = pl.BlockSpec(memory_space=pl.ANY)
    shape = jax.ShapeDtypeStruct
    return pl.pallas_call(
        mid_kernel,
        in_specs=[vmem] * 4 + [hbm] * 11,
        out_specs=[vmem] * 4 + [hbm] + [vmem] * 4,
        out_shape=[
            shape((rows, D), BF),
            shape((rows, width), BF),
            shape((rows, width), BF),
            shape((rows, D), BF),
            shape((D, 2 * (2 * units + width)), BF),
            shape((8, 2 * units), F32),
            shape((8, 2 * width), F32),
            shape((8, D), F32),
            shape((parts, 48, 128), BF),
        ],
        scratch_shapes=[
            pltpu.VMEM((8, 2 * units), F32),
            pltpu.VMEM((8, 2 * width), F32),
            pltpu.VMEM((D, 2 * units), BF),
            pltpu.VMEM((2 * units, D), BF),
            pltpu.VMEM((2 * width, D), BF),
            pltpu.VMEM((rows, 2 * units), F32),
            pltpu.VMEM((rows, 2 * units), F32),
            pltpu.VMEM((rows, 2 * units), BF),
            pltpu.VMEM((rows, D), F32),
            pltpu.VMEM((rows, D), F32),
            pltpu.VMEM((rows, D), F32),
            pltpu.VMEM((rows, 2 * width), F32),
            pltpu.VMEM((rows, D), F32),
            pltpu.VMEM((rows, 2 * width), BF),
            pltpu.VMEM((D, rows), BF),
            pltpu.VMEM((D, rows), BF),
            pltpu.VMEM((2, D, UCH), BF),
            pltpu.VMEM((rows, D), BF),
            pltpu.VMEM((rows, D), BF),
            pltpu.SemaphoreType.DMA((13,)),
            pltpu.SemaphoreType.DMA((2,)),
            pltpu.SemaphoreType.DMA((2,)),
            pltpu.SemaphoreType.DMA((2,)),
        ],
        compiler_params=pltpu.CompilerParams(vmem_limit_bytes=62 << 20, collective_id=3, has_side_effects=True),
        cost_estimate=pl.CostEstimate(flops=21 * 10**9, bytes_accessed=30 * 10**6, transcendentals=0),
        name="middle",
    )(att_m, att_o, vec_all, vec_got, hid, cot, *w1, *wo, *w2)


def final_kernel(
    bits, hid, vec_all, dq, dk, dv, wq, wk, wv, gmix, ext, sum_k, sum_v, relay, first_done, first_other, packed,
    gin, late_out, vec_out, early_out,
    loc_s, far_s, unit_s, mine_s, norm_s, send_c, recv_c, send_p, recv_p, give_c, give_p, late_s, small_s,
    vec_s, vec_r, done_s, sems_a, sems_b, loc_sems, *stage_refs,
):
    device = lax.axis_index("dp")
    side = lax.axis_index("tensor")
    across = {"dp": device, "tensor": 1 - side}
    peers = [{"dp": bit_peer(device, b), "tensor": side} for b in range(bits)]
    rows, width = dq.shape
    prompt = sum_k.shape[0]
    conts = rows - prompt
    half_p, half_c = prompt // 2, conts // 2
    own_p = pl.multiple_of(side * half_p, 128)
    their_p = pl.multiple_of((1 - side) * half_p, 128)
    own_c = pl.multiple_of(prompt + side * half_c, 128)
    their_c = pl.multiple_of(prompt + (1 - side) * half_c, 128)
    lanes = 3 * width + 128

    greet(peers + [across])
    count = [0]

    def remote(src, dst, peer):
        i = count[0]
        count[0] += 1
        copy = pltpu.make_async_remote_copy(
            src_ref=src, dst_ref=dst, send_sem=sems_a.at[i], recv_sem=sems_b.at[i], device_id=peer, device_id_type=MESH
        )
        copy.start()
        return copy

    share = remote(relay, far_s, peers[1])

    begin, after0, after1, after2, after3, settle = reducer(packed, device, side, 0, stage_refs[-10:], done_s)

    def each(act):
        for c in range(EARLY):
            act(c)

    each(begin)

    gain_f = vec_all[:, pl.ds(0, D)]
    bias_f = vec_all[:, pl.ds(D, D)]

    def unit_rows(at, size):
        x = hid[pl.ds(at, size), :].astype(F32)
        center = jnp.mean(x, axis=1, keepdims=True)
        scale = lax.rsqrt(jnp.mean(x * x, axis=1, keepdims=True) - center * center + EPSILON)
        return (x - center) * scale, scale

    def part_of(at, size, k_rows, v_rows):
        return dot_nt(dq[pl.ds(at, size), :], wq[...]) + dot_nt(k_rows, wk[...]) + dot_nt(v_rows, wv[...])

    def gather(part, unit):
        return column_sum(part * unit), column_sum(part)

    def normed_rows(at, size, unit):
        norm_s[:, pl.ds(at, size)] = jnp.transpose(unit * gain_f + bias_f).astype(BF)

    part = part_of(their_c, half_c, dk[pl.ds(their_c, half_c), :], dv[pl.ds(their_c, half_c), :])
    send_c[...] = part.astype(BF)
    y_cont = remote(send_c, recv_c, across)
    unit, _ = unit_rows(their_c, half_c)
    gain_grad, bias_grad = gather(part, unit)
    normed_rows(their_c, half_c, unit)
    unit, scale_c = unit_rows(own_c, half_c)
    part = part_of(own_c, half_c, dk[pl.ds(own_c, half_c), :], dv[pl.ds(own_c, half_c), :])
    mine_s[pl.ds(half_p, half_c), :] = part
    unit_s[pl.ds(half_p, half_c), :] = unit
    g, b = gather(part, unit)
    gain_grad, bias_grad = gain_grad + g, bias_grad + b
    normed_rows(own_c, half_c, unit)

    each(after0)
    share.wait_recv()
    for i, total in enumerate((sum_k, sum_v)):
        loc_s[i, :, pl.ds(0, width - 128)] = total[:, pl.ds(0, width - 128)]
        loc_s[i, :, pl.ds(width - 128, 128)] = (
            total[:, pl.ds(width - 128, 128)].astype(F32) + far_s[i].astype(F32)
        ).astype(BF)
    part = part_of(their_p, half_p, loc_s[0, pl.ds(their_p, half_p), :], loc_s[1, pl.ds(their_p, half_p), :])
    send_p[...] = part.astype(BF)
    y_prompt = remote(send_p, recv_p, across)
    unit, _ = unit_rows(their_p, half_p)
    normed_rows(their_p, half_p, unit)
    g, b = gather(part, unit)
    gain_grad, bias_grad = gain_grad + g, bias_grad + b
    unit, scale_p = unit_rows(own_p, half_p)
    unit_s[pl.ds(0, half_p), :] = unit
    normed_rows(own_p, half_p, unit)
    part = part_of(own_p, half_p, loc_s[0, pl.ds(own_p, half_p), :], loc_s[1, pl.ds(own_p, half_p), :])
    mine_s[pl.ds(0, half_p), :] = part
    g, b = gather(part, unit)
    gain_grad, bias_grad = gain_grad + g, bias_grad + b

    blocks = 1 << bits
    block = D // blocks

    def keep(value, lane):
        low = value.astype(BF)
        for i in range(blocks):
            late_s[i // 2, i % 2, :, pl.ds(lane, width)] = low[i * block : (i + 1) * block, :]

    keep(dot_nn(norm_s[...], dq[...]), 0)
    q_bias = column_sum(dq[...].astype(F32))
    for i, rest in enumerate((dk, dv)):
        keep(
            dot_nn(norm_s[:, pl.ds(0, prompt)], loc_s[i])
            + dot_nn(norm_s[:, pl.ds(prompt, conts)], rest[pl.ds(prompt, conts), :]),
            (i + 1) * width,
        )
    v_bias = column_sum(loc_s[1].astype(F32)) + column_sum(dv[pl.ds(prompt, conts), :].astype(F32))

    def norm_back(total, unit, scale, mixed):
        shaped = total * gain_f
        return mixed.astype(F32) + scale * (
            shaped - jnp.mean(shaped, axis=1, keepdims=True) - unit * jnp.mean(shaped * unit, axis=1, keepdims=True)
        )

    small_s[...] = jnp.zeros_like(small_s)
    small_s[0:1, pl.ds(0, width)] = q_bias
    small_s[1:2, pl.ds(0, width)] = v_bias
    small_s[2:3, pl.ds(0, D)] = gain_grad
    small_s[3:4, pl.ds(0, D)] = bias_grad
    small = small_s[...]
    row_id = lax.broadcasted_iota(jnp.int32, (8, 128), 0)
    for i in range(blocks):
        narrow = window(small, i * (width // blocks))
        broad = window(small, i * block)
        tail = jnp.concatenate([ext[i, pl.ds(32, 16), :].astype(F32)[0:8], jnp.where(row_id < 2, narrow, broad)], axis=0)
        late_s[i // 2, i % 2, pl.ds(0, 32), pl.ds(3 * width, 128)] = ext[i, pl.ds(0, 32), :]
        late_s[i // 2, i % 2, pl.ds(32, 16), pl.ds(3 * width, 128)] = tail.astype(BF)

    def input_rows(arrived, at, size, scale, held, rows_at, sem):
        arrived[0].wait_recv()
        here = pl.ds(at, size)
        total = mine_s[here, :] + arrived[1][...].astype(F32)
        held[...] = norm_back(total, unit_s[here, :], scale, gmix[here, :]).astype(BF)
        back = remote(held, gin.at[pl.ds(rows_at, size), :], across)
        kept = pltpu.make_async_copy(held, gin.at[pl.ds(rows_at, size), :], loc_sems.at[sem])
        kept.start()
        return back, kept

    source = late_s
    stages = []
    for bit in range(bits):
        landing, kept = stage_refs[2 * bit], stage_refs[2 * bit + 1]
        mine = (device // (1 << bit)) % 2
        copy = remote(source.at[:, 1 - mine], landing, peers[bit])
        if bit == 0:
            back_c, keep_c = input_rows((y_cont, recv_c), half_p, half_c, scale_c, give_c, own_c, 0)
        if bit == 1:
            each(after1)
            back_p, keep_p = input_rows((y_prompt, recv_p), 0, half_p, scale_p, give_p, own_p, 1)
        if bit == 2:
            each(after2)
        if bit == 3:
            each(after3)
        copy.wait_recv()
        stages.append(copy)
        for i in range(landing.shape[0]):
            kept[i // 2, i % 2] = (source[i, mine].astype(F32) + landing[i].astype(F32)).astype(BF)
        source = kept
    late_out[...] = source[0, 0, :, pl.ds(0, 3 * width)].astype(F32)
    vec_s[...] = source[0, 0, :, pl.ds(3 * width, 128)]
    swap = remote(vec_s, vec_r, across)
    last_e = done_s.shape[1]
    early_out[:, pl.ds(0, last_e)] = done_s[...].astype(F32) + first_other[:, pl.ds(0, last_e)].astype(F32)
    rest_e = first_done.shape[1]
    early_out[:, pl.ds(last_e, rest_e)] = first_done[...].astype(F32) + first_other[:, pl.ds(last_e, rest_e)].astype(F32)
    settle()
    swap.wait_recv()
    own_v, got_v = vec_s[...].astype(F32), vec_r[...].astype(F32)
    vec_out[0:8, :] = own_v[0:8] + got_v[8:16]
    vec_out[8:16, :] = own_v[16:24] + got_v[24:32]
    vec_out[16:24, :] = own_v[32:40] + got_v[32:40]
    vec_out[24:32, :] = own_v[40:48] + jnp.where(row_id < 2, 0.0, got_v[40:48])
    for copy in stages + [share, y_cont, y_prompt, swap]:
        copy.wait_send()
    for copy in (back_c, back_p):
        copy.wait_recv()
        copy.wait_send()
    keep_c.wait()
    keep_p.wait()


def finish(hid, vec_all, dq, dk, dv, wq, wk, wv, gmix, ext, sum_k, sum_v, relay, first_done, first_other, packed):
    rows, width = dq.shape
    ranks = lax.axis_size("dp")
    bits = ranks.bit_length() - 1
    block = D // ranks
    prompt = sum_k.shape[0]
    conts = rows - prompt
    lanes = 3 * width + 128
    vmem = pl.BlockSpec(memory_space=pltpu.VMEM)
    hbm = pl.BlockSpec(memory_space=pl.ANY)
    shape = jax.ShapeDtypeStruct
    copies = 6 + bits
    cut = (packed.shape[-1] - EARLY * FIRST_CUT) // EARLY
    stages = []
    for bit in range(bits):
        left = ranks >> (bit + 1)
        stages.append(pltpu.VMEM((left, block, lanes), BF))
        stages.append(pltpu.VMEM((max(left // 2, 1), min(left, 2), block, lanes), BF))
    return pl.pallas_call(
        functools.partial(final_kernel, bits),
        in_specs=[vmem] * 15 + [hbm],
        out_specs=[hbm, vmem, vmem, vmem],
        out_shape=[shape((rows, D), BF), shape((block, 3 * width), F32), shape((32, 128), F32), shape((block, packed.shape[-1] // 2), F32)],
        scratch_shapes=[
            pltpu.VMEM((2, prompt, width), BF),
            pltpu.VMEM((2, prompt, 128), BF),
            pltpu.VMEM((rows // 2, D), F32),
            pltpu.VMEM((rows // 2, D), F32),
            pltpu.VMEM((D, rows), BF),
            pltpu.VMEM((conts // 2, D), BF),
            pltpu.VMEM((conts // 2, D), BF),
            pltpu.VMEM((prompt // 2, D), BF),
            pltpu.VMEM((prompt // 2, D), BF),
            pltpu.VMEM((conts // 2, D), BF),
            pltpu.VMEM((prompt // 2, D), BF),
            pltpu.VMEM((ranks // 2, 2, block, lanes), BF),
            pltpu.VMEM((8, D + 128), F32),
            pltpu.VMEM((block, 128), BF),
            pltpu.VMEM((block, 128), BF),
            pltpu.VMEM((block, EARLY * cut), BF),
            pltpu.SemaphoreType.DMA((copies,)),
            pltpu.SemaphoreType.DMA((copies,)),
            pltpu.SemaphoreType.DMA((2,)),
        ]
        + stages
        + reducer_scratch(EARLY, block, cut),
        compiler_params=pltpu.CompilerParams(vmem_limit_bytes=56 << 20, collective_id=1, has_side_effects=True),
        cost_estimate=pl.CostEstimate(flops=5 * 10**9, bytes_accessed=20 * 10**6, transcendentals=0),
        name="finish",
    )(hid, vec_all, dq, dk, dv, wq, wk, wv, gmix, ext, sum_k, sum_v, relay, first_done, first_other, packed)


def flip(value, axis, bit):
    return lax.ppermute(value, axis, [(i, i ^ (1 << bit)) for i in range(lax.axis_size(axis))])


def contract_rows(left, right):
    return lax.dot_general(left, right, (((0,), (0,)), ((), ())), preferred_element_type=F32)


def back_project(left, right):
    return lax.dot_general(left, right, (((1,), (1,)), ((), ())), preferred_element_type=F32)


def norm_rows(values, gain, bias):
    center = jnp.mean(values, axis=-1, keepdims=True)
    spread = jnp.mean(values * values, axis=-1, keepdims=True) - center * center
    scaled = lax.rsqrt(spread + EPSILON)
    unit_rows = (values - center) * scaled
    return (unit_rows * gain + bias, unit_rows, scaled)


def norm_back(grad_rows, gain, unit_rows, scaled):
    shaped = grad_rows * gain
    return scaled * (
        shaped
        - jnp.mean(shaped, axis=-1, keepdims=True)
        - unit_rows * jnp.mean(shaped * unit_rows, axis=-1, keepdims=True)
    )


def in_order(which, mine, other, axis):
    return jnp.where(
        which == 0,
        jnp.concatenate([mine, other], axis=axis),
        jnp.concatenate([other, mine], axis=axis),
    )


def halving(value, device):
    bits = lax.axis_size("dp").bit_length() - 1
    rows, columns = value.shape
    current = value
    for bit in range(bits):
        upper = device // (1 << bit) % 2
        left = bits - bit
        view = current.reshape((1 << (left - 1), 2, -1, columns))
        kept = lax.dynamic_index_in_dim(view, upper, 1, keepdims=False)
        sent = lax.dynamic_index_in_dim(view, 1 - upper, 1, keepdims=False)
        got = flip(sent, "dp", bit)
        current = (kept.astype(F32) + got.astype(F32)).astype(BF)
    return current.reshape(rows >> bits, columns)


def side_by_side(parts):
    total = sum(part.shape[0] for part in parts)
    row, at = jnp.zeros((total,), F32), 0
    for part in parts:
        size = part.shape[0]
        row = row + jnp.pad(part.astype(F32), (at, total - at - size))
        at += size
    return row[None]


def half_of(value, which):
    prompt, conts = CHUNK // 2, (value.shape[0] - CHUNK) // 2
    return jnp.concatenate(
        [
            lax.dynamic_slice_in_dim(value, which * prompt, prompt),
            lax.dynamic_slice_in_dim(value, CHUNK + which * conts, conts),
        ]
    )


def joined(which, mine, other):
    prompt = CHUNK // 2
    low = jnp.where(which == 0, mine, other)
    high = jnp.where(which == 0, other, mine)
    return jnp.concatenate([low[:prompt], high[:prompt], low[prompt:], high[prompt:]])


def body(
    hidden_in,
    cotangent,
    prompt_start,
    cont_gap,
    seg_len,
    dilation_rate,
    pre_gain,
    pre_bias,
    query_weight,
    query_bias,
    key_weight,
    value_weight,
    value_bias,
    sub_gain,
    sub_bias,
    out_weight,
    out_bias,
    mid_gain,
    mid_bias,
    inner_weight,
    inner_bias,
    ffn_gain,
    ffn_bias,
    outer_weight,
    outer_bias,
):
    device = lax.axis_index("dp")
    ranks = lax.axis_size("dp")
    group_id = device // GDEV
    member = device % GDEV
    tensor_id = lax.axis_index("tensor")
    core = device % 2
    width = query_weight.shape[1]
    units = inner_weight.shape[1]
    pairs = width // 128
    rows = hidden_in.shape[0]
    prompt_rows = CHUNK
    cont_count = (rows - prompt_rows) // CONT

    vectors = side_by_side(
        [
            pre_gain,
            pre_bias,
            query_bias,
            value_bias,
            ffn_gain,
            ffn_bias,
            inner_bias,
            sub_gain,
            sub_bias,
            out_bias,
            mid_gain,
            mid_bias,
            outer_bias,
        ]
    )
    pre_gain_f = pre_gain.astype(F32)

    (
        weighed,
        inverse,
        queries,
        keys,
        values,
        prompt_keys,
        prompt_values,
        attended,
        att_mine,
        att_got,
        *pieces,
        vectors_other,
    ) = attend(
        prompt_start,
        cont_gap,
        seg_len.T,
        dilation_rate.T,
        hidden_in,
        vectors,
        query_weight,
        key_weight,
        value_weight,
        inner_weight,
        out_weight,
        outer_weight,
    )
    inner_parts = (inner_weight, pieces[0], pieces[1])
    out_parts = (out_weight, pieces[2], pieces[3])
    outer_parts = (outer_weight, pieces[4], pieces[5])

    fused = ranks == 16
    out_half, grad_mine, grad_theirs, grad_mixed_low, packed, sum_u, sum_w, sum_d, ext = middle(
        att_mine,
        att_got,
        hidden_in,
        cotangent,
        vectors,
        vectors_other,
        inner_parts,
        outer_parts,
        out_parts,
        ranks if fused else 1,
    )

    grad_query_in, own_key_grad, own_value_grad, key_sum, value_sum, relay, out_got, *early = attend_back(
        queries,
        keys,
        values,
        prompt_keys,
        prompt_values,
        attended,
        inverse,
        weighed,
        grad_mine,
        grad_theirs,
        out_half,
        packed.reshape(2, 2, 2, 2, D // ranks, -1) if fused else None,
    )
    if not fused:
        early = lax.psum_scatter(packed, "dp", scatter_dimension=0, tiled=True)
        early_mine, early_other = jnp.split(early, 2, axis=1)
        early_sum = early_mine.astype(F32) + flip(early_other, "tensor", 0).astype(F32)
    output = joined(tensor_id, out_half, out_got)
    block = D // ranks
    per_u, per_w, per_d = units // ranks, width // ranks, D // ranks
    if fused:
        input_low, late, vec, early_sum = finish(
            hidden_in,
            vectors,
            grad_query_in,
            own_key_grad,
            own_value_grad,
            query_weight,
            key_weight,
            value_weight,
            grad_mixed_low,
            ext,
            key_sum,
            value_sum,
            relay,
            *early,
            packed.reshape(2, 2, 2, 2, D // ranks, -1),
        )
        ffn_gain_grad, ffn_bias_grad, inner_bias_grad = [vec[i, :per_u] for i in range(3)]
        sub_gain_grad, sub_bias_grad = [vec[8 + i, :per_w] for i in range(2)]
        out_bias_grad, mid_gain_grad, mid_bias_grad, outer_bias_grad = [vec[16 + i, :per_d] for i in range(4)]
        query_bias_grad, value_bias_grad = [vec[24 + i, :per_w] for i in range(2)]
        pre_gain_grad, pre_bias_grad = [vec[26 + i, :per_d] for i in range(2)]
    else:
        pre_normed, pre_unit, pre_scale = norm_rows(hidden_in.astype(F32), pre_gain_f, pre_bias.astype(F32))
        pre_low = pre_normed.astype(BF)
        last = width - 128
        far = flip(relay, "dp", 1).astype(F32)
        summed = jnp.stack([key_sum, value_sum]).astype(F32)
        summed = jnp.concatenate([summed[:, :, :last], summed[:, :, last:] + far], axis=2).astype(BF)
        grad_keys = jnp.concatenate([summed[0], own_key_grad[prompt_rows:]], axis=0)
        grad_values = jnp.concatenate([summed[1], own_value_grad[prompt_rows:]], axis=0)

        query_weight_grad = contract_rows(pre_low, grad_query_in)
        key_weight_grad = contract_rows(pre_low, grad_keys)
        value_weight_grad = contract_rows(pre_low, grad_values)
        query_bias_grad = jnp.sum(grad_query_in.astype(F32), axis=0)
        value_bias_grad = jnp.sum(grad_values.astype(F32), axis=0)
        grad_normed_part = (
            back_project(grad_query_in, query_weight)
            + back_project(grad_keys, key_weight)
            + back_project(grad_values, value_weight)
        )
        grad_normed_low = grad_normed_part.astype(BF)
        grad_normed = grad_normed_low.astype(F32) + flip(grad_normed_low, "tensor", 0).astype(F32)
        pre_gain_grad = jnp.sum(grad_normed * pre_unit, axis=0)
        pre_bias_grad = jnp.sum(grad_normed, axis=0)
        grad_mixed_all = joined(tensor_id, grad_mixed_low, flip(grad_mixed_low, "tensor", 0)).astype(F32)
        input_low = (grad_mixed_all + norm_back(grad_normed, pre_gain_f, pre_unit, pre_scale)).astype(BF)

        vec = jnp.concatenate(
            [
                sum_u[:3].reshape(3, 2, ranks, per_u).transpose(2, 1, 0, 3).reshape(ranks, 6 * per_u),
                sum_w[:2].reshape(2, 2, ranks, per_w).transpose(2, 1, 0, 3).reshape(ranks, 4 * per_w),
                sum_d[:4].reshape(4, ranks, per_d).swapaxes(0, 1).reshape(ranks, 4 * per_d),
                jnp.stack([query_bias_grad, value_bias_grad]).reshape(2, ranks, per_w).swapaxes(0, 1).reshape(ranks, 2 * per_w),
                jnp.stack([pre_gain_grad, pre_bias_grad]).reshape(2, ranks, per_d).swapaxes(0, 1).reshape(ranks, 2 * per_d),
            ],
            axis=1,
        )
        count = vec.shape[1]
        vec = jnp.pad(vec, ((0, 0), (0, block * 128 - count))).reshape(D, 128)
        late = halving(
            jnp.concatenate(
                [p.astype(BF) for p in (query_weight_grad, key_weight_grad, value_weight_grad, vec)], axis=1
            ),
            device,
        )
        vec = late[:, 3 * width :].reshape(-1)[:count]
        late = late[:, : 3 * width].astype(F32)
        at_w = 6 * per_u
        at_d = at_w + 4 * per_w
        at_late = at_d + 4 * per_d
        got = flip(vec[:at_late], "tensor", 0).astype(F32)
        vec = vec.astype(F32)
        ffn_gain_grad, ffn_bias_grad, inner_bias_grad = (vec[: 3 * per_u] + got[3 * per_u : at_w]).reshape(3, per_u)
        sub_gain_grad, sub_bias_grad = (vec[at_w : at_w + 2 * per_w] + got[at_w + 2 * per_w : at_d]).reshape(2, per_w)
        out_bias_grad, mid_gain_grad, mid_bias_grad, outer_bias_grad = (vec[at_d:at_late] + got[at_d:]).reshape(4, per_d)
        query_bias_grad, value_bias_grad = vec[at_late : at_late + 2 * per_w].reshape(2, per_w)
        pre_gain_grad, pre_bias_grad = vec[at_late + 2 * per_w :].reshape(2, per_d)
    inner_weight_grad = early_sum[:, :units]
    outer_weight_grad = early_sum[:, units : 2 * units].T
    out_weight_grad = early_sum[:, 2 * units :].T
    return (
        output,
        input_low,
        pre_gain_grad,
        pre_bias_grad,
        late[:, :width],
        query_bias_grad,
        late[:, width : 2 * width],
        late[:, 2 * width : 3 * width],
        value_bias_grad,
        sub_gain_grad,
        sub_bias_grad,
        out_weight_grad,
        out_bias_grad,
        mid_gain_grad,
        mid_bias_grad,
        inner_weight_grad,
        inner_bias_grad,
        ffn_gain_grad,
        ffn_bias_grad,
        outer_weight_grad,
        outer_bias_grad,
    )

def solution(mesh):
    placed = (
        P("dp", None),
        P("dp", None),
        P(),
        P(),
        P(),
        P(),
        P(),
        P(),
        P(None, "tensor"),
        P("tensor"),
        P(None, "tensor"),
        P(None, "tensor"),
        P("tensor"),
        P("tensor"),
        P("tensor"),
        P("tensor", None),
        P(),
        P(),
        P(),
        P(None, "tensor"),
        P("tensor"),
        P("tensor"),
        P("tensor"),
        P("tensor", None),
        P(),
    )
    return jax.shard_map(
        body,
        mesh=mesh,
        in_specs=placed,
        out_specs=(
            P("dp", None),
            P("dp", None),
            P("dp"),
            P("dp"),
            P("dp", "tensor"),
            P(("tensor", "dp")),
            P("dp", "tensor"),
            P("dp", "tensor"),
            P(("tensor", "dp")),
            P(("tensor", "dp")),
            P(("tensor", "dp")),
            P("tensor", "dp"),
            P("dp"),
            P("dp"),
            P("dp"),
            P("dp", "tensor"),
            P(("tensor", "dp")),
            P(("tensor", "dp")),
            P(("tensor", "dp")),
            P("tensor", "dp"),
            P("dp"),
        ),
        check_vma=False,
    )
```

```python
import functools

import jax
import jax.numpy as jnp
from jax import lax
from jax.experimental import pallas as pl
from jax.experimental.pallas import tpu as pltpu
from jax.sharding import PartitionSpec as P

HD = 64
PROMPT = 2048
CONT = 256
GDEV = 4
TILE = 256
CHUNK = PROMPT // GDEV
PTILES = CHUNK // TILE
LOG2E = 1.4426950408889634
BF = jnp.bfloat16
F32 = jnp.float32
D = 768
EPSILON = 1e-05
MESH = pl.DeviceIdType.MESH


def dot_nt(a, b):
    return lax.dot_general(a, b, (((1,), (1,)), ((), ())), preferred_element_type=F32)


def dot_nn(a, b):
    return lax.dot_general(a, b, (((1,), (0,)), ((), ())), preferred_element_type=F32)


def low_half(rows):
    return lax.broadcasted_iota(jnp.int32, (rows, 128), 1) < HD


MASKED = -1e30
CLASSES = 36


def lane_classes(head):
    lane = lax.broadcasted_iota(jnp.int32, (8, 128), 1) - (HD if head == 0 else 0)
    number = lane.astype(F32)
    main = lane < CLASSES
    number = jnp.where(main, number, 4.0 * (number - CLASSES) + 3.0)
    number = jnp.where((lane >= 0) & (lane < CLASSES + CLASSES // 4), number, -5.0)
    combo = jnp.floor((number + 0.5) * 0.25)
    step0 = jnp.floor((combo + 0.5) * (1.0 / 3.0))
    step1 = combo - 3.0 * step0
    rest = number - 4.0 * combo
    flag1 = jnp.where(rest > 1.5, 1.0, 0.0)
    return number, step0, step1, flag1, rest - 2.0 * flag1, jnp.where(main, 0.0, 1.0)


def key_side(keys, first, cells, classes):
    size = keys.shape[0]
    at = first + lax.broadcasted_iota(jnp.int32, (8, size), 1).astype(F32)
    base = jnp.full((8, size), 0.0, F32) + first
    row = lax.broadcasted_iota(jnp.int32, (8, size), 0)

    def cell(i):
        return cells[i][:, 0:1]

    step0 = jnp.floor((at + 0.5) * cell(0)) - jnp.floor((base + 0.5) * cell(0))
    step1 = jnp.floor((at + 0.5) * cell(1)) - jnp.floor((base + 0.5) * cell(1))
    rest1 = at - cell(2) * jnp.floor((at + 0.5) * cell(3))
    rest2 = at - cell(4) * jnp.floor((at + 0.5) * cell(5))
    flag1 = jnp.where(rest1 == jnp.where(row == 0, cell(6), cell(7)), 2.0, 0.0)
    flag2 = jnp.where(rest2 == jnp.where(row == 0, cell(8), cell(9)), 1.0, 0.0)
    columns = jnp.transpose(4.0 * (3.0 * step0 + step1) + flag1 + flag2)
    low = low_half(size)
    hot = [jnp.where(columns[:, h : h + 1] == classes[h][0][0:1], 1.0, 0.0).astype(BF) for h in range(2)]
    return [jnp.where(low, keys, hot[0]), jnp.where(low, hot[1], keys)]


def query_side(head, queries, qc, first, cells, lanes, low):
    _, step0, step1, flag1, flag2, small = lanes
    base = jnp.zeros((8, 128), F32) + first
    kc0 = (jnp.floor((base + 0.5) * cells[0]) + step0)[0:1]
    kc1 = jnp.where(flag1 > 0.5, jnp.floor((base + 0.5) * cells[1]) + step1, -1.0)[0:1]
    weight = jnp.where(qc[0] == kc0, 1.0, 0.0) + jnp.where(qc[1 + head] == kc1, 1.0, 0.0)
    weight = weight + qc[3 + head] * flag2[0:1]
    logs = jnp.maximum(jnp.log2(weight), MASKED)
    logs = jnp.where(small[0:1] > 0.5, logs - logs.astype(BF).astype(F32), logs).astype(BF)
    return jnp.where(low, queries, logs) if head == 0 else jnp.where(low, logs, queries)


def settings(seg, rate, pair):
    def row(value):
        return jnp.full((1, 128), value, jnp.int32).astype(F32)

    def rest(number, period):
        return number - period * jnp.floor((number + 0.5) / period)

    second, third = row(rate[1, pair]), row(rate[2, pair])
    head = row(2 * pair)
    return (
        1.0 / row(seg[0, pair]),
        1.0 / row(seg[1, pair]),
        second,
        1.0 / second,
        third,
        1.0 / third,
        rest(head, second),
        rest(head + 1.0, second),
        rest(head, third),
        rest(head + 1.0, third),
    )


def codes(at, cells, miss):
    first = jnp.floor((at + 0.5) * cells[0])
    second = jnp.floor((at + 0.5) * cells[1])
    rest1 = at - cells[2] * jnp.floor((at + 0.5) * cells[3])
    rest2 = at - cells[4] * jnp.floor((at + 0.5) * cells[5])
    return [
        first,
        jnp.where(rest1 == cells[6], second, miss),
        jnp.where(rest1 == cells[7], second, miss),
        jnp.where(rest2 == cells[8], 1.0, 0.0),
        jnp.where(rest2 == cells[9], 1.0, 0.0),
    ]


def bit_peer(device, bit):
    step = 1 << bit
    return device + (1 - 2 * ((device // step) % 2)) * step


def greet(peers):
    barrier = pltpu.get_barrier_semaphore()
    for peer in peers:
        pl.semaphore_signal(barrier, inc=1, device_id=peer, device_id_type=MESH)
    pl.semaphore_wait(barrier, len(peers))


def xor_bits(a, b):
    return (a % 2 + b % 2) % 2 + 2 * ((a // 2 + b // 2) % 2)


def fwd_kernel(
    starts, gaps, seg, rate, hid, vec, wq, wk, wv, w1, wo, w2, vec_hbm,
    e_ref, li_ref, q_out, k_out, v_out, kp_out, vp_out, o_out, mine_out, got_out,
    w1_got, w1_swap, wo_got, wo_swap, w2_got, w2_swap, vec_got,
    t_s, ka_s, kv_s, low_s, q_s, qe_s, ko_s, vo_s, o_s, sems_a, sems_b, loc_sems,
):
    pair = pl.program_id(0)
    step = pl.program_id(1)
    pairs = pl.num_programs(0)
    device = lax.axis_index("dp")
    side = lax.axis_index("tensor")
    member = device % GDEV
    core = device % 2
    rows, width = q_s.shape
    n_pairs = width // 128
    last_pair = n_pairs - 1
    conts = rows - CHUNK
    near = {"dp": bit_peer(device, 0), "tensor": side}
    far = {"dp": bit_peer(device, 1), "tensor": side}
    across = {"dp": device, "tensor": 1 - side}
    half_u = w1.shape[1] // 2
    half_w = wo.shape[0] // 2
    half_p, half_c = CHUNK // 2, conts // 2
    sent_u = pl.multiple_of(core * half_u, 128)
    shared_at = 2 * D + 2 * width
    sent_w = pl.multiple_of(core * half_w, 64)

    def remote(i, src, dst, peer):
        return pltpu.make_async_remote_copy(
            src_ref=src, dst_ref=dst, send_sem=sems_a.at[i], recv_sem=sems_b.at[i], device_id=peer, device_id_type=MESH
        )

    def to_far(p):
        lanes = pl.ds(p * 128, 128)
        return remote(3 * p, kv_s.at[0, :, :, lanes], kv_s.at[2, :, :, lanes], far)

    def to_near(p):
        lanes = pl.ds(p * 128, 128)
        return remote(3 * p + 1, kv_s.at[0, :, :, lanes], kv_s.at[1, :, :, lanes], near)

    def relay(p):
        lanes = pl.ds(p * 128, 128)
        return remote(3 * p + 2, kv_s.at[2, :, :, lanes], kv_s.at[3, :, :, lanes], near)

    base = 3 * n_pairs
    fetch_y = [
        remote(base, wo.at[pl.ds(sent_w, half_w), :], wo_got, across),
        remote(base + 1, w1.at[:, pl.ds(sent_u, half_u)], w1_got, across),
        remote(base + 2, vec_hbm.at[:, pl.ds(shared_at, vec_got.shape[1])], vec_got, across),
        remote(base + 3, w2.at[pl.ds(sent_u, half_u // 2), :], w2_got, across),
    ]
    fetch_core = [
        remote(base + 4, wo_got, wo_swap, near),
        remote(base + 5, w1_got, w1_swap, near),
        remote(base + 6, w2_got, w2_swap, near),
    ]

    def give(p, piece):
        lanes = pl.ds(p * 128, 128)
        their_p = pl.multiple_of((1 - side) * half_p, 128)
        their_c = pl.multiple_of(CHUNK + (1 - side) * half_c, 128)
        third = half_c // 3
        if piece == 0:
            source, target = pl.ds(their_p, half_p), pl.ds(0, half_p)
        else:
            source = pl.ds(pl.multiple_of(their_c + (piece - 1) * third, 128), third)
            target = pl.ds(half_p + (piece - 1) * third, third)
        return remote(base + 7 + 4 * p + piece, o_s.at[source, lanes], got_out.at[target, lanes], across)

    def keeps():
        own_p = pl.multiple_of(side * half_p, 128)
        own_c = pl.multiple_of(CHUNK + side * half_c, 128)
        return [
            pltpu.make_async_copy(o_s, o_out, loc_sems.at[0]),
            pltpu.make_async_copy(o_s.at[pl.ds(own_p, half_p), :], mine_out.at[pl.ds(0, half_p), :], loc_sems.at[1]),
            pltpu.make_async_copy(o_s.at[pl.ds(own_c, half_c), :], mine_out.at[pl.ds(half_p, half_c), :], loc_sems.at[2]),
        ]

    def saves():
        out = [
            pltpu.make_async_copy(q_s, q_out, loc_sems.at[3]),
            pltpu.make_async_copy(ko_s, k_out, loc_sems.at[0]),
            pltpu.make_async_copy(vo_s, v_out, loc_sems.at[5]),
        ]
        for r in range(GDEV):
            span = pl.ds(r * CHUNK, CHUNK)
            out.append(pltpu.make_async_copy(kv_s.at[r, 0], kp_out.at[span, :], loc_sems.at[6 + 2 * r]))
            out.append(pltpu.make_async_copy(kv_s.at[r, 1], vp_out.at[span, :], loc_sems.at[7 + 2 * r]))
        return out

    @pl.when((pair == 0) & (step == 0))
    def _():
        greet([near, far, across])
        for copy in fetch_y:
            copy.start()
        gain_f, bias_f = vec[:, pl.ds(0, D)], vec[:, pl.ds(D, D)]
        query_bias = vec[:, pl.ds(2 * D, width)]
        value_bias = vec[:, pl.ds(2 * D + width, width)]

        def norm(at, size):
            x = hid[at : at + size, :].astype(F32)
            center = jnp.mean(x, axis=1, keepdims=True)
            scale = lax.rsqrt(jnp.mean(x * x, axis=1, keepdims=True) - center * center + EPSILON)
            low = ((x - center) * scale * gain_f + bias_f).astype(BF)
            low_s[at : at + size, :] = low
            return low

        low = norm(0, CHUNK)
        kv_s[0, 0] = dot_nn(low, wk[...]).astype(BF)
        kv_s[0, 1] = (dot_nn(low, wv[...]) + value_bias).astype(BF)
        to_far(0).start()
        for p in range(n_pairs):
            to_near(p).start()
        for at in range(CHUNK, rows, TILE):
            low = norm(at, TILE)
            ko_s[at - CHUNK : at - CHUNK + TILE, :] = dot_nn(low, wk[...]).astype(BF)
            vo_s[at - CHUNK : at - CHUNK + TILE, :] = (dot_nn(low, wv[...]) + value_bias).astype(BF)
        to_far(0).wait_send()
        for p in range(1, n_pairs):
            to_far(p).start()
        for at in range(0, rows, TILE):
            scaled = (dot_nn(low_s[at : at + TILE, :], wq[...]) + query_bias) * 0.125
            q_s[at : at + TILE, :] = scaled.astype(BF)
            qe_s[at : at + TILE, :] = (scaled * LOG2E).astype(BF)
        to_far(0).wait_recv()
        relay(0).start()

    for p in range(n_pairs):
        @pl.when((pair == p) & (step == 0))
        def _():
            to_near(p).wait_recv()
            relay(p).wait_recv()

        if p + 1 < n_pairs:
            @pl.when((pair == p) & (step == 3))
            def _():
                to_far(p + 1).wait_recv()
                relay(p + 1).start()

    lanes = pl.ds(pl.multiple_of(pair * 128, 128), 128)
    low = low_half(TILE)
    q = qe_s[pl.ds(pl.multiple_of(step * TILE, TILE), TILE), lanes]
    row = lax.broadcasted_iota(jnp.int32, (TILE, 128), 0).astype(F32)
    group = device // GDEV
    start = starts[group]
    first_cont = member * (conts // CONT)
    own_gap = gaps[group, first_cont + jnp.maximum(step - PTILES, 0)]
    base_q = start + jnp.where(step < PTILES, member * CHUNK + step * TILE, PROMPT + own_gap)
    cells = settings(seg, rate, side * n_pairs + pair)
    at_q = base_q.astype(F32) + row
    qc = codes(at_q, cells, -2.0)
    classes = [lane_classes(h) for h in range(2)]
    first_at = start.astype(F32)

    @pl.when(step == 0)
    def _():
        for j in range(GDEV):
            first = first_at + (xor_bits(j, member) * CHUNK).astype(F32)
            for h, made in enumerate(key_side(kv_s[j, 0, :, lanes], first, cells, classes)):
                ka_s[h, j * CHUNK : (j + 1) * CHUNK, :] = made

    def logits(h, top, keys, first, causal, at, width):
        t = dot_nt(query_side(h, q, qc, first, cells, classes[h], low), keys)
        if causal is not None:
            t = jnp.where(causal, t, MASKED)
        t_s[h, :, pl.ds(at, width)] = t
        for g in range(width // 128):
            top = jnp.maximum(top, t[:, g * 128 : (g + 1) * 128])
        return top

    def weigh(h, carry, vals, m, at, width):
        total, acc = carry
        parts = []
        for g in range(width // 128):
            e = jnp.exp2(t_s[h, :, pl.ds(at + g * 128, 128)] - m)
            total = total + e
            parts.append(e.astype(BF))
        el = jnp.concatenate(parts, axis=1)
        e_ref[h, :, pl.ds(at, width)] = el
        return total, acc + dot_nn(el, vals)

    def finish_rows(carry):
        (sums0, acc0), (sums1, acc1) = carry
        sums, accs = (sums0, sums1), (acc0, acc1)
        li = [1.0 / jnp.sum(s, axis=1, keepdims=True) for s in sums]
        lfull = jnp.where(low, li[0], li[1])
        li_ref[...] = lfull
        o_s[pl.ds(pl.multiple_of(step * TILE, TILE), TILE), lanes] = (jnp.where(low, accs[0], accs[1]) * lfull).astype(BF)

    def tops(mx):
        return jnp.broadcast_to(jnp.max(mx, axis=1, keepdims=True), (TILE, 128))

    neg = jnp.full((TILE, 128), -jnp.inf, F32)
    zf = jnp.zeros((TILE, 128), F32)

    def held_keys(h, at):
        return ka_s[h, pl.ds(at, CHUNK), :]

    @pl.when(step < PTILES)
    def _():
        rows_id = lax.broadcasted_iota(jnp.int32, (TILE, CHUNK), 0) + step * TILE
        cols = lax.broadcasted_iota(jnp.int32, (TILE, CHUNK), 1)
        here = first_at + (member * CHUNK).astype(F32)

        def place(j):
            return pl.multiple_of(xor_bits(j, member) * CHUNK, CHUNK)

        def score(h, j, top):
            return logits(h, top, held_keys(h, place(j)), first_at + (j * CHUNK).astype(F32), None, place(j), CHUNK)

        def spread(h, j, m, carry):
            return weigh(h, carry, kv_s[xor_bits(j, member), 1, :, lanes], m, place(j), CHUNK)

        top = lax.fori_loop(0, member, lambda j, top: score(0, j, top), neg)
        m0 = tops(logits(0, top, held_keys(0, 0), here, cols <= rows_id, 0, CHUNK))

        def both(j, carry):
            return spread(0, j, m0, carry[0]), score(1, j, carry[1])

        first, top = lax.fori_loop(0, member, both, ((zf, zf), neg))
        first = weigh(0, first, kv_s[0, 1, :, lanes], m0, 0, CHUNK)
        m1 = tops(logits(1, top, held_keys(1, 0), here, cols <= rows_id, 0, CHUNK))
        finish_rows((first, lax.fori_loop(0, member + 1, lambda j, carry: spread(1, j, m1, carry), (zf, zf))))

    @pl.when(step >= PTILES)
    def _():
        own_rows = pl.ds(pl.multiple_of((step - PTILES) * TILE, TILE), TILE)
        rows_id = lax.broadcasted_iota(jnp.int32, (TILE, CONT), 0)
        cols = lax.broadcasted_iota(jnp.int32, (TILE, CONT), 1)
        own_at = base_q.astype(F32)
        own = key_side(ko_s[own_rows, lanes], own_at, cells, classes)

        def score(h, j, top):
            if j == GDEV:
                return logits(h, top, own[h], own_at, cols <= rows_id, PROMPT, CONT)
            first = first_at + (xor_bits(j, member) * CHUNK).astype(F32)
            return logits(h, top, held_keys(h, j * CHUNK), first, None, j * CHUNK, CHUNK)

        def spread(h, j, m, carry):
            if j == GDEV:
                return weigh(h, carry, vo_s[own_rows, lanes], m, PROMPT, CONT)
            return weigh(h, carry, kv_s[j, 1, :, lanes], m, j * CHUNK, CHUNK)

        top = neg
        for j in range(GDEV + 1):
            top = score(0, j, top)
        m0, top, first, second = tops(top), neg, (zf, zf), (zf, zf)
        for j in range(GDEV + 1):
            first = spread(0, j, m0, first)
            top = score(1, j, top)
        m1 = tops(top)
        for j in range(GDEV + 1):
            second = spread(1, j, m1, second)
        finish_rows((first, second))

    end = pl.num_programs(1) - 1
    for p in range(n_pairs):
        @pl.when((pair == p) & (step == 1 - side))
        def _():
            give(p, 0).start()

        for unit in range(6):
            @pl.when((pair == p) & (step == PTILES + unit // 2) & (side == 1 - unit // 3))
            def _():
                give(p, 1 + unit % 3).start()

    @pl.when((pair == last_pair - 1) & (step == 3))
    def _():
        for i in range(2):
            fetch_y[i].wait_recv()
            fetch_core[i].start()

    @pl.when((pair == last_pair) & (step == 3))
    def _():
        fetch_y[3].wait_recv()
        fetch_core[2].start()

    @pl.when((pair == last_pair) & (step == 0))
    def _():
        for copy in saves():
            copy.start()

    @pl.when((pair == last_pair) & (step == end))
    def _():
        for copy in keeps():
            copy.start()
        fetch_y[2].wait_recv()
        for copy in fetch_core:
            copy.wait_recv()
        for p in range(n_pairs):
            for piece in range(4):
                copy = give(p, piece)
                copy.wait_recv()
                copy.wait_send()
            if p > 0:
                to_far(p).wait_send()
            to_near(p).wait_send()
            relay(p).wait_send()
        for copy in fetch_y + fetch_core:
            copy.wait_send()
        for copy in keeps() + saves():
            copy.wait()


def attend(starts, gaps, seg, rate, hid, vec, wq, wk, wv, w1, wo, w2):
    rows = hid.shape[0]
    width = wq.shape[1]
    pairs = width // 128
    span = PROMPT + CONT
    conts = rows - CHUNK
    units = w1.shape[1]
    vmem = pl.BlockSpec(memory_space=pltpu.VMEM)
    hbm = pl.BlockSpec(memory_space=pl.ANY)
    shape = jax.ShapeDtypeStruct
    copies = 3 * pairs + 7 + 4 * pairs
    shared = 3 * units + 2 * width
    smem = pl.BlockSpec(memory_space=pltpu.SMEM)
    return pl.pallas_call(
        fwd_kernel,
        grid_spec=pltpu.PrefetchScalarGridSpec(
            num_scalar_prefetch=0,
            grid=(pairs, rows // TILE),
            in_specs=[smem] * 4 + [vmem] * 5 + [hbm] * 4,
            out_specs=[
                pl.BlockSpec((2, TILE, span), lambda a, t: (a, t, 0)),
                pl.BlockSpec((TILE, 128), lambda a, t: (t, a)),
            ]
            + [hbm] * 15,
            scratch_shapes=[
                pltpu.VMEM((2, TILE, span), F32),
                pltpu.VMEM((2, PROMPT, 128), BF),
                pltpu.VMEM((GDEV, 2, CHUNK, width), BF),
                pltpu.VMEM((rows, D), BF),
                pltpu.VMEM((rows, width), BF),
                pltpu.VMEM((rows, width), BF),
                pltpu.VMEM((conts, width), BF),
                pltpu.VMEM((conts, width), BF),
                pltpu.VMEM((rows, width), BF),
                pltpu.SemaphoreType.DMA((copies,)),
                pltpu.SemaphoreType.DMA((copies,)),
                pltpu.SemaphoreType.DMA((6 + 2 * GDEV,)),
            ],
        ),
        out_shape=[
            shape((2 * pairs, rows, span), BF),
            shape((rows, width), F32),
            shape((rows, width), BF),
            shape((conts, width), BF),
            shape((conts, width), BF),
            shape((PROMPT, width), BF),
            shape((PROMPT, width), BF),
            shape((rows, width), BF),
            shape((rows // 2, width), BF),
            shape((rows // 2, width), BF),
            shape((D, units // 2), BF),
            shape((D, units // 2), BF),
            shape((width // 2, D), BF),
            shape((width // 2, D), BF),
            shape((units // 4, D), BF),
            shape((units // 4, D), BF),
            shape((1, shared), F32),
        ],
        compiler_params=pltpu.CompilerParams(vmem_limit_bytes=56 << 20, collective_id=0, has_side_effects=True),
        cost_estimate=pl.CostEstimate(flops=20 * 10**9, bytes_accessed=60 * 10**6, transcendentals=0),
        name="attend",
    )(starts, gaps, seg, rate, hid, vec, wq, wk, wv, w1, wo, w2, vec)


EARLY = 2
FIRST_CUT = 1920


def reducer_scratch(count, block, cut):
    return [
        pltpu.VMEM((count, 2, 2, 2, block, cut), BF),
        pltpu.VMEM((count, 2, 2, 2, block, cut), BF),
        pltpu.VMEM((count, 2, 2, block, cut), BF),
        pltpu.VMEM((count, 2, 2, block, cut), BF),
        pltpu.VMEM((count, 2, block, cut), BF),
        pltpu.VMEM((count, 2, block, cut), BF),
        pltpu.VMEM((count, block, cut), BF),
        pltpu.SemaphoreType.DMA((4 * count,)),
        pltpu.SemaphoreType.DMA((4 * count,)),
        pltpu.SemaphoreType.DMA((count,)),
    ]


def reducer(packed, device, side, base, refs, done):
    held, got0, got1, held1, got2, held2, got3, sems_a, sems_b, sems_l = refs
    bit = [(device // (1 << b)) % 2 for b in range(4)]
    peers = [{"dp": bit_peer(device, b), "tensor": side} for b in range(4)]
    cut = held.shape[-1]

    def passing(c, stage, source, target, peer):
        return pltpu.make_async_remote_copy(
            src_ref=source,
            dst_ref=target,
            send_sem=sems_a.at[4 * c + stage],
            recv_sem=sems_b.at[4 * c + stage],
            device_id=peer,
            device_id_type=MESH,
        )

    count = held.shape[0]

    def columns_of(c, first):
        return pl.ds(first + (count - 1 - c) * cut, cut)

    def own_half(c):
        return pltpu.make_async_copy(packed.at[:, :, :, bit[0], :, columns_of(c, base)], held.at[c], sems_l.at[c])

    def stage0(c):
        return passing(c, 0, packed.at[:, :, :, 1 - bit[0], :, columns_of(c, base)], got0.at[c], peers[0])

    def stage1(c):
        if c % 2:
            return passing(c, 1, held.at[c, :, 1 - bit[2]], got1.at[c], peers[2])
        return passing(c, 1, held.at[c, :, :, 1 - bit[1]], got1.at[c], peers[1])

    def stage2(c):
        b = 1 if c % 2 else 2
        return passing(c, 2, held1.at[c, :, 1 - bit[b]], got2.at[c], peers[b])

    def stage3(c):
        return passing(c, 3, held2.at[c, 1 - bit[3]], got3.at[c], peers[3])

    def begin(c):
        own_half(c).start()
        stage0(c).start()

    def after0(c):
        own_half(c).wait()
        stage0(c).wait_recv()
        held[c] = held[c] + got0[c]
        stage1(c).start()

    def after1(c):
        stage1(c).wait_recv()
        kept = held[c, :, bit[2]] if c % 2 else held[c, :, :, bit[1]]
        held1[c] = kept + got1[c]
        stage2(c).start()

    def after2(c):
        stage2(c).wait_recv()
        held2[c] = held1[c, :, bit[1 if c % 2 else 2]] + got2[c]
        stage3(c).start()

    def after3(c):
        stage3(c).wait_recv()
        done[:, columns_of(c, 0)] = held2[c, bit[3]] + got3[c]

    def settle():
        for c in range(count):
            for copy in (stage0(c), stage1(c), stage2(c), stage3(c)):
                copy.wait_send()

    return begin, after0, after1, after2, after3, settle


def tile_at(step, last):
    side = lax.axis_index("tensor")
    prompt = (step + side) % PTILES
    conts = (1 - side) * step + side * (PTILES + last - step)
    return jnp.where(step < PTILES, prompt, conts)


def bwd_kernel(
    fused, q_ref, kp_ref, vp_ref, ko_ref, vo_ref, o_ref, li_ref, e_ref, g_mine, g_theirs, out_half, *refs
):
    packed = refs[0] if fused else None
    refs = refs[1:] if fused else refs
    dq_ref, dko_ref, dvo_ref, sum_k, sum_v, relay_out, out_got = refs[:7]
    done_out, other_out = refs[7:9] if fused else (None, None)
    refs = refs[9:] if fused else refs[7:]
    dk_s, dv_s, g_s, grad_s, near_s, relay_s, far_s, sems_a, sems_b, loc_sems = refs[:10]
    pair = pl.program_id(0)
    step = pl.program_id(1)
    tile = tile_at(step, pl.num_programs(1) - 1)
    device = lax.axis_index("dp")
    side = lax.axis_index("tensor")
    member = device % GDEV
    rows, width = g_s.shape
    n_pairs = width // 128
    conts = rows - CHUNK
    half_p, half_c = CHUNK // 2, conts // 2
    near = {"dp": bit_peer(device, 0), "tensor": side}
    far = {"dp": bit_peer(device, 1), "tensor": side}
    across = {"dp": device, "tensor": 1 - side}
    lanes = pl.ds(pl.multiple_of(pair * 128, 128), 128)
    mine_p = pl.ds(pl.multiple_of(side * half_p, 128), half_p)
    mine_c = pl.ds(pl.multiple_of(CHUNK + side * half_c, 128), half_c)

    def remote(i, src, dst, peer):
        return pltpu.make_async_remote_copy(
            src_ref=src, dst_ref=dst, send_sem=sems_a.at[i], recv_sem=sems_b.at[i], device_id=peer, device_id_type=MESH
        )

    def heads():
        return [
            remote(0, g_theirs.at[pl.ds(0, half_p), :], g_s.at[mine_p, :], across),
            remote(1, g_theirs.at[pl.ds(half_p, half_c), :], g_s.at[mine_c, :], across),
            remote(2, out_half, out_got, across),
        ]

    def local():
        return [
            pltpu.make_async_copy(g_mine.at[pl.ds(0, half_p), :], g_s.at[mine_p, :], loc_sems.at[0]),
            pltpu.make_async_copy(g_mine.at[pl.ds(half_p, half_c), :], g_s.at[mine_c, :], loc_sems.at[1]),
        ]

    def cores(p):
        part = pl.ds(p * 128, 128)
        return remote(3 + 2 * p, grad_s.at[:, :, 1, :, part], near_s.at[:, :, :, part], near)

    def chips(p):
        part = pl.ds(p * 128, 128)
        return remote(4 + 2 * p, relay_s.at[:, :, part], far_s.at[:, :, part], far)

    if fused:
        *early_refs, done_s, other_a, early_sems = refs[10:]
        begin, after0, after1, after2, after3, settle = reducer(
            packed, device, side, packed.shape[-1] - EARLY * FIRST_CUT, early_refs, done_s
        )
        half_e = packed.shape[-1] // 2
        tail_e = EARLY * FIRST_CUT - half_e
        peers = [{"dp": bit_peer(device, b), "tensor": side} for b in range(4)]
        swap = pltpu.make_async_remote_copy(
            src_ref=done_s.at[:, pl.ds(tail_e, half_e)],
            dst_ref=other_a,
            send_sem=early_sems.at[0],
            recv_sem=early_sems.at[1],
            device_id=across,
            device_id_type=MESH,
        )
        tick = pair * pl.num_programs(1) + step

    @pl.when((pair == 0) & (step == 0))
    def _():
        greet([near, far, across] + (peers[2:] if fused else []))
        for copy in heads() + local():
            copy.start()
        for copy in local():
            copy.wait()

    if fused:
        for c in range(EARLY):
            for at, act in ((0, begin), (1 + c, after0), (5 + c, after1), (8 + c, after2), (12, after3)):
                @pl.when(tick == at)
                def _():
                    act(c)

        @pl.when(tick == 12)
        def _():
            swap.start()

    @pl.when((pair == 0) & (step == 1))
    def _():
        heads()[0].wait_recv()

    @pl.when((pair == 0) & (step == 3))
    def _():
        heads()[1].wait_recv()

    low = low_half(TILE)
    g = g_s[pl.ds(pl.multiple_of(tile * TILE, TILE), TILE), lanes].astype(F32) * li_ref[...]
    prod = g * o_ref[...].astype(F32)
    zf = jnp.zeros((TILE, 128), F32)
    deltas = [
        jnp.sum(jnp.where(low, prod, zf), axis=1, keepdims=True),
        jnp.sum(jnp.where(low, zf, prod), axis=1, keepdims=True),
    ]
    gs = [jnp.where(low, g, zf).astype(BF), jnp.where(low, zf, g).astype(BF)]
    gt = jnp.transpose(g).astype(BF)
    qt = jnp.transpose(q_ref[...].astype(F32)).astype(BF)

    def grads(dq, keys, vals, at, width):
        out, dks, dvs = [], [], []
        for h in range(2):
            e = e_ref[h, :, pl.ds(at, width)]
            dp = dot_nt(gs[h], vals)
            ds = (e.astype(F32) * (dp - deltas[h])).astype(BF)
            out.append(dq[h] + dot_nn(ds, keys))
            dks.append(dot_nn(qt[h * HD : (h + 1) * HD, :], ds))
            dvs.append(dot_nn(gt[h * HD : (h + 1) * HD, :], e))
        return tuple(out), dks, dvs

    @pl.when(step == 0)
    def _():
        dk_s[...] = jnp.zeros_like(dk_s)
        dv_s[...] = jnp.zeros_like(dv_s)

    def add(at, width, dks, dvs):
        for h in range(2):
            dk_s[h * HD : (h + 1) * HD, pl.ds(at, width)] += dks[h]
            dv_s[h * HD : (h + 1) * HD, pl.ds(at, width)] += dvs[h]

    def scaled(dq):
        return (jnp.where(low, dq[0], dq[1]).astype(BF).astype(F32) * 0.125).astype(BF)

    @pl.when(step < PTILES)
    def _():
        def one(j, dq):
            at = pl.multiple_of(xor_bits(j, member) * CHUNK, CHUNK)
            dq, dks, dvs = grads(dq, kp_ref[pl.ds(at, CHUNK), :], vp_ref[pl.ds(at, CHUNK), :], at, CHUNK)
            add(at, CHUNK, dks, dvs)
            return dq

        dq_ref[...] = scaled(lax.fori_loop(0, member + 1, one, (zf, zf)))
        dko_ref[...] = jnp.zeros_like(dko_ref)
        dvo_ref[...] = jnp.zeros_like(dvo_ref)

    @pl.when(step >= PTILES)
    def _():
        dq = (zf, zf)
        for j in range(GDEV):
            span = slice(j * CHUNK, (j + 1) * CHUNK)
            dq, dks, dvs = grads(dq, kp_ref[span, :], vp_ref[span, :], j * CHUNK, CHUNK)
            add(j * CHUNK, CHUNK, dks, dvs)
        dq, dks, dvs = grads(dq, ko_ref[...], vo_ref[...], PROMPT, CONT)
        dq_ref[...] = scaled(dq)
        dko_ref[...] = jnp.transpose(jnp.concatenate(dks, axis=0)).astype(BF)
        dvo_ref[...] = jnp.transpose(jnp.concatenate(dvs, axis=0)).astype(BF)

    end = pl.num_programs(1) - 1

    @pl.when(step == end)
    def _():
        for j in range(GDEV):
            span = slice(j * CHUNK, (j + 1) * CHUNK)
            grad_s[0, j // 2, j % 2, :, lanes] = jnp.transpose(dk_s[:, span]).astype(BF)
            grad_s[1, j // 2, j % 2, :, lanes] = jnp.transpose(dv_s[:, span]).astype(BF)

    for p in range(n_pairs):
        @pl.when((pair == p) & (step == end))
        def _():
            cores(p).start()

        if p + 1 < n_pairs:
            @pl.when((pair == p + 1) & (step == 2))
            def _():
                part = pl.ds(p * 128, 128)
                cores(p).wait_recv()
                relay_s[:, :, part] = (
                    grad_s[:, 1, 0, :, part].astype(F32) + near_s[:, 1, :, part].astype(F32)
                ).astype(BF)
                chips(p).start()

    @pl.when((pair == n_pairs - 1) & (step == end))
    def _():
        last = n_pairs - 1
        sums = (sum_k, sum_v)
        for p in range(last):
            part = pl.ds(p * 128, 128)
            chips(p).wait_recv()
            for i in range(2):
                sums[i][:, part] = (
                    grad_s[i, 0, 0, :, part].astype(F32) + near_s[i, 0, :, part].astype(F32) + far_s[i, :, part].astype(F32)
                ).astype(BF)
        part = pl.ds(last * 128, 128)
        cores(last).wait_recv()
        for i in range(2):
            relay_out[i] = (grad_s[i, 1, 0, :, part].astype(F32) + near_s[i, 1, :, part].astype(F32)).astype(BF)
            sums[i][:, part] = (grad_s[i, 0, 0, :, part].astype(F32) + near_s[i, 0, :, part].astype(F32)).astype(BF)
        if fused:
            swap.wait_recv()
            done_out[...] = done_s[:, pl.ds(0, tail_e)]
            other_out[...] = other_a[...]
            settle()
            swap.wait_send()
        heads()[2].wait_recv()
        for copy in heads():
            copy.wait_send()
        for p in range(n_pairs):
            cores(p).wait_send()
            if p < last:
                chips(p).wait_send()


def attend_back(q, k, v, kp, vp, o, li, e, g_mine, g_theirs, out_half, packed):
    rows, width = q.shape
    pairs = width // 128
    span = PROMPT + CONT
    last = rows // TILE - 1
    tile = pl.BlockSpec((TILE, 128), lambda a, t: (tile_at(t, last), a))
    whole = pl.BlockSpec((PROMPT, 128), lambda a, t: (0, a))
    own = pl.BlockSpec((TILE, 128), lambda a, t: (jnp.maximum(tile_at(t, last) - PTILES, 0), a))
    vmem = pl.BlockSpec(memory_space=pltpu.VMEM)
    hbm = pl.BlockSpec(memory_space=pl.ANY)
    shape = jax.ShapeDtypeStruct
    copies = 3 + 2 * pairs
    fused = packed is not None
    more_in, more_out, more_scratch = [], [], []
    if fused:
        block, half_e = packed.shape[-2], packed.shape[-1] // 2
        more_in = [packed]
        more_out = [shape((block, EARLY * FIRST_CUT - half_e), BF), shape((block, half_e), BF)]
        more_scratch = reducer_scratch(EARLY, block, FIRST_CUT) + [
            pltpu.VMEM((block, EARLY * FIRST_CUT), BF),
            pltpu.VMEM((block, half_e), BF),
            pltpu.SemaphoreType.DMA((2,)),
        ]
    return pl.pallas_call(
        functools.partial(bwd_kernel, fused),
        grid=(pairs, rows // TILE),
        in_specs=[tile, whole, whole, own, own, tile, tile, pl.BlockSpec((2, TILE, span), lambda a, t: (a, tile_at(t, last), 0))]
        + [hbm] * (3 + len(more_in)),
        out_specs=[tile, tile, tile, vmem, vmem, vmem, hbm] + [vmem] * len(more_out),
        out_shape=[
            shape((rows, width), BF),
            shape((rows, width), BF),
            shape((rows, width), BF),
            shape((CHUNK, width), BF),
            shape((CHUNK, width), BF),
            shape((2, CHUNK, 128), BF),
            shape(out_half.shape, BF),
        ]
        + more_out,
        scratch_shapes=[
            pltpu.VMEM((128, PROMPT), F32),
            pltpu.VMEM((128, PROMPT), F32),
            pltpu.VMEM((rows, width), BF),
            pltpu.VMEM((2, 2, 2, CHUNK, width), BF),
            pltpu.VMEM((2, 2, CHUNK, width), BF),
            pltpu.VMEM((2, CHUNK, width), BF),
            pltpu.VMEM((2, CHUNK, width), BF),
            pltpu.SemaphoreType.DMA((copies,)),
            pltpu.SemaphoreType.DMA((copies,)),
            pltpu.SemaphoreType.DMA((2,)),
        ]
        + more_scratch,
        compiler_params=pltpu.CompilerParams(vmem_limit_bytes=60 << 20, collective_id=2, has_side_effects=True),
        cost_estimate=pl.CostEstimate(flops=30 * 10**9, bytes_accessed=60 * 10**6, transcendentals=0),
        name="attend_back",
    )(q, kp, vp, k, v, o, li, e, g_mine, g_theirs, out_half, *more_in)


UCH = 768


def polynomial(x, terms):
    out = jnp.full_like(x, terms[0])
    for term in terms[1:]:
        out = out * x + term
    return out


def gelu_pair(v):
    bell = jnp.exp(-0.5 * v * v)
    t = 1.0 / (1.0 + (0.3275911 * 0.7071067811865476) * jnp.abs(v))
    terms = (0.5307027145, -0.7265760135, 0.7107068705, -0.142248368, 0.127414796)
    half = polynomial(t, terms) * t * bell
    phi = jnp.where(v < 0.0, half, 1.0 - half)
    return v * phi, phi + v * (bell * 0.3989422804014327)


def column_sum(x):
    return jnp.sum(x, axis=0, keepdims=True)


def mid_kernel(
    att_m, att_o, vec_all, vec_got, hid_all, cot_all, w1_own, w1_got, w1_swap, wo_own, wo_got, wo_swap, w2_own, w2_got, w2_swap,
    out_ref, gatt_m, gatt_o, gmix_ref, packed, su_ref, sw_ref, sd_ref, ext_ref,
    vec_u, vec_w, w1, w2, wo, act_s, shp_s, dg_s, wide_s, acc_s, gmid_s, sub_s, mid_s, low_s, midt_s, cott_s, stage, hid, cot, sems, out_sems, send_sems, recv_sems,
):
    device = lax.axis_index("dp")
    side = lax.axis_index("tensor")
    core = device % 2
    near = {"dp": bit_peer(device, 0), "tensor": side}
    across = {"dp": device, "tensor": 1 - side}
    units = w1_own.shape[1]
    width = wo_own.shape[0]
    rows = hid.shape[0]
    full = 2 * units
    half = units // 2
    half_w = width // 2
    here_u = pl.multiple_of(units + core * half, 128)
    there_u = pl.multiple_of(units + (1 - core) * half, 128)
    here_w = pl.multiple_of(width + core * half_w, 64)
    there_w = pl.multiple_of(width + (1 - core) * half_w, 64)
    prompt, conts = CHUNK // 2, (hid_all.shape[0] - CHUNK) // 2
    own_p = pl.ds(pl.multiple_of(side * prompt, 128), prompt)
    own_c = pl.ds(pl.multiple_of(CHUNK + side * conts, 128), conts)
    at_own = 2 * D + 2 * width
    vec_own = vec_all.at[:, pl.ds(at_own, 3 * units + 2 * width)]
    vec_d = vec_all.at[:, pl.ds(at_own + 3 * units + 2 * width, 4 * D)]
    rows_in = []
    for i, (all_rows, held) in enumerate(((hid_all, hid), (cot_all, cot))):
        for j, (span, at, size) in enumerate(((own_p, 0, prompt), (own_c, prompt, conts))):
            copy = pltpu.make_async_copy(all_rows.at[span, :], held.at[pl.ds(at, size), :], sems.at[9 + 2 * i + j])
            copy.start()
            rows_in.append(copy)
    loads = []
    for i, (src, dst) in enumerate(
        [
            (wo_own, wo.at[pl.ds(0, width), :]),
            (wo_got, wo.at[pl.ds(here_w, half_w), :]),
            (wo_swap, wo.at[pl.ds(there_w, half_w), :]),
            (w1_own, w1.at[:, pl.ds(0, units)]),
            (w1_got, w1.at[:, pl.ds(here_u, half)]),
            (w1_swap, w1.at[:, pl.ds(there_u, half)]),
            (w2_own, w2.at[pl.ds(0, units), :]),
            (w2_got, w2.at[pl.ds(here_u, half // 2), :]),
            (w2_swap, w2.at[pl.ds(there_u, half // 2), :]),
        ]
    ):
        copy = pltpu.make_async_copy(src, dst, sems.at[i])
        copy.start()
        loads.append(copy)

    piece = half // 2
    greet([near, across])

    def remote(i, src, dst, peer):
        return pltpu.make_async_remote_copy(
            src_ref=src, dst_ref=dst, send_sem=send_sems.at[i], recv_sem=recv_sems.at[i], device_id=peer, device_id_type=MESH
        )

    from_own = pl.ds(pl.multiple_of(core * half + piece, 128), piece)
    landed = w2.at[pl.ds(pl.multiple_of(units + core * half + piece, 128), piece), :]
    over = remote(0, w2_own.at[from_own, :], landed, across)
    passed = remote(1, landed, landed, near)
    over.start()

    for i in range(3):
        for j, vec in enumerate((vec_own, vec_got)):
            vec_u[i : i + 1, pl.ds(j * units, units)] = vec[0:1, pl.ds(i * units, units)]
    for i in range(2):
        for j, vec in enumerate((vec_own, vec_got)):
            vec_w[i : i + 1, pl.ds(j * width, width)] = vec[0:1, pl.ds(3 * units + i * width, width)]

    a0 = att_m[...].astype(F32)
    a1 = att_o[...].astype(F32)
    center = (jnp.sum(a0, axis=1, keepdims=True) + jnp.sum(a1, axis=1, keepdims=True)) * (1.0 / D)
    square = (jnp.sum(a0 * a0, axis=1, keepdims=True) + jnp.sum(a1 * a1, axis=1, keepdims=True)) * (1.0 / D)
    sub_scale = lax.rsqrt(square - center * center + EPSILON)
    sub_s[:, 0:width] = (a0 - center) * sub_scale
    sub_s[:, width : 2 * width] = (a1 - center) * sub_scale
    sub_gain = vec_w[0:1, :]
    low_s[...] = (sub_s[...] * sub_gain + vec_w[1:2, :]).astype(BF)
    for copy in loads[0:3] + rows_in:
        copy.wait()
    mixed = hid[...].astype(F32) + (dot_nn(low_s[...], wo[...]) + vec_d[0:1, pl.ds(0, D)])
    wide_s[...] = mixed
    mean = jnp.mean(mixed, axis=1, keepdims=True)
    mid_scale = lax.rsqrt(jnp.mean(mixed * mixed, axis=1, keepdims=True) - mean * mean + EPSILON)
    mid_s[...] = (mixed - mean) * mid_scale
    mid_gain = vec_d[0:1, pl.ds(768, D)]
    mid_full = mid_s[...] * mid_gain + vec_d[0:1, pl.ds(1536, D)]
    mid_low = mid_full.astype(BF)
    midt_s[...] = jnp.transpose(mid_full).astype(BF)
    cot_full = cot[...].astype(F32)
    cott_s[...] = jnp.transpose(cot_full).astype(BF)
    sd_ref[...] = jnp.zeros_like(sd_ref)
    sd_ref[3:4, :] = column_sum(cot_full)
    for copy in loads[3:6]:
        copy.wait()

    def unrolled(low, high, step, carry):
        for c in range(low, high):
            carry = step(c, carry)
        return carry

    def lanes_sum(x):
        total = x[:, 0:128]
        for i in range(1, x.shape[1] // 128):
            total = total + x[:, i * 128 : (i + 1) * 128]
        return total

    zero = jnp.zeros((rows, 128), F32)
    act_sum, act_square = zero, zero

    def inner_of(c):
        at = c * UCH
        shp_s[:, at : at + UCH] = dot_nn(mid_low, w1[:, at : at + UCH]) + vec_u[2:3, at : at + UCH]

    inner_of(0)
    for c in range(full // UCH):
        at = c * UCH
        if c + 1 < full // UCH:
            inner_of(c + 1)
        act, slope = gelu_pair(shp_s[:, at : at + UCH])
        act_s[:, at : at + UCH] = act
        dg_s[:, at : at + UCH] = slope.astype(BF)
        act_sum, act_square = act_sum + lanes_sum(act), act_square + lanes_sum(act * act)
    ffn_center = jnp.sum(act_sum, axis=1, keepdims=True) * (1.0 / full)
    ffn_scale = lax.rsqrt(
        jnp.sum(act_square, axis=1, keepdims=True) * (1.0 / full) - ffn_center * ffn_center + EPSILON
    )
    for copy in loads[6:9]:
        copy.wait()
    over.wait_recv()
    passed.start()
    acc_s[...] = jnp.zeros_like(acc_s)
    per = units // UCH
    wide = 2 * units + width

    def column_of(c, extra):
        return pl.multiple_of((c // per) * wide + (c % per) * UCH + extra, 128)

    def send(slot, column):
        return pltpu.make_async_copy(stage.at[slot], packed.at[:, pl.ds(column, UCH)], out_sems.at[slot])

    def put(c, value, extra):
        slot = c % 2

        @pl.when(c >= 2)
        def _():
            send(slot, column_of(c - 2, extra)).wait()

        stage[slot] = value
        send(slot, column_of(c, extra)).start()

    def drain(extra):
        for c in range(full // UCH - 2, full // UCH):
            send(c % 2, column_of(c, extra)).wait()

    def second(c, carry):
        at = pl.multiple_of(c * UCH, UCH)
        unit = (act_s[:, pl.ds(at, UCH)] - ffn_center) * ffn_scale
        act_s[:, pl.ds(at, UCH)] = unit
        gain = vec_u[0:1, pl.ds(at, UCH)]
        low = (unit * gain + vec_u[1:2, pl.ds(at, UCH)]).astype(BF)
        acc_s[...] += dot_nn(low, w2[pl.ds(at, UCH), :])
        grad = dot_nt(cot[...], w2[pl.ds(at, UCH), :])
        cross = grad * unit
        su_ref[0:1, pl.ds(at, UCH)] = column_sum(cross)
        su_ref[1:2, pl.ds(at, UCH)] = column_sum(grad)
        shaped = grad * gain
        shp_s[:, pl.ds(at, UCH)] = shaped
        put(c, dot_nn(cott_s[...], low).astype(BF), units)
        return carry[0] + lanes_sum(shaped), carry[1] + lanes_sum(shaped * unit)

    su_ref[...] = jnp.zeros_like(su_ref)
    sums = unrolled(0, per, second, (zero, zero))
    passed.wait_recv()
    s_sum, s_cross = unrolled(per, 2 * per, second, sums)
    drain(units)
    shaped_mean = jnp.sum(s_sum, axis=1, keepdims=True) * (1.0 / full)
    cross_mean = jnp.sum(s_cross, axis=1, keepdims=True) * (1.0 / full)
    out_ref[...] = (wide_s[...] + (acc_s[...] + vec_d[0:1, pl.ds(2304, D)])).astype(BF)
    gmid_s[...] = jnp.zeros_like(gmid_s)

    def third(c, carry):
        at = pl.multiple_of(c * UCH, UCH)
        g = ffn_scale * (shp_s[:, pl.ds(at, UCH)] - shaped_mean - act_s[:, pl.ds(at, UCH)] * cross_mean)
        low = (g * dg_s[:, pl.ds(at, UCH)].astype(F32)).astype(BF)
        su_ref[2:3, pl.ds(at, UCH)] = column_sum(low.astype(F32))
        gmid_s[...] += dot_nt(low, w1[:, pl.ds(at, UCH)])
        put(c, dot_nn(midt_s[...], low).astype(BF), 0)
        return carry

    unrolled(0, 2 * per, third, 0)
    drain(0)

    grad_mid = gmid_s[...]
    unit = mid_s[...]
    sd_ref[1:2, :] = column_sum(grad_mid * unit)
    sd_ref[2:3, :] = column_sum(grad_mid)
    shaped = grad_mid * mid_gain
    grad_mixed = cot[...].astype(F32) + mid_scale * (
        shaped - jnp.mean(shaped, axis=1, keepdims=True) - unit * jnp.mean(shaped * unit, axis=1, keepdims=True)
    )
    branch = grad_mixed.astype(BF)
    gmix_ref[...] = branch
    branch_f = branch.astype(F32)
    sd_ref[0:1, :] = column_sum(branch_f)
    out_grad = dot_nn(jnp.transpose(branch_f).astype(BF), low_s[...]).astype(BF)
    stage[0, :, 0:width] = out_grad[:, 0:width]
    stage[1, :, 0:width] = out_grad[:, width : 2 * width]
    last = [
        pltpu.make_async_copy(stage.at[i, :, pl.ds(0, width)], packed.at[:, pl.ds(i * wide + 2 * units, width)], out_sems.at[i])
        for i in range(2)
    ]
    for copy in last:
        copy.start()
    grad_sub = dot_nt(branch, wo[...])
    unit = sub_s[...]
    cross = grad_sub * unit
    sw_ref[...] = jnp.zeros_like(sw_ref)
    sw_ref[0:1, :] = column_sum(cross)
    sw_ref[1:2, :] = column_sum(grad_sub)
    shaped = grad_sub * sub_gain
    grad_att = sub_scale * (
        shaped - jnp.mean(shaped, axis=1, keepdims=True) - unit * jnp.mean(shaped * unit, axis=1, keepdims=True)
    )
    gatt_m[...] = grad_att[:, 0:width].astype(BF)
    gatt_o[...] = grad_att[:, width : 2 * width].astype(BF)
    parts = ext_ref.shape[0]
    if parts > 1:
        sums_u, sums_w, sums_d = su_ref[...], sw_ref[...], sd_ref[...]
        for i in range(parts):
            ext_ref[i] = jnp.concatenate(
                [
                    window(sums_u, i * (units // parts)),
                    window(sums_u, units + i * (units // parts)),
                    window(sums_w, i * (width // parts)),
                    window(sums_w, width + i * (width // parts)),
                    window(sums_d, i * (D // parts)),
                    jnp.zeros((8, 128), F32),
                ],
                axis=0,
            ).astype(BF)
    for copy in last:
        copy.wait()
    over.wait_send()
    passed.wait_send()


def window(rows8, start):
    base = start // 128 * 128
    size = min(256, rows8.shape[1] - base)
    view = rows8[:, base : base + size]
    shift = start - base
    if shift:
        view = pltpu.roll(view, size - shift, 1)
    return view[:, 0:128]


def middle(att_m, att_o, hid, cot, vec_all, vec_got, w1, w2, wo, parts):
    rows = att_m.shape[0]
    units = w2[0].shape[0]
    width = wo[0].shape[0]
    vmem = pl.BlockSpec(memory_space=pltpu.VMEM)
    hbm = pl.BlockSpec(memory_space=pl.ANY)
    shape = jax.ShapeDtypeStruct
    return pl.pallas_call(
        mid_kernel,
        in_specs=[vmem] * 4 + [hbm] * 11,
        out_specs=[vmem] * 4 + [hbm] + [vmem] * 4,
        out_shape=[
            shape((rows, D), BF),
            shape((rows, width), BF),
            shape((rows, width), BF),
            shape((rows, D), BF),
            shape((D, 2 * (2 * units + width)), BF),
            shape((8, 2 * units), F32),
            shape((8, 2 * width), F32),
            shape((8, D), F32),
            shape((parts, 48, 128), BF),
        ],
        scratch_shapes=[
            pltpu.VMEM((8, 2 * units), F32),
            pltpu.VMEM((8, 2 * width), F32),
            pltpu.VMEM((D, 2 * units), BF),
            pltpu.VMEM((2 * units, D), BF),
            pltpu.VMEM((2 * width, D), BF),
            pltpu.VMEM((rows, 2 * units), F32),
            pltpu.VMEM((rows, 2 * units), F32),
            pltpu.VMEM((rows, 2 * units), BF),
            pltpu.VMEM((rows, D), F32),
            pltpu.VMEM((rows, D), F32),
            pltpu.VMEM((rows, D), F32),
            pltpu.VMEM((rows, 2 * width), F32),
            pltpu.VMEM((rows, D), F32),
            pltpu.VMEM((rows, 2 * width), BF),
            pltpu.VMEM((D, rows), BF),
            pltpu.VMEM((D, rows), BF),
            pltpu.VMEM((2, D, UCH), BF),
            pltpu.VMEM((rows, D), BF),
            pltpu.VMEM((rows, D), BF),
            pltpu.SemaphoreType.DMA((13,)),
            pltpu.SemaphoreType.DMA((2,)),
            pltpu.SemaphoreType.DMA((2,)),
            pltpu.SemaphoreType.DMA((2,)),
        ],
        compiler_params=pltpu.CompilerParams(vmem_limit_bytes=62 << 20, collective_id=3, has_side_effects=True),
        cost_estimate=pl.CostEstimate(flops=21 * 10**9, bytes_accessed=30 * 10**6, transcendentals=0),
        name="middle",
    )(att_m, att_o, vec_all, vec_got, hid, cot, *w1, *wo, *w2)


def final_kernel(
    bits, hid, vec_all, dq, dk, dv, wq, wk, wv, gmix, ext, sum_k, sum_v, relay, first_done, first_other, packed,
    gin, late_out, vec_out, early_out,
    loc_s, far_s, unit_s, mine_s, norm_s, send_c, recv_c, send_p, recv_p, give_c, give_p, late_s, small_s,
    vec_s, vec_r, done_s, sems_a, sems_b, loc_sems, *stage_refs,
):
    device = lax.axis_index("dp")
    side = lax.axis_index("tensor")
    across = {"dp": device, "tensor": 1 - side}
    peers = [{"dp": bit_peer(device, b), "tensor": side} for b in range(bits)]
    rows, width = dq.shape
    prompt = sum_k.shape[0]
    conts = rows - prompt
    half_p, half_c = prompt // 2, conts // 2
    own_p = pl.multiple_of(side * half_p, 128)
    their_p = pl.multiple_of((1 - side) * half_p, 128)
    own_c = pl.multiple_of(prompt + side * half_c, 128)
    their_c = pl.multiple_of(prompt + (1 - side) * half_c, 128)
    lanes = 3 * width + 128

    greet(peers + [across])
    count = [0]

    def remote(src, dst, peer):
        i = count[0]
        count[0] += 1
        copy = pltpu.make_async_remote_copy(
            src_ref=src, dst_ref=dst, send_sem=sems_a.at[i], recv_sem=sems_b.at[i], device_id=peer, device_id_type=MESH
        )
        copy.start()
        return copy

    share = remote(relay, far_s, peers[1])

    begin, after0, after1, after2, after3, settle = reducer(packed, device, side, 0, stage_refs[-10:], done_s)

    def each(act):
        for c in range(EARLY):
            act(c)

    each(begin)

    gain_f = vec_all[:, pl.ds(0, D)]
    bias_f = vec_all[:, pl.ds(D, D)]

    def unit_rows(at, size):
        x = hid[pl.ds(at, size), :].astype(F32)
        center = jnp.mean(x, axis=1, keepdims=True)
        scale = lax.rsqrt(jnp.mean(x * x, axis=1, keepdims=True) - center * center + EPSILON)
        return (x - center) * scale, scale

    def part_of(at, size, k_rows, v_rows):
        return dot_nt(dq[pl.ds(at, size), :], wq[...]) + dot_nt(k_rows, wk[...]) + dot_nt(v_rows, wv[...])

    def gather(part, unit):
        return column_sum(part * unit), column_sum(part)

    def normed_rows(at, size, unit):
        norm_s[:, pl.ds(at, size)] = jnp.transpose(unit * gain_f + bias_f).astype(BF)

    part = part_of(their_c, half_c, dk[pl.ds(their_c, half_c), :], dv[pl.ds(their_c, half_c), :])
    send_c[...] = part.astype(BF)
    y_cont = remote(send_c, recv_c, across)
    unit, _ = unit_rows(their_c, half_c)
    gain_grad, bias_grad = gather(part, unit)
    normed_rows(their_c, half_c, unit)
    unit, scale_c = unit_rows(own_c, half_c)
    part = part_of(own_c, half_c, dk[pl.ds(own_c, half_c), :], dv[pl.ds(own_c, half_c), :])
    mine_s[pl.ds(half_p, half_c), :] = part
    unit_s[pl.ds(half_p, half_c), :] = unit
    g, b = gather(part, unit)
    gain_grad, bias_grad = gain_grad + g, bias_grad + b
    normed_rows(own_c, half_c, unit)

    each(after0)
    share.wait_recv()
    for i, total in enumerate((sum_k, sum_v)):
        loc_s[i, :, pl.ds(0, width - 128)] = total[:, pl.ds(0, width - 128)]
        loc_s[i, :, pl.ds(width - 128, 128)] = (
            total[:, pl.ds(width - 128, 128)].astype(F32) + far_s[i].astype(F32)
        ).astype(BF)
    part = part_of(their_p, half_p, loc_s[0, pl.ds(their_p, half_p), :], loc_s[1, pl.ds(their_p, half_p), :])
    send_p[...] = part.astype(BF)
    y_prompt = remote(send_p, recv_p, across)
    unit, _ = unit_rows(their_p, half_p)
    normed_rows(their_p, half_p, unit)
    g, b = gather(part, unit)
    gain_grad, bias_grad = gain_grad + g, bias_grad + b
    unit, scale_p = unit_rows(own_p, half_p)
    unit_s[pl.ds(0, half_p), :] = unit
    normed_rows(own_p, half_p, unit)
    part = part_of(own_p, half_p, loc_s[0, pl.ds(own_p, half_p), :], loc_s[1, pl.ds(own_p, half_p), :])
    mine_s[pl.ds(0, half_p), :] = part
    g, b = gather(part, unit)
    gain_grad, bias_grad = gain_grad + g, bias_grad + b

    blocks = 1 << bits
    block = D // blocks

    def keep(value, lane):
        low = value.astype(BF)
        for i in range(blocks):
            late_s[i // 2, i % 2, :, pl.ds(lane, width)] = low[i * block : (i + 1) * block, :]

    keep(dot_nn(norm_s[...], dq[...]), 0)
    q_bias = column_sum(dq[...].astype(F32))
    for i, rest in enumerate((dk, dv)):
        keep(
            dot_nn(norm_s[:, pl.ds(0, prompt)], loc_s[i])
            + dot_nn(norm_s[:, pl.ds(prompt, conts)], rest[pl.ds(prompt, conts), :]),
            (i + 1) * width,
        )
    v_bias = column_sum(loc_s[1].astype(F32)) + column_sum(dv[pl.ds(prompt, conts), :].astype(F32))

    def norm_back(total, unit, scale, mixed):
        shaped = total * gain_f
        return mixed.astype(F32) + scale * (
            shaped - jnp.mean(shaped, axis=1, keepdims=True) - unit * jnp.mean(shaped * unit, axis=1, keepdims=True)
        )

    small_s[...] = jnp.zeros_like(small_s)
    small_s[0:1, pl.ds(0, width)] = q_bias
    small_s[1:2, pl.ds(0, width)] = v_bias
    small_s[2:3, pl.ds(0, D)] = gain_grad
    small_s[3:4, pl.ds(0, D)] = bias_grad
    small = small_s[...]
    row_id = lax.broadcasted_iota(jnp.int32, (8, 128), 0)
    for i in range(blocks):
        narrow = window(small, i * (width // blocks))
        broad = window(small, i * block)
        tail = jnp.concatenate([ext[i, pl.ds(32, 16), :].astype(F32)[0:8], jnp.where(row_id < 2, narrow, broad)], axis=0)
        late_s[i // 2, i % 2, pl.ds(0, 32), pl.ds(3 * width, 128)] = ext[i, pl.ds(0, 32), :]
        late_s[i // 2, i % 2, pl.ds(32, 16), pl.ds(3 * width, 128)] = tail.astype(BF)

    def input_rows(arrived, at, size, scale, held, rows_at, sem):
        arrived[0].wait_recv()
        here = pl.ds(at, size)
        total = mine_s[here, :] + arrived[1][...].astype(F32)
        held[...] = norm_back(total, unit_s[here, :], scale, gmix[here, :]).astype(BF)
        back = remote(held, gin.at[pl.ds(rows_at, size), :], across)
        kept = pltpu.make_async_copy(held, gin.at[pl.ds(rows_at, size), :], loc_sems.at[sem])
        kept.start()
        return back, kept

    source = late_s
    stages = []
    for bit in range(bits):
        landing, kept = stage_refs[2 * bit], stage_refs[2 * bit + 1]
        mine = (device // (1 << bit)) % 2
        copy = remote(source.at[:, 1 - mine], landing, peers[bit])
        if bit == 0:
            back_c, keep_c = input_rows((y_cont, recv_c), half_p, half_c, scale_c, give_c, own_c, 0)
        if bit == 1:
            each(after1)
            back_p, keep_p = input_rows((y_prompt, recv_p), 0, half_p, scale_p, give_p, own_p, 1)
        if bit == 2:
            each(after2)
        if bit == 3:
            each(after3)
        copy.wait_recv()
        stages.append(copy)
        for i in range(landing.shape[0]):
            kept[i // 2, i % 2] = (source[i, mine].astype(F32) + landing[i].astype(F32)).astype(BF)
        source = kept
    late_out[...] = source[0, 0, :, pl.ds(0, 3 * width)].astype(F32)
    vec_s[...] = source[0, 0, :, pl.ds(3 * width, 128)]
    swap = remote(vec_s, vec_r, across)
    last_e = done_s.shape[1]
    early_out[:, pl.ds(0, last_e)] = done_s[...].astype(F32) + first_other[:, pl.ds(0, last_e)].astype(F32)
    rest_e = first_done.shape[1]
    early_out[:, pl.ds(last_e, rest_e)] = first_done[...].astype(F32) + first_other[:, pl.ds(last_e, rest_e)].astype(F32)
    settle()
    swap.wait_recv()
    own_v, got_v = vec_s[...].astype(F32), vec_r[...].astype(F32)
    vec_out[0:8, :] = own_v[0:8] + got_v[8:16]
    vec_out[8:16, :] = own_v[16:24] + got_v[24:32]
    vec_out[16:24, :] = own_v[32:40] + got_v[32:40]
    vec_out[24:32, :] = own_v[40:48] + jnp.where(row_id < 2, 0.0, got_v[40:48])
    for copy in stages + [share, y_cont, y_prompt, swap]:
        copy.wait_send()
    for copy in (back_c, back_p):
        copy.wait_recv()
        copy.wait_send()
    keep_c.wait()
    keep_p.wait()


def finish(hid, vec_all, dq, dk, dv, wq, wk, wv, gmix, ext, sum_k, sum_v, relay, first_done, first_other, packed):
    rows, width = dq.shape
    ranks = lax.axis_size("dp")
    bits = ranks.bit_length() - 1
    block = D // ranks
    prompt = sum_k.shape[0]
    conts = rows - prompt
    lanes = 3 * width + 128
    vmem = pl.BlockSpec(memory_space=pltpu.VMEM)
    hbm = pl.BlockSpec(memory_space=pl.ANY)
    shape = jax.ShapeDtypeStruct
    copies = 6 + bits
    cut = (packed.shape[-1] - EARLY * FIRST_CUT) // EARLY
    stages = []
    for bit in range(bits):
        left = ranks >> (bit + 1)
        stages.append(pltpu.VMEM((left, block, lanes), BF))
        stages.append(pltpu.VMEM((max(left // 2, 1), min(left, 2), block, lanes), BF))
    return pl.pallas_call(
        functools.partial(final_kernel, bits),
        in_specs=[vmem] * 15 + [hbm],
        out_specs=[hbm, vmem, vmem, vmem],
        out_shape=[shape((rows, D), BF), shape((block, 3 * width), F32), shape((32, 128), F32), shape((block, packed.shape[-1] // 2), F32)],
        scratch_shapes=[
            pltpu.VMEM((2, prompt, width), BF),
            pltpu.VMEM((2, prompt, 128), BF),
            pltpu.VMEM((rows // 2, D), F32),
            pltpu.VMEM((rows // 2, D), F32),
            pltpu.VMEM((D, rows), BF),
            pltpu.VMEM((conts // 2, D), BF),
            pltpu.VMEM((conts // 2, D), BF),
            pltpu.VMEM((prompt // 2, D), BF),
            pltpu.VMEM((prompt // 2, D), BF),
            pltpu.VMEM((conts // 2, D), BF),
            pltpu.VMEM((prompt // 2, D), BF),
            pltpu.VMEM((ranks // 2, 2, block, lanes), BF),
            pltpu.VMEM((8, D + 128), F32),
            pltpu.VMEM((block, 128), BF),
            pltpu.VMEM((block, 128), BF),
            pltpu.VMEM((block, EARLY * cut), BF),
            pltpu.SemaphoreType.DMA((copies,)),
            pltpu.SemaphoreType.DMA((copies,)),
            pltpu.SemaphoreType.DMA((2,)),
        ]
        + stages
        + reducer_scratch(EARLY, block, cut),
        compiler_params=pltpu.CompilerParams(vmem_limit_bytes=56 << 20, collective_id=1, has_side_effects=True),
        cost_estimate=pl.CostEstimate(flops=5 * 10**9, bytes_accessed=20 * 10**6, transcendentals=0),
        name="finish",
    )(hid, vec_all, dq, dk, dv, wq, wk, wv, gmix, ext, sum_k, sum_v, relay, first_done, first_other, packed)


def flip(value, axis, bit):
    return lax.ppermute(value, axis, [(i, i ^ (1 << bit)) for i in range(lax.axis_size(axis))])


def contract_rows(left, right):
    return lax.dot_general(left, right, (((0,), (0,)), ((), ())), preferred_element_type=F32)


def back_project(left, right):
    return lax.dot_general(left, right, (((1,), (1,)), ((), ())), preferred_element_type=F32)


def norm_rows(values, gain, bias):
    center = jnp.mean(values, axis=-1, keepdims=True)
    spread = jnp.mean(values * values, axis=-1, keepdims=True) - center * center
    scaled = lax.rsqrt(spread + EPSILON)
    unit_rows = (values - center) * scaled
    return (unit_rows * gain + bias, unit_rows, scaled)


def norm_back(grad_rows, gain, unit_rows, scaled):
    shaped = grad_rows * gain
    return scaled * (
        shaped
        - jnp.mean(shaped, axis=-1, keepdims=True)
        - unit_rows * jnp.mean(shaped * unit_rows, axis=-1, keepdims=True)
    )


def in_order(which, mine, other, axis):
    return jnp.where(
        which == 0,
        jnp.concatenate([mine, other], axis=axis),
        jnp.concatenate([other, mine], axis=axis),
    )


def halving(value, device):
    bits = lax.axis_size("dp").bit_length() - 1
    rows, columns = value.shape
    current = value
    for bit in range(bits):
        upper = device // (1 << bit) % 2
        left = bits - bit
        view = current.reshape((1 << (left - 1), 2, -1, columns))
        kept = lax.dynamic_index_in_dim(view, upper, 1, keepdims=False)
        sent = lax.dynamic_index_in_dim(view, 1 - upper, 1, keepdims=False)
        got = flip(sent, "dp", bit)
        current = (kept.astype(F32) + got.astype(F32)).astype(BF)
    return current.reshape(rows >> bits, columns)


def side_by_side(parts):
    total = sum(part.shape[0] for part in parts)
    row, at = jnp.zeros((total,), F32), 0
    for part in parts:
        size = part.shape[0]
        row = row + jnp.pad(part.astype(F32), (at, total - at - size))
        at += size
    return row[None]


def half_of(value, which):
    prompt, conts = CHUNK // 2, (value.shape[0] - CHUNK) // 2
    return jnp.concatenate(
        [
            lax.dynamic_slice_in_dim(value, which * prompt, prompt),
            lax.dynamic_slice_in_dim(value, CHUNK + which * conts, conts),
        ]
    )


def joined(which, mine, other):
    prompt = CHUNK // 2
    low = jnp.where(which == 0, mine, other)
    high = jnp.where(which == 0, other, mine)
    return jnp.concatenate([low[:prompt], high[:prompt], low[prompt:], high[prompt:]])


def body(
    hidden_in,
    cotangent,
    prompt_start,
    cont_gap,
    seg_len,
    dilation_rate,
    pre_gain,
    pre_bias,
    query_weight,
    query_bias,
    key_weight,
    value_weight,
    value_bias,
    sub_gain,
    sub_bias,
    out_weight,
    out_bias,
    mid_gain,
    mid_bias,
    inner_weight,
    inner_bias,
    ffn_gain,
    ffn_bias,
    outer_weight,
    outer_bias,
):
    device = lax.axis_index("dp")
    ranks = lax.axis_size("dp")
    group_id = device // GDEV
    member = device % GDEV
    tensor_id = lax.axis_index("tensor")
    core = device % 2
    width = query_weight.shape[1]
    units = inner_weight.shape[1]
    pairs = width // 128
    rows = hidden_in.shape[0]
    prompt_rows = CHUNK
    cont_count = (rows - prompt_rows) // CONT

    vectors = side_by_side(
        [
            pre_gain,
            pre_bias,
            query_bias,
            value_bias,
            ffn_gain,
            ffn_bias,
            inner_bias,
            sub_gain,
            sub_bias,
            out_bias,
            mid_gain,
            mid_bias,
            outer_bias,
        ]
    )
    pre_gain_f = pre_gain.astype(F32)

    (
        weighed,
        inverse,
        queries,
        keys,
        values,
        prompt_keys,
        prompt_values,
        attended,
        att_mine,
        att_got,
        *pieces,
        vectors_other,
    ) = attend(
        prompt_start,
        cont_gap,
        seg_len.T,
        dilation_rate.T,
        hidden_in,
        vectors,
        query_weight,
        key_weight,
        value_weight,
        inner_weight,
        out_weight,
        outer_weight,
    )
    inner_parts = (inner_weight, pieces[0], pieces[1])
    out_parts = (out_weight, pieces[2], pieces[3])
    outer_parts = (outer_weight, pieces[4], pieces[5])

    fused = ranks == 16
    out_half, grad_mine, grad_theirs, grad_mixed_low, packed, sum_u, sum_w, sum_d, ext = middle(
        att_mine,
        att_got,
        hidden_in,
        cotangent,
        vectors,
        vectors_other,
        inner_parts,
        outer_parts,
        out_parts,
        ranks if fused else 1,
    )

    grad_query_in, own_key_grad, own_value_grad, key_sum, value_sum, relay, out_got, *early = attend_back(
        queries,
        keys,
        values,
        prompt_keys,
        prompt_values,
        attended,
        inverse,
        weighed,
        grad_mine,
        grad_theirs,
        out_half,
        packed.reshape(2, 2, 2, 2, D // ranks, -1) if fused else None,
    )
    if not fused:
        early = lax.psum_scatter(packed, "dp", scatter_dimension=0, tiled=True)
        early_mine, early_other = jnp.split(early, 2, axis=1)
        early_sum = early_mine.astype(F32) + flip(early_other, "tensor", 0).astype(F32)
    output = joined(tensor_id, out_half, out_got)
    block = D // ranks
    per_u, per_w, per_d = units // ranks, width // ranks, D // ranks
    if fused:
        input_low, late, vec, early_sum = finish(
            hidden_in,
            vectors,
            grad_query_in,
            own_key_grad,
            own_value_grad,
            query_weight,
            key_weight,
            value_weight,
            grad_mixed_low,
            ext,
            key_sum,
            value_sum,
            relay,
            *early,
            packed.reshape(2, 2, 2, 2, D // ranks, -1),
        )
        ffn_gain_grad, ffn_bias_grad, inner_bias_grad = [vec[i, :per_u] for i in range(3)]
        sub_gain_grad, sub_bias_grad = [vec[8 + i, :per_w] for i in range(2)]
        out_bias_grad, mid_gain_grad, mid_bias_grad, outer_bias_grad = [vec[16 + i, :per_d] for i in range(4)]
        query_bias_grad, value_bias_grad = [vec[24 + i, :per_w] for i in range(2)]
        pre_gain_grad, pre_bias_grad = [vec[26 + i, :per_d] for i in range(2)]
    else:
        pre_normed, pre_unit, pre_scale = norm_rows(hidden_in.astype(F32), pre_gain_f, pre_bias.astype(F32))
        pre_low = pre_normed.astype(BF)
        last = width - 128
        far = flip(relay, "dp", 1).astype(F32)
        summed = jnp.stack([key_sum, value_sum]).astype(F32)
        summed = jnp.concatenate([summed[:, :, :last], summed[:, :, last:] + far], axis=2).astype(BF)
        grad_keys = jnp.concatenate([summed[0], own_key_grad[prompt_rows:]], axis=0)
        grad_values = jnp.concatenate([summed[1], own_value_grad[prompt_rows:]], axis=0)

        query_weight_grad = contract_rows(pre_low, grad_query_in)
        key_weight_grad = contract_rows(pre_low, grad_keys)
        value_weight_grad = contract_rows(pre_low, grad_values)
        query_bias_grad = jnp.sum(grad_query_in.astype(F32), axis=0)
        value_bias_grad = jnp.sum(grad_values.astype(F32), axis=0)
        grad_normed_part = (
            back_project(grad_query_in, query_weight)
            + back_project(grad_keys, key_weight)
            + back_project(grad_values, value_weight)
        )
        grad_normed_low = grad_normed_part.astype(BF)
        grad_normed = grad_normed_low.astype(F32) + flip(grad_normed_low, "tensor", 0).astype(F32)
        pre_gain_grad = jnp.sum(grad_normed * pre_unit, axis=0)
        pre_bias_grad = jnp.sum(grad_normed, axis=0)
        grad_mixed_all = joined(tensor_id, grad_mixed_low, flip(grad_mixed_low, "tensor", 0)).astype(F32)
        input_low = (grad_mixed_all + norm_back(grad_normed, pre_gain_f, pre_unit, pre_scale)).astype(BF)

        vec = jnp.concatenate(
            [
                sum_u[:3].reshape(3, 2, ranks, per_u).transpose(2, 1, 0, 3).reshape(ranks, 6 * per_u),
                sum_w[:2].reshape(2, 2, ranks, per_w).transpose(2, 1, 0, 3).reshape(ranks, 4 * per_w),
                sum_d[:4].reshape(4, ranks, per_d).swapaxes(0, 1).reshape(ranks, 4 * per_d),
                jnp.stack([query_bias_grad, value_bias_grad]).reshape(2, ranks, per_w).swapaxes(0, 1).reshape(ranks, 2 * per_w),
                jnp.stack([pre_gain_grad, pre_bias_grad]).reshape(2, ranks, per_d).swapaxes(0, 1).reshape(ranks, 2 * per_d),
            ],
            axis=1,
        )
        count = vec.shape[1]
        vec = jnp.pad(vec, ((0, 0), (0, block * 128 - count))).reshape(D, 128)
        late = halving(
            jnp.concatenate(
                [p.astype(BF) for p in (query_weight_grad, key_weight_grad, value_weight_grad, vec)], axis=1
            ),
            device,
        )
        vec = late[:, 3 * width :].reshape(-1)[:count]
        late = late[:, : 3 * width].astype(F32)
        at_w = 6 * per_u
        at_d = at_w + 4 * per_w
        at_late = at_d + 4 * per_d
        got = flip(vec[:at_late], "tensor", 0).astype(F32)
        vec = vec.astype(F32)
        ffn_gain_grad, ffn_bias_grad, inner_bias_grad = (vec[: 3 * per_u] + got[3 * per_u : at_w]).reshape(3, per_u)
        sub_gain_grad, sub_bias_grad = (vec[at_w : at_w + 2 * per_w] + got[at_w + 2 * per_w : at_d]).reshape(2, per_w)
        out_bias_grad, mid_gain_grad, mid_bias_grad, outer_bias_grad = (vec[at_d:at_late] + got[at_d:]).reshape(4, per_d)
        query_bias_grad, value_bias_grad = vec[at_late : at_late + 2 * per_w].reshape(2, per_w)
        pre_gain_grad, pre_bias_grad = vec[at_late + 2 * per_w :].reshape(2, per_d)
    inner_weight_grad = early_sum[:, :units]
    outer_weight_grad = early_sum[:, units : 2 * units].T
    out_weight_grad = early_sum[:, 2 * units :].T
    return (
        output,
        input_low,
        pre_gain_grad,
        pre_bias_grad,
        late[:, :width],
        query_bias_grad,
        late[:, width : 2 * width],
        late[:, 2 * width : 3 * width],
        value_bias_grad,
        sub_gain_grad,
        sub_bias_grad,
        out_weight_grad,
        out_bias_grad,
        mid_gain_grad,
        mid_bias_grad,
        inner_weight_grad,
        inner_bias_grad,
        ffn_gain_grad,
        ffn_bias_grad,
        outer_weight_grad,
        outer_bias_grad,
    )

def solution(mesh):
    placed = (
        P("dp", None),
        P("dp", None),
        P(),
        P(),
        P(),
        P(),
        P(),
        P(),
        P(None, "tensor"),
        P("tensor"),
        P(None, "tensor"),
        P(None, "tensor"),
        P("tensor"),
        P("tensor"),
        P("tensor"),
        P("tensor", None),
        P(),
        P(),
        P(),
        P(None, "tensor"),
        P("tensor"),
        P("tensor"),
        P("tensor"),
        P("tensor", None),
        P(),
    )
    return jax.shard_map(
        body,
        mesh=mesh,
        in_specs=placed,
        out_specs=(
            P("dp", None),
            P("dp", None),
            P("dp"),
            P("dp"),
            P("dp", "tensor"),
            P(("tensor", "dp")),
            P("dp", "tensor"),
            P("dp", "tensor"),
            P(("tensor", "dp")),
            P(("tensor", "dp")),
            P(("tensor", "dp")),
            P("tensor", "dp"),
            P("dp"),
            P("dp"),
            P("dp"),
            P("dp", "tensor"),
            P(("tensor", "dp")),
            P(("tensor", "dp")),
            P(("tensor", "dp")),
            P("tensor", "dp"),
            P("dp"),
        ),
        check_vma=False,
    )
```

```python
import functools

import jax
import jax.numpy as jnp
from jax import lax
from jax.experimental import pallas as pl
from jax.experimental.pallas import tpu as pltpu
from jax.sharding import PartitionSpec as P

HD = 64
PROMPT = 2048
CONT = 256
GDEV = 4
TILE = 256
CHUNK = PROMPT // GDEV
PTILES = CHUNK // TILE
LOG2E = 1.4426950408889634
BF = jnp.bfloat16
F32 = jnp.float32
D = 768
EPSILON = 1e-05
MESH = pl.DeviceIdType.MESH


def dot_nt(a, b):
    return lax.dot_general(a, b, (((1,), (1,)), ((), ())), preferred_element_type=F32)


def dot_nn(a, b):
    return lax.dot_general(a, b, (((1,), (0,)), ((), ())), preferred_element_type=F32)


def low_half(rows):
    return lax.broadcasted_iota(jnp.int32, (rows, 128), 1) < HD


MASKED = -1e30
CLASSES = 36


def lane_classes(head):
    lane = lax.broadcasted_iota(jnp.int32, (8, 128), 1) - (HD if head == 0 else 0)
    number = lane.astype(F32)
    main = lane < CLASSES
    number = jnp.where(main, number, 4.0 * (number - CLASSES) + 3.0)
    number = jnp.where((lane >= 0) & (lane < CLASSES + CLASSES // 4), number, -5.0)
    combo = jnp.floor((number + 0.5) * 0.25)
    step0 = jnp.floor((combo + 0.5) * (1.0 / 3.0))
    step1 = combo - 3.0 * step0
    rest = number - 4.0 * combo
    flag1 = jnp.where(rest > 1.5, 1.0, 0.0)
    return number, step0, step1, flag1, rest - 2.0 * flag1, jnp.where(main, 0.0, 1.0)


def key_side(keys, first, cells, classes):
    size = keys.shape[0]
    at = first + lax.broadcasted_iota(jnp.int32, (8, size), 1).astype(F32)
    base = jnp.full((8, size), 0.0, F32) + first
    row = lax.broadcasted_iota(jnp.int32, (8, size), 0)

    def cell(i):
        return cells[i][:, 0:1]

    step0 = jnp.floor((at + 0.5) * cell(0)) - jnp.floor((base + 0.5) * cell(0))
    step1 = jnp.floor((at + 0.5) * cell(1)) - jnp.floor((base + 0.5) * cell(1))
    rest1 = at - cell(2) * jnp.floor((at + 0.5) * cell(3))
    rest2 = at - cell(4) * jnp.floor((at + 0.5) * cell(5))
    flag1 = jnp.where(rest1 == jnp.where(row == 0, cell(6), cell(7)), 2.0, 0.0)
    flag2 = jnp.where(rest2 == jnp.where(row == 0, cell(8), cell(9)), 1.0, 0.0)
    columns = jnp.transpose(4.0 * (3.0 * step0 + step1) + flag1 + flag2)
    low = low_half(size)
    hot = [jnp.where(columns[:, h : h + 1] == classes[h][0][0:1], 1.0, 0.0).astype(BF) for h in range(2)]
    return [jnp.where(low, keys, hot[0]), jnp.where(low, hot[1], keys)]


def query_side(head, queries, qc, first, cells, lanes, low):
    _, step0, step1, flag1, flag2, small = lanes
    base = jnp.zeros((8, 128), F32) + first
    kc0 = (jnp.floor((base + 0.5) * cells[0]) + step0)[0:1]
    kc1 = jnp.where(flag1 > 0.5, jnp.floor((base + 0.5) * cells[1]) + step1, -1.0)[0:1]
    weight = jnp.where(qc[0] == kc0, 1.0, 0.0) + jnp.where(qc[1 + head] == kc1, 1.0, 0.0)
    weight = weight + qc[3 + head] * flag2[0:1]
    logs = jnp.maximum(jnp.log2(weight), MASKED)
    logs = jnp.where(small[0:1] > 0.5, logs - logs.astype(BF).astype(F32), logs).astype(BF)
    return jnp.where(low, queries, logs) if head == 0 else jnp.where(low, logs, queries)


def settings(seg, rate, pair):
    def row(value):
        return jnp.full((1, 128), value, jnp.int32).astype(F32)

    def rest(number, period):
        return number - period * jnp.floor((number + 0.5) / period)

    second, third = row(rate[1, pair]), row(rate[2, pair])
    head = row(2 * pair)
    return (
        1.0 / row(seg[0, pair]),
        1.0 / row(seg[1, pair]),
        second,
        1.0 / second,
        third,
        1.0 / third,
        rest(head, second),
        rest(head + 1.0, second),
        rest(head, third),
        rest(head + 1.0, third),
    )


def codes(at, cells, miss):
    first = jnp.floor((at + 0.5) * cells[0])
    second = jnp.floor((at + 0.5) * cells[1])
    rest1 = at - cells[2] * jnp.floor((at + 0.5) * cells[3])
    rest2 = at - cells[4] * jnp.floor((at + 0.5) * cells[5])
    return [
        first,
        jnp.where(rest1 == cells[6], second, miss),
        jnp.where(rest1 == cells[7], second, miss),
        jnp.where(rest2 == cells[8], 1.0, 0.0),
        jnp.where(rest2 == cells[9], 1.0, 0.0),
    ]


def bit_peer(device, bit):
    step = 1 << bit
    return device + (1 - 2 * ((device // step) % 2)) * step


def greet(peers):
    barrier = pltpu.get_barrier_semaphore()
    for peer in peers:
        pl.semaphore_signal(barrier, inc=1, device_id=peer, device_id_type=MESH)
    pl.semaphore_wait(barrier, len(peers))


def xor_bits(a, b):
    return (a % 2 + b % 2) % 2 + 2 * ((a // 2 + b // 2) % 2)


def fwd_kernel(
    starts, gaps, seg, rate, hid, vec, wq, wk, wv, w1, wo, w2, vec_hbm,
    e_ref, li_ref, q_out, k_out, v_out, kp_out, vp_out, o_out, mine_out, got_out,
    w1_got, w1_swap, wo_got, wo_swap, w2_got, w2_swap, vec_got,
    t_s, ka_s, kv_s, low_s, q_s, qe_s, ko_s, vo_s, o_s, sems_a, sems_b, loc_sems,
):
    pair = pl.program_id(0)
    step = pl.program_id(1)
    pairs = pl.num_programs(0)
    device = lax.axis_index("dp")
    side = lax.axis_index("tensor")
    member = device % GDEV
    core = device % 2
    rows, width = q_s.shape
    n_pairs = width // 128
    last_pair = n_pairs - 1
    conts = rows - CHUNK
    near = {"dp": bit_peer(device, 0), "tensor": side}
    far = {"dp": bit_peer(device, 1), "tensor": side}
    across = {"dp": device, "tensor": 1 - side}
    half_u = w1.shape[1] // 2
    half_w = wo.shape[0] // 2
    half_p, half_c = CHUNK // 2, conts // 2
    sent_u = pl.multiple_of(core * half_u, 128)
    shared_at = 2 * D + 2 * width
    sent_w = pl.multiple_of(core * half_w, 64)

    def remote(i, src, dst, peer):
        return pltpu.make_async_remote_copy(
            src_ref=src, dst_ref=dst, send_sem=sems_a.at[i], recv_sem=sems_b.at[i], device_id=peer, device_id_type=MESH
        )

    def to_far(p):
        lanes = pl.ds(p * 128, 128)
        return remote(3 * p, kv_s.at[0, :, :, lanes], kv_s.at[2, :, :, lanes], far)

    def to_near(p):
        lanes = pl.ds(p * 128, 128)
        return remote(3 * p + 1, kv_s.at[0, :, :, lanes], kv_s.at[1, :, :, lanes], near)

    def relay(p):
        lanes = pl.ds(p * 128, 128)
        return remote(3 * p + 2, kv_s.at[2, :, :, lanes], kv_s.at[3, :, :, lanes], near)

    base = 3 * n_pairs
    fetch_y = [
        remote(base, wo.at[pl.ds(sent_w, half_w), :], wo_got, across),
        remote(base + 1, w1.at[:, pl.ds(sent_u, half_u)], w1_got, across),
        remote(base + 2, vec_hbm.at[:, pl.ds(shared_at, vec_got.shape[1])], vec_got, across),
        remote(base + 3, w2.at[pl.ds(sent_u, half_u // 2), :], w2_got, across),
    ]
    fetch_core = [
        remote(base + 4, wo_got, wo_swap, near),
        remote(base + 5, w1_got, w1_swap, near),
        remote(base + 6, w2_got, w2_swap, near),
    ]

    def give(p, piece):
        lanes = pl.ds(p * 128, 128)
        their_p = pl.multiple_of((1 - side) * half_p, 128)
        their_c = pl.multiple_of(CHUNK + (1 - side) * half_c, 128)
        third = half_c // 3
        if piece == 0:
            source, target = pl.ds(their_p, half_p), pl.ds(0, half_p)
        else:
            source = pl.ds(pl.multiple_of(their_c + (piece - 1) * third, 128), third)
            target = pl.ds(half_p + (piece - 1) * third, third)
        return remote(base + 7 + 4 * p + piece, o_s.at[source, lanes], got_out.at[target, lanes], across)

    def keeps():
        own_p = pl.multiple_of(side * half_p, 128)
        own_c = pl.multiple_of(CHUNK + side * half_c, 128)
        return [
            pltpu.make_async_copy(o_s, o_out, loc_sems.at[0]),
            pltpu.make_async_copy(o_s.at[pl.ds(own_p, half_p), :], mine_out.at[pl.ds(0, half_p), :], loc_sems.at[1]),
            pltpu.make_async_copy(o_s.at[pl.ds(own_c, half_c), :], mine_out.at[pl.ds(half_p, half_c), :], loc_sems.at[2]),
        ]

    def saves():
        out = [
            pltpu.make_async_copy(q_s, q_out, loc_sems.at[3]),
            pltpu.make_async_copy(ko_s, k_out, loc_sems.at[0]),
            pltpu.make_async_copy(vo_s, v_out, loc_sems.at[5]),
        ]
        for r in range(GDEV):
            span = pl.ds(r * CHUNK, CHUNK)
            out.append(pltpu.make_async_copy(kv_s.at[r, 0], kp_out.at[span, :], loc_sems.at[6 + 2 * r]))
            out.append(pltpu.make_async_copy(kv_s.at[r, 1], vp_out.at[span, :], loc_sems.at[7 + 2 * r]))
        return out

    @pl.when((pair == 0) & (step == 0))
    def _():
        greet([near, far, across])
        for copy in fetch_y:
            copy.start()
        gain_f, bias_f = vec[:, pl.ds(0, D)], vec[:, pl.ds(D, D)]
        query_bias = vec[:, pl.ds(2 * D, width)]
        value_bias = vec[:, pl.ds(2 * D + width, width)]

        def norm(at, size):
            x = hid[at : at + size, :].astype(F32)
            center = jnp.mean(x, axis=1, keepdims=True)
            scale = lax.rsqrt(jnp.mean(x * x, axis=1, keepdims=True) - center * center + EPSILON)
            low = ((x - center) * scale * gain_f + bias_f).astype(BF)
            low_s[at : at + size, :] = low
            return low

        low = norm(0, CHUNK)
        kv_s[0, 0] = dot_nn(low, wk[...]).astype(BF)
        kv_s[0, 1] = (dot_nn(low, wv[...]) + value_bias).astype(BF)
        to_far(0).start()
        for p in range(n_pairs):
            to_near(p).start()
        for at in range(CHUNK, rows, TILE):
            low = norm(at, TILE)
            ko_s[at - CHUNK : at - CHUNK + TILE, :] = dot_nn(low, wk[...]).astype(BF)
            vo_s[at - CHUNK : at - CHUNK + TILE, :] = (dot_nn(low, wv[...]) + value_bias).astype(BF)
        to_far(0).wait_send()
        for p in range(1, n_pairs):
            to_far(p).start()
        for at in range(0, rows, TILE):
            scaled = (dot_nn(low_s[at : at + TILE, :], wq[...]) + query_bias) * 0.125
            q_s[at : at + TILE, :] = scaled.astype(BF)
            qe_s[at : at + TILE, :] = (scaled * LOG2E).astype(BF)
        to_far(0).wait_recv()
        relay(0).start()

    for p in range(n_pairs):
        @pl.when((pair == p) & (step == 0))
        def _():
            to_near(p).wait_recv()
            relay(p).wait_recv()

        if p + 1 < n_pairs:
            @pl.when((pair == p) & (step == 3))
            def _():
                to_far(p + 1).wait_recv()
                relay(p + 1).start()

    lanes = pl.ds(pl.multiple_of(pair * 128, 128), 128)
    low = low_half(TILE)
    q = qe_s[pl.ds(pl.multiple_of(step * TILE, TILE), TILE), lanes]
    row = lax.broadcasted_iota(jnp.int32, (TILE, 128), 0).astype(F32)
    group = device // GDEV
    start = starts[group]
    first_cont = member * (conts // CONT)
    own_gap = gaps[group, first_cont + jnp.maximum(step - PTILES, 0)]
    base_q = start + jnp.where(step < PTILES, member * CHUNK + step * TILE, PROMPT + own_gap)
    cells = settings(seg, rate, side * n_pairs + pair)
    at_q = base_q.astype(F32) + row
    qc = codes(at_q, cells, -2.0)
    classes = [lane_classes(h) for h in range(2)]
    first_at = start.astype(F32)

    @pl.when(step == 0)
    def _():
        for j in range(GDEV):
            first = first_at + (xor_bits(j, member) * CHUNK).astype(F32)
            for h, made in enumerate(key_side(kv_s[j, 0, :, lanes], first, cells, classes)):
                ka_s[h, j * CHUNK : (j + 1) * CHUNK, :] = made

    def logits(h, top, keys, first, causal, at, width):
        t = dot_nt(query_side(h, q, qc, first, cells, classes[h], low), keys)
        if causal is not None:
            t = jnp.where(causal, t, MASKED)
        t_s[h, :, pl.ds(at, width)] = t
        for g in range(width // 128):
            top = jnp.maximum(top, t[:, g * 128 : (g + 1) * 128])
        return top

    def weigh(h, carry, vals, m, at, width):
        total, acc = carry
        parts = []
        for g in range(width // 128):
            e = jnp.exp2(t_s[h, :, pl.ds(at + g * 128, 128)] - m)
            total = total + e
            parts.append(e.astype(BF))
        el = jnp.concatenate(parts, axis=1)
        e_ref[h, :, pl.ds(at, width)] = el
        return total, acc + dot_nn(el, vals)

    def finish_rows(carry):
        (sums0, acc0), (sums1, acc1) = carry
        sums, accs = (sums0, sums1), (acc0, acc1)
        li = [1.0 / jnp.sum(s, axis=1, keepdims=True) for s in sums]
        lfull = jnp.where(low, li[0], li[1])
        li_ref[...] = lfull
        o_s[pl.ds(pl.multiple_of(step * TILE, TILE), TILE), lanes] = (jnp.where(low, accs[0], accs[1]) * lfull).astype(BF)

    def tops(mx):
        return jnp.broadcast_to(jnp.max(mx, axis=1, keepdims=True), (TILE, 128))

    neg = jnp.full((TILE, 128), -jnp.inf, F32)
    zf = jnp.zeros((TILE, 128), F32)

    def held_keys(h, at):
        return ka_s[h, pl.ds(at, CHUNK), :]

    @pl.when(step < PTILES)
    def _():
        rows_id = lax.broadcasted_iota(jnp.int32, (TILE, CHUNK), 0) + step * TILE
        cols = lax.broadcasted_iota(jnp.int32, (TILE, CHUNK), 1)
        here = first_at + (member * CHUNK).astype(F32)

        def place(j):
            return pl.multiple_of(xor_bits(j, member) * CHUNK, CHUNK)

        def score(h, j, top):
            return logits(h, top, held_keys(h, place(j)), first_at + (j * CHUNK).astype(F32), None, place(j), CHUNK)

        def spread(h, j, m, carry):
            return weigh(h, carry, kv_s[xor_bits(j, member), 1, :, lanes], m, place(j), CHUNK)

        top = lax.fori_loop(0, member, lambda j, top: score(0, j, top), neg)
        m0 = tops(logits(0, top, held_keys(0, 0), here, cols <= rows_id, 0, CHUNK))

        def both(j, carry):
            return spread(0, j, m0, carry[0]), score(1, j, carry[1])

        first, top = lax.fori_loop(0, member, both, ((zf, zf), neg))
        first = weigh(0, first, kv_s[0, 1, :, lanes], m0, 0, CHUNK)
        m1 = tops(logits(1, top, held_keys(1, 0), here, cols <= rows_id, 0, CHUNK))
        finish_rows((first, lax.fori_loop(0, member + 1, lambda j, carry: spread(1, j, m1, carry), (zf, zf))))

    @pl.when(step >= PTILES)
    def _():
        own_rows = pl.ds(pl.multiple_of((step - PTILES) * TILE, TILE), TILE)
        rows_id = lax.broadcasted_iota(jnp.int32, (TILE, CONT), 0)
        cols = lax.broadcasted_iota(jnp.int32, (TILE, CONT), 1)
        own_at = base_q.astype(F32)
        own = key_side(ko_s[own_rows, lanes], own_at, cells, classes)

        def score(h, j, top):
            if j == GDEV:
                return logits(h, top, own[h], own_at, cols <= rows_id, PROMPT, CONT)
            first = first_at + (xor_bits(j, member) * CHUNK).astype(F32)
            return logits(h, top, held_keys(h, j * CHUNK), first, None, j * CHUNK, CHUNK)

        def spread(h, j, m, carry):
            if j == GDEV:
                return weigh(h, carry, vo_s[own_rows, lanes], m, PROMPT, CONT)
            return weigh(h, carry, kv_s[j, 1, :, lanes], m, j * CHUNK, CHUNK)

        top = neg
        for j in range(GDEV + 1):
            top = score(0, j, top)
        m0, top, first, second = tops(top), neg, (zf, zf), (zf, zf)
        for j in range(GDEV + 1):
            first = spread(0, j, m0, first)
            top = score(1, j, top)
        m1 = tops(top)
        for j in range(GDEV + 1):
            second = spread(1, j, m1, second)
        finish_rows((first, second))

    end = pl.num_programs(1) - 1
    for p in range(n_pairs):
        @pl.when((pair == p) & (step == 1 - side))
        def _():
            give(p, 0).start()

        for unit in range(6):
            @pl.when((pair == p) & (step == PTILES + unit // 2) & (side == 1 - unit // 3))
            def _():
                give(p, 1 + unit % 3).start()

    @pl.when((pair == last_pair - 1) & (step == 3))
    def _():
        for i in range(2):
            fetch_y[i].wait_recv()
            fetch_core[i].start()

    @pl.when((pair == last_pair) & (step == 3))
    def _():
        fetch_y[3].wait_recv()
        fetch_core[2].start()

    @pl.when((pair == last_pair) & (step == 0))
    def _():
        for copy in saves():
            copy.start()

    @pl.when((pair == last_pair) & (step == end))
    def _():
        for copy in keeps():
            copy.start()
        fetch_y[2].wait_recv()
        for copy in fetch_core:
            copy.wait_recv()
        for p in range(n_pairs):
            for piece in range(4):
                copy = give(p, piece)
                copy.wait_recv()
                copy.wait_send()
            if p > 0:
                to_far(p).wait_send()
            to_near(p).wait_send()
            relay(p).wait_send()
        for copy in fetch_y + fetch_core:
            copy.wait_send()
        for copy in keeps() + saves():
            copy.wait()


def attend(starts, gaps, seg, rate, hid, vec, wq, wk, wv, w1, wo, w2):
    rows = hid.shape[0]
    width = wq.shape[1]
    pairs = width // 128
    span = PROMPT + CONT
    conts = rows - CHUNK
    units = w1.shape[1]
    vmem = pl.BlockSpec(memory_space=pltpu.VMEM)
    hbm = pl.BlockSpec(memory_space=pl.ANY)
    shape = jax.ShapeDtypeStruct
    copies = 3 * pairs + 7 + 4 * pairs
    shared = 3 * units + 2 * width
    smem = pl.BlockSpec(memory_space=pltpu.SMEM)
    return pl.pallas_call(
        fwd_kernel,
        grid_spec=pltpu.PrefetchScalarGridSpec(
            num_scalar_prefetch=0,
            grid=(pairs, rows // TILE),
            in_specs=[smem] * 4 + [vmem] * 5 + [hbm] * 4,
            out_specs=[
                pl.BlockSpec((2, TILE, span), lambda a, t: (a, t, 0)),
                pl.BlockSpec((TILE, 128), lambda a, t: (t, a)),
            ]
            + [hbm] * 15,
            scratch_shapes=[
                pltpu.VMEM((2, TILE, span), F32),
                pltpu.VMEM((2, PROMPT, 128), BF),
                pltpu.VMEM((GDEV, 2, CHUNK, width), BF),
                pltpu.VMEM((rows, D), BF),
                pltpu.VMEM((rows, width), BF),
                pltpu.VMEM((rows, width), BF),
                pltpu.VMEM((conts, width), BF),
                pltpu.VMEM((conts, width), BF),
                pltpu.VMEM((rows, width), BF),
                pltpu.SemaphoreType.DMA((copies,)),
                pltpu.SemaphoreType.DMA((copies,)),
                pltpu.SemaphoreType.DMA((6 + 2 * GDEV,)),
            ],
        ),
        out_shape=[
            shape((2 * pairs, rows, span), BF),
            shape((rows, width), F32),
            shape((rows, width), BF),
            shape((conts, width), BF),
            shape((conts, width), BF),
            shape((PROMPT, width), BF),
            shape((PROMPT, width), BF),
            shape((rows, width), BF),
            shape((rows // 2, width), BF),
            shape((rows // 2, width), BF),
            shape((D, units // 2), BF),
            shape((D, units // 2), BF),
            shape((width // 2, D), BF),
            shape((width // 2, D), BF),
            shape((units // 4, D), BF),
            shape((units // 4, D), BF),
            shape((1, shared), F32),
        ],
        compiler_params=pltpu.CompilerParams(vmem_limit_bytes=56 << 20, collective_id=0, has_side_effects=True),
        cost_estimate=pl.CostEstimate(flops=20 * 10**9, bytes_accessed=60 * 10**6, transcendentals=0),
        name="attend",
    )(starts, gaps, seg, rate, hid, vec, wq, wk, wv, w1, wo, w2, vec)


EARLY = 2
FIRST_CUT = 1920


def reducer_scratch(count, block, cut):
    return [
        pltpu.VMEM((count, 2, 2, 2, block, cut), BF),
        pltpu.VMEM((count, 2, 2, 2, block, cut), BF),
        pltpu.VMEM((count, 2, 2, block, cut), BF),
        pltpu.VMEM((count, 2, 2, block, cut), BF),
        pltpu.VMEM((count, 2, block, cut), BF),
        pltpu.VMEM((count, 2, block, cut), BF),
        pltpu.VMEM((count, block, cut), BF),
        pltpu.SemaphoreType.DMA((4 * count,)),
        pltpu.SemaphoreType.DMA((4 * count,)),
        pltpu.SemaphoreType.DMA((count,)),
    ]


def reducer(packed, device, side, base, refs, done):
    held, got0, got1, held1, got2, held2, got3, sems_a, sems_b, sems_l = refs
    bit = [(device // (1 << b)) % 2 for b in range(4)]
    peers = [{"dp": bit_peer(device, b), "tensor": side} for b in range(4)]
    cut = held.shape[-1]

    def passing(c, stage, source, target, peer):
        return pltpu.make_async_remote_copy(
            src_ref=source,
            dst_ref=target,
            send_sem=sems_a.at[4 * c + stage],
            recv_sem=sems_b.at[4 * c + stage],
            device_id=peer,
            device_id_type=MESH,
        )

    count = held.shape[0]

    def columns_of(c, first):
        return pl.ds(first + (count - 1 - c) * cut, cut)

    def own_half(c):
        return pltpu.make_async_copy(packed.at[:, :, :, bit[0], :, columns_of(c, base)], held.at[c], sems_l.at[c])

    def stage0(c):
        return passing(c, 0, packed.at[:, :, :, 1 - bit[0], :, columns_of(c, base)], got0.at[c], peers[0])

    def stage1(c):
        if c % 2:
            return passing(c, 1, held.at[c, :, 1 - bit[2]], got1.at[c], peers[2])
        return passing(c, 1, held.at[c, :, :, 1 - bit[1]], got1.at[c], peers[1])

    def stage2(c):
        b = 1 if c % 2 else 2
        return passing(c, 2, held1.at[c, :, 1 - bit[b]], got2.at[c], peers[b])

    def stage3(c):
        return passing(c, 3, held2.at[c, 1 - bit[3]], got3.at[c], peers[3])

    def begin(c):
        own_half(c).start()
        stage0(c).start()

    def after0(c):
        own_half(c).wait()
        stage0(c).wait_recv()
        held[c] = held[c] + got0[c]
        stage1(c).start()

    def after1(c):
        stage1(c).wait_recv()
        kept = held[c, :, bit[2]] if c % 2 else held[c, :, :, bit[1]]
        held1[c] = kept + got1[c]
        stage2(c).start()

    def after2(c):
        stage2(c).wait_recv()
        held2[c] = held1[c, :, bit[1 if c % 2 else 2]] + got2[c]
        stage3(c).start()

    def after3(c):
        stage3(c).wait_recv()
        done[:, columns_of(c, 0)] = held2[c, bit[3]] + got3[c]

    def settle():
        for c in range(count):
            for copy in (stage0(c), stage1(c), stage2(c), stage3(c)):
                copy.wait_send()

    return begin, after0, after1, after2, after3, settle


def tile_at(step, last):
    side = lax.axis_index("tensor")
    prompt = (step + side) % PTILES
    conts = (1 - side) * step + side * (PTILES + last - step)
    return jnp.where(step < PTILES, prompt, conts)


def bwd_kernel(
    fused, q_ref, kp_ref, vp_ref, ko_ref, vo_ref, o_ref, li_ref, e_ref, g_mine, g_theirs, out_half, *refs
):
    packed = refs[0] if fused else None
    refs = refs[1:] if fused else refs
    dq_ref, dko_ref, dvo_ref, sum_k, sum_v, relay_out, out_got = refs[:7]
    done_out, other_out = refs[7:9] if fused else (None, None)
    refs = refs[9:] if fused else refs[7:]
    dk_s, dv_s, g_s, grad_s, near_s, relay_s, far_s, sems_a, sems_b, loc_sems = refs[:10]
    pair = pl.program_id(0)
    step = pl.program_id(1)
    tile = tile_at(step, pl.num_programs(1) - 1)
    device = lax.axis_index("dp")
    side = lax.axis_index("tensor")
    member = device % GDEV
    rows, width = g_s.shape
    n_pairs = width // 128
    conts = rows - CHUNK
    half_p, half_c = CHUNK // 2, conts // 2
    near = {"dp": bit_peer(device, 0), "tensor": side}
    far = {"dp": bit_peer(device, 1), "tensor": side}
    across = {"dp": device, "tensor": 1 - side}
    lanes = pl.ds(pl.multiple_of(pair * 128, 128), 128)
    mine_p = pl.ds(pl.multiple_of(side * half_p, 128), half_p)
    mine_c = pl.ds(pl.multiple_of(CHUNK + side * half_c, 128), half_c)

    def remote(i, src, dst, peer):
        return pltpu.make_async_remote_copy(
            src_ref=src, dst_ref=dst, send_sem=sems_a.at[i], recv_sem=sems_b.at[i], device_id=peer, device_id_type=MESH
        )

    def heads():
        return [
            remote(0, g_theirs.at[pl.ds(0, half_p), :], g_s.at[mine_p, :], across),
            remote(1, g_theirs.at[pl.ds(half_p, half_c), :], g_s.at[mine_c, :], across),
            remote(2, out_half, out_got, across),
        ]

    def local():
        return [
            pltpu.make_async_copy(g_mine.at[pl.ds(0, half_p), :], g_s.at[mine_p, :], loc_sems.at[0]),
            pltpu.make_async_copy(g_mine.at[pl.ds(half_p, half_c), :], g_s.at[mine_c, :], loc_sems.at[1]),
        ]

    def cores(p):
        part = pl.ds(p * 128, 128)
        return remote(3 + 2 * p, grad_s.at[:, :, 1, :, part], near_s.at[:, :, :, part], near)

    def chips(p):
        part = pl.ds(p * 128, 128)
        return remote(4 + 2 * p, relay_s.at[:, :, part], far_s.at[:, :, part], far)

    if fused:
        *early_refs, done_s, other_a, early_sems = refs[10:]
        begin, after0, after1, after2, after3, settle = reducer(
            packed, device, side, packed.shape[-1] - EARLY * FIRST_CUT, early_refs, done_s
        )
        half_e = packed.shape[-1] // 2
        tail_e = EARLY * FIRST_CUT - half_e
        peers = [{"dp": bit_peer(device, b), "tensor": side} for b in range(4)]
        swap = pltpu.make_async_remote_copy(
            src_ref=done_s.at[:, pl.ds(tail_e, half_e)],
            dst_ref=other_a,
            send_sem=early_sems.at[0],
            recv_sem=early_sems.at[1],
            device_id=across,
            device_id_type=MESH,
        )
        tick = pair * pl.num_programs(1) + step

    @pl.when((pair == 0) & (step == 0))
    def _():
        greet([near, far, across] + (peers[2:] if fused else []))
        for copy in heads() + local():
            copy.start()
        for copy in local():
            copy.wait()

    if fused:
        for c in range(EARLY):
            for at, act in ((0, begin), (1 + c, after0), (5 + c, after1), (8 + c, after2), (12, after3)):
                @pl.when(tick == at)
                def _():
                    act(c)

        @pl.when(tick == 12)
        def _():
            swap.start()

    @pl.when((pair == 0) & (step == 1))
    def _():
        heads()[0].wait_recv()

    @pl.when((pair == 0) & (step == 3))
    def _():
        heads()[1].wait_recv()

    low = low_half(TILE)
    g = g_s[pl.ds(pl.multiple_of(tile * TILE, TILE), TILE), lanes].astype(F32) * li_ref[...]
    prod = g * o_ref[...].astype(F32)
    zf = jnp.zeros((TILE, 128), F32)
    deltas = [
        jnp.sum(jnp.where(low, prod, zf), axis=1, keepdims=True),
        jnp.sum(jnp.where(low, zf, prod), axis=1, keepdims=True),
    ]
    gs = [jnp.where(low, g, zf).astype(BF), jnp.where(low, zf, g).astype(BF)]
    gt = jnp.transpose(g).astype(BF)
    qt = jnp.transpose(q_ref[...].astype(F32)).astype(BF)

    def grads(dq, keys, vals, at, width):
        out, dks, dvs = [], [], []
        for h in range(2):
            e = e_ref[h, :, pl.ds(at, width)]
            dp = dot_nt(gs[h], vals)
            ds = (e.astype(F32) * (dp - deltas[h])).astype(BF)
            out.append(dq[h] + dot_nn(ds, keys))
            dks.append(dot_nn(qt[h * HD : (h + 1) * HD, :], ds))
            dvs.append(dot_nn(gt[h * HD : (h + 1) * HD, :], e))
        return tuple(out), dks, dvs

    @pl.when(step == 0)
    def _():
        dk_s[...] = jnp.zeros_like(dk_s)
        dv_s[...] = jnp.zeros_like(dv_s)

    def add(at, width, dks, dvs):
        for h in range(2):
            dk_s[h * HD : (h + 1) * HD, pl.ds(at, width)] += dks[h]
            dv_s[h * HD : (h + 1) * HD, pl.ds(at, width)] += dvs[h]

    def scaled(dq):
        return (jnp.where(low, dq[0], dq[1]).astype(BF).astype(F32) * 0.125).astype(BF)

    @pl.when(step < PTILES)
    def _():
        def one(j, dq):
            at = pl.multiple_of(xor_bits(j, member) * CHUNK, CHUNK)
            dq, dks, dvs = grads(dq, kp_ref[pl.ds(at, CHUNK), :], vp_ref[pl.ds(at, CHUNK), :], at, CHUNK)
            add(at, CHUNK, dks, dvs)
            return dq

        dq_ref[...] = scaled(lax.fori_loop(0, member + 1, one, (zf, zf)))
        dko_ref[...] = jnp.zeros_like(dko_ref)
        dvo_ref[...] = jnp.zeros_like(dvo_ref)

    @pl.when(step >= PTILES)
    def _():
        dq = (zf, zf)
        for j in range(GDEV):
            span = slice(j * CHUNK, (j + 1) * CHUNK)
            dq, dks, dvs = grads(dq, kp_ref[span, :], vp_ref[span, :], j * CHUNK, CHUNK)
            add(j * CHUNK, CHUNK, dks, dvs)
        dq, dks, dvs = grads(dq, ko_ref[...], vo_ref[...], PROMPT, CONT)
        dq_ref[...] = scaled(dq)
        dko_ref[...] = jnp.transpose(jnp.concatenate(dks, axis=0)).astype(BF)
        dvo_ref[...] = jnp.transpose(jnp.concatenate(dvs, axis=0)).astype(BF)

    end = pl.num_programs(1) - 1

    @pl.when(step == end)
    def _():
        for j in range(GDEV):
            span = slice(j * CHUNK, (j + 1) * CHUNK)
            grad_s[0, j // 2, j % 2, :, lanes] = jnp.transpose(dk_s[:, span]).astype(BF)
            grad_s[1, j // 2, j % 2, :, lanes] = jnp.transpose(dv_s[:, span]).astype(BF)

    for p in range(n_pairs):
        @pl.when((pair == p) & (step == end))
        def _():
            cores(p).start()

        if p + 1 < n_pairs:
            @pl.when((pair == p + 1) & (step == 2))
            def _():
                part = pl.ds(p * 128, 128)
                cores(p).wait_recv()
                relay_s[:, :, part] = (
                    grad_s[:, 1, 0, :, part].astype(F32) + near_s[:, 1, :, part].astype(F32)
                ).astype(BF)
                chips(p).start()

    @pl.when((pair == n_pairs - 1) & (step == end))
    def _():
        last = n_pairs - 1
        sums = (sum_k, sum_v)
        for p in range(last):
            part = pl.ds(p * 128, 128)
            chips(p).wait_recv()
            for i in range(2):
                sums[i][:, part] = (
                    grad_s[i, 0, 0, :, part].astype(F32) + near_s[i, 0, :, part].astype(F32) + far_s[i, :, part].astype(F32)
                ).astype(BF)
        part = pl.ds(last * 128, 128)
        cores(last).wait_recv()
        for i in range(2):
            relay_out[i] = (grad_s[i, 1, 0, :, part].astype(F32) + near_s[i, 1, :, part].astype(F32)).astype(BF)
            sums[i][:, part] = (grad_s[i, 0, 0, :, part].astype(F32) + near_s[i, 0, :, part].astype(F32)).astype(BF)
        if fused:
            swap.wait_recv()
            done_out[...] = done_s[:, pl.ds(0, tail_e)]
            other_out[...] = other_a[...]
            settle()
            swap.wait_send()
        heads()[2].wait_recv()
        for copy in heads():
            copy.wait_send()
        for p in range(n_pairs):
            cores(p).wait_send()
            if p < last:
                chips(p).wait_send()


def attend_back(q, k, v, kp, vp, o, li, e, g_mine, g_theirs, out_half, packed):
    rows, width = q.shape
    pairs = width // 128
    span = PROMPT + CONT
    last = rows // TILE - 1
    tile = pl.BlockSpec((TILE, 128), lambda a, t: (tile_at(t, last), a))
    whole = pl.BlockSpec((PROMPT, 128), lambda a, t: (0, a))
    own = pl.BlockSpec((TILE, 128), lambda a, t: (jnp.maximum(tile_at(t, last) - PTILES, 0), a))
    vmem = pl.BlockSpec(memory_space=pltpu.VMEM)
    hbm = pl.BlockSpec(memory_space=pl.ANY)
    shape = jax.ShapeDtypeStruct
    copies = 3 + 2 * pairs
    fused = packed is not None
    more_in, more_out, more_scratch = [], [], []
    if fused:
        block, half_e = packed.shape[-2], packed.shape[-1] // 2
        more_in = [packed]
        more_out = [shape((block, EARLY * FIRST_CUT - half_e), BF), shape((block, half_e), BF)]
        more_scratch = reducer_scratch(EARLY, block, FIRST_CUT) + [
            pltpu.VMEM((block, EARLY * FIRST_CUT), BF),
            pltpu.VMEM((block, half_e), BF),
            pltpu.SemaphoreType.DMA((2,)),
        ]
    return pl.pallas_call(
        functools.partial(bwd_kernel, fused),
        grid=(pairs, rows // TILE),
        in_specs=[tile, whole, whole, own, own, tile, tile, pl.BlockSpec((2, TILE, span), lambda a, t: (a, tile_at(t, last), 0))]
        + [hbm] * (3 + len(more_in)),
        out_specs=[tile, tile, tile, vmem, vmem, vmem, hbm] + [vmem] * len(more_out),
        out_shape=[
            shape((rows, width), BF),
            shape((rows, width), BF),
            shape((rows, width), BF),
            shape((CHUNK, width), BF),
            shape((CHUNK, width), BF),
            shape((2, CHUNK, 128), BF),
            shape(out_half.shape, BF),
        ]
        + more_out,
        scratch_shapes=[
            pltpu.VMEM((128, PROMPT), F32),
            pltpu.VMEM((128, PROMPT), F32),
            pltpu.VMEM((rows, width), BF),
            pltpu.VMEM((2, 2, 2, CHUNK, width), BF),
            pltpu.VMEM((2, 2, CHUNK, width), BF),
            pltpu.VMEM((2, CHUNK, width), BF),
            pltpu.VMEM((2, CHUNK, width), BF),
            pltpu.SemaphoreType.DMA((copies,)),
            pltpu.SemaphoreType.DMA((copies,)),
            pltpu.SemaphoreType.DMA((2,)),
        ]
        + more_scratch,
        compiler_params=pltpu.CompilerParams(vmem_limit_bytes=60 << 20, collective_id=2, has_side_effects=True),
        cost_estimate=pl.CostEstimate(flops=30 * 10**9, bytes_accessed=60 * 10**6, transcendentals=0),
        name="attend_back",
    )(q, kp, vp, k, v, o, li, e, g_mine, g_theirs, out_half, *more_in)


UCH = 768


def polynomial(x, terms):
    out = jnp.full_like(x, terms[0])
    for term in terms[1:]:
        out = out * x + term
    return out


def gelu_pair(v):
    bell = jnp.exp(-0.5 * v * v)
    t = 1.0 / (1.0 + (0.3275911 * 0.7071067811865476) * jnp.abs(v))
    terms = (0.5307027145, -0.7265760135, 0.7107068705, -0.142248368, 0.127414796)
    half = polynomial(t, terms) * t * bell
    phi = jnp.where(v < 0.0, half, 1.0 - half)
    return v * phi, phi + v * (bell * 0.3989422804014327)


def column_sum(x):
    return jnp.sum(x, axis=0, keepdims=True)


def mid_kernel(
    att_m, att_o, vec_all, vec_got, hid_all, cot_all, w1_own, w1_got, w1_swap, wo_own, wo_got, wo_swap, w2_own, w2_got, w2_swap,
    out_ref, gatt_m, gatt_o, gmix_ref, packed, su_ref, sw_ref, sd_ref, ext_ref,
    vec_u, vec_w, w1, w2, wo, act_s, shp_s, dg_s, wide_s, acc_s, gmid_s, sub_s, mid_s, low_s, midt_s, cott_s, stage, hid, cot, sems, out_sems, send_sems, recv_sems,
):
    device = lax.axis_index("dp")
    side = lax.axis_index("tensor")
    core = device % 2
    near = {"dp": bit_peer(device, 0), "tensor": side}
    across = {"dp": device, "tensor": 1 - side}
    units = w1_own.shape[1]
    width = wo_own.shape[0]
    rows = hid.shape[0]
    full = 2 * units
    half = units // 2
    half_w = width // 2
    here_u = pl.multiple_of(units + core * half, 128)
    there_u = pl.multiple_of(units + (1 - core) * half, 128)
    here_w = pl.multiple_of(width + core * half_w, 64)
    there_w = pl.multiple_of(width + (1 - core) * half_w, 64)
    prompt, conts = CHUNK // 2, (hid_all.shape[0] - CHUNK) // 2
    own_p = pl.ds(pl.multiple_of(side * prompt, 128), prompt)
    own_c = pl.ds(pl.multiple_of(CHUNK + side * conts, 128), conts)
    at_own = 2 * D + 2 * width
    vec_own = vec_all.at[:, pl.ds(at_own, 3 * units + 2 * width)]
    vec_d = vec_all.at[:, pl.ds(at_own + 3 * units + 2 * width, 4 * D)]
    rows_in = []
    for i, (all_rows, held) in enumerate(((hid_all, hid), (cot_all, cot))):
        for j, (span, at, size) in enumerate(((own_p, 0, prompt), (own_c, prompt, conts))):
            copy = pltpu.make_async_copy(all_rows.at[span, :], held.at[pl.ds(at, size), :], sems.at[9 + 2 * i + j])
            copy.start()
            rows_in.append(copy)
    loads = []
    for i, (src, dst) in enumerate(
        [
            (wo_own, wo.at[pl.ds(0, width), :]),
            (wo_got, wo.at[pl.ds(here_w, half_w), :]),
            (wo_swap, wo.at[pl.ds(there_w, half_w), :]),
            (w1_own, w1.at[:, pl.ds(0, units)]),
            (w1_got, w1.at[:, pl.ds(here_u, half)]),
            (w1_swap, w1.at[:, pl.ds(there_u, half)]),
            (w2_own, w2.at[pl.ds(0, units), :]),
            (w2_got, w2.at[pl.ds(here_u, half // 2), :]),
            (w2_swap, w2.at[pl.ds(there_u, half // 2), :]),
        ]
    ):
        copy = pltpu.make_async_copy(src, dst, sems.at[i])
        copy.start()
        loads.append(copy)

    piece = half // 2
    greet([near, across])

    def remote(i, src, dst, peer):
        return pltpu.make_async_remote_copy(
            src_ref=src, dst_ref=dst, send_sem=send_sems.at[i], recv_sem=recv_sems.at[i], device_id=peer, device_id_type=MESH
        )

    from_own = pl.ds(pl.multiple_of(core * half + piece, 128), piece)
    landed = w2.at[pl.ds(pl.multiple_of(units + core * half + piece, 128), piece), :]
    over = remote(0, w2_own.at[from_own, :], landed, across)
    passed = remote(1, landed, landed, near)
    over.start()

    for i in range(3):
        for j, vec in enumerate((vec_own, vec_got)):
            vec_u[i : i + 1, pl.ds(j * units, units)] = vec[0:1, pl.ds(i * units, units)]
    for i in range(2):
        for j, vec in enumerate((vec_own, vec_got)):
            vec_w[i : i + 1, pl.ds(j * width, width)] = vec[0:1, pl.ds(3 * units + i * width, width)]

    a0 = att_m[...].astype(F32)
    a1 = att_o[...].astype(F32)
    center = (jnp.sum(a0, axis=1, keepdims=True) + jnp.sum(a1, axis=1, keepdims=True)) * (1.0 / D)
    square = (jnp.sum(a0 * a0, axis=1, keepdims=True) + jnp.sum(a1 * a1, axis=1, keepdims=True)) * (1.0 / D)
    sub_scale = lax.rsqrt(square - center * center + EPSILON)
    sub_s[:, 0:width] = (a0 - center) * sub_scale
    sub_s[:, width : 2 * width] = (a1 - center) * sub_scale
    sub_gain = vec_w[0:1, :]
    low_s[...] = (sub_s[...] * sub_gain + vec_w[1:2, :]).astype(BF)
    for copy in loads[0:3] + rows_in:
        copy.wait()
    mixed = hid[...].astype(F32) + (dot_nn(low_s[...], wo[...]) + vec_d[0:1, pl.ds(0, D)])
    wide_s[...] = mixed
    mean = jnp.mean(mixed, axis=1, keepdims=True)
    mid_scale = lax.rsqrt(jnp.mean(mixed * mixed, axis=1, keepdims=True) - mean * mean + EPSILON)
    mid_s[...] = (mixed - mean) * mid_scale
    mid_gain = vec_d[0:1, pl.ds(768, D)]
    mid_full = mid_s[...] * mid_gain + vec_d[0:1, pl.ds(1536, D)]
    mid_low = mid_full.astype(BF)
    midt_s[...] = jnp.transpose(mid_full).astype(BF)
    cot_full = cot[...].astype(F32)
    cott_s[...] = jnp.transpose(cot_full).astype(BF)
    sd_ref[...] = jnp.zeros_like(sd_ref)
    sd_ref[3:4, :] = column_sum(cot_full)
    for copy in loads[3:6]:
        copy.wait()

    def unrolled(low, high, step, carry):
        for c in range(low, high):
            carry = step(c, carry)
        return carry

    def lanes_sum(x):
        total = x[:, 0:128]
        for i in range(1, x.shape[1] // 128):
            total = total + x[:, i * 128 : (i + 1) * 128]
        return total

    zero = jnp.zeros((rows, 128), F32)
    act_sum, act_square = zero, zero

    def inner_of(c):
        at = c * UCH
        shp_s[:, at : at + UCH] = dot_nn(mid_low, w1[:, at : at + UCH]) + vec_u[2:3, at : at + UCH]

    inner_of(0)
    for c in range(full // UCH):
        at = c * UCH
        if c + 1 < full // UCH:
            inner_of(c + 1)
        act, slope = gelu_pair(shp_s[:, at : at + UCH])
        act_s[:, at : at + UCH] = act
        dg_s[:, at : at + UCH] = slope.astype(BF)
        act_sum, act_square = act_sum + lanes_sum(act), act_square + lanes_sum(act * act)
    ffn_center = jnp.sum(act_sum, axis=1, keepdims=True) * (1.0 / full)
    ffn_scale = lax.rsqrt(
        jnp.sum(act_square, axis=1, keepdims=True) * (1.0 / full) - ffn_center * ffn_center + EPSILON
    )
    for copy in loads[6:9]:
        copy.wait()
    over.wait_recv()
    passed.start()
    acc_s[...] = jnp.zeros_like(acc_s)
    per = units // UCH
    wide = 2 * units + width

    def column_of(c, extra):
        return pl.multiple_of((c // per) * wide + (c % per) * UCH + extra, 128)

    def send(slot, column):
        return pltpu.make_async_copy(stage.at[slot], packed.at[:, pl.ds(column, UCH)], out_sems.at[slot])

    def put(c, value, extra):
        slot = c % 2

        @pl.when(c >= 2)
        def _():
            send(slot, column_of(c - 2, extra)).wait()

        stage[slot] = value
        send(slot, column_of(c, extra)).start()

    def drain(extra):
        for c in range(full // UCH - 2, full // UCH):
            send(c % 2, column_of(c, extra)).wait()

    def second(c, carry):
        at = pl.multiple_of(c * UCH, UCH)
        unit = (act_s[:, pl.ds(at, UCH)] - ffn_center) * ffn_scale
        act_s[:, pl.ds(at, UCH)] = unit
        gain = vec_u[0:1, pl.ds(at, UCH)]
        low = (unit * gain + vec_u[1:2, pl.ds(at, UCH)]).astype(BF)
        acc_s[...] += dot_nn(low, w2[pl.ds(at, UCH), :])
        grad = dot_nt(cot[...], w2[pl.ds(at, UCH), :])
        cross = grad * unit
        su_ref[0:1, pl.ds(at, UCH)] = column_sum(cross)
        su_ref[1:2, pl.ds(at, UCH)] = column_sum(grad)
        shaped = grad * gain
        shp_s[:, pl.ds(at, UCH)] = shaped
        put(c, dot_nn(cott_s[...], low).astype(BF), units)
        return carry[0] + lanes_sum(shaped), carry[1] + lanes_sum(shaped * unit)

    su_ref[...] = jnp.zeros_like(su_ref)
    sums = unrolled(0, per, second, (zero, zero))
    passed.wait_recv()
    s_sum, s_cross = unrolled(per, 2 * per, second, sums)
    drain(units)
    shaped_mean = jnp.sum(s_sum, axis=1, keepdims=True) * (1.0 / full)
    cross_mean = jnp.sum(s_cross, axis=1, keepdims=True) * (1.0 / full)
    out_ref[...] = (wide_s[...] + (acc_s[...] + vec_d[0:1, pl.ds(2304, D)])).astype(BF)
    gmid_s[...] = jnp.zeros_like(gmid_s)

    def third(c, carry):
        at = pl.multiple_of(c * UCH, UCH)
        g = ffn_scale * (shp_s[:, pl.ds(at, UCH)] - shaped_mean - act_s[:, pl.ds(at, UCH)] * cross_mean)
        low = (g * dg_s[:, pl.ds(at, UCH)].astype(F32)).astype(BF)
        su_ref[2:3, pl.ds(at, UCH)] = column_sum(low.astype(F32))
        gmid_s[...] += dot_nt(low, w1[:, pl.ds(at, UCH)])
        put(c, dot_nn(midt_s[...], low).astype(BF), 0)
        return carry

    unrolled(0, 2 * per, third, 0)
    drain(0)

    grad_mid = gmid_s[...]
    unit = mid_s[...]
    sd_ref[1:2, :] = column_sum(grad_mid * unit)
    sd_ref[2:3, :] = column_sum(grad_mid)
    shaped = grad_mid * mid_gain
    grad_mixed = cot[...].astype(F32) + mid_scale * (
        shaped - jnp.mean(shaped, axis=1, keepdims=True) - unit * jnp.mean(shaped * unit, axis=1, keepdims=True)
    )
    branch = grad_mixed.astype(BF)
    gmix_ref[...] = branch
    branch_f = branch.astype(F32)
    sd_ref[0:1, :] = column_sum(branch_f)
    out_grad = dot_nn(jnp.transpose(branch_f).astype(BF), low_s[...]).astype(BF)
    stage[0, :, 0:width] = out_grad[:, 0:width]
    stage[1, :, 0:width] = out_grad[:, width : 2 * width]
    last = [
        pltpu.make_async_copy(stage.at[i, :, pl.ds(0, width)], packed.at[:, pl.ds(i * wide + 2 * units, width)], out_sems.at[i])
        for i in range(2)
    ]
    for copy in last:
        copy.start()
    grad_sub = dot_nt(branch, wo[...])
    unit = sub_s[...]
    cross = grad_sub * unit
    sw_ref[...] = jnp.zeros_like(sw_ref)
    sw_ref[0:1, :] = column_sum(cross)
    sw_ref[1:2, :] = column_sum(grad_sub)
    shaped = grad_sub * sub_gain
    grad_att = sub_scale * (
        shaped - jnp.mean(shaped, axis=1, keepdims=True) - unit * jnp.mean(shaped * unit, axis=1, keepdims=True)
    )
    gatt_m[...] = grad_att[:, 0:width].astype(BF)
    gatt_o[...] = grad_att[:, width : 2 * width].astype(BF)
    parts = ext_ref.shape[0]
    if parts > 1:
        sums_u, sums_w, sums_d = su_ref[...], sw_ref[...], sd_ref[...]
        for i in range(parts):
            ext_ref[i] = jnp.concatenate(
                [
                    window(sums_u, i * (units // parts)),
                    window(sums_u, units + i * (units // parts)),
                    window(sums_w, i * (width // parts)),
                    window(sums_w, width + i * (width // parts)),
                    window(sums_d, i * (D // parts)),
                    jnp.zeros((8, 128), F32),
                ],
                axis=0,
            ).astype(BF)
    for copy in last:
        copy.wait()
    over.wait_send()
    passed.wait_send()


def window(rows8, start):
    base = start // 128 * 128
    size = min(256, rows8.shape[1] - base)
    view = rows8[:, base : base + size]
    shift = start - base
    if shift:
        view = pltpu.roll(view, size - shift, 1)
    return view[:, 0:128]


def middle(att_m, att_o, hid, cot, vec_all, vec_got, w1, w2, wo, parts):
    rows = att_m.shape[0]
    units = w2[0].shape[0]
    width = wo[0].shape[0]
    vmem = pl.BlockSpec(memory_space=pltpu.VMEM)
    hbm = pl.BlockSpec(memory_space=pl.ANY)
    shape = jax.ShapeDtypeStruct
    return pl.pallas_call(
        mid_kernel,
        in_specs=[vmem] * 4 + [hbm] * 11,
        out_specs=[vmem] * 4 + [hbm] + [vmem] * 4,
        out_shape=[
            shape((rows, D), BF),
            shape((rows, width), BF),
            shape((rows, width), BF),
            shape((rows, D), BF),
            shape((D, 2 * (2 * units + width)), BF),
            shape((8, 2 * units), F32),
            shape((8, 2 * width), F32),
            shape((8, D), F32),
            shape((parts, 48, 128), BF),
        ],
        scratch_shapes=[
            pltpu.VMEM((8, 2 * units), F32),
            pltpu.VMEM((8, 2 * width), F32),
            pltpu.VMEM((D, 2 * units), BF),
            pltpu.VMEM((2 * units, D), BF),
            pltpu.VMEM((2 * width, D), BF),
            pltpu.VMEM((rows, 2 * units), F32),
            pltpu.VMEM((rows, 2 * units), F32),
            pltpu.VMEM((rows, 2 * units), BF),
            pltpu.VMEM((rows, D), F32),
            pltpu.VMEM((rows, D), F32),
            pltpu.VMEM((rows, D), F32),
            pltpu.VMEM((rows, 2 * width), F32),
            pltpu.VMEM((rows, D), F32),
            pltpu.VMEM((rows, 2 * width), BF),
            pltpu.VMEM((D, rows), BF),
            pltpu.VMEM((D, rows), BF),
            pltpu.VMEM((2, D, UCH), BF),
            pltpu.VMEM((rows, D), BF),
            pltpu.VMEM((rows, D), BF),
            pltpu.SemaphoreType.DMA((13,)),
            pltpu.SemaphoreType.DMA((2,)),
            pltpu.SemaphoreType.DMA((2,)),
            pltpu.SemaphoreType.DMA((2,)),
        ],
        compiler_params=pltpu.CompilerParams(vmem_limit_bytes=62 << 20, collective_id=3, has_side_effects=True),
        cost_estimate=pl.CostEstimate(flops=21 * 10**9, bytes_accessed=30 * 10**6, transcendentals=0),
        name="middle",
    )(att_m, att_o, vec_all, vec_got, hid, cot, *w1, *wo, *w2)


def final_kernel(
    bits, hid_all, vec_all, dq, dk, dv, wq, wk, wv, gmix_all, ext, sum_k, sum_v, relay, first_done, first_other, packed,
    gin, late_out, vec_out, early_out,
    loc_s, far_s, unit_s, mine_s, norm_s, send_c, recv_c, send_p, recv_p, give_c, give_p, late_s, small_s,
    vec_s, vec_r, done_s, hid, gmix, sems_a, sems_b, loc_sems, *stage_refs,
):
    device = lax.axis_index("dp")
    side = lax.axis_index("tensor")
    across = {"dp": device, "tensor": 1 - side}
    peers = [{"dp": bit_peer(device, b), "tensor": side} for b in range(bits)]
    rows, width = dq.shape
    prompt = sum_k.shape[0]
    conts = rows - prompt
    half_p, half_c = prompt // 2, conts // 2
    own_p = pl.multiple_of(side * half_p, 128)
    their_p = pl.multiple_of((1 - side) * half_p, 128)
    own_c = pl.multiple_of(prompt + side * half_c, 128)
    their_c = pl.multiple_of(prompt + (1 - side) * half_c, 128)
    lanes = 3 * width + 128

    brought = [
        pltpu.make_async_copy(hid_all, hid, loc_sems.at[2]),
        pltpu.make_async_copy(gmix_all, gmix, loc_sems.at[3]),
    ]
    for copy in brought:
        copy.start()
    greet(peers + [across])
    count = [0]

    def remote(src, dst, peer):
        i = count[0]
        count[0] += 1
        copy = pltpu.make_async_remote_copy(
            src_ref=src, dst_ref=dst, send_sem=sems_a.at[i], recv_sem=sems_b.at[i], device_id=peer, device_id_type=MESH
        )
        copy.start()
        return copy

    share = remote(relay, far_s, peers[1])

    begin, after0, after1, after2, after3, settle = reducer(packed, device, side, 0, stage_refs[-10:], done_s)

    def each(act):
        for c in range(EARLY):
            act(c)

    each(begin)

    gain_f = vec_all[:, pl.ds(0, D)]
    bias_f = vec_all[:, pl.ds(D, D)]

    def unit_rows(at, size):
        x = hid[pl.ds(at, size), :].astype(F32)
        center = jnp.mean(x, axis=1, keepdims=True)
        scale = lax.rsqrt(jnp.mean(x * x, axis=1, keepdims=True) - center * center + EPSILON)
        return (x - center) * scale, scale

    def part_of(at, size, k_rows, v_rows):
        return dot_nt(dq[pl.ds(at, size), :], wq[...]) + dot_nt(k_rows, wk[...]) + dot_nt(v_rows, wv[...])

    def gather(part, unit):
        return column_sum(part * unit), column_sum(part)

    def normed_rows(at, size, unit):
        norm_s[:, pl.ds(at, size)] = jnp.transpose(unit * gain_f + bias_f).astype(BF)

    part = part_of(their_c, half_c, dk[pl.ds(their_c, half_c), :], dv[pl.ds(their_c, half_c), :])
    send_c[...] = part.astype(BF)
    y_cont = remote(send_c, recv_c, across)
    for copy in brought:
        copy.wait()
    unit, _ = unit_rows(their_c, half_c)
    gain_grad, bias_grad = gather(part, unit)
    normed_rows(their_c, half_c, unit)
    unit, scale_c = unit_rows(own_c, half_c)
    part = part_of(own_c, half_c, dk[pl.ds(own_c, half_c), :], dv[pl.ds(own_c, half_c), :])
    mine_s[pl.ds(half_p, half_c), :] = part
    unit_s[pl.ds(half_p, half_c), :] = unit
    g, b = gather(part, unit)
    gain_grad, bias_grad = gain_grad + g, bias_grad + b
    normed_rows(own_c, half_c, unit)

    each(after0)
    share.wait_recv()
    for i, total in enumerate((sum_k, sum_v)):
        loc_s[i, :, pl.ds(0, width - 128)] = total[:, pl.ds(0, width - 128)]
        loc_s[i, :, pl.ds(width - 128, 128)] = (
            total[:, pl.ds(width - 128, 128)].astype(F32) + far_s[i].astype(F32)
        ).astype(BF)
    part = part_of(their_p, half_p, loc_s[0, pl.ds(their_p, half_p), :], loc_s[1, pl.ds(their_p, half_p), :])
    send_p[...] = part.astype(BF)
    y_prompt = remote(send_p, recv_p, across)
    unit, _ = unit_rows(their_p, half_p)
    normed_rows(their_p, half_p, unit)
    g, b = gather(part, unit)
    gain_grad, bias_grad = gain_grad + g, bias_grad + b
    unit, scale_p = unit_rows(own_p, half_p)
    unit_s[pl.ds(0, half_p), :] = unit
    normed_rows(own_p, half_p, unit)
    part = part_of(own_p, half_p, loc_s[0, pl.ds(own_p, half_p), :], loc_s[1, pl.ds(own_p, half_p), :])
    mine_s[pl.ds(0, half_p), :] = part
    g, b = gather(part, unit)
    gain_grad, bias_grad = gain_grad + g, bias_grad + b

    blocks = 1 << bits
    block = D // blocks

    def keep(value, lane):
        low = value.astype(BF)
        for i in range(blocks):
            late_s[i // 2, i % 2, :, pl.ds(lane, width)] = low[i * block : (i + 1) * block, :]

    keep(dot_nn(norm_s[...], dq[...]), 0)
    q_bias = column_sum(dq[...].astype(F32))
    for i, rest in enumerate((dk, dv)):
        keep(
            dot_nn(norm_s[:, pl.ds(0, prompt)], loc_s[i])
            + dot_nn(norm_s[:, pl.ds(prompt, conts)], rest[pl.ds(prompt, conts), :]),
            (i + 1) * width,
        )
    v_bias = column_sum(loc_s[1].astype(F32)) + column_sum(dv[pl.ds(prompt, conts), :].astype(F32))

    def norm_back(total, unit, scale, mixed):
        shaped = total * gain_f
        return mixed.astype(F32) + scale * (
            shaped - jnp.mean(shaped, axis=1, keepdims=True) - unit * jnp.mean(shaped * unit, axis=1, keepdims=True)
        )

    small_s[...] = jnp.zeros_like(small_s)
    small_s[0:1, pl.ds(0, width)] = q_bias
    small_s[1:2, pl.ds(0, width)] = v_bias
    small_s[2:3, pl.ds(0, D)] = gain_grad
    small_s[3:4, pl.ds(0, D)] = bias_grad
    small = small_s[...]
    row_id = lax.broadcasted_iota(jnp.int32, (8, 128), 0)
    for i in range(blocks):
        narrow = window(small, i * (width // blocks))
        broad = window(small, i * block)
        tail = jnp.concatenate([ext[i, pl.ds(32, 16), :].astype(F32)[0:8], jnp.where(row_id < 2, narrow, broad)], axis=0)
        late_s[i // 2, i % 2, pl.ds(0, 32), pl.ds(3 * width, 128)] = ext[i, pl.ds(0, 32), :]
        late_s[i // 2, i % 2, pl.ds(32, 16), pl.ds(3 * width, 128)] = tail.astype(BF)

    def input_rows(arrived, at, size, scale, held, rows_at, sem):
        arrived[0].wait_recv()
        here = pl.ds(at, size)
        total = mine_s[here, :] + arrived[1][...].astype(F32)
        held[...] = norm_back(total, unit_s[here, :], scale, gmix[here, :]).astype(BF)
        back = remote(held, gin.at[pl.ds(rows_at, size), :], across)
        kept = pltpu.make_async_copy(held, gin.at[pl.ds(rows_at, size), :], loc_sems.at[sem])
        kept.start()
        return back, kept

    source = late_s
    stages = []
    for bit in range(bits):
        landing, kept = stage_refs[2 * bit], stage_refs[2 * bit + 1]
        mine = (device // (1 << bit)) % 2
        copy = remote(source.at[:, 1 - mine], landing, peers[bit])
        if bit == 0:
            back_c, keep_c = input_rows((y_cont, recv_c), half_p, half_c, scale_c, give_c, own_c, 0)
        if bit == 1:
            each(after1)
            back_p, keep_p = input_rows((y_prompt, recv_p), 0, half_p, scale_p, give_p, own_p, 1)
        if bit == 2:
            each(after2)
        if bit == 3:
            each(after3)
        copy.wait_recv()
        stages.append(copy)
        for i in range(landing.shape[0]):
            kept[i // 2, i % 2] = (source[i, mine].astype(F32) + landing[i].astype(F32)).astype(BF)
        source = kept
    late_out[...] = source[0, 0, :, pl.ds(0, 3 * width)].astype(F32)
    vec_s[...] = source[0, 0, :, pl.ds(3 * width, 128)]
    swap = remote(vec_s, vec_r, across)
    last_e = done_s.shape[1]
    early_out[:, pl.ds(0, last_e)] = done_s[...].astype(F32) + first_other[:, pl.ds(0, last_e)].astype(F32)
    rest_e = first_done.shape[1]
    early_out[:, pl.ds(last_e, rest_e)] = first_done[...].astype(F32) + first_other[:, pl.ds(last_e, rest_e)].astype(F32)
    settle()
    swap.wait_recv()
    own_v, got_v = vec_s[...].astype(F32), vec_r[...].astype(F32)
    vec_out[0:8, :] = own_v[0:8] + got_v[8:16]
    vec_out[8:16, :] = own_v[16:24] + got_v[24:32]
    vec_out[16:24, :] = own_v[32:40] + got_v[32:40]
    vec_out[24:32, :] = own_v[40:48] + jnp.where(row_id < 2, 0.0, got_v[40:48])
    for copy in stages + [share, y_cont, y_prompt, swap]:
        copy.wait_send()
    for copy in (back_c, back_p):
        copy.wait_recv()
        copy.wait_send()
    keep_c.wait()
    keep_p.wait()


def finish(hid, vec_all, dq, dk, dv, wq, wk, wv, gmix, ext, sum_k, sum_v, relay, first_done, first_other, packed):
    rows, width = dq.shape
    ranks = lax.axis_size("dp")
    bits = ranks.bit_length() - 1
    block = D // ranks
    prompt = sum_k.shape[0]
    conts = rows - prompt
    lanes = 3 * width + 128
    vmem = pl.BlockSpec(memory_space=pltpu.VMEM)
    hbm = pl.BlockSpec(memory_space=pl.ANY)
    shape = jax.ShapeDtypeStruct
    copies = 6 + bits
    cut = (packed.shape[-1] - EARLY * FIRST_CUT) // EARLY
    stages = []
    for bit in range(bits):
        left = ranks >> (bit + 1)
        stages.append(pltpu.VMEM((left, block, lanes), BF))
        stages.append(pltpu.VMEM((max(left // 2, 1), min(left, 2), block, lanes), BF))
    return pl.pallas_call(
        functools.partial(final_kernel, bits),
        in_specs=[hbm, vmem, vmem, vmem, vmem, vmem, vmem, vmem, hbm, vmem, vmem, vmem, vmem, vmem, vmem, hbm],
        out_specs=[hbm, vmem, vmem, vmem],
        out_shape=[shape((rows, D), BF), shape((block, 3 * width), F32), shape((32, 128), F32), shape((block, packed.shape[-1] // 2), F32)],
        scratch_shapes=[
            pltpu.VMEM((2, prompt, width), BF),
            pltpu.VMEM((2, prompt, 128), BF),
            pltpu.VMEM((rows // 2, D), F32),
            pltpu.VMEM((rows // 2, D), F32),
            pltpu.VMEM((D, rows), BF),
            pltpu.VMEM((conts // 2, D), BF),
            pltpu.VMEM((conts // 2, D), BF),
            pltpu.VMEM((prompt // 2, D), BF),
            pltpu.VMEM((prompt // 2, D), BF),
            pltpu.VMEM((conts // 2, D), BF),
            pltpu.VMEM((prompt // 2, D), BF),
            pltpu.VMEM((ranks // 2, 2, block, lanes), BF),
            pltpu.VMEM((8, D + 128), F32),
            pltpu.VMEM((block, 128), BF),
            pltpu.VMEM((block, 128), BF),
            pltpu.VMEM((block, EARLY * cut), BF),
            pltpu.VMEM((rows, D), BF),
            pltpu.VMEM((rows // 2, D), BF),
            pltpu.SemaphoreType.DMA((copies,)),
            pltpu.SemaphoreType.DMA((copies,)),
            pltpu.SemaphoreType.DMA((4,)),
        ]
        + stages
        + reducer_scratch(EARLY, block, cut),
        compiler_params=pltpu.CompilerParams(vmem_limit_bytes=56 << 20, collective_id=1, has_side_effects=True),
        cost_estimate=pl.CostEstimate(flops=5 * 10**9, bytes_accessed=20 * 10**6, transcendentals=0),
        name="finish",
    )(hid, vec_all, dq, dk, dv, wq, wk, wv, gmix, ext, sum_k, sum_v, relay, first_done, first_other, packed)


def flip(value, axis, bit):
    return lax.ppermute(value, axis, [(i, i ^ (1 << bit)) for i in range(lax.axis_size(axis))])


def contract_rows(left, right):
    return lax.dot_general(left, right, (((0,), (0,)), ((), ())), preferred_element_type=F32)


def back_project(left, right):
    return lax.dot_general(left, right, (((1,), (1,)), ((), ())), preferred_element_type=F32)


def norm_rows(values, gain, bias):
    center = jnp.mean(values, axis=-1, keepdims=True)
    spread = jnp.mean(values * values, axis=-1, keepdims=True) - center * center
    scaled = lax.rsqrt(spread + EPSILON)
    unit_rows = (values - center) * scaled
    return (unit_rows * gain + bias, unit_rows, scaled)


def norm_back(grad_rows, gain, unit_rows, scaled):
    shaped = grad_rows * gain
    return scaled * (
        shaped
        - jnp.mean(shaped, axis=-1, keepdims=True)
        - unit_rows * jnp.mean(shaped * unit_rows, axis=-1, keepdims=True)
    )


def in_order(which, mine, other, axis):
    return jnp.where(
        which == 0,
        jnp.concatenate([mine, other], axis=axis),
        jnp.concatenate([other, mine], axis=axis),
    )


def halving(value, device):
    bits = lax.axis_size("dp").bit_length() - 1
    rows, columns = value.shape
    current = value
    for bit in range(bits):
        upper = device // (1 << bit) % 2
        left = bits - bit
        view = current.reshape((1 << (left - 1), 2, -1, columns))
        kept = lax.dynamic_index_in_dim(view, upper, 1, keepdims=False)
        sent = lax.dynamic_index_in_dim(view, 1 - upper, 1, keepdims=False)
        got = flip(sent, "dp", bit)
        current = (kept.astype(F32) + got.astype(F32)).astype(BF)
    return current.reshape(rows >> bits, columns)


def side_by_side(parts):
    total = sum(part.shape[0] for part in parts)
    row, at = jnp.zeros((total,), F32), 0
    for part in parts:
        size = part.shape[0]
        row = row + jnp.pad(part.astype(F32), (at, total - at - size))
        at += size
    return row[None]


def half_of(value, which):
    prompt, conts = CHUNK // 2, (value.shape[0] - CHUNK) // 2
    return jnp.concatenate(
        [
            lax.dynamic_slice_in_dim(value, which * prompt, prompt),
            lax.dynamic_slice_in_dim(value, CHUNK + which * conts, conts),
        ]
    )


def joined(which, mine, other):
    prompt = CHUNK // 2
    low = jnp.where(which == 0, mine, other)
    high = jnp.where(which == 0, other, mine)
    return jnp.concatenate([low[:prompt], high[:prompt], low[prompt:], high[prompt:]])


def body(
    hidden_in,
    cotangent,
    prompt_start,
    cont_gap,
    seg_len,
    dilation_rate,
    pre_gain,
    pre_bias,
    query_weight,
    query_bias,
    key_weight,
    value_weight,
    value_bias,
    sub_gain,
    sub_bias,
    out_weight,
    out_bias,
    mid_gain,
    mid_bias,
    inner_weight,
    inner_bias,
    ffn_gain,
    ffn_bias,
    outer_weight,
    outer_bias,
):
    device = lax.axis_index("dp")
    ranks = lax.axis_size("dp")
    group_id = device // GDEV
    member = device % GDEV
    tensor_id = lax.axis_index("tensor")
    core = device % 2
    width = query_weight.shape[1]
    units = inner_weight.shape[1]
    pairs = width // 128
    rows = hidden_in.shape[0]
    prompt_rows = CHUNK
    cont_count = (rows - prompt_rows) // CONT

    vectors = side_by_side(
        [
            pre_gain,
            pre_bias,
            query_bias,
            value_bias,
            ffn_gain,
            ffn_bias,
            inner_bias,
            sub_gain,
            sub_bias,
            out_bias,
            mid_gain,
            mid_bias,
            outer_bias,
        ]
    )
    pre_gain_f = pre_gain.astype(F32)

    (
        weighed,
        inverse,
        queries,
        keys,
        values,
        prompt_keys,
        prompt_values,
        attended,
        att_mine,
        att_got,
        *pieces,
        vectors_other,
    ) = attend(
        prompt_start,
        cont_gap,
        seg_len.T,
        dilation_rate.T,
        hidden_in,
        vectors,
        query_weight,
        key_weight,
        value_weight,
        inner_weight,
        out_weight,
        outer_weight,
    )
    inner_parts = (inner_weight, pieces[0], pieces[1])
    out_parts = (out_weight, pieces[2], pieces[3])
    outer_parts = (outer_weight, pieces[4], pieces[5])

    fused = ranks == 16
    out_half, grad_mine, grad_theirs, grad_mixed_low, packed, sum_u, sum_w, sum_d, ext = middle(
        att_mine,
        att_got,
        hidden_in,
        cotangent,
        vectors,
        vectors_other,
        inner_parts,
        outer_parts,
        out_parts,
        ranks if fused else 1,
    )

    grad_query_in, own_key_grad, own_value_grad, key_sum, value_sum, relay, out_got, *early = attend_back(
        queries,
        keys,
        values,
        prompt_keys,
        prompt_values,
        attended,
        inverse,
        weighed,
        grad_mine,
        grad_theirs,
        out_half,
        packed.reshape(2, 2, 2, 2, D // ranks, -1) if fused else None,
    )
    if not fused:
        early = lax.psum_scatter(packed, "dp", scatter_dimension=0, tiled=True)
        early_mine, early_other = jnp.split(early, 2, axis=1)
        early_sum = early_mine.astype(F32) + flip(early_other, "tensor", 0).astype(F32)
    output = joined(tensor_id, out_half, out_got)
    block = D // ranks
    per_u, per_w, per_d = units // ranks, width // ranks, D // ranks
    if fused:
        input_low, late, vec, early_sum = finish(
            hidden_in,
            vectors,
            grad_query_in,
            own_key_grad,
            own_value_grad,
            query_weight,
            key_weight,
            value_weight,
            grad_mixed_low,
            ext,
            key_sum,
            value_sum,
            relay,
            *early,
            packed.reshape(2, 2, 2, 2, D // ranks, -1),
        )
        ffn_gain_grad, ffn_bias_grad, inner_bias_grad = [vec[i, :per_u] for i in range(3)]
        sub_gain_grad, sub_bias_grad = [vec[8 + i, :per_w] for i in range(2)]
        out_bias_grad, mid_gain_grad, mid_bias_grad, outer_bias_grad = [vec[16 + i, :per_d] for i in range(4)]
        query_bias_grad, value_bias_grad = [vec[24 + i, :per_w] for i in range(2)]
        pre_gain_grad, pre_bias_grad = [vec[26 + i, :per_d] for i in range(2)]
    else:
        pre_normed, pre_unit, pre_scale = norm_rows(hidden_in.astype(F32), pre_gain_f, pre_bias.astype(F32))
        pre_low = pre_normed.astype(BF)
        last = width - 128
        far = flip(relay, "dp", 1).astype(F32)
        summed = jnp.stack([key_sum, value_sum]).astype(F32)
        summed = jnp.concatenate([summed[:, :, :last], summed[:, :, last:] + far], axis=2).astype(BF)
        grad_keys = jnp.concatenate([summed[0], own_key_grad[prompt_rows:]], axis=0)
        grad_values = jnp.concatenate([summed[1], own_value_grad[prompt_rows:]], axis=0)

        query_weight_grad = contract_rows(pre_low, grad_query_in)
        key_weight_grad = contract_rows(pre_low, grad_keys)
        value_weight_grad = contract_rows(pre_low, grad_values)
        query_bias_grad = jnp.sum(grad_query_in.astype(F32), axis=0)
        value_bias_grad = jnp.sum(grad_values.astype(F32), axis=0)
        grad_normed_part = (
            back_project(grad_query_in, query_weight)
            + back_project(grad_keys, key_weight)
            + back_project(grad_values, value_weight)
        )
        grad_normed_low = grad_normed_part.astype(BF)
        grad_normed = grad_normed_low.astype(F32) + flip(grad_normed_low, "tensor", 0).astype(F32)
        pre_gain_grad = jnp.sum(grad_normed * pre_unit, axis=0)
        pre_bias_grad = jnp.sum(grad_normed, axis=0)
        grad_mixed_all = joined(tensor_id, grad_mixed_low, flip(grad_mixed_low, "tensor", 0)).astype(F32)
        input_low = (grad_mixed_all + norm_back(grad_normed, pre_gain_f, pre_unit, pre_scale)).astype(BF)

        vec = jnp.concatenate(
            [
                sum_u[:3].reshape(3, 2, ranks, per_u).transpose(2, 1, 0, 3).reshape(ranks, 6 * per_u),
                sum_w[:2].reshape(2, 2, ranks, per_w).transpose(2, 1, 0, 3).reshape(ranks, 4 * per_w),
                sum_d[:4].reshape(4, ranks, per_d).swapaxes(0, 1).reshape(ranks, 4 * per_d),
                jnp.stack([query_bias_grad, value_bias_grad]).reshape(2, ranks, per_w).swapaxes(0, 1).reshape(ranks, 2 * per_w),
                jnp.stack([pre_gain_grad, pre_bias_grad]).reshape(2, ranks, per_d).swapaxes(0, 1).reshape(ranks, 2 * per_d),
            ],
            axis=1,
        )
        count = vec.shape[1]
        vec = jnp.pad(vec, ((0, 0), (0, block * 128 - count))).reshape(D, 128)
        late = halving(
            jnp.concatenate(
                [p.astype(BF) for p in (query_weight_grad, key_weight_grad, value_weight_grad, vec)], axis=1
            ),
            device,
        )
        vec = late[:, 3 * width :].reshape(-1)[:count]
        late = late[:, : 3 * width].astype(F32)
        at_w = 6 * per_u
        at_d = at_w + 4 * per_w
        at_late = at_d + 4 * per_d
        got = flip(vec[:at_late], "tensor", 0).astype(F32)
        vec = vec.astype(F32)
        ffn_gain_grad, ffn_bias_grad, inner_bias_grad = (vec[: 3 * per_u] + got[3 * per_u : at_w]).reshape(3, per_u)
        sub_gain_grad, sub_bias_grad = (vec[at_w : at_w + 2 * per_w] + got[at_w + 2 * per_w : at_d]).reshape(2, per_w)
        out_bias_grad, mid_gain_grad, mid_bias_grad, outer_bias_grad = (vec[at_d:at_late] + got[at_d:]).reshape(4, per_d)
        query_bias_grad, value_bias_grad = vec[at_late : at_late + 2 * per_w].reshape(2, per_w)
        pre_gain_grad, pre_bias_grad = vec[at_late + 2 * per_w :].reshape(2, per_d)
    inner_weight_grad = early_sum[:, :units]
    outer_weight_grad = early_sum[:, units : 2 * units].T
    out_weight_grad = early_sum[:, 2 * units :].T
    return (
        output,
        input_low,
        pre_gain_grad,
        pre_bias_grad,
        late[:, :width],
        query_bias_grad,
        late[:, width : 2 * width],
        late[:, 2 * width : 3 * width],
        value_bias_grad,
        sub_gain_grad,
        sub_bias_grad,
        out_weight_grad,
        out_bias_grad,
        mid_gain_grad,
        mid_bias_grad,
        inner_weight_grad,
        inner_bias_grad,
        ffn_gain_grad,
        ffn_bias_grad,
        outer_weight_grad,
        outer_bias_grad,
    )

def solution(mesh):
    placed = (
        P("dp", None),
        P("dp", None),
        P(),
        P(),
        P(),
        P(),
        P(),
        P(),
        P(None, "tensor"),
        P("tensor"),
        P(None, "tensor"),
        P(None, "tensor"),
        P("tensor"),
        P("tensor"),
        P("tensor"),
        P("tensor", None),
        P(),
        P(),
        P(),
        P(None, "tensor"),
        P("tensor"),
        P("tensor"),
        P("tensor"),
        P("tensor", None),
        P(),
    )
    return jax.shard_map(
        body,
        mesh=mesh,
        in_specs=placed,
        out_specs=(
            P("dp", None),
            P("dp", None),
            P("dp"),
            P("dp"),
            P("dp", "tensor"),
            P(("tensor", "dp")),
            P("dp", "tensor"),
            P("dp", "tensor"),
            P(("tensor", "dp")),
            P(("tensor", "dp")),
            P(("tensor", "dp")),
            P("tensor", "dp"),
            P("dp"),
            P("dp"),
            P("dp"),
            P("dp", "tensor"),
            P(("tensor", "dp")),
            P(("tensor", "dp")),
            P(("tensor", "dp")),
            P("tensor", "dp"),
            P("dp"),
        ),
        check_vma=False,
    )
```
